32 devices in a mesh: grp: 4 (over y, x), seq: 8 (over z, core).
Axes of the slice: x: 2, y: 2, z: 4, core: 2. Of those that a mesh axis runs over, the one named last changes fastest.
Arguments:
- tokens: bfloat16 [4096, 1536], P(('grp', 'seq')), may hold values from -6 to 6
- cotangent: bfloat16 [4096, 1536], P(('grp', 'seq')), may hold values from -12 to 12
- shard_segment: int32 [4, 8], replicated, may hold values from 0 to 2, as said below
- gain_attn: bfloat16 [1536], replicated, may hold values from 0.099609375 to 1.8984375
- qkv_weight: bfloat16 [2048, 1536], P(('grp', 'seq')), may hold values from -0.21875 to 0.21875
- qkv_bias: bfloat16 [2048], P(('grp', 'seq')), may hold values from -3 to 3
- out_weight: bfloat16 [1536, 1536], P(('grp', 'seq')), may hold values from -0.625 to 0.625
- gain_mlp: bfloat16 [1536], replicated, may hold values from 0.099609375 to 1.8984375
- mlp_weight: bfloat16 [8960, 3, 1536], P(('grp', 'seq')), may hold values from -0.15625 to 0.15625
Outputs:
- output: bfloat16 [4096, 1536], P(('grp', 'seq'))
- grad_tokens: float32 [4096, 1536], P(('grp', 'seq'))
- grad_gain_attn: float32 [1536], P(('grp', 'seq'))
- grad_qkv_weight: float32 [2048, 1536], P(('grp', 'seq'))
- grad_qkv_bias: float32 [2048], P(('grp', 'seq'))
- grad_out_weight: float32 [1536, 1536], P(('grp', 'seq'))
- grad_gain_mlp: float32 [1536], P(('grp', 'seq'))
- grad_mlp_weight: float32 [8960, 3, 1536], P(('grp', 'seq'))
The draws below stay inside these ranges and needn't reach their ends.
Inputs may be any that keep to these rules, and one draw needn't show every extreme that they name: For every group g, shard_segment[g, s] = 0 for s < 4; the later shards form runs of 2 or 4 shards with one number, one continuation each, numbered 1, 2, ... in order; every run starts at an even shard, a run of 4 at 4 plus a multiple of 4; some group has only runs of 2, and some group has a run of 4.
All inputs are finite; a program needn't handle non-finite values.
Results may differ from the reference program's by a relative error of at most 0.02.
Values may be sent and summed in bfloat16 or wider, within the bound.
A program may use at most 576 MiB of HBM per device.

```python
import math
import jax
import jax.numpy as jnp
from jax import lax

D = 1536
H = 12
KVH = 2
HD = 128
FF = 8960
TOK_DEV = 128
QKV = 2048
A = 1536
TOKENS = 4096
N_GRP = 4
N_SEQ = 8


def draw_shard_segment(key, part):
    half_count = N_SEQ // 2
    unit_count = half_count // 4
    bits_key, pick_key = jax.random.split(jax.random.fold_in(key, 17), 2)
    split_bits = jax.random.randint(bits_key, (N_GRP, unit_count), 0, 2).astype(jnp.int32)
    chosen_group = jax.random.randint(pick_key, (), 0, N_GRP).astype(jnp.int32)
    other_group = ((chosen_group + 1) % N_GRP).astype(jnp.int32)
    group_order = jnp.arange(N_GRP, dtype=jnp.int32)[:, None]
    unit_order = jnp.arange(unit_count, dtype=jnp.int32)[None, :]
    split_bits = jnp.where((group_order == other_group) & (unit_order == 0), 0, split_bits).astype(jnp.int32)
    split_bits = jnp.where(group_order == chosen_group, 1, split_bits).astype(jnp.int32)
    pair_starts = jnp.stack([jnp.ones_like(split_bits), split_bits], axis=2).reshape(N_GRP, half_count // 2)
    pair_segment = jnp.cumsum(pair_starts, axis=1).astype(jnp.int32)
    tail_segment = jnp.repeat(pair_segment, 2, axis=1)
    return jnp.concatenate([jnp.zeros((N_GRP, half_count), jnp.int32), tail_segment], axis=1).astype(jnp.int32)


def draw_cotangent(key, part):
    first_key = jax.random.fold_in(key, 0)
    row_rise = 1.0 + 2.0 * jnp.arange(TOKENS, dtype=jnp.float32)[:, None] / TOKENS
    base_draw = jnp.clip(jax.random.normal(first_key, (TOKENS, D), jnp.float32), -4.0, 4.0)
    return (base_draw * row_rise).astype(jnp.bfloat16)


def block_scale(own_key, dims, shards, smallest, top_value):
    def one(axis_at, shards_of):
        heights = jax.random.uniform(jax.random.fold_in(jax.random.fold_in(own_key, 6), axis_at), (shards_of,), jnp.float32, smallest / len(shards), top_value / len(shards))
        return jnp.repeat(jnp.exp(heights), dims[axis_at] // shards_of).reshape((-1,) + (1,) * (len(dims) - axis_at - 1))

    gain = one(*shards[0])
    for cut in shards[1:]:
        gain = gain * one(*cut)
    return gain


def normal_values(own_key, dims, deviation, most, pieces=(), kind=jnp.bfloat16):
    gain = block_scale(own_key, dims, pieces, -0.22, 0.18) if pieces else 1.0
    drawn = jax.random.normal(own_key, dims, jnp.float32) * deviation * gain
    return jnp.minimum(jnp.maximum(drawn, -most), most).astype(kind)


def setup_inputs(seed: int = 0) -> dict:
    key_of = jax.random.split(jax.random.key(seed), 10)
    tokens = normal_values(key_of[0], (TOKENS, D), 1.0, 6.0, ((0, 32),))
    cotangent = draw_cotangent(jax.random.fold_in(key_of[9], 71), 0)
    shard_segment = draw_shard_segment(jax.random.fold_in(key_of[9], 71), 0)
    gain_attn = jnp.clip(1.0 + 0.18 * jax.random.normal(key_of[3], (D,), jnp.float32), 0.099609375, 1.8984375).astype(jnp.bfloat16)
    qkv_weight = normal_values(key_of[4], (QKV, D), (D // 2) ** -0.5, 0.21875, ((0, 32),))
    qkv_bias = normal_values(key_of[5], (QKV,), 0.5, 3.0, ((0, 32),))
    out_weight = normal_values(key_of[6], (A, D), (A // 16) ** -0.5, 0.625, ((0, 32),))
    gain_mlp = jnp.clip(1.0 + 0.18 * jax.random.normal(key_of[7], (D,), jnp.float32), 0.099609375, 1.8984375).astype(jnp.bfloat16)
    mlp_weight = normal_values(key_of[8], (FF, 3, D), D ** -0.5, 0.15625, ((0, 32),))
    return dict(tokens=tokens, cotangent=cotangent, shard_segment=shard_segment, gain_attn=gain_attn, qkv_weight=qkv_weight, qkv_bias=qkv_bias, out_weight=out_weight, gain_mlp=gain_mlp, mlp_weight=mlp_weight)


EPS = 1e-06
THETA = 10000.0

@jax.custom_vjp
def low(v):
    return lax.optimization_barrier(v.astype(jnp.bfloat16)).astype(jnp.float32)

@jax.custom_vjp
def low_back(v):
    return v

def low_keep(v):
    return (low(v), None)

def low_pass(kept, grad):
    return (grad,)

def back_keep(v):
    return (v, None)

def back_low(kept, grad):
    return (low(grad),)
low.defvjp(low_keep, low_pass)
low_back.defvjp(back_keep, back_low)

def rms_scale(values, gain_vec):
    return values * lax.rsqrt(lax.optimization_barrier(jnp.mean(values * values, axis=-1, keepdims=True)) + EPS) * gain_vec

def rotary_tables(positions, head_dim):
    half_dim = head_dim // 2
    freqs = THETA ** (-(jnp.arange(half_dim, dtype=jnp.float32) * 2.0) / head_dim)
    angles = positions.astype(jnp.float32)[:, None] * freqs[None, :]
    cosine_table = jnp.concatenate([jnp.cos(angles), jnp.cos(angles)], axis=-1)
    sine_table = jnp.concatenate([jnp.sin(angles), jnp.sin(angles)], axis=-1)
    return (cosine_table, sine_table)

def rotate(values, cosine_table, sine_table):
    half_dim = values.shape[-1] // 2
    turned = jnp.concatenate([-values[..., half_dim:], values[..., :half_dim]], axis=-1)
    return values * cosine_table[:, None, :] + turned * sine_table[:, None, :]

def shard_starts(segments, tok_dev, prompt_len):
    shard_total = segments.shape[0]
    shard_order = jnp.arange(shard_total, dtype=jnp.int32)
    same_seg = segments[:, None] == segments[None, :]
    first_shard = lax.optimization_barrier(jnp.min(jnp.where(same_seg, shard_order[None, :], shard_total), axis=1))
    cont_start = prompt_len + (shard_order - first_shard) * tok_dev
    return jnp.where(segments == 0, shard_order * tok_dev, cont_start).astype(jnp.int32)

def product(left, right):
    return jnp.dot(left, right, precision=lax.Precision.HIGHEST, preferred_element_type=jnp.float32)

def reference(tokens, cotangent, shard_segment, gain_attn, qkv_weight, qkv_bias, out_weight, gain_mlp, mlp_weight):
    group_tok = TOK_DEV * N_SEQ
    heads_per = H // KVH
    kv_width = KVH * HD
    att_width = H * HD
    query_block = min(512, group_tok)
    row_block = min(4096, group_tok)
    score_scale = 1.0 / math.sqrt(HD)

    def forward(x_all, gain_one, qkv_w, qkv_b, out_w, gain_two, mlp_w):

        def one_group(inputs):
            x_rows, segments = inputs
            starts = shard_starts(segments, TOK_DEV, group_tok // 2)
            seg_tok = jnp.repeat(segments, TOK_DEV, total_repeat_length=group_tok)
            pos_tok = jnp.repeat(starts, TOK_DEV, total_repeat_length=group_tok) + jnp.tile(jnp.arange(TOK_DEV, dtype=jnp.int32), N_SEQ)
            cosine_table, sine_table = rotary_tables(pos_tok, HD)
            normed_one = low(rms_scale(x_rows, gain_one))
            qkv_all = low_back(product(normed_one, qkv_w.T) + qkv_b[None, :])
            query_rot = low(rotate(qkv_all[:, :att_width].reshape(group_tok, H, HD), cosine_table, sine_table))
            key_rot = low(rotate(qkv_all[:, att_width:att_width + kv_width].reshape(group_tok, KVH, HD), cosine_table, sine_table))
            value_low = low(qkv_all[:, att_width + kv_width:].reshape(group_tok, KVH, HD))

            def attend(block_args):
                query_part, pos_part, seg_part = block_args
                query_heads = query_part.reshape(query_block, KVH, heads_per, HD)
                raw_scores = jnp.einsum('bkgd,jkd->kgbj', query_heads, key_rot, precision=lax.Precision.HIGHEST)
                scores = low_back(raw_scores * score_scale)
                allowed = ((seg_tok[None, :] == 0) | (seg_tok[None, :] == seg_part[:, None])) & (pos_tok[None, :] <= pos_part[:, None])
                masked = jnp.where(allowed[None, None], scores, -1e+30)
                row_top = lax.optimization_barrier(jnp.max(masked, axis=-1, keepdims=True))
                expo_vals = jnp.where(allowed[None, None], jnp.exp(masked - row_top), 0.0)
                prob_low = low(expo_vals / lax.optimization_barrier(jnp.sum(expo_vals, axis=-1, keepdims=True)))
                mixed_sum = jnp.einsum('kgbj,jkd->bkgd', prob_low, value_low, precision=lax.Precision.HIGHEST)
                return mixed_sum.reshape(query_block, att_width)
            block_total = group_tok // query_block
            attn_all = lax.map(jax.checkpoint(attend), (query_rot.reshape(block_total, query_block, H, HD), pos_tok.reshape(block_total, query_block), seg_tok.reshape(block_total, query_block)))
            attn_low = low(low_back(attn_all.reshape(group_tok, att_width)))
            state = x_rows + low_back(product(attn_low, out_w))
            normed_two = low(rms_scale(state, gain_two))

            def feed(rows_in):
                gate_vals = low_back(product(rows_in, mlp_w[:, 0, :].T))
                upper_vals = low_back(product(rows_in, mlp_w[:, 1, :].T))
                hidden = low(jax.nn.silu(gate_vals) * upper_vals)
                return low_back(product(hidden, mlp_w[:, 2, :]))
            row_total = group_tok // row_block
            mlp_out = lax.map(jax.checkpoint(feed), normed_two.reshape(row_total, row_block, D)).reshape(group_tok, D)
            return state + mlp_out
        outputs = lax.map(one_group, (x_all.reshape(N_GRP, group_tok, D), shard_segment))
        return outputs.reshape(N_GRP * group_tok, D)
    primals = (tokens.astype(jnp.float32), gain_attn.astype(jnp.float32), qkv_weight.astype(jnp.float32), qkv_bias.astype(jnp.float32), out_weight.astype(jnp.float32), gain_mlp.astype(jnp.float32), mlp_weight.astype(jnp.float32))
    result, pull_back = jax.vjp(forward, *primals)
    grads = pull_back(cotangent.astype(jnp.float32))
    return (result.astype(jnp.bfloat16), grads[0], grads[1], grads[2], grads[3], grads[4], grads[5], grads[6])
```

```python
import math

import jax
import jax.numpy as jnp
from jax import lax
from jax.sharding import PartitionSpec as P

H = 12
KVH = 2
HD = 128
FF = 8960


EPS = 1e-06
THETA = 10000.0


def rms_scale(values, gain_vec):
    return values * lax.rsqrt(jnp.mean(values * values, axis=-1, keepdims=True) + EPS) * gain_vec


def rotary_tables(positions, head_dim):
    half_dim = head_dim // 2
    freqs = THETA ** (-(jnp.arange(half_dim, dtype=jnp.float32) * 2.0) / head_dim)
    angles = positions.astype(jnp.float32)[:, None] * freqs[None, :]
    cosine_table = jnp.concatenate([jnp.cos(angles), jnp.cos(angles)], axis=-1)
    sine_table = jnp.concatenate([jnp.sin(angles), jnp.sin(angles)], axis=-1)
    return (cosine_table, sine_table)


def rotate(values, cosine_table, sine_table):
    half_dim = values.shape[-1] // 2
    turned = jnp.concatenate([-values[..., half_dim:], values[..., :half_dim]], axis=-1)
    return values * cosine_table[:, None, :] + turned * sine_table[:, None, :]


def unrotate(grad_rows, cosine_table, sine_table):
    half_dim = grad_rows.shape[-1] // 2
    scaled = grad_rows * sine_table[:, None, :]
    turned = jnp.concatenate([scaled[..., half_dim:], -scaled[..., :half_dim]], axis=-1)
    return grad_rows * cosine_table[:, None, :] + turned


def shard_starts(segments, tok_dev, prompt_len):
    shard_total = segments.shape[0]
    shard_order = jnp.arange(shard_total, dtype=jnp.int32)
    same_seg = segments[:, None] == segments[None, :]
    first_shard = jnp.min(jnp.where(same_seg, shard_order[None, :], shard_total), axis=1)
    cont_start = prompt_len + (shard_order - first_shard) * tok_dev
    return jnp.where(segments == 0, shard_order * tok_dev, cont_start)


def swish_product(gate_vals, upper_vals):
    return jax.nn.silu(gate_vals) * upper_vals


AXES = ("grp", "seq")
CONTRACT_LAST = (((1,), (1,)), ((), ()))
CONTRACT_FIRST = (((0,), (0,)), ((), ()))


def columns_to_owners(rows, row_unit):
    grp_count, seq_count = lax.axis_size("grp"), lax.axis_size("seq")
    tok_rows = rows.shape[0]
    split = rows.reshape(tok_rows, grp_count, seq_count, row_unit).transpose(2, 0, 1, 3)
    split = split.reshape(seq_count * tok_rows, grp_count * row_unit)
    return lax.all_to_all(split, "seq", split_axis=0, concat_axis=0, tiled=True)


def owners_to_columns(rows, row_unit):
    grp_count, seq_count = lax.axis_size("grp"), lax.axis_size("seq")
    tok_rows = rows.shape[0] // seq_count
    moved = lax.all_to_all(rows, "seq", split_axis=0, concat_axis=0, tiled=True)
    moved = moved.reshape(seq_count, tok_rows, grp_count, row_unit).transpose(1, 2, 0, 3)
    return moved.reshape(tok_rows, grp_count * seq_count * row_unit)


def per_device(
    tokens,
    cotangent,
    shard_segment,
    gain_attn,
    qkv_weight,
    qkv_bias,
    out_weight,
    gain_mlp,
    mlp_weight,
):
    tok_rows = tokens.shape[0]
    seq_count = lax.axis_size("seq")
    grp_count = lax.axis_size("grp")
    group_tok = tok_rows * seq_count
    heads_per = H // KVH
    kv_width = KVH * HD
    att_width = H * HD
    query_rows = heads_per * tok_rows
    score_scale = 1.0 / math.sqrt(HD)
    contract_last = CONTRACT_LAST
    contract_first = CONTRACT_FIRST
    seq_place = lax.axis_index("seq")
    grp_place = lax.axis_index("grp")
    segments = lax.dynamic_index_in_dim(shard_segment, grp_place, 0, keepdims=False)
    starts = shard_starts(segments, tok_rows, group_tok // 2)
    shard_order = jnp.arange(seq_count, dtype=jnp.int32)
    own_seg = jnp.sum(jnp.where(shard_order == seq_place, segments, 0))
    own_start = jnp.sum(jnp.where(shard_order == seq_place, starts, 0))
    positions = own_start + jnp.arange(tok_rows, dtype=jnp.int32)
    cosine_table, sine_table = rotary_tables(positions, HD)
    query_pos = jnp.tile(positions, heads_per)
    tokens_wide = tokens.astype(jnp.float32)
    gain_one = gain_attn.astype(jnp.float32)
    gain_two = gain_mlp.astype(jnp.float32)
    normed_one = rms_scale(tokens_wide, gain_one).astype(jnp.bfloat16)
    normed_one_all = lax.all_gather(normed_one, "seq", axis=0, tiled=True)
    qkv_rows = lax.all_gather(qkv_weight, "grp", axis=0, tiled=True)
    bias_rows = lax.all_gather(qkv_bias, "grp", axis=0, tiled=True)
    mlp_rows = lax.all_gather(mlp_weight, "grp", axis=0, tiled=True)
    cotangent_all = lax.all_gather(cotangent, "seq", axis=0, tiled=True)
    out_full = lax.all_gather(out_weight, AXES, axis=0, tiled=True)
    projected = lax.dot_general(
        normed_one_all, qkv_rows, contract_last, preferred_element_type=jnp.float32
    )
    projected = (projected + bias_rows.astype(jnp.float32)[None, :]).astype(jnp.bfloat16)
    projected = owners_to_columns(projected, qkv_weight.shape[0]).astype(jnp.float32)
    query_rot = rotate(
        projected[:, :att_width].reshape(tok_rows, H, HD), cosine_table, sine_table
    ).astype(jnp.bfloat16)
    key_rot = rotate(
        projected[:, att_width : att_width + kv_width].reshape(tok_rows, KVH, HD),
        cosine_table,
        sine_table,
    ).astype(jnp.bfloat16)
    value_low = projected[:, att_width + kv_width :].astype(jnp.bfloat16)
    keys_all, values_all = (
        lax.all_gather(key_rot.reshape(tok_rows, kv_width), "seq", axis=0, tiled=True),
        lax.all_gather(value_low, "seq", axis=0, tiled=True),
    )
    queries = (
        query_rot.reshape(tok_rows, KVH, heads_per, HD)
        .transpose(1, 2, 0, 3)
        .reshape(KVH, query_rows, HD)
    )
    key_block = min(512, group_tok)
    block_count = group_tok // key_block
    block_order = jnp.arange(block_count, dtype=jnp.int32)

    def block_mask(block_index):
        key_index = block_index * key_block + jnp.arange(key_block, dtype=jnp.int32)
        key_shard = key_index // tok_rows
        onehot = key_shard[:, None] == shard_order[None, :]
        key_seg = jnp.sum(jnp.where(onehot, segments[None, :], 0), axis=1)
        key_pos = jnp.sum(jnp.where(onehot, starts[None, :], 0), axis=1) + key_index % tok_rows
        visible = (key_seg == 0) | (key_seg == own_seg)
        return visible[None, :] & (key_pos[None, :] <= query_pos[:, None])

    def block_keys(block_index):
        key_part = lax.dynamic_slice_in_dim(
            keys_all, block_index * key_block, key_block, 0
        ).reshape(key_block, KVH, HD)
        value_part = lax.dynamic_slice_in_dim(
            values_all, block_index * key_block, key_block, 0
        ).reshape(key_block, KVH, HD)
        return (key_part, value_part)

    def block_scores(key_part):
        return (
            jnp.einsum("krd,jkd->krj", queries, key_part, preferred_element_type=jnp.float32)
            * score_scale
        )

    def stat_step(stats_now, block_index):
        allowed = block_mask(block_index)

        def stat_visit(current):
            top_old, total_old = current
            key_part, value_part = block_keys(block_index)
            scores = jnp.where(allowed[None], block_scores(key_part), -1e30)
            top_new = jnp.maximum(top_old, jnp.max(scores, axis=-1))
            weights = jnp.where(allowed[None], jnp.exp(scores - top_new[..., None]), 0.0)
            return (top_new, total_old * jnp.exp(top_old - top_new) + jnp.sum(weights, axis=-1))

        return (lax.cond(jnp.any(allowed), stat_visit, lambda current: current, stats_now), None)

    start_stats = (
        jnp.full((KVH, query_rows), -1e30, jnp.float32),
        jnp.zeros((KVH, query_rows), jnp.float32),
    )
    (top_all, total_all), unused = lax.scan(stat_step, start_stats, block_order)
    log_total = top_all + jnp.log(total_all)

    def mix_step(mixed_sum, block_index):
        allowed = block_mask(block_index)

        def mix_visit(current):
            key_part, value_part = block_keys(block_index)
            prob_low = jnp.where(
                allowed[None], jnp.exp(block_scores(key_part) - log_total[..., None]), 0.0
            ).astype(jnp.bfloat16)
            return current + jnp.einsum(
                "krj,jkd->krd", prob_low, value_part, preferred_element_type=jnp.float32
            )

        return (lax.cond(jnp.any(allowed), mix_visit, lambda current: current, mixed_sum), None)

    mixed_sum, unused = lax.scan(
        mix_step, jnp.zeros((KVH, query_rows, HD), jnp.float32), block_order
    )
    attn_wide = (
        mixed_sum.reshape(KVH, heads_per, tok_rows, HD)
        .transpose(2, 0, 1, 3)
        .reshape(tok_rows, att_width)
    )
    attn_low = attn_wide.astype(jnp.bfloat16)
    attn_proj = jnp.dot(attn_low, out_full, preferred_element_type=jnp.float32)
    state = tokens_wide + attn_proj
    normed_two = rms_scale(state, gain_two).astype(jnp.bfloat16)
    normed_two_all = lax.all_gather(normed_two, "seq", axis=0, tiled=True)
    gate_rows, upper_rows, down_rows = mlp_rows[:, 0, :], mlp_rows[:, 1, :], mlp_rows[:, 2, :]
    gate_vals = lax.dot_general(
        normed_two_all, gate_rows, contract_last, preferred_element_type=jnp.float32
    )
    upper_vals = lax.dot_general(
        normed_two_all, upper_rows, contract_last, preferred_element_type=jnp.float32
    )
    unit_wide, pull_back = jax.vjp(swish_product, gate_vals, upper_vals)
    unit_low = unit_wide.astype(jnp.bfloat16)
    unit_grad = lax.dot_general(
        cotangent_all, down_rows, contract_last, preferred_element_type=jnp.float32
    )
    gate_grad, upper_grad = pull_back(unit_grad)
    gate_grad = gate_grad.astype(jnp.bfloat16)
    upper_grad = upper_grad.astype(jnp.bfloat16)
    input_grad = jnp.dot(gate_grad, gate_rows, preferred_element_type=jnp.float32) + jnp.dot(
        upper_grad, upper_rows, preferred_element_type=jnp.float32
    )
    grad_part = lax.psum_scatter(
        input_grad.astype(jnp.bfloat16), "seq", scatter_dimension=0, tiled=True
    ).astype(jnp.float32)
    out_part = lax.psum_scatter(
        jnp.dot(unit_low, down_rows, preferred_element_type=jnp.float32).astype(jnp.bfloat16),
        "seq",
        scatter_dimension=0,
        tiled=True,
    ).astype(jnp.float32)
    mlp_terms = jnp.stack(
        [
            lax.dot_general(
                gate_grad, normed_two_all, contract_first, preferred_element_type=jnp.float32
            ),
            lax.dot_general(
                upper_grad, normed_two_all, contract_first, preferred_element_type=jnp.float32
            ),
            lax.dot_general(
                unit_low, cotangent_all, contract_first, preferred_element_type=jnp.float32
            ),
        ],
        axis=1,
    )
    mlp_grad = lax.psum_scatter(mlp_terms, "grp", scatter_dimension=0, tiled=True)
    output = (state + out_part).astype(jnp.bfloat16)
    unused_state, norm_two_back = jax.vjp(rms_scale, state, gain_two)
    state_norm_grad, gain_two_grad = norm_two_back(grad_part)
    state_grad = state_norm_grad + cotangent.astype(jnp.float32)
    state_low = state_grad.astype(jnp.bfloat16)
    attn_grad = lax.dot_general(
        state_low, out_full, contract_last, preferred_element_type=jnp.float32
    )
    attn_grad_low = attn_grad.astype(jnp.bfloat16)
    attn_owned = columns_to_owners(attn_low, out_weight.shape[0])
    state_low_all = lax.all_gather(state_low, "seq", axis=0, tiled=True)
    out_grad = lax.psum_scatter(
        lax.dot_general(
            attn_owned, state_low_all, contract_first, preferred_element_type=jnp.float32
        ),
        "grp",
        scatter_dimension=0,
        tiled=True,
    )
    grad_heads = (
        attn_grad_low.reshape(tok_rows, KVH, heads_per, HD)
        .transpose(1, 2, 0, 3)
        .reshape(KVH, query_rows, HD)
    )
    delta_rows = jnp.sum(
        (attn_grad_low.astype(jnp.float32) * attn_wide).reshape(tok_rows, H, HD), axis=-1
    )
    delta_rows = (
        delta_rows.reshape(tok_rows, KVH, heads_per).transpose(1, 2, 0).reshape(KVH, query_rows)
    )

    def back_step(query_grad, block_index):
        allowed = block_mask(block_index)

        def back_visit(current):
            key_part, value_part = block_keys(block_index)
            prob_vals = jnp.where(
                allowed[None], jnp.exp(block_scores(key_part) - log_total[..., None]), 0.0
            )
            prob_grad = jnp.einsum(
                "krd,jkd->krj", grad_heads, value_part, preferred_element_type=jnp.float32
            )
            score_grad = (prob_vals * (prob_grad - delta_rows[..., None])).astype(jnp.bfloat16)
            new_grad = (
                current
                + jnp.einsum(
                    "krj,jkd->krd", score_grad, key_part, preferred_element_type=jnp.float32
                )
                * score_scale
            )
            key_grad = (
                jnp.einsum("krj,krd->jkd", score_grad, queries, preferred_element_type=jnp.float32)
                * score_scale
            )
            value_grad = jnp.einsum(
                "krj,krd->jkd",
                prob_vals.astype(jnp.bfloat16),
                grad_heads,
                preferred_element_type=jnp.float32,
            )
            return (
                new_grad,
                (key_grad.reshape(key_block, kv_width), value_grad.reshape(key_block, kv_width)),
            )

        def skip_block(current):
            blank_rows = jnp.zeros((key_block, kv_width), jnp.float32)
            return (current, (blank_rows, blank_rows))

        return lax.cond(jnp.any(allowed), back_visit, skip_block, query_grad)

    query_grad, (key_grads, value_grads) = lax.scan(
        back_step, jnp.zeros((KVH, query_rows, HD), jnp.float32), block_order
    )
    key_own, value_own = (
        lax.psum_scatter(
            key_grads.reshape(group_tok, kv_width).astype(jnp.bfloat16),
            "seq",
            scatter_dimension=0,
            tiled=True,
        ).astype(jnp.float32),
        lax.psum_scatter(
            value_grads.reshape(group_tok, kv_width).astype(jnp.bfloat16),
            "seq",
            scatter_dimension=0,
            tiled=True,
        ).astype(jnp.float32),
    )
    query_back = unrotate(
        query_grad.reshape(KVH, heads_per, tok_rows, HD)
        .transpose(2, 0, 1, 3)
        .reshape(tok_rows, H, HD),
        cosine_table,
        sine_table,
    )
    key_back = unrotate(key_own.reshape(tok_rows, KVH, HD), cosine_table, sine_table)
    qkv_grad_low = jnp.concatenate(
        [query_back.reshape(tok_rows, att_width), key_back.reshape(tok_rows, kv_width), value_own],
        axis=1,
    ).astype(jnp.bfloat16)
    qkv_grad_owned = columns_to_owners(qkv_grad_low, qkv_weight.shape[0])
    bias_terms = jnp.sum(qkv_grad_owned.astype(jnp.float32), axis=0)
    normed_one_grad = lax.psum_scatter(
        jnp.dot(qkv_grad_owned, qkv_rows, preferred_element_type=jnp.float32).astype(jnp.bfloat16),
        "seq",
        scatter_dimension=0,
        tiled=True,
    ).astype(jnp.float32)
    qkv_grad = lax.psum_scatter(
        lax.dot_general(
            qkv_grad_owned, normed_one_all, contract_first, preferred_element_type=jnp.float32
        ),
        "grp",
        scatter_dimension=0,
        tiled=True,
    )
    unused_tokens, norm_one_back = jax.vjp(rms_scale, tokens_wide, gain_one)
    token_norm_grad, gain_one_grad = norm_one_back(normed_one_grad)
    token_grad = token_norm_grad + state_grad
    bias_part = lax.psum_scatter(bias_terms, "grp", scatter_dimension=0, tiled=True)
    gain_one_part, gain_two_part = (
        lax.psum_scatter(gain_one_grad, AXES, scatter_dimension=0, tiled=True),
        lax.psum_scatter(gain_two_grad, AXES, scatter_dimension=0, tiled=True),
    )
    return (
        output,
        token_grad,
        gain_one_part,
        qkv_grad,
        bias_part,
        out_grad,
        gain_two_part,
        mlp_grad,
    )


def solution(mesh):
    return jax.shard_map(
        per_device,
        mesh=mesh,
        in_specs=(
            P(("grp", "seq"), None),
            P(("grp", "seq"), None),
            P(),
            P(),
            P(("grp", "seq"), None),
            P(("grp", "seq")),
            P(("grp", "seq"), None),
            P(),
            P(("grp", "seq"), None, None),
        ),
        out_specs=(
            P(("grp", "seq"), None),
            P(("grp", "seq"), None),
            P(("grp", "seq")),
            P(("grp", "seq"), None),
            P(("grp", "seq")),
            P(("grp", "seq"), None),
            P(("grp", "seq")),
            P(("grp", "seq"), None, None),
        ),
        check_vma=False,
    )
```

```python
import functools
import math

import jax
import jax.numpy as jnp
from jax import lax
from jax.experimental import pallas as pl
from jax.experimental.pallas import tpu as pltpu
from jax.sharding import PartitionSpec as P

H = 12
KVH = 2
HD = 128
FF = 8960


EPS = 1e-06
THETA = 10000.0


def rms_scale(values, gain_vec):
    return values * lax.rsqrt(jnp.mean(values * values, axis=-1, keepdims=True) + EPS) * gain_vec


def rotary_tables(positions, head_dim):
    half_dim = head_dim // 2
    freqs = THETA ** (-(jnp.arange(half_dim, dtype=jnp.float32) * 2.0) / head_dim)
    angles = positions.astype(jnp.float32)[:, None] * freqs[None, :]
    cosine_table = jnp.concatenate([jnp.cos(angles), jnp.cos(angles)], axis=-1)
    sine_table = jnp.concatenate([jnp.sin(angles), jnp.sin(angles)], axis=-1)
    return (cosine_table, sine_table)


def rotate(values, cosine_table, sine_table):
    half_dim = values.shape[-1] // 2
    turned = jnp.concatenate([-values[..., half_dim:], values[..., :half_dim]], axis=-1)
    return values * cosine_table[:, None, :] + turned * sine_table[:, None, :]


def unrotate(grad_rows, cosine_table, sine_table):
    half_dim = grad_rows.shape[-1] // 2
    scaled = grad_rows * sine_table[:, None, :]
    turned = jnp.concatenate([scaled[..., half_dim:], -scaled[..., :half_dim]], axis=-1)
    return grad_rows * cosine_table[:, None, :] + turned


def shard_starts(segments, tok_dev, prompt_len):
    shard_total = segments.shape[0]
    shard_order = jnp.arange(shard_total, dtype=jnp.int32)
    same_seg = segments[:, None] == segments[None, :]
    first_shard = jnp.min(jnp.where(same_seg, shard_order[None, :], shard_total), axis=1)
    cont_start = prompt_len + (shard_order - first_shard) * tok_dev
    return jnp.where(segments == 0, shard_order * tok_dev, cont_start)


def swish_product(gate_vals, upper_vals):
    return jax.nn.silu(gate_vals) * upper_vals


AXES = ("grp", "seq")
CONTRACT_LAST = (((1,), (1,)), ((), ()))
CONTRACT_FIRST = (((0,), (0,)), ((), ()))


MESH = pl.DeviceIdType.MESH


def remote(src, dst, send_sem, recv_sem, grp, seq):
    return pltpu.make_async_remote_copy(
        src_ref=src, dst_ref=dst, send_sem=send_sem, recv_sem=recv_sem,
        device_id=(grp, seq), device_id_type=MESH,
    )


def nearest_chip(place, order, chips):
    both = 2 * jnp.minimum(place, chips - 1 - place)
    offset = (order + 1) // 2
    near = jnp.where(order % 2 == 1, place - offset, place + offset)
    rest = jnp.where(place < chips - 1 - place, order, chips - 1 - order)
    return jnp.where(order <= both, near, rest)


def line_barrier(chips):
    grp, seq = lax.axis_index("grp"), lax.axis_index("seq")
    chip, core = seq // 2, seq % 2
    mate = seq + 1 - 2 * core
    barrier = pltpu.get_barrier_semaphore()

    def greet(other):
        pl.semaphore_signal(barrier, inc=1, device_id=(grp, other), device_id_type=MESH)

    greet(mate)
    pl.when(chip > 0)(lambda: greet(seq - 2))
    pl.when(chip < chips - 1)(lambda: greet(seq + 2))
    inner = jnp.where((chip > 0) & (chip < chips - 1), 1, 0)
    pl.semaphore_wait(barrier, 2 + inner)


class LineGather:
    def __init__(self, buf, send_sem, recv_sem, chips):
        self.buf, self.send_sem, self.recv_sem, self.chips = buf, send_sem, recv_sem, chips
        self.grp, self.seq = lax.axis_index("grp"), lax.axis_index("seq")
        self.chip, self.core = self.seq // 2, self.seq % 2
        self.mate = self.seq + 1 - 2 * self.core

    def copy(self, way, slot):
        to = (self.seq + 2, self.seq - 2, self.mate)[way]
        return remote(
            self.buf.at[slot], self.buf.at[slot], self.send_sem.at[way, slot],
            self.recv_sem.at[slot], self.grp, to,
        )

    def wait_recv(self, slot):
        self.copy(2, slot).wait_recv()

    def start(self):
        pl.when(self.chip < self.chips - 1)(lambda: self.copy(0, self.seq).start())
        pl.when(self.chip > 0)(lambda: self.copy(1, self.seq).start())
        self.copy(2, self.seq).start()

    def forward(self, step):
        @pl.when(self.chip - step >= 0)
        def _():
            slot = self.seq - 2 * step
            self.wait_recv(slot)
            pl.when(self.chip < self.chips - 1)(lambda: self.copy(0, slot).start())
            self.copy(2, slot).start()

        @pl.when(self.chip + step < self.chips)
        def _():
            slot = self.seq + 2 * step
            self.wait_recv(slot)
            pl.when(self.chip > 0)(lambda: self.copy(1, slot).start())
            self.copy(2, slot).start()

    def wait_mate(self, chip):
        self.wait_recv(2 * chip + 1 - self.core)

    def drain(self):
        for other in range(self.chips):
            slot = 2 * other + self.core
            self.copy(2, slot).wait_send()
            pl.when((other <= self.chip) & (self.chip < self.chips - 1))(
                lambda slot=slot: self.copy(0, slot).wait_send()
            )
            pl.when((other >= self.chip) & (self.chip > 0))(
                lambda slot=slot: self.copy(1, slot).wait_send()
            )


class LineScatter:
    def __init__(self, part, mate_in, left_in, right_in, send_sem, recv_sem, chips):
        self.part, self.mate_in, self.left_in, self.right_in = part, mate_in, left_in, right_in
        self.send_sem, self.recv_sem, self.chips = send_sem, recv_sem, chips
        self.grp, self.seq = lax.axis_index("grp"), lax.axis_index("seq")
        self.chip, self.core = self.seq // 2, self.seq % 2
        self.mate = self.seq + 1 - 2 * self.core

    def to_mate(self, r, chip):
        return remote(
            self.part.at[r, 2 * chip + 1 - self.core], self.mate_in.at[r, chip],
            self.send_sem.at[0, r, chip], self.recv_sem.at[0, r, chip], self.grp, self.mate,
        )

    def to_right(self, r, chip):
        return remote(
            self.part.at[r, 2 * chip + self.core], self.left_in.at[r, chip],
            self.send_sem.at[1, r, chip], self.recv_sem.at[1, r, chip], self.grp, self.seq + 2,
        )

    def to_left(self, r, chip):
        return remote(
            self.part.at[r, 2 * chip + self.core], self.right_in.at[r, chip],
            self.send_sem.at[2, r, chip], self.recv_sem.at[2, r, chip], self.grp, self.seq - 2,
        )

    def step(self, r, order):
        last = self.chips - 1
        far = last - order

        @pl.when(far > self.chip)
        def _():
            self.to_mate(r, far).wait_recv()
            slot = 2 * far + self.core
            total = self.part[r, slot].astype(jnp.float32) + self.mate_in[r, far].astype(jnp.float32)

            @pl.when(self.chip > 0)
            def _():
                self.to_right(r, far).wait_recv()
                self.part[r, slot] = (total + self.left_in[r, far].astype(jnp.float32)).astype(jnp.bfloat16)

            @pl.when(self.chip == 0)
            def _():
                self.part[r, slot] = total.astype(jnp.bfloat16)

            self.to_right(r, far).start()

        @pl.when(order < self.chip)
        def _():
            self.to_mate(r, order).wait_recv()
            slot = 2 * order + self.core
            total = self.part[r, slot].astype(jnp.float32) + self.mate_in[r, order].astype(jnp.float32)

            @pl.when(self.chip < last)
            def _():
                self.to_left(r, order).wait_recv()
                self.part[r, slot] = (total + self.right_in[r, order].astype(jnp.float32)).astype(jnp.bfloat16)

            @pl.when(self.chip == last)
            def _():
                self.part[r, slot] = total.astype(jnp.bfloat16)

            self.to_left(r, order).start()

    def finish(self, r, out_ref):
        self.to_mate(r, self.chip).wait_recv()
        out_ref[...] = self.part[r, self.seq].astype(jnp.float32) + self.mate_in[r, self.chip].astype(jnp.float32)

        @pl.when(self.chip > 0)
        def _():
            self.to_right(r, self.chip).wait_recv()
            out_ref[...] += self.left_in[r, self.chip].astype(jnp.float32)

        @pl.when(self.chip < self.chips - 1)
        def _():
            self.to_left(r, self.chip).wait_recv()
            out_ref[...] += self.right_in[r, self.chip].astype(jnp.float32)

    def drain(self, r):
        for other in range(self.chips):
            self.to_mate(r, other).wait_send()
            pl.when(other > self.chip)(lambda other=other: self.to_right(r, other).wait_send())
            pl.when(other < self.chip)(lambda other=other: self.to_left(r, other).wait_send())


def mlp_kernel(chips, grps, row_tiles, n2_ref, cot_ref, *refs):
    w_refs, refs = refs[:grps], refs[grps:]
    (
        n2g_ref, outp_ref, grads_ref, tok, w, acts, part, mate_in, left_in, right_in, stage,
        lsem, gsend, grecv, ssend, srecv, wsem, osem,
    ) = refs
    seq = lax.axis_index("seq")
    chip, core = seq // 2, seq % 2
    shard, width = n2_ref.shape
    units = w.shape[1]
    block = units // grps
    tile = units // row_tiles
    own = pltpu.make_async_copy(n2_ref, tok.at[0, seq], lsem.at[0])
    own.start()
    cot_copy = pltpu.make_async_copy(cot_ref, tok.at[1], lsem.at[1])
    cot_copy.start()

    def w_copy(j, b):
        return pltpu.make_async_copy(w_refs[b].at[j], w.at[j, pl.ds(b * block, block)], wsem.at[j, b])

    for j in range(3):
        for b in range(grps):
            w_copy(j, b).start()
    line_barrier(chips)
    gather = LineGather(tok.at[0], gsend, grecv, chips)
    scatter = LineScatter(part, mate_in, left_in, right_in, ssend, srecv, chips)
    own.wait()
    gather.start()

    @pl.loop(0, chips)
    def _(order):
        @pl.when(order == 0)
        def _():
            cot_copy.wait()
            for j in range(3):
                for b in range(grps):
                    w_copy(j, b).wait()

        pl.when(order > 0)(lambda: gather.forward(order))
        at = nearest_chip(chip, order, chips)
        gather.wait_mate(at)
        x = tok[0, pl.ds(2 * at, 2)].reshape(2 * shard, width)
        y = tok[1, pl.ds(2 * at, 2)].reshape(2 * shard, width)
        gate = lax.dot_general(x, w[0], CONTRACT_LAST, preferred_element_type=jnp.float32)
        up = lax.dot_general(x, w[1], CONTRACT_LAST, preferred_element_type=jnp.float32)
        unit_grad = lax.dot_general(y, w[2], CONTRACT_LAST, preferred_element_type=jnp.float32)
        sig = 1.0 / (1.0 + jnp.exp(-gate))
        silu = gate * sig
        rows = pl.ds(at * (2 * shard), 2 * shard)
        gate_grad = (unit_grad * up * sig * (1.0 + gate * (1.0 - sig))).astype(jnp.bfloat16)
        up_grad = (unit_grad * silu).astype(jnp.bfloat16)
        acts[0, rows] = gate_grad
        acts[1, rows] = up_grad
        acts[2, rows] = (silu * up).astype(jnp.bfloat16)
        back = jnp.dot(gate_grad, w[0], preferred_element_type=jnp.float32) + jnp.dot(
            up_grad, w[1], preferred_element_type=jnp.float32
        )
        part[0, pl.ds(2 * at, 2)] = back.astype(jnp.bfloat16).reshape(2, shard, width)
        scatter.to_mate(0, at).start()

    def out_copy(t):
        return pltpu.make_async_copy(
            stage.at[t % 2],
            grads_ref.at[t // row_tiles, pl.ds((t % row_tiles) * tile, tile)],
            osem.at[t % 2],
        )

    @pl.loop(0, 3 * row_tiles)
    def _(t):
        @pl.when(t < 2 * chips)
        def _():
            scatter.step(t // chips, t % chips)

        @pl.when(t < chips)
        def _():
            h = acts[2, pl.ds(t * (2 * shard), 2 * shard)]
            part[1, pl.ds(2 * t, 2)] = (
                jnp.dot(h, w[2], preferred_element_type=jnp.float32)
                .astype(jnp.bfloat16).reshape(2, shard, width)
            )
            scatter.to_mate(1, t).start()

        @pl.when(t >= 2)
        def _():
            out_copy(t - 2).wait()

        kind = t // row_tiles
        lhs = acts[kind, :, pl.ds(pl.multiple_of((t % row_tiles) * tile, 128), tile)]
        rhs = tok[kind // 2].reshape(2 * chips * shard, width)
        stage[t % 2] = lax.dot_general(
            lhs, rhs, CONTRACT_FIRST, preferred_element_type=jnp.float32
        ).astype(jnp.bfloat16)
        out_copy(t).start()

    scatter.finish(0, n2g_ref)
    scatter.finish(1, outp_ref)
    out_copy(3 * row_tiles - 2).wait()
    out_copy(3 * row_tiles - 1).wait()
    gather.drain()
    scatter.drain(0)
    scatter.drain(1)


def mlp_call(n2, cot_all, w_blocks, row_tiles=3):
    grps, (_, block, width) = len(w_blocks), w_blocks[0].shape
    slots, shard, _ = cot_all.shape
    chips = slots // 2
    units = grps * block
    vm, anyspace = pltpu.VMEM, pl.BlockSpec(memory_space=pl.ANY)
    vspec = pl.BlockSpec(memory_space=pltpu.VMEM)
    dma = pltpu.SemaphoreType.DMA
    flops = 2 * 9 * slots * shard * units * width
    return pl.pallas_call(
        functools.partial(mlp_kernel, chips, grps, row_tiles),
        out_shape=(
            jax.ShapeDtypeStruct((shard, width), jnp.float32),
            jax.ShapeDtypeStruct((shard, width), jnp.float32),
            jax.ShapeDtypeStruct((3, units, width), jnp.bfloat16),
        ),
        in_specs=[vspec, anyspace] + [anyspace] * grps,
        out_specs=(vspec, vspec, anyspace),
        scratch_shapes=[
            vm((2, slots, shard, width), jnp.bfloat16),
            vm((3, units, width), jnp.bfloat16),
            vm((3, slots * shard, units), jnp.bfloat16),
            vm((2, slots, shard, width), jnp.bfloat16),
            vm((2, chips, shard, width), jnp.bfloat16),
            vm((2, chips, shard, width), jnp.bfloat16),
            vm((2, chips, shard, width), jnp.bfloat16),
            vm((2, units // row_tiles, width), jnp.bfloat16),
            dma((2,)), dma((3, slots)), dma((slots,)), dma((3, 2, chips)), dma((3, 2, chips)),
            dma((3, grps)), dma((2,)),
        ],
        compiler_params=pltpu.CompilerParams(
            collective_id=1, has_side_effects=True, vmem_limit_bytes=62 * 2**20
        ),
        cost_estimate=pl.CostEstimate(flops=flops, bytes_accessed=30 * 2**20, transcendentals=0),
        name="mlp",
    )(n2, cot_all, *w_blocks)


def columns_to_owners(rows, row_unit):
    grp_count, seq_count = lax.axis_size("grp"), lax.axis_size("seq")
    tok_rows = rows.shape[0]
    split = rows.reshape(tok_rows, grp_count, seq_count, row_unit).transpose(2, 0, 1, 3)
    split = split.reshape(seq_count * tok_rows, grp_count * row_unit)
    return lax.all_to_all(split, "seq", split_axis=0, concat_axis=0, tiled=True)


def owners_to_columns(rows, row_unit):
    grp_count, seq_count = lax.axis_size("grp"), lax.axis_size("seq")
    tok_rows = rows.shape[0] // seq_count
    moved = lax.all_to_all(rows, "seq", split_axis=0, concat_axis=0, tiled=True)
    moved = moved.reshape(seq_count, tok_rows, grp_count, row_unit).transpose(1, 2, 0, 3)
    return moved.reshape(tok_rows, grp_count * seq_count * row_unit)


def plain_mlp(normed_two, cotangent_all, mlp_weight):
    contract_last, contract_first = CONTRACT_LAST, CONTRACT_FIRST
    mlp_rows = lax.all_gather(mlp_weight, "grp", axis=0, tiled=True)
    normed_two_all = lax.all_gather(normed_two, "seq", axis=0, tiled=True)
    gate_rows, upper_rows, down_rows = mlp_rows[:, 0, :], mlp_rows[:, 1, :], mlp_rows[:, 2, :]
    gate_vals = lax.dot_general(
        normed_two_all, gate_rows, contract_last, preferred_element_type=jnp.float32
    )
    upper_vals = lax.dot_general(
        normed_two_all, upper_rows, contract_last, preferred_element_type=jnp.float32
    )
    unit_wide, pull_back = jax.vjp(swish_product, gate_vals, upper_vals)
    unit_low = unit_wide.astype(jnp.bfloat16)
    unit_grad = lax.dot_general(
        cotangent_all, down_rows, contract_last, preferred_element_type=jnp.float32
    )
    gate_grad, upper_grad = pull_back(unit_grad)
    gate_grad = gate_grad.astype(jnp.bfloat16)
    upper_grad = upper_grad.astype(jnp.bfloat16)
    input_grad = jnp.dot(gate_grad, gate_rows, preferred_element_type=jnp.float32) + jnp.dot(
        upper_grad, upper_rows, preferred_element_type=jnp.float32
    )
    grad_part = lax.psum_scatter(
        input_grad.astype(jnp.bfloat16), "seq", scatter_dimension=0, tiled=True
    ).astype(jnp.float32)
    out_part = lax.psum_scatter(
        jnp.dot(unit_low, down_rows, preferred_element_type=jnp.float32).astype(jnp.bfloat16),
        "seq",
        scatter_dimension=0,
        tiled=True,
    ).astype(jnp.float32)
    mlp_terms = jnp.stack(
        [
            lax.dot_general(
                gate_grad, normed_two_all, contract_first, preferred_element_type=jnp.float32
            ),
            lax.dot_general(
                upper_grad, normed_two_all, contract_first, preferred_element_type=jnp.float32
            ),
            lax.dot_general(
                unit_low, cotangent_all, contract_first, preferred_element_type=jnp.float32
            ),
        ],
        axis=1,
    )
    mlp_grad = lax.psum_scatter(mlp_terms, "grp", scatter_dimension=0, tiled=True)
    return grad_part, out_part, mlp_grad


def padded_rows(mlp_weight):
    rows = mlp_weight.transpose(1, 0, 2)
    return jnp.pad(rows, ((0, 0), (0, -rows.shape[1] % 32), (0, 0)))


def from_peer(values, offset, grp_count):
    return lax.ppermute(values, "grp", [(g, g ^ offset) for g in range(grp_count)])


def exchange_blocks(rows, grp_count):
    return [rows] + [from_peer(rows, offset, grp_count) for offset in range(1, grp_count)]


def sum_blocks(terms, grp_count):
    block = terms.shape[1] // grp_count
    total = terms[:, :block].astype(jnp.float32)
    for offset in range(1, grp_count):
        piece = terms[:, offset * block : (offset + 1) * block]
        total = total + from_peer(piece, offset, grp_count).astype(jnp.float32)
    return total


def per_device(
    tokens,
    cotangent,
    shard_segment,
    gain_attn,
    qkv_weight,
    qkv_bias,
    out_weight,
    gain_mlp,
    mlp_weight,
):
    tok_rows = tokens.shape[0]
    seq_count = lax.axis_size("seq")
    grp_count = lax.axis_size("grp")
    group_tok = tok_rows * seq_count
    heads_per = H // KVH
    kv_width = KVH * HD
    att_width = H * HD
    query_rows = heads_per * tok_rows
    score_scale = 1.0 / math.sqrt(HD)
    contract_last = CONTRACT_LAST
    contract_first = CONTRACT_FIRST
    seq_place = lax.axis_index("seq")
    grp_place = lax.axis_index("grp")
    segments = lax.dynamic_index_in_dim(shard_segment, grp_place, 0, keepdims=False)
    starts = shard_starts(segments, tok_rows, group_tok // 2)
    shard_order = jnp.arange(seq_count, dtype=jnp.int32)
    own_seg = jnp.sum(jnp.where(shard_order == seq_place, segments, 0))
    own_start = jnp.sum(jnp.where(shard_order == seq_place, starts, 0))
    positions = own_start + jnp.arange(tok_rows, dtype=jnp.int32)
    cosine_table, sine_table = rotary_tables(positions, HD)
    query_pos = jnp.tile(positions, heads_per)
    tokens_wide = tokens.astype(jnp.float32)
    gain_one = gain_attn.astype(jnp.float32)
    gain_two = gain_mlp.astype(jnp.float32)
    normed_one = rms_scale(tokens_wide, gain_one).astype(jnp.bfloat16)
    normed_one_all = lax.all_gather(normed_one, "seq", axis=0, tiled=True)
    qkv_rows = lax.all_gather(qkv_weight, "grp", axis=0, tiled=True)
    bias_rows = lax.all_gather(qkv_bias, "grp", axis=0, tiled=True)
    use_kernels = group_tok <= 1024
    mlp_blocks = exchange_blocks(padded_rows(mlp_weight), grp_count) if use_kernels else None
    cotangent_all = lax.all_gather(cotangent, "seq", axis=0, tiled=True)
    out_full = lax.all_gather(out_weight, AXES, axis=0, tiled=True)
    projected = lax.dot_general(
        normed_one_all, qkv_rows, contract_last, preferred_element_type=jnp.float32
    )
    projected = (projected + bias_rows.astype(jnp.float32)[None, :]).astype(jnp.bfloat16)
    projected = owners_to_columns(projected, qkv_weight.shape[0]).astype(jnp.float32)
    query_rot = rotate(
        projected[:, :att_width].reshape(tok_rows, H, HD), cosine_table, sine_table
    ).astype(jnp.bfloat16)
    key_rot = rotate(
        projected[:, att_width : att_width + kv_width].reshape(tok_rows, KVH, HD),
        cosine_table,
        sine_table,
    ).astype(jnp.bfloat16)
    value_low = projected[:, att_width + kv_width :].astype(jnp.bfloat16)
    keys_all, values_all = (
        lax.all_gather(key_rot.reshape(tok_rows, kv_width), "seq", axis=0, tiled=True),
        lax.all_gather(value_low, "seq", axis=0, tiled=True),
    )
    queries = (
        query_rot.reshape(tok_rows, KVH, heads_per, HD)
        .transpose(1, 2, 0, 3)
        .reshape(KVH, query_rows, HD)
    )
    key_block = min(512, group_tok)
    block_count = group_tok // key_block
    block_order = jnp.arange(block_count, dtype=jnp.int32)

    def block_mask(block_index):
        key_index = block_index * key_block + jnp.arange(key_block, dtype=jnp.int32)
        key_shard = key_index // tok_rows
        onehot = key_shard[:, None] == shard_order[None, :]
        key_seg = jnp.sum(jnp.where(onehot, segments[None, :], 0), axis=1)
        key_pos = jnp.sum(jnp.where(onehot, starts[None, :], 0), axis=1) + key_index % tok_rows
        visible = (key_seg == 0) | (key_seg == own_seg)
        return visible[None, :] & (key_pos[None, :] <= query_pos[:, None])

    def block_keys(block_index):
        key_part = lax.dynamic_slice_in_dim(
            keys_all, block_index * key_block, key_block, 0
        ).reshape(key_block, KVH, HD)
        value_part = lax.dynamic_slice_in_dim(
            values_all, block_index * key_block, key_block, 0
        ).reshape(key_block, KVH, HD)
        return (key_part, value_part)

    def block_scores(key_part):
        return (
            jnp.einsum("krd,jkd->krj", queries, key_part, preferred_element_type=jnp.float32)
            * score_scale
        )

    def stat_step(stats_now, block_index):
        allowed = block_mask(block_index)

        def stat_visit(current):
            top_old, total_old = current
            key_part, value_part = block_keys(block_index)
            scores = jnp.where(allowed[None], block_scores(key_part), -1e30)
            top_new = jnp.maximum(top_old, jnp.max(scores, axis=-1))
            weights = jnp.where(allowed[None], jnp.exp(scores - top_new[..., None]), 0.0)
            return (top_new, total_old * jnp.exp(top_old - top_new) + jnp.sum(weights, axis=-1))

        return (lax.cond(jnp.any(allowed), stat_visit, lambda current: current, stats_now), None)

    start_stats = (
        jnp.full((KVH, query_rows), -1e30, jnp.float32),
        jnp.zeros((KVH, query_rows), jnp.float32),
    )
    (top_all, total_all), unused = lax.scan(stat_step, start_stats, block_order)
    log_total = top_all + jnp.log(total_all)

    def mix_step(mixed_sum, block_index):
        allowed = block_mask(block_index)

        def mix_visit(current):
            key_part, value_part = block_keys(block_index)
            prob_low = jnp.where(
                allowed[None], jnp.exp(block_scores(key_part) - log_total[..., None]), 0.0
            ).astype(jnp.bfloat16)
            return current + jnp.einsum(
                "krj,jkd->krd", prob_low, value_part, preferred_element_type=jnp.float32
            )

        return (lax.cond(jnp.any(allowed), mix_visit, lambda current: current, mixed_sum), None)

    mixed_sum, unused = lax.scan(
        mix_step, jnp.zeros((KVH, query_rows, HD), jnp.float32), block_order
    )
    attn_wide = (
        mixed_sum.reshape(KVH, heads_per, tok_rows, HD)
        .transpose(2, 0, 1, 3)
        .reshape(tok_rows, att_width)
    )
    attn_low = attn_wide.astype(jnp.bfloat16)
    attn_proj = jnp.dot(attn_low, out_full, preferred_element_type=jnp.float32)
    state = tokens_wide + attn_proj
    normed_two = rms_scale(state, gain_two).astype(jnp.bfloat16)
    if use_kernels:
        grad_part, out_part, mlp_terms = mlp_call(
            normed_two, cotangent_all.reshape(seq_count, tok_rows, -1), mlp_blocks
        )
        mlp_grad = sum_blocks(mlp_terms, grp_count)[:, : mlp_weight.shape[0]].transpose(1, 0, 2)
    else:
        grad_part, out_part, mlp_grad = plain_mlp(normed_two, cotangent_all, mlp_weight)
    output = (state + out_part).astype(jnp.bfloat16)
    unused_state, norm_two_back = jax.vjp(rms_scale, state, gain_two)
    state_norm_grad, gain_two_grad = norm_two_back(grad_part)
    state_grad = state_norm_grad + cotangent.astype(jnp.float32)
    state_low = state_grad.astype(jnp.bfloat16)
    attn_grad = lax.dot_general(
        state_low, out_full, contract_last, preferred_element_type=jnp.float32
    )
    attn_grad_low = attn_grad.astype(jnp.bfloat16)
    attn_owned = columns_to_owners(attn_low, out_weight.shape[0])
    state_low_all = lax.all_gather(state_low, "seq", axis=0, tiled=True)
    out_grad = lax.psum_scatter(
        lax.dot_general(
            attn_owned, state_low_all, contract_first, preferred_element_type=jnp.float32
        ),
        "grp",
        scatter_dimension=0,
        tiled=True,
    )
    grad_heads = (
        attn_grad_low.reshape(tok_rows, KVH, heads_per, HD)
        .transpose(1, 2, 0, 3)
        .reshape(KVH, query_rows, HD)
    )
    delta_rows = jnp.sum(
        (attn_grad_low.astype(jnp.float32) * attn_wide).reshape(tok_rows, H, HD), axis=-1
    )
    delta_rows = (
        delta_rows.reshape(tok_rows, KVH, heads_per).transpose(1, 2, 0).reshape(KVH, query_rows)
    )

    def back_step(query_grad, block_index):
        allowed = block_mask(block_index)

        def back_visit(current):
            key_part, value_part = block_keys(block_index)
            prob_vals = jnp.where(
                allowed[None], jnp.exp(block_scores(key_part) - log_total[..., None]), 0.0
            )
            prob_grad = jnp.einsum(
                "krd,jkd->krj", grad_heads, value_part, preferred_element_type=jnp.float32
            )
            score_grad = (prob_vals * (prob_grad - delta_rows[..., None])).astype(jnp.bfloat16)
            new_grad = (
                current
                + jnp.einsum(
                    "krj,jkd->krd", score_grad, key_part, preferred_element_type=jnp.float32
                )
                * score_scale
            )
            key_grad = (
                jnp.einsum("krj,krd->jkd", score_grad, queries, preferred_element_type=jnp.float32)
                * score_scale
            )
            value_grad = jnp.einsum(
                "krj,krd->jkd",
                prob_vals.astype(jnp.bfloat16),
                grad_heads,
                preferred_element_type=jnp.float32,
            )
            return (
                new_grad,
                (key_grad.reshape(key_block, kv_width), value_grad.reshape(key_block, kv_width)),
            )

        def skip_block(current):
            blank_rows = jnp.zeros((key_block, kv_width), jnp.float32)
            return (current, (blank_rows, blank_rows))

        return lax.cond(jnp.any(allowed), back_visit, skip_block, query_grad)

    query_grad, (key_grads, value_grads) = lax.scan(
        back_step, jnp.zeros((KVH, query_rows, HD), jnp.float32), block_order
    )
    key_own, value_own = (
        lax.psum_scatter(
            key_grads.reshape(group_tok, kv_width).astype(jnp.bfloat16),
            "seq",
            scatter_dimension=0,
            tiled=True,
        ).astype(jnp.float32),
        lax.psum_scatter(
            value_grads.reshape(group_tok, kv_width).astype(jnp.bfloat16),
            "seq",
            scatter_dimension=0,
            tiled=True,
        ).astype(jnp.float32),
    )
    query_back = unrotate(
        query_grad.reshape(KVH, heads_per, tok_rows, HD)
        .transpose(2, 0, 1, 3)
        .reshape(tok_rows, H, HD),
        cosine_table,
        sine_table,
    )
    key_back = unrotate(key_own.reshape(tok_rows, KVH, HD), cosine_table, sine_table)
    qkv_grad_low = jnp.concatenate(
        [query_back.reshape(tok_rows, att_width), key_back.reshape(tok_rows, kv_width), value_own],
        axis=1,
    ).astype(jnp.bfloat16)
    qkv_grad_owned = columns_to_owners(qkv_grad_low, qkv_weight.shape[0])
    bias_terms = jnp.sum(qkv_grad_owned.astype(jnp.float32), axis=0)
    normed_one_grad = lax.psum_scatter(
        jnp.dot(qkv_grad_owned, qkv_rows, preferred_element_type=jnp.float32).astype(jnp.bfloat16),
        "seq",
        scatter_dimension=0,
        tiled=True,
    ).astype(jnp.float32)
    qkv_grad = lax.psum_scatter(
        lax.dot_general(
            qkv_grad_owned, normed_one_all, contract_first, preferred_element_type=jnp.float32
        ),
        "grp",
        scatter_dimension=0,
        tiled=True,
    )
    unused_tokens, norm_one_back = jax.vjp(rms_scale, tokens_wide, gain_one)
    token_norm_grad, gain_one_grad = norm_one_back(normed_one_grad)
    token_grad = token_norm_grad + state_grad
    bias_part = lax.psum_scatter(bias_terms, "grp", scatter_dimension=0, tiled=True)
    gain_one_part, gain_two_part = (
        lax.psum_scatter(gain_one_grad, AXES, scatter_dimension=0, tiled=True),
        lax.psum_scatter(gain_two_grad, AXES, scatter_dimension=0, tiled=True),
    )
    return (
        output,
        token_grad,
        gain_one_part,
        qkv_grad,
        bias_part,
        out_grad,
        gain_two_part,
        mlp_grad,
    )


def solution(mesh):
    return jax.shard_map(
        per_device,
        mesh=mesh,
        in_specs=(
            P(("grp", "seq"), None),
            P(("grp", "seq"), None),
            P(),
            P(),
            P(("grp", "seq"), None),
            P(("grp", "seq")),
            P(("grp", "seq"), None),
            P(),
            P(("grp", "seq"), None, None),
        ),
        out_specs=(
            P(("grp", "seq"), None),
            P(("grp", "seq"), None),
            P(("grp", "seq")),
            P(("grp", "seq"), None),
            P(("grp", "seq")),
            P(("grp", "seq"), None),
            P(("grp", "seq")),
            P(("grp", "seq"), None, None),
        ),
        check_vma=False,
    )
```

```python
import functools
import math

import jax
import jax.numpy as jnp
from jax import lax
from jax.experimental import pallas as pl
from jax.experimental.pallas import tpu as pltpu
from jax.sharding import PartitionSpec as P

H = 12
KVH = 2
HD = 128
FF = 8960


EPS = 1e-06
THETA = 10000.0


def rms_scale(values, gain_vec):
    return values * lax.rsqrt(jnp.mean(values * values, axis=-1, keepdims=True) + EPS) * gain_vec


def rotary_tables(positions, head_dim):
    half_dim = head_dim // 2
    freqs = THETA ** (-(jnp.arange(half_dim, dtype=jnp.float32) * 2.0) / head_dim)
    angles = positions.astype(jnp.float32)[:, None] * freqs[None, :]
    cosine_table = jnp.concatenate([jnp.cos(angles), jnp.cos(angles)], axis=-1)
    sine_table = jnp.concatenate([jnp.sin(angles), jnp.sin(angles)], axis=-1)
    return (cosine_table, sine_table)


def rotate(values, cosine_table, sine_table):
    half_dim = values.shape[-1] // 2
    turned = jnp.concatenate([-values[..., half_dim:], values[..., :half_dim]], axis=-1)
    return values * cosine_table[:, None, :] + turned * sine_table[:, None, :]


def unrotate(grad_rows, cosine_table, sine_table):
    half_dim = grad_rows.shape[-1] // 2
    scaled = grad_rows * sine_table[:, None, :]
    turned = jnp.concatenate([scaled[..., half_dim:], -scaled[..., :half_dim]], axis=-1)
    return grad_rows * cosine_table[:, None, :] + turned


def shard_starts(segments, tok_dev, prompt_len):
    shard_total = segments.shape[0]
    shard_order = jnp.arange(shard_total, dtype=jnp.int32)
    same_seg = segments[:, None] == segments[None, :]
    first_shard = jnp.min(jnp.where(same_seg, shard_order[None, :], shard_total), axis=1)
    cont_start = prompt_len + (shard_order - first_shard) * tok_dev
    return jnp.where(segments == 0, shard_order * tok_dev, cont_start)


def swish_product(gate_vals, upper_vals):
    return jax.nn.silu(gate_vals) * upper_vals


AXES = ("grp", "seq")
CONTRACT_LAST = (((1,), (1,)), ((), ()))
CONTRACT_FIRST = (((0,), (0,)), ((), ()))


MESH = pl.DeviceIdType.MESH


def remote(src, dst, send_sem, recv_sem, grp, seq):
    return pltpu.make_async_remote_copy(
        src_ref=src, dst_ref=dst, send_sem=send_sem, recv_sem=recv_sem,
        device_id=(grp, seq), device_id_type=MESH,
    )


def nearest_chip(place, order, chips):
    both = 2 * jnp.minimum(place, chips - 1 - place)
    offset = (order + 1) // 2
    near = jnp.where(order % 2 == 1, place - offset, place + offset)
    rest = jnp.where(place < chips - 1 - place, order, chips - 1 - order)
    return jnp.where(order <= both, near, rest)


def line_barrier(chips):
    grp, seq = lax.axis_index("grp"), lax.axis_index("seq")
    chip, core = seq // 2, seq % 2
    mate = seq + 1 - 2 * core
    barrier = pltpu.get_barrier_semaphore()

    def greet(other):
        pl.semaphore_signal(barrier, inc=1, device_id=(grp, other), device_id_type=MESH)

    greet(mate)
    pl.when(chip > 0)(lambda: greet(seq - 2))
    pl.when(chip < chips - 1)(lambda: greet(seq + 2))
    inner = jnp.where((chip > 0) & (chip < chips - 1), 1, 0)
    pl.semaphore_wait(barrier, 2 + inner)


class LineGather:
    def __init__(self, buf, send_sem, recv_sem, chips):
        self.buf, self.send_sem, self.recv_sem, self.chips = buf, send_sem, recv_sem, chips
        self.grp, self.seq = lax.axis_index("grp"), lax.axis_index("seq")
        self.chip, self.core = self.seq // 2, self.seq % 2
        self.mate = self.seq + 1 - 2 * self.core

    def copy(self, way, slot):
        to = (self.seq + 2, self.seq - 2, self.mate)[way]
        return remote(
            self.buf.at[slot], self.buf.at[slot], self.send_sem.at[way, slot],
            self.recv_sem.at[slot], self.grp, to,
        )

    def wait_recv(self, slot):
        self.copy(2, slot).wait_recv()

    def start(self):
        pl.when(self.chip < self.chips - 1)(lambda: self.copy(0, self.seq).start())
        pl.when(self.chip > 0)(lambda: self.copy(1, self.seq).start())
        self.copy(2, self.seq).start()

    def forward(self, step):
        @pl.when(self.chip - step >= 0)
        def _():
            slot = self.seq - 2 * step
            self.wait_recv(slot)
            pl.when(self.chip < self.chips - 1)(lambda: self.copy(0, slot).start())
            self.copy(2, slot).start()

        @pl.when(self.chip + step < self.chips)
        def _():
            slot = self.seq + 2 * step
            self.wait_recv(slot)
            pl.when(self.chip > 0)(lambda: self.copy(1, slot).start())
            self.copy(2, slot).start()

    def wait_mate(self, chip):
        self.wait_recv(2 * chip + 1 - self.core)

    def drain(self):
        for other in range(self.chips):
            slot = 2 * other + self.core
            self.copy(2, slot).wait_send()
            pl.when((other <= self.chip) & (self.chip < self.chips - 1))(
                lambda slot=slot: self.copy(0, slot).wait_send()
            )
            pl.when((other >= self.chip) & (self.chip > 0))(
                lambda slot=slot: self.copy(1, slot).wait_send()
            )


class LineScatter:
    def __init__(self, part, mate_in, left_in, right_in, send_sem, recv_sem, chips):
        self.part, self.mate_in, self.left_in, self.right_in = part, mate_in, left_in, right_in
        self.send_sem, self.recv_sem, self.chips = send_sem, recv_sem, chips
        self.grp, self.seq = lax.axis_index("grp"), lax.axis_index("seq")
        self.chip, self.core = self.seq // 2, self.seq % 2
        self.mate = self.seq + 1 - 2 * self.core

    def to_mate(self, r, chip):
        return remote(
            self.part.at[r, 2 * chip + 1 - self.core], self.mate_in.at[r, chip],
            self.send_sem.at[0, r, chip], self.recv_sem.at[0, r, chip], self.grp, self.mate,
        )

    def to_right(self, r, chip):
        return remote(
            self.part.at[r, 2 * chip + self.core], self.left_in.at[r, chip],
            self.send_sem.at[1, r, chip], self.recv_sem.at[1, r, chip], self.grp, self.seq + 2,
        )

    def to_left(self, r, chip):
        return remote(
            self.part.at[r, 2 * chip + self.core], self.right_in.at[r, chip],
            self.send_sem.at[2, r, chip], self.recv_sem.at[2, r, chip], self.grp, self.seq - 2,
        )

    def step(self, r, order):
        last = self.chips - 1
        far = last - order

        @pl.when(far > self.chip)
        def _():
            self.to_mate(r, far).wait_recv()
            slot = 2 * far + self.core
            total = self.part[r, slot].astype(jnp.float32) + self.mate_in[r, far].astype(jnp.float32)

            @pl.when(self.chip > 0)
            def _():
                self.to_right(r, far).wait_recv()
                self.part[r, slot] = (total + self.left_in[r, far].astype(jnp.float32)).astype(jnp.bfloat16)

            @pl.when(self.chip == 0)
            def _():
                self.part[r, slot] = total.astype(jnp.bfloat16)

            self.to_right(r, far).start()

        @pl.when(order < self.chip)
        def _():
            self.to_mate(r, order).wait_recv()
            slot = 2 * order + self.core
            total = self.part[r, slot].astype(jnp.float32) + self.mate_in[r, order].astype(jnp.float32)

            @pl.when(self.chip < last)
            def _():
                self.to_left(r, order).wait_recv()
                self.part[r, slot] = (total + self.right_in[r, order].astype(jnp.float32)).astype(jnp.bfloat16)

            @pl.when(self.chip == last)
            def _():
                self.part[r, slot] = total.astype(jnp.bfloat16)

            self.to_left(r, order).start()

    def finish(self, r, out_ref):
        self.to_mate(r, self.chip).wait_recv()
        out_ref[...] = self.part[r, self.seq].astype(jnp.float32) + self.mate_in[r, self.chip].astype(jnp.float32)

        @pl.when(self.chip > 0)
        def _():
            self.to_right(r, self.chip).wait_recv()
            out_ref[...] += self.left_in[r, self.chip].astype(jnp.float32)

        @pl.when(self.chip < self.chips - 1)
        def _():
            self.to_left(r, self.chip).wait_recv()
            out_ref[...] += self.right_in[r, self.chip].astype(jnp.float32)

    def drain(self, r):
        for other in range(self.chips):
            self.to_mate(r, other).wait_send()
            pl.when(other > self.chip)(lambda other=other: self.to_right(r, other).wait_send())
            pl.when(other < self.chip)(lambda other=other: self.to_left(r, other).wait_send())


def mlp_kernel(chips, grps, row_tiles, n2_ref, cot_ref, *refs):
    w_refs, refs = refs[:grps], refs[grps:]
    (
        n2g_ref, outp_ref, grads_ref, tok, w, acts, part, mate_in, left_in, right_in, stage,
        lsem, gsend, grecv, ssend, srecv, wsem, osem,
    ) = refs
    seq = lax.axis_index("seq")
    chip, core = seq // 2, seq % 2
    shard, width = n2_ref.shape
    units = w.shape[1]
    block = units // grps
    tile = units // row_tiles
    own = pltpu.make_async_copy(n2_ref, tok.at[0, seq], lsem.at[0])
    own.start()
    cot_copy = pltpu.make_async_copy(cot_ref, tok.at[1], lsem.at[1])
    cot_copy.start()

    def w_copy(j, b):
        return pltpu.make_async_copy(w_refs[b].at[j], w.at[j, pl.ds(b * block, block)], wsem.at[j, b])

    for j in range(3):
        for b in range(grps):
            w_copy(j, b).start()
    line_barrier(chips)
    gather = LineGather(tok.at[0], gsend, grecv, chips)
    scatter = LineScatter(part, mate_in, left_in, right_in, ssend, srecv, chips)
    own.wait()
    gather.start()

    @pl.loop(0, chips)
    def _(order):
        @pl.when(order == 0)
        def _():
            cot_copy.wait()
            for j in range(3):
                for b in range(grps):
                    w_copy(j, b).wait()

        pl.when(order > 0)(lambda: gather.forward(order))
        at = nearest_chip(chip, order, chips)
        gather.wait_mate(at)
        x = tok[0, pl.ds(2 * at, 2)].reshape(2 * shard, width)
        y = tok[1, pl.ds(2 * at, 2)].reshape(2 * shard, width)
        gate = lax.dot_general(x, w[0], CONTRACT_LAST, preferred_element_type=jnp.float32)
        up = lax.dot_general(x, w[1], CONTRACT_LAST, preferred_element_type=jnp.float32)
        unit_grad = lax.dot_general(y, w[2], CONTRACT_LAST, preferred_element_type=jnp.float32)
        sig = 1.0 / (1.0 + jnp.exp(-gate))
        silu = gate * sig
        rows = pl.ds(at * (2 * shard), 2 * shard)
        gate_grad = (unit_grad * up * sig * (1.0 + gate * (1.0 - sig))).astype(jnp.bfloat16)
        up_grad = (unit_grad * silu).astype(jnp.bfloat16)
        acts[0, rows] = gate_grad
        acts[1, rows] = up_grad
        acts[2, rows] = (silu * up).astype(jnp.bfloat16)
        back = jnp.dot(gate_grad, w[0], preferred_element_type=jnp.float32) + jnp.dot(
            up_grad, w[1], preferred_element_type=jnp.float32
        )
        part[0, pl.ds(2 * at, 2)] = back.astype(jnp.bfloat16).reshape(2, shard, width)
        scatter.to_mate(0, at).start()

    def out_copy(t):
        return pltpu.make_async_copy(
            stage.at[t % 2],
            grads_ref.at[t // row_tiles, pl.ds((t % row_tiles) * tile, tile)],
            osem.at[t % 2],
        )

    @pl.loop(0, 3 * row_tiles)
    def _(t):
        @pl.when(t < 2 * chips)
        def _():
            scatter.step(t // chips, t % chips)

        @pl.when(t < chips)
        def _():
            h = acts[2, pl.ds(t * (2 * shard), 2 * shard)]
            part[1, pl.ds(2 * t, 2)] = (
                jnp.dot(h, w[2], preferred_element_type=jnp.float32)
                .astype(jnp.bfloat16).reshape(2, shard, width)
            )
            scatter.to_mate(1, t).start()

        @pl.when(t >= 2)
        def _():
            out_copy(t - 2).wait()

        kind = t // row_tiles
        lhs = acts[kind, :, pl.ds(pl.multiple_of((t % row_tiles) * tile, 128), tile)]
        rhs = tok[kind // 2].reshape(2 * chips * shard, width)
        stage[t % 2] = lax.dot_general(
            lhs, rhs, CONTRACT_FIRST, preferred_element_type=jnp.float32
        ).astype(jnp.bfloat16)
        out_copy(t).start()

    scatter.finish(0, n2g_ref)
    scatter.finish(1, outp_ref)
    out_copy(3 * row_tiles - 2).wait()
    out_copy(3 * row_tiles - 1).wait()
    gather.drain()
    scatter.drain(0)
    scatter.drain(1)


def mlp_call(n2, cot_all, w_blocks, row_tiles=3):
    grps, (_, block, width) = len(w_blocks), w_blocks[0].shape
    slots, shard, _ = cot_all.shape
    chips = slots // 2
    units = grps * block
    vm, anyspace = pltpu.VMEM, pl.BlockSpec(memory_space=pl.ANY)
    vspec = pl.BlockSpec(memory_space=pltpu.VMEM)
    dma = pltpu.SemaphoreType.DMA
    flops = 2 * 9 * slots * shard * units * width
    return pl.pallas_call(
        functools.partial(mlp_kernel, chips, grps, row_tiles),
        out_shape=(
            jax.ShapeDtypeStruct((shard, width), jnp.float32),
            jax.ShapeDtypeStruct((shard, width), jnp.float32),
            jax.ShapeDtypeStruct((3, units, width), jnp.bfloat16),
        ),
        in_specs=[vspec, anyspace] + [anyspace] * grps,
        out_specs=(vspec, vspec, anyspace),
        scratch_shapes=[
            vm((2, slots, shard, width), jnp.bfloat16),
            vm((3, units, width), jnp.bfloat16),
            vm((3, slots * shard, units), jnp.bfloat16),
            vm((2, slots, shard, width), jnp.bfloat16),
            vm((2, chips, shard, width), jnp.bfloat16),
            vm((2, chips, shard, width), jnp.bfloat16),
            vm((2, chips, shard, width), jnp.bfloat16),
            vm((2, units // row_tiles, width), jnp.bfloat16),
            dma((2,)), dma((3, slots)), dma((slots,)), dma((3, 2, chips)), dma((3, 2, chips)),
            dma((3, grps)), dma((2,)),
        ],
        compiler_params=pltpu.CompilerParams(
            collective_id=1, has_side_effects=True, vmem_limit_bytes=62 * 2**20
        ),
        cost_estimate=pl.CostEstimate(flops=flops, bytes_accessed=30 * 2**20, transcendentals=0),
        name="mlp",
    )(n2, cot_all, *w_blocks)


class Place:
    def __init__(self, chips):
        self.chips = chips
        self.grp, self.seq = lax.axis_index("grp"), lax.axis_index("seq")
        self.chip, self.core = self.seq // 2, self.seq % 2
        self.mate = self.seq + 1 - 2 * self.core

    def peer(self, offset):
        low, high = self.grp % 2, self.grp // 2
        low = 1 - low if offset % 2 else low
        high = 1 - high if offset // 2 else high
        return 2 * high + low

    def barrier(self, grps):
        barrier = pltpu.get_barrier_semaphore()
        for chip in range(self.chips):
            @pl.when(chip != self.chip)
            def _(chip=chip):
                pl.semaphore_signal(
                    barrier, inc=1, device_id=(self.grp, 2 * chip + self.core), device_id_type=MESH
                )
        pl.semaphore_signal(barrier, inc=1, device_id=(self.grp, self.mate), device_id_type=MESH)
        for offset in range(1, grps):
            pl.semaphore_signal(
                barrier, inc=1, device_id=(self.peer(offset), self.seq), device_id_type=MESH
            )
        pl.semaphore_wait(barrier, self.chips - 1 + 1 + grps - 1)


class RailGather:
    def __init__(self, place, view, send_sem, recv_sem):
        self.place, self.view, self.send_sem, self.recv_sem = place, view, send_sem, recv_sem

    def copy(self, way, chip, core):
        p = self.place
        to = (p.seq + 2, p.seq - 2, p.mate)[way]
        return remote(
            self.view(chip, core), self.view(chip, core), self.send_sem.at[way, chip],
            self.recv_sem.at[chip, core], p.grp, to,
        )

    def start(self):
        p = self.place
        pl.when(p.chip < p.chips - 1)(lambda: self.copy(0, p.chip, p.core).start())
        pl.when(p.chip > 0)(lambda: self.copy(1, p.chip, p.core).start())
        self.copy(2, p.chip, p.core).start()

    def forward(self, step):
        p = self.place

        @pl.when(p.chip - step >= 0)
        def _():
            chip = p.chip - step
            self.copy(2, chip, p.core).wait_recv()
            pl.when(p.chip < p.chips - 1)(lambda: self.copy(0, chip, p.core).start())
            self.copy(2, chip, p.core).start()

        @pl.when(p.chip + step < p.chips)
        def _():
            chip = p.chip + step
            self.copy(2, chip, p.core).wait_recv()
            pl.when(p.chip > 0)(lambda: self.copy(1, chip, p.core).start())
            self.copy(2, chip, p.core).start()

    def wait_mate(self, chip):
        self.copy(2, chip, 1 - self.place.core).wait_recv()

    def drain(self):
        p = self.place
        for chip in range(p.chips):
            self.copy(2, chip, p.core).wait_send()
            pl.when((chip <= p.chip) & (p.chip < p.chips - 1))(
                lambda chip=chip: self.copy(0, chip, p.core).wait_send()
            )
            pl.when((chip >= p.chip) & (p.chip > 0))(
                lambda chip=chip: self.copy(1, chip, p.core).wait_send()
            )


def front_kernel(chips, scale,
                 n1_ref, cot_ref, wq_ref, bias_ref, wo_ref, wm_ref, cos_ref, sin_ref, mask_ref,
                 attn_ref, lse_ref, q_out_ref, kv_out_ref, n1_all_ref, cot_all_ref, wo_all_ref, wq_all_ref,
                 wm1_ref, wm2_ref, wm3_ref,
                 nbuf, wq, bias, stage, qbuf, kvbuf,
                 lsem, n_send, n_recv, c_send, c_recv, o_send, o_recv, ox_send, ox_recv, om_send, om_recv,
                 wq_send, wq_recv, b_send, b_recv, m_send, m_recv, q_send, q_recv, k_send, k_recv):
    p = Place(chips)
    grps = 4
    half = wq_ref.shape[0]
    rows = pl.ds(p.core * half, half)
    mates_rows = pl.ds((1 - p.core) * half, half)
    wm_refs = (wm_ref, wm1_ref, wm2_ref, wm3_ref)
    part = wm_ref.shape[1] // 2

    own = [
        pltpu.make_async_copy(n1_ref, nbuf.at[p.chip, p.core], lsem.at[0]),
        pltpu.make_async_copy(wq_ref, wq.at[0, rows], lsem.at[1]),
        pltpu.make_async_copy(bias_ref, bias.at[0, p.core], lsem.at[2]),
        pltpu.make_async_copy(wo_ref, wo_all_ref.at[p.grp, p.chip, p.core], lsem.at[3]),
        pltpu.make_async_copy(cot_ref, cot_all_ref.at[p.chip, p.core], lsem.at[4]),
    ]
    for copy in own:
        copy.start()
    p.barrier(grps)

    n1_line = RailGather(p, lambda chip, core: nbuf.at[chip, core], n_send, n_recv)
    cot_line = RailGather(p, lambda chip, core: cot_all_ref.at[chip, core], c_send, c_recv)
    out_line = RailGather(p, lambda chip, core: wo_all_ref.at[p.grp, chip, core], o_send, o_recv)

    def wq_direct(b):
        return remote(wq_ref, wq.at[b, rows], wq_send.at[0, b], wq_recv.at[b, 0], p.peer(b), p.seq)

    def wq_mate(b):
        return remote(wq.at[b, rows], wq.at[b, rows], wq_send.at[1, b], wq_recv.at[b, 1], p.grp, p.mate)

    def bias_direct(b):
        return remote(bias_ref, bias.at[b, p.core], b_send.at[0, b], b_recv.at[b, 0], p.peer(b), p.seq)

    def bias_mate(b):
        return remote(bias.at[b, p.core], bias.at[b, p.core], b_send.at[1, b], b_recv.at[b, 1], p.grp, p.mate)

    def m_half(ref, i):
        return ref.at[:, pl.ds(i * part, part)]

    def m_direct(b, i):
        return remote(m_half(wm_ref, i), m_half(wm_refs[b], i), m_send.at[b, i], m_recv.at[b, i], p.peer(b), p.seq)

    def m_forward(b):
        return remote(
            m_half(wm_refs[b], b - 1), m_half(wm3_ref, b - 1), m_send.at[3, b - 1], m_recv.at[3, b - 1],
            p.peer(3 - b), p.seq,
        )

    def out_cross(b):
        view = lambda grp: wo_all_ref.at[grp, :, p.core]
        return remote(view(p.grp), view(p.grp), ox_send.at[b], ox_recv.at[b], p.peer(b), p.seq)

    def out_mate(b):
        view = wo_all_ref.at[p.peer(b), :, p.core]
        return remote(view, view, om_send.at[b], om_recv.at[b], p.grp, p.mate)

    def q_copy(chip):
        return remote(
            stage.at[chip, pl.ds(0, 3)], qbuf.at[p.chip], q_send.at[chip], q_recv.at[p.chip],
            p.grp, 2 * chip + p.core,
        )

    def q_arrival(chip):
        return remote(stage.at[chip, pl.ds(0, 3)], qbuf.at[chip], q_send.at[chip], q_recv.at[chip], p.grp, p.mate)

    def k_copy(chip, to_chip):
        return remote(
            stage.at[chip, 3], kvbuf.at[p.chip, p.core, chip], k_send.at[0, chip, to_chip],
            k_recv.at[p.chip, p.core, chip], p.grp, 2 * to_chip + p.core,
        )

    def k_mate(head, chip, src=None):
        view = kvbuf.at[head, p.core, chip]
        return remote(
            view if src is None else src, view, k_send.at[1, head, chip],
            k_recv.at[head, p.core, chip], p.grp, p.mate,
        )

    def k_arrival(head, core, chip):
        view = kvbuf.at[head, core, chip]
        return remote(view, view, k_send.at[1, head, chip], k_recv.at[head, core, chip], p.grp, p.mate)

    own[1].wait()
    own[2].wait()
    for b in range(1, grps):
        wq_direct(b).start()
        bias_direct(b).start()
    wq_mate(0).start()
    bias_mate(0).start()
    own[0].wait()
    n1_line.start()
    own[3].wait()
    out_line.start()
    for b in range(1, grps):
        wq_direct(b).wait_recv()
        wq_mate(b).start()
        bias_direct(b).wait_recv()
        bias_mate(b).start()
    m_direct(1, 0).start()
    m_direct(2, 1).start()
    for b in range(grps):
        wq_mate(b).wait_recv()
        bias_mate(b).wait_recv()

    @pl.loop(0, chips)
    def _(order):
        @pl.when(order > 0)
        def _():
            n1_line.forward(order)
            out_line.forward(order)

        at = nearest_chip(p.chip, order, chips)
        x = nbuf[at, p.core]
        weights = wq[...].reshape(grps * 2 * half, x.shape[1])
        rows_all = lax.dot_general(x, weights, CONTRACT_LAST, preferred_element_type=jnp.float32)
        cosine, sine = cos_ref[at, p.core], sin_ref[at, p.core]
        for b in range(grps):
            u = rows_all[:, 2 * half * b : 2 * half * (b + 1)] + (bias[b, 0, 0:1] + bias[b, 1, 0:1])
            turned = u * cosine + pltpu.roll(u, half, 1) * sine
            place = p.peer(b)
            keep = jnp.where((place == grps - 1) & (p.chip >= chips // 2), 1.0, 0.0)
            value = (u * keep + turned * (1.0 - keep)).astype(jnp.bfloat16)
            stage[at, place] = value

            @pl.when(place == grps - 1)
            def _(value=value):
                kvbuf[p.chip, p.core, at] = value

            @pl.when((place < grps - 1) & (at == p.chip))
            def _(value=value, place=place):
                qbuf[p.chip, place] = value

        pl.when(at != p.chip)(lambda: q_copy(at).start())
        for to_chip in range(chips):
            pl.when(to_chip != p.chip)(lambda to_chip=to_chip: k_copy(at, to_chip).start())
        k_mate(p.chip, at, stage.at[at, 3]).start()

    for b in range(1, grps):
        out_cross(b).start()
    own[4].wait()
    cot_line.start()

    @pl.loop(0, chips)
    def _(order):
        for head in range(chips):
            @pl.when(head != p.chip)
            def _(head=head):
                chip = nearest_chip(head, order, chips)
                k_arrival(head, p.core, chip).wait_recv()
                k_mate(head, chip).start()

    for chip in range(chips):
        pl.when(chip != p.chip)(lambda chip=chip: q_arrival(chip).wait_recv())
        for head in range(chips):
            k_arrival(head, 1 - p.core, chip).wait_recv()
    for b in (1, 2):
        m_direct(b, b - 1).wait_recv()
        m_forward(b).start()
    cot_line.forward(1)

    mask = mask_ref[...]
    shard = mask.shape[0]
    heads_per = H // KVH
    for kv in range(KVH):
        heads = [kv * heads_per + i for i in range(heads_per)]
        queries = jnp.concatenate([qbuf[h % chips, h // chips] for h in heads], axis=0)
        keys = kvbuf[kv].reshape(mask.shape[1], 2 * half)
        values = kvbuf[KVH + kv].reshape(mask.shape[1], 2 * half)
        scores = lax.dot_general(queries, keys, CONTRACT_LAST, preferred_element_type=jnp.float32) * scale
        scores = scores.reshape(heads_per, shard, mask.shape[1]) + mask[None]
        top = jnp.max(scores, axis=-1, keepdims=True)
        weights = jnp.exp(scores - top)
        total = jnp.sum(weights, axis=-1, keepdims=True)
        probs = (weights / total).astype(jnp.bfloat16).reshape(heads_per * shard, mask.shape[1])
        mixed = jnp.dot(probs, values, preferred_element_type=jnp.float32)
        log_total = (top + jnp.log(total)).reshape(heads_per * shard, 1)
        lse_ref[kv] = jnp.broadcast_to(log_total, (heads_per * shard, 2 * half))
        for i, h in enumerate(heads):
            attn_ref[:, h * 2 * half : (h + 1) * 2 * half] = mixed[i * shard : (i + 1) * shard]
        cot_line.forward(kv + 2)

    for b in range(1, grps):
        out_cross(b).wait_recv()
        out_mate(b).start()
    m_direct(1, 1).start()
    m_direct(2, 0).start()
    outs = [
        pltpu.make_async_copy(nbuf, n1_all_ref, lsem.at[5]),
        pltpu.make_async_copy(wq, wq_all_ref, lsem.at[6]),
        pltpu.make_async_copy(qbuf, q_out_ref, lsem.at[7]),
        pltpu.make_async_copy(kvbuf, kv_out_ref, lsem.at[8]),
    ]
    for chip in range(chips):
        n1_line.wait_mate(chip)
        out_line.wait_mate(chip)
        cot_line.wait_mate(chip)
    for copy in outs:
        copy.start()
    for b in (1, 2):
        m_direct(b, 2 - b).wait_recv()
        m_forward(3 - b).wait_recv()
    for b in range(1, grps):
        om = remote(
            wo_all_ref.at[p.peer(b), :, 1 - p.core], wo_all_ref.at[p.peer(b), :, 1 - p.core],
            om_send.at[b], om_recv.at[b], p.grp, p.mate,
        )
        om.wait_recv()
    for copy in outs:
        copy.wait()
    n1_line.drain()
    out_line.drain()
    cot_line.drain()
    for b in range(grps):
        wq_mate(b).wait_send()
        bias_mate(b).wait_send()
    for b in range(1, grps):
        wq_direct(b).wait_send()
        bias_direct(b).wait_send()
        out_cross(b).wait_send()
        out_mate(b).wait_send()
    for b in (1, 2):
        m_direct(b, 0).wait_send()
        m_direct(b, 1).wait_send()
        m_forward(b).wait_send()
    for chip in range(chips):
        pl.when(chip != p.chip)(lambda chip=chip: q_copy(chip).wait_send())
        for other in range(chips):
            pl.when(other != p.chip)(lambda chip=chip, other=other: k_copy(chip, other).wait_send())
            k_mate(other, chip).wait_send()


def front_call(n1, cot, qkv_weight, bias_rows, out_weight, mlp_rows, cosine, sine, mask):
    chips = cosine.shape[0]
    grps = 4
    shard, width = n1.shape
    half = qkv_weight.shape[0]
    vm, dma = pltpu.VMEM, pltpu.SemaphoreType.DMA
    anyspace = pl.BlockSpec(memory_space=pl.ANY)
    vspec = pl.BlockSpec(memory_space=pltpu.VMEM)
    low, wide = jnp.bfloat16, jnp.float32
    struct = jax.ShapeDtypeStruct
    return pl.pallas_call(
        functools.partial(front_kernel, chips, 1.0 / math.sqrt(HD)),
        out_shape=(
            struct((shard, H * HD), wide),
            struct((KVH, H // KVH * shard, HD), wide),
            struct((chips, 3, shard, HD), low),
            struct((chips, 2, chips, shard, HD), low),
            struct((chips, 2, shard, width), low),
            struct((chips, 2, shard, width), low),
            struct((grps, chips, 2) + out_weight.shape, low),
            struct((grps, 2 * half, width), low),
        ) + (struct(mlp_rows.shape, low),) * 3,
        in_specs=[anyspace] * 6 + [vspec] * 3,
        out_specs=(vspec,) * 2 + (anyspace,) * 9,
        scratch_shapes=[
            vm((chips, 2, shard, width), low),
            vm((grps, 2 * half, width), low),
            vm((grps, 2) + bias_rows.shape, wide),
            vm((chips, grps, shard, HD), low),
            vm((chips, 3, shard, HD), low),
            vm((chips, 2, chips, shard, HD), low),
            dma((9,)),
            dma((3, chips)), dma((chips, 2)),
            dma((3, chips)), dma((chips, 2)),
            dma((3, chips)), dma((chips, 2)),
            dma((grps,)), dma((grps,)), dma((grps,)), dma((grps,)),
            dma((2, grps)), dma((grps, 2)),
            dma((2, grps)), dma((grps, 2)),
            dma((grps, 2)), dma((grps, 2)),
            dma((chips,)), dma((chips,)),
            dma((2, chips, chips)), dma((chips, 2, chips)),
        ],
        compiler_params=pltpu.CompilerParams(
            collective_id=2, has_side_effects=True, vmem_limit_bytes=56 * 2**20
        ),
        name="front",
    )(n1, cot, qkv_weight, bias_rows, out_weight, mlp_rows, cosine, sine, mask)


def columns_to_owners(rows, row_unit):
    grp_count, seq_count = lax.axis_size("grp"), lax.axis_size("seq")
    tok_rows = rows.shape[0]
    split = rows.reshape(tok_rows, grp_count, seq_count, row_unit).transpose(2, 0, 1, 3)
    split = split.reshape(seq_count * tok_rows, grp_count * row_unit)
    return lax.all_to_all(split, "seq", split_axis=0, concat_axis=0, tiled=True)


def owners_to_columns(rows, row_unit):
    grp_count, seq_count = lax.axis_size("grp"), lax.axis_size("seq")
    tok_rows = rows.shape[0] // seq_count
    moved = lax.all_to_all(rows, "seq", split_axis=0, concat_axis=0, tiled=True)
    moved = moved.reshape(seq_count, tok_rows, grp_count, row_unit).transpose(1, 2, 0, 3)
    return moved.reshape(tok_rows, grp_count * seq_count * row_unit)


def plain_mlp(normed_two, cotangent_all, mlp_weight):
    contract_last, contract_first = CONTRACT_LAST, CONTRACT_FIRST
    mlp_rows = lax.all_gather(mlp_weight, "grp", axis=0, tiled=True)
    normed_two_all = lax.all_gather(normed_two, "seq", axis=0, tiled=True)
    gate_rows, upper_rows, down_rows = mlp_rows[:, 0, :], mlp_rows[:, 1, :], mlp_rows[:, 2, :]
    gate_vals = lax.dot_general(
        normed_two_all, gate_rows, contract_last, preferred_element_type=jnp.float32
    )
    upper_vals = lax.dot_general(
        normed_two_all, upper_rows, contract_last, preferred_element_type=jnp.float32
    )
    unit_wide, pull_back = jax.vjp(swish_product, gate_vals, upper_vals)
    unit_low = unit_wide.astype(jnp.bfloat16)
    unit_grad = lax.dot_general(
        cotangent_all, down_rows, contract_last, preferred_element_type=jnp.float32
    )
    gate_grad, upper_grad = pull_back(unit_grad)
    gate_grad = gate_grad.astype(jnp.bfloat16)
    upper_grad = upper_grad.astype(jnp.bfloat16)
    input_grad = jnp.dot(gate_grad, gate_rows, preferred_element_type=jnp.float32) + jnp.dot(
        upper_grad, upper_rows, preferred_element_type=jnp.float32
    )
    grad_part = lax.psum_scatter(
        input_grad.astype(jnp.bfloat16), "seq", scatter_dimension=0, tiled=True
    ).astype(jnp.float32)
    out_part = lax.psum_scatter(
        jnp.dot(unit_low, down_rows, preferred_element_type=jnp.float32).astype(jnp.bfloat16),
        "seq",
        scatter_dimension=0,
        tiled=True,
    ).astype(jnp.float32)
    mlp_terms = jnp.stack(
        [
            lax.dot_general(
                gate_grad, normed_two_all, contract_first, preferred_element_type=jnp.float32
            ),
            lax.dot_general(
                upper_grad, normed_two_all, contract_first, preferred_element_type=jnp.float32
            ),
            lax.dot_general(
                unit_low, cotangent_all, contract_first, preferred_element_type=jnp.float32
            ),
        ],
        axis=1,
    )
    mlp_grad = lax.psum_scatter(mlp_terms, "grp", scatter_dimension=0, tiled=True)
    return grad_part, out_part, mlp_grad


def padded_rows(mlp_weight):
    rows = mlp_weight.transpose(1, 0, 2)
    return jnp.pad(rows, ((0, 0), (0, -rows.shape[1] % 32), (0, 0)))


def from_peer(values, offset, grp_count):
    return lax.ppermute(values, "grp", [(g, g ^ offset) for g in range(grp_count)])


def exchange_blocks(rows, grp_count):
    return [rows] + [from_peer(rows, offset, grp_count) for offset in range(1, grp_count)]


def sum_blocks(terms, grp_count):
    block = terms.shape[1] // grp_count
    total = terms[:, :block].astype(jnp.float32)
    for offset in range(1, grp_count):
        piece = terms[:, offset * block : (offset + 1) * block]
        total = total + from_peer(piece, offset, grp_count).astype(jnp.float32)
    return total


def per_device(
    tokens,
    cotangent,
    shard_segment,
    gain_attn,
    qkv_weight,
    qkv_bias,
    out_weight,
    gain_mlp,
    mlp_weight,
):
    tok_rows = tokens.shape[0]
    seq_count = lax.axis_size("seq")
    grp_count = lax.axis_size("grp")
    group_tok = tok_rows * seq_count
    heads_per = H // KVH
    kv_width = KVH * HD
    att_width = H * HD
    query_rows = heads_per * tok_rows
    score_scale = 1.0 / math.sqrt(HD)
    contract_last = CONTRACT_LAST
    contract_first = CONTRACT_FIRST
    seq_place = lax.axis_index("seq")
    grp_place = lax.axis_index("grp")
    segments = lax.dynamic_index_in_dim(shard_segment, grp_place, 0, keepdims=False)
    starts = shard_starts(segments, tok_rows, group_tok // 2)
    shard_order = jnp.arange(seq_count, dtype=jnp.int32)
    own_seg = jnp.sum(jnp.where(shard_order == seq_place, segments, 0))
    own_start = jnp.sum(jnp.where(shard_order == seq_place, starts, 0))
    positions = own_start + jnp.arange(tok_rows, dtype=jnp.int32)
    cosine_table, sine_table = rotary_tables(positions, HD)
    query_pos = jnp.tile(positions, heads_per)
    tokens_wide = tokens.astype(jnp.float32)
    gain_one = gain_attn.astype(jnp.float32)
    gain_two = gain_mlp.astype(jnp.float32)
    normed_one = rms_scale(tokens_wide, gain_one).astype(jnp.bfloat16)
    use_kernels = (seq_count, grp_count, H, KVH, HD) == (8, 4, 12, 2, 128)
    if use_kernels:
        chips = seq_count // 2
        lanes = jnp.arange(HD)
        all_pos = (starts[:, None] + jnp.arange(tok_rows, dtype=jnp.int32)[None, :]).reshape(-1)
        all_cosine, all_sine = rotary_tables(all_pos, HD)
        all_sine = jnp.where(lanes < HD // 2, -all_sine, all_sine)
        by_shard = lambda table: table.reshape(chips, 2, tok_rows, HD)
        key_pos = all_pos.reshape(chips, 2, tok_rows).swapaxes(0, 1).reshape(-1)
        key_seg = jnp.repeat(segments.reshape(chips, 2).swapaxes(0, 1).reshape(-1), tok_rows)
        visible = ((key_seg == 0) | (key_seg == own_seg))[None, :] & (
            key_pos[None, :] <= positions[:, None]
        )
        mask = jnp.where(visible, 0.0, -1e30).astype(jnp.float32)
        bias_half = qkv_bias.astype(jnp.float32)
        bias_pair = jnp.concatenate([bias_half, jnp.zeros_like(bias_half)])
        bias_row = jnp.where(seq_place % 2 == 0, bias_pair, jnp.roll(bias_pair, HD // 2))
        bias_rows8 = jnp.broadcast_to(bias_row[None, :], (8, HD))
        own_rows = padded_rows(mlp_weight)
        (
            attn_wide, lse, q_heads, kv_heads, n1_all, cot_all, out_all, qkv_all, *peer_rows
        ) = front_call(
            normed_one, cotangent, qkv_weight, bias_rows8, out_weight, own_rows,
            by_shard(all_cosine), by_shard(all_sine), mask,
        )
        mlp_blocks = [own_rows, *peer_rows]
        normed_one_all = n1_all.reshape(group_tok, -1)
        cotangent_all = cot_all.reshape(group_tok, -1)
        out_full = out_all.reshape(att_width, -1)
        qkv_rows = lax.all_gather(qkv_weight, "grp", axis=0, tiled=True)
        query_rot = q_heads.transpose(2, 1, 0, 3).reshape(tok_rows, H, HD)
        kv_rows = kv_heads.reshape(2, KVH, 2, chips, tok_rows, HD).transpose(0, 3, 2, 4, 1, 5)
        keys_all, values_all = kv_rows.reshape(2, group_tok, kv_width)
    else:
        normed_one_all = lax.all_gather(normed_one, "seq", axis=0, tiled=True)
        qkv_rows = lax.all_gather(qkv_weight, "grp", axis=0, tiled=True)
        bias_rows = lax.all_gather(qkv_bias, "grp", axis=0, tiled=True)
        cotangent_all = lax.all_gather(cotangent, "seq", axis=0, tiled=True)
        out_full = lax.all_gather(out_weight, AXES, axis=0, tiled=True)
        projected = lax.dot_general(
            normed_one_all, qkv_rows, contract_last, preferred_element_type=jnp.float32
        )
        projected = (projected + bias_rows.astype(jnp.float32)[None, :]).astype(jnp.bfloat16)
        projected = owners_to_columns(projected, qkv_weight.shape[0]).astype(jnp.float32)
        query_rot = rotate(
            projected[:, :att_width].reshape(tok_rows, H, HD), cosine_table, sine_table
        ).astype(jnp.bfloat16)
        key_rot = rotate(
            projected[:, att_width : att_width + kv_width].reshape(tok_rows, KVH, HD),
            cosine_table,
            sine_table,
        ).astype(jnp.bfloat16)
        value_low = projected[:, att_width + kv_width :].astype(jnp.bfloat16)
        keys_all, values_all = (
            lax.all_gather(key_rot.reshape(tok_rows, kv_width), "seq", axis=0, tiled=True),
            lax.all_gather(value_low, "seq", axis=0, tiled=True),
        )
    queries = (
        query_rot.reshape(tok_rows, KVH, heads_per, HD)
        .transpose(1, 2, 0, 3)
        .reshape(KVH, query_rows, HD)
    )
    key_block = min(512, group_tok)
    block_count = group_tok // key_block
    block_order = jnp.arange(block_count, dtype=jnp.int32)

    def block_mask(block_index):
        key_index = block_index * key_block + jnp.arange(key_block, dtype=jnp.int32)
        key_shard = key_index // tok_rows
        onehot = key_shard[:, None] == shard_order[None, :]
        key_seg = jnp.sum(jnp.where(onehot, segments[None, :], 0), axis=1)
        key_pos = jnp.sum(jnp.where(onehot, starts[None, :], 0), axis=1) + key_index % tok_rows
        visible = (key_seg == 0) | (key_seg == own_seg)
        return visible[None, :] & (key_pos[None, :] <= query_pos[:, None])

    def block_keys(block_index):
        key_part = lax.dynamic_slice_in_dim(
            keys_all, block_index * key_block, key_block, 0
        ).reshape(key_block, KVH, HD)
        value_part = lax.dynamic_slice_in_dim(
            values_all, block_index * key_block, key_block, 0
        ).reshape(key_block, KVH, HD)
        return (key_part, value_part)

    def block_scores(key_part):
        return (
            jnp.einsum("krd,jkd->krj", queries, key_part, preferred_element_type=jnp.float32)
            * score_scale
        )

    if use_kernels:
        log_total = lse[:, :, 0]
    else:
        def stat_step(stats_now, block_index):
            allowed = block_mask(block_index)

            def stat_visit(current):
                top_old, total_old = current
                key_part, value_part = block_keys(block_index)
                scores = jnp.where(allowed[None], block_scores(key_part), -1e30)
                top_new = jnp.maximum(top_old, jnp.max(scores, axis=-1))
                weights = jnp.where(allowed[None], jnp.exp(scores - top_new[..., None]), 0.0)
                return (top_new, total_old * jnp.exp(top_old - top_new) + jnp.sum(weights, axis=-1))

            return (lax.cond(jnp.any(allowed), stat_visit, lambda current: current, stats_now), None)

        start_stats = (
            jnp.full((KVH, query_rows), -1e30, jnp.float32),
            jnp.zeros((KVH, query_rows), jnp.float32),
        )
        (top_all, total_all), unused = lax.scan(stat_step, start_stats, block_order)
        log_total = top_all + jnp.log(total_all)

        def mix_step(mixed_sum, block_index):
            allowed = block_mask(block_index)

            def mix_visit(current):
                key_part, value_part = block_keys(block_index)
                prob_low = jnp.where(
                    allowed[None], jnp.exp(block_scores(key_part) - log_total[..., None]), 0.0
                ).astype(jnp.bfloat16)
                return current + jnp.einsum(
                    "krj,jkd->krd", prob_low, value_part, preferred_element_type=jnp.float32
                )

            return (lax.cond(jnp.any(allowed), mix_visit, lambda current: current, mixed_sum), None)

        mixed_sum, unused = lax.scan(
            mix_step, jnp.zeros((KVH, query_rows, HD), jnp.float32), block_order
        )
        attn_wide = (
            mixed_sum.reshape(KVH, heads_per, tok_rows, HD)
            .transpose(2, 0, 1, 3)
            .reshape(tok_rows, att_width)
        )
    attn_low = attn_wide.astype(jnp.bfloat16)
    attn_proj = jnp.dot(attn_low, out_full, preferred_element_type=jnp.float32)
    state = tokens_wide + attn_proj
    normed_two = rms_scale(state, gain_two).astype(jnp.bfloat16)
    if use_kernels:
        grad_part, out_part, mlp_terms = mlp_call(
            normed_two, cotangent_all.reshape(seq_count, tok_rows, -1), mlp_blocks
        )
        mlp_grad = sum_blocks(mlp_terms, grp_count)[:, : mlp_weight.shape[0]].transpose(1, 0, 2)
    else:
        grad_part, out_part, mlp_grad = plain_mlp(normed_two, cotangent_all, mlp_weight)
    output = (state + out_part).astype(jnp.bfloat16)
    unused_state, norm_two_back = jax.vjp(rms_scale, state, gain_two)
    state_norm_grad, gain_two_grad = norm_two_back(grad_part)
    state_grad = state_norm_grad + cotangent.astype(jnp.float32)
    state_low = state_grad.astype(jnp.bfloat16)
    attn_grad = lax.dot_general(
        state_low, out_full, contract_last, preferred_element_type=jnp.float32
    )
    attn_grad_low = attn_grad.astype(jnp.bfloat16)
    attn_owned = columns_to_owners(attn_low, out_weight.shape[0])
    state_low_all = lax.all_gather(state_low, "seq", axis=0, tiled=True)
    out_grad = lax.psum_scatter(
        lax.dot_general(
            attn_owned, state_low_all, contract_first, preferred_element_type=jnp.float32
        ),
        "grp",
        scatter_dimension=0,
        tiled=True,
    )
    grad_heads = (
        attn_grad_low.reshape(tok_rows, KVH, heads_per, HD)
        .transpose(1, 2, 0, 3)
        .reshape(KVH, query_rows, HD)
    )
    delta_rows = jnp.sum(
        (attn_grad_low.astype(jnp.float32) * attn_wide).reshape(tok_rows, H, HD), axis=-1
    )
    delta_rows = (
        delta_rows.reshape(tok_rows, KVH, heads_per).transpose(1, 2, 0).reshape(KVH, query_rows)
    )

    def back_step(query_grad, block_index):
        allowed = block_mask(block_index)

        def back_visit(current):
            key_part, value_part = block_keys(block_index)
            prob_vals = jnp.where(
                allowed[None], jnp.exp(block_scores(key_part) - log_total[..., None]), 0.0
            )
            prob_grad = jnp.einsum(
                "krd,jkd->krj", grad_heads, value_part, preferred_element_type=jnp.float32
            )
            score_grad = (prob_vals * (prob_grad - delta_rows[..., None])).astype(jnp.bfloat16)
            new_grad = (
                current
                + jnp.einsum(
                    "krj,jkd->krd", score_grad, key_part, preferred_element_type=jnp.float32
                )
                * score_scale
            )
            key_grad = (
                jnp.einsum("krj,krd->jkd", score_grad, queries, preferred_element_type=jnp.float32)
                * score_scale
            )
            value_grad = jnp.einsum(
                "krj,krd->jkd",
                prob_vals.astype(jnp.bfloat16),
                grad_heads,
                preferred_element_type=jnp.float32,
            )
            return (
                new_grad,
                (key_grad.reshape(key_block, kv_width), value_grad.reshape(key_block, kv_width)),
            )

        def skip_block(current):
            blank_rows = jnp.zeros((key_block, kv_width), jnp.float32)
            return (current, (blank_rows, blank_rows))

        return lax.cond(jnp.any(allowed), back_visit, skip_block, query_grad)

    query_grad, (key_grads, value_grads) = lax.scan(
        back_step, jnp.zeros((KVH, query_rows, HD), jnp.float32), block_order
    )
    key_own, value_own = (
        lax.psum_scatter(
            key_grads.reshape(group_tok, kv_width).astype(jnp.bfloat16),
            "seq",
            scatter_dimension=0,
            tiled=True,
        ).astype(jnp.float32),
        lax.psum_scatter(
            value_grads.reshape(group_tok, kv_width).astype(jnp.bfloat16),
            "seq",
            scatter_dimension=0,
            tiled=True,
        ).astype(jnp.float32),
    )
    query_back = unrotate(
        query_grad.reshape(KVH, heads_per, tok_rows, HD)
        .transpose(2, 0, 1, 3)
        .reshape(tok_rows, H, HD),
        cosine_table,
        sine_table,
    )
    key_back = unrotate(key_own.reshape(tok_rows, KVH, HD), cosine_table, sine_table)
    qkv_grad_low = jnp.concatenate(
        [query_back.reshape(tok_rows, att_width), key_back.reshape(tok_rows, kv_width), value_own],
        axis=1,
    ).astype(jnp.bfloat16)
    qkv_grad_owned = columns_to_owners(qkv_grad_low, qkv_weight.shape[0])
    bias_terms = jnp.sum(qkv_grad_owned.astype(jnp.float32), axis=0)
    normed_one_grad = lax.psum_scatter(
        jnp.dot(qkv_grad_owned, qkv_rows, preferred_element_type=jnp.float32).astype(jnp.bfloat16),
        "seq",
        scatter_dimension=0,
        tiled=True,
    ).astype(jnp.float32)
    qkv_grad = lax.psum_scatter(
        lax.dot_general(
            qkv_grad_owned, normed_one_all, contract_first, preferred_element_type=jnp.float32
        ),
        "grp",
        scatter_dimension=0,
        tiled=True,
    )
    unused_tokens, norm_one_back = jax.vjp(rms_scale, tokens_wide, gain_one)
    token_norm_grad, gain_one_grad = norm_one_back(normed_one_grad)
    token_grad = token_norm_grad + state_grad
    bias_part = lax.psum_scatter(bias_terms, "grp", scatter_dimension=0, tiled=True)
    gain_one_part, gain_two_part = (
        lax.psum_scatter(gain_one_grad, AXES, scatter_dimension=0, tiled=True),
        lax.psum_scatter(gain_two_grad, AXES, scatter_dimension=0, tiled=True),
    )
    return (
        output,
        token_grad,
        gain_one_part,
        qkv_grad,
        bias_part,
        out_grad,
        gain_two_part,
        mlp_grad,
    )


def solution(mesh):
    return jax.shard_map(
        per_device,
        mesh=mesh,
        in_specs=(
            P(("grp", "seq"), None),
            P(("grp", "seq"), None),
            P(),
            P(),
            P(("grp", "seq"), None),
            P(("grp", "seq")),
            P(("grp", "seq"), None),
            P(),
            P(("grp", "seq"), None, None),
        ),
        out_specs=(
            P(("grp", "seq"), None),
            P(("grp", "seq"), None),
            P(("grp", "seq")),
            P(("grp", "seq"), None),
            P(("grp", "seq")),
            P(("grp", "seq"), None),
            P(("grp", "seq")),
            P(("grp", "seq"), None, None),
        ),
        check_vma=False,
    )
```

```python
import functools
import math

import jax
import jax.numpy as jnp
from jax import lax
from jax.experimental import pallas as pl
from jax.experimental.pallas import tpu as pltpu
from jax.sharding import PartitionSpec as P

H = 12
KVH = 2
HD = 128
FF = 8960


EPS = 1e-06
THETA = 10000.0


def rms_scale(values, gain_vec):
    return values * lax.rsqrt(jnp.mean(values * values, axis=-1, keepdims=True) + EPS) * gain_vec


def rotary_tables(positions, head_dim):
    half_dim = head_dim // 2
    freqs = THETA ** (-(jnp.arange(half_dim, dtype=jnp.float32) * 2.0) / head_dim)
    angles = positions.astype(jnp.float32)[:, None] * freqs[None, :]
    cosine_table = jnp.concatenate([jnp.cos(angles), jnp.cos(angles)], axis=-1)
    sine_table = jnp.concatenate([jnp.sin(angles), jnp.sin(angles)], axis=-1)
    return (cosine_table, sine_table)


def rotate(values, cosine_table, sine_table):
    half_dim = values.shape[-1] // 2
    turned = jnp.concatenate([-values[..., half_dim:], values[..., :half_dim]], axis=-1)
    return values * cosine_table[:, None, :] + turned * sine_table[:, None, :]


def unrotate(grad_rows, cosine_table, sine_table):
    half_dim = grad_rows.shape[-1] // 2
    scaled = grad_rows * sine_table[:, None, :]
    turned = jnp.concatenate([scaled[..., half_dim:], -scaled[..., :half_dim]], axis=-1)
    return grad_rows * cosine_table[:, None, :] + turned


def shard_starts(segments, tok_dev, prompt_len):
    shard_total = segments.shape[0]
    shard_order = jnp.arange(shard_total, dtype=jnp.int32)
    same_seg = segments[:, None] == segments[None, :]
    first_shard = jnp.min(jnp.where(same_seg, shard_order[None, :], shard_total), axis=1)
    cont_start = prompt_len + (shard_order - first_shard) * tok_dev
    return jnp.where(segments == 0, shard_order * tok_dev, cont_start)


def swish_product(gate_vals, upper_vals):
    return jax.nn.silu(gate_vals) * upper_vals


AXES = ("grp", "seq")
CONTRACT_LAST = (((1,), (1,)), ((), ()))
CONTRACT_FIRST = (((0,), (0,)), ((), ()))


MESH = pl.DeviceIdType.MESH


def remote(src, dst, send_sem, recv_sem, grp, seq):
    return pltpu.make_async_remote_copy(
        src_ref=src, dst_ref=dst, send_sem=send_sem, recv_sem=recv_sem,
        device_id=(grp, seq), device_id_type=MESH,
    )


def nearest_chip(place, order, chips):
    both = 2 * jnp.minimum(place, chips - 1 - place)
    offset = (order + 1) // 2
    near = jnp.where(order % 2 == 1, place - offset, place + offset)
    rest = jnp.where(place < chips - 1 - place, order, chips - 1 - order)
    return jnp.where(order <= both, near, rest)


def line_barrier(chips):
    grp, seq = lax.axis_index("grp"), lax.axis_index("seq")
    chip, core = seq // 2, seq % 2
    mate = seq + 1 - 2 * core
    barrier = pltpu.get_barrier_semaphore()

    def greet(other):
        pl.semaphore_signal(barrier, inc=1, device_id=(grp, other), device_id_type=MESH)

    greet(mate)
    pl.when(chip > 0)(lambda: greet(seq - 2))
    pl.when(chip < chips - 1)(lambda: greet(seq + 2))
    inner = jnp.where((chip > 0) & (chip < chips - 1), 1, 0)
    pl.semaphore_wait(barrier, 2 + inner)


class LineGather:
    def __init__(self, buf, send_sem, recv_sem, chips):
        self.buf, self.send_sem, self.recv_sem, self.chips = buf, send_sem, recv_sem, chips
        self.grp, self.seq = lax.axis_index("grp"), lax.axis_index("seq")
        self.chip, self.core = self.seq // 2, self.seq % 2
        self.mate = self.seq + 1 - 2 * self.core

    def copy(self, way, slot):
        to = (self.seq + 2, self.seq - 2, self.mate)[way]
        return remote(
            self.buf.at[slot], self.buf.at[slot], self.send_sem.at[way, slot],
            self.recv_sem.at[slot], self.grp, to,
        )

    def wait_recv(self, slot):
        self.copy(2, slot).wait_recv()

    def start(self):
        pl.when(self.chip < self.chips - 1)(lambda: self.copy(0, self.seq).start())
        pl.when(self.chip > 0)(lambda: self.copy(1, self.seq).start())
        self.copy(2, self.seq).start()

    def forward(self, step):
        @pl.when(self.chip - step >= 0)
        def _():
            slot = self.seq - 2 * step
            self.wait_recv(slot)
            pl.when(self.chip < self.chips - 1)(lambda: self.copy(0, slot).start())
            self.copy(2, slot).start()

        @pl.when(self.chip + step < self.chips)
        def _():
            slot = self.seq + 2 * step
            self.wait_recv(slot)
            pl.when(self.chip > 0)(lambda: self.copy(1, slot).start())
            self.copy(2, slot).start()

    def wait_mate(self, chip):
        self.wait_recv(2 * chip + 1 - self.core)

    def drain(self):
        for other in range(self.chips):
            slot = 2 * other + self.core
            self.copy(2, slot).wait_send()
            pl.when((other <= self.chip) & (self.chip < self.chips - 1))(
                lambda slot=slot: self.copy(0, slot).wait_send()
            )
            pl.when((other >= self.chip) & (self.chip > 0))(
                lambda slot=slot: self.copy(1, slot).wait_send()
            )


class LineScatter:
    def __init__(self, part, mate_in, left_in, right_in, send_sem, recv_sem, chips):
        self.part, self.mate_in, self.left_in, self.right_in = part, mate_in, left_in, right_in
        self.send_sem, self.recv_sem, self.chips = send_sem, recv_sem, chips
        self.grp, self.seq = lax.axis_index("grp"), lax.axis_index("seq")
        self.chip, self.core = self.seq // 2, self.seq % 2
        self.mate = self.seq + 1 - 2 * self.core

    def to_mate(self, r, chip):
        return remote(
            self.part.at[r, 2 * chip + 1 - self.core], self.mate_in.at[r, chip],
            self.send_sem.at[0, r, chip], self.recv_sem.at[0, r, chip], self.grp, self.mate,
        )

    def to_right(self, r, chip):
        return remote(
            self.part.at[r, 2 * chip + self.core], self.left_in.at[r, chip],
            self.send_sem.at[1, r, chip], self.recv_sem.at[1, r, chip], self.grp, self.seq + 2,
        )

    def to_left(self, r, chip):
        return remote(
            self.part.at[r, 2 * chip + self.core], self.right_in.at[r, chip],
            self.send_sem.at[2, r, chip], self.recv_sem.at[2, r, chip], self.grp, self.seq - 2,
        )

    def step(self, r, order):
        last = self.chips - 1
        far = last - order

        @pl.when(far > self.chip)
        def _():
            self.to_mate(r, far).wait_recv()
            slot = 2 * far + self.core
            total = self.part[r, slot].astype(jnp.float32) + self.mate_in[r, far].astype(jnp.float32)

            @pl.when(self.chip > 0)
            def _():
                self.to_right(r, far).wait_recv()
                self.part[r, slot] = (total + self.left_in[r, far].astype(jnp.float32)).astype(jnp.bfloat16)

            @pl.when(self.chip == 0)
            def _():
                self.part[r, slot] = total.astype(jnp.bfloat16)

            self.to_right(r, far).start()

        @pl.when(order < self.chip)
        def _():
            self.to_mate(r, order).wait_recv()
            slot = 2 * order + self.core
            total = self.part[r, slot].astype(jnp.float32) + self.mate_in[r, order].astype(jnp.float32)

            @pl.when(self.chip < last)
            def _():
                self.to_left(r, order).wait_recv()
                self.part[r, slot] = (total + self.right_in[r, order].astype(jnp.float32)).astype(jnp.bfloat16)

            @pl.when(self.chip == last)
            def _():
                self.part[r, slot] = total.astype(jnp.bfloat16)

            self.to_left(r, order).start()

    def finish(self, r, out_ref):
        self.to_mate(r, self.chip).wait_recv()
        out_ref[...] = self.part[r, self.seq].astype(jnp.float32) + self.mate_in[r, self.chip].astype(jnp.float32)

        @pl.when(self.chip > 0)
        def _():
            self.to_right(r, self.chip).wait_recv()
            out_ref[...] += self.left_in[r, self.chip].astype(jnp.float32)

        @pl.when(self.chip < self.chips - 1)
        def _():
            self.to_left(r, self.chip).wait_recv()
            out_ref[...] += self.right_in[r, self.chip].astype(jnp.float32)

    def drain(self, r):
        for other in range(self.chips):
            self.to_mate(r, other).wait_send()
            pl.when(other > self.chip)(lambda other=other: self.to_right(r, other).wait_send())
            pl.when(other < self.chip)(lambda other=other: self.to_left(r, other).wait_send())


def mlp_kernel(chips, grps, row_tiles, n2_ref, cot_ref, *refs):
    w_refs, refs = refs[:grps], refs[grps:]
    (
        n2g_ref, outp_ref, grads_ref, tok, w, acts, part, mate_in, left_in, right_in, stage,
        lsem, gsend, grecv, ssend, srecv, wsem, osem,
    ) = refs
    seq = lax.axis_index("seq")
    chip, core = seq // 2, seq % 2
    shard, width = n2_ref.shape
    units = w.shape[1]
    block = units // grps
    tile = units // row_tiles
    own = pltpu.make_async_copy(n2_ref, tok.at[0, seq], lsem.at[0])
    own.start()
    cot_copy = pltpu.make_async_copy(cot_ref, tok.at[1], lsem.at[1])
    cot_copy.start()

    def w_copy(j, b):
        return pltpu.make_async_copy(w_refs[b].at[j], w.at[j, pl.ds(b * block, block)], wsem.at[j, b])

    for j in range(3):
        for b in range(grps):
            w_copy(j, b).start()
    line_barrier(chips)
    gather = LineGather(tok.at[0], gsend, grecv, chips)
    scatter = LineScatter(part, mate_in, left_in, right_in, ssend, srecv, chips)
    own.wait()
    gather.start()

    @pl.loop(0, chips)
    def _(order):
        @pl.when(order == 0)
        def _():
            cot_copy.wait()
            for j in range(3):
                for b in range(grps):
                    w_copy(j, b).wait()

        pl.when(order > 0)(lambda: gather.forward(order))
        at = nearest_chip(chip, order, chips)
        gather.wait_mate(at)
        x = tok[0, pl.ds(2 * at, 2)].reshape(2 * shard, width)
        y = tok[1, pl.ds(2 * at, 2)].reshape(2 * shard, width)
        gate = lax.dot_general(x, w[0], CONTRACT_LAST, preferred_element_type=jnp.float32)
        up = lax.dot_general(x, w[1], CONTRACT_LAST, preferred_element_type=jnp.float32)
        unit_grad = lax.dot_general(y, w[2], CONTRACT_LAST, preferred_element_type=jnp.float32)
        sig = 1.0 / (1.0 + jnp.exp(-gate))
        silu = gate * sig
        rows = pl.ds(at * (2 * shard), 2 * shard)
        gate_grad = (unit_grad * up * sig * (1.0 + gate * (1.0 - sig))).astype(jnp.bfloat16)
        up_grad = (unit_grad * silu).astype(jnp.bfloat16)
        acts[0, rows] = gate_grad
        acts[1, rows] = up_grad
        acts[2, rows] = (silu * up).astype(jnp.bfloat16)
        back = jnp.dot(gate_grad, w[0], preferred_element_type=jnp.float32) + jnp.dot(
            up_grad, w[1], preferred_element_type=jnp.float32
        )
        part[0, pl.ds(2 * at, 2)] = back.astype(jnp.bfloat16).reshape(2, shard, width)
        scatter.to_mate(0, at).start()

    def out_copy(t):
        return pltpu.make_async_copy(
            stage.at[t % 2],
            grads_ref.at[t // row_tiles, pl.ds((t % row_tiles) * tile, tile)],
            osem.at[t % 2],
        )

    @pl.loop(0, 3 * row_tiles)
    def _(t):
        @pl.when(t < 2 * chips)
        def _():
            scatter.step(t // chips, t % chips)

        @pl.when(t < chips)
        def _():
            h = acts[2, pl.ds(t * (2 * shard), 2 * shard)]
            part[1, pl.ds(2 * t, 2)] = (
                jnp.dot(h, w[2], preferred_element_type=jnp.float32)
                .astype(jnp.bfloat16).reshape(2, shard, width)
            )
            scatter.to_mate(1, t).start()

        @pl.when(t >= 2)
        def _():
            out_copy(t - 2).wait()

        kind = t // row_tiles
        lhs = acts[kind, :, pl.ds(pl.multiple_of((t % row_tiles) * tile, 128), tile)]
        rhs = tok[kind // 2].reshape(2 * chips * shard, width)
        stage[t % 2] = lax.dot_general(
            lhs, rhs, CONTRACT_FIRST, preferred_element_type=jnp.float32
        ).astype(jnp.bfloat16)
        out_copy(t).start()

    scatter.finish(0, n2g_ref)
    scatter.finish(1, outp_ref)
    out_copy(3 * row_tiles - 2).wait()
    out_copy(3 * row_tiles - 1).wait()
    gather.drain()
    scatter.drain(0)
    scatter.drain(1)


def mlp_call(n2, cot_all, w_blocks, row_tiles=3):
    grps, (_, block, width) = len(w_blocks), w_blocks[0].shape
    slots, shard, _ = cot_all.shape
    chips = slots // 2
    units = grps * block
    vm, anyspace = pltpu.VMEM, pl.BlockSpec(memory_space=pl.ANY)
    vspec = pl.BlockSpec(memory_space=pltpu.VMEM)
    dma = pltpu.SemaphoreType.DMA
    flops = 2 * 9 * slots * shard * units * width
    return pl.pallas_call(
        functools.partial(mlp_kernel, chips, grps, row_tiles),
        out_shape=(
            jax.ShapeDtypeStruct((shard, width), jnp.float32),
            jax.ShapeDtypeStruct((shard, width), jnp.float32),
            jax.ShapeDtypeStruct((3, units, width), jnp.bfloat16),
        ),
        in_specs=[vspec, anyspace] + [anyspace] * grps,
        out_specs=(vspec, vspec, anyspace),
        scratch_shapes=[
            vm((2, slots, shard, width), jnp.bfloat16),
            vm((3, units, width), jnp.bfloat16),
            vm((3, slots * shard, units), jnp.bfloat16),
            vm((2, slots, shard, width), jnp.bfloat16),
            vm((2, chips, shard, width), jnp.bfloat16),
            vm((2, chips, shard, width), jnp.bfloat16),
            vm((2, chips, shard, width), jnp.bfloat16),
            vm((2, units // row_tiles, width), jnp.bfloat16),
            dma((2,)), dma((3, slots)), dma((slots,)), dma((3, 2, chips)), dma((3, 2, chips)),
            dma((3, grps)), dma((2,)),
        ],
        compiler_params=pltpu.CompilerParams(
            collective_id=1, has_side_effects=True, vmem_limit_bytes=62 * 2**20
        ),
        cost_estimate=pl.CostEstimate(flops=flops, bytes_accessed=30 * 2**20, transcendentals=0),
        name="mlp",
    )(n2, cot_all, *w_blocks)


class Place:
    def __init__(self, chips):
        self.chips = chips
        self.grp, self.seq = lax.axis_index("grp"), lax.axis_index("seq")
        self.chip, self.core = self.seq // 2, self.seq % 2
        self.mate = self.seq + 1 - 2 * self.core

    def peer(self, offset):
        low, high = self.grp % 2, self.grp // 2
        low = 1 - low if offset % 2 else low
        high = 1 - high if offset // 2 else high
        return 2 * high + low

    def barrier(self, grps):
        barrier = pltpu.get_barrier_semaphore()
        for chip in range(self.chips):
            @pl.when(chip != self.chip)
            def _(chip=chip):
                pl.semaphore_signal(
                    barrier, inc=1, device_id=(self.grp, 2 * chip + self.core), device_id_type=MESH
                )
        pl.semaphore_signal(barrier, inc=1, device_id=(self.grp, self.mate), device_id_type=MESH)
        for offset in range(1, grps):
            pl.semaphore_signal(
                barrier, inc=1, device_id=(self.peer(offset), self.seq), device_id_type=MESH
            )
        pl.semaphore_wait(barrier, self.chips - 1 + 1 + grps - 1)


class RailGather:
    def __init__(self, place, view, send_sem, recv_sem):
        self.place, self.view, self.send_sem, self.recv_sem = place, view, send_sem, recv_sem

    def copy(self, way, chip, core):
        p = self.place
        to = (p.seq + 2, p.seq - 2, p.mate)[way]
        return remote(
            self.view(chip, core), self.view(chip, core), self.send_sem.at[way, chip],
            self.recv_sem.at[chip, core], p.grp, to,
        )

    def start(self):
        p = self.place
        pl.when(p.chip < p.chips - 1)(lambda: self.copy(0, p.chip, p.core).start())
        pl.when(p.chip > 0)(lambda: self.copy(1, p.chip, p.core).start())
        self.copy(2, p.chip, p.core).start()

    def forward(self, step):
        p = self.place

        @pl.when(p.chip - step >= 0)
        def _():
            chip = p.chip - step
            self.copy(2, chip, p.core).wait_recv()
            pl.when(p.chip < p.chips - 1)(lambda: self.copy(0, chip, p.core).start())
            self.copy(2, chip, p.core).start()

        @pl.when(p.chip + step < p.chips)
        def _():
            chip = p.chip + step
            self.copy(2, chip, p.core).wait_recv()
            pl.when(p.chip > 0)(lambda: self.copy(1, chip, p.core).start())
            self.copy(2, chip, p.core).start()

    def wait_mate(self, chip):
        self.copy(2, chip, 1 - self.place.core).wait_recv()

    def drain(self):
        p = self.place
        for chip in range(p.chips):
            self.copy(2, chip, p.core).wait_send()
            pl.when((chip <= p.chip) & (p.chip < p.chips - 1))(
                lambda chip=chip: self.copy(0, chip, p.core).wait_send()
            )
            pl.when((chip >= p.chip) & (p.chip > 0))(
                lambda chip=chip: self.copy(1, chip, p.core).wait_send()
            )


def front_kernel(chips, scale,
                 n1_ref, cot_ref, wq_ref, bias_ref, wo_ref, wm_ref, cos_ref, sin_ref, mask_ref,
                 attn_ref, lse_ref, q_out_ref, kv_out_ref, n1_all_ref, cot_all_ref, wo_all_ref, wq_all_ref,
                 wm1_ref, wm2_ref, wm3_ref,
                 nbuf, wq, bias, stage, qbuf, kvbuf,
                 lsem, n_send, n_recv, c_send, c_recv, o_send, o_recv, ox_send, ox_recv, om_send, om_recv,
                 wq_send, wq_recv, b_send, b_recv, m_send, m_recv, q_send, q_recv, k_send, k_recv):
    p = Place(chips)
    grps = 4
    half = wq_ref.shape[0]
    rows = pl.ds(p.core * half, half)
    mates_rows = pl.ds((1 - p.core) * half, half)
    wm_refs = (wm_ref, wm1_ref, wm2_ref, wm3_ref)
    part = wm_ref.shape[1] // 2

    own = [
        pltpu.make_async_copy(n1_ref, nbuf.at[p.chip, p.core], lsem.at[0]),
        pltpu.make_async_copy(wq_ref, wq.at[0, rows], lsem.at[1]),
        pltpu.make_async_copy(bias_ref, bias.at[0, p.core], lsem.at[2]),
        pltpu.make_async_copy(wo_ref, wo_all_ref.at[p.grp, p.chip, p.core], lsem.at[3]),
        pltpu.make_async_copy(cot_ref, cot_all_ref.at[p.chip, p.core], lsem.at[4]),
    ]
    for copy in own:
        copy.start()
    p.barrier(grps)

    n1_line = RailGather(p, lambda chip, core: nbuf.at[chip, core], n_send, n_recv)
    cot_line = RailGather(p, lambda chip, core: cot_all_ref.at[chip, core], c_send, c_recv)
    out_line = RailGather(p, lambda chip, core: wo_all_ref.at[p.grp, chip, core], o_send, o_recv)

    def wq_direct(b):
        return remote(wq_ref, wq.at[b, rows], wq_send.at[0, b], wq_recv.at[b, 0], p.peer(b), p.seq)

    def wq_mate(b):
        return remote(wq.at[b, rows], wq.at[b, rows], wq_send.at[1, b], wq_recv.at[b, 1], p.grp, p.mate)

    def bias_direct(b):
        return remote(bias_ref, bias.at[b, p.core], b_send.at[0, b], b_recv.at[b, 0], p.peer(b), p.seq)

    def bias_mate(b):
        return remote(bias.at[b, p.core], bias.at[b, p.core], b_send.at[1, b], b_recv.at[b, 1], p.grp, p.mate)

    def m_half(ref, i):
        return ref.at[:, pl.ds(i * part, part)]

    def m_direct(b, i):
        return remote(m_half(wm_ref, i), m_half(wm_refs[b], i), m_send.at[b, i], m_recv.at[b, i], p.peer(b), p.seq)

    def m_forward(b):
        return remote(
            m_half(wm_refs[b], b - 1), m_half(wm3_ref, b - 1), m_send.at[3, b - 1], m_recv.at[3, b - 1],
            p.peer(3 - b), p.seq,
        )

    def out_cross(b):
        view = lambda grp: wo_all_ref.at[grp, :, p.core]
        return remote(view(p.grp), view(p.grp), ox_send.at[b], ox_recv.at[b], p.peer(b), p.seq)

    def out_mate(b):
        view = wo_all_ref.at[p.peer(b), :, p.core]
        return remote(view, view, om_send.at[b], om_recv.at[b], p.grp, p.mate)

    def q_copy(chip):
        return remote(
            stage.at[chip, pl.ds(0, 3)], qbuf.at[p.chip], q_send.at[chip], q_recv.at[p.chip],
            p.grp, 2 * chip + p.core,
        )

    def q_arrival(chip):
        return remote(stage.at[chip, pl.ds(0, 3)], qbuf.at[chip], q_send.at[chip], q_recv.at[chip], p.grp, p.mate)

    def k_copy(chip, to_chip):
        return remote(
            stage.at[chip, 3], kvbuf.at[p.chip, p.core, chip], k_send.at[0, chip, to_chip],
            k_recv.at[p.chip, p.core, chip], p.grp, 2 * to_chip + p.core,
        )

    def k_mate(head, chip, src=None):
        view = kvbuf.at[head, p.core, chip]
        return remote(
            view if src is None else src, view, k_send.at[1, head, chip],
            k_recv.at[head, p.core, chip], p.grp, p.mate,
        )

    def k_arrival(head, core, chip):
        view = kvbuf.at[head, core, chip]
        return remote(view, view, k_send.at[1, head, chip], k_recv.at[head, core, chip], p.grp, p.mate)

    own[1].wait()
    own[2].wait()
    for b in range(1, grps):
        wq_direct(b).start()
        bias_direct(b).start()
    wq_mate(0).start()
    bias_mate(0).start()
    own[0].wait()
    n1_line.start()
    own[3].wait()
    out_line.start()
    for b in range(1, grps):
        wq_direct(b).wait_recv()
        wq_mate(b).start()
        bias_direct(b).wait_recv()
        bias_mate(b).start()
    m_direct(1, 0).start()
    m_direct(2, 1).start()
    for b in range(grps):
        wq_mate(b).wait_recv()
        bias_mate(b).wait_recv()

    @pl.loop(0, chips)
    def _(order):
        @pl.when(order > 0)
        def _():
            n1_line.forward(order)
            out_line.forward(order)

        at = nearest_chip(p.chip, order, chips)
        x = nbuf[at, p.core]
        weights = wq[...].reshape(grps * 2 * half, x.shape[1])
        rows_all = lax.dot_general(x, weights, CONTRACT_LAST, preferred_element_type=jnp.float32)
        cosine, sine = cos_ref[at, p.core], sin_ref[at, p.core]
        for b in range(grps):
            u = rows_all[:, 2 * half * b : 2 * half * (b + 1)] + (bias[b, 0, 0:1] + bias[b, 1, 0:1])
            turned = u * cosine + pltpu.roll(u, half, 1) * sine
            place = p.peer(b)
            keep = jnp.where((place == grps - 1) & (p.chip >= chips // 2), 1.0, 0.0)
            value = (u * keep + turned * (1.0 - keep)).astype(jnp.bfloat16)
            stage[at, place] = value

            @pl.when(place == grps - 1)
            def _(value=value):
                kvbuf[p.chip, p.core, at] = value

            @pl.when((place < grps - 1) & (at == p.chip))
            def _(value=value, place=place):
                qbuf[p.chip, place] = value

        pl.when(at != p.chip)(lambda: q_copy(at).start())
        for to_chip in range(chips):
            pl.when(to_chip != p.chip)(lambda to_chip=to_chip: k_copy(at, to_chip).start())
        k_mate(p.chip, at, stage.at[at, 3]).start()

    for b in range(1, grps):
        out_cross(b).start()
    own[4].wait()
    cot_line.start()

    @pl.loop(0, chips)
    def _(order):
        for head in range(chips):
            @pl.when(head != p.chip)
            def _(head=head):
                chip = nearest_chip(head, order, chips)
                k_arrival(head, p.core, chip).wait_recv()
                k_mate(head, chip).start()

    for chip in range(chips):
        pl.when(chip != p.chip)(lambda chip=chip: q_arrival(chip).wait_recv())
        for head in range(chips):
            k_arrival(head, 1 - p.core, chip).wait_recv()
    for b in (1, 2):
        m_direct(b, b - 1).wait_recv()
        m_forward(b).start()
    cot_line.forward(1)

    mask = mask_ref[...]
    shard = mask.shape[0]
    heads_per = H // KVH
    for kv in range(KVH):
        heads = [kv * heads_per + i for i in range(heads_per)]
        queries = jnp.concatenate([qbuf[h % chips, h // chips] for h in heads], axis=0)
        keys = kvbuf[kv].reshape(mask.shape[1], 2 * half)
        values = kvbuf[KVH + kv].reshape(mask.shape[1], 2 * half)
        scores = lax.dot_general(queries, keys, CONTRACT_LAST, preferred_element_type=jnp.float32) * scale
        scores = scores.reshape(heads_per, shard, mask.shape[1]) + mask[None]
        top = jnp.max(scores, axis=-1, keepdims=True)
        weights = jnp.exp(scores - top)
        total = jnp.sum(weights, axis=-1, keepdims=True)
        probs = (weights / total).astype(jnp.bfloat16).reshape(heads_per * shard, mask.shape[1])
        mixed = jnp.dot(probs, values, preferred_element_type=jnp.float32)
        log_total = (top + jnp.log(total)).reshape(heads_per * shard, 1)
        lse_ref[kv] = jnp.broadcast_to(log_total, (heads_per * shard, 2 * half))
        for i, h in enumerate(heads):
            attn_ref[:, h * 2 * half : (h + 1) * 2 * half] = mixed[i * shard : (i + 1) * shard]
        cot_line.forward(kv + 2)

    for b in range(1, grps):
        out_cross(b).wait_recv()
        out_mate(b).start()
    m_direct(1, 1).start()
    m_direct(2, 0).start()
    outs = [
        pltpu.make_async_copy(nbuf, n1_all_ref, lsem.at[5]),
        pltpu.make_async_copy(wq, wq_all_ref, lsem.at[6]),
        pltpu.make_async_copy(qbuf, q_out_ref, lsem.at[7]),
        pltpu.make_async_copy(kvbuf, kv_out_ref, lsem.at[8]),
    ]
    for chip in range(chips):
        n1_line.wait_mate(chip)
        out_line.wait_mate(chip)
        cot_line.wait_mate(chip)
    for copy in outs:
        copy.start()
    for b in (1, 2):
        m_direct(b, 2 - b).wait_recv()
        m_forward(3 - b).wait_recv()
    for b in range(1, grps):
        om = remote(
            wo_all_ref.at[p.peer(b), :, 1 - p.core], wo_all_ref.at[p.peer(b), :, 1 - p.core],
            om_send.at[b], om_recv.at[b], p.grp, p.mate,
        )
        om.wait_recv()
    for copy in outs:
        copy.wait()
    n1_line.drain()
    out_line.drain()
    cot_line.drain()
    for b in range(grps):
        wq_mate(b).wait_send()
        bias_mate(b).wait_send()
    for b in range(1, grps):
        wq_direct(b).wait_send()
        bias_direct(b).wait_send()
        out_cross(b).wait_send()
        out_mate(b).wait_send()
    for b in (1, 2):
        m_direct(b, 0).wait_send()
        m_direct(b, 1).wait_send()
        m_forward(b).wait_send()
    for chip in range(chips):
        pl.when(chip != p.chip)(lambda chip=chip: q_copy(chip).wait_send())
        for other in range(chips):
            pl.when(other != p.chip)(lambda chip=chip, other=other: k_copy(chip, other).wait_send())
            k_mate(other, chip).wait_send()


def front_call(n1, cot, qkv_weight, bias_rows, out_weight, mlp_rows, cosine, sine, mask):
    chips = cosine.shape[0]
    grps = 4
    shard, width = n1.shape
    half = qkv_weight.shape[0]
    vm, dma = pltpu.VMEM, pltpu.SemaphoreType.DMA
    anyspace = pl.BlockSpec(memory_space=pl.ANY)
    vspec = pl.BlockSpec(memory_space=pltpu.VMEM)
    low, wide = jnp.bfloat16, jnp.float32
    struct = jax.ShapeDtypeStruct
    return pl.pallas_call(
        functools.partial(front_kernel, chips, 1.0 / math.sqrt(HD)),
        out_shape=(
            struct((shard, H * HD), wide),
            struct((KVH, H // KVH * shard, HD), wide),
            struct((chips, 3, shard, HD), low),
            struct((chips, 2, chips, shard, HD), low),
            struct((chips, 2, shard, width), low),
            struct((chips, 2, shard, width), low),
            struct((grps, chips, 2) + out_weight.shape, low),
            struct((grps, 2 * half, width), low),
        ) + (struct(mlp_rows.shape, low),) * 3,
        in_specs=[anyspace] * 6 + [vspec] * 3,
        out_specs=(vspec,) * 2 + (anyspace,) * 9,
        scratch_shapes=[
            vm((chips, 2, shard, width), low),
            vm((grps, 2 * half, width), low),
            vm((grps, 2) + bias_rows.shape, wide),
            vm((chips, grps, shard, HD), low),
            vm((chips, 3, shard, HD), low),
            vm((chips, 2, chips, shard, HD), low),
            dma((9,)),
            dma((3, chips)), dma((chips, 2)),
            dma((3, chips)), dma((chips, 2)),
            dma((3, chips)), dma((chips, 2)),
            dma((grps,)), dma((grps,)), dma((grps,)), dma((grps,)),
            dma((2, grps)), dma((grps, 2)),
            dma((2, grps)), dma((grps, 2)),
            dma((grps, 2)), dma((grps, 2)),
            dma((chips,)), dma((chips,)),
            dma((2, chips, chips)), dma((chips, 2, chips)),
        ],
        compiler_params=pltpu.CompilerParams(
            collective_id=2, has_side_effects=True, vmem_limit_bytes=56 * 2**20
        ),
        name="front",
    )(n1, cot, qkv_weight, bias_rows, out_weight, mlp_rows, cosine, sine, mask)


def unturn(rows, cosine, sine, half):
    return rows * cosine + pltpu.roll(rows * sine, half, 1)


def back_kernel(chips, scale,
                n2g_ref, state_ref, cot_ref, tokens_ref, gains_ref, attn_ref, q_ref, kv_ref, mask_ref,
                cos_ref, sin_ref, wq_ref, wo_ref, n1_ref, terms_ref,
                tok_grad_ref, wq_grad_ref, wo_grad_ref, gain_ref, mlp_ref,
                wo, stbuf, n1x, at_stage, at_all, dq_stage, gq_in, kv_part, km_in, k_sum, k_own, kr_in,
                cols, part, left_in, right_in, wgrad, wm_in, w_send_buf, w_in, o_terms, o_send_buf, o_in,
                m_own, m_in, gain_own, gain_in, gain_mid, gain_mid_in, state_grad,
                lsem, s_send, s_recv, a_send, a_recv, q_send, q_recv, km_send, km_recv, kr_send, kr_recv,
                r_send, r_recv, wm_send, wm_recv, w_send, w_recv, o_send, o_recv, m_send, m_recv,
                ml_sem, g_send, g_recv, h_send, h_recv):
    p = Place(chips)
    grps = 4
    shard, width = n2g_ref.shape
    slots = 2 * chips
    heads_per = H // KVH
    half = HD // 2
    low, wide = jnp.bfloat16, jnp.float32
    block = terms_ref.shape[1] // grps
    mhalf = block // 2
    last = chips - 1

    loads = [
        pltpu.make_async_copy(wo_ref, wo, lsem.at[0]),
        pltpu.make_async_copy(n1_ref.at[:, p.core], n1x.at[:, :, pl.ds(0, width)], lsem.at[1]),
    ]
    for copy in loads:
        copy.start()

    def seq_peer(i):
        return (p.seq + i) % slots

    barrier = pltpu.get_barrier_semaphore()
    for i in range(1, slots):
        pl.semaphore_signal(barrier, inc=1, device_id=(p.grp, seq_peer(i)), device_id_type=MESH)
    for b in range(1, grps):
        pl.semaphore_signal(barrier, inc=1, device_id=(p.peer(b), p.seq), device_id_type=MESH)
    pl.semaphore_wait(barrier, slots - 1 + grps - 1)

    def m_rows(b, i):
        return terms_ref.at[:, pl.ds(b * block + i * mhalf, mhalf)]

    def m_copy(slot, src, peer):
        return remote(src, m_in.at[slot], m_send.at[slot], m_recv.at[slot], p.peer(peer), p.seq)

    m_first = [
        m_copy(1, m_rows(3, 0), 1), m_copy(3, m_rows(3, 1), 2),
        m_copy(0, m_rows(1, 0), 1), m_copy(2, m_rows(2, 1), 2),
    ]
    for copy in m_first:
        copy.start()
    m_second = [m_copy(4, m_own.at[0], 1), m_copy(5, m_own.at[1], 2)]
    m_loads = [
        pltpu.make_async_copy(m_rows(1, 1), m_own.at[0], ml_sem.at[0]),
        pltpu.make_async_copy(m_rows(2, 0), m_own.at[1], ml_sem.at[1]),
        pltpu.make_async_copy(m_rows(0, 0), m_own.at[2], ml_sem.at[2]),
        pltpu.make_async_copy(m_rows(0, 1), m_own.at[3], ml_sem.at[3]),
    ]
    for copy in m_loads:
        copy.start()

    state = state_ref[...]
    gain_two = gains_ref[1]
    n2g = n2g_ref[...]
    scale_two = lax.rsqrt(jnp.mean(state * state, axis=-1, keepdims=True) + EPS)
    normed = state * scale_two
    gain_own[1] = jnp.sum(n2g * normed, axis=0, keepdims=True)
    lifted = n2g * gain_two
    state_grad[...] = cot_ref[...].astype(wide) + scale_two * (
        lifted - normed * jnp.mean(lifted * normed, axis=-1, keepdims=True)
    )
    state_low = state_grad[...].astype(low)
    stbuf[p.chip, p.core] = state_low
    line = RailGather(p, lambda chip, core: stbuf.at[chip, core], s_send, s_recv)
    line.start()

    attn = attn_ref[...]
    unit = wo.shape[0] // (grps * slots)
    at_rows = attn.astype(low).T
    at_stage[...] = at_rows.reshape(grps, slots, unit, shard)

    def at_copy(i, to):
        return remote(
            at_stage.at[:, to], at_all.at[:, :, pl.ds(pl.multiple_of(p.seq * shard, shard), shard)],
            a_send.at[i], a_recv.at[p.seq], p.grp, to,
        )

    def at_arrival(slot):
        return remote(
            at_stage.at[:, slot], at_all.at[:, :, pl.ds(pl.multiple_of(slot * shard, shard), shard)],
            a_send.at[0], a_recv.at[slot], p.grp, p.mate,
        )

    for i in range(1, slots):
        at_copy(i, seq_peer(i)).start()
    at_all[:, :, pl.ds(pl.multiple_of(p.seq * shard, shard), shard)] = at_stage[:, p.seq]

    loads[0].wait()
    attn_grad = lax.dot_general(state_low, wo[...], CONTRACT_LAST, preferred_element_type=wide).astype(low)
    line.forward(1)
    mask = mask_ref[...]
    keys_total = mask.shape[1]
    own_cos, own_sin = cos_ref[p.chip, p.core], sin_ref[p.chip, p.core]

    def km_copy(head):
        return remote(
            kv_part.at[head, 1 - p.core], km_in.at[head], km_send.at[head], km_recv.at[head], p.grp, p.mate
        )

    def kr_copy(head):
        return remote(
            k_sum.at[head], kr_in.at[p.chip], kr_send.at[head], kr_recv.at[p.chip], p.grp, 2 * head + p.core
        )

    def kr_arrival(chip):
        return remote(k_sum.at[chip], kr_in.at[chip], kr_send.at[chip], kr_recv.at[chip], p.grp, p.mate)

    def q_copy(chip):
        return remote(
            dq_stage.at[chip], gq_in.at[p.chip], q_send.at[chip], q_recv.at[p.chip], p.grp, 2 * chip + p.core
        )

    def q_arrival(chip):
        return remote(dq_stage.at[chip], gq_in.at[chip], q_send.at[chip], q_recv.at[chip], p.grp, p.mate)

    def key_sum(head):
        km_copy(head).wait_recv()
        total = kv_part[head, p.core].astype(wide) + km_in[head].astype(wide)

        @pl.when(p.chip == head)
        def _():
            k_own[...] = total

        @pl.when(p.chip != head)
        def _():
            k_sum[head] = total.astype(low)
            kr_copy(head).start()

    for kv in range(KVH):
        heads = [kv * heads_per + i for i in range(heads_per)]
        queries = jnp.concatenate([q_ref[h % chips, h // chips] for h in heads], axis=0)
        grads = jnp.concatenate([attn_grad[:, h * HD : (h + 1) * HD] for h in heads], axis=0)
        mixed = jnp.concatenate([attn[:, h * HD : (h + 1) * HD] for h in heads], axis=0)
        delta = jnp.sum(grads.astype(wide) * mixed, axis=-1, keepdims=True)
        keys = kv_ref[kv].reshape(keys_total, HD)
        values = kv_ref[KVH + kv].reshape(keys_total, HD)
        scores = lax.dot_general(queries, keys, CONTRACT_LAST, preferred_element_type=wide) * scale
        scores = (scores.reshape(heads_per, shard, keys_total) + mask[None]).reshape(heads_per * shard, keys_total)
        weights = jnp.exp(scores - jnp.max(scores, axis=-1, keepdims=True))
        probs = weights * (1.0 / jnp.sum(weights, axis=-1, keepdims=True))
        prob_grad = lax.dot_general(grads, values, CONTRACT_LAST, preferred_element_type=wide)
        score_grad = (probs * (prob_grad - delta)).astype(low)
        key_grad = lax.dot_general(score_grad, queries, CONTRACT_FIRST, preferred_element_type=wide) * scale
        value_grad = lax.dot_general(probs.astype(low), grads, CONTRACT_FIRST, preferred_element_type=wide)
        kv_part[kv] = key_grad.astype(low).reshape(2, chips, shard, HD)
        kv_part[KVH + kv] = value_grad.astype(low).reshape(2, chips, shard, HD)
        km_copy(kv).start()
        km_copy(KVH + kv).start()
        query_grad = jnp.dot(score_grad, keys, preferred_element_type=wide) * scale
        for i, h in enumerate(heads):
            turned = unturn(query_grad[i * shard : (i + 1) * shard], own_cos, own_sin, half).astype(low)
            dq_stage[h % chips, h // chips] = turned

            @pl.when(p.chip == h % chips)
            def _(turned=turned, h=h):
                gq_in[h % chips, h // chips] = turned

        line.forward(2 + kv)
    for chip in range(chips):
        pl.when(chip != p.chip)(lambda chip=chip: q_copy(chip).start())
    for head in (0, 2, 1, 3):
        key_sum(head)
    loads[1].wait()
    lane = lax.broadcasted_iota(jnp.int32, (chips, shard, HD), 2)
    n1x[:, :, width:] = jnp.where(lane == 0, 1.0, 0.0).astype(low)
    for chip in range(chips):
        line.wait_mate(chip)
    for i in range(1, slots):
        at_arrival(seq_peer(i)).wait_recv()
    o_terms[...] = jnp.dot(
        at_all[...].reshape(grps * unit, slots * shard), stbuf[...].reshape(slots * shard, width),
        preferred_element_type=wide,
    ).reshape(grps, unit, width)
    o_send_buf[...] = o_terms[...].astype(low)

    def o_copy(b):
        return remote(
            o_send_buf.at[p.peer(b)], o_in.at[b], o_send.at[b], o_recv.at[b], p.peer(b), p.seq
        )

    for b in range(1, grps):
        o_copy(b).start()

    def m_add(dst, src):
        for j in range(3):
            @pl.loop(0, mhalf // 16)
            def _(t, j=j):
                rows = pl.ds(pl.multiple_of(t * 16, 16), 16)
                m_own[dst, j, rows] = (
                    m_own[dst, j, rows].astype(wide) + m_in[src, j, rows].astype(wide)
                ).astype(low)

    for chip in range(chips):
        pl.when(chip != p.chip)(lambda chip=chip: q_arrival(chip).wait_recv())
        pl.when(chip != p.chip)(lambda chip=chip: kr_arrival(chip).wait_recv())
    is_value = jnp.where(p.chip >= chips // 2, 1.0, 0.0)

    @pl.loop(0, chips)
    def _(chip):
        key_total = k_own[chip]
        for other in range(chips):
            key_total = key_total + jnp.where(other == p.chip, 0.0, kr_in[other, chip].astype(wide))
        turned = unturn(key_total, cos_ref[chip, p.core], sin_ref[chip, p.core], half)
        last_head = (key_total * is_value + turned * (1.0 - is_value)).astype(low)
        for b in range(grps):
            place = p.peer(b)
            query_head = gq_in[chip, jnp.minimum(place, grps - 2)]
            cols[chip, :, b * HD : (b + 1) * HD] = jnp.where(place == grps - 1, last_head, query_head)
        part[chip] = jnp.dot(
            cols[chip], wq_ref[...], preferred_element_type=wide
        ).astype(low)

    def to_right(chip):
        return remote(part.at[chip], left_in.at[chip], r_send.at[0, chip], r_recv.at[0, chip], p.grp, p.seq + 2)

    def to_left(chip):
        return remote(part.at[chip], right_in.at[chip], r_send.at[1, chip], r_recv.at[1, chip], p.grp, p.seq - 2)

    def rail_step(order):
        far = last - order

        @pl.when(far > p.chip)
        def _():
            @pl.when(p.chip > 0)
            def _():
                to_right(far).wait_recv()
                part[far] = (part[far].astype(wide) + left_in[far].astype(wide)).astype(low)

            to_right(far).start()

        @pl.when(order < p.chip)
        def _():
            @pl.when(p.chip < last)
            def _():
                to_left(order).wait_recv()
                part[order] = (part[order].astype(wide) + right_in[order].astype(wide)).astype(low)

            to_left(order).start()

    rail_step(0)
    wgrad[...] = lax.dot_general(
        cols[...].reshape(chips * shard, grps * HD), n1x[...].reshape(chips * shard, width + HD),
        CONTRACT_FIRST, preferred_element_type=wide,
    ).reshape(grps, 2, half, width + HD)
    wm = remote(wgrad.at[:, 1 - p.core], wm_in, wm_send, wm_recv, p.grp, p.mate)
    wm.start()
    rail_step(1)
    wm.wait_recv()
    w_send_buf[...] = (wgrad[:, p.core] + wm_in[...]).astype(low)

    def w_copy(b):
        return remote(w_send_buf.at[b], w_in.at[b], w_send.at[b], w_recv.at[b], p.peer(b), p.seq)

    for b in range(1, grps):
        w_copy(b).start()
    rail_step(2)
    m_loads[0].wait()
    m_first[1].wait_recv()
    m_add(0, 3)
    m_second[0].start()
    m_loads[1].wait()
    m_first[0].wait_recv()
    m_add(1, 1)
    m_second[1].start()
    rail_step(3)

    tokens = tokens_ref[...].astype(wide)
    tok_grad_ref[...] = part[p.chip].astype(wide)

    @pl.when(p.chip > 0)
    def _():
        to_right(p.chip).wait_recv()
        tok_grad_ref[...] += left_in[p.chip].astype(wide)

    @pl.when(p.chip < last)
    def _():
        to_left(p.chip).wait_recv()
        tok_grad_ref[...] += right_in[p.chip].astype(wide)

    n1g = tok_grad_ref[...]
    scale_one = lax.rsqrt(jnp.mean(tokens * tokens, axis=-1, keepdims=True) + EPS)
    normed = tokens * scale_one
    gain_own[0] = jnp.sum(n1g * normed, axis=0, keepdims=True)
    lifted = n1g * gains_ref[0]
    tok_grad_ref[...] = state_grad[...] + scale_one * (
        lifted - normed * jnp.mean(lifted * normed, axis=-1, keepdims=True)
    )

    def g_copy(i):
        return remote(gain_own, gain_in.at[i], g_send.at[i], g_recv.at[i], p.grp, seq_peer(i))

    for i in range(1, slots):
        g_copy(i).start()
    total = gain_own[...]
    for i in range(1, slots):
        g_copy(i).wait_recv()
        total = total + gain_in[i]
    gain_mid[...] = total

    def h_copy(b):
        return remote(gain_mid, gain_mid_in.at[b], h_send.at[b], h_recv.at[b], p.peer(b), p.seq)

    for b in range(1, grps):
        h_copy(b).start()

    wo_grad = o_terms[p.grp]
    wq_grad = wgrad[0, p.core] + wm_in[0]
    for b in range(1, grps):
        o_copy(b).wait_recv()
        wo_grad = wo_grad + o_in[b].astype(wide)
        w_copy(b).wait_recv()
        wq_grad = wq_grad + w_in[b].astype(wide)
    wo_grad_ref[...] = wo_grad
    wq_grad_ref[...] = wq_grad
    total = gain_mid[...]
    for b in range(1, grps):
        h_copy(b).wait_recv()
        total = total + gain_mid_in[b]
    gain_ref[...] = total

    m_loads[2].wait()
    m_loads[3].wait()

    def m_total(own, direct, second, i):
        for j in range(3):
            @pl.loop(0, mhalf // 16)
            def _(t, j=j):
                rows = pl.ds(pl.multiple_of(t * 16, 16), 16)
                mlp_ref[j, pl.ds(pl.multiple_of(i * mhalf + t * 16, 16), 16)] = (
                    m_own[own, j, rows].astype(wide) + m_in[direct, j, rows].astype(wide)
                ) + m_in[second, j, rows].astype(wide)

    m_first[2].wait_recv()
    m_second[1].wait_recv()
    m_total(2, 0, 5, 0)
    m_first[3].wait_recv()
    m_second[0].wait_recv()
    m_total(3, 2, 4, 1)

    for copy in m_first + m_second:
        copy.wait_send()
    line.drain()
    wm.wait_send()
    for i in range(1, slots):
        at_copy(i, seq_peer(i)).wait_send()
        g_copy(i).wait_send()
    for b in range(1, grps):
        o_copy(b).wait_send()
        w_copy(b).wait_send()
        h_copy(b).wait_send()
    for chip in range(chips):
        km_copy(chip).wait_send()

        @pl.when(chip != p.chip)
        def _(chip=chip):
            q_copy(chip).wait_send()
            kr_copy(chip).wait_send()

        pl.when(chip > p.chip)(lambda chip=chip: to_right(chip).wait_send())
        pl.when(chip < p.chip)(lambda chip=chip: to_left(chip).wait_send())


def back_call(n2g, state, cotangent, tokens, gains, attn, q_heads, kv_heads, mask, cosine, sine,
              qkv_all, out_full, n1_all, terms):
    chips = cosine.shape[0]
    grps = 4
    slots = 2 * chips
    shard, width = tokens.shape
    att, block = out_full.shape[0], terms.shape[1] // grps
    unit, half = att // (grps * slots), HD // 2
    vm, dma = pltpu.VMEM, pltpu.SemaphoreType.DMA
    anyspace = pl.BlockSpec(memory_space=pl.ANY)
    vspec = pl.BlockSpec(memory_space=pltpu.VMEM)
    low, wide = jnp.bfloat16, jnp.float32
    struct = jax.ShapeDtypeStruct
    return pl.pallas_call(
        functools.partial(back_kernel, chips, 1.0 / math.sqrt(HD)),
        out_shape=(
            struct((shard, width), wide),
            struct((half, width + HD), wide),
            struct((unit, width), wide),
            struct((2, 1, width), wide),
            struct((3, block, width), wide),
        ),
        in_specs=[vspec] * 12 + [anyspace] * 3,
        out_specs=(vspec,) * 5,
        scratch_shapes=[
            vm((att, width), low),
            vm((chips, 2, shard, width), low),
            vm((chips, shard, width + HD), low),
            vm((grps, slots, unit, shard), low),
            vm((grps, unit, slots * shard), low),
            vm((chips, 3, shard, HD), low),
            vm((chips, 3, shard, HD), low),
            vm((chips, 2, chips, shard, HD), low),
            vm((chips, chips, shard, HD), low),
            vm((chips, chips, shard, HD), low),
            vm((chips, shard, HD), wide),
            vm((chips, chips, shard, HD), low),
            vm((chips, shard, grps * HD), low),
            vm((chips, shard, width), low),
            vm((chips, shard, width), low),
            vm((chips, shard, width), low),
            vm((grps, 2, half, width + HD), wide),
            vm((grps, half, width + HD), wide),
            vm((grps, half, width + HD), low),
            vm((grps, half, width + HD), low),
            vm((grps, unit, width), wide),
            vm((grps, unit, width), low),
            vm((grps, unit, width), low),
            vm((4, 3, block // 2, width), low),
            vm((6, 3, block // 2, width), low),
            vm((2, 1, width), wide),
            vm((slots, 2, 1, width), wide),
            vm((2, 1, width), wide),
            vm((grps, 2, 1, width), wide),
            vm((shard, width), wide),
            dma((2,)),
            dma((3, chips)), dma((chips, 2)),
            dma((slots,)), dma((slots,)),
            dma((chips,)), dma((chips,)),
            dma((chips,)), dma((chips,)),
            dma((chips,)), dma((chips,)),
            dma((2, chips)), dma((2, chips)),
            dma, dma,
            dma((grps,)), dma((grps,)),
            dma((grps,)), dma((grps,)),
            dma((6,)), dma((6,)),
            dma((4,)),
            dma((slots,)), dma((slots,)),
            dma((grps,)), dma((grps,)),
        ],
        compiler_params=pltpu.CompilerParams(
            collective_id=3, has_side_effects=True, vmem_limit_bytes=62 * 2**20
        ),
        name="back",
    )(n2g, state, cotangent, tokens, gains, attn, q_heads, kv_heads, mask, cosine, sine,
      qkv_all, out_full, n1_all, terms)


def columns_to_owners(rows, row_unit):
    grp_count, seq_count = lax.axis_size("grp"), lax.axis_size("seq")
    tok_rows = rows.shape[0]
    split = rows.reshape(tok_rows, grp_count, seq_count, row_unit).transpose(2, 0, 1, 3)
    split = split.reshape(seq_count * tok_rows, grp_count * row_unit)
    return lax.all_to_all(split, "seq", split_axis=0, concat_axis=0, tiled=True)


def owners_to_columns(rows, row_unit):
    grp_count, seq_count = lax.axis_size("grp"), lax.axis_size("seq")
    tok_rows = rows.shape[0] // seq_count
    moved = lax.all_to_all(rows, "seq", split_axis=0, concat_axis=0, tiled=True)
    moved = moved.reshape(seq_count, tok_rows, grp_count, row_unit).transpose(1, 2, 0, 3)
    return moved.reshape(tok_rows, grp_count * seq_count * row_unit)


def plain_mlp(normed_two, cotangent_all, mlp_weight):
    contract_last, contract_first = CONTRACT_LAST, CONTRACT_FIRST
    mlp_rows = lax.all_gather(mlp_weight, "grp", axis=0, tiled=True)
    normed_two_all = lax.all_gather(normed_two, "seq", axis=0, tiled=True)
    gate_rows, upper_rows, down_rows = mlp_rows[:, 0, :], mlp_rows[:, 1, :], mlp_rows[:, 2, :]
    gate_vals = lax.dot_general(
        normed_two_all, gate_rows, contract_last, preferred_element_type=jnp.float32
    )
    upper_vals = lax.dot_general(
        normed_two_all, upper_rows, contract_last, preferred_element_type=jnp.float32
    )
    unit_wide, pull_back = jax.vjp(swish_product, gate_vals, upper_vals)
    unit_low = unit_wide.astype(jnp.bfloat16)
    unit_grad = lax.dot_general(
        cotangent_all, down_rows, contract_last, preferred_element_type=jnp.float32
    )
    gate_grad, upper_grad = pull_back(unit_grad)
    gate_grad = gate_grad.astype(jnp.bfloat16)
    upper_grad = upper_grad.astype(jnp.bfloat16)
    input_grad = jnp.dot(gate_grad, gate_rows, preferred_element_type=jnp.float32) + jnp.dot(
        upper_grad, upper_rows, preferred_element_type=jnp.float32
    )
    grad_part = lax.psum_scatter(
        input_grad.astype(jnp.bfloat16), "seq", scatter_dimension=0, tiled=True
    ).astype(jnp.float32)
    out_part = lax.psum_scatter(
        jnp.dot(unit_low, down_rows, preferred_element_type=jnp.float32).astype(jnp.bfloat16),
        "seq",
        scatter_dimension=0,
        tiled=True,
    ).astype(jnp.float32)
    mlp_terms = jnp.stack(
        [
            lax.dot_general(
                gate_grad, normed_two_all, contract_first, preferred_element_type=jnp.float32
            ),
            lax.dot_general(
                upper_grad, normed_two_all, contract_first, preferred_element_type=jnp.float32
            ),
            lax.dot_general(
                unit_low, cotangent_all, contract_first, preferred_element_type=jnp.float32
            ),
        ],
        axis=1,
    )
    mlp_grad = lax.psum_scatter(mlp_terms, "grp", scatter_dimension=0, tiled=True)
    return grad_part, out_part, mlp_grad


def padded_rows(mlp_weight):
    rows = mlp_weight.transpose(1, 0, 2)
    return jnp.pad(rows, ((0, 0), (0, -rows.shape[1] % 32), (0, 0)))


def from_peer(values, offset, grp_count):
    return lax.ppermute(values, "grp", [(g, g ^ offset) for g in range(grp_count)])


def exchange_blocks(rows, grp_count):
    return [rows] + [from_peer(rows, offset, grp_count) for offset in range(1, grp_count)]


def sum_blocks(terms, grp_count):
    block = terms.shape[1] // grp_count
    total = terms[:, :block].astype(jnp.float32)
    for offset in range(1, grp_count):
        piece = terms[:, offset * block : (offset + 1) * block]
        total = total + from_peer(piece, offset, grp_count).astype(jnp.float32)
    return total


def per_device(
    tokens,
    cotangent,
    shard_segment,
    gain_attn,
    qkv_weight,
    qkv_bias,
    out_weight,
    gain_mlp,
    mlp_weight,
):
    tok_rows = tokens.shape[0]
    seq_count = lax.axis_size("seq")
    grp_count = lax.axis_size("grp")
    group_tok = tok_rows * seq_count
    heads_per = H // KVH
    kv_width = KVH * HD
    att_width = H * HD
    query_rows = heads_per * tok_rows
    score_scale = 1.0 / math.sqrt(HD)
    contract_last = CONTRACT_LAST
    contract_first = CONTRACT_FIRST
    seq_place = lax.axis_index("seq")
    grp_place = lax.axis_index("grp")
    segments = lax.dynamic_index_in_dim(shard_segment, grp_place, 0, keepdims=False)
    starts = shard_starts(segments, tok_rows, group_tok // 2)
    shard_order = jnp.arange(seq_count, dtype=jnp.int32)
    own_seg = jnp.sum(jnp.where(shard_order == seq_place, segments, 0))
    own_start = jnp.sum(jnp.where(shard_order == seq_place, starts, 0))
    positions = own_start + jnp.arange(tok_rows, dtype=jnp.int32)
    cosine_table, sine_table = rotary_tables(positions, HD)
    query_pos = jnp.tile(positions, heads_per)
    tokens_wide = tokens.astype(jnp.float32)
    gain_one = gain_attn.astype(jnp.float32)
    gain_two = gain_mlp.astype(jnp.float32)
    normed_one = rms_scale(tokens_wide, gain_one).astype(jnp.bfloat16)
    use_kernels = (seq_count, grp_count, H, KVH, HD) == (8, 4, 12, 2, 128)
    if use_kernels:
        chips = seq_count // 2
        lanes = jnp.arange(HD)
        all_pos = (starts[:, None] + jnp.arange(tok_rows, dtype=jnp.int32)[None, :]).reshape(-1)
        all_cosine, all_sine = rotary_tables(all_pos, HD)
        all_sine = jnp.where(lanes < HD // 2, -all_sine, all_sine)
        by_shard = lambda table: table.reshape(chips, 2, tok_rows, HD)
        key_pos = all_pos.reshape(chips, 2, tok_rows).swapaxes(0, 1).reshape(-1)
        key_seg = jnp.repeat(segments.reshape(chips, 2).swapaxes(0, 1).reshape(-1), tok_rows)
        visible = ((key_seg == 0) | (key_seg == own_seg))[None, :] & (
            key_pos[None, :] <= positions[:, None]
        )
        mask = jnp.where(visible, 0.0, -1e30).astype(jnp.float32)
        bias_half = qkv_bias.astype(jnp.float32)
        bias_pair = jnp.concatenate([bias_half, jnp.zeros_like(bias_half)])
        bias_row = jnp.where(seq_place % 2 == 0, bias_pair, jnp.roll(bias_pair, HD // 2))
        bias_rows8 = jnp.broadcast_to(bias_row[None, :], (8, HD))
        own_rows = padded_rows(mlp_weight)
        (
            attn_wide, lse, q_heads, kv_heads, n1_all, cot_all, out_all, qkv_all, *peer_rows
        ) = front_call(
            normed_one, cotangent, qkv_weight, bias_rows8, out_weight, own_rows,
            by_shard(all_cosine), by_shard(all_sine), mask,
        )
        mlp_blocks = [own_rows, *peer_rows]
        normed_one_all = n1_all.reshape(group_tok, -1)
        cotangent_all = cot_all.reshape(group_tok, -1)
        out_full = out_all.reshape(att_width, -1)
        query_rot = q_heads.transpose(2, 1, 0, 3).reshape(tok_rows, H, HD)
        kv_rows = kv_heads.reshape(2, KVH, 2, chips, tok_rows, HD).transpose(0, 3, 2, 4, 1, 5)
        keys_all, values_all = kv_rows.reshape(2, group_tok, kv_width)
    else:
        normed_one_all = lax.all_gather(normed_one, "seq", axis=0, tiled=True)
        qkv_rows = lax.all_gather(qkv_weight, "grp", axis=0, tiled=True)
        bias_rows = lax.all_gather(qkv_bias, "grp", axis=0, tiled=True)
        cotangent_all = lax.all_gather(cotangent, "seq", axis=0, tiled=True)
        out_full = lax.all_gather(out_weight, AXES, axis=0, tiled=True)
        projected = lax.dot_general(
            normed_one_all, qkv_rows, contract_last, preferred_element_type=jnp.float32
        )
        projected = (projected + bias_rows.astype(jnp.float32)[None, :]).astype(jnp.bfloat16)
        projected = owners_to_columns(projected, qkv_weight.shape[0]).astype(jnp.float32)
        query_rot = rotate(
            projected[:, :att_width].reshape(tok_rows, H, HD), cosine_table, sine_table
        ).astype(jnp.bfloat16)
        key_rot = rotate(
            projected[:, att_width : att_width + kv_width].reshape(tok_rows, KVH, HD),
            cosine_table,
            sine_table,
        ).astype(jnp.bfloat16)
        value_low = projected[:, att_width + kv_width :].astype(jnp.bfloat16)
        keys_all, values_all = (
            lax.all_gather(key_rot.reshape(tok_rows, kv_width), "seq", axis=0, tiled=True),
            lax.all_gather(value_low, "seq", axis=0, tiled=True),
        )
    queries = (
        query_rot.reshape(tok_rows, KVH, heads_per, HD)
        .transpose(1, 2, 0, 3)
        .reshape(KVH, query_rows, HD)
    )
    key_block = min(512, group_tok)
    block_count = group_tok // key_block
    block_order = jnp.arange(block_count, dtype=jnp.int32)

    def block_mask(block_index):
        key_index = block_index * key_block + jnp.arange(key_block, dtype=jnp.int32)
        key_shard = key_index // tok_rows
        onehot = key_shard[:, None] == shard_order[None, :]
        key_seg = jnp.sum(jnp.where(onehot, segments[None, :], 0), axis=1)
        key_pos = jnp.sum(jnp.where(onehot, starts[None, :], 0), axis=1) + key_index % tok_rows
        visible = (key_seg == 0) | (key_seg == own_seg)
        return visible[None, :] & (key_pos[None, :] <= query_pos[:, None])

    def block_keys(block_index):
        key_part = lax.dynamic_slice_in_dim(
            keys_all, block_index * key_block, key_block, 0
        ).reshape(key_block, KVH, HD)
        value_part = lax.dynamic_slice_in_dim(
            values_all, block_index * key_block, key_block, 0
        ).reshape(key_block, KVH, HD)
        return (key_part, value_part)

    def block_scores(key_part):
        return (
            jnp.einsum("krd,jkd->krj", queries, key_part, preferred_element_type=jnp.float32)
            * score_scale
        )

    if use_kernels:
        log_total = lse[:, :, 0]
    else:
        def stat_step(stats_now, block_index):
            allowed = block_mask(block_index)

            def stat_visit(current):
                top_old, total_old = current
                key_part, value_part = block_keys(block_index)
                scores = jnp.where(allowed[None], block_scores(key_part), -1e30)
                top_new = jnp.maximum(top_old, jnp.max(scores, axis=-1))
                weights = jnp.where(allowed[None], jnp.exp(scores - top_new[..., None]), 0.0)
                return (top_new, total_old * jnp.exp(top_old - top_new) + jnp.sum(weights, axis=-1))

            return (lax.cond(jnp.any(allowed), stat_visit, lambda current: current, stats_now), None)

        start_stats = (
            jnp.full((KVH, query_rows), -1e30, jnp.float32),
            jnp.zeros((KVH, query_rows), jnp.float32),
        )
        (top_all, total_all), unused = lax.scan(stat_step, start_stats, block_order)
        log_total = top_all + jnp.log(total_all)

        def mix_step(mixed_sum, block_index):
            allowed = block_mask(block_index)

            def mix_visit(current):
                key_part, value_part = block_keys(block_index)
                prob_low = jnp.where(
                    allowed[None], jnp.exp(block_scores(key_part) - log_total[..., None]), 0.0
                ).astype(jnp.bfloat16)
                return current + jnp.einsum(
                    "krj,jkd->krd", prob_low, value_part, preferred_element_type=jnp.float32
                )

            return (lax.cond(jnp.any(allowed), mix_visit, lambda current: current, mixed_sum), None)

        mixed_sum, unused = lax.scan(
            mix_step, jnp.zeros((KVH, query_rows, HD), jnp.float32), block_order
        )
        attn_wide = (
            mixed_sum.reshape(KVH, heads_per, tok_rows, HD)
            .transpose(2, 0, 1, 3)
            .reshape(tok_rows, att_width)
        )
    attn_low = attn_wide.astype(jnp.bfloat16)
    attn_proj = jnp.dot(attn_low, out_full, preferred_element_type=jnp.float32)
    state = tokens_wide + attn_proj
    normed_two = rms_scale(state, gain_two).astype(jnp.bfloat16)
    if use_kernels:
        grad_part, out_part, mlp_terms = mlp_call(
            normed_two, cotangent_all.reshape(seq_count, tok_rows, -1), mlp_blocks
        )
        output = (state + out_part).astype(jnp.bfloat16)
        gains = jnp.stack([gain_one, gain_two])[:, None, :]
        token_grad, qkv_terms, out_grad, gain_sums, mlp_sums = back_call(
            grad_part, state, cotangent, tokens, gains, attn_wide, q_heads, kv_heads, mask,
            by_shard(all_cosine), by_shard(all_sine), qkv_all.reshape(-1, qkv_all.shape[-1]),
            out_full, n1_all, mlp_terms,
        )
        width = tokens.shape[1]
        own = width // (grp_count * seq_count)
        gain_parts = lax.dynamic_slice_in_dim(
            gain_sums[:, 0], (grp_place * seq_count + seq_place) * own, own, 1
        )
        return (
            output,
            token_grad,
            gain_parts[0],
            qkv_terms[:, :width],
            qkv_terms[:, width],
            out_grad,
            gain_parts[1],
            mlp_sums[:, : mlp_weight.shape[0]].transpose(1, 0, 2),
        )
    grad_part, out_part, mlp_grad = plain_mlp(normed_two, cotangent_all, mlp_weight)
    output = (state + out_part).astype(jnp.bfloat16)
    unused_state, norm_two_back = jax.vjp(rms_scale, state, gain_two)
    state_norm_grad, gain_two_grad = norm_two_back(grad_part)
    state_grad = state_norm_grad + cotangent.astype(jnp.float32)
    state_low = state_grad.astype(jnp.bfloat16)
    attn_grad = lax.dot_general(
        state_low, out_full, contract_last, preferred_element_type=jnp.float32
    )
    attn_grad_low = attn_grad.astype(jnp.bfloat16)
    attn_owned = columns_to_owners(attn_low, out_weight.shape[0])
    state_low_all = lax.all_gather(state_low, "seq", axis=0, tiled=True)
    out_grad = lax.psum_scatter(
        lax.dot_general(
            attn_owned, state_low_all, contract_first, preferred_element_type=jnp.float32
        ),
        "grp",
        scatter_dimension=0,
        tiled=True,
    )
    grad_heads = (
        attn_grad_low.reshape(tok_rows, KVH, heads_per, HD)
        .transpose(1, 2, 0, 3)
        .reshape(KVH, query_rows, HD)
    )
    delta_rows = jnp.sum(
        (attn_grad_low.astype(jnp.float32) * attn_wide).reshape(tok_rows, H, HD), axis=-1
    )
    delta_rows = (
        delta_rows.reshape(tok_rows, KVH, heads_per).transpose(1, 2, 0).reshape(KVH, query_rows)
    )

    def back_step(query_grad, block_index):
        allowed = block_mask(block_index)

        def back_visit(current):
            key_part, value_part = block_keys(block_index)
            prob_vals = jnp.where(
                allowed[None], jnp.exp(block_scores(key_part) - log_total[..., None]), 0.0
            )
            prob_grad = jnp.einsum(
                "krd,jkd->krj", grad_heads, value_part, preferred_element_type=jnp.float32
            )
            score_grad = (prob_vals * (prob_grad - delta_rows[..., None])).astype(jnp.bfloat16)
            new_grad = (
                current
                + jnp.einsum(
                    "krj,jkd->krd", score_grad, key_part, preferred_element_type=jnp.float32
                )
                * score_scale
            )
            key_grad = (
                jnp.einsum("krj,krd->jkd", score_grad, queries, preferred_element_type=jnp.float32)
                * score_scale
            )
            value_grad = jnp.einsum(
                "krj,krd->jkd",
                prob_vals.astype(jnp.bfloat16),
                grad_heads,
                preferred_element_type=jnp.float32,
            )
            return (
                new_grad,
                (key_grad.reshape(key_block, kv_width), value_grad.reshape(key_block, kv_width)),
            )

        def skip_block(current):
            blank_rows = jnp.zeros((key_block, kv_width), jnp.float32)
            return (current, (blank_rows, blank_rows))

        return lax.cond(jnp.any(allowed), back_visit, skip_block, query_grad)

    query_grad, (key_grads, value_grads) = lax.scan(
        back_step, jnp.zeros((KVH, query_rows, HD), jnp.float32), block_order
    )
    key_own, value_own = (
        lax.psum_scatter(
            key_grads.reshape(group_tok, kv_width).astype(jnp.bfloat16),
            "seq",
            scatter_dimension=0,
            tiled=True,
        ).astype(jnp.float32),
        lax.psum_scatter(
            value_grads.reshape(group_tok, kv_width).astype(jnp.bfloat16),
            "seq",
            scatter_dimension=0,
            tiled=True,
        ).astype(jnp.float32),
    )
    query_back = unrotate(
        query_grad.reshape(KVH, heads_per, tok_rows, HD)
        .transpose(2, 0, 1, 3)
        .reshape(tok_rows, H, HD),
        cosine_table,
        sine_table,
    )
    key_back = unrotate(key_own.reshape(tok_rows, KVH, HD), cosine_table, sine_table)
    qkv_grad_low = jnp.concatenate(
        [query_back.reshape(tok_rows, att_width), key_back.reshape(tok_rows, kv_width), value_own],
        axis=1,
    ).astype(jnp.bfloat16)
    qkv_grad_owned = columns_to_owners(qkv_grad_low, qkv_weight.shape[0])
    bias_terms = jnp.sum(qkv_grad_owned.astype(jnp.float32), axis=0)
    normed_one_grad = lax.psum_scatter(
        jnp.dot(qkv_grad_owned, qkv_rows, preferred_element_type=jnp.float32).astype(jnp.bfloat16),
        "seq",
        scatter_dimension=0,
        tiled=True,
    ).astype(jnp.float32)
    qkv_grad = lax.psum_scatter(
        lax.dot_general(
            qkv_grad_owned, normed_one_all, contract_first, preferred_element_type=jnp.float32
        ),
        "grp",
        scatter_dimension=0,
        tiled=True,
    )
    unused_tokens, norm_one_back = jax.vjp(rms_scale, tokens_wide, gain_one)
    token_norm_grad, gain_one_grad = norm_one_back(normed_one_grad)
    token_grad = token_norm_grad + state_grad
    bias_part = lax.psum_scatter(bias_terms, "grp", scatter_dimension=0, tiled=True)
    gain_one_part, gain_two_part = (
        lax.psum_scatter(gain_one_grad, AXES, scatter_dimension=0, tiled=True),
        lax.psum_scatter(gain_two_grad, AXES, scatter_dimension=0, tiled=True),
    )
    return (
        output,
        token_grad,
        gain_one_part,
        qkv_grad,
        bias_part,
        out_grad,
        gain_two_part,
        mlp_grad,
    )


def solution(mesh):
    return jax.shard_map(
        per_device,
        mesh=mesh,
        in_specs=(
            P(("grp", "seq"), None),
            P(("grp", "seq"), None),
            P(),
            P(),
            P(("grp", "seq"), None),
            P(("grp", "seq")),
            P(("grp", "seq"), None),
            P(),
            P(("grp", "seq"), None, None),
        ),
        out_specs=(
            P(("grp", "seq"), None),
            P(("grp", "seq"), None),
            P(("grp", "seq")),
            P(("grp", "seq"), None),
            P(("grp", "seq")),
            P(("grp", "seq"), None),
            P(("grp", "seq")),
            P(("grp", "seq"), None, None),
        ),
        check_vma=False,
    )
```

```python
import functools
import math

import jax
import jax.numpy as jnp
from jax import lax
from jax.experimental import pallas as pl
from jax.experimental.pallas import tpu as pltpu
from jax.sharding import PartitionSpec as P

H = 12
KVH = 2
HD = 128
FF = 8960


EPS = 1e-06
THETA = 10000.0


def rms_scale(values, gain_vec):
    return values * lax.rsqrt(jnp.mean(values * values, axis=-1, keepdims=True) + EPS) * gain_vec


def rotary_tables(positions, head_dim):
    half_dim = head_dim // 2
    freqs = THETA ** (-(jnp.arange(half_dim, dtype=jnp.float32) * 2.0) / head_dim)
    angles = positions.astype(jnp.float32)[:, None] * freqs[None, :]
    cosine_table = jnp.concatenate([jnp.cos(angles), jnp.cos(angles)], axis=-1)
    sine_table = jnp.concatenate([jnp.sin(angles), jnp.sin(angles)], axis=-1)
    return (cosine_table, sine_table)


def rotate(values, cosine_table, sine_table):
    half_dim = values.shape[-1] // 2
    turned = jnp.concatenate([-values[..., half_dim:], values[..., :half_dim]], axis=-1)
    return values * cosine_table[:, None, :] + turned * sine_table[:, None, :]


def unrotate(grad_rows, cosine_table, sine_table):
    half_dim = grad_rows.shape[-1] // 2
    scaled = grad_rows * sine_table[:, None, :]
    turned = jnp.concatenate([scaled[..., half_dim:], -scaled[..., :half_dim]], axis=-1)
    return grad_rows * cosine_table[:, None, :] + turned


def shard_starts(segments, tok_dev, prompt_len):
    shard_total = segments.shape[0]
    shard_order = jnp.arange(shard_total, dtype=jnp.int32)
    same_seg = segments[:, None] == segments[None, :]
    first_shard = jnp.min(jnp.where(same_seg, shard_order[None, :], shard_total), axis=1)
    cont_start = prompt_len + (shard_order - first_shard) * tok_dev
    return jnp.where(segments == 0, shard_order * tok_dev, cont_start)


def swish_product(gate_vals, upper_vals):
    return jax.nn.silu(gate_vals) * upper_vals


AXES = ("grp", "seq")
CONTRACT_LAST = (((1,), (1,)), ((), ()))
CONTRACT_FIRST = (((0,), (0,)), ((), ()))


MESH = pl.DeviceIdType.MESH


def remote(src, dst, send_sem, recv_sem, grp, seq):
    return pltpu.make_async_remote_copy(
        src_ref=src, dst_ref=dst, send_sem=send_sem, recv_sem=recv_sem,
        device_id=(grp, seq), device_id_type=MESH,
    )


def nearest_chip(place, order, chips):
    both = 2 * jnp.minimum(place, chips - 1 - place)
    offset = (order + 1) // 2
    near = jnp.where(order % 2 == 1, place - offset, place + offset)
    rest = jnp.where(place < chips - 1 - place, order, chips - 1 - order)
    return jnp.where(order <= both, near, rest)


class Place:
    def __init__(self, chips):
        self.chips = chips
        self.grp, self.seq = lax.axis_index("grp"), lax.axis_index("seq")
        self.chip, self.core = self.seq // 2, self.seq % 2
        self.mate = self.seq + 1 - 2 * self.core

    def peer(self, offset):
        low, high = self.grp % 2, self.grp // 2
        low = 1 - low if offset % 2 else low
        high = 1 - high if offset // 2 else high
        return 2 * high + low

    def barrier(self, grps):
        barrier = pltpu.get_barrier_semaphore()
        for chip in range(self.chips):
            @pl.when(chip != self.chip)
            def _(chip=chip):
                pl.semaphore_signal(
                    barrier, inc=1, device_id=(self.grp, 2 * chip + self.core), device_id_type=MESH
                )
        pl.semaphore_signal(barrier, inc=1, device_id=(self.grp, self.mate), device_id_type=MESH)
        for offset in range(1, grps):
            pl.semaphore_signal(
                barrier, inc=1, device_id=(self.peer(offset), self.seq), device_id_type=MESH
            )
        pl.semaphore_wait(barrier, self.chips - 1 + 1 + grps - 1)


class RailGather:
    def __init__(self, place, view, send_sem, recv_sem):
        self.place, self.view, self.send_sem, self.recv_sem = place, view, send_sem, recv_sem

    def copy(self, way, chip, core):
        p = self.place
        to = (p.seq + 2, p.seq - 2, p.mate)[way]
        return remote(
            self.view(chip, core), self.view(chip, core), self.send_sem.at[way, chip],
            self.recv_sem.at[chip, core], p.grp, to,
        )

    def start(self):
        p = self.place
        pl.when(p.chip < p.chips - 1)(lambda: self.copy(0, p.chip, p.core).start())
        pl.when(p.chip > 0)(lambda: self.copy(1, p.chip, p.core).start())
        self.copy(2, p.chip, p.core).start()

    def forward(self, step):
        p = self.place

        @pl.when(p.chip - step >= 0)
        def _():
            chip = p.chip - step
            self.copy(2, chip, p.core).wait_recv()
            pl.when(p.chip < p.chips - 1)(lambda: self.copy(0, chip, p.core).start())
            self.copy(2, chip, p.core).start()

        @pl.when(p.chip + step < p.chips)
        def _():
            chip = p.chip + step
            self.copy(2, chip, p.core).wait_recv()
            pl.when(p.chip > 0)(lambda: self.copy(1, chip, p.core).start())
            self.copy(2, chip, p.core).start()

    def wait_mate(self, chip):
        self.copy(2, chip, 1 - self.place.core).wait_recv()

    def drain(self):
        p = self.place
        for chip in range(p.chips):
            self.copy(2, chip, p.core).wait_send()
            pl.when((chip <= p.chip) & (p.chip < p.chips - 1))(
                lambda chip=chip: self.copy(0, chip, p.core).wait_send()
            )
            pl.when((chip >= p.chip) & (p.chip > 0))(
                lambda chip=chip: self.copy(1, chip, p.core).wait_send()
            )


class LineScatter:
    def __init__(self, place, part, mate_in, left_in, right_in, send_sem, recv_sem):
        self.place, self.part = place, part
        self.mate_in, self.left_in, self.right_in = mate_in, left_in, right_in
        self.send_sem, self.recv_sem = send_sem, recv_sem

    def copy(self, way, src, landing, r, chip, to):
        return remote(
            src, landing.at[r, chip], self.send_sem.at[way, r, chip], self.recv_sem.at[way, r, chip],
            self.place.grp, to,
        )

    def to_mate(self, r, chip):
        p = self.place
        return self.copy(0, self.part.at[r, 2 * chip + 1 - p.core], self.mate_in, r, chip, p.mate)

    def to_right(self, r, chip):
        p = self.place
        return self.copy(1, self.part.at[r, 2 * chip + p.core], self.left_in, r, chip, p.seq + 2)

    def to_left(self, r, chip):
        p = self.place
        return self.copy(2, self.part.at[r, 2 * chip + p.core], self.right_in, r, chip, p.seq - 2)

    def step(self, r, chip):
        p = self.place
        last = p.chips - 1
        slot = 2 * chip + p.core

        @pl.when(chip != p.chip)
        def _():
            self.to_mate(r, chip).wait_recv()
            total = self.part[r, slot].astype(jnp.float32) + self.mate_in[r, chip].astype(jnp.float32)
            self.part[r, slot] = total.astype(jnp.bfloat16)

        @pl.when(chip > p.chip)
        def _():
            @pl.when(p.chip > 0)
            def _():
                self.to_right(r, chip).wait_recv()
                self.part[r, slot] = (
                    self.part[r, slot].astype(jnp.float32) + self.left_in[r, chip].astype(jnp.float32)
                ).astype(jnp.bfloat16)

            self.to_right(r, chip).start()

        @pl.when(chip < p.chip)
        def _():
            @pl.when(p.chip < last)
            def _():
                self.to_left(r, chip).wait_recv()
                self.part[r, slot] = (
                    self.part[r, slot].astype(jnp.float32) + self.right_in[r, chip].astype(jnp.float32)
                ).astype(jnp.bfloat16)

            self.to_left(r, chip).start()

    def finish(self, r, out_ref):
        p = self.place
        self.to_mate(r, p.chip).wait_recv()
        out_ref[...] = self.part[r, p.seq].astype(jnp.float32) + self.mate_in[r, p.chip].astype(jnp.float32)

        @pl.when(p.chip > 0)
        def _():
            self.to_right(r, p.chip).wait_recv()
            out_ref[...] += self.left_in[r, p.chip].astype(jnp.float32)

        @pl.when(p.chip < p.chips - 1)
        def _():
            self.to_left(r, p.chip).wait_recv()
            out_ref[...] += self.right_in[r, p.chip].astype(jnp.float32)

    def drain(self, r):
        p = self.place
        for other in range(p.chips):
            self.to_mate(r, other).wait_send()
            pl.when(other > p.chip)(lambda other=other: self.to_right(r, other).wait_send())
            pl.when(other < p.chip)(lambda other=other: self.to_left(r, other).wait_send())


def front_kernel(chips, scale,
                 tokens_ref, gains_ref, cot_ref, wq_ref, bias_ref, wo_ref, wm_ref, cos_ref, sin_ref, mask_ref,
                 attn_ref, state_ref, q_out_ref, kv_out_ref, n1_all_ref, n2_all_ref, cot_all_ref, wo_all_ref,
                 wq_all_ref, columns_ref, wm1_ref, wm2_ref, wm3_ref,
                 nbuf, n2buf, wq, wo, bias, stage, qbuf, kvbuf, columns,
                 lsem, n_send, n_recv, n2_send, n2_recv, c_send, c_recv, o_send, o_recv, ox_send, ox_recv,
                 om_send, om_recv, wq_send, wq_recv, b_send, b_recv, m_send, m_recv, q_send, q_recv, k_send, k_recv):
    p = Place(chips)
    grps = 4
    half = wq_ref.shape[0]
    rows = pl.ds(p.core * half, half)
    mates_rows = pl.ds((1 - p.core) * half, half)
    wm_refs = (wm_ref, wm1_ref, wm2_ref, wm3_ref)
    part = wm_ref.shape[1] // 2

    own = [
        pltpu.make_async_copy(wq_ref, wq.at[0, rows], lsem.at[0]),
        pltpu.make_async_copy(bias_ref, bias.at[0, p.core], lsem.at[1]),
        pltpu.make_async_copy(wo_ref, wo.at[p.grp, p.chip, p.core], lsem.at[2]),
        pltpu.make_async_copy(cot_ref, cot_all_ref.at[p.chip, p.core], lsem.at[3]),
    ]
    for copy in own:
        copy.start()
    tokens = tokens_ref[...].astype(jnp.float32)
    nbuf[p.chip, p.core] = rms_scale(tokens, gains_ref[0]).astype(jnp.bfloat16)
    p.barrier(grps)

    n1_line = RailGather(p, lambda chip, core: nbuf.at[chip, core], n_send, n_recv)
    cot_line = RailGather(p, lambda chip, core: cot_all_ref.at[chip, core], c_send, c_recv)
    n2_line = RailGather(p, lambda chip, core: n2buf.at[chip, core], n2_send, n2_recv)
    out_line = RailGather(p, lambda chip, core: wo.at[p.grp, chip, core], o_send, o_recv)

    def wq_direct(b):
        return remote(wq_ref, wq.at[b, rows], wq_send.at[0, b], wq_recv.at[b, 0], p.peer(b), p.seq)

    def wq_mate(b):
        return remote(wq.at[b, rows], wq.at[b, rows], wq_send.at[1, b], wq_recv.at[b, 1], p.grp, p.mate)

    def bias_direct(b):
        return remote(bias_ref, bias.at[b, p.core], b_send.at[0, b], b_recv.at[b, 0], p.peer(b), p.seq)

    def bias_mate(b):
        return remote(bias.at[b, p.core], bias.at[b, p.core], b_send.at[1, b], b_recv.at[b, 1], p.grp, p.mate)

    def m_half(ref, i):
        return ref.at[:, pl.ds(i * part, part)]

    def m_direct(b, i):
        return remote(m_half(wm_ref, i), m_half(wm_refs[b], i), m_send.at[b, i], m_recv.at[b, i], p.peer(b), p.seq)

    def m_forward(b):
        return remote(
            m_half(wm_refs[b], b - 1), m_half(wm3_ref, b - 1), m_send.at[3, b - 1], m_recv.at[3, b - 1],
            p.peer(3 - b), p.seq,
        )

    def out_view(grp, i, core):
        return wo.at[grp, pl.ds(i * (chips // 2), chips // 2), core]

    def out_direct(b, i):
        view = out_view(p.grp, i, p.core)
        return remote(view, view, ox_send.at[b, i], ox_recv.at[b, i], p.peer(b), p.seq)

    def out_forward(b):
        view = out_view(p.peer(b), b - 1, p.core)
        return remote(view, view, ox_send.at[3, b - 1], ox_recv.at[3, b - 1], p.peer(3 - b), p.seq)

    def out_mate(b, i, core):
        view = out_view(p.peer(b), i, core)
        return remote(view, view, om_send.at[b, i], om_recv.at[b, i], p.grp, p.mate)

    def q_copy(chip):
        return remote(
            stage.at[chip, pl.ds(0, 3)], qbuf.at[p.chip], q_send.at[chip], q_recv.at[p.chip],
            p.grp, 2 * chip + p.core,
        )

    def q_arrival(chip):
        return remote(stage.at[chip, pl.ds(0, 3)], qbuf.at[chip], q_send.at[chip], q_recv.at[chip], p.grp, p.mate)

    def k_copy(chip, to_chip):
        return remote(
            stage.at[chip, 3], kvbuf.at[p.chip, p.core, chip], k_send.at[0, chip, to_chip],
            k_recv.at[p.chip, p.core, chip], p.grp, 2 * to_chip + p.core,
        )

    def k_mate(head, chip, src=None):
        view = kvbuf.at[head, p.core, chip]
        return remote(
            view if src is None else src, view, k_send.at[1, head, chip],
            k_recv.at[head, p.core, chip], p.grp, p.mate,
        )

    def k_arrival(head, core, chip):
        view = kvbuf.at[head, core, chip]
        return remote(view, view, k_send.at[1, head, chip], k_recv.at[head, core, chip], p.grp, p.mate)

    own[0].wait()
    own[1].wait()
    for b in range(1, grps):
        wq_direct(b).start()
        bias_direct(b).start()
    wq_mate(0).start()
    bias_mate(0).start()
    n1_line.start()
    own[2].wait()
    out_line.start()
    for b in range(1, grps):
        wq_direct(b).wait_recv()
        wq_mate(b).start()
        bias_direct(b).wait_recv()
        bias_mate(b).start()
    m_direct(1, 0).start()
    m_direct(2, 1).start()
    for b in range(grps):
        wq_mate(b).wait_recv()
        bias_mate(b).wait_recv()

    @pl.loop(0, chips)
    def _(order):
        @pl.when(order > 0)
        def _():
            n1_line.forward(order)
            out_line.forward(order)

        at = nearest_chip(p.chip, order, chips)
        x = nbuf[at, p.core]
        weights = wq[...].reshape(grps * 2 * half, x.shape[1])
        rows_all = lax.dot_general(x, weights, CONTRACT_LAST, preferred_element_type=jnp.float32)
        cosine, sine = cos_ref[at, p.core], sin_ref[at, p.core]
        for b in range(grps):
            u = rows_all[:, 2 * half * b : 2 * half * (b + 1)] + (bias[b, 0, 0:1] + bias[b, 1, 0:1])
            turned = u * cosine + pltpu.roll(u, half, 1) * sine
            place = p.peer(b)
            keep = jnp.where((place == grps - 1) & (p.chip >= chips // 2), 1.0, 0.0)
            value = (u * keep + turned * (1.0 - keep)).astype(jnp.bfloat16)
            stage[at, place] = value

            @pl.when(place == grps - 1)
            def _(value=value):
                kvbuf[p.chip, p.core, at] = value

            @pl.when((place < grps - 1) & (at == p.chip))
            def _(value=value, place=place):
                qbuf[p.chip, place] = value

        pl.when(at != p.chip)(lambda: q_copy(at).start())
        for to_chip in range(chips):
            pl.when(to_chip != p.chip)(lambda to_chip=to_chip: k_copy(at, to_chip).start())
        k_mate(p.chip, at, stage.at[at, 3]).start()

    for b in (1, 2):
        out_direct(b, b - 1).start()
    for b in (1, 2):
        out_direct(b, 2 - b).start()
    own[3].wait()
    cot_line.start()

    @pl.loop(0, chips)
    def _(order):
        for head in range(chips):
            @pl.when(head != p.chip)
            def _(head=head):
                chip = nearest_chip(head, order, chips)
                k_arrival(head, p.core, chip).wait_recv()
                k_mate(head, chip).start()

    for chip in range(chips):
        pl.when(chip != p.chip)(lambda chip=chip: q_arrival(chip).wait_recv())
        for head in range(chips):
            k_arrival(head, 1 - p.core, chip).wait_recv()
    cot_line.forward(1)

    mask = mask_ref[...]
    shard = mask.shape[0]
    heads_per = H // KVH
    for kv in range(KVH):
        heads = [kv * heads_per + i for i in range(heads_per)]
        queries = jnp.concatenate([qbuf[h % chips, h // chips] for h in heads], axis=0)
        keys = kvbuf[kv].reshape(mask.shape[1], 2 * half)
        values = kvbuf[KVH + kv].reshape(mask.shape[1], 2 * half)
        scores = lax.dot_general(queries, keys, CONTRACT_LAST, preferred_element_type=jnp.float32) * scale
        scores = scores.reshape(heads_per, shard, mask.shape[1]) + mask[None]
        weights = jnp.exp(scores - jnp.max(scores, axis=-1, keepdims=True))
        inverse = 1.0 / jnp.sum(weights, axis=-1, keepdims=True)
        probs = (weights * inverse).astype(jnp.bfloat16).reshape(heads_per * shard, mask.shape[1])
        mixed = jnp.dot(probs, values, preferred_element_type=jnp.float32)
        for i, h in enumerate(heads):
            attn_ref[:, h * 2 * half : (h + 1) * 2 * half] = mixed[i * shard : (i + 1) * shard]
        if kv == 0:
            for b in (1, 2):
                out_direct(b, b - 1).wait_recv()
                out_forward(b).start()
                out_mate(b, b - 1, p.core).start()
        cot_line.forward(kv + 2)

    for b in (1, 2):
        out_direct(b, 2 - b).wait_recv()
        out_mate(b, 2 - b, p.core).start()
    for b in (1, 2):
        m_direct(b, b - 1).wait_recv()
        m_forward(b).start()
    m_direct(1, 1).start()
    m_direct(2, 0).start()
    attn_low = attn_ref[...].astype(jnp.bfloat16)
    unit = wo.shape[3]
    columns[...] = attn_low.T.reshape(columns.shape)
    for i in (0, 1):
        out_forward(i + 1).wait_recv()
        out_mate(3, i, p.core).start()
    for b in range(1, grps):
        for i in (0, 1):
            out_mate(b, i, 1 - p.core).wait_recv()
    for chip in range(chips):
        out_line.wait_mate(chip)
    state = tokens_ref[...].astype(jnp.float32) + jnp.dot(
        attn_low, wo[...].reshape(grps * chips * 2 * unit, tokens_ref.shape[1]),
        preferred_element_type=jnp.float32,
    )
    state_ref[...] = state
    n2buf[p.chip, p.core] = rms_scale(state, gains_ref[1]).astype(jnp.bfloat16)
    n2_line.start()
    outs = [
        pltpu.make_async_copy(nbuf, n1_all_ref, lsem.at[4]),
        pltpu.make_async_copy(wq, wq_all_ref, lsem.at[5]),
        pltpu.make_async_copy(qbuf, q_out_ref, lsem.at[6]),
        pltpu.make_async_copy(kvbuf, kv_out_ref, lsem.at[7]),
        pltpu.make_async_copy(wo, wo_all_ref, lsem.at[8]),
        pltpu.make_async_copy(columns, columns_ref, lsem.at[9]),
    ]
    for chip in range(chips):
        n1_line.wait_mate(chip)
    for copy in outs:
        copy.start()
    for step in range(1, chips):
        n2_line.forward(step)
    for chip in range(chips):
        cot_line.wait_mate(chip)
        n2_line.wait_mate(chip)
    last = pltpu.make_async_copy(n2buf, n2_all_ref, lsem.at[10])
    last.start()
    for b in (1, 2):
        m_direct(b, 2 - b).wait_recv()
        m_forward(3 - b).wait_recv()
    for copy in outs:
        copy.wait()
    last.wait()
    n1_line.drain()
    n2_line.drain()
    out_line.drain()
    cot_line.drain()
    for b in range(grps):
        wq_mate(b).wait_send()
        bias_mate(b).wait_send()
    for b in range(1, grps):
        wq_direct(b).wait_send()
        bias_direct(b).wait_send()
        for i in (0, 1):
            out_mate(b, i, p.core).wait_send()
    for b in (1, 2):
        for i in (0, 1):
            m_direct(b, i).wait_send()
            out_direct(b, i).wait_send()
        m_forward(b).wait_send()
        out_forward(b).wait_send()
    for chip in range(chips):
        pl.when(chip != p.chip)(lambda chip=chip: q_copy(chip).wait_send())
        for other in range(chips):
            pl.when(other != p.chip)(lambda chip=chip, other=other: k_copy(chip, other).wait_send())
            k_mate(other, chip).wait_send()


def front_call(tokens, gains, cot, qkv_weight, bias_rows, out_weight, mlp_rows, cosine, sine, mask):
    chips = cosine.shape[0]
    grps = 4
    shard, width = tokens.shape
    half = qkv_weight.shape[0]
    vm, dma = pltpu.VMEM, pltpu.SemaphoreType.DMA
    anyspace = pl.BlockSpec(memory_space=pl.ANY)
    vspec = pl.BlockSpec(memory_space=pltpu.VMEM)
    low, wide = jnp.bfloat16, jnp.float32
    struct = jax.ShapeDtypeStruct
    wo_shape = (grps, chips, 2) + out_weight.shape
    columns_shape = (grps, 2 * chips, out_weight.shape[0], shard)
    return pl.pallas_call(
        functools.partial(front_kernel, chips, 1.0 / math.sqrt(HD)),
        out_shape=(
            struct((shard, H * HD), wide),
            struct((shard, width), wide),
            struct((chips, 3, shard, HD), low),
            struct((chips, 2, chips, shard, HD), low),
            struct((chips, 2, shard, width), low),
            struct((chips, 2, shard, width), low),
            struct((chips, 2, shard, width), low),
            struct(wo_shape, low),
            struct((grps, 2 * half, width), low),
            struct(columns_shape, low),
        ) + (struct(mlp_rows.shape, low),) * 3,
        in_specs=[vspec] * 2 + [anyspace] * 5 + [vspec] * 3,
        out_specs=(vspec,) * 2 + (anyspace,) * 11,
        scratch_shapes=[
            vm((chips, 2, shard, width), low),
            vm((chips, 2, shard, width), low),
            vm((grps, 2 * half, width), low),
            vm(wo_shape, low),
            vm((grps, 2) + bias_rows.shape, wide),
            vm((chips, grps, shard, HD), low),
            vm((chips, 3, shard, HD), low),
            vm((chips, 2, chips, shard, HD), low),
            vm(columns_shape, low),
            dma((11,)),
            dma((3, chips)), dma((chips, 2)),
            dma((3, chips)), dma((chips, 2)),
            dma((3, chips)), dma((chips, 2)),
            dma((3, chips)), dma((chips, 2)),
            dma((grps, 2)), dma((grps, 2)), dma((grps, 2)), dma((grps, 2)),
            dma((2, grps)), dma((grps, 2)),
            dma((2, grps)), dma((grps, 2)),
            dma((grps, 2)), dma((grps, 2)),
            dma((chips,)), dma((chips,)),
            dma((2, chips, chips)), dma((chips, 2, chips)),
        ],
        compiler_params=pltpu.CompilerParams(
            collective_id=2, has_side_effects=True, vmem_limit_bytes=60 * 2**20
        ),
        name="front",
    )(tokens, gains, cot, qkv_weight, bias_rows, out_weight, mlp_rows, cosine, sine, mask)


def mlp_kernel(chips, grps, row_tiles, n2_ref, cot_ref, columns_ref, *refs):
    w_refs, refs = refs[:grps], refs[grps:]
    (
        n2g_ref, outp_ref, grads_ref, owned_ref, tok, w, acts, part, mate_in, left_in, right_in, stage, owned,
        lsem, ssend, srecv, wsem, osem, a_send, a_recv,
    ) = refs
    p = Place(chips)
    slots = 2 * chips
    shard, width = n2_ref.shape[1:]
    units = w.shape[1]
    block = units // grps
    tile = units // row_tiles
    loads = [
        pltpu.make_async_copy(n2_ref, tok.at[0], lsem.at[0]),
        pltpu.make_async_copy(cot_ref, tok.at[1], lsem.at[1]),
        pltpu.make_async_copy(columns_ref.at[:, p.seq], owned.at[:, :, pl.ds(pl.multiple_of(p.seq * shard, shard), shard)], lsem.at[2]),
    ]
    for copy in loads:
        copy.start()

    def w_copy(j, b):
        return pltpu.make_async_copy(w_refs[b].at[j], w.at[j, pl.ds(b * block, block)], wsem.at[j, b])

    for j in range(3):
        for b in range(grps):
            w_copy(j, b).start()

    def seq_peer(i):
        return (p.seq + i) % slots

    barrier = pltpu.get_barrier_semaphore()
    for i in range(1, slots):
        pl.semaphore_signal(barrier, inc=1, device_id=(p.grp, seq_peer(i)), device_id_type=MESH)
    pl.semaphore_wait(barrier, slots - 1)
    scatter = LineScatter(p, part, mate_in, left_in, right_in, ssend, srecv)

    def a_copy(i, to, slot):
        return remote(
            columns_ref.at[:, to], owned.at[:, :, pl.ds(pl.multiple_of(slot * shard, shard), shard)],
            a_send.at[i], a_recv.at[slot], p.grp, to,
        )

    for i in range(1, slots):
        a_copy(i, seq_peer(i), p.seq).start()
    for copy in loads:
        copy.wait()
    for j in range(3):
        for b in range(grps):
            w_copy(j, b).wait()

    @pl.loop(0, chips + 1)
    def _(order):
        @pl.when(order < chips)
        def _():
            at = nearest_chip(p.chip, chips - 1 - order, chips)
            x = tok[0, pl.ds(2 * at, 2)].reshape(2 * shard, width)
            y = tok[1, pl.ds(2 * at, 2)].reshape(2 * shard, width)
            gate = lax.dot_general(x, w[0], CONTRACT_LAST, preferred_element_type=jnp.float32)
            up = lax.dot_general(x, w[1], CONTRACT_LAST, preferred_element_type=jnp.float32)
            unit_grad = lax.dot_general(y, w[2], CONTRACT_LAST, preferred_element_type=jnp.float32)
            sig = 1.0 / (1.0 + jnp.exp(-gate))
            silu = gate * sig
            rows = pl.ds(at * (2 * shard), 2 * shard)
            gate_grad = (unit_grad * up * sig * (1.0 + gate * (1.0 - sig))).astype(jnp.bfloat16)
            up_grad = (unit_grad * silu).astype(jnp.bfloat16)
            acts[0, rows] = gate_grad
            acts[1, rows] = up_grad
            acts[2, rows] = (silu * up).astype(jnp.bfloat16)
            back = jnp.dot(gate_grad, w[0], preferred_element_type=jnp.float32) + jnp.dot(
                up_grad, w[1], preferred_element_type=jnp.float32
            )
            part[0, pl.ds(2 * at, 2)] = back.astype(jnp.bfloat16).reshape(2, shard, width)
            scatter.to_mate(0, at).start()

        pl.when(order > 0)(lambda: scatter.step(0, nearest_chip(p.chip, chips - order, chips)))

    def out_copy(t):
        return pltpu.make_async_copy(
            stage.at[t % 2],
            grads_ref.at[t // row_tiles, pl.ds((t % row_tiles) * tile, tile)],
            osem.at[t % 2],
        )

    @pl.loop(0, 3 * row_tiles)
    def _(t):
        @pl.when(t < chips)
        def _():
            at = nearest_chip(p.chip, chips - 1 - t, chips)
            h = acts[2, pl.ds(at * (2 * shard), 2 * shard)]
            part[1, pl.ds(2 * at, 2)] = (
                jnp.dot(h, w[2], preferred_element_type=jnp.float32)
                .astype(jnp.bfloat16).reshape(2, shard, width)
            )
            scatter.to_mate(1, at).start()

        @pl.when((t > 0) & (t <= chips))
        def _():
            scatter.step(1, nearest_chip(p.chip, chips - t, chips))

        @pl.when(t >= 2)
        def _():
            out_copy(t - 2).wait()

        kind = t // row_tiles
        lhs = acts[kind, :, pl.ds(pl.multiple_of((t % row_tiles) * tile, 128), tile)]
        rhs = tok[kind // 2].reshape(2 * chips * shard, width)
        stage[t % 2] = lax.dot_general(
            lhs, rhs, CONTRACT_FIRST, preferred_element_type=jnp.float32
        ).astype(jnp.bfloat16)
        out_copy(t).start()

    scatter.finish(0, n2g_ref)
    for i in range(1, slots):
        a_copy(i, seq_peer(i), seq_peer(i)).wait_recv()
    moved = pltpu.make_async_copy(owned, owned_ref, lsem.at[0])
    moved.start()
    scatter.finish(1, outp_ref)
    out_copy(3 * row_tiles - 2).wait()
    out_copy(3 * row_tiles - 1).wait()
    moved.wait()
    scatter.drain(0)
    scatter.drain(1)
    for i in range(1, slots):
        a_copy(i, seq_peer(i), p.seq).wait_send()


def mlp_call(n2_all, cot_all, columns, w_blocks, row_tiles=3):
    grps, (_, block, width) = len(w_blocks), w_blocks[0].shape
    slots, shard, _ = cot_all.shape
    chips = slots // 2
    units = grps * block
    vm, anyspace = pltpu.VMEM, pl.BlockSpec(memory_space=pl.ANY)
    vspec = pl.BlockSpec(memory_space=pltpu.VMEM)
    dma = pltpu.SemaphoreType.DMA
    owned_shape = columns.shape[:1] + columns.shape[2:3] + (slots * shard,)
    return pl.pallas_call(
        functools.partial(mlp_kernel, chips, grps, row_tiles),
        out_shape=(
            jax.ShapeDtypeStruct((shard, width), jnp.float32),
            jax.ShapeDtypeStruct((shard, width), jnp.float32),
            jax.ShapeDtypeStruct((3, units, width), jnp.bfloat16),
            jax.ShapeDtypeStruct(owned_shape, jnp.bfloat16),
        ),
        in_specs=[anyspace] * (3 + grps),
        out_specs=(vspec, vspec, anyspace, anyspace),
        scratch_shapes=[
            vm((2, slots, shard, width), jnp.bfloat16),
            vm((3, units, width), jnp.bfloat16),
            vm((3, slots * shard, units), jnp.bfloat16),
            vm((2, slots, shard, width), jnp.bfloat16),
            vm((2, chips, shard, width), jnp.bfloat16),
            vm((2, chips, shard, width), jnp.bfloat16),
            vm((2, chips, shard, width), jnp.bfloat16),
            vm((2, units // row_tiles, width), jnp.bfloat16),
            vm(owned_shape, jnp.bfloat16),
            dma((3,)), dma((3, 2, chips)), dma((3, 2, chips)),
            dma((3, grps)), dma((2,)), dma((slots,)), dma((slots,)),
        ],
        compiler_params=pltpu.CompilerParams(
            collective_id=1, has_side_effects=True, vmem_limit_bytes=62 * 2**20
        ),
        name="mlp",
    )(n2_all, cot_all, columns, *w_blocks)


def unturn(rows, cosine, sine, half):
    return rows * cosine + pltpu.roll(rows * sine, half, 1)


def back_kernel(chips, scale,
                n2g_ref, state_ref, cot_ref, tokens_ref, gains_ref, attn_ref, q_ref, kv_ref, mask_ref,
                cos_ref, sin_ref, wq_ref, wo_ref, n1_ref, terms_ref, owned_ref,
                tok_grad_ref, wq_grad_ref, wo_grad_ref, gain_ref, mlp_ref,
                wo, stbuf, n1x, at_all, dq_stage, gq_in, kv_part, km_in, k_sum, k_own, kr_in,
                cols, part, left_in, right_in, wgrad, wm_in, w_send_buf, w_in, o_terms, o_send_buf, o_in,
                m_own, m_in, gain_own, gain_in, gain_mid, gain_mid_in, state_grad,
                lsem, s_send, s_recv, q_send, q_recv, km_send, km_recv, kr_send, kr_recv,
                r_send, r_recv, wm_send, wm_recv, w_send, w_recv, o_send, o_recv, m_send, m_recv,
                ml_sem, g_send, g_recv, h_send, h_recv):
    p = Place(chips)
    grps = 4
    shard, width = n2g_ref.shape
    slots = 2 * chips
    heads_per = H // KVH
    half = HD // 2
    low, wide = jnp.bfloat16, jnp.float32
    block = terms_ref.shape[1] // grps
    mhalf = block // 2
    last = chips - 1

    loads = [
        pltpu.make_async_copy(wo_ref, wo, lsem.at[0]),
        pltpu.make_async_copy(n1_ref.at[:, p.core], n1x.at[:, :, pl.ds(0, width)], lsem.at[1]),
        pltpu.make_async_copy(owned_ref, at_all, lsem.at[2]),
    ]
    for copy in loads:
        copy.start()

    def seq_peer(i):
        return (p.seq + i) % slots

    barrier = pltpu.get_barrier_semaphore()
    for i in range(1, slots):
        pl.semaphore_signal(barrier, inc=1, device_id=(p.grp, seq_peer(i)), device_id_type=MESH)
    for b in range(1, grps):
        pl.semaphore_signal(barrier, inc=1, device_id=(p.peer(b), p.seq), device_id_type=MESH)
    pl.semaphore_wait(barrier, slots - 1 + grps - 1)

    def m_rows(b, i):
        return terms_ref.at[:, pl.ds(b * block + i * mhalf, mhalf)]

    def m_copy(slot, src, peer):
        return remote(src, m_in.at[slot], m_send.at[slot], m_recv.at[slot], p.peer(peer), p.seq)

    m_first = [
        m_copy(1, m_rows(3, 0), 1), m_copy(3, m_rows(3, 1), 2),
        m_copy(0, m_rows(1, 0), 1), m_copy(2, m_rows(2, 1), 2),
    ]
    for copy in m_first:
        copy.start()
    m_second = [m_copy(4, m_own.at[0], 1), m_copy(5, m_own.at[1], 2)]
    m_loads = [
        pltpu.make_async_copy(m_rows(1, 1), m_own.at[0], ml_sem.at[0]),
        pltpu.make_async_copy(m_rows(2, 0), m_own.at[1], ml_sem.at[1]),
        pltpu.make_async_copy(m_rows(0, 0), m_own.at[2], ml_sem.at[2]),
        pltpu.make_async_copy(m_rows(0, 1), m_own.at[3], ml_sem.at[3]),
    ]
    for copy in m_loads:
        copy.start()

    state = state_ref[...]
    gain_two = gains_ref[1]
    n2g = n2g_ref[...]
    scale_two = lax.rsqrt(jnp.mean(state * state, axis=-1, keepdims=True) + EPS)
    normed = state * scale_two
    gain_own[1] = jnp.sum(n2g * normed, axis=0, keepdims=True)
    lifted = n2g * gain_two
    state_grad[...] = cot_ref[...].astype(wide) + scale_two * (
        lifted - normed * jnp.mean(lifted * normed, axis=-1, keepdims=True)
    )
    state_low = state_grad[...].astype(low)
    stbuf[p.chip, p.core] = state_low
    line = RailGather(p, lambda chip, core: stbuf.at[chip, core], s_send, s_recv)
    line.start()

    attn = attn_ref[...]
    unit = wo.shape[0] // (grps * slots)
    loads[0].wait()
    attn_grad = lax.dot_general(state_low, wo[...], CONTRACT_LAST, preferred_element_type=wide).astype(low)
    line.forward(1)
    mask = mask_ref[...]
    keys_total = mask.shape[1]
    own_cos, own_sin = cos_ref[p.chip, p.core], sin_ref[p.chip, p.core]

    def km_copy(head):
        return remote(
            kv_part.at[head, 1 - p.core], km_in.at[head], km_send.at[head], km_recv.at[head], p.grp, p.mate
        )

    def kr_copy(head):
        return remote(
            k_sum.at[head], kr_in.at[p.chip], kr_send.at[head], kr_recv.at[p.chip], p.grp, 2 * head + p.core
        )

    def kr_arrival(chip):
        return remote(k_sum.at[chip], kr_in.at[chip], kr_send.at[chip], kr_recv.at[chip], p.grp, p.mate)

    def q_copy(chip):
        return remote(
            dq_stage.at[chip], gq_in.at[p.chip], q_send.at[chip], q_recv.at[p.chip], p.grp, 2 * chip + p.core
        )

    def q_arrival(chip):
        return remote(dq_stage.at[chip], gq_in.at[chip], q_send.at[chip], q_recv.at[chip], p.grp, p.mate)

    def key_sum(head):
        km_copy(head).wait_recv()
        total = kv_part[head, p.core].astype(wide) + km_in[head].astype(wide)

        @pl.when(p.chip == head)
        def _():
            k_own[...] = total

        @pl.when(p.chip != head)
        def _():
            k_sum[head] = total.astype(low)
            kr_copy(head).start()

    for kv in range(KVH):
        heads = [kv * heads_per + i for i in range(heads_per)]
        queries = jnp.concatenate([q_ref[h % chips, h // chips] for h in heads], axis=0)
        grads = jnp.concatenate([attn_grad[:, h * HD : (h + 1) * HD] for h in heads], axis=0)
        mixed = jnp.concatenate([attn[:, h * HD : (h + 1) * HD] for h in heads], axis=0)
        delta = jnp.sum(grads.astype(wide) * mixed, axis=-1, keepdims=True)
        keys = kv_ref[kv].reshape(keys_total, HD)
        values = kv_ref[KVH + kv].reshape(keys_total, HD)
        scores = lax.dot_general(queries, keys, CONTRACT_LAST, preferred_element_type=wide) * scale
        scores = (scores.reshape(heads_per, shard, keys_total) + mask[None]).reshape(heads_per * shard, keys_total)
        weights = jnp.exp(scores - jnp.max(scores, axis=-1, keepdims=True))
        probs = weights * (1.0 / jnp.sum(weights, axis=-1, keepdims=True))
        prob_grad = lax.dot_general(grads, values, CONTRACT_LAST, preferred_element_type=wide)
        score_grad = (probs * (prob_grad - delta)).astype(low)
        key_grad = lax.dot_general(score_grad, queries, CONTRACT_FIRST, preferred_element_type=wide) * scale
        value_grad = lax.dot_general(probs.astype(low), grads, CONTRACT_FIRST, preferred_element_type=wide)
        kv_part[kv] = key_grad.astype(low).reshape(2, chips, shard, HD)
        kv_part[KVH + kv] = value_grad.astype(low).reshape(2, chips, shard, HD)
        km_copy(kv).start()
        km_copy(KVH + kv).start()
        query_grad = jnp.dot(score_grad, keys, preferred_element_type=wide) * scale
        for i, h in enumerate(heads):
            turned = unturn(query_grad[i * shard : (i + 1) * shard], own_cos, own_sin, half).astype(low)
            dq_stage[h % chips, h // chips] = turned

            @pl.when(p.chip == h % chips)
            def _(turned=turned, h=h):
                gq_in[h % chips, h // chips] = turned

        line.forward(2 + kv)
    for chip in range(chips):
        pl.when(chip != p.chip)(lambda chip=chip: q_copy(chip).start())
    for head in (0, 2, 1, 3):
        key_sum(head)
    loads[1].wait()
    lane = lax.broadcasted_iota(jnp.int32, (chips, shard, HD), 2)
    n1x[:, :, width:] = jnp.where(lane == 0, 1.0, 0.0).astype(low)
    for chip in range(chips):
        line.wait_mate(chip)
    loads[2].wait()
    o_terms[...] = jnp.dot(
        at_all[...].reshape(grps * unit, slots * shard), stbuf[...].reshape(slots * shard, width),
        preferred_element_type=wide,
    ).reshape(grps, unit, width)
    o_send_buf[...] = o_terms[...].astype(low)

    def o_copy(b):
        return remote(
            o_send_buf.at[p.peer(b)], o_in.at[b], o_send.at[b], o_recv.at[b], p.peer(b), p.seq
        )

    for b in range(1, grps):
        o_copy(b).start()

    def m_add(dst, src):
        for j in range(3):
            @pl.loop(0, mhalf // 16)
            def _(t, j=j):
                rows = pl.ds(pl.multiple_of(t * 16, 16), 16)
                m_own[dst, j, rows] = (
                    m_own[dst, j, rows].astype(wide) + m_in[src, j, rows].astype(wide)
                ).astype(low)

    for chip in range(chips):
        pl.when(chip != p.chip)(lambda chip=chip: q_arrival(chip).wait_recv())
        pl.when(chip != p.chip)(lambda chip=chip: kr_arrival(chip).wait_recv())
    is_value = jnp.where(p.chip >= chips // 2, 1.0, 0.0)

    @pl.loop(0, chips)
    def _(chip):
        key_total = k_own[chip]
        for other in range(chips):
            key_total = key_total + jnp.where(other == p.chip, 0.0, kr_in[other, chip].astype(wide))
        turned = unturn(key_total, cos_ref[chip, p.core], sin_ref[chip, p.core], half)
        last_head = (key_total * is_value + turned * (1.0 - is_value)).astype(low)
        for b in range(grps):
            place = p.peer(b)
            query_head = gq_in[chip, jnp.minimum(place, grps - 2)]
            cols[chip, :, b * HD : (b + 1) * HD] = jnp.where(place == grps - 1, last_head, query_head)
        part[chip] = jnp.dot(
            cols[chip], wq_ref[...], preferred_element_type=wide
        ).astype(low)

    def to_right(chip):
        return remote(part.at[chip], left_in.at[chip], r_send.at[0, chip], r_recv.at[0, chip], p.grp, p.seq + 2)

    def to_left(chip):
        return remote(part.at[chip], right_in.at[chip], r_send.at[1, chip], r_recv.at[1, chip], p.grp, p.seq - 2)

    def rail_step(order):
        far = last - order

        @pl.when(far > p.chip)
        def _():
            @pl.when(p.chip > 0)
            def _():
                to_right(far).wait_recv()
                part[far] = (part[far].astype(wide) + left_in[far].astype(wide)).astype(low)

            to_right(far).start()

        @pl.when(order < p.chip)
        def _():
            @pl.when(p.chip < last)
            def _():
                to_left(order).wait_recv()
                part[order] = (part[order].astype(wide) + right_in[order].astype(wide)).astype(low)

            to_left(order).start()

    rail_step(0)
    wgrad[...] = lax.dot_general(
        cols[...].reshape(chips * shard, grps * HD), n1x[...].reshape(chips * shard, width + HD),
        CONTRACT_FIRST, preferred_element_type=wide,
    ).reshape(grps, 2, half, width + HD)
    wm = remote(wgrad.at[:, 1 - p.core], wm_in, wm_send, wm_recv, p.grp, p.mate)
    wm.start()
    rail_step(1)
    wm.wait_recv()
    w_send_buf[...] = (wgrad[:, p.core] + wm_in[...]).astype(low)

    def w_copy(b):
        return remote(w_send_buf.at[b], w_in.at[b], w_send.at[b], w_recv.at[b], p.peer(b), p.seq)

    for b in range(1, grps):
        w_copy(b).start()
    rail_step(2)
    m_loads[0].wait()
    m_first[1].wait_recv()
    m_add(0, 3)
    m_second[0].start()
    m_loads[1].wait()
    m_first[0].wait_recv()
    m_add(1, 1)
    m_second[1].start()
    rail_step(3)

    tokens = tokens_ref[...].astype(wide)
    tok_grad_ref[...] = part[p.chip].astype(wide)

    @pl.when(p.chip > 0)
    def _():
        to_right(p.chip).wait_recv()
        tok_grad_ref[...] += left_in[p.chip].astype(wide)

    @pl.when(p.chip < last)
    def _():
        to_left(p.chip).wait_recv()
        tok_grad_ref[...] += right_in[p.chip].astype(wide)

    n1g = tok_grad_ref[...]
    scale_one = lax.rsqrt(jnp.mean(tokens * tokens, axis=-1, keepdims=True) + EPS)
    normed = tokens * scale_one
    gain_own[0] = jnp.sum(n1g * normed, axis=0, keepdims=True)
    lifted = n1g * gains_ref[0]
    tok_grad_ref[...] = state_grad[...] + scale_one * (
        lifted - normed * jnp.mean(lifted * normed, axis=-1, keepdims=True)
    )

    def g_copy(i):
        return remote(gain_own, gain_in.at[i], g_send.at[i], g_recv.at[i], p.grp, seq_peer(i))

    for i in range(1, slots):
        g_copy(i).start()
    total = gain_own[...]
    for i in range(1, slots):
        g_copy(i).wait_recv()
        total = total + gain_in[i]
    gain_mid[...] = total

    def h_copy(b):
        return remote(gain_mid, gain_mid_in.at[b], h_send.at[b], h_recv.at[b], p.peer(b), p.seq)

    for b in range(1, grps):
        h_copy(b).start()

    wo_grad = o_terms[p.grp]
    wq_grad = wgrad[0, p.core] + wm_in[0]
    for b in range(1, grps):
        o_copy(b).wait_recv()
        wo_grad = wo_grad + o_in[b].astype(wide)
        w_copy(b).wait_recv()
        wq_grad = wq_grad + w_in[b].astype(wide)
    wo_grad_ref[...] = wo_grad
    wq_grad_ref[...] = wq_grad
    total = gain_mid[...]
    for b in range(1, grps):
        h_copy(b).wait_recv()
        total = total + gain_mid_in[b]
    gain_ref[...] = total

    m_loads[2].wait()
    m_loads[3].wait()

    def m_total(own, direct, second, i):
        for j in range(3):
            @pl.loop(0, mhalf // 16)
            def _(t, j=j):
                rows = pl.ds(pl.multiple_of(t * 16, 16), 16)
                mlp_ref[j, pl.ds(pl.multiple_of(i * mhalf + t * 16, 16), 16)] = (
                    m_own[own, j, rows].astype(wide) + m_in[direct, j, rows].astype(wide)
                ) + m_in[second, j, rows].astype(wide)

    m_first[2].wait_recv()
    m_second[1].wait_recv()
    m_total(2, 0, 5, 0)
    m_first[3].wait_recv()
    m_second[0].wait_recv()
    m_total(3, 2, 4, 1)

    for copy in m_first + m_second:
        copy.wait_send()
    line.drain()
    wm.wait_send()
    for i in range(1, slots):
        g_copy(i).wait_send()
    for b in range(1, grps):
        o_copy(b).wait_send()
        w_copy(b).wait_send()
        h_copy(b).wait_send()
    for chip in range(chips):
        km_copy(chip).wait_send()

        @pl.when(chip != p.chip)
        def _(chip=chip):
            q_copy(chip).wait_send()
            kr_copy(chip).wait_send()

        pl.when(chip > p.chip)(lambda chip=chip: to_right(chip).wait_send())
        pl.when(chip < p.chip)(lambda chip=chip: to_left(chip).wait_send())


def back_call(n2g, state, cotangent, tokens, gains, attn, q_heads, kv_heads, mask, cosine, sine,
              qkv_all, out_full, n1_all, terms, owned):
    chips = cosine.shape[0]
    grps = 4
    slots = 2 * chips
    shard, width = tokens.shape
    att, block = out_full.shape[0], terms.shape[1] // grps
    unit, half = att // (grps * slots), HD // 2
    vm, dma = pltpu.VMEM, pltpu.SemaphoreType.DMA
    anyspace = pl.BlockSpec(memory_space=pl.ANY)
    vspec = pl.BlockSpec(memory_space=pltpu.VMEM)
    low, wide = jnp.bfloat16, jnp.float32
    struct = jax.ShapeDtypeStruct
    return pl.pallas_call(
        functools.partial(back_kernel, chips, 1.0 / math.sqrt(HD)),
        out_shape=(
            struct((shard, width), wide),
            struct((half, width + HD), wide),
            struct((unit, width), wide),
            struct((2, 1, width), wide),
            struct((3, block, width), wide),
        ),
        in_specs=[vspec] * 12 + [anyspace] * 4,
        out_specs=(vspec,) * 5,
        scratch_shapes=[
            vm((att, width), low),
            vm((chips, 2, shard, width), low),
            vm((chips, shard, width + HD), low),
            vm((grps, unit, slots * shard), low),
            vm((chips, 3, shard, HD), low),
            vm((chips, 3, shard, HD), low),
            vm((chips, 2, chips, shard, HD), low),
            vm((chips, chips, shard, HD), low),
            vm((chips, chips, shard, HD), low),
            vm((chips, shard, HD), wide),
            vm((chips, chips, shard, HD), low),
            vm((chips, shard, grps * HD), low),
            vm((chips, shard, width), low),
            vm((chips, shard, width), low),
            vm((chips, shard, width), low),
            vm((grps, 2, half, width + HD), wide),
            vm((grps, half, width + HD), wide),
            vm((grps, half, width + HD), low),
            vm((grps, half, width + HD), low),
            vm((grps, unit, width), wide),
            vm((grps, unit, width), low),
            vm((grps, unit, width), low),
            vm((4, 3, block // 2, width), low),
            vm((6, 3, block // 2, width), low),
            vm((2, 1, width), wide),
            vm((slots, 2, 1, width), wide),
            vm((2, 1, width), wide),
            vm((grps, 2, 1, width), wide),
            vm((shard, width), wide),
            dma((3,)),
            dma((3, chips)), dma((chips, 2)),
            dma((chips,)), dma((chips,)),
            dma((chips,)), dma((chips,)),
            dma((chips,)), dma((chips,)),
            dma((2, chips)), dma((2, chips)),
            dma, dma,
            dma((grps,)), dma((grps,)),
            dma((grps,)), dma((grps,)),
            dma((6,)), dma((6,)),
            dma((4,)),
            dma((slots,)), dma((slots,)),
            dma((grps,)), dma((grps,)),
        ],
        compiler_params=pltpu.CompilerParams(
            collective_id=3, has_side_effects=True, vmem_limit_bytes=62 * 2**20
        ),
        name="back",
    )(n2g, state, cotangent, tokens, gains, attn, q_heads, kv_heads, mask, cosine, sine,
      qkv_all, out_full, n1_all, terms, owned)


def columns_to_owners(rows, row_unit):
    grp_count, seq_count = lax.axis_size("grp"), lax.axis_size("seq")
    tok_rows = rows.shape[0]
    split = rows.reshape(tok_rows, grp_count, seq_count, row_unit).transpose(2, 0, 1, 3)
    split = split.reshape(seq_count * tok_rows, grp_count * row_unit)
    return lax.all_to_all(split, "seq", split_axis=0, concat_axis=0, tiled=True)


def owners_to_columns(rows, row_unit):
    grp_count, seq_count = lax.axis_size("grp"), lax.axis_size("seq")
    tok_rows = rows.shape[0] // seq_count
    moved = lax.all_to_all(rows, "seq", split_axis=0, concat_axis=0, tiled=True)
    moved = moved.reshape(seq_count, tok_rows, grp_count, row_unit).transpose(1, 2, 0, 3)
    return moved.reshape(tok_rows, grp_count * seq_count * row_unit)


def plain_mlp(normed_two, cotangent_all, mlp_weight):
    contract_last, contract_first = CONTRACT_LAST, CONTRACT_FIRST
    mlp_rows = lax.all_gather(mlp_weight, "grp", axis=0, tiled=True)
    normed_two_all = lax.all_gather(normed_two, "seq", axis=0, tiled=True)
    gate_rows, upper_rows, down_rows = mlp_rows[:, 0, :], mlp_rows[:, 1, :], mlp_rows[:, 2, :]
    gate_vals = lax.dot_general(
        normed_two_all, gate_rows, contract_last, preferred_element_type=jnp.float32
    )
    upper_vals = lax.dot_general(
        normed_two_all, upper_rows, contract_last, preferred_element_type=jnp.float32
    )
    unit_wide, pull_back = jax.vjp(swish_product, gate_vals, upper_vals)
    unit_low = unit_wide.astype(jnp.bfloat16)
    unit_grad = lax.dot_general(
        cotangent_all, down_rows, contract_last, preferred_element_type=jnp.float32
    )
    gate_grad, upper_grad = pull_back(unit_grad)
    gate_grad = gate_grad.astype(jnp.bfloat16)
    upper_grad = upper_grad.astype(jnp.bfloat16)
    input_grad = jnp.dot(gate_grad, gate_rows, preferred_element_type=jnp.float32) + jnp.dot(
        upper_grad, upper_rows, preferred_element_type=jnp.float32
    )
    grad_part = lax.psum_scatter(
        input_grad.astype(jnp.bfloat16), "seq", scatter_dimension=0, tiled=True
    ).astype(jnp.float32)
    out_part = lax.psum_scatter(
        jnp.dot(unit_low, down_rows, preferred_element_type=jnp.float32).astype(jnp.bfloat16),
        "seq",
        scatter_dimension=0,
        tiled=True,
    ).astype(jnp.float32)
    mlp_terms = jnp.stack(
        [
            lax.dot_general(
                gate_grad, normed_two_all, contract_first, preferred_element_type=jnp.float32
            ),
            lax.dot_general(
                upper_grad, normed_two_all, contract_first, preferred_element_type=jnp.float32
            ),
            lax.dot_general(
                unit_low, cotangent_all, contract_first, preferred_element_type=jnp.float32
            ),
        ],
        axis=1,
    )
    mlp_grad = lax.psum_scatter(mlp_terms, "grp", scatter_dimension=0, tiled=True)
    return grad_part, out_part, mlp_grad


def padded_rows(mlp_weight):
    rows = mlp_weight.transpose(1, 0, 2)
    return jnp.pad(rows, ((0, 0), (0, -rows.shape[1] % 32), (0, 0)))


def per_device(
    tokens,
    cotangent,
    shard_segment,
    gain_attn,
    qkv_weight,
    qkv_bias,
    out_weight,
    gain_mlp,
    mlp_weight,
):
    tok_rows = tokens.shape[0]
    seq_count = lax.axis_size("seq")
    grp_count = lax.axis_size("grp")
    group_tok = tok_rows * seq_count
    heads_per = H // KVH
    kv_width = KVH * HD
    att_width = H * HD
    query_rows = heads_per * tok_rows
    score_scale = 1.0 / math.sqrt(HD)
    contract_last = CONTRACT_LAST
    contract_first = CONTRACT_FIRST
    seq_place = lax.axis_index("seq")
    grp_place = lax.axis_index("grp")
    segments = lax.dynamic_index_in_dim(shard_segment, grp_place, 0, keepdims=False)
    starts = shard_starts(segments, tok_rows, group_tok // 2)
    shard_order = jnp.arange(seq_count, dtype=jnp.int32)
    own_seg = jnp.sum(jnp.where(shard_order == seq_place, segments, 0))
    own_start = jnp.sum(jnp.where(shard_order == seq_place, starts, 0))
    positions = own_start + jnp.arange(tok_rows, dtype=jnp.int32)
    cosine_table, sine_table = rotary_tables(positions, HD)
    query_pos = jnp.tile(positions, heads_per)
    tokens_wide = tokens.astype(jnp.float32)
    gain_one = gain_attn.astype(jnp.float32)
    gain_two = gain_mlp.astype(jnp.float32)
    normed_one = rms_scale(tokens_wide, gain_one).astype(jnp.bfloat16)
    use_kernels = (seq_count, grp_count, H, KVH, HD) == (8, 4, 12, 2, 128)
    if use_kernels:
        chips = seq_count // 2
        lanes = jnp.arange(HD)
        all_pos = (starts[:, None] + jnp.arange(tok_rows, dtype=jnp.int32)[None, :]).reshape(-1)
        all_cosine, all_sine = rotary_tables(all_pos, HD)
        all_sine = jnp.where(lanes < HD // 2, -all_sine, all_sine)
        by_shard = lambda table: table.reshape(chips, 2, tok_rows, HD)
        key_pos = all_pos.reshape(chips, 2, tok_rows).swapaxes(0, 1).reshape(-1)
        key_seg = jnp.repeat(segments.reshape(chips, 2).swapaxes(0, 1).reshape(-1), tok_rows)
        visible = ((key_seg == 0) | (key_seg == own_seg))[None, :] & (
            key_pos[None, :] <= positions[:, None]
        )
        mask = jnp.where(visible, 0.0, -1e30).astype(jnp.float32)
        bias_half = qkv_bias.astype(jnp.float32)
        bias_pair = jnp.concatenate([bias_half, jnp.zeros_like(bias_half)])
        bias_row = jnp.where(seq_place % 2 == 0, bias_pair, jnp.roll(bias_pair, HD // 2))
        bias_rows8 = jnp.broadcast_to(bias_row[None, :], (8, HD))
        own_rows = padded_rows(mlp_weight)
        gains = jnp.stack([gain_one, gain_two])[:, None, :]
        (
            attn_wide, state, q_heads, kv_heads, n1_all, n2_all, cot_all, out_all, qkv_all, columns, *peer_rows
        ) = front_call(
            tokens, gains, cotangent, qkv_weight, bias_rows8, out_weight, own_rows,
            by_shard(all_cosine), by_shard(all_sine), mask,
        )
        by_slot = lambda rows: rows.reshape((seq_count,) + rows.shape[2:])
        grad_part, out_part, mlp_terms, owned = mlp_call(
            by_slot(n2_all), by_slot(cot_all), columns, [own_rows, *peer_rows]
        )
        output = (state + out_part).astype(jnp.bfloat16)
        token_grad, qkv_terms, out_grad, gain_sums, mlp_sums = back_call(
            grad_part, state, cotangent, tokens, gains, attn_wide, q_heads, kv_heads, mask,
            by_shard(all_cosine), by_shard(all_sine), qkv_all.reshape(-1, qkv_all.shape[-1]),
            out_all.reshape(att_width, -1), n1_all, mlp_terms, owned,
        )
        width = tokens.shape[1]
        own = width // (grp_count * seq_count)
        gain_parts = lax.dynamic_slice_in_dim(
            gain_sums[:, 0], (grp_place * seq_count + seq_place) * own, own, 1
        )
        return (
            output,
            token_grad,
            gain_parts[0],
            qkv_terms[:, :width],
            qkv_terms[:, width],
            out_grad,
            gain_parts[1],
            mlp_sums[:, : mlp_weight.shape[0]].transpose(1, 0, 2),
        )
    normed_one_all = lax.all_gather(normed_one, "seq", axis=0, tiled=True)
    qkv_rows = lax.all_gather(qkv_weight, "grp", axis=0, tiled=True)
    bias_rows = lax.all_gather(qkv_bias, "grp", axis=0, tiled=True)
    cotangent_all = lax.all_gather(cotangent, "seq", axis=0, tiled=True)
    out_full = lax.all_gather(out_weight, AXES, axis=0, tiled=True)
    projected = lax.dot_general(
        normed_one_all, qkv_rows, contract_last, preferred_element_type=jnp.float32
    )
    projected = (projected + bias_rows.astype(jnp.float32)[None, :]).astype(jnp.bfloat16)
    projected = owners_to_columns(projected, qkv_weight.shape[0]).astype(jnp.float32)
    query_rot = rotate(
        projected[:, :att_width].reshape(tok_rows, H, HD), cosine_table, sine_table
    ).astype(jnp.bfloat16)
    key_rot = rotate(
        projected[:, att_width : att_width + kv_width].reshape(tok_rows, KVH, HD),
        cosine_table,
        sine_table,
    ).astype(jnp.bfloat16)
    value_low = projected[:, att_width + kv_width :].astype(jnp.bfloat16)
    keys_all, values_all = (
        lax.all_gather(key_rot.reshape(tok_rows, kv_width), "seq", axis=0, tiled=True),
        lax.all_gather(value_low, "seq", axis=0, tiled=True),
    )
    queries = (
        query_rot.reshape(tok_rows, KVH, heads_per, HD)
        .transpose(1, 2, 0, 3)
        .reshape(KVH, query_rows, HD)
    )
    key_block = min(512, group_tok)
    block_count = group_tok // key_block
    block_order = jnp.arange(block_count, dtype=jnp.int32)

    def block_mask(block_index):
        key_index = block_index * key_block + jnp.arange(key_block, dtype=jnp.int32)
        key_shard = key_index // tok_rows
        onehot = key_shard[:, None] == shard_order[None, :]
        key_seg = jnp.sum(jnp.where(onehot, segments[None, :], 0), axis=1)
        key_pos = jnp.sum(jnp.where(onehot, starts[None, :], 0), axis=1) + key_index % tok_rows
        visible = (key_seg == 0) | (key_seg == own_seg)
        return visible[None, :] & (key_pos[None, :] <= query_pos[:, None])

    def block_keys(block_index):
        key_part = lax.dynamic_slice_in_dim(
            keys_all, block_index * key_block, key_block, 0
        ).reshape(key_block, KVH, HD)
        value_part = lax.dynamic_slice_in_dim(
            values_all, block_index * key_block, key_block, 0
        ).reshape(key_block, KVH, HD)
        return (key_part, value_part)

    def block_scores(key_part):
        return (
            jnp.einsum("krd,jkd->krj", queries, key_part, preferred_element_type=jnp.float32)
            * score_scale
        )

    def stat_step(stats_now, block_index):
        allowed = block_mask(block_index)

        def stat_visit(current):
            top_old, total_old = current
            key_part, value_part = block_keys(block_index)
            scores = jnp.where(allowed[None], block_scores(key_part), -1e30)
            top_new = jnp.maximum(top_old, jnp.max(scores, axis=-1))
            weights = jnp.where(allowed[None], jnp.exp(scores - top_new[..., None]), 0.0)
            return (top_new, total_old * jnp.exp(top_old - top_new) + jnp.sum(weights, axis=-1))

        return (lax.cond(jnp.any(allowed), stat_visit, lambda current: current, stats_now), None)

    start_stats = (
        jnp.full((KVH, query_rows), -1e30, jnp.float32),
        jnp.zeros((KVH, query_rows), jnp.float32),
    )
    (top_all, total_all), unused = lax.scan(stat_step, start_stats, block_order)
    log_total = top_all + jnp.log(total_all)

    def mix_step(mixed_sum, block_index):
        allowed = block_mask(block_index)

        def mix_visit(current):
            key_part, value_part = block_keys(block_index)
            prob_low = jnp.where(
                allowed[None], jnp.exp(block_scores(key_part) - log_total[..., None]), 0.0
            ).astype(jnp.bfloat16)
            return current + jnp.einsum(
                "krj,jkd->krd", prob_low, value_part, preferred_element_type=jnp.float32
            )

        return (lax.cond(jnp.any(allowed), mix_visit, lambda current: current, mixed_sum), None)

    mixed_sum, unused = lax.scan(
        mix_step, jnp.zeros((KVH, query_rows, HD), jnp.float32), block_order
    )
    attn_wide = (
        mixed_sum.reshape(KVH, heads_per, tok_rows, HD)
        .transpose(2, 0, 1, 3)
        .reshape(tok_rows, att_width)
    )
    attn_low = attn_wide.astype(jnp.bfloat16)
    attn_proj = jnp.dot(attn_low, out_full, preferred_element_type=jnp.float32)
    state = tokens_wide + attn_proj
    normed_two = rms_scale(state, gain_two).astype(jnp.bfloat16)
    grad_part, out_part, mlp_grad = plain_mlp(normed_two, cotangent_all, mlp_weight)
    output = (state + out_part).astype(jnp.bfloat16)
    unused_state, norm_two_back = jax.vjp(rms_scale, state, gain_two)
    state_norm_grad, gain_two_grad = norm_two_back(grad_part)
    state_grad = state_norm_grad + cotangent.astype(jnp.float32)
    state_low = state_grad.astype(jnp.bfloat16)
    attn_grad = lax.dot_general(
        state_low, out_full, contract_last, preferred_element_type=jnp.float32
    )
    attn_grad_low = attn_grad.astype(jnp.bfloat16)
    attn_owned = columns_to_owners(attn_low, out_weight.shape[0])
    state_low_all = lax.all_gather(state_low, "seq", axis=0, tiled=True)
    out_grad = lax.psum_scatter(
        lax.dot_general(
            attn_owned, state_low_all, contract_first, preferred_element_type=jnp.float32
        ),
        "grp",
        scatter_dimension=0,
        tiled=True,
    )
    grad_heads = (
        attn_grad_low.reshape(tok_rows, KVH, heads_per, HD)
        .transpose(1, 2, 0, 3)
        .reshape(KVH, query_rows, HD)
    )
    delta_rows = jnp.sum(
        (attn_grad_low.astype(jnp.float32) * attn_wide).reshape(tok_rows, H, HD), axis=-1
    )
    delta_rows = (
        delta_rows.reshape(tok_rows, KVH, heads_per).transpose(1, 2, 0).reshape(KVH, query_rows)
    )

    def back_step(query_grad, block_index):
        allowed = block_mask(block_index)

        def back_visit(current):
            key_part, value_part = block_keys(block_index)
            prob_vals = jnp.where(
                allowed[None], jnp.exp(block_scores(key_part) - log_total[..., None]), 0.0
            )
            prob_grad = jnp.einsum(
                "krd,jkd->krj", grad_heads, value_part, preferred_element_type=jnp.float32
            )
            score_grad = (prob_vals * (prob_grad - delta_rows[..., None])).astype(jnp.bfloat16)
            new_grad = (
                current
                + jnp.einsum(
                    "krj,jkd->krd", score_grad, key_part, preferred_element_type=jnp.float32
                )
                * score_scale
            )
            key_grad = (
                jnp.einsum("krj,krd->jkd", score_grad, queries, preferred_element_type=jnp.float32)
                * score_scale
            )
            value_grad = jnp.einsum(
                "krj,krd->jkd",
                prob_vals.astype(jnp.bfloat16),
                grad_heads,
                preferred_element_type=jnp.float32,
            )
            return (
                new_grad,
                (key_grad.reshape(key_block, kv_width), value_grad.reshape(key_block, kv_width)),
            )

        def skip_block(current):
            blank_rows = jnp.zeros((key_block, kv_width), jnp.float32)
            return (current, (blank_rows, blank_rows))

        return lax.cond(jnp.any(allowed), back_visit, skip_block, query_grad)

    query_grad, (key_grads, value_grads) = lax.scan(
        back_step, jnp.zeros((KVH, query_rows, HD), jnp.float32), block_order
    )
    key_own, value_own = (
        lax.psum_scatter(
            key_grads.reshape(group_tok, kv_width).astype(jnp.bfloat16),
            "seq",
            scatter_dimension=0,
            tiled=True,
        ).astype(jnp.float32),
        lax.psum_scatter(
            value_grads.reshape(group_tok, kv_width).astype(jnp.bfloat16),
            "seq",
            scatter_dimension=0,
            tiled=True,
        ).astype(jnp.float32),
    )
    query_back = unrotate(
        query_grad.reshape(KVH, heads_per, tok_rows, HD)
        .transpose(2, 0, 1, 3)
        .reshape(tok_rows, H, HD),
        cosine_table,
        sine_table,
    )
    key_back = unrotate(key_own.reshape(tok_rows, KVH, HD), cosine_table, sine_table)
    qkv_grad_low = jnp.concatenate(
        [query_back.reshape(tok_rows, att_width), key_back.reshape(tok_rows, kv_width), value_own],
        axis=1,
    ).astype(jnp.bfloat16)
    qkv_grad_owned = columns_to_owners(qkv_grad_low, qkv_weight.shape[0])
    bias_terms = jnp.sum(qkv_grad_owned.astype(jnp.float32), axis=0)
    normed_one_grad = lax.psum_scatter(
        jnp.dot(qkv_grad_owned, qkv_rows, preferred_element_type=jnp.float32).astype(jnp.bfloat16),
        "seq",
        scatter_dimension=0,
        tiled=True,
    ).astype(jnp.float32)
    qkv_grad = lax.psum_scatter(
        lax.dot_general(
            qkv_grad_owned, normed_one_all, contract_first, preferred_element_type=jnp.float32
        ),
        "grp",
        scatter_dimension=0,
        tiled=True,
    )
    unused_tokens, norm_one_back = jax.vjp(rms_scale, tokens_wide, gain_one)
    token_norm_grad, gain_one_grad = norm_one_back(normed_one_grad)
    token_grad = token_norm_grad + state_grad
    bias_part = lax.psum_scatter(bias_terms, "grp", scatter_dimension=0, tiled=True)
    gain_one_part, gain_two_part = (
        lax.psum_scatter(gain_one_grad, AXES, scatter_dimension=0, tiled=True),
        lax.psum_scatter(gain_two_grad, AXES, scatter_dimension=0, tiled=True),
    )
    return (
        output,
        token_grad,
        gain_one_part,
        qkv_grad,
        bias_part,
        out_grad,
        gain_two_part,
        mlp_grad,
    )


def solution(mesh):
    return jax.shard_map(
        per_device,
        mesh=mesh,
        in_specs=(
            P(("grp", "seq"), None),
            P(("grp", "seq"), None),
            P(),
            P(),
            P(("grp", "seq"), None),
            P(("grp", "seq")),
            P(("grp", "seq"), None),
            P(),
            P(("grp", "seq"), None, None),
        ),
        out_specs=(
            P(("grp", "seq"), None),
            P(("grp", "seq"), None),
            P(("grp", "seq")),
            P(("grp", "seq"), None),
            P(("grp", "seq")),
            P(("grp", "seq"), None),
            P(("grp", "seq")),
            P(("grp", "seq"), None, None),
        ),
        check_vma=False,
    )
```

```python
import functools
import math

import jax
import jax.numpy as jnp
from jax import lax
from jax.experimental import pallas as pl
from jax.experimental.pallas import tpu as pltpu
from jax.sharding import PartitionSpec as P

H = 12
KVH = 2
HD = 128
FF = 8960


EPS = 1e-06
THETA = 10000.0


def rms_scale(values, gain_vec):
    return values * lax.rsqrt(jnp.mean(values * values, axis=-1, keepdims=True) + EPS) * gain_vec


def rotary_tables(positions, head_dim):
    half_dim = head_dim // 2
    freqs = THETA ** (-(jnp.arange(half_dim, dtype=jnp.float32) * 2.0) / head_dim)
    angles = positions.astype(jnp.float32)[:, None] * freqs[None, :]
    cosine_table = jnp.concatenate([jnp.cos(angles), jnp.cos(angles)], axis=-1)
    sine_table = jnp.concatenate([jnp.sin(angles), jnp.sin(angles)], axis=-1)
    return (cosine_table, sine_table)


def rotate(values, cosine_table, sine_table):
    half_dim = values.shape[-1] // 2
    turned = jnp.concatenate([-values[..., half_dim:], values[..., :half_dim]], axis=-1)
    return values * cosine_table[:, None, :] + turned * sine_table[:, None, :]


def unrotate(grad_rows, cosine_table, sine_table):
    half_dim = grad_rows.shape[-1] // 2
    scaled = grad_rows * sine_table[:, None, :]
    turned = jnp.concatenate([scaled[..., half_dim:], -scaled[..., :half_dim]], axis=-1)
    return grad_rows * cosine_table[:, None, :] + turned


def shard_starts(segments, tok_dev, prompt_len):
    shard_total = segments.shape[0]
    shard_order = jnp.arange(shard_total, dtype=jnp.int32)
    same_seg = segments[:, None] == segments[None, :]
    first_shard = jnp.min(jnp.where(same_seg, shard_order[None, :], shard_total), axis=1)
    cont_start = prompt_len + (shard_order - first_shard) * tok_dev
    return jnp.where(segments == 0, shard_order * tok_dev, cont_start)


def swish_product(gate_vals, upper_vals):
    return jax.nn.silu(gate_vals) * upper_vals


AXES = ("grp", "seq")
CONTRACT_LAST = (((1,), (1,)), ((), ()))
CONTRACT_FIRST = (((0,), (0,)), ((), ()))


MESH = pl.DeviceIdType.MESH


def remote(src, dst, send_sem, recv_sem, grp, seq):
    return pltpu.make_async_remote_copy(
        src_ref=src, dst_ref=dst, send_sem=send_sem, recv_sem=recv_sem,
        device_id=(grp, seq), device_id_type=MESH,
    )


def nearest_chip(place, order, chips):
    both = 2 * jnp.minimum(place, chips - 1 - place)
    offset = (order + 1) // 2
    near = jnp.where(order % 2 == 1, place - offset, place + offset)
    rest = jnp.where(place < chips - 1 - place, order, chips - 1 - order)
    return jnp.where(order <= both, near, rest)


class Place:
    def __init__(self, chips):
        self.chips = chips
        self.grp, self.seq = lax.axis_index("grp"), lax.axis_index("seq")
        self.chip, self.core = self.seq // 2, self.seq % 2
        self.mate = self.seq + 1 - 2 * self.core

    def peer(self, offset):
        low, high = self.grp % 2, self.grp // 2
        low = 1 - low if offset % 2 else low
        high = 1 - high if offset // 2 else high
        return 2 * high + low

    def barrier(self, grps):
        barrier = pltpu.get_barrier_semaphore()
        for chip in range(self.chips):
            @pl.when(chip != self.chip)
            def _(chip=chip):
                pl.semaphore_signal(
                    barrier, inc=1, device_id=(self.grp, 2 * chip + self.core), device_id_type=MESH
                )
        pl.semaphore_signal(barrier, inc=1, device_id=(self.grp, self.mate), device_id_type=MESH)
        for offset in range(1, grps):
            pl.semaphore_signal(
                barrier, inc=1, device_id=(self.peer(offset), self.seq), device_id_type=MESH
            )
        pl.semaphore_wait(barrier, self.chips - 1 + 1 + grps - 1)


class RailGather:
    def __init__(self, place, view, send_sem, recv_sem):
        self.place, self.view, self.send_sem, self.recv_sem = place, view, send_sem, recv_sem

    def copy(self, way, chip, core):
        p = self.place
        to = (p.seq + 2, p.seq - 2, p.mate)[way]
        return remote(
            self.view(chip, core), self.view(chip, core), self.send_sem.at[way, chip],
            self.recv_sem.at[chip, core], p.grp, to,
        )

    def start(self):
        p = self.place
        pl.when(p.chip < p.chips - 1)(lambda: self.copy(0, p.chip, p.core).start())
        pl.when(p.chip > 0)(lambda: self.copy(1, p.chip, p.core).start())
        self.copy(2, p.chip, p.core).start()

    def forward(self, step):
        p = self.place

        @pl.when(p.chip - step >= 0)
        def _():
            chip = p.chip - step
            self.copy(2, chip, p.core).wait_recv()
            pl.when(p.chip < p.chips - 1)(lambda: self.copy(0, chip, p.core).start())
            self.copy(2, chip, p.core).start()

        @pl.when(p.chip + step < p.chips)
        def _():
            chip = p.chip + step
            self.copy(2, chip, p.core).wait_recv()
            pl.when(p.chip > 0)(lambda: self.copy(1, chip, p.core).start())
            self.copy(2, chip, p.core).start()

    def wait_mate(self, chip):
        self.copy(2, chip, 1 - self.place.core).wait_recv()

    def drain(self):
        p = self.place
        for chip in range(p.chips):
            self.copy(2, chip, p.core).wait_send()
            pl.when((chip <= p.chip) & (p.chip < p.chips - 1))(
                lambda chip=chip: self.copy(0, chip, p.core).wait_send()
            )
            pl.when((chip >= p.chip) & (p.chip > 0))(
                lambda chip=chip: self.copy(1, chip, p.core).wait_send()
            )


class LineScatter:
    def __init__(self, place, part, mate_in, left_in, right_in, send_sem, recv_sem):
        self.place, self.part = place, part
        self.mate_in, self.left_in, self.right_in = mate_in, left_in, right_in
        self.send_sem, self.recv_sem = send_sem, recv_sem

    def copy(self, way, src, landing, r, chip, to):
        return remote(
            src, landing.at[r, chip], self.send_sem.at[way, r, chip], self.recv_sem.at[way, r, chip],
            self.place.grp, to,
        )

    def to_mate(self, r, chip):
        p = self.place
        return self.copy(0, self.part.at[r, 2 * chip + 1 - p.core], self.mate_in, r, chip, p.mate)

    def to_right(self, r, chip):
        p = self.place
        return self.copy(1, self.part.at[r, 2 * chip + p.core], self.left_in, r, chip, p.seq + 2)

    def to_left(self, r, chip):
        p = self.place
        return self.copy(2, self.part.at[r, 2 * chip + p.core], self.right_in, r, chip, p.seq - 2)

    def step(self, r, chip):
        p = self.place
        last = p.chips - 1
        slot = 2 * chip + p.core

        @pl.when(chip != p.chip)
        def _():
            self.to_mate(r, chip).wait_recv()
            total = self.part[r, slot].astype(jnp.float32) + self.mate_in[r, chip].astype(jnp.float32)
            self.part[r, slot] = total.astype(jnp.bfloat16)

        @pl.when(chip > p.chip)
        def _():
            @pl.when(p.chip > 0)
            def _():
                self.to_right(r, chip).wait_recv()
                self.part[r, slot] = (
                    self.part[r, slot].astype(jnp.float32) + self.left_in[r, chip].astype(jnp.float32)
                ).astype(jnp.bfloat16)

            self.to_right(r, chip).start()

        @pl.when(chip < p.chip)
        def _():
            @pl.when(p.chip < last)
            def _():
                self.to_left(r, chip).wait_recv()
                self.part[r, slot] = (
                    self.part[r, slot].astype(jnp.float32) + self.right_in[r, chip].astype(jnp.float32)
                ).astype(jnp.bfloat16)

            self.to_left(r, chip).start()

    def finish(self, r, out_ref):
        p = self.place
        self.to_mate(r, p.chip).wait_recv()
        out_ref[...] = self.part[r, p.seq].astype(jnp.float32) + self.mate_in[r, p.chip].astype(jnp.float32)

        @pl.when(p.chip > 0)
        def _():
            self.to_right(r, p.chip).wait_recv()
            out_ref[...] += self.left_in[r, p.chip].astype(jnp.float32)

        @pl.when(p.chip < p.chips - 1)
        def _():
            self.to_left(r, p.chip).wait_recv()
            out_ref[...] += self.right_in[r, p.chip].astype(jnp.float32)

    def drain(self, r):
        p = self.place
        for other in range(p.chips):
            self.to_mate(r, other).wait_send()
            pl.when(other > p.chip)(lambda other=other: self.to_right(r, other).wait_send())
            pl.when(other < p.chip)(lambda other=other: self.to_left(r, other).wait_send())


def front_kernel(chips, scale,
                 tokens_ref, gain_one_ref, gain_two_ref, segment_ref, freq_ref, bias_ref,
                 cot_ref, wq_ref, wo_ref, wm_ref,
                 attn_ref, state_ref, cos_ref, sin_ref, mask_ref, q_out_ref, kv_out_ref, n1_all_ref, n2_all_ref,
                 cot_all_ref, wo_all_ref, wq_all_ref, columns_ref, wm1_ref, wm2_ref, wm3_ref,
                 nbuf, n2buf, wq, wo, bias_own, bias, stage, qbuf, kvbuf, columns,
                 lsem, n_send, n_recv, n2_send, n2_recv, c_send, c_recv, o_send, o_recv, ox_send, ox_recv,
                 om_send, om_recv, wq_send, wq_recv, b_send, b_recv, m_send, m_recv, q_send, q_recv, k_send, k_recv):
    p = Place(chips)
    grps = 4
    half = wq_ref.shape[0]
    rows = pl.ds(p.core * half, half)
    mates_rows = pl.ds((1 - p.core) * half, half)
    wm_refs = (wm_ref, wm1_ref, wm2_ref, wm3_ref)
    part = wm_ref.shape[1] // 2

    own = [
        pltpu.make_async_copy(wq_ref, wq.at[0, rows], lsem.at[0]),
        pltpu.make_async_copy(wo_ref, wo.at[p.grp, p.chip, p.core], lsem.at[2]),
        pltpu.make_async_copy(cot_ref, cot_all_ref.at[p.chip, p.core], lsem.at[3]),
    ]
    for copy in own:
        copy.start()
    tokens = tokens_ref[...].astype(jnp.float32)
    nbuf[p.chip, p.core] = rms_scale(tokens, gain_one_ref[...].astype(jnp.float32)).astype(jnp.bfloat16)
    shard = tokens.shape[0]
    lane = lax.broadcasted_iota(jnp.int32, (1, 2 * half), 1)
    bias_wide = bias_ref[...].astype(jnp.float32)
    bias_pair = jnp.concatenate([bias_wide, bias_wide], axis=1)
    bias_own[...] = jnp.broadcast_to(jnp.where(lane // half == p.core, bias_pair, 0.0), bias_own.shape)
    bias[0, p.core] = bias_own[...]
    p.barrier(grps)

    n1_line = RailGather(p, lambda chip, core: nbuf.at[chip, core], n_send, n_recv)
    cot_line = RailGather(p, lambda chip, core: cot_all_ref.at[chip, core], c_send, c_recv)
    n2_line = RailGather(p, lambda chip, core: n2buf.at[chip, core], n2_send, n2_recv)
    out_line = RailGather(p, lambda chip, core: wo.at[p.grp, chip, core], o_send, o_recv)

    def wq_direct(b):
        return remote(wq_ref, wq.at[b, rows], wq_send.at[0, b], wq_recv.at[b, 0], p.peer(b), p.seq)

    def wq_mate(b):
        return remote(wq.at[b, rows], wq.at[b, rows], wq_send.at[1, b], wq_recv.at[b, 1], p.grp, p.mate)

    def bias_direct(b):
        return remote(bias_own, bias.at[b, p.core], b_send.at[0, b], b_recv.at[b, 0], p.peer(b), p.seq)

    def bias_mate(b):
        return remote(bias.at[b, p.core], bias.at[b, p.core], b_send.at[1, b], b_recv.at[b, 1], p.grp, p.mate)

    def m_part(ref, i, j):
        return ref.at[j, pl.ds(i * part, part)]

    def m_direct(b, i, j):
        return remote(
            m_part(wm_ref, i, j), m_part(wm_refs[b], i, j), m_send.at[b, i, j], m_recv.at[b, i, j],
            p.peer(b), p.seq,
        )

    def m_forward(b, j):
        return remote(
            m_part(wm_refs[b], b - 1, j), m_part(wm3_ref, b - 1, j), m_send.at[3, b - 1, j],
            m_recv.at[3, b - 1, j], p.peer(3 - b), p.seq,
        )

    def out_view(grp, i, core):
        return wo.at[grp, pl.ds(i * (chips // 2), chips // 2), core]

    def out_direct(b, i):
        view = out_view(p.grp, i, p.core)
        return remote(view, view, ox_send.at[b, i], ox_recv.at[b, i], p.peer(b), p.seq)

    def out_forward(b):
        view = out_view(p.peer(b), b - 1, p.core)
        return remote(view, view, ox_send.at[3, b - 1], ox_recv.at[3, b - 1], p.peer(3 - b), p.seq)

    def out_mate(b, i, core):
        view = out_view(p.peer(b), i, core)
        return remote(view, view, om_send.at[b, i], om_recv.at[b, i], p.grp, p.mate)

    def q_copy(chip):
        return remote(
            stage.at[chip, pl.ds(0, 3)], qbuf.at[p.chip], q_send.at[chip], q_recv.at[p.chip],
            p.grp, 2 * chip + p.core,
        )

    def q_arrival(chip):
        return remote(stage.at[chip, pl.ds(0, 3)], qbuf.at[chip], q_send.at[chip], q_recv.at[chip], p.grp, p.mate)

    def k_copy(chip, to_chip):
        return remote(
            stage.at[chip, 3], kvbuf.at[p.chip, p.core, chip], k_send.at[0, chip, to_chip],
            k_recv.at[p.chip, p.core, chip], p.grp, 2 * to_chip + p.core,
        )

    def k_mate(head, chip, src=None):
        view = kvbuf.at[head, p.core, chip]
        return remote(
            view if src is None else src, view, k_send.at[1, head, chip],
            k_recv.at[head, p.core, chip], p.grp, p.mate,
        )

    def k_arrival(head, core, chip):
        view = kvbuf.at[head, core, chip]
        return remote(view, view, k_send.at[1, head, chip], k_recv.at[head, core, chip], p.grp, p.mate)

    def make_tables():
        segs = [segment_ref[p.grp, t] for t in range(2 * chips)]
        starts = []
        for t in range(2 * chips):
            first = jnp.int32(t)
            for other in reversed(range(t)):
                first = jnp.where(segs[other] == segs[t], jnp.int32(other), first)
            starts.append(
                jnp.where(segs[t] == 0, jnp.int32(t * shard), chips * shard + (t - first) * shard)
            )

        def own_of(values):
            own = values[0]
            for t in range(1, 2 * chips):
                own = jnp.where(p.seq == t, values[t], own)
            return own

        own_seg, own_start = own_of(segs), own_of(starts)
        row = lax.broadcasted_iota(jnp.int32, (shard, 2 * half), 0)
        column = lax.broadcasted_iota(jnp.int32, (shard, 2 * half), 1)
        freq = freq_ref[...]
        sign = jnp.where(column < half, -1.0, 1.0)
        for chip in range(chips):
            start = jnp.where(p.core == 0, starts[2 * chip], starts[2 * chip + 1])
            angle = (start + row).astype(jnp.float32) * freq
            cos_ref[chip] = jnp.cos(angle)
            sin_ref[chip] = jnp.sin(angle) * sign
        for core in range(2):
            for chip in range(chips):
                t = 2 * chip + core
                seen = jnp.where((segs[t] == 0) | (segs[t] == own_seg), jnp.int32(1), jnp.int32(0))
                allowed = (starts[t] + column <= own_start + row) & (row * 0 + seen > 0)
                block = core * chips + chip
                mask_ref[:, block * shard : (block + 1) * shard] = jnp.where(allowed, 0.0, -1e30)

    own[0].wait()
    for b in range(1, grps):
        wq_direct(b).start()
        bias_direct(b).start()
    wq_mate(0).start()
    bias_mate(0).start()
    n1_line.start()
    own[1].wait()
    out_line.start()
    for b in range(1, grps):
        wq_direct(b).wait_recv()
        wq_mate(b).start()
        bias_direct(b).wait_recv()
        bias_mate(b).start()
    for j in (0, 1):
        m_direct(1, 0, j).start()
        m_direct(2, 1, j).start()
    make_tables()
    for b in range(grps):
        wq_mate(b).wait_recv()
        bias_mate(b).wait_recv()

    @pl.loop(0, chips)
    def _(order):
        @pl.when(order > 0)
        def _():
            n1_line.forward(order)
            out_line.forward(order)

        at = nearest_chip(p.chip, order, chips)
        x = nbuf[at, p.core]
        weights = wq[...].reshape(grps * 2 * half, x.shape[1])
        rows_all = lax.dot_general(x, weights, CONTRACT_LAST, preferred_element_type=jnp.float32)
        cosine, sine = cos_ref[at], sin_ref[at]
        for b in range(grps):
            u = rows_all[:, 2 * half * b : 2 * half * (b + 1)] + (bias[b, 0, 0:1] + bias[b, 1, 0:1])
            turned = u * cosine + pltpu.roll(u, half, 1) * sine
            place = p.peer(b)
            keep = jnp.where((place == grps - 1) & (p.chip >= chips // 2), 1.0, 0.0)
            value = (u * keep + turned * (1.0 - keep)).astype(jnp.bfloat16)
            stage[at, place] = value

            @pl.when(place == grps - 1)
            def _(value=value):
                kvbuf[p.chip, p.core, at] = value

            @pl.when((place < grps - 1) & (at == p.chip))
            def _(value=value, place=place):
                qbuf[p.chip, place] = value

        pl.when(at != p.chip)(lambda: q_copy(at).start())
        for to_chip in range(chips):
            pl.when(to_chip != p.chip)(lambda to_chip=to_chip: k_copy(at, to_chip).start())
        k_mate(p.chip, at, stage.at[at, 3]).start()

    for b in (1, 2):
        out_direct(b, b - 1).start()
    for b in (1, 2):
        out_direct(b, 2 - b).start()
    own[2].wait()
    cot_line.start()

    @pl.loop(0, chips)
    def _(order):
        for head in range(chips):
            @pl.when(head != p.chip)
            def _(head=head):
                chip = nearest_chip(head, order, chips)
                k_arrival(head, p.core, chip).wait_recv()
                k_mate(head, chip).start()

    for chip in range(chips):
        pl.when(chip != p.chip)(lambda chip=chip: q_arrival(chip).wait_recv())
        for head in range(chips):
            k_arrival(head, 1 - p.core, chip).wait_recv()
    cot_line.forward(1)

    mask = mask_ref[...]
    heads_per = H // KVH
    for kv in range(KVH):
        heads = [kv * heads_per + i for i in range(heads_per)]
        queries = jnp.concatenate([qbuf[h % chips, h // chips] for h in heads], axis=0)
        keys = kvbuf[kv].reshape(mask.shape[1], 2 * half)
        values = kvbuf[KVH + kv].reshape(mask.shape[1], 2 * half)
        scores = lax.dot_general(queries, keys, CONTRACT_LAST, preferred_element_type=jnp.float32) * scale
        scores = scores.reshape(heads_per, shard, mask.shape[1]) + mask[None]
        weights = jnp.exp(scores - jnp.max(scores, axis=-1, keepdims=True))
        inverse = 1.0 / jnp.sum(weights, axis=-1, keepdims=True)
        probs = (weights * inverse).astype(jnp.bfloat16).reshape(heads_per * shard, mask.shape[1])
        mixed = jnp.dot(probs, values, preferred_element_type=jnp.float32)
        for i, h in enumerate(heads):
            attn_ref[:, h * 2 * half : (h + 1) * 2 * half] = mixed[i * shard : (i + 1) * shard]
        if kv == 0:
            for b in (1, 2):
                out_direct(b, b - 1).wait_recv()
                out_forward(b).start()
                out_mate(b, b - 1, p.core).start()
            for b in (1, 2):
                for j in (0, 1):
                    m_direct(b, b - 1, j).wait_recv()
                    m_forward(b, j).start()
            m_direct(1, 0, 2).start()
            m_direct(2, 1, 2).start()
        cot_line.forward(kv + 2)

    for b in (1, 2):
        out_direct(b, 2 - b).wait_recv()
        out_mate(b, 2 - b, p.core).start()
    for j in range(3):
        m_direct(1, 1, j).start()
        m_direct(2, 0, j).start()
    attn_low = attn_ref[...].astype(jnp.bfloat16)
    unit = wo.shape[3]
    columns[...] = attn_low.T.reshape(columns.shape)
    for i in (0, 1):
        out_forward(i + 1).wait_recv()
        out_mate(3, i, p.core).start()
    for b in range(1, grps):
        for i in (0, 1):
            out_mate(b, i, 1 - p.core).wait_recv()
    for chip in range(chips):
        out_line.wait_mate(chip)
    state = tokens_ref[...].astype(jnp.float32) + jnp.dot(
        attn_low, wo[...].reshape(grps * chips * 2 * unit, tokens_ref.shape[1]),
        preferred_element_type=jnp.float32,
    )
    state_ref[...] = state
    n2buf[p.chip, p.core] = rms_scale(state, gain_two_ref[...].astype(jnp.float32)).astype(jnp.bfloat16)
    n2_line.start()
    outs = [
        pltpu.make_async_copy(nbuf, n1_all_ref, lsem.at[4]),
        pltpu.make_async_copy(wq, wq_all_ref, lsem.at[5]),
        pltpu.make_async_copy(qbuf, q_out_ref, lsem.at[6]),
        pltpu.make_async_copy(kvbuf, kv_out_ref, lsem.at[7]),
        pltpu.make_async_copy(wo, wo_all_ref, lsem.at[8]),
        pltpu.make_async_copy(columns, columns_ref, lsem.at[9]),
    ]
    for chip in range(chips):
        n1_line.wait_mate(chip)
    for copy in outs:
        copy.start()
    n2_line.forward(1)
    for b in (1, 2):
        m_direct(b, b - 1, 2).wait_recv()
        m_forward(b, 2).start()
    for step in range(2, chips):
        n2_line.forward(step)
    for chip in range(chips):
        cot_line.wait_mate(chip)
        n2_line.wait_mate(chip)
    last = pltpu.make_async_copy(n2buf, n2_all_ref, lsem.at[10])
    last.start()
    for b in (1, 2):
        for j in range(3):
            m_direct(b, 2 - b, j).wait_recv()
            m_forward(3 - b, j).wait_recv()
    for copy in outs:
        copy.wait()
    last.wait()
    n1_line.drain()
    n2_line.drain()
    out_line.drain()
    cot_line.drain()
    for b in range(grps):
        wq_mate(b).wait_send()
        bias_mate(b).wait_send()
    for b in range(1, grps):
        wq_direct(b).wait_send()
        bias_direct(b).wait_send()
        for i in (0, 1):
            out_mate(b, i, p.core).wait_send()
    for b in (1, 2):
        for i in (0, 1):
            for j in range(3):
                m_direct(b, i, j).wait_send()
            out_direct(b, i).wait_send()
        for j in range(3):
            m_forward(b, j).wait_send()
        out_forward(b).wait_send()
    for chip in range(chips):
        pl.when(chip != p.chip)(lambda chip=chip: q_copy(chip).wait_send())
        for other in range(chips):
            pl.when(other != p.chip)(lambda chip=chip, other=other: k_copy(chip, other).wait_send())
            k_mate(other, chip).wait_send()


def front_call(tokens, gain_one, gain_two, segments, freqs, bias, cot, qkv_weight, out_weight, mlp_rows):
    chips = segments.shape[1] // 2
    grps = 4
    shard, width = tokens.shape
    half = qkv_weight.shape[0]
    vm, dma = pltpu.VMEM, pltpu.SemaphoreType.DMA
    anyspace = pl.BlockSpec(memory_space=pl.ANY)
    vspec = pl.BlockSpec(memory_space=pltpu.VMEM)
    low, wide = jnp.bfloat16, jnp.float32
    struct = jax.ShapeDtypeStruct
    wo_shape = (grps, chips, 2) + out_weight.shape
    columns_shape = (grps, 2 * chips, out_weight.shape[0], shard)
    return pl.pallas_call(
        functools.partial(front_kernel, chips, 1.0 / math.sqrt(HD)),
        out_shape=(
            struct((shard, H * HD), wide),
            struct((shard, width), wide),
            struct((chips, shard, HD), wide),
            struct((chips, shard, HD), wide),
            struct((shard, 2 * chips * shard), wide),
            struct((chips, 3, shard, HD), low),
            struct((chips, 2, chips, shard, HD), low),
            struct((chips, 2, shard, width), low),
            struct((chips, 2, shard, width), low),
            struct((chips, 2, shard, width), low),
            struct(wo_shape, low),
            struct((grps, 2 * half, width), low),
            struct(columns_shape, low),
        ) + (struct(mlp_rows.shape, low),) * 3,
        in_specs=[vspec] * 3
        + [pl.BlockSpec(memory_space=pltpu.SMEM)]
        + [vspec] * 2
        + [anyspace] * 4,
        out_specs=(vspec,) * 5 + (anyspace,) * 11,
        scratch_shapes=[
            vm((chips, 2, shard, width), low),
            vm((chips, 2, shard, width), low),
            vm((grps, 2 * half, width), low),
            vm(wo_shape, low),
            vm((8, HD), wide),
            vm((grps, 2, 8, HD), wide),
            vm((chips, grps, shard, HD), low),
            vm((chips, 3, shard, HD), low),
            vm((chips, 2, chips, shard, HD), low),
            vm(columns_shape, low),
            dma((11,)),
            dma((3, chips)), dma((chips, 2)),
            dma((3, chips)), dma((chips, 2)),
            dma((3, chips)), dma((chips, 2)),
            dma((3, chips)), dma((chips, 2)),
            dma((grps, 2)), dma((grps, 2)), dma((grps, 2)), dma((grps, 2)),
            dma((2, grps)), dma((grps, 2)),
            dma((2, grps)), dma((grps, 2)),
            dma((grps, 2, 3)), dma((grps, 2, 3)),
            dma((chips,)), dma((chips,)),
            dma((2, chips, chips)), dma((chips, 2, chips)),
        ],
        compiler_params=pltpu.CompilerParams(
            collective_id=2, has_side_effects=True, vmem_limit_bytes=60 * 2**20
        ),
        name="front",
    )(tokens, gain_one, gain_two, segments, freqs, bias, cot, qkv_weight, out_weight, mlp_rows)


def mlp_kernel(chips, grps, row_tiles, n2_ref, cot_ref, columns_ref, *refs):
    w_refs, refs = refs[:grps], refs[grps:]
    (
        n2g_ref, outp_ref, grads_ref, owned_ref, tok, w, acts, part, mate_in, left_in, right_in, stage, owned,
        lsem, ssend, srecv, wsem, osem, a_send, a_recv,
    ) = refs
    p = Place(chips)
    slots = 2 * chips
    shard, width = n2_ref.shape[1:]
    units = w.shape[1]
    block = units // grps
    tile = units // row_tiles
    loads = [
        pltpu.make_async_copy(n2_ref, tok.at[0], lsem.at[0]),
        pltpu.make_async_copy(cot_ref, tok.at[1], lsem.at[1]),
        pltpu.make_async_copy(columns_ref.at[:, p.seq], owned.at[:, :, pl.ds(pl.multiple_of(p.seq * shard, shard), shard)], lsem.at[2]),
    ]
    for copy in loads:
        copy.start()

    def w_copy(j, b):
        return pltpu.make_async_copy(w_refs[b].at[j], w.at[j, pl.ds(b * block, block)], wsem.at[j, b])

    for j in range(3):
        for b in range(grps):
            w_copy(j, b).start()

    def seq_peer(i):
        return (p.seq + i) % slots

    barrier = pltpu.get_barrier_semaphore()
    for i in range(1, slots):
        pl.semaphore_signal(barrier, inc=1, device_id=(p.grp, seq_peer(i)), device_id_type=MESH)
    pl.semaphore_wait(barrier, slots - 1)
    scatter = LineScatter(p, part, mate_in, left_in, right_in, ssend, srecv)

    def a_copy(i, to, slot):
        return remote(
            columns_ref.at[:, to], owned.at[:, :, pl.ds(pl.multiple_of(slot * shard, shard), shard)],
            a_send.at[i], a_recv.at[slot], p.grp, to,
        )

    for i in range(1, slots):
        a_copy(i, seq_peer(i), p.seq).start()
    for copy in loads:
        copy.wait()
    for j in range(3):
        for b in range(grps):
            w_copy(j, b).wait()

    @pl.loop(0, chips + 1)
    def _(order):
        @pl.when(order < chips)
        def _():
            at = nearest_chip(p.chip, chips - 1 - order, chips)
            x = tok[0, pl.ds(2 * at, 2)].reshape(2 * shard, width)
            y = tok[1, pl.ds(2 * at, 2)].reshape(2 * shard, width)
            gate = lax.dot_general(x, w[0], CONTRACT_LAST, preferred_element_type=jnp.float32)
            up = lax.dot_general(x, w[1], CONTRACT_LAST, preferred_element_type=jnp.float32)
            unit_grad = lax.dot_general(y, w[2], CONTRACT_LAST, preferred_element_type=jnp.float32)
            sig = 1.0 / (1.0 + jnp.exp(-gate))
            silu = gate * sig
            rows = pl.ds(at * (2 * shard), 2 * shard)
            gate_grad = (unit_grad * up * sig * (1.0 + gate * (1.0 - sig))).astype(jnp.bfloat16)
            up_grad = (unit_grad * silu).astype(jnp.bfloat16)
            acts[0, rows] = gate_grad
            acts[1, rows] = up_grad
            acts[2, rows] = (silu * up).astype(jnp.bfloat16)
            back = jnp.dot(gate_grad, w[0], preferred_element_type=jnp.float32) + jnp.dot(
                up_grad, w[1], preferred_element_type=jnp.float32
            )
            part[0, pl.ds(2 * at, 2)] = back.astype(jnp.bfloat16).reshape(2, shard, width)
            scatter.to_mate(0, at).start()

        pl.when(order > 0)(lambda: scatter.step(0, nearest_chip(p.chip, chips - order, chips)))

    def out_copy(t):
        return pltpu.make_async_copy(
            stage.at[t % 2],
            grads_ref.at[t // row_tiles, pl.ds((t % row_tiles) * tile, tile)],
            osem.at[t % 2],
        )

    @pl.loop(0, 3 * row_tiles)
    def _(t):
        @pl.when(t < chips)
        def _():
            at = nearest_chip(p.chip, chips - 1 - t, chips)
            h = acts[2, pl.ds(at * (2 * shard), 2 * shard)]
            part[1, pl.ds(2 * at, 2)] = (
                jnp.dot(h, w[2], preferred_element_type=jnp.float32)
                .astype(jnp.bfloat16).reshape(2, shard, width)
            )
            scatter.to_mate(1, at).start()

        @pl.when((t > 0) & (t <= chips))
        def _():
            scatter.step(1, nearest_chip(p.chip, chips - t, chips))

        @pl.when(t >= 2)
        def _():
            out_copy(t - 2).wait()

        kind = t // row_tiles
        lhs = acts[kind, :, pl.ds(pl.multiple_of((t % row_tiles) * tile, 128), tile)]
        rhs = tok[kind // 2].reshape(2 * chips * shard, width)
        stage[t % 2] = lax.dot_general(
            lhs, rhs, CONTRACT_FIRST, preferred_element_type=jnp.float32
        ).astype(jnp.bfloat16)
        out_copy(t).start()

    scatter.finish(0, n2g_ref)
    for i in range(1, slots):
        a_copy(i, seq_peer(i), seq_peer(i)).wait_recv()
    moved = pltpu.make_async_copy(owned, owned_ref, lsem.at[0])
    moved.start()
    scatter.finish(1, outp_ref)
    out_copy(3 * row_tiles - 2).wait()
    out_copy(3 * row_tiles - 1).wait()
    moved.wait()
    scatter.drain(0)
    scatter.drain(1)
    for i in range(1, slots):
        a_copy(i, seq_peer(i), p.seq).wait_send()


def mlp_call(n2_all, cot_all, columns, w_blocks, row_tiles=3):
    grps, (_, block, width) = len(w_blocks), w_blocks[0].shape
    slots, shard, _ = cot_all.shape
    chips = slots // 2
    units = grps * block
    vm, anyspace = pltpu.VMEM, pl.BlockSpec(memory_space=pl.ANY)
    vspec = pl.BlockSpec(memory_space=pltpu.VMEM)
    dma = pltpu.SemaphoreType.DMA
    owned_shape = columns.shape[:1] + columns.shape[2:3] + (slots * shard,)
    return pl.pallas_call(
        functools.partial(mlp_kernel, chips, grps, row_tiles),
        out_shape=(
            jax.ShapeDtypeStruct((shard, width), jnp.float32),
            jax.ShapeDtypeStruct((shard, width), jnp.float32),
            jax.ShapeDtypeStruct((3, units, width), jnp.bfloat16),
            jax.ShapeDtypeStruct(owned_shape, jnp.bfloat16),
        ),
        in_specs=[anyspace] * (3 + grps),
        out_specs=(vspec, vspec, anyspace, anyspace),
        scratch_shapes=[
            vm((2, slots, shard, width), jnp.bfloat16),
            vm((3, units, width), jnp.bfloat16),
            vm((3, slots * shard, units), jnp.bfloat16),
            vm((2, slots, shard, width), jnp.bfloat16),
            vm((2, chips, shard, width), jnp.bfloat16),
            vm((2, chips, shard, width), jnp.bfloat16),
            vm((2, chips, shard, width), jnp.bfloat16),
            vm((2, units // row_tiles, width), jnp.bfloat16),
            vm(owned_shape, jnp.bfloat16),
            dma((3,)), dma((3, 2, chips)), dma((3, 2, chips)),
            dma((3, grps)), dma((2,)), dma((slots,)), dma((slots,)),
        ],
        compiler_params=pltpu.CompilerParams(
            collective_id=1, has_side_effects=True, vmem_limit_bytes=62 * 2**20
        ),
        name="mlp",
    )(n2_all, cot_all, columns, *w_blocks)


def unturn(rows, cosine, sine, half):
    return rows * cosine + pltpu.roll(rows * sine, half, 1)


def back_kernel(chips, scale,
                n2g_ref, state_ref, cot_ref, tokens_ref, gain_one_ref, gain_two_ref, attn_ref, q_ref, kv_ref,
                mask_ref, cos_ref, sin_ref, wq_ref, wo_ref, n1_ref, terms_ref, owned_ref,
                tok_grad_ref, wq_grad_ref, wo_grad_ref, gain_ref, mlp_ref,
                wo, stbuf, n1x, at_all, dq_stage, gq_in, kv_part, km_in, k_sum, k_own, kr_in,
                cols, part, left_in, right_in, wgrad, wm_in, w_send_buf, w_in, o_terms, o_send_buf, o_in,
                m_own, m_in, gain_own, gain_in, gain_mid, gain_mid_in, state_grad,
                lsem, s_send, s_recv, q_send, q_recv, km_send, km_recv, kr_send, kr_recv,
                r_send, r_recv, wm_send, wm_recv, w_send, w_recv, o_send, o_recv, m_send, m_recv,
                ml_sem, g_send, g_recv, h_send, h_recv):
    p = Place(chips)
    grps = 4
    shard, width = n2g_ref.shape
    slots = 2 * chips
    heads_per = H // KVH
    half = HD // 2
    low, wide = jnp.bfloat16, jnp.float32
    block = terms_ref.shape[1] // grps
    mhalf = block // 2
    last = chips - 1

    loads = [
        pltpu.make_async_copy(wo_ref, wo, lsem.at[0]),
        pltpu.make_async_copy(n1_ref.at[:, p.core], n1x.at[:, :, pl.ds(0, width)], lsem.at[1]),
        pltpu.make_async_copy(owned_ref, at_all, lsem.at[2]),
    ]
    for copy in loads:
        copy.start()

    def seq_peer(i):
        return (p.seq + i) % slots

    barrier = pltpu.get_barrier_semaphore()
    for i in range(1, slots):
        pl.semaphore_signal(barrier, inc=1, device_id=(p.grp, seq_peer(i)), device_id_type=MESH)
    for b in range(1, grps):
        pl.semaphore_signal(barrier, inc=1, device_id=(p.peer(b), p.seq), device_id_type=MESH)
    pl.semaphore_wait(barrier, slots - 1 + grps - 1)

    def m_rows(b, i):
        return terms_ref.at[:, pl.ds(b * block + i * mhalf, mhalf)]

    def m_copy(slot, src, peer):
        return remote(src, m_in.at[slot], m_send.at[slot], m_recv.at[slot], p.peer(peer), p.seq)

    m_first = [
        m_copy(1, m_rows(3, 0), 1), m_copy(3, m_rows(3, 1), 2),
        m_copy(0, m_rows(1, 0), 1), m_copy(2, m_rows(2, 1), 2),
    ]
    for copy in m_first:
        copy.start()
    m_second = [m_copy(4, m_own.at[0], 1), m_copy(5, m_own.at[1], 2)]
    m_loads = [
        pltpu.make_async_copy(m_rows(1, 1), m_own.at[0], ml_sem.at[0]),
        pltpu.make_async_copy(m_rows(2, 0), m_own.at[1], ml_sem.at[1]),
        pltpu.make_async_copy(m_rows(0, 0), m_own.at[2], ml_sem.at[2]),
        pltpu.make_async_copy(m_rows(0, 1), m_own.at[3], ml_sem.at[3]),
    ]
    for copy in m_loads:
        copy.start()

    state = state_ref[...]
    gain_two = gain_two_ref[...].astype(wide)
    n2g = n2g_ref[...]
    scale_two = lax.rsqrt(jnp.mean(state * state, axis=-1, keepdims=True) + EPS)
    normed = state * scale_two
    gain_own[1] = jnp.sum(n2g * normed, axis=0, keepdims=True)
    lifted = n2g * gain_two
    state_grad[...] = cot_ref[...].astype(wide) + scale_two * (
        lifted - normed * jnp.mean(lifted * normed, axis=-1, keepdims=True)
    )
    state_low = state_grad[...].astype(low)
    stbuf[p.chip, p.core] = state_low
    line = RailGather(p, lambda chip, core: stbuf.at[chip, core], s_send, s_recv)
    line.start()

    attn = attn_ref[...]
    unit = wo.shape[0] // (grps * slots)
    loads[0].wait()
    attn_grad = lax.dot_general(state_low, wo[...], CONTRACT_LAST, preferred_element_type=wide).astype(low)
    line.forward(1)
    mask = mask_ref[...]
    keys_total = mask.shape[1]
    own_cos, own_sin = cos_ref[p.chip], sin_ref[p.chip]

    def km_copy(head):
        return remote(
            kv_part.at[head, 1 - p.core], km_in.at[head], km_send.at[head], km_recv.at[head], p.grp, p.mate
        )

    def kr_copy(head):
        return remote(
            k_sum.at[head], kr_in.at[p.chip], kr_send.at[head], kr_recv.at[p.chip], p.grp, 2 * head + p.core
        )

    def kr_arrival(chip):
        return remote(k_sum.at[chip], kr_in.at[chip], kr_send.at[chip], kr_recv.at[chip], p.grp, p.mate)

    def q_copy(chip):
        return remote(
            dq_stage.at[chip], gq_in.at[p.chip], q_send.at[chip], q_recv.at[p.chip], p.grp, 2 * chip + p.core
        )

    def q_arrival(chip):
        return remote(dq_stage.at[chip], gq_in.at[chip], q_send.at[chip], q_recv.at[chip], p.grp, p.mate)

    def key_sum(head):
        km_copy(head).wait_recv()
        total = kv_part[head, p.core].astype(wide) + km_in[head].astype(wide)

        @pl.when(p.chip == head)
        def _():
            k_own[...] = total

        @pl.when(p.chip != head)
        def _():
            k_sum[head] = total.astype(low)
            kr_copy(head).start()

    for kv in range(KVH):
        heads = [kv * heads_per + i for i in range(heads_per)]
        queries = jnp.concatenate([q_ref[h % chips, h // chips] for h in heads], axis=0)
        grads = jnp.concatenate([attn_grad[:, h * HD : (h + 1) * HD] for h in heads], axis=0)
        mixed = jnp.concatenate([attn[:, h * HD : (h + 1) * HD] for h in heads], axis=0)
        delta = jnp.sum(grads.astype(wide) * mixed, axis=-1, keepdims=True)
        keys = kv_ref[kv].reshape(keys_total, HD)
        values = kv_ref[KVH + kv].reshape(keys_total, HD)
        scores = lax.dot_general(queries, keys, CONTRACT_LAST, preferred_element_type=wide) * scale
        scores = (scores.reshape(heads_per, shard, keys_total) + mask[None]).reshape(heads_per * shard, keys_total)
        weights = jnp.exp(scores - jnp.max(scores, axis=-1, keepdims=True))
        probs = weights * (1.0 / jnp.sum(weights, axis=-1, keepdims=True))
        prob_grad = lax.dot_general(grads, values, CONTRACT_LAST, preferred_element_type=wide)
        score_grad = (probs * (prob_grad - delta)).astype(low)
        key_grad = lax.dot_general(score_grad, queries, CONTRACT_FIRST, preferred_element_type=wide) * scale
        value_grad = lax.dot_general(probs.astype(low), grads, CONTRACT_FIRST, preferred_element_type=wide)
        kv_part[kv] = key_grad.astype(low).reshape(2, chips, shard, HD)
        kv_part[KVH + kv] = value_grad.astype(low).reshape(2, chips, shard, HD)
        km_copy(kv).start()
        km_copy(KVH + kv).start()
        query_grad = jnp.dot(score_grad, keys, preferred_element_type=wide) * scale
        for i, h in enumerate(heads):
            turned = unturn(query_grad[i * shard : (i + 1) * shard], own_cos, own_sin, half).astype(low)
            dq_stage[h % chips, h // chips] = turned

            @pl.when(p.chip == h % chips)
            def _(turned=turned, h=h):
                gq_in[h % chips, h // chips] = turned

        line.forward(2 + kv)
    for chip in range(chips):
        pl.when(chip != p.chip)(lambda chip=chip: q_copy(chip).start())
    for head in (0, 2, 1, 3):
        key_sum(head)
    loads[1].wait()
    lane = lax.broadcasted_iota(jnp.int32, (chips, shard, HD), 2)
    n1x[:, :, width:] = jnp.where(lane == 0, 1.0, 0.0).astype(low)
    for chip in range(chips):
        line.wait_mate(chip)
    loads[2].wait()
    o_terms[...] = jnp.dot(
        at_all[...].reshape(grps * unit, slots * shard), stbuf[...].reshape(slots * shard, width),
        preferred_element_type=wide,
    ).reshape(grps, unit, width)
    o_send_buf[...] = o_terms[...].astype(low)

    def o_copy(b):
        return remote(
            o_send_buf.at[p.peer(b)], o_in.at[b], o_send.at[b], o_recv.at[b], p.peer(b), p.seq
        )

    for b in range(1, grps):
        o_copy(b).start()

    def m_add(dst, src):
        for j in range(3):
            @pl.loop(0, mhalf // 16)
            def _(t, j=j):
                rows = pl.ds(pl.multiple_of(t * 16, 16), 16)
                m_own[dst, j, rows] = (
                    m_own[dst, j, rows].astype(wide) + m_in[src, j, rows].astype(wide)
                ).astype(low)

    for chip in range(chips):
        pl.when(chip != p.chip)(lambda chip=chip: q_arrival(chip).wait_recv())
        pl.when(chip != p.chip)(lambda chip=chip: kr_arrival(chip).wait_recv())
    is_value = jnp.where(p.chip >= chips // 2, 1.0, 0.0)

    @pl.loop(0, chips)
    def _(chip):
        key_total = k_own[chip]
        for other in range(chips):
            key_total = key_total + jnp.where(other == p.chip, 0.0, kr_in[other, chip].astype(wide))
        turned = unturn(key_total, cos_ref[chip], sin_ref[chip], half)
        last_head = (key_total * is_value + turned * (1.0 - is_value)).astype(low)
        for b in range(grps):
            place = p.peer(b)
            query_head = gq_in[chip, jnp.minimum(place, grps - 2)]
            cols[chip, :, b * HD : (b + 1) * HD] = jnp.where(place == grps - 1, last_head, query_head)
        part[chip] = jnp.dot(
            cols[chip], wq_ref[...], preferred_element_type=wide
        ).astype(low)

    def to_right(chip):
        return remote(part.at[chip], left_in.at[chip], r_send.at[0, chip], r_recv.at[0, chip], p.grp, p.seq + 2)

    def to_left(chip):
        return remote(part.at[chip], right_in.at[chip], r_send.at[1, chip], r_recv.at[1, chip], p.grp, p.seq - 2)

    def rail_step(order):
        far = last - order

        @pl.when(far > p.chip)
        def _():
            @pl.when(p.chip > 0)
            def _():
                to_right(far).wait_recv()
                part[far] = (part[far].astype(wide) + left_in[far].astype(wide)).astype(low)

            to_right(far).start()

        @pl.when(order < p.chip)
        def _():
            @pl.when(p.chip < last)
            def _():
                to_left(order).wait_recv()
                part[order] = (part[order].astype(wide) + right_in[order].astype(wide)).astype(low)

            to_left(order).start()

    rail_step(0)
    wgrad[...] = lax.dot_general(
        cols[...].reshape(chips * shard, grps * HD), n1x[...].reshape(chips * shard, width + HD),
        CONTRACT_FIRST, preferred_element_type=wide,
    ).reshape(grps, 2, half, width + HD)
    wm = remote(wgrad.at[:, 1 - p.core], wm_in, wm_send, wm_recv, p.grp, p.mate)
    wm.start()
    rail_step(1)
    wm.wait_recv()
    w_send_buf[...] = (wgrad[:, p.core] + wm_in[...]).astype(low)

    def w_copy(b):
        return remote(w_send_buf.at[b], w_in.at[b], w_send.at[b], w_recv.at[b], p.peer(b), p.seq)

    for b in range(1, grps):
        w_copy(b).start()
    rail_step(2)
    m_loads[0].wait()
    m_first[1].wait_recv()
    m_add(0, 3)
    m_second[0].start()
    m_loads[1].wait()
    m_first[0].wait_recv()
    m_add(1, 1)
    m_second[1].start()
    rail_step(3)

    tokens = tokens_ref[...].astype(wide)
    tok_grad_ref[...] = part[p.chip].astype(wide)

    @pl.when(p.chip > 0)
    def _():
        to_right(p.chip).wait_recv()
        tok_grad_ref[...] += left_in[p.chip].astype(wide)

    @pl.when(p.chip < last)
    def _():
        to_left(p.chip).wait_recv()
        tok_grad_ref[...] += right_in[p.chip].astype(wide)

    n1g = tok_grad_ref[...]
    scale_one = lax.rsqrt(jnp.mean(tokens * tokens, axis=-1, keepdims=True) + EPS)
    normed = tokens * scale_one
    gain_own[0] = jnp.sum(n1g * normed, axis=0, keepdims=True)
    lifted = n1g * gain_one_ref[...].astype(wide)
    tok_grad_ref[...] = state_grad[...] + scale_one * (
        lifted - normed * jnp.mean(lifted * normed, axis=-1, keepdims=True)
    )

    def g_copy(i):
        return remote(gain_own, gain_in.at[i], g_send.at[i], g_recv.at[i], p.grp, seq_peer(i))

    for i in range(1, slots):
        g_copy(i).start()
    total = gain_own[...]
    for i in range(1, slots):
        g_copy(i).wait_recv()
        total = total + gain_in[i]
    gain_mid[...] = total

    def h_copy(b):
        return remote(gain_mid, gain_mid_in.at[b], h_send.at[b], h_recv.at[b], p.peer(b), p.seq)

    for b in range(1, grps):
        h_copy(b).start()

    wo_grad = o_terms[p.grp]
    wq_grad = wgrad[0, p.core] + wm_in[0]
    for b in range(1, grps):
        o_copy(b).wait_recv()
        wo_grad = wo_grad + o_in[b].astype(wide)
        w_copy(b).wait_recv()
        wq_grad = wq_grad + w_in[b].astype(wide)
    wo_grad_ref[...] = wo_grad
    wq_grad_ref[...] = wq_grad
    total = gain_mid[...]
    for b in range(1, grps):
        h_copy(b).wait_recv()
        total = total + gain_mid_in[b]
    gain_ref[...] = total

    m_loads[2].wait()
    m_loads[3].wait()

    def m_total(own, direct, second, i):
        for j in range(3):
            @pl.loop(0, mhalf // 16)
            def _(t, j=j):
                rows = pl.ds(pl.multiple_of(t * 16, 16), 16)
                mlp_ref[j, pl.ds(pl.multiple_of(i * mhalf + t * 16, 16), 16)] = (
                    m_own[own, j, rows].astype(wide) + m_in[direct, j, rows].astype(wide)
                ) + m_in[second, j, rows].astype(wide)

    m_first[2].wait_recv()
    m_second[1].wait_recv()
    m_total(2, 0, 5, 0)
    m_first[3].wait_recv()
    m_second[0].wait_recv()
    m_total(3, 2, 4, 1)

    for copy in m_first + m_second:
        copy.wait_send()
    line.drain()
    wm.wait_send()
    for i in range(1, slots):
        g_copy(i).wait_send()
    for b in range(1, grps):
        o_copy(b).wait_send()
        w_copy(b).wait_send()
        h_copy(b).wait_send()
    for chip in range(chips):
        km_copy(chip).wait_send()

        @pl.when(chip != p.chip)
        def _(chip=chip):
            q_copy(chip).wait_send()
            kr_copy(chip).wait_send()

        pl.when(chip > p.chip)(lambda chip=chip: to_right(chip).wait_send())
        pl.when(chip < p.chip)(lambda chip=chip: to_left(chip).wait_send())


def back_call(n2g, state, cotangent, tokens, gain_one, gain_two, attn, q_heads, kv_heads, mask, cosine, sine,
              qkv_all, out_full, n1_all, terms, owned):
    chips = cosine.shape[0]
    grps = 4
    slots = 2 * chips
    shard, width = tokens.shape
    att, block = out_full.shape[0], terms.shape[1] // grps
    unit, half = att // (grps * slots), HD // 2
    vm, dma = pltpu.VMEM, pltpu.SemaphoreType.DMA
    anyspace = pl.BlockSpec(memory_space=pl.ANY)
    vspec = pl.BlockSpec(memory_space=pltpu.VMEM)
    low, wide = jnp.bfloat16, jnp.float32
    struct = jax.ShapeDtypeStruct
    return pl.pallas_call(
        functools.partial(back_kernel, chips, 1.0 / math.sqrt(HD)),
        out_shape=(
            struct((shard, width), wide),
            struct((half, width + HD), wide),
            struct((unit, width), wide),
            struct((2, 1, width), wide),
            struct((3, block, width), wide),
        ),
        in_specs=[vspec] * 13 + [anyspace] * 4,
        out_specs=(vspec,) * 5,
        scratch_shapes=[
            vm((att, width), low),
            vm((chips, 2, shard, width), low),
            vm((chips, shard, width + HD), low),
            vm((grps, unit, slots * shard), low),
            vm((chips, 3, shard, HD), low),
            vm((chips, 3, shard, HD), low),
            vm((chips, 2, chips, shard, HD), low),
            vm((chips, chips, shard, HD), low),
            vm((chips, chips, shard, HD), low),
            vm((chips, shard, HD), wide),
            vm((chips, chips, shard, HD), low),
            vm((chips, shard, grps * HD), low),
            vm((chips, shard, width), low),
            vm((chips, shard, width), low),
            vm((chips, shard, width), low),
            vm((grps, 2, half, width + HD), wide),
            vm((grps, half, width + HD), wide),
            vm((grps, half, width + HD), low),
            vm((grps, half, width + HD), low),
            vm((grps, unit, width), wide),
            vm((grps, unit, width), low),
            vm((grps, unit, width), low),
            vm((4, 3, block // 2, width), low),
            vm((6, 3, block // 2, width), low),
            vm((2, 1, width), wide),
            vm((slots, 2, 1, width), wide),
            vm((2, 1, width), wide),
            vm((grps, 2, 1, width), wide),
            vm((shard, width), wide),
            dma((3,)),
            dma((3, chips)), dma((chips, 2)),
            dma((chips,)), dma((chips,)),
            dma((chips,)), dma((chips,)),
            dma((chips,)), dma((chips,)),
            dma((2, chips)), dma((2, chips)),
            dma, dma,
            dma((grps,)), dma((grps,)),
            dma((grps,)), dma((grps,)),
            dma((6,)), dma((6,)),
            dma((4,)),
            dma((slots,)), dma((slots,)),
            dma((grps,)), dma((grps,)),
        ],
        compiler_params=pltpu.CompilerParams(
            collective_id=3, has_side_effects=True, vmem_limit_bytes=62 * 2**20
        ),
        name="back",
    )(n2g, state, cotangent, tokens, gain_one, gain_two, attn, q_heads, kv_heads, mask, cosine, sine,
      qkv_all, out_full, n1_all, terms, owned)


def columns_to_owners(rows, row_unit):
    grp_count, seq_count = lax.axis_size("grp"), lax.axis_size("seq")
    tok_rows = rows.shape[0]
    split = rows.reshape(tok_rows, grp_count, seq_count, row_unit).transpose(2, 0, 1, 3)
    split = split.reshape(seq_count * tok_rows, grp_count * row_unit)
    return lax.all_to_all(split, "seq", split_axis=0, concat_axis=0, tiled=True)


def owners_to_columns(rows, row_unit):
    grp_count, seq_count = lax.axis_size("grp"), lax.axis_size("seq")
    tok_rows = rows.shape[0] // seq_count
    moved = lax.all_to_all(rows, "seq", split_axis=0, concat_axis=0, tiled=True)
    moved = moved.reshape(seq_count, tok_rows, grp_count, row_unit).transpose(1, 2, 0, 3)
    return moved.reshape(tok_rows, grp_count * seq_count * row_unit)


def plain_mlp(normed_two, cotangent_all, mlp_weight):
    contract_last, contract_first = CONTRACT_LAST, CONTRACT_FIRST
    mlp_rows = lax.all_gather(mlp_weight, "grp", axis=0, tiled=True)
    normed_two_all = lax.all_gather(normed_two, "seq", axis=0, tiled=True)
    gate_rows, upper_rows, down_rows = mlp_rows[:, 0, :], mlp_rows[:, 1, :], mlp_rows[:, 2, :]
    gate_vals = lax.dot_general(
        normed_two_all, gate_rows, contract_last, preferred_element_type=jnp.float32
    )
    upper_vals = lax.dot_general(
        normed_two_all, upper_rows, contract_last, preferred_element_type=jnp.float32
    )
    unit_wide, pull_back = jax.vjp(swish_product, gate_vals, upper_vals)
    unit_low = unit_wide.astype(jnp.bfloat16)
    unit_grad = lax.dot_general(
        cotangent_all, down_rows, contract_last, preferred_element_type=jnp.float32
    )
    gate_grad, upper_grad = pull_back(unit_grad)
    gate_grad = gate_grad.astype(jnp.bfloat16)
    upper_grad = upper_grad.astype(jnp.bfloat16)
    input_grad = jnp.dot(gate_grad, gate_rows, preferred_element_type=jnp.float32) + jnp.dot(
        upper_grad, upper_rows, preferred_element_type=jnp.float32
    )
    grad_part = lax.psum_scatter(
        input_grad.astype(jnp.bfloat16), "seq", scatter_dimension=0, tiled=True
    ).astype(jnp.float32)
    out_part = lax.psum_scatter(
        jnp.dot(unit_low, down_rows, preferred_element_type=jnp.float32).astype(jnp.bfloat16),
        "seq",
        scatter_dimension=0,
        tiled=True,
    ).astype(jnp.float32)
    mlp_terms = jnp.stack(
        [
            lax.dot_general(
                gate_grad, normed_two_all, contract_first, preferred_element_type=jnp.float32
            ),
            lax.dot_general(
                upper_grad, normed_two_all, contract_first, preferred_element_type=jnp.float32
            ),
            lax.dot_general(
                unit_low, cotangent_all, contract_first, preferred_element_type=jnp.float32
            ),
        ],
        axis=1,
    )
    mlp_grad = lax.psum_scatter(mlp_terms, "grp", scatter_dimension=0, tiled=True)
    return grad_part, out_part, mlp_grad


def padded_rows(mlp_weight):
    rows = mlp_weight.transpose(1, 0, 2)
    return jnp.pad(rows, ((0, 0), (0, -rows.shape[1] % 32), (0, 0)))


def per_device(
    tokens,
    cotangent,
    shard_segment,
    gain_attn,
    qkv_weight,
    qkv_bias,
    out_weight,
    gain_mlp,
    mlp_weight,
):
    tok_rows = tokens.shape[0]
    seq_count = lax.axis_size("seq")
    grp_count = lax.axis_size("grp")
    group_tok = tok_rows * seq_count
    heads_per = H // KVH
    kv_width = KVH * HD
    att_width = H * HD
    query_rows = heads_per * tok_rows
    score_scale = 1.0 / math.sqrt(HD)
    contract_last = CONTRACT_LAST
    contract_first = CONTRACT_FIRST
    seq_place = lax.axis_index("seq")
    grp_place = lax.axis_index("grp")
    use_kernels = (seq_count, grp_count, H, KVH, HD) == (8, 4, 12, 2, 128)
    if use_kernels:
        freqs = THETA ** (-(jnp.arange(HD // 2, dtype=jnp.float32) * 2.0) / HD)
        freqs = jnp.concatenate([freqs, freqs])[None, :]
        gain_rows = (gain_attn[None, :], gain_mlp[None, :])
        own_rows = padded_rows(mlp_weight)
        (
            attn_wide, state, cosine, sine, mask, q_heads, kv_heads, n1_all, n2_all, cot_all, out_all,
            qkv_all, columns, *peer_rows
        ) = front_call(
            tokens, *gain_rows, shard_segment, freqs, qkv_bias[None, :], cotangent, qkv_weight, out_weight,
            own_rows,
        )
        by_slot = lambda rows: rows.reshape((seq_count,) + rows.shape[2:])
        grad_part, out_part, mlp_terms, owned = mlp_call(
            by_slot(n2_all), by_slot(cot_all), columns, [own_rows, *peer_rows]
        )
        output = (state + out_part).astype(jnp.bfloat16)
        token_grad, qkv_terms, out_grad, gain_sums, mlp_sums = back_call(
            grad_part, state, cotangent, tokens, *gain_rows, attn_wide, q_heads, kv_heads, mask,
            cosine, sine, qkv_all.reshape(-1, qkv_all.shape[-1]),
            out_all.reshape(att_width, -1), n1_all, mlp_terms, owned,
        )
        width = tokens.shape[1]
        own = width // (grp_count * seq_count)
        gain_parts = lax.dynamic_slice_in_dim(
            gain_sums[:, 0], (grp_place * seq_count + seq_place) * own, own, 1
        )
        return (
            output,
            token_grad,
            gain_parts[0],
            qkv_terms[:, :width],
            qkv_terms[:, width],
            out_grad,
            gain_parts[1],
            mlp_sums[:, : mlp_weight.shape[0]].transpose(1, 0, 2),
        )
    segments = lax.dynamic_index_in_dim(shard_segment, grp_place, 0, keepdims=False)
    starts = shard_starts(segments, tok_rows, group_tok // 2)
    shard_order = jnp.arange(seq_count, dtype=jnp.int32)
    own_seg = jnp.sum(jnp.where(shard_order == seq_place, segments, 0))
    own_start = jnp.sum(jnp.where(shard_order == seq_place, starts, 0))
    positions = own_start + jnp.arange(tok_rows, dtype=jnp.int32)
    cosine_table, sine_table = rotary_tables(positions, HD)
    query_pos = jnp.tile(positions, heads_per)
    tokens_wide = tokens.astype(jnp.float32)
    gain_one = gain_attn.astype(jnp.float32)
    gain_two = gain_mlp.astype(jnp.float32)
    normed_one = rms_scale(tokens_wide, gain_one).astype(jnp.bfloat16)
    normed_one_all = lax.all_gather(normed_one, "seq", axis=0, tiled=True)
    qkv_rows = lax.all_gather(qkv_weight, "grp", axis=0, tiled=True)
    bias_rows = lax.all_gather(qkv_bias, "grp", axis=0, tiled=True)
    cotangent_all = lax.all_gather(cotangent, "seq", axis=0, tiled=True)
    out_full = lax.all_gather(out_weight, AXES, axis=0, tiled=True)
    projected = lax.dot_general(
        normed_one_all, qkv_rows, contract_last, preferred_element_type=jnp.float32
    )
    projected = (projected + bias_rows.astype(jnp.float32)[None, :]).astype(jnp.bfloat16)
    projected = owners_to_columns(projected, qkv_weight.shape[0]).astype(jnp.float32)
    query_rot = rotate(
        projected[:, :att_width].reshape(tok_rows, H, HD), cosine_table, sine_table
    ).astype(jnp.bfloat16)
    key_rot = rotate(
        projected[:, att_width : att_width + kv_width].reshape(tok_rows, KVH, HD),
        cosine_table,
        sine_table,
    ).astype(jnp.bfloat16)
    value_low = projected[:, att_width + kv_width :].astype(jnp.bfloat16)
    keys_all, values_all = (
        lax.all_gather(key_rot.reshape(tok_rows, kv_width), "seq", axis=0, tiled=True),
        lax.all_gather(value_low, "seq", axis=0, tiled=True),
    )
    queries = (
        query_rot.reshape(tok_rows, KVH, heads_per, HD)
        .transpose(1, 2, 0, 3)
        .reshape(KVH, query_rows, HD)
    )
    key_block = min(512, group_tok)
    block_count = group_tok // key_block
    block_order = jnp.arange(block_count, dtype=jnp.int32)

    def block_mask(block_index):
        key_index = block_index * key_block + jnp.arange(key_block, dtype=jnp.int32)
        key_shard = key_index // tok_rows
        onehot = key_shard[:, None] == shard_order[None, :]
        key_seg = jnp.sum(jnp.where(onehot, segments[None, :], 0), axis=1)
        key_pos = jnp.sum(jnp.where(onehot, starts[None, :], 0), axis=1) + key_index % tok_rows
        visible = (key_seg == 0) | (key_seg == own_seg)
        return visible[None, :] & (key_pos[None, :] <= query_pos[:, None])

    def block_keys(block_index):
        key_part = lax.dynamic_slice_in_dim(
            keys_all, block_index * key_block, key_block, 0
        ).reshape(key_block, KVH, HD)
        value_part = lax.dynamic_slice_in_dim(
            values_all, block_index * key_block, key_block, 0
        ).reshape(key_block, KVH, HD)
        return (key_part, value_part)

    def block_scores(key_part):
        return (
            jnp.einsum("krd,jkd->krj", queries, key_part, preferred_element_type=jnp.float32)
            * score_scale
        )

    def stat_step(stats_now, block_index):
        allowed = block_mask(block_index)

        def stat_visit(current):
            top_old, total_old = current
            key_part, value_part = block_keys(block_index)
            scores = jnp.where(allowed[None], block_scores(key_part), -1e30)
            top_new = jnp.maximum(top_old, jnp.max(scores, axis=-1))
            weights = jnp.where(allowed[None], jnp.exp(scores - top_new[..., None]), 0.0)
            return (top_new, total_old * jnp.exp(top_old - top_new) + jnp.sum(weights, axis=-1))

        return (lax.cond(jnp.any(allowed), stat_visit, lambda current: current, stats_now), None)

    start_stats = (
        jnp.full((KVH, query_rows), -1e30, jnp.float32),
        jnp.zeros((KVH, query_rows), jnp.float32),
    )
    (top_all, total_all), unused = lax.scan(stat_step, start_stats, block_order)
    log_total = top_all + jnp.log(total_all)

    def mix_step(mixed_sum, block_index):
        allowed = block_mask(block_index)

        def mix_visit(current):
            key_part, value_part = block_keys(block_index)
            prob_low = jnp.where(
                allowed[None], jnp.exp(block_scores(key_part) - log_total[..., None]), 0.0
            ).astype(jnp.bfloat16)
            return current + jnp.einsum(
                "krj,jkd->krd", prob_low, value_part, preferred_element_type=jnp.float32
            )

        return (lax.cond(jnp.any(allowed), mix_visit, lambda current: current, mixed_sum), None)

    mixed_sum, unused = lax.scan(
        mix_step, jnp.zeros((KVH, query_rows, HD), jnp.float32), block_order
    )
    attn_wide = (
        mixed_sum.reshape(KVH, heads_per, tok_rows, HD)
        .transpose(2, 0, 1, 3)
        .reshape(tok_rows, att_width)
    )
    attn_low = attn_wide.astype(jnp.bfloat16)
    attn_proj = jnp.dot(attn_low, out_full, preferred_element_type=jnp.float32)
    state = tokens_wide + attn_proj
    normed_two = rms_scale(state, gain_two).astype(jnp.bfloat16)
    grad_part, out_part, mlp_grad = plain_mlp(normed_two, cotangent_all, mlp_weight)
    output = (state + out_part).astype(jnp.bfloat16)
    unused_state, norm_two_back = jax.vjp(rms_scale, state, gain_two)
    state_norm_grad, gain_two_grad = norm_two_back(grad_part)
    state_grad = state_norm_grad + cotangent.astype(jnp.float32)
    state_low = state_grad.astype(jnp.bfloat16)
    attn_grad = lax.dot_general(
        state_low, out_full, contract_last, preferred_element_type=jnp.float32
    )
    attn_grad_low = attn_grad.astype(jnp.bfloat16)
    attn_owned = columns_to_owners(attn_low, out_weight.shape[0])
    state_low_all = lax.all_gather(state_low, "seq", axis=0, tiled=True)
    out_grad = lax.psum_scatter(
        lax.dot_general(
            attn_owned, state_low_all, contract_first, preferred_element_type=jnp.float32
        ),
        "grp",
        scatter_dimension=0,
        tiled=True,
    )
    grad_heads = (
        attn_grad_low.reshape(tok_rows, KVH, heads_per, HD)
        .transpose(1, 2, 0, 3)
        .reshape(KVH, query_rows, HD)
    )
    delta_rows = jnp.sum(
        (attn_grad_low.astype(jnp.float32) * attn_wide).reshape(tok_rows, H, HD), axis=-1
    )
    delta_rows = (
        delta_rows.reshape(tok_rows, KVH, heads_per).transpose(1, 2, 0).reshape(KVH, query_rows)
    )

    def back_step(query_grad, block_index):
        allowed = block_mask(block_index)

        def back_visit(current):
            key_part, value_part = block_keys(block_index)
            prob_vals = jnp.where(
                allowed[None], jnp.exp(block_scores(key_part) - log_total[..., None]), 0.0
            )
            prob_grad = jnp.einsum(
                "krd,jkd->krj", grad_heads, value_part, preferred_element_type=jnp.float32
            )
            score_grad = (prob_vals * (prob_grad - delta_rows[..., None])).astype(jnp.bfloat16)
            new_grad = (
                current
                + jnp.einsum(
                    "krj,jkd->krd", score_grad, key_part, preferred_element_type=jnp.float32
                )
                * score_scale
            )
            key_grad = (
                jnp.einsum("krj,krd->jkd", score_grad, queries, preferred_element_type=jnp.float32)
                * score_scale
            )
            value_grad = jnp.einsum(
                "krj,krd->jkd",
                prob_vals.astype(jnp.bfloat16),
                grad_heads,
                preferred_element_type=jnp.float32,
            )
            return (
                new_grad,
                (key_grad.reshape(key_block, kv_width), value_grad.reshape(key_block, kv_width)),
            )

        def skip_block(current):
            blank_rows = jnp.zeros((key_block, kv_width), jnp.float32)
            return (current, (blank_rows, blank_rows))

        return lax.cond(jnp.any(allowed), back_visit, skip_block, query_grad)

    query_grad, (key_grads, value_grads) = lax.scan(
        back_step, jnp.zeros((KVH, query_rows, HD), jnp.float32), block_order
    )
    key_own, value_own = (
        lax.psum_scatter(
            key_grads.reshape(group_tok, kv_width).astype(jnp.bfloat16),
            "seq",
            scatter_dimension=0,
            tiled=True,
        ).astype(jnp.float32),
        lax.psum_scatter(
            value_grads.reshape(group_tok, kv_width).astype(jnp.bfloat16),
            "seq",
            scatter_dimension=0,
            tiled=True,
        ).astype(jnp.float32),
    )
    query_back = unrotate(
        query_grad.reshape(KVH, heads_per, tok_rows, HD)
        .transpose(2, 0, 1, 3)
        .reshape(tok_rows, H, HD),
        cosine_table,
        sine_table,
    )
    key_back = unrotate(key_own.reshape(tok_rows, KVH, HD), cosine_table, sine_table)
    qkv_grad_low = jnp.concatenate(
        [query_back.reshape(tok_rows, att_width), key_back.reshape(tok_rows, kv_width), value_own],
        axis=1,
    ).astype(jnp.bfloat16)
    qkv_grad_owned = columns_to_owners(qkv_grad_low, qkv_weight.shape[0])
    bias_terms = jnp.sum(qkv_grad_owned.astype(jnp.float32), axis=0)
    normed_one_grad = lax.psum_scatter(
        jnp.dot(qkv_grad_owned, qkv_rows, preferred_element_type=jnp.float32).astype(jnp.bfloat16),
        "seq",
        scatter_dimension=0,
        tiled=True,
    ).astype(jnp.float32)
    qkv_grad = lax.psum_scatter(
        lax.dot_general(
            qkv_grad_owned, normed_one_all, contract_first, preferred_element_type=jnp.float32
        ),
        "grp",
        scatter_dimension=0,
        tiled=True,
    )
    unused_tokens, norm_one_back = jax.vjp(rms_scale, tokens_wide, gain_one)
    token_norm_grad, gain_one_grad = norm_one_back(normed_one_grad)
    token_grad = token_norm_grad + state_grad
    bias_part = lax.psum_scatter(bias_terms, "grp", scatter_dimension=0, tiled=True)
    gain_one_part, gain_two_part = (
        lax.psum_scatter(gain_one_grad, AXES, scatter_dimension=0, tiled=True),
        lax.psum_scatter(gain_two_grad, AXES, scatter_dimension=0, tiled=True),
    )
    return (
        output,
        token_grad,
        gain_one_part,
        qkv_grad,
        bias_part,
        out_grad,
        gain_two_part,
        mlp_grad,
    )


def solution(mesh):
    return jax.shard_map(
        per_device,
        mesh=mesh,
        in_specs=(
            P(("grp", "seq"), None),
            P(("grp", "seq"), None),
            P(),
            P(),
            P(("grp", "seq"), None),
            P(("grp", "seq")),
            P(("grp", "seq"), None),
            P(),
            P(("grp", "seq"), None, None),
        ),
        out_specs=(
            P(("grp", "seq"), None),
            P(("grp", "seq"), None),
            P(("grp", "seq")),
            P(("grp", "seq"), None),
            P(("grp", "seq")),
            P(("grp", "seq"), None),
            P(("grp", "seq")),
            P(("grp", "seq"), None, None),
        ),
        check_vma=False,
    )
```

```python
import functools
import math

import jax
import jax.numpy as jnp
from jax import lax
from jax.experimental import pallas as pl
from jax.experimental.pallas import tpu as pltpu
from jax.sharding import PartitionSpec as P

H = 12
KVH = 2
HD = 128
FF = 8960


EPS = 1e-06
THETA = 10000.0


def rms_scale(values, gain_vec):
    return values * lax.rsqrt(jnp.mean(values * values, axis=-1, keepdims=True) + EPS) * gain_vec


def rotary_tables(positions, head_dim):
    half_dim = head_dim // 2
    freqs = THETA ** (-(jnp.arange(half_dim, dtype=jnp.float32) * 2.0) / head_dim)
    angles = positions.astype(jnp.float32)[:, None] * freqs[None, :]
    cosine_table = jnp.concatenate([jnp.cos(angles), jnp.cos(angles)], axis=-1)
    sine_table = jnp.concatenate([jnp.sin(angles), jnp.sin(angles)], axis=-1)
    return (cosine_table, sine_table)


def rotate(values, cosine_table, sine_table):
    half_dim = values.shape[-1] // 2
    turned = jnp.concatenate([-values[..., half_dim:], values[..., :half_dim]], axis=-1)
    return values * cosine_table[:, None, :] + turned * sine_table[:, None, :]


def unrotate(grad_rows, cosine_table, sine_table):
    half_dim = grad_rows.shape[-1] // 2
    scaled = grad_rows * sine_table[:, None, :]
    turned = jnp.concatenate([scaled[..., half_dim:], -scaled[..., :half_dim]], axis=-1)
    return grad_rows * cosine_table[:, None, :] + turned


def shard_starts(segments, tok_dev, prompt_len):
    shard_total = segments.shape[0]
    shard_order = jnp.arange(shard_total, dtype=jnp.int32)
    same_seg = segments[:, None] == segments[None, :]
    first_shard = jnp.min(jnp.where(same_seg, shard_order[None, :], shard_total), axis=1)
    cont_start = prompt_len + (shard_order - first_shard) * tok_dev
    return jnp.where(segments == 0, shard_order * tok_dev, cont_start)


def swish_product(gate_vals, upper_vals):
    return jax.nn.silu(gate_vals) * upper_vals


AXES = ("grp", "seq")
CONTRACT_LAST = (((1,), (1,)), ((), ()))
CONTRACT_FIRST = (((0,), (0,)), ((), ()))


MESH = pl.DeviceIdType.MESH


def remote(src, dst, send_sem, recv_sem, grp, seq):
    return pltpu.make_async_remote_copy(
        src_ref=src, dst_ref=dst, send_sem=send_sem, recv_sem=recv_sem,
        device_id=(grp, seq), device_id_type=MESH,
    )


def nearest_chip(place, order, chips):
    both = 2 * jnp.minimum(place, chips - 1 - place)
    offset = (order + 1) // 2
    near = jnp.where(order % 2 == 1, place - offset, place + offset)
    rest = jnp.where(place < chips - 1 - place, order, chips - 1 - order)
    return jnp.where(order <= both, near, rest)


class Place:
    def __init__(self, chips):
        self.chips = chips
        self.grp, self.seq = lax.axis_index("grp"), lax.axis_index("seq")
        self.chip, self.core = self.seq // 2, self.seq % 2
        self.mate = self.seq + 1 - 2 * self.core

    def peer(self, offset):
        low, high = self.grp % 2, self.grp // 2
        low = 1 - low if offset % 2 else low
        high = 1 - high if offset // 2 else high
        return 2 * high + low

    def barrier(self, grps):
        barrier = pltpu.get_barrier_semaphore()
        for chip in range(self.chips):
            @pl.when(chip != self.chip)
            def _(chip=chip):
                pl.semaphore_signal(
                    barrier, inc=1, device_id=(self.grp, 2 * chip + self.core), device_id_type=MESH
                )
        pl.semaphore_signal(barrier, inc=1, device_id=(self.grp, self.mate), device_id_type=MESH)
        for offset in range(1, grps):
            pl.semaphore_signal(
                barrier, inc=1, device_id=(self.peer(offset), self.seq), device_id_type=MESH
            )
        pl.semaphore_wait(barrier, self.chips - 1 + 1 + grps - 1)


class RailGather:
    def __init__(self, place, view, send_sem, recv_sem):
        self.place, self.view, self.send_sem, self.recv_sem = place, view, send_sem, recv_sem

    def copy(self, way, chip, core):
        p = self.place
        to = (p.seq + 2, p.seq - 2, p.mate)[way]
        return remote(
            self.view(chip, core), self.view(chip, core), self.send_sem.at[way, chip],
            self.recv_sem.at[chip, core], p.grp, to,
        )

    def start(self):
        p = self.place
        pl.when(p.chip < p.chips - 1)(lambda: self.copy(0, p.chip, p.core).start())
        pl.when(p.chip > 0)(lambda: self.copy(1, p.chip, p.core).start())
        self.copy(2, p.chip, p.core).start()

    def forward(self, step):
        p = self.place

        @pl.when(p.chip - step >= 0)
        def _():
            chip = p.chip - step
            self.copy(2, chip, p.core).wait_recv()
            pl.when(p.chip < p.chips - 1)(lambda: self.copy(0, chip, p.core).start())
            self.copy(2, chip, p.core).start()

        @pl.when(p.chip + step < p.chips)
        def _():
            chip = p.chip + step
            self.copy(2, chip, p.core).wait_recv()
            pl.when(p.chip > 0)(lambda: self.copy(1, chip, p.core).start())
            self.copy(2, chip, p.core).start()

    def wait_mate(self, chip):
        self.copy(2, chip, 1 - self.place.core).wait_recv()

    def drain(self):
        p = self.place
        for chip in range(p.chips):
            self.copy(2, chip, p.core).wait_send()
            pl.when((chip <= p.chip) & (p.chip < p.chips - 1))(
                lambda chip=chip: self.copy(0, chip, p.core).wait_send()
            )
            pl.when((chip >= p.chip) & (p.chip > 0))(
                lambda chip=chip: self.copy(1, chip, p.core).wait_send()
            )


class LineScatter:
    def __init__(self, place, part, mate_in, left_in, right_in, send_sem, recv_sem):
        self.place, self.part = place, part
        self.mate_in, self.left_in, self.right_in = mate_in, left_in, right_in
        self.send_sem, self.recv_sem = send_sem, recv_sem

    def copy(self, way, src, landing, r, chip, to):
        return remote(
            src, landing.at[r, chip], self.send_sem.at[way, r, chip], self.recv_sem.at[way, r, chip],
            self.place.grp, to,
        )

    def to_mate(self, r, chip):
        p = self.place
        return self.copy(0, self.part.at[r, 2 * chip + 1 - p.core], self.mate_in, r, chip, p.mate)

    def to_right(self, r, chip):
        p = self.place
        return self.copy(1, self.part.at[r, 2 * chip + p.core], self.left_in, r, chip, p.seq + 2)

    def to_left(self, r, chip):
        p = self.place
        return self.copy(2, self.part.at[r, 2 * chip + p.core], self.right_in, r, chip, p.seq - 2)

    def step(self, r, chip):
        p = self.place
        last = p.chips - 1
        slot = 2 * chip + p.core

        @pl.when(chip != p.chip)
        def _():
            self.to_mate(r, chip).wait_recv()
            total = self.part[r, slot].astype(jnp.float32) + self.mate_in[r, chip].astype(jnp.float32)
            self.part[r, slot] = total.astype(jnp.bfloat16)

        @pl.when(chip > p.chip)
        def _():
            @pl.when(p.chip > 0)
            def _():
                self.to_right(r, chip).wait_recv()
                self.part[r, slot] = (
                    self.part[r, slot].astype(jnp.float32) + self.left_in[r, chip].astype(jnp.float32)
                ).astype(jnp.bfloat16)

            self.to_right(r, chip).start()

        @pl.when(chip < p.chip)
        def _():
            @pl.when(p.chip < last)
            def _():
                self.to_left(r, chip).wait_recv()
                self.part[r, slot] = (
                    self.part[r, slot].astype(jnp.float32) + self.right_in[r, chip].astype(jnp.float32)
                ).astype(jnp.bfloat16)

            self.to_left(r, chip).start()

    def finish(self, r, out_ref):
        p = self.place
        self.to_mate(r, p.chip).wait_recv()
        out_ref[...] = self.part[r, p.seq].astype(jnp.float32) + self.mate_in[r, p.chip].astype(jnp.float32)

        @pl.when(p.chip > 0)
        def _():
            self.to_right(r, p.chip).wait_recv()
            out_ref[...] += self.left_in[r, p.chip].astype(jnp.float32)

        @pl.when(p.chip < p.chips - 1)
        def _():
            self.to_left(r, p.chip).wait_recv()
            out_ref[...] += self.right_in[r, p.chip].astype(jnp.float32)

    def drain(self, r):
        p = self.place
        for other in range(p.chips):
            self.to_mate(r, other).wait_send()
            pl.when(other > p.chip)(lambda other=other: self.to_right(r, other).wait_send())
            pl.when(other < p.chip)(lambda other=other: self.to_left(r, other).wait_send())


def front_kernel(chips, scale,
                 tokens_ref, gain_one_ref, gain_two_ref, segment_ref, freq_ref, bias_ref,
                 cot_ref, wq_ref, wo_ref, wm_ref,
                 attn_ref, state_ref, cos_ref, sin_ref, mask_ref, q_out_ref, kv_out_ref, n1_all_ref, n2_all_ref,
                 cot_all_ref, wo_all_ref, wq_all_ref, columns_ref, wm1_ref, wm2_ref, wm3_ref,
                 nbuf, n2buf, wq, wo, bias_own, bias, stage, qbuf, kvbuf, columns,
                 lsem, n_send, n_recv, n2_send, n2_recv, c_send, c_recv, o_send, o_recv, ox_send, ox_recv,
                 om_send, om_recv, wq_send, wq_recv, b_send, b_recv, m_send, m_recv, q_send, q_recv, k_send, k_recv):
    p = Place(chips)
    grps = 4
    half = wq_ref.shape[0]
    rows = pl.ds(p.core * half, half)
    mates_rows = pl.ds((1 - p.core) * half, half)
    wm_refs = (wm_ref, wm1_ref, wm2_ref, wm3_ref)
    part = wm_ref.shape[1] // 2

    own = [
        pltpu.make_async_copy(wq_ref, wq.at[0, rows], lsem.at[0]),
        pltpu.make_async_copy(wo_ref, wo.at[p.grp, p.chip, p.core], lsem.at[2]),
        pltpu.make_async_copy(cot_ref, cot_all_ref.at[p.chip, p.core], lsem.at[3]),
    ]
    for copy in own:
        copy.start()
    tokens = tokens_ref[...].astype(jnp.float32)
    nbuf[p.chip, p.core] = rms_scale(tokens, gain_one_ref[...].astype(jnp.float32)).astype(jnp.bfloat16)
    shard = tokens.shape[0]
    lane = lax.broadcasted_iota(jnp.int32, (1, 2 * half), 1)
    bias_wide = bias_ref[...].astype(jnp.float32)
    bias_pair = jnp.concatenate([bias_wide, bias_wide], axis=1)
    bias_own[...] = jnp.broadcast_to(jnp.where(lane // half == p.core, bias_pair, 0.0), bias_own.shape)
    bias[0, p.core] = bias_own[...]
    p.barrier(grps)

    n1_line = RailGather(p, lambda chip, core: nbuf.at[chip, core], n_send, n_recv)
    cot_line = RailGather(p, lambda chip, core: cot_all_ref.at[chip, core], c_send, c_recv)
    n2_line = RailGather(p, lambda chip, core: n2buf.at[chip, core], n2_send, n2_recv)
    out_line = RailGather(p, lambda chip, core: wo.at[p.grp, chip, core], o_send, o_recv)

    def wq_direct(b):
        return remote(wq_ref, wq.at[b, rows], wq_send.at[0, b], wq_recv.at[b, 0], p.peer(b), p.seq)

    def wq_mate(b):
        return remote(wq.at[b, rows], wq.at[b, rows], wq_send.at[1, b], wq_recv.at[b, 1], p.grp, p.mate)

    def bias_direct(b):
        return remote(bias_own, bias.at[b, p.core], b_send.at[0, b], b_recv.at[b, 0], p.peer(b), p.seq)

    def bias_mate(b):
        return remote(bias.at[b, p.core], bias.at[b, p.core], b_send.at[1, b], b_recv.at[b, 1], p.grp, p.mate)

    def m_part(ref, i, j):
        return ref.at[j, pl.ds(i * part, part)]

    def m_direct(b, i, j):
        return remote(
            m_part(wm_ref, i, j), m_part(wm_refs[b], i, j), m_send.at[b, i, j], m_recv.at[b, i, j],
            p.peer(b), p.seq,
        )

    def m_forward(b, j):
        return remote(
            m_part(wm_refs[b], b - 1, j), m_part(wm3_ref, b - 1, j), m_send.at[3, b - 1, j],
            m_recv.at[3, b - 1, j], p.peer(3 - b), p.seq,
        )

    def out_cross(b, chip):
        view = wo.at[p.grp, chip, p.core]
        return remote(view, view, ox_send.at[b, chip], ox_recv.at[b, chip], p.peer(b), p.seq)

    def out_arrival(b, chip):
        view = wo.at[p.peer(b), chip, p.core]
        return remote(view, view, ox_send.at[b, chip], ox_recv.at[b, chip], p.grp, p.mate)

    def out_mate(b, core):
        view = wo.at[p.peer(b), :, core]
        return remote(view, view, om_send.at[b], om_recv.at[b], p.grp, p.mate)

    def q_copy(chip):
        return remote(
            stage.at[chip, pl.ds(0, 3)], qbuf.at[p.chip], q_send.at[chip], q_recv.at[p.chip],
            p.grp, 2 * chip + p.core,
        )

    def q_arrival(chip):
        return remote(stage.at[chip, pl.ds(0, 3)], qbuf.at[chip], q_send.at[chip], q_recv.at[chip], p.grp, p.mate)

    def k_copy(chip, to_chip):
        return remote(
            stage.at[chip, 3], kvbuf.at[p.chip, p.core, chip], k_send.at[0, chip, to_chip],
            k_recv.at[p.chip, p.core, chip], p.grp, 2 * to_chip + p.core,
        )

    def k_mate(head, chip, src=None):
        view = kvbuf.at[head, p.core, chip]
        return remote(
            view if src is None else src, view, k_send.at[1, head, chip],
            k_recv.at[head, p.core, chip], p.grp, p.mate,
        )

    def k_arrival(head, core, chip):
        view = kvbuf.at[head, core, chip]
        return remote(view, view, k_send.at[1, head, chip], k_recv.at[head, core, chip], p.grp, p.mate)

    def make_tables():
        segs = [segment_ref[p.grp, t] for t in range(2 * chips)]
        starts = []
        for t in range(2 * chips):
            first = jnp.int32(t)
            for other in reversed(range(t)):
                first = jnp.where(segs[other] == segs[t], jnp.int32(other), first)
            starts.append(
                jnp.where(segs[t] == 0, jnp.int32(t * shard), chips * shard + (t - first) * shard)
            )

        def own_of(values):
            own = values[0]
            for t in range(1, 2 * chips):
                own = jnp.where(p.seq == t, values[t], own)
            return own

        own_seg, own_start = own_of(segs), own_of(starts)
        row = lax.broadcasted_iota(jnp.int32, (shard, 2 * half), 0)
        column = lax.broadcasted_iota(jnp.int32, (shard, 2 * half), 1)
        freq = freq_ref[...]
        sign = jnp.where(column < half, -1.0, 1.0)
        for chip in range(chips):
            start = jnp.where(p.core == 0, starts[2 * chip], starts[2 * chip + 1])
            angle = (start + row).astype(jnp.float32) * freq
            cos_ref[chip] = jnp.cos(angle)
            sin_ref[chip] = jnp.sin(angle) * sign
        for core in range(2):
            for chip in range(chips):
                t = 2 * chip + core
                seen = jnp.where((segs[t] == 0) | (segs[t] == own_seg), jnp.int32(1), jnp.int32(0))
                allowed = (starts[t] + column <= own_start + row) & (row * 0 + seen > 0)
                block = core * chips + chip
                mask_ref[:, block * shard : (block + 1) * shard] = jnp.where(allowed, 0.0, -1e30)

    own[0].wait()
    for b in range(1, grps):
        wq_direct(b).start()
        bias_direct(b).start()
    wq_mate(0).start()
    bias_mate(0).start()
    n1_line.start()
    own[1].wait()
    out_line.start()
    for b in range(1, grps):
        wq_direct(b).wait_recv()
        wq_mate(b).start()
        bias_direct(b).wait_recv()
        bias_mate(b).start()
    for b in range(1, grps):
        out_cross(b, p.chip).start()
    for j in range(3):
        m_direct(1, 0, j).start()
        m_direct(2, 1, j).start()
    make_tables()
    for b in range(grps):
        wq_mate(b).wait_recv()
        bias_mate(b).wait_recv()

    @pl.loop(0, chips)
    def _(order):
        @pl.when(order > 0)
        def _():
            n1_line.forward(order)
            out_line.forward(order)
            for b in range(1, grps):
                pl.when(p.chip - order >= 0)(lambda b=b: out_cross(b, p.chip - order).start())
                pl.when(p.chip + order < chips)(lambda b=b: out_cross(b, p.chip + order).start())

        at = nearest_chip(p.chip, order, chips)
        x = nbuf[at, p.core]
        weights = wq[...].reshape(grps * 2 * half, x.shape[1])
        rows_all = lax.dot_general(x, weights, CONTRACT_LAST, preferred_element_type=jnp.float32)
        cosine, sine = cos_ref[at], sin_ref[at]
        for b in range(grps):
            u = rows_all[:, 2 * half * b : 2 * half * (b + 1)] + (bias[b, 0, 0:1] + bias[b, 1, 0:1])
            turned = u * cosine + pltpu.roll(u, half, 1) * sine
            place = p.peer(b)
            keep = jnp.where((place == grps - 1) & (p.chip >= chips // 2), 1.0, 0.0)
            value = (u * keep + turned * (1.0 - keep)).astype(jnp.bfloat16)
            stage[at, place] = value

            @pl.when(place == grps - 1)
            def _(value=value):
                kvbuf[p.chip, p.core, at] = value

            @pl.when((place < grps - 1) & (at == p.chip))
            def _(value=value, place=place):
                qbuf[p.chip, place] = value

        pl.when(at != p.chip)(lambda: q_copy(at).start())
        for to_chip in range(chips):
            pl.when(to_chip != p.chip)(lambda to_chip=to_chip: k_copy(at, to_chip).start())
        k_mate(p.chip, at, stage.at[at, 3]).start()

    own[2].wait()
    cot_line.start()

    @pl.loop(0, chips)
    def _(order):
        for head in range(chips):
            @pl.when(head != p.chip)
            def _(head=head):
                chip = nearest_chip(head, order, chips)
                k_arrival(head, p.core, chip).wait_recv()
                k_mate(head, chip).start()

    for chip in range(chips):
        pl.when(chip != p.chip)(lambda chip=chip: q_arrival(chip).wait_recv())
        for head in range(chips):
            k_arrival(head, 1 - p.core, chip).wait_recv()
    cot_line.forward(1)
    for j in (0, 1):
        for b in (1, 2):
            m_direct(b, b - 1, j).wait_recv()
            m_forward(b, j).start()
    for j in range(3):
        m_direct(1, 1, j).start()
        m_direct(2, 0, j).start()

    mask = mask_ref[...]
    heads_per = H // KVH
    for kv in range(KVH):
        heads = [kv * heads_per + i for i in range(heads_per)]
        queries = jnp.concatenate([qbuf[h % chips, h // chips] for h in heads], axis=0)
        keys = kvbuf[kv].reshape(mask.shape[1], 2 * half)
        values = kvbuf[KVH + kv].reshape(mask.shape[1], 2 * half)
        scores = lax.dot_general(queries, keys, CONTRACT_LAST, preferred_element_type=jnp.float32) * scale
        scores = scores.reshape(heads_per, shard, mask.shape[1]) + mask[None]
        weights = jnp.exp(scores - jnp.max(scores, axis=-1, keepdims=True))
        inverse = 1.0 / jnp.sum(weights, axis=-1, keepdims=True)
        probs = (weights * inverse).astype(jnp.bfloat16).reshape(heads_per * shard, mask.shape[1])
        mixed = jnp.dot(probs, values, preferred_element_type=jnp.float32)
        for i, h in enumerate(heads):
            attn_ref[:, h * 2 * half : (h + 1) * 2 * half] = mixed[i * shard : (i + 1) * shard]
        cot_line.forward(kv + 2)

    for b in range(1, grps):
        for chip in range(chips):
            out_arrival(b, chip).wait_recv()
        out_mate(b, p.core).start()
    for b in (1, 2):
        m_direct(b, b - 1, 2).wait_recv()
        m_forward(b, 2).start()
    attn_low = attn_ref[...].astype(jnp.bfloat16)
    unit = wo.shape[3]
    columns[...] = attn_low.T.reshape(columns.shape)
    for b in range(1, grps):
        out_mate(b, 1 - p.core).wait_recv()
    for chip in range(chips):
        out_line.wait_mate(chip)
    state = tokens_ref[...].astype(jnp.float32) + jnp.dot(
        attn_low, wo[...].reshape(grps * chips * 2 * unit, tokens_ref.shape[1]),
        preferred_element_type=jnp.float32,
    )
    state_ref[...] = state
    n2buf[p.chip, p.core] = rms_scale(state, gain_two_ref[...].astype(jnp.float32)).astype(jnp.bfloat16)
    n2_line.start()
    outs = [
        pltpu.make_async_copy(nbuf, n1_all_ref, lsem.at[4]),
        pltpu.make_async_copy(wq, wq_all_ref, lsem.at[5]),
        pltpu.make_async_copy(qbuf, q_out_ref, lsem.at[6]),
        pltpu.make_async_copy(kvbuf, kv_out_ref, lsem.at[7]),
        pltpu.make_async_copy(wo, wo_all_ref, lsem.at[8]),
        pltpu.make_async_copy(columns, columns_ref, lsem.at[9]),
    ]
    for chip in range(chips):
        n1_line.wait_mate(chip)
    for copy in outs:
        copy.start()
    for step in range(1, chips):
        n2_line.forward(step)
    for chip in range(chips):
        cot_line.wait_mate(chip)
        n2_line.wait_mate(chip)
    last = pltpu.make_async_copy(n2buf, n2_all_ref, lsem.at[10])
    last.start()
    for b in (1, 2):
        for j in range(3):
            m_direct(b, 2 - b, j).wait_recv()
            m_forward(3 - b, j).wait_recv()
    for copy in outs:
        copy.wait()
    last.wait()
    n1_line.drain()
    n2_line.drain()
    out_line.drain()
    cot_line.drain()
    for b in range(grps):
        wq_mate(b).wait_send()
        bias_mate(b).wait_send()
    for b in range(1, grps):
        wq_direct(b).wait_send()
        bias_direct(b).wait_send()
        out_mate(b, p.core).wait_send()
        for chip in range(chips):
            out_cross(b, chip).wait_send()
    for b in (1, 2):
        for i in (0, 1):
            for j in range(3):
                m_direct(b, i, j).wait_send()
        for j in range(3):
            m_forward(b, j).wait_send()
    for chip in range(chips):
        pl.when(chip != p.chip)(lambda chip=chip: q_copy(chip).wait_send())
        for other in range(chips):
            pl.when(other != p.chip)(lambda chip=chip, other=other: k_copy(chip, other).wait_send())
            k_mate(other, chip).wait_send()


def front_call(tokens, gain_one, gain_two, segments, freqs, bias, cot, qkv_weight, out_weight, mlp_rows):
    chips = segments.shape[1] // 2
    grps = 4
    shard, width = tokens.shape
    half = qkv_weight.shape[0]
    vm, dma = pltpu.VMEM, pltpu.SemaphoreType.DMA
    anyspace = pl.BlockSpec(memory_space=pl.ANY)
    vspec = pl.BlockSpec(memory_space=pltpu.VMEM)
    low, wide = jnp.bfloat16, jnp.float32
    struct = jax.ShapeDtypeStruct
    wo_shape = (grps, chips, 2) + out_weight.shape
    columns_shape = (grps, 2 * chips, out_weight.shape[0], shard)
    return pl.pallas_call(
        functools.partial(front_kernel, chips, 1.0 / math.sqrt(HD)),
        out_shape=(
            struct((shard, H * HD), wide),
            struct((shard, width), wide),
            struct((chips, shard, HD), wide),
            struct((chips, shard, HD), wide),
            struct((shard, 2 * chips * shard), wide),
            struct((chips, 3, shard, HD), low),
            struct((chips, 2, chips, shard, HD), low),
            struct((chips, 2, shard, width), low),
            struct((chips, 2, shard, width), low),
            struct((chips, 2, shard, width), low),
            struct(wo_shape, low),
            struct((grps, 2 * half, width), low),
            struct(columns_shape, low),
        ) + (struct(mlp_rows.shape, low),) * 3,
        in_specs=[vspec] * 3
        + [pl.BlockSpec(memory_space=pltpu.SMEM)]
        + [vspec] * 2
        + [anyspace] * 4,
        out_specs=(vspec,) * 5 + (anyspace,) * 11,
        scratch_shapes=[
            vm((chips, 2, shard, width), low),
            vm((chips, 2, shard, width), low),
            vm((grps, 2 * half, width), low),
            vm(wo_shape, low),
            vm((8, HD), wide),
            vm((grps, 2, 8, HD), wide),
            vm((chips, grps, shard, HD), low),
            vm((chips, 3, shard, HD), low),
            vm((chips, 2, chips, shard, HD), low),
            vm(columns_shape, low),
            dma((11,)),
            dma((3, chips)), dma((chips, 2)),
            dma((3, chips)), dma((chips, 2)),
            dma((3, chips)), dma((chips, 2)),
            dma((3, chips)), dma((chips, 2)),
            dma((grps, chips)), dma((grps, chips)), dma((grps,)), dma((grps,)),
            dma((2, grps)), dma((grps, 2)),
            dma((2, grps)), dma((grps, 2)),
            dma((grps, 2, 3)), dma((grps, 2, 3)),
            dma((chips,)), dma((chips,)),
            dma((2, chips, chips)), dma((chips, 2, chips)),
        ],
        compiler_params=pltpu.CompilerParams(
            collective_id=2, has_side_effects=True, vmem_limit_bytes=60 * 2**20
        ),
        name="front",
    )(tokens, gain_one, gain_two, segments, freqs, bias, cot, qkv_weight, out_weight, mlp_rows)


def mlp_kernel(chips, grps, row_tiles, n2_ref, cot_ref, columns_ref, *refs):
    w_refs, refs = refs[:grps], refs[grps:]
    (
        n2g_ref, outp_ref, grads_ref, owned_ref, tok, w, acts, part, mate_in, left_in, right_in, stage, owned,
        lsem, ssend, srecv, wsem, osem, a_send, a_recv,
    ) = refs
    p = Place(chips)
    slots = 2 * chips
    shard, width = n2_ref.shape[1:]
    units = w.shape[1]
    block = units // grps
    tile = units // row_tiles
    loads = [
        pltpu.make_async_copy(n2_ref, tok.at[0], lsem.at[0]),
        pltpu.make_async_copy(cot_ref, tok.at[1], lsem.at[1]),
        pltpu.make_async_copy(columns_ref.at[:, p.seq], owned.at[:, :, pl.ds(pl.multiple_of(p.seq * shard, shard), shard)], lsem.at[2]),
    ]
    for copy in loads:
        copy.start()

    def w_copy(j, b):
        return pltpu.make_async_copy(w_refs[b].at[j], w.at[j, pl.ds(b * block, block)], wsem.at[j, b])

    for j in range(3):
        for b in range(grps):
            w_copy(j, b).start()

    def seq_peer(i):
        return (p.seq + i) % slots

    barrier = pltpu.get_barrier_semaphore()
    for i in range(1, slots):
        pl.semaphore_signal(barrier, inc=1, device_id=(p.grp, seq_peer(i)), device_id_type=MESH)
    pl.semaphore_wait(barrier, slots - 1)
    scatter = LineScatter(p, part, mate_in, left_in, right_in, ssend, srecv)

    def a_copy(i, to, slot):
        return remote(
            columns_ref.at[:, to], owned.at[:, :, pl.ds(pl.multiple_of(slot * shard, shard), shard)],
            a_send.at[i], a_recv.at[slot], p.grp, to,
        )

    for i in range(1, slots):
        a_copy(i, seq_peer(i), p.seq).start()
    for copy in loads:
        copy.wait()
    for j in range(3):
        for b in range(grps):
            w_copy(j, b).wait()

    @pl.loop(0, chips + 1)
    def _(order):
        @pl.when(order < chips)
        def _():
            at = nearest_chip(p.chip, chips - 1 - order, chips)
            x = tok[0, pl.ds(2 * at, 2)].reshape(2 * shard, width)
            y = tok[1, pl.ds(2 * at, 2)].reshape(2 * shard, width)
            gate = lax.dot_general(x, w[0], CONTRACT_LAST, preferred_element_type=jnp.float32)
            up = lax.dot_general(x, w[1], CONTRACT_LAST, preferred_element_type=jnp.float32)
            unit_grad = lax.dot_general(y, w[2], CONTRACT_LAST, preferred_element_type=jnp.float32)
            sig = 1.0 / (1.0 + jnp.exp(-gate))
            silu = gate * sig
            rows = pl.ds(at * (2 * shard), 2 * shard)
            gate_grad = (unit_grad * up * sig * (1.0 + gate * (1.0 - sig))).astype(jnp.bfloat16)
            up_grad = (unit_grad * silu).astype(jnp.bfloat16)
            acts[0, rows] = gate_grad
            acts[1, rows] = up_grad
            acts[2, rows] = (silu * up).astype(jnp.bfloat16)
            back = jnp.dot(gate_grad, w[0], preferred_element_type=jnp.float32) + jnp.dot(
                up_grad, w[1], preferred_element_type=jnp.float32
            )
            part[0, pl.ds(2 * at, 2)] = back.astype(jnp.bfloat16).reshape(2, shard, width)
            scatter.to_mate(0, at).start()

        pl.when(order > 0)(lambda: scatter.step(0, nearest_chip(p.chip, chips - order, chips)))

    def out_copy(t):
        return pltpu.make_async_copy(
            stage.at[t % 2],
            grads_ref.at[t // row_tiles, pl.ds((t % row_tiles) * tile, tile)],
            osem.at[t % 2],
        )

    @pl.loop(0, 3 * row_tiles)
    def _(t):
        @pl.when(t < chips)
        def _():
            at = nearest_chip(p.chip, chips - 1 - t, chips)
            h = acts[2, pl.ds(at * (2 * shard), 2 * shard)]
            part[1, pl.ds(2 * at, 2)] = (
                jnp.dot(h, w[2], preferred_element_type=jnp.float32)
                .astype(jnp.bfloat16).reshape(2, shard, width)
            )
            scatter.to_mate(1, at).start()

        @pl.when((t > 0) & (t <= chips))
        def _():
            scatter.step(1, nearest_chip(p.chip, chips - t, chips))

        @pl.when(t >= 2)
        def _():
            out_copy(t - 2).wait()

        kind = t // row_tiles
        lhs = acts[kind, :, pl.ds(pl.multiple_of((t % row_tiles) * tile, 128), tile)]
        rhs = tok[kind // 2].reshape(2 * chips * shard, width)
        stage[t % 2] = lax.dot_general(
            lhs, rhs, CONTRACT_FIRST, preferred_element_type=jnp.float32
        ).astype(jnp.bfloat16)
        out_copy(t).start()

    scatter.finish(0, n2g_ref)
    for i in range(1, slots):
        a_copy(i, seq_peer(i), seq_peer(i)).wait_recv()
    moved = pltpu.make_async_copy(owned, owned_ref, lsem.at[0])
    moved.start()
    scatter.finish(1, outp_ref)
    out_copy(3 * row_tiles - 2).wait()
    out_copy(3 * row_tiles - 1).wait()
    moved.wait()
    scatter.drain(0)
    scatter.drain(1)
    for i in range(1, slots):
        a_copy(i, seq_peer(i), p.seq).wait_send()


def mlp_call(n2_all, cot_all, columns, w_blocks, row_tiles=3):
    grps, (_, block, width) = len(w_blocks), w_blocks[0].shape
    slots, shard, _ = cot_all.shape
    chips = slots // 2
    units = grps * block
    vm, anyspace = pltpu.VMEM, pl.BlockSpec(memory_space=pl.ANY)
    vspec = pl.BlockSpec(memory_space=pltpu.VMEM)
    dma = pltpu.SemaphoreType.DMA
    owned_shape = columns.shape[:1] + columns.shape[2:3] + (slots * shard,)
    return pl.pallas_call(
        functools.partial(mlp_kernel, chips, grps, row_tiles),
        out_shape=(
            jax.ShapeDtypeStruct((shard, width), jnp.float32),
            jax.ShapeDtypeStruct((shard, width), jnp.float32),
            jax.ShapeDtypeStruct((3, units, width), jnp.bfloat16),
            jax.ShapeDtypeStruct(owned_shape, jnp.bfloat16),
        ),
        in_specs=[anyspace] * (3 + grps),
        out_specs=(vspec, vspec, anyspace, anyspace),
        scratch_shapes=[
            vm((2, slots, shard, width), jnp.bfloat16),
            vm((3, units, width), jnp.bfloat16),
            vm((3, slots * shard, units), jnp.bfloat16),
            vm((2, slots, shard, width), jnp.bfloat16),
            vm((2, chips, shard, width), jnp.bfloat16),
            vm((2, chips, shard, width), jnp.bfloat16),
            vm((2, chips, shard, width), jnp.bfloat16),
            vm((2, units // row_tiles, width), jnp.bfloat16),
            vm(owned_shape, jnp.bfloat16),
            dma((3,)), dma((3, 2, chips)), dma((3, 2, chips)),
            dma((3, grps)), dma((2,)), dma((slots,)), dma((slots,)),
        ],
        compiler_params=pltpu.CompilerParams(
            collective_id=1, has_side_effects=True, vmem_limit_bytes=62 * 2**20
        ),
        name="mlp",
    )(n2_all, cot_all, columns, *w_blocks)


def unturn(rows, cosine, sine, half):
    return rows * cosine + pltpu.roll(rows * sine, half, 1)


def back_kernel(chips, scale,
                n2g_ref, state_ref, cot_ref, tokens_ref, gain_one_ref, gain_two_ref, attn_ref, q_ref, kv_ref,
                mask_ref, cos_ref, sin_ref, wq_ref, wo_ref, n1_ref, terms_ref, owned_ref,
                tok_grad_ref, wq_grad_ref, wo_grad_ref, gain_ref, mlp_ref,
                wo, stbuf, n1x, at_all, dq_stage, gq_in, kv_part, km_in, k_sum, k_own, kr_in,
                cols, part, left_in, right_in, wgrad, wm_in, w_send_buf, w_in, o_terms, o_send_buf, o_in,
                m_own, m_in, gain_own, gain_in, gain_mid, gain_mid_in, state_grad,
                lsem, s_send, s_recv, q_send, q_recv, km_send, km_recv, kr_send, kr_recv,
                r_send, r_recv, wm_send, wm_recv, w_send, w_recv, o_send, o_recv, m_send, m_recv,
                ml_sem, g_send, g_recv, h_send, h_recv):
    p = Place(chips)
    grps = 4
    shard, width = n2g_ref.shape
    slots = 2 * chips
    heads_per = H // KVH
    half = HD // 2
    low, wide = jnp.bfloat16, jnp.float32
    block = terms_ref.shape[1] // grps
    mhalf = block // 2
    last = chips - 1

    loads = [
        pltpu.make_async_copy(wo_ref, wo, lsem.at[0]),
        pltpu.make_async_copy(n1_ref.at[:, p.core], n1x.at[:, :, pl.ds(0, width)], lsem.at[1]),
        pltpu.make_async_copy(owned_ref, at_all, lsem.at[2]),
    ]
    for copy in loads:
        copy.start()

    def seq_peer(i):
        return (p.seq + i) % slots

    barrier = pltpu.get_barrier_semaphore()
    for i in range(1, slots):
        pl.semaphore_signal(barrier, inc=1, device_id=(p.grp, seq_peer(i)), device_id_type=MESH)
    for b in range(1, grps):
        pl.semaphore_signal(barrier, inc=1, device_id=(p.peer(b), p.seq), device_id_type=MESH)
    pl.semaphore_wait(barrier, slots - 1 + grps - 1)

    def m_rows(b, i):
        return terms_ref.at[:, pl.ds(b * block + i * mhalf, mhalf)]

    def m_copy(slot, src, peer):
        return remote(src, m_in.at[slot], m_send.at[slot], m_recv.at[slot], p.peer(peer), p.seq)

    m_first = [
        m_copy(1, m_rows(3, 0), 1), m_copy(3, m_rows(3, 1), 2),
        m_copy(0, m_rows(1, 0), 1), m_copy(2, m_rows(2, 1), 2),
    ]
    for copy in m_first:
        copy.start()
    m_second = [m_copy(4, m_own.at[0], 1), m_copy(5, m_own.at[1], 2)]
    m_loads = [
        pltpu.make_async_copy(m_rows(1, 1), m_own.at[0], ml_sem.at[0]),
        pltpu.make_async_copy(m_rows(2, 0), m_own.at[1], ml_sem.at[1]),
        pltpu.make_async_copy(m_rows(0, 0), m_own.at[2], ml_sem.at[2]),
        pltpu.make_async_copy(m_rows(0, 1), m_own.at[3], ml_sem.at[3]),
    ]
    for copy in m_loads:
        copy.start()

    state = state_ref[...]
    gain_two = gain_two_ref[...].astype(wide)
    n2g = n2g_ref[...]
    scale_two = lax.rsqrt(jnp.mean(state * state, axis=-1, keepdims=True) + EPS)
    normed = state * scale_two
    gain_own[1] = jnp.sum(n2g * normed, axis=0, keepdims=True)
    lifted = n2g * gain_two
    state_grad[...] = cot_ref[...].astype(wide) + scale_two * (
        lifted - normed * jnp.mean(lifted * normed, axis=-1, keepdims=True)
    )
    state_low = state_grad[...].astype(low)
    stbuf[p.chip, p.core] = state_low
    line = RailGather(p, lambda chip, core: stbuf.at[chip, core], s_send, s_recv)
    line.start()

    attn = attn_ref[...]
    unit = wo.shape[0] // (grps * slots)
    loads[0].wait()
    attn_grad = lax.dot_general(state_low, wo[...], CONTRACT_LAST, preferred_element_type=wide).astype(low)
    mask = mask_ref[...]
    keys_total = mask.shape[1]
    own_cos, own_sin = cos_ref[p.chip], sin_ref[p.chip]

    def km_copy(head):
        return remote(
            kv_part.at[head, 1 - p.core], km_in.at[head], km_send.at[head], km_recv.at[head], p.grp, p.mate
        )

    def kr_copy(head):
        return remote(
            k_sum.at[head], kr_in.at[p.chip], kr_send.at[head], kr_recv.at[p.chip], p.grp, 2 * head + p.core
        )

    def kr_arrival(chip):
        return remote(k_sum.at[chip], kr_in.at[chip], kr_send.at[chip], kr_recv.at[chip], p.grp, p.mate)

    def q_copy(chip):
        return remote(
            dq_stage.at[chip], gq_in.at[p.chip], q_send.at[chip], q_recv.at[p.chip], p.grp, 2 * chip + p.core
        )

    def q_arrival(chip):
        return remote(dq_stage.at[chip], gq_in.at[chip], q_send.at[chip], q_recv.at[chip], p.grp, p.mate)

    def key_sum(head):
        km_copy(head).wait_recv()
        total = kv_part[head, p.core].astype(wide) + km_in[head].astype(wide)

        @pl.when(p.chip == head)
        def _():
            k_own[...] = total

        @pl.when(p.chip != head)
        def _():
            k_sum[head] = total.astype(low)
            kr_copy(head).start()

    for kv in range(KVH):
        heads = [kv * heads_per + i for i in range(heads_per)]
        queries = jnp.concatenate([q_ref[h % chips, h // chips] for h in heads], axis=0)
        grads = jnp.concatenate([attn_grad[:, h * HD : (h + 1) * HD] for h in heads], axis=0)
        mixed = jnp.concatenate([attn[:, h * HD : (h + 1) * HD] for h in heads], axis=0)
        delta = jnp.sum(grads.astype(wide) * mixed, axis=-1, keepdims=True)
        keys = kv_ref[kv].reshape(keys_total, HD)
        values = kv_ref[KVH + kv].reshape(keys_total, HD)
        scores = lax.dot_general(queries, keys, CONTRACT_LAST, preferred_element_type=wide) * scale
        scores = (scores.reshape(heads_per, shard, keys_total) + mask[None]).reshape(heads_per * shard, keys_total)
        weights = jnp.exp(scores - jnp.max(scores, axis=-1, keepdims=True))
        probs = weights * (1.0 / jnp.sum(weights, axis=-1, keepdims=True))
        prob_grad = lax.dot_general(grads, values, CONTRACT_LAST, preferred_element_type=wide)
        score_grad = (probs * (prob_grad - delta)).astype(low)
        key_grad = lax.dot_general(score_grad, queries, CONTRACT_FIRST, preferred_element_type=wide) * scale
        value_grad = lax.dot_general(probs.astype(low), grads, CONTRACT_FIRST, preferred_element_type=wide)
        kv_part[kv] = key_grad.astype(low).reshape(2, chips, shard, HD)
        kv_part[KVH + kv] = value_grad.astype(low).reshape(2, chips, shard, HD)
        km_copy(kv).start()
        km_copy(KVH + kv).start()
        query_grad = jnp.dot(score_grad, keys, preferred_element_type=wide) * scale
        for i, h in enumerate(heads):
            turned = unturn(query_grad[i * shard : (i + 1) * shard], own_cos, own_sin, half).astype(low)
            dq_stage[h % chips, h // chips] = turned

            @pl.when(p.chip == h % chips)
            def _(turned=turned, h=h):
                gq_in[h % chips, h // chips] = turned

        line.forward(1 + kv)
    for chip in range(chips):
        pl.when(chip != p.chip)(lambda chip=chip: q_copy(chip).start())
    for head in (0, 2, 1, 3):
        key_sum(head)
    def m_add(dst, src):
        for j in range(3):
            @pl.loop(0, mhalf // 16)
            def _(t, j=j):
                rows = pl.ds(pl.multiple_of(t * 16, 16), 16)
                m_own[dst, j, rows] = (
                    m_own[dst, j, rows].astype(wide) + m_in[src, j, rows].astype(wide)
                ).astype(low)

    m_loads[0].wait()
    m_first[1].wait_recv()
    m_add(0, 3)
    m_second[0].start()
    m_loads[1].wait()
    m_first[0].wait_recv()
    m_add(1, 1)
    m_second[1].start()
    line.forward(3)
    loads[1].wait()
    lane = lax.broadcasted_iota(jnp.int32, (chips, shard, HD), 2)
    n1x[:, :, width:] = jnp.where(lane == 0, 1.0, 0.0).astype(low)
    for chip in range(chips):
        line.wait_mate(chip)
    loads[2].wait()
    o_terms[...] = jnp.dot(
        at_all[...].reshape(grps * unit, slots * shard), stbuf[...].reshape(slots * shard, width),
        preferred_element_type=wide,
    ).reshape(grps, unit, width)
    o_send_buf[...] = o_terms[...].astype(low)

    def o_copy(b):
        return remote(
            o_send_buf.at[p.peer(b)], o_in.at[b], o_send.at[b], o_recv.at[b], p.peer(b), p.seq
        )

    for b in range(1, grps):
        o_copy(b).start()

    for chip in range(chips):
        pl.when(chip != p.chip)(lambda chip=chip: q_arrival(chip).wait_recv())
        pl.when(chip != p.chip)(lambda chip=chip: kr_arrival(chip).wait_recv())
    is_value = jnp.where(p.chip >= chips // 2, 1.0, 0.0)

    @pl.loop(0, chips)
    def _(order):
        chip = nearest_chip(p.chip, last - order, chips)
        key_total = k_own[chip]
        for other in range(chips):
            key_total = key_total + jnp.where(other == p.chip, 0.0, kr_in[other, chip].astype(wide))
        turned = unturn(key_total, cos_ref[chip], sin_ref[chip], half)
        last_head = (key_total * is_value + turned * (1.0 - is_value)).astype(low)
        for b in range(grps):
            place = p.peer(b)
            query_head = gq_in[chip, jnp.minimum(place, grps - 2)]
            cols[chip, :, b * HD : (b + 1) * HD] = jnp.where(place == grps - 1, last_head, query_head)
        part[chip] = jnp.dot(
            cols[chip], wq_ref[...], preferred_element_type=wide
        ).astype(low)

    def to_right(chip):
        return remote(part.at[chip], left_in.at[chip], r_send.at[0, chip], r_recv.at[0, chip], p.grp, p.seq + 2)

    def to_left(chip):
        return remote(part.at[chip], right_in.at[chip], r_send.at[1, chip], r_recv.at[1, chip], p.grp, p.seq - 2)

    def rail_step(order):
        far = last - order

        @pl.when(far > p.chip)
        def _():
            @pl.when(p.chip > 0)
            def _():
                to_right(far).wait_recv()
                part[far] = (part[far].astype(wide) + left_in[far].astype(wide)).astype(low)

            to_right(far).start()

        @pl.when(order < p.chip)
        def _():
            @pl.when(p.chip < last)
            def _():
                to_left(order).wait_recv()
                part[order] = (part[order].astype(wide) + right_in[order].astype(wide)).astype(low)

            to_left(order).start()

    rail_step(0)
    wgrad[...] = lax.dot_general(
        cols[...].reshape(chips * shard, grps * HD), n1x[...].reshape(chips * shard, width + HD),
        CONTRACT_FIRST, preferred_element_type=wide,
    ).reshape(grps, 2, half, width + HD)
    wm = remote(wgrad.at[:, 1 - p.core], wm_in, wm_send, wm_recv, p.grp, p.mate)
    wm.start()
    rail_step(1)
    wm.wait_recv()
    w_send_buf[...] = (wgrad[:, p.core] + wm_in[...]).astype(low)

    def w_copy(b):
        return remote(w_send_buf.at[b], w_in.at[b], w_send.at[b], w_recv.at[b], p.peer(b), p.seq)

    for b in range(1, grps):
        w_copy(b).start()
    rail_step(2)
    rail_step(3)

    tokens = tokens_ref[...].astype(wide)
    tok_grad_ref[...] = part[p.chip].astype(wide)

    @pl.when(p.chip > 0)
    def _():
        to_right(p.chip).wait_recv()
        tok_grad_ref[...] += left_in[p.chip].astype(wide)

    @pl.when(p.chip < last)
    def _():
        to_left(p.chip).wait_recv()
        tok_grad_ref[...] += right_in[p.chip].astype(wide)

    n1g = tok_grad_ref[...]
    scale_one = lax.rsqrt(jnp.mean(tokens * tokens, axis=-1, keepdims=True) + EPS)
    normed = tokens * scale_one
    gain_own[0] = jnp.sum(n1g * normed, axis=0, keepdims=True)
    lifted = n1g * gain_one_ref[...].astype(wide)
    tok_grad_ref[...] = state_grad[...] + scale_one * (
        lifted - normed * jnp.mean(lifted * normed, axis=-1, keepdims=True)
    )

    def g_copy(i):
        return remote(gain_own, gain_in.at[i], g_send.at[i], g_recv.at[i], p.grp, seq_peer(i))

    for i in range(1, slots):
        g_copy(i).start()
    total = gain_own[...]
    for i in range(1, slots):
        g_copy(i).wait_recv()
        total = total + gain_in[i]
    gain_mid[...] = total

    def h_copy(b):
        return remote(gain_mid, gain_mid_in.at[b], h_send.at[b], h_recv.at[b], p.peer(b), p.seq)

    for b in range(1, grps):
        h_copy(b).start()

    wo_grad = o_terms[p.grp]
    wq_grad = wgrad[0, p.core] + wm_in[0]
    for b in range(1, grps):
        o_copy(b).wait_recv()
        wo_grad = wo_grad + o_in[b].astype(wide)
        w_copy(b).wait_recv()
        wq_grad = wq_grad + w_in[b].astype(wide)
    wo_grad_ref[...] = wo_grad
    wq_grad_ref[...] = wq_grad
    total = gain_mid[...]
    for b in range(1, grps):
        h_copy(b).wait_recv()
        total = total + gain_mid_in[b]
    gain_ref[...] = total

    m_loads[2].wait()
    m_loads[3].wait()

    def m_total(own, direct, second, i):
        for j in range(3):
            @pl.loop(0, mhalf // 16)
            def _(t, j=j):
                rows = pl.ds(pl.multiple_of(t * 16, 16), 16)
                mlp_ref[j, pl.ds(pl.multiple_of(i * mhalf + t * 16, 16), 16)] = (
                    m_own[own, j, rows].astype(wide) + m_in[direct, j, rows].astype(wide)
                ) + m_in[second, j, rows].astype(wide)

    m_first[2].wait_recv()
    m_second[1].wait_recv()
    m_total(2, 0, 5, 0)
    m_first[3].wait_recv()
    m_second[0].wait_recv()
    m_total(3, 2, 4, 1)

    for copy in m_first + m_second:
        copy.wait_send()
    line.drain()
    wm.wait_send()
    for i in range(1, slots):
        g_copy(i).wait_send()
    for b in range(1, grps):
        o_copy(b).wait_send()
        w_copy(b).wait_send()
        h_copy(b).wait_send()
    for chip in range(chips):
        km_copy(chip).wait_send()

        @pl.when(chip != p.chip)
        def _(chip=chip):
            q_copy(chip).wait_send()
            kr_copy(chip).wait_send()

        pl.when(chip > p.chip)(lambda chip=chip: to_right(chip).wait_send())
        pl.when(chip < p.chip)(lambda chip=chip: to_left(chip).wait_send())


def back_call(n2g, state, cotangent, tokens, gain_one, gain_two, attn, q_heads, kv_heads, mask, cosine, sine,
              qkv_all, out_full, n1_all, terms, owned):
    chips = cosine.shape[0]
    grps = 4
    slots = 2 * chips
    shard, width = tokens.shape
    att, block = out_full.shape[0], terms.shape[1] // grps
    unit, half = att // (grps * slots), HD // 2
    vm, dma = pltpu.VMEM, pltpu.SemaphoreType.DMA
    anyspace = pl.BlockSpec(memory_space=pl.ANY)
    vspec = pl.BlockSpec(memory_space=pltpu.VMEM)
    low, wide = jnp.bfloat16, jnp.float32
    struct = jax.ShapeDtypeStruct
    return pl.pallas_call(
        functools.partial(back_kernel, chips, 1.0 / math.sqrt(HD)),
        out_shape=(
            struct((shard, width), wide),
            struct((half, width + HD), wide),
            struct((unit, width), wide),
            struct((2, 1, width), wide),
            struct((3, block, width), wide),
        ),
        in_specs=[vspec] * 13 + [anyspace] * 4,
        out_specs=(vspec,) * 5,
        scratch_shapes=[
            vm((att, width), low),
            vm((chips, 2, shard, width), low),
            vm((chips, shard, width + HD), low),
            vm((grps, unit, slots * shard), low),
            vm((chips, 3, shard, HD), low),
            vm((chips, 3, shard, HD), low),
            vm((chips, 2, chips, shard, HD), low),
            vm((chips, chips, shard, HD), low),
            vm((chips, chips, shard, HD), low),
            vm((chips, shard, HD), wide),
            vm((chips, chips, shard, HD), low),
            vm((chips, shard, grps * HD), low),
            vm((chips, shard, width), low),
            vm((chips, shard, width), low),
            vm((chips, shard, width), low),
            vm((grps, 2, half, width + HD), wide),
            vm((grps, half, width + HD), wide),
            vm((grps, half, width + HD), low),
            vm((grps, half, width + HD), low),
            vm((grps, unit, width), wide),
            vm((grps, unit, width), low),
            vm((grps, unit, width), low),
            vm((4, 3, block // 2, width), low),
            vm((6, 3, block // 2, width), low),
            vm((2, 1, width), wide),
            vm((slots, 2, 1, width), wide),
            vm((2, 1, width), wide),
            vm((grps, 2, 1, width), wide),
            vm((shard, width), wide),
            dma((3,)),
            dma((3, chips)), dma((chips, 2)),
            dma((chips,)), dma((chips,)),
            dma((chips,)), dma((chips,)),
            dma((chips,)), dma((chips,)),
            dma((2, chips)), dma((2, chips)),
            dma, dma,
            dma((grps,)), dma((grps,)),
            dma((grps,)), dma((grps,)),
            dma((6,)), dma((6,)),
            dma((4,)),
            dma((slots,)), dma((slots,)),
            dma((grps,)), dma((grps,)),
        ],
        compiler_params=pltpu.CompilerParams(
            collective_id=3, has_side_effects=True, vmem_limit_bytes=62 * 2**20
        ),
        name="back",
    )(n2g, state, cotangent, tokens, gain_one, gain_two, attn, q_heads, kv_heads, mask, cosine, sine,
      qkv_all, out_full, n1_all, terms, owned)


def columns_to_owners(rows, row_unit):
    grp_count, seq_count = lax.axis_size("grp"), lax.axis_size("seq")
    tok_rows = rows.shape[0]
    split = rows.reshape(tok_rows, grp_count, seq_count, row_unit).transpose(2, 0, 1, 3)
    split = split.reshape(seq_count * tok_rows, grp_count * row_unit)
    return lax.all_to_all(split, "seq", split_axis=0, concat_axis=0, tiled=True)


def owners_to_columns(rows, row_unit):
    grp_count, seq_count = lax.axis_size("grp"), lax.axis_size("seq")
    tok_rows = rows.shape[0] // seq_count
    moved = lax.all_to_all(rows, "seq", split_axis=0, concat_axis=0, tiled=True)
    moved = moved.reshape(seq_count, tok_rows, grp_count, row_unit).transpose(1, 2, 0, 3)
    return moved.reshape(tok_rows, grp_count * seq_count * row_unit)


def plain_mlp(normed_two, cotangent_all, mlp_weight):
    contract_last, contract_first = CONTRACT_LAST, CONTRACT_FIRST
    mlp_rows = lax.all_gather(mlp_weight, "grp", axis=0, tiled=True)
    normed_two_all = lax.all_gather(normed_two, "seq", axis=0, tiled=True)
    gate_rows, upper_rows, down_rows = mlp_rows[:, 0, :], mlp_rows[:, 1, :], mlp_rows[:, 2, :]
    gate_vals = lax.dot_general(
        normed_two_all, gate_rows, contract_last, preferred_element_type=jnp.float32
    )
    upper_vals = lax.dot_general(
        normed_two_all, upper_rows, contract_last, preferred_element_type=jnp.float32
    )
    unit_wide, pull_back = jax.vjp(swish_product, gate_vals, upper_vals)
    unit_low = unit_wide.astype(jnp.bfloat16)
    unit_grad = lax.dot_general(
        cotangent_all, down_rows, contract_last, preferred_element_type=jnp.float32
    )
    gate_grad, upper_grad = pull_back(unit_grad)
    gate_grad = gate_grad.astype(jnp.bfloat16)
    upper_grad = upper_grad.astype(jnp.bfloat16)
    input_grad = jnp.dot(gate_grad, gate_rows, preferred_element_type=jnp.float32) + jnp.dot(
        upper_grad, upper_rows, preferred_element_type=jnp.float32
    )
    grad_part = lax.psum_scatter(
        input_grad.astype(jnp.bfloat16), "seq", scatter_dimension=0, tiled=True
    ).astype(jnp.float32)
    out_part = lax.psum_scatter(
        jnp.dot(unit_low, down_rows, preferred_element_type=jnp.float32).astype(jnp.bfloat16),
        "seq",
        scatter_dimension=0,
        tiled=True,
    ).astype(jnp.float32)
    mlp_terms = jnp.stack(
        [
            lax.dot_general(
                gate_grad, normed_two_all, contract_first, preferred_element_type=jnp.float32
            ),
            lax.dot_general(
                upper_grad, normed_two_all, contract_first, preferred_element_type=jnp.float32
            ),
            lax.dot_general(
                unit_low, cotangent_all, contract_first, preferred_element_type=jnp.float32
            ),
        ],
        axis=1,
    )
    mlp_grad = lax.psum_scatter(mlp_terms, "grp", scatter_dimension=0, tiled=True)
    return grad_part, out_part, mlp_grad


def padded_rows(mlp_weight):
    rows = mlp_weight.transpose(1, 0, 2)
    return jnp.pad(rows, ((0, 0), (0, -rows.shape[1] % 32), (0, 0)))


def per_device(
    tokens,
    cotangent,
    shard_segment,
    gain_attn,
    qkv_weight,
    qkv_bias,
    out_weight,
    gain_mlp,
    mlp_weight,
):
    tok_rows = tokens.shape[0]
    seq_count = lax.axis_size("seq")
    grp_count = lax.axis_size("grp")
    group_tok = tok_rows * seq_count
    heads_per = H // KVH
    kv_width = KVH * HD
    att_width = H * HD
    query_rows = heads_per * tok_rows
    score_scale = 1.0 / math.sqrt(HD)
    contract_last = CONTRACT_LAST
    contract_first = CONTRACT_FIRST
    seq_place = lax.axis_index("seq")
    grp_place = lax.axis_index("grp")
    use_kernels = (seq_count, grp_count, H, KVH, HD) == (8, 4, 12, 2, 128)
    if use_kernels:
        freqs = THETA ** (-(jnp.arange(HD // 2, dtype=jnp.float32) * 2.0) / HD)
        freqs = jnp.concatenate([freqs, freqs])[None, :]
        gain_rows = (gain_attn[None, :], gain_mlp[None, :])
        own_rows = padded_rows(mlp_weight)
        (
            attn_wide, state, cosine, sine, mask, q_heads, kv_heads, n1_all, n2_all, cot_all, out_all,
            qkv_all, columns, *peer_rows
        ) = front_call(
            tokens, *gain_rows, shard_segment, freqs, qkv_bias[None, :], cotangent, qkv_weight, out_weight,
            own_rows,
        )
        by_slot = lambda rows: rows.reshape((seq_count,) + rows.shape[2:])
        grad_part, out_part, mlp_terms, owned = mlp_call(
            by_slot(n2_all), by_slot(cot_all), columns, [own_rows, *peer_rows]
        )
        output = (state + out_part).astype(jnp.bfloat16)
        token_grad, qkv_terms, out_grad, gain_sums, mlp_sums = back_call(
            grad_part, state, cotangent, tokens, *gain_rows, attn_wide, q_heads, kv_heads, mask,
            cosine, sine, qkv_all.reshape(-1, qkv_all.shape[-1]),
            out_all.reshape(att_width, -1), n1_all, mlp_terms, owned,
        )
        width = tokens.shape[1]
        own = width // (grp_count * seq_count)
        gain_parts = lax.dynamic_slice_in_dim(
            gain_sums[:, 0], (grp_place * seq_count + seq_place) * own, own, 1
        )
        return (
            output,
            token_grad,
            gain_parts[0],
            qkv_terms[:, :width],
            qkv_terms[:, width],
            out_grad,
            gain_parts[1],
            mlp_sums[:, : mlp_weight.shape[0]].transpose(1, 0, 2),
        )
    segments = lax.dynamic_index_in_dim(shard_segment, grp_place, 0, keepdims=False)
    starts = shard_starts(segments, tok_rows, group_tok // 2)
    shard_order = jnp.arange(seq_count, dtype=jnp.int32)
    own_seg = jnp.sum(jnp.where(shard_order == seq_place, segments, 0))
    own_start = jnp.sum(jnp.where(shard_order == seq_place, starts, 0))
    positions = own_start + jnp.arange(tok_rows, dtype=jnp.int32)
    cosine_table, sine_table = rotary_tables(positions, HD)
    query_pos = jnp.tile(positions, heads_per)
    tokens_wide = tokens.astype(jnp.float32)
    gain_one = gain_attn.astype(jnp.float32)
    gain_two = gain_mlp.astype(jnp.float32)
    normed_one = rms_scale(tokens_wide, gain_one).astype(jnp.bfloat16)
    normed_one_all = lax.all_gather(normed_one, "seq", axis=0, tiled=True)
    qkv_rows = lax.all_gather(qkv_weight, "grp", axis=0, tiled=True)
    bias_rows = lax.all_gather(qkv_bias, "grp", axis=0, tiled=True)
    cotangent_all = lax.all_gather(cotangent, "seq", axis=0, tiled=True)
    out_full = lax.all_gather(out_weight, AXES, axis=0, tiled=True)
    projected = lax.dot_general(
        normed_one_all, qkv_rows, contract_last, preferred_element_type=jnp.float32
    )
    projected = (projected + bias_rows.astype(jnp.float32)[None, :]).astype(jnp.bfloat16)
    projected = owners_to_columns(projected, qkv_weight.shape[0]).astype(jnp.float32)
    query_rot = rotate(
        projected[:, :att_width].reshape(tok_rows, H, HD), cosine_table, sine_table
    ).astype(jnp.bfloat16)
    key_rot = rotate(
        projected[:, att_width : att_width + kv_width].reshape(tok_rows, KVH, HD),
        cosine_table,
        sine_table,
    ).astype(jnp.bfloat16)
    value_low = projected[:, att_width + kv_width :].astype(jnp.bfloat16)
    keys_all, values_all = (
        lax.all_gather(key_rot.reshape(tok_rows, kv_width), "seq", axis=0, tiled=True),
        lax.all_gather(value_low, "seq", axis=0, tiled=True),
    )
    queries = (
        query_rot.reshape(tok_rows, KVH, heads_per, HD)
        .transpose(1, 2, 0, 3)
        .reshape(KVH, query_rows, HD)
    )
    key_block = min(512, group_tok)
    block_count = group_tok // key_block
    block_order = jnp.arange(block_count, dtype=jnp.int32)

    def block_mask(block_index):
        key_index = block_index * key_block + jnp.arange(key_block, dtype=jnp.int32)
        key_shard = key_index // tok_rows
        onehot = key_shard[:, None] == shard_order[None, :]
        key_seg = jnp.sum(jnp.where(onehot, segments[None, :], 0), axis=1)
        key_pos = jnp.sum(jnp.where(onehot, starts[None, :], 0), axis=1) + key_index % tok_rows
        visible = (key_seg == 0) | (key_seg == own_seg)
        return visible[None, :] & (key_pos[None, :] <= query_pos[:, None])

    def block_keys(block_index):
        key_part = lax.dynamic_slice_in_dim(
            keys_all, block_index * key_block, key_block, 0
        ).reshape(key_block, KVH, HD)
        value_part = lax.dynamic_slice_in_dim(
            values_all, block_index * key_block, key_block, 0
        ).reshape(key_block, KVH, HD)
        return (key_part, value_part)

    def block_scores(key_part):
        return (
            jnp.einsum("krd,jkd->krj", queries, key_part, preferred_element_type=jnp.float32)
            * score_scale
        )

    def stat_step(stats_now, block_index):
        allowed = block_mask(block_index)

        def stat_visit(current):
            top_old, total_old = current
            key_part, value_part = block_keys(block_index)
            scores = jnp.where(allowed[None], block_scores(key_part), -1e30)
            top_new = jnp.maximum(top_old, jnp.max(scores, axis=-1))
            weights = jnp.where(allowed[None], jnp.exp(scores - top_new[..., None]), 0.0)
            return (top_new, total_old * jnp.exp(top_old - top_new) + jnp.sum(weights, axis=-1))

        return (lax.cond(jnp.any(allowed), stat_visit, lambda current: current, stats_now), None)

    start_stats = (
        jnp.full((KVH, query_rows), -1e30, jnp.float32),
        jnp.zeros((KVH, query_rows), jnp.float32),
    )
    (top_all, total_all), unused = lax.scan(stat_step, start_stats, block_order)
    log_total = top_all + jnp.log(total_all)

    def mix_step(mixed_sum, block_index):
        allowed = block_mask(block_index)

        def mix_visit(current):
            key_part, value_part = block_keys(block_index)
            prob_low = jnp.where(
                allowed[None], jnp.exp(block_scores(key_part) - log_total[..., None]), 0.0
            ).astype(jnp.bfloat16)
            return current + jnp.einsum(
                "krj,jkd->krd", prob_low, value_part, preferred_element_type=jnp.float32
            )

        return (lax.cond(jnp.any(allowed), mix_visit, lambda current: current, mixed_sum), None)

    mixed_sum, unused = lax.scan(
        mix_step, jnp.zeros((KVH, query_rows, HD), jnp.float32), block_order
    )
    attn_wide = (
        mixed_sum.reshape(KVH, heads_per, tok_rows, HD)
        .transpose(2, 0, 1, 3)
        .reshape(tok_rows, att_width)
    )
    attn_low = attn_wide.astype(jnp.bfloat16)
    attn_proj = jnp.dot(attn_low, out_full, preferred_element_type=jnp.float32)
    state = tokens_wide + attn_proj
    normed_two = rms_scale(state, gain_two).astype(jnp.bfloat16)
    grad_part, out_part, mlp_grad = plain_mlp(normed_two, cotangent_all, mlp_weight)
    output = (state + out_part).astype(jnp.bfloat16)
    unused_state, norm_two_back = jax.vjp(rms_scale, state, gain_two)
    state_norm_grad, gain_two_grad = norm_two_back(grad_part)
    state_grad = state_norm_grad + cotangent.astype(jnp.float32)
    state_low = state_grad.astype(jnp.bfloat16)
    attn_grad = lax.dot_general(
        state_low, out_full, contract_last, preferred_element_type=jnp.float32
    )
    attn_grad_low = attn_grad.astype(jnp.bfloat16)
    attn_owned = columns_to_owners(attn_low, out_weight.shape[0])
    state_low_all = lax.all_gather(state_low, "seq", axis=0, tiled=True)
    out_grad = lax.psum_scatter(
        lax.dot_general(
            attn_owned, state_low_all, contract_first, preferred_element_type=jnp.float32
        ),
        "grp",
        scatter_dimension=0,
        tiled=True,
    )
    grad_heads = (
        attn_grad_low.reshape(tok_rows, KVH, heads_per, HD)
        .transpose(1, 2, 0, 3)
        .reshape(KVH, query_rows, HD)
    )
    delta_rows = jnp.sum(
        (attn_grad_low.astype(jnp.float32) * attn_wide).reshape(tok_rows, H, HD), axis=-1
    )
    delta_rows = (
        delta_rows.reshape(tok_rows, KVH, heads_per).transpose(1, 2, 0).reshape(KVH, query_rows)
    )

    def back_step(query_grad, block_index):
        allowed = block_mask(block_index)

        def back_visit(current):
            key_part, value_part = block_keys(block_index)
            prob_vals = jnp.where(
                allowed[None], jnp.exp(block_scores(key_part) - log_total[..., None]), 0.0
            )
            prob_grad = jnp.einsum(
                "krd,jkd->krj", grad_heads, value_part, preferred_element_type=jnp.float32
            )
            score_grad = (prob_vals * (prob_grad - delta_rows[..., None])).astype(jnp.bfloat16)
            new_grad = (
                current
                + jnp.einsum(
                    "krj,jkd->krd", score_grad, key_part, preferred_element_type=jnp.float32
                )
                * score_scale
            )
            key_grad = (
                jnp.einsum("krj,krd->jkd", score_grad, queries, preferred_element_type=jnp.float32)
                * score_scale
            )
            value_grad = jnp.einsum(
                "krj,krd->jkd",
                prob_vals.astype(jnp.bfloat16),
                grad_heads,
                preferred_element_type=jnp.float32,
            )
            return (
                new_grad,
                (key_grad.reshape(key_block, kv_width), value_grad.reshape(key_block, kv_width)),
            )

        def skip_block(current):
            blank_rows = jnp.zeros((key_block, kv_width), jnp.float32)
            return (current, (blank_rows, blank_rows))

        return lax.cond(jnp.any(allowed), back_visit, skip_block, query_grad)

    query_grad, (key_grads, value_grads) = lax.scan(
        back_step, jnp.zeros((KVH, query_rows, HD), jnp.float32), block_order
    )
    key_own, value_own = (
        lax.psum_scatter(
            key_grads.reshape(group_tok, kv_width).astype(jnp.bfloat16),
            "seq",
            scatter_dimension=0,
            tiled=True,
        ).astype(jnp.float32),
        lax.psum_scatter(
            value_grads.reshape(group_tok, kv_width).astype(jnp.bfloat16),
            "seq",
            scatter_dimension=0,
            tiled=True,
        ).astype(jnp.float32),
    )
    query_back = unrotate(
        query_grad.reshape(KVH, heads_per, tok_rows, HD)
        .transpose(2, 0, 1, 3)
        .reshape(tok_rows, H, HD),
        cosine_table,
        sine_table,
    )
    key_back = unrotate(key_own.reshape(tok_rows, KVH, HD), cosine_table, sine_table)
    qkv_grad_low = jnp.concatenate(
        [query_back.reshape(tok_rows, att_width), key_back.reshape(tok_rows, kv_width), value_own],
        axis=1,
    ).astype(jnp.bfloat16)
    qkv_grad_owned = columns_to_owners(qkv_grad_low, qkv_weight.shape[0])
    bias_terms = jnp.sum(qkv_grad_owned.astype(jnp.float32), axis=0)
    normed_one_grad = lax.psum_scatter(
        jnp.dot(qkv_grad_owned, qkv_rows, preferred_element_type=jnp.float32).astype(jnp.bfloat16),
        "seq",
        scatter_dimension=0,
        tiled=True,
    ).astype(jnp.float32)
    qkv_grad = lax.psum_scatter(
        lax.dot_general(
            qkv_grad_owned, normed_one_all, contract_first, preferred_element_type=jnp.float32
        ),
        "grp",
        scatter_dimension=0,
        tiled=True,
    )
    unused_tokens, norm_one_back = jax.vjp(rms_scale, tokens_wide, gain_one)
    token_norm_grad, gain_one_grad = norm_one_back(normed_one_grad)
    token_grad = token_norm_grad + state_grad
    bias_part = lax.psum_scatter(bias_terms, "grp", scatter_dimension=0, tiled=True)
    gain_one_part, gain_two_part = (
        lax.psum_scatter(gain_one_grad, AXES, scatter_dimension=0, tiled=True),
        lax.psum_scatter(gain_two_grad, AXES, scatter_dimension=0, tiled=True),
    )
    return (
        output,
        token_grad,
        gain_one_part,
        qkv_grad,
        bias_part,
        out_grad,
        gain_two_part,
        mlp_grad,
    )


def solution(mesh):
    return jax.shard_map(
        per_device,
        mesh=mesh,
        in_specs=(
            P(("grp", "seq"), None),
            P(("grp", "seq"), None),
            P(),
            P(),
            P(("grp", "seq"), None),
            P(("grp", "seq")),
            P(("grp", "seq"), None),
            P(),
            P(("grp", "seq"), None, None),
        ),
        out_specs=(
            P(("grp", "seq"), None),
            P(("grp", "seq"), None),
            P(("grp", "seq")),
            P(("grp", "seq"), None),
            P(("grp", "seq")),
            P(("grp", "seq"), None),
            P(("grp", "seq")),
            P(("grp", "seq"), None, None),
        ),
        check_vma=False,
    )
```

```python
import functools
import math

import jax
import jax.numpy as jnp
from jax import lax
from jax.experimental import pallas as pl
from jax.experimental.pallas import tpu as pltpu
from jax.sharding import PartitionSpec as P

H = 12
KVH = 2
HD = 128
FF = 8960


EPS = 1e-06
THETA = 10000.0


def rms_scale(values, gain_vec):
    return values * lax.rsqrt(jnp.mean(values * values, axis=-1, keepdims=True) + EPS) * gain_vec


def rotary_tables(positions, head_dim):
    half_dim = head_dim // 2
    freqs = THETA ** (-(jnp.arange(half_dim, dtype=jnp.float32) * 2.0) / head_dim)
    angles = positions.astype(jnp.float32)[:, None] * freqs[None, :]
    cosine_table = jnp.concatenate([jnp.cos(angles), jnp.cos(angles)], axis=-1)
    sine_table = jnp.concatenate([jnp.sin(angles), jnp.sin(angles)], axis=-1)
    return (cosine_table, sine_table)


def rotate(values, cosine_table, sine_table):
    half_dim = values.shape[-1] // 2
    turned = jnp.concatenate([-values[..., half_dim:], values[..., :half_dim]], axis=-1)
    return values * cosine_table[:, None, :] + turned * sine_table[:, None, :]


def unrotate(grad_rows, cosine_table, sine_table):
    half_dim = grad_rows.shape[-1] // 2
    scaled = grad_rows * sine_table[:, None, :]
    turned = jnp.concatenate([scaled[..., half_dim:], -scaled[..., :half_dim]], axis=-1)
    return grad_rows * cosine_table[:, None, :] + turned


def shard_starts(segments, tok_dev, prompt_len):
    shard_total = segments.shape[0]
    shard_order = jnp.arange(shard_total, dtype=jnp.int32)
    same_seg = segments[:, None] == segments[None, :]
    first_shard = jnp.min(jnp.where(same_seg, shard_order[None, :], shard_total), axis=1)
    cont_start = prompt_len + (shard_order - first_shard) * tok_dev
    return jnp.where(segments == 0, shard_order * tok_dev, cont_start)


def swish_product(gate_vals, upper_vals):
    return jax.nn.silu(gate_vals) * upper_vals


AXES = ("grp", "seq")
CONTRACT_LAST = (((1,), (1,)), ((), ()))
CONTRACT_FIRST = (((0,), (0,)), ((), ()))


MESH = pl.DeviceIdType.MESH


def remote(src, dst, send_sem, recv_sem, grp, seq):
    return pltpu.make_async_remote_copy(
        src_ref=src, dst_ref=dst, send_sem=send_sem, recv_sem=recv_sem,
        device_id=(grp, seq), device_id_type=MESH,
    )


def nearest_chip(place, order, chips):
    both = 2 * jnp.minimum(place, chips - 1 - place)
    offset = (order + 1) // 2
    near = jnp.where(order % 2 == 1, place - offset, place + offset)
    rest = jnp.where(place < chips - 1 - place, order, chips - 1 - order)
    return jnp.where(order <= both, near, rest)


class Place:
    def __init__(self, chips):
        self.chips = chips
        self.grp, self.seq = lax.axis_index("grp"), lax.axis_index("seq")
        self.chip, self.core = self.seq // 2, self.seq % 2
        self.mate = self.seq + 1 - 2 * self.core

    def peer(self, offset):
        low, high = self.grp % 2, self.grp // 2
        low = 1 - low if offset % 2 else low
        high = 1 - high if offset // 2 else high
        return 2 * high + low

    def barrier(self, grps):
        barrier = pltpu.get_barrier_semaphore()
        for chip in range(self.chips):
            @pl.when(chip != self.chip)
            def _(chip=chip):
                pl.semaphore_signal(
                    barrier, inc=1, device_id=(self.grp, 2 * chip + self.core), device_id_type=MESH
                )
        pl.semaphore_signal(barrier, inc=1, device_id=(self.grp, self.mate), device_id_type=MESH)
        for offset in range(1, grps):
            pl.semaphore_signal(
                barrier, inc=1, device_id=(self.peer(offset), self.seq), device_id_type=MESH
            )
        pl.semaphore_wait(barrier, self.chips - 1 + 1 + grps - 1)


class RailGather:
    def __init__(self, place, view, send_sem, recv_sem):
        self.place, self.view, self.send_sem, self.recv_sem = place, view, send_sem, recv_sem

    def copy(self, way, chip, core):
        p = self.place
        to = (p.seq + 2, p.seq - 2, p.mate)[way]
        return remote(
            self.view(chip, core), self.view(chip, core), self.send_sem.at[way, chip],
            self.recv_sem.at[chip, core], p.grp, to,
        )

    def start(self):
        p = self.place
        pl.when(p.chip < p.chips - 1)(lambda: self.copy(0, p.chip, p.core).start())
        pl.when(p.chip > 0)(lambda: self.copy(1, p.chip, p.core).start())
        self.copy(2, p.chip, p.core).start()

    def forward(self, step):
        p = self.place

        @pl.when(p.chip - step >= 0)
        def _():
            chip = p.chip - step
            self.copy(2, chip, p.core).wait_recv()
            pl.when(p.chip < p.chips - 1)(lambda: self.copy(0, chip, p.core).start())
            self.copy(2, chip, p.core).start()

        @pl.when(p.chip + step < p.chips)
        def _():
            chip = p.chip + step
            self.copy(2, chip, p.core).wait_recv()
            pl.when(p.chip > 0)(lambda: self.copy(1, chip, p.core).start())
            self.copy(2, chip, p.core).start()

    def wait_mate(self, chip):
        self.copy(2, chip, 1 - self.place.core).wait_recv()

    def drain(self):
        p = self.place
        for chip in range(p.chips):
            self.copy(2, chip, p.core).wait_send()
            pl.when((chip <= p.chip) & (p.chip < p.chips - 1))(
                lambda chip=chip: self.copy(0, chip, p.core).wait_send()
            )
            pl.when((chip >= p.chip) & (p.chip > 0))(
                lambda chip=chip: self.copy(1, chip, p.core).wait_send()
            )


class LineScatter:
    def __init__(self, place, part, mate_in, left_in, right_in, send_sem, recv_sem):
        self.place, self.part = place, part
        self.mate_in, self.left_in, self.right_in = mate_in, left_in, right_in
        self.send_sem, self.recv_sem = send_sem, recv_sem

    def copy(self, way, src, landing, r, chip, to):
        return remote(
            src, landing.at[r, chip], self.send_sem.at[way, r, chip], self.recv_sem.at[way, r, chip],
            self.place.grp, to,
        )

    def to_mate(self, r, chip):
        p = self.place
        return self.copy(0, self.part.at[r, 2 * chip + 1 - p.core], self.mate_in, r, chip, p.mate)

    def to_right(self, r, chip):
        p = self.place
        return self.copy(1, self.part.at[r, 2 * chip + p.core], self.left_in, r, chip, p.seq + 2)

    def to_left(self, r, chip):
        p = self.place
        return self.copy(2, self.part.at[r, 2 * chip + p.core], self.right_in, r, chip, p.seq - 2)

    def step(self, r, chip):
        p = self.place
        last = p.chips - 1
        slot = 2 * chip + p.core

        @pl.when(chip != p.chip)
        def _():
            self.to_mate(r, chip).wait_recv()
            total = self.part[r, slot].astype(jnp.float32) + self.mate_in[r, chip].astype(jnp.float32)
            self.part[r, slot] = total.astype(jnp.bfloat16)

        @pl.when(chip > p.chip)
        def _():
            @pl.when(p.chip > 0)
            def _():
                self.to_right(r, chip).wait_recv()
                self.part[r, slot] = (
                    self.part[r, slot].astype(jnp.float32) + self.left_in[r, chip].astype(jnp.float32)
                ).astype(jnp.bfloat16)

            self.to_right(r, chip).start()

        @pl.when(chip < p.chip)
        def _():
            @pl.when(p.chip < last)
            def _():
                self.to_left(r, chip).wait_recv()
                self.part[r, slot] = (
                    self.part[r, slot].astype(jnp.float32) + self.right_in[r, chip].astype(jnp.float32)
                ).astype(jnp.bfloat16)

            self.to_left(r, chip).start()

    def finish(self, r, out_ref):
        p = self.place
        self.to_mate(r, p.chip).wait_recv()
        out_ref[...] = self.part[r, p.seq].astype(jnp.float32) + self.mate_in[r, p.chip].astype(jnp.float32)

        @pl.when(p.chip > 0)
        def _():
            self.to_right(r, p.chip).wait_recv()
            out_ref[...] += self.left_in[r, p.chip].astype(jnp.float32)

        @pl.when(p.chip < p.chips - 1)
        def _():
            self.to_left(r, p.chip).wait_recv()
            out_ref[...] += self.right_in[r, p.chip].astype(jnp.float32)

    def drain(self, r):
        p = self.place
        for other in range(p.chips):
            self.to_mate(r, other).wait_send()
            pl.when(other > p.chip)(lambda other=other: self.to_right(r, other).wait_send())
            pl.when(other < p.chip)(lambda other=other: self.to_left(r, other).wait_send())


def front_kernel(chips, scale,
                 tokens_ref, gain_one_ref, gain_two_ref, segment_ref, freq_ref, bias_ref,
                 cot_ref, wq_ref, wo_ref, wm_ref,
                 attn_ref, state_ref, cos_ref, sin_ref, mask_ref, q_out_ref, kv_out_ref, n1_all_ref, n2_all_ref,
                 cot_all_ref, wo_all_ref, wq_all_ref, columns_ref, wm1_ref, wm2_ref, wm3_ref,
                 nbuf, n2buf, wq, wo, bias_own, bias, stage, qbuf, kvbuf, columns,
                 lsem, n_send, n_recv, n2_send, n2_recv, c_send, c_recv, o_send, o_recv, ox_send, ox_recv,
                 om_send, om_recv, wq_send, wq_recv, b_send, b_recv, m_send, m_recv, q_send, q_recv, k_send, k_recv):
    p = Place(chips)
    grps = 4
    half = wq_ref.shape[0]
    rows = pl.ds(p.core * half, half)
    mates_rows = pl.ds((1 - p.core) * half, half)
    wm_refs = (wm_ref, wm1_ref, wm2_ref, wm3_ref)
    part = wm_ref.shape[1] // 2

    own = [
        pltpu.make_async_copy(wq_ref, wq.at[0, rows], lsem.at[0]),
        pltpu.make_async_copy(wo_ref, wo.at[p.grp, p.chip, p.core], lsem.at[2]),
        pltpu.make_async_copy(cot_ref, cot_all_ref.at[p.chip, p.core], lsem.at[3]),
    ]
    for copy in own:
        copy.start()
    tokens = tokens_ref[...].astype(jnp.float32)
    nbuf[p.chip, p.core] = rms_scale(tokens, gain_one_ref[...].astype(jnp.float32)).astype(jnp.bfloat16)
    shard = tokens.shape[0]
    lane = lax.broadcasted_iota(jnp.int32, (1, 2 * half), 1)
    bias_wide = bias_ref[...].astype(jnp.float32)
    bias_pair = jnp.concatenate([bias_wide, bias_wide], axis=1)
    bias_own[...] = jnp.broadcast_to(jnp.where(lane // half == p.core, bias_pair, 0.0), bias_own.shape)
    bias[0, p.core] = bias_own[...]
    p.barrier(grps)

    n1_line = RailGather(p, lambda chip, core: nbuf.at[chip, core], n_send, n_recv)
    cot_line = RailGather(p, lambda chip, core: cot_all_ref.at[chip, core], c_send, c_recv)
    n2_line = RailGather(p, lambda chip, core: n2buf.at[chip, core], n2_send, n2_recv)
    out_line = RailGather(p, lambda chip, core: wo.at[p.grp, chip, core], o_send, o_recv)

    def wq_direct(b):
        return remote(wq_ref, wq.at[b, rows], wq_send.at[0, b], wq_recv.at[b, 0], p.peer(b), p.seq)

    def wq_mate(b):
        return remote(wq.at[b, rows], wq.at[b, rows], wq_send.at[1, b], wq_recv.at[b, 1], p.grp, p.mate)

    def bias_direct(b):
        return remote(bias_own, bias.at[b, p.core], b_send.at[0, b], b_recv.at[b, 0], p.peer(b), p.seq)

    def bias_mate(b):
        return remote(bias.at[b, p.core], bias.at[b, p.core], b_send.at[1, b], b_recv.at[b, 1], p.grp, p.mate)

    def m_part(ref, i, j):
        return ref.at[j, pl.ds(i * part, part)]

    def m_direct(b, i, j):
        return remote(
            m_part(wm_ref, i, j), m_part(wm_refs[b], i, j), m_send.at[b, i, j], m_recv.at[b, i, j],
            p.peer(b), p.seq,
        )

    def m_forward(b, j):
        return remote(
            m_part(wm_refs[b], b - 1, j), m_part(wm3_ref, b - 1, j), m_send.at[3, b - 1, j],
            m_recv.at[3, b - 1, j], p.peer(3 - b), p.seq,
        )

    def out_cross(b, chip):
        view = wo.at[p.grp, chip, p.core]
        return remote(view, view, ox_send.at[b, chip], ox_recv.at[b, chip], p.peer(b), p.seq)

    def out_arrival(b, chip):
        view = wo.at[p.peer(b), chip, p.core]
        return remote(view, view, ox_send.at[b, chip], ox_recv.at[b, chip], p.grp, p.mate)

    def out_mate(b, core):
        view = wo.at[p.peer(b), :, core]
        return remote(view, view, om_send.at[b], om_recv.at[b], p.grp, p.mate)

    def q_copy(chip):
        return remote(
            stage.at[chip, pl.ds(0, 3)], qbuf.at[p.chip], q_send.at[chip], q_recv.at[p.chip],
            p.grp, 2 * chip + p.core,
        )

    def q_arrival(chip):
        return remote(stage.at[chip, pl.ds(0, 3)], qbuf.at[chip], q_send.at[chip], q_recv.at[chip], p.grp, p.mate)

    def k_copy(chip, to_chip):
        return remote(
            stage.at[chip, 3], kvbuf.at[p.chip, p.core, chip], k_send.at[0, chip, to_chip],
            k_recv.at[p.chip, p.core, chip], p.grp, 2 * to_chip + p.core,
        )

    def k_mate(head, chip, src=None):
        view = kvbuf.at[head, p.core, chip]
        return remote(
            view if src is None else src, view, k_send.at[1, head, chip],
            k_recv.at[head, p.core, chip], p.grp, p.mate,
        )

    def k_arrival(head, core, chip):
        view = kvbuf.at[head, core, chip]
        return remote(view, view, k_send.at[1, head, chip], k_recv.at[head, core, chip], p.grp, p.mate)

    def make_tables():
        segs = [segment_ref[p.grp, t] for t in range(2 * chips)]
        starts = []
        for t in range(2 * chips):
            first = jnp.int32(t)
            for other in reversed(range(t)):
                first = jnp.where(segs[other] == segs[t], jnp.int32(other), first)
            starts.append(
                jnp.where(segs[t] == 0, jnp.int32(t * shard), chips * shard + (t - first) * shard)
            )

        def own_of(values):
            own = values[0]
            for t in range(1, 2 * chips):
                own = jnp.where(p.seq == t, values[t], own)
            return own

        own_seg, own_start = own_of(segs), own_of(starts)
        row = lax.broadcasted_iota(jnp.int32, (shard, 2 * half), 0)
        column = lax.broadcasted_iota(jnp.int32, (shard, 2 * half), 1)
        freq = freq_ref[...]
        sign = jnp.where(column < half, -1.0, 1.0)
        for chip in range(chips):
            start = jnp.where(p.core == 0, starts[2 * chip], starts[2 * chip + 1])
            angle = (start + row).astype(jnp.float32) * freq
            cos_ref[chip] = jnp.cos(angle)
            sin_ref[chip] = jnp.sin(angle) * sign
        for core in range(2):
            for chip in range(chips):
                t = 2 * chip + core
                seen = jnp.where((segs[t] == 0) | (segs[t] == own_seg), jnp.int32(1), jnp.int32(0))
                allowed = (starts[t] + column <= own_start + row) & (row * 0 + seen > 0)
                block = core * chips + chip
                mask_ref[:, block * shard : (block + 1) * shard] = jnp.where(allowed, 0.0, -1e30)

    own[0].wait()
    for b in range(1, grps):
        wq_direct(b).start()
        bias_direct(b).start()
    wq_mate(0).start()
    bias_mate(0).start()
    n1_line.start()
    own[1].wait()
    out_line.start()
    for b in range(1, grps):
        wq_direct(b).wait_recv()
        wq_mate(b).start()
        bias_direct(b).wait_recv()
        bias_mate(b).start()
    for b in range(1, grps):
        out_cross(b, p.chip).start()
    for j in range(3):
        m_direct(1, 0, j).start()
        m_direct(2, 1, j).start()
    make_tables()
    for b in range(grps):
        wq_mate(b).wait_recv()
        bias_mate(b).wait_recv()

    @pl.loop(0, chips)
    def _(order):
        @pl.when(order > 0)
        def _():
            n1_line.forward(order)
            out_line.forward(order)
            for b in range(1, grps):
                pl.when(p.chip - order >= 0)(lambda b=b: out_cross(b, p.chip - order).start())
                pl.when(p.chip + order < chips)(lambda b=b: out_cross(b, p.chip + order).start())

        at = nearest_chip(p.chip, order, chips)
        x = nbuf[at, p.core]
        weights = wq[...].reshape(grps * 2 * half, x.shape[1])
        rows_all = lax.dot_general(x, weights, CONTRACT_LAST, preferred_element_type=jnp.float32)
        cosine, sine = cos_ref[at], sin_ref[at]
        for b in range(grps):
            u = rows_all[:, 2 * half * b : 2 * half * (b + 1)] + (bias[b, 0, 0:1] + bias[b, 1, 0:1])
            turned = u * cosine + pltpu.roll(u, half, 1) * sine
            place = p.peer(b)
            keep = jnp.where((place == grps - 1) & (p.chip >= chips // 2), 1.0, 0.0)
            value = (u * keep + turned * (1.0 - keep)).astype(jnp.bfloat16)
            stage[at, place] = value

            @pl.when(place == grps - 1)
            def _(value=value):
                kvbuf[p.chip, p.core, at] = value

            @pl.when((place < grps - 1) & (at == p.chip))
            def _(value=value, place=place):
                qbuf[p.chip, place] = value

        pl.when(at != p.chip)(lambda: q_copy(at).start())
        for to_chip in range(chips):
            pl.when(to_chip != p.chip)(lambda to_chip=to_chip: k_copy(at, to_chip).start())
        k_mate(p.chip, at, stage.at[at, 3]).start()


    @pl.loop(0, chips)
    def _(order):
        for head in range(chips):
            @pl.when(head != p.chip)
            def _(head=head):
                chip = nearest_chip(head, order, chips)
                k_arrival(head, p.core, chip).wait_recv()
                k_mate(head, chip).start()

    for chip in range(chips):
        pl.when(chip != p.chip)(lambda chip=chip: q_arrival(chip).wait_recv())
        for head in range(chips):
            k_arrival(head, 1 - p.core, chip).wait_recv()
    own[2].wait()
    cot_line.start()
    for j in (0, 1):
        for b in (1, 2):
            m_direct(b, b - 1, j).wait_recv()
            m_forward(b, j).start()
    for j in range(3):
        m_direct(1, 1, j).start()
        m_direct(2, 0, j).start()

    mask = mask_ref[...]
    heads_per = H // KVH
    for kv in range(KVH):
        heads = [kv * heads_per + i for i in range(heads_per)]
        queries = jnp.concatenate([qbuf[h % chips, h // chips] for h in heads], axis=0)
        keys = kvbuf[kv].reshape(mask.shape[1], 2 * half)
        values = kvbuf[KVH + kv].reshape(mask.shape[1], 2 * half)
        scores = lax.dot_general(queries, keys, CONTRACT_LAST, preferred_element_type=jnp.float32) * scale
        scores = scores.reshape(heads_per, shard, mask.shape[1]) + mask[None]
        weights = jnp.exp(scores - jnp.max(scores, axis=-1, keepdims=True))
        inverse = 1.0 / jnp.sum(weights, axis=-1, keepdims=True)
        probs = (weights * inverse).astype(jnp.bfloat16).reshape(heads_per * shard, mask.shape[1])
        mixed = jnp.dot(probs, values, preferred_element_type=jnp.float32)
        for i, h in enumerate(heads):
            attn_ref[:, h * 2 * half : (h + 1) * 2 * half] = mixed[i * shard : (i + 1) * shard]
        cot_line.forward(kv + 1)

    for b in range(1, grps):
        for chip in range(chips):
            out_arrival(b, chip).wait_recv()
        out_mate(b, p.core).start()
    for b in (1, 2):
        m_direct(b, b - 1, 2).wait_recv()
        m_forward(b, 2).start()
    attn_low = attn_ref[...].astype(jnp.bfloat16)
    unit = wo.shape[3]
    for owner in range(grps):
        columns[owner] = attn_low[:, owner * columns.shape[2] : (owner + 1) * columns.shape[2]]
    for b in range(1, grps):
        out_mate(b, 1 - p.core).wait_recv()
    for chip in range(chips):
        out_line.wait_mate(chip)
    state = tokens_ref[...].astype(jnp.float32) + jnp.dot(
        attn_low, wo[...].reshape(grps * chips * 2 * unit, tokens_ref.shape[1]),
        preferred_element_type=jnp.float32,
    )
    state_ref[...] = state
    n2buf[p.chip, p.core] = rms_scale(state, gain_two_ref[...].astype(jnp.float32)).astype(jnp.bfloat16)
    n2_line.start()
    cot_line.forward(3)
    outs = [
        pltpu.make_async_copy(nbuf, n1_all_ref, lsem.at[4]),
        pltpu.make_async_copy(wq, wq_all_ref, lsem.at[5]),
        pltpu.make_async_copy(qbuf, q_out_ref, lsem.at[6]),
        pltpu.make_async_copy(kvbuf, kv_out_ref, lsem.at[7]),
        pltpu.make_async_copy(wo, wo_all_ref, lsem.at[8]),
        pltpu.make_async_copy(columns, columns_ref, lsem.at[9]),
    ]
    for chip in range(chips):
        n1_line.wait_mate(chip)
    for copy in outs:
        copy.start()
    for step in range(1, chips):
        n2_line.forward(step)
    for chip in range(chips):
        cot_line.wait_mate(chip)
        n2_line.wait_mate(chip)
    last = pltpu.make_async_copy(n2buf, n2_all_ref, lsem.at[10])
    last.start()
    for b in (1, 2):
        for j in range(3):
            m_direct(b, 2 - b, j).wait_recv()
            m_forward(3 - b, j).wait_recv()
    for copy in outs:
        copy.wait()
    last.wait()
    n1_line.drain()
    n2_line.drain()
    out_line.drain()
    cot_line.drain()
    for b in range(grps):
        wq_mate(b).wait_send()
        bias_mate(b).wait_send()
    for b in range(1, grps):
        wq_direct(b).wait_send()
        bias_direct(b).wait_send()
        out_mate(b, p.core).wait_send()
        for chip in range(chips):
            out_cross(b, chip).wait_send()
    for b in (1, 2):
        for i in (0, 1):
            for j in range(3):
                m_direct(b, i, j).wait_send()
        for j in range(3):
            m_forward(b, j).wait_send()
    for chip in range(chips):
        pl.when(chip != p.chip)(lambda chip=chip: q_copy(chip).wait_send())
        for other in range(chips):
            pl.when(other != p.chip)(lambda chip=chip, other=other: k_copy(chip, other).wait_send())
            k_mate(other, chip).wait_send()


def front_call(tokens, gain_one, gain_two, segments, freqs, bias, cot, qkv_weight, out_weight, mlp_rows):
    chips = segments.shape[1] // 2
    grps = 4
    shard, width = tokens.shape
    half = qkv_weight.shape[0]
    vm, dma = pltpu.VMEM, pltpu.SemaphoreType.DMA
    anyspace = pl.BlockSpec(memory_space=pl.ANY)
    vspec = pl.BlockSpec(memory_space=pltpu.VMEM)
    low, wide = jnp.bfloat16, jnp.float32
    struct = jax.ShapeDtypeStruct
    wo_shape = (grps, chips, 2) + out_weight.shape
    columns_shape = (grps, shard, H * HD // grps)
    return pl.pallas_call(
        functools.partial(front_kernel, chips, 1.0 / math.sqrt(HD)),
        out_shape=(
            struct((shard, H * HD), wide),
            struct((shard, width), wide),
            struct((chips, shard, HD), wide),
            struct((chips, shard, HD), wide),
            struct((shard, 2 * chips * shard), wide),
            struct((chips, 3, shard, HD), low),
            struct((chips, 2, chips, shard, HD), low),
            struct((chips, 2, shard, width), low),
            struct((chips, 2, shard, width), low),
            struct((chips, 2, shard, width), low),
            struct(wo_shape, low),
            struct((grps, 2 * half, width), low),
            struct(columns_shape, low),
        ) + (struct(mlp_rows.shape, low),) * 3,
        in_specs=[vspec] * 3
        + [pl.BlockSpec(memory_space=pltpu.SMEM)]
        + [vspec] * 2
        + [anyspace] * 4,
        out_specs=(vspec,) * 5 + (anyspace,) * 11,
        scratch_shapes=[
            vm((chips, 2, shard, width), low),
            vm((chips, 2, shard, width), low),
            vm((grps, 2 * half, width), low),
            vm(wo_shape, low),
            vm((8, HD), wide),
            vm((grps, 2, 8, HD), wide),
            vm((chips, grps, shard, HD), low),
            vm((chips, 3, shard, HD), low),
            vm((chips, 2, chips, shard, HD), low),
            vm(columns_shape, low),
            dma((11,)),
            dma((3, chips)), dma((chips, 2)),
            dma((3, chips)), dma((chips, 2)),
            dma((3, chips)), dma((chips, 2)),
            dma((3, chips)), dma((chips, 2)),
            dma((grps, chips)), dma((grps, chips)), dma((grps,)), dma((grps,)),
            dma((2, grps)), dma((grps, 2)),
            dma((2, grps)), dma((grps, 2)),
            dma((grps, 2, 3)), dma((grps, 2, 3)),
            dma((chips,)), dma((chips,)),
            dma((2, chips, chips)), dma((chips, 2, chips)),
        ],
        compiler_params=pltpu.CompilerParams(
            collective_id=2, has_side_effects=True, vmem_limit_bytes=60 * 2**20
        ),
        name="front",
    )(tokens, gain_one, gain_two, segments, freqs, bias, cot, qkv_weight, out_weight, mlp_rows)


FIRST_HOPS = ((1, 0, 1), (3, 0, 1), (2, 1, 2), (3, 1, 2))
EARLY_HOPS = tuple((hop, kind) for kind in (2, 0) for hop in (1, 3, 0, 2))


def mlp_kernel(chips, grps, row_tiles, n2_ref, cot_ref, columns_ref, *refs):
    w_refs, refs = refs[:grps], refs[grps:]
    (
        n2g_ref, outp_ref, grads_ref, owned_ref, passing_ref, arrived_ref, tok, w, acts, part, mate_in, left_in, right_in, stage,
        lsem, ssend, srecv, wsem, osem, a_send, a_recv, e_send, e_recv,
    ) = refs
    p = Place(chips)
    shard, width = n2_ref.shape[1:]
    units = w.shape[1]
    block = units // grps
    tile = units // row_tiles
    loads = [
        pltpu.make_async_copy(n2_ref, tok.at[0], lsem.at[0]),
        pltpu.make_async_copy(cot_ref, tok.at[1], lsem.at[1]),
        pltpu.make_async_copy(columns_ref.at[p.grp], owned_ref.at[0], lsem.at[2]),
    ]
    for copy in loads:
        copy.start()

    def w_copy(j, b):
        return pltpu.make_async_copy(w_refs[b].at[j], w.at[j, pl.ds(b * block, block)], wsem.at[j, b])

    for j in range(3):
        for b in range(grps):
            w_copy(j, b).start()

    barrier = pltpu.get_barrier_semaphore()
    inner = jnp.where((p.chip > 0) & (p.chip < chips - 1), 1, 0)

    def greet(grp, seq):
        pl.semaphore_signal(barrier, inc=1, device_id=(grp, seq), device_id_type=MESH)

    greet(p.grp, p.mate)
    pl.when(p.chip > 0)(lambda: greet(p.grp, p.seq - 2))
    pl.when(p.chip < chips - 1)(lambda: greet(p.grp, p.seq + 2))
    for b in range(1, grps):
        greet(p.peer(b), p.seq)
    pl.semaphore_wait(barrier, 2 + inner + grps - 1)
    scatter = LineScatter(p, part, mate_in, left_in, right_in, ssend, srecv)

    def a_copy(b):
        return remote(
            columns_ref.at[p.peer(b)], owned_ref.at[b], a_send.at[b], a_recv.at[b], p.peer(b), p.seq
        )

    for b in range(1, grps):
        a_copy(b).start()
    for copy in loads:
        copy.wait()
    for j in range(3):
        for b in range(grps):
            w_copy(j, b).wait()

    def kind_of(t):
        return (t // row_tiles + 2) % 3

    def early(slot, kind):
        b, i, to = FIRST_HOPS[slot]
        half = block // 2
        rows = grads_ref.at[kind, pl.ds(b * block + i * half, half)]
        land = arrived_ref.at[kind // 2, pl.ds(i * half, half)] if b < 3 else passing_ref.at[i, kind]
        at = EARLY_HOPS.index((slot, kind))
        return remote(rows, land, e_send.at[at], e_recv.at[at], p.peer(to), p.seq)

    def out_copy(t):
        return pltpu.make_async_copy(
            stage.at[t % 2],
            grads_ref.at[kind_of(t), pl.ds((t % row_tiles) * tile, tile)],
            osem.at[t % 2],
        )

    def tile_grad(t):
        kind = kind_of(t)
        lhs = acts[kind, :, pl.ds(pl.multiple_of((t % row_tiles) * tile, 128), tile)]
        rhs = tok[kind // 2].reshape(2 * chips * shard, width)
        stage[t % 2] = lax.dot_general(
            lhs, rhs, CONTRACT_FIRST, preferred_element_type=jnp.float32
        ).astype(jnp.bfloat16)
        out_copy(t).start()

    def start_early(kind):
        for hop in EARLY_HOPS:
            if hop[1] == kind:
                early(*hop).start()

    def far_chip(order):
        return nearest_chip(p.chip, chips - 1 - order, chips)

    @pl.loop(0, chips + 1)
    def _(order):
        @pl.when(order < chips)
        def _():
            at = far_chip(order)
            x = tok[0, pl.ds(2 * at, 2)].reshape(2 * shard, width)
            gate = lax.dot_general(x, w[0], CONTRACT_LAST, preferred_element_type=jnp.float32)
            up = lax.dot_general(x, w[1], CONTRACT_LAST, preferred_element_type=jnp.float32)
            sig = 1.0 / (1.0 + jnp.exp(-gate))
            silu = gate * sig
            rows = pl.ds(at * (2 * shard), 2 * shard)
            acts[0, rows] = (up * sig * (1.0 + gate * (1.0 - sig))).astype(jnp.bfloat16)
            acts[1, rows] = silu.astype(jnp.bfloat16)
            hidden = (silu * up).astype(jnp.bfloat16)
            acts[2, rows] = hidden
            part[1, pl.ds(2 * at, 2)] = (
                jnp.dot(hidden, w[2], preferred_element_type=jnp.float32)
                .astype(jnp.bfloat16).reshape(2, shard, width)
            )
            scatter.to_mate(1, at).start()

        pl.when(order > 0)(lambda: scatter.step(1, far_chip(order - 1)))

    @pl.loop(0, row_tiles)
    def _(t):
        pl.when(t >= 2)(lambda: out_copy(t - 2).wait())
        tile_grad(t)

    @pl.loop(0, chips + 1)
    def _(order):
        @pl.when(order < chips)
        def _():
            at = far_chip(order)
            y = tok[1, pl.ds(2 * at, 2)].reshape(2 * shard, width)
            unit_grad = lax.dot_general(y, w[2], CONTRACT_LAST, preferred_element_type=jnp.float32)
            rows = pl.ds(at * (2 * shard), 2 * shard)
            gate_grad = (unit_grad * acts[0, rows].astype(jnp.float32)).astype(jnp.bfloat16)
            up_grad = (unit_grad * acts[1, rows].astype(jnp.float32)).astype(jnp.bfloat16)
            acts[0, rows] = gate_grad
            acts[1, rows] = up_grad
            back = jnp.dot(gate_grad, w[0], preferred_element_type=jnp.float32) + jnp.dot(
                up_grad, w[1], preferred_element_type=jnp.float32
            )
            part[0, pl.ds(2 * at, 2)] = back.astype(jnp.bfloat16).reshape(2, shard, width)
            scatter.to_mate(0, at).start()

        @pl.when(order == 1)
        def _():
            out_copy(row_tiles - 2).wait()
            out_copy(row_tiles - 1).wait()
            start_early(2)

        pl.when(order > 0)(lambda: scatter.step(0, far_chip(order - 1)))

    @pl.loop(row_tiles, 3 * row_tiles)
    def _(t):
        pl.when(t >= row_tiles + 2)(lambda: out_copy(t - 2).wait())
        pl.when(t == 2 * row_tiles + 1)(lambda: start_early(0))
        tile_grad(t)

    scatter.finish(0, n2g_ref)
    scatter.finish(1, outp_ref)
    out_copy(3 * row_tiles - 2).wait()
    out_copy(3 * row_tiles - 1).wait()
    for hop in EARLY_HOPS:
        early(*hop).wait_recv()
        early(*hop).wait_send()
    scatter.drain(0)
    scatter.drain(1)
    for b in range(1, grps):
        a_copy(b).wait_recv()
        a_copy(b).wait_send()


def mlp_call(n2_all, cot_all, columns, w_blocks, row_tiles=3):
    grps, (_, block, width) = len(w_blocks), w_blocks[0].shape
    slots, shard, _ = cot_all.shape
    chips = slots // 2
    units = grps * block
    vm, anyspace = pltpu.VMEM, pl.BlockSpec(memory_space=pl.ANY)
    vspec = pl.BlockSpec(memory_space=pltpu.VMEM)
    dma = pltpu.SemaphoreType.DMA
    return pl.pallas_call(
        functools.partial(mlp_kernel, chips, grps, row_tiles),
        out_shape=(
            jax.ShapeDtypeStruct((shard, width), jnp.float32),
            jax.ShapeDtypeStruct((shard, width), jnp.float32),
            jax.ShapeDtypeStruct((3, units, width), jnp.bfloat16),
            jax.ShapeDtypeStruct(columns.shape, jnp.bfloat16),
            jax.ShapeDtypeStruct((2, 3, block // 2, width), jnp.bfloat16),
            jax.ShapeDtypeStruct((2, block, width), jnp.bfloat16),
        ),
        in_specs=[anyspace] * (3 + grps),
        out_specs=(vspec, vspec) + (anyspace,) * 4,
        scratch_shapes=[
            vm((2, slots, shard, width), jnp.bfloat16),
            vm((3, units, width), jnp.bfloat16),
            vm((3, slots * shard, units), jnp.bfloat16),
            vm((2, slots, shard, width), jnp.bfloat16),
            vm((2, chips, shard, width), jnp.bfloat16),
            vm((2, chips, shard, width), jnp.bfloat16),
            vm((2, chips, shard, width), jnp.bfloat16),
            vm((2, units // row_tiles, width), jnp.bfloat16),
            dma((3,)), dma((3, 2, chips)), dma((3, 2, chips)),
            dma((3, grps)), dma((2,)), dma((grps,)), dma((grps,)),
            dma((len(EARLY_HOPS),)), dma((len(EARLY_HOPS),)),
        ],
        compiler_params=pltpu.CompilerParams(
            collective_id=1, has_side_effects=True, vmem_limit_bytes=62 * 2**20
        ),
        name="mlp",
    )(n2_all, cot_all, columns, *w_blocks)


def unturn(rows, cosine, sine, half):
    return rows * cosine + pltpu.roll(rows * sine, half, 1)


def back_kernel(chips, scale,
                n2g_ref, state_ref, cot_ref, tokens_ref, gain_one_ref, gain_two_ref, attn_ref, q_ref, kv_ref,
                mask_ref, cos_ref, sin_ref, wq_ref, wo_ref, n1_ref, terms_ref, owned_ref, passing_ref, early_ref,
                tok_grad_ref, wq_grad_ref, wo_grad_ref, gain_ref, direct_ref, second_ref,
                wo, stbuf, n1x, at_all, dq_stage, gq_in, kv_part, km_in, k_sum, k_own, kr_in,
                cols, part, left_in, right_in, wgrad, wm_in, w_send_buf, w_in, o_terms, ob_in, o_send_buf, o_in,
                m_own, m_in, gain_own, gain_in, gain_mid, gain_mid_in, state_grad,
                lsem, s_send, s_recv, q_send, q_recv, km_send, km_recv, kr_send, kr_recv,
                r_send, r_recv, wm_send, wm_recv, w_send, w_recv, ob_send, ob_recv, o_send, o_recv, m_send, m_recv,
                ml_sem, g_send, g_recv, h_send, h_recv):
    p = Place(chips)
    grps = 4
    shard, width = n2g_ref.shape
    slots = 2 * chips
    heads_per = H // KVH
    half = HD // 2
    low, wide = jnp.bfloat16, jnp.float32
    block = terms_ref.shape[1] // grps
    mhalf = block // 2
    last = chips - 1

    loads = [
        pltpu.make_async_copy(wo_ref, wo, lsem.at[0]),
        pltpu.make_async_copy(n1_ref.at[:, p.core], n1x.at[:, :, pl.ds(0, width)], lsem.at[1]),
        pltpu.make_async_copy(owned_ref, at_all, lsem.at[2]),
    ]
    for copy in loads:
        copy.start()

    def seq_peer(i):
        return (p.seq + i) % slots

    barrier = pltpu.get_barrier_semaphore()
    for i in range(1, slots):
        pl.semaphore_signal(barrier, inc=1, device_id=(p.grp, seq_peer(i)), device_id_type=MESH)
    for b in range(1, grps):
        pl.semaphore_signal(barrier, inc=1, device_id=(p.peer(b), p.seq), device_id_type=MESH)
    pl.semaphore_wait(barrier, slots - 1 + grps - 1)

    def m_rows(b, i, kind):
        return terms_ref.at[kind, pl.ds(b * block + i * mhalf, mhalf)]

    def m_first(hop, kind):
        b, i, to = FIRST_HOPS[hop]
        land = direct_ref.at[kind, pl.ds(i * mhalf, mhalf)] if b < 3 else m_in.at[i, kind]
        return remote(
            m_rows(b, i, kind), land, m_send.at[hop, kind], m_recv.at[hop, kind], p.peer(to), p.seq
        )

    def m_second(i, kind):
        return remote(
            m_own.at[i, kind], second_ref.at[kind, pl.ds(i * mhalf, mhalf)], m_send.at[4 + i, kind],
            m_recv.at[4 + i, kind], p.peer(2 - i), p.seq,
        )

    late_hops = [(hop, kind) for kind in (1, 0, 2) for hop in (1, 3, 0, 2) if (hop, kind) not in EARLY_HOPS]
    for hop in late_hops:
        m_first(*hop).start()
    m_loads = [
        pltpu.make_async_copy(m_rows(2 - i, i, kind), m_own.at[i, kind], ml_sem.at[i, kind])
        for i in (0, 1)
        for kind in range(3)
    ]
    for hop, kind in EARLY_HOPS:
        if FIRST_HOPS[hop][0] == 3:
            i = FIRST_HOPS[hop][1]
            m_loads.append(pltpu.make_async_copy(passing_ref.at[i, kind], m_in.at[i, kind], ml_sem.at[2 + i, kind]))
    early_copies = [
        pltpu.make_async_copy(early_ref.at[kind // 2], direct_ref.at[kind], ml_sem.at[4, kind]) for kind in (0, 2)
    ]
    for copy in early_copies:
        copy.start()
    for copy in m_loads:
        copy.start()

    def m_turn(kind):
        for i in (0, 1):
            if (1 + 2 * i, kind) in late_hops:
                m_first(1 + 2 * i, kind).wait_recv()

            @pl.loop(0, mhalf // 16)
            def _(t, i=i):
                rows = pl.ds(pl.multiple_of(t * 16, 16), 16)
                m_own[i, kind, rows] = (
                    m_own[i, kind, rows].astype(wide) + m_in[i, kind, rows].astype(wide)
                ).astype(low)

            m_second(i, kind).start()

    state = state_ref[...]
    gain_two = gain_two_ref[...].astype(wide)
    n2g = n2g_ref[...]
    scale_two = lax.rsqrt(jnp.mean(state * state, axis=-1, keepdims=True) + EPS)
    normed = state * scale_two
    gain_own[1] = jnp.sum(n2g * normed, axis=0, keepdims=True)
    lifted = n2g * gain_two
    state_grad[...] = cot_ref[...].astype(wide) + scale_two * (
        lifted - normed * jnp.mean(lifted * normed, axis=-1, keepdims=True)
    )
    state_low = state_grad[...].astype(low)
    stbuf[0] = state_low

    def state_copy(b):
        return remote(stbuf.at[0], stbuf.at[b], s_send.at[b], s_recv.at[b], p.peer(b), p.seq)

    attn = attn_ref[...]
    unit = wo.shape[0] // (grps * slots)
    loads[0].wait()
    attn_grad = lax.dot_general(state_low, wo[...], CONTRACT_LAST, preferred_element_type=wide).astype(low)
    mask = mask_ref[...]
    keys_total = mask.shape[1]
    own_cos, own_sin = cos_ref[p.chip], sin_ref[p.chip]

    def km_copy(head):
        return remote(
            kv_part.at[head, 1 - p.core], km_in.at[head], km_send.at[head], km_recv.at[head], p.grp, p.mate
        )

    def kr_copy(head):
        return remote(
            k_sum.at[head], kr_in.at[p.chip], kr_send.at[head], kr_recv.at[p.chip], p.grp, 2 * head + p.core
        )

    def kr_arrival(chip):
        return remote(k_sum.at[chip], kr_in.at[chip], kr_send.at[chip], kr_recv.at[chip], p.grp, p.mate)

    def q_copy(chip):
        return remote(
            dq_stage.at[chip], gq_in.at[p.chip], q_send.at[chip], q_recv.at[p.chip], p.grp, 2 * chip + p.core
        )

    def q_arrival(chip):
        return remote(dq_stage.at[chip], gq_in.at[chip], q_send.at[chip], q_recv.at[chip], p.grp, p.mate)

    def key_sum(head):
        km_copy(head).wait_recv()
        total = kv_part[head, p.core].astype(wide) + km_in[head].astype(wide)

        @pl.when(p.chip == head)
        def _():
            k_own[...] = total

        @pl.when(p.chip != head)
        def _():
            k_sum[head] = total.astype(low)
            kr_copy(head).start()

    for kv in range(KVH):
        heads = [kv * heads_per + i for i in range(heads_per)]
        queries = jnp.concatenate([q_ref[h % chips, h // chips] for h in heads], axis=0)
        grads = jnp.concatenate([attn_grad[:, h * HD : (h + 1) * HD] for h in heads], axis=0)
        mixed = jnp.concatenate([attn[:, h * HD : (h + 1) * HD] for h in heads], axis=0)
        delta = jnp.sum(grads.astype(wide) * mixed, axis=-1, keepdims=True)
        keys = kv_ref[kv].reshape(keys_total, HD)
        values = kv_ref[KVH + kv].reshape(keys_total, HD)
        scores = lax.dot_general(queries, keys, CONTRACT_LAST, preferred_element_type=wide) * scale
        scores = (scores.reshape(heads_per, shard, keys_total) + mask[None]).reshape(heads_per * shard, keys_total)
        weights = jnp.exp(scores - jnp.max(scores, axis=-1, keepdims=True))
        probs = weights * (1.0 / jnp.sum(weights, axis=-1, keepdims=True))
        prob_grad = lax.dot_general(grads, values, CONTRACT_LAST, preferred_element_type=wide)
        score_grad = (probs * (prob_grad - delta)).astype(low)
        key_grad = lax.dot_general(score_grad, queries, CONTRACT_FIRST, preferred_element_type=wide) * scale
        value_grad = lax.dot_general(probs.astype(low), grads, CONTRACT_FIRST, preferred_element_type=wide)
        kv_part[kv] = key_grad.astype(low).reshape(2, chips, shard, HD)
        kv_part[KVH + kv] = value_grad.astype(low).reshape(2, chips, shard, HD)
        km_copy(kv).start()
        km_copy(KVH + kv).start()
        query_grad = jnp.dot(score_grad, keys, preferred_element_type=wide) * scale
        for i, h in enumerate(heads):
            turned = unturn(query_grad[i * shard : (i + 1) * shard], own_cos, own_sin, half).astype(low)
            dq_stage[h % chips, h // chips] = turned

            @pl.when(p.chip == h % chips)
            def _(turned=turned, h=h):
                gq_in[h % chips, h // chips] = turned

        if kv == 0:
            for copy in m_loads:
                copy.wait()
            m_turn(2)
            m_turn(0)
            for b in range(1, grps):
                state_copy(b).start()
    for chip in range(chips):
        pl.when(chip != p.chip)(lambda chip=chip: q_copy(chip).start())
    for head in (0, 2, 1, 3):
        key_sum(head)
    m_turn(1)
    loads[1].wait()
    lane = lax.broadcasted_iota(jnp.int32, (chips, shard, HD), 2)
    n1x[:, :, width:] = jnp.where(lane == 0, 1.0, 0.0).astype(low)

    for chip in range(chips):
        pl.when(chip != p.chip)(lambda chip=chip: q_arrival(chip).wait_recv())
        pl.when(chip != p.chip)(lambda chip=chip: kr_arrival(chip).wait_recv())
    is_value = jnp.where(p.chip >= chips // 2, 1.0, 0.0)

    @pl.loop(0, chips)
    def _(order):
        chip = nearest_chip(p.chip, last - order, chips)
        key_total = k_own[chip]
        for other in range(chips):
            key_total = key_total + jnp.where(other == p.chip, 0.0, kr_in[other, chip].astype(wide))
        turned = unturn(key_total, cos_ref[chip], sin_ref[chip], half)
        last_head = (key_total * is_value + turned * (1.0 - is_value)).astype(low)
        for b in range(grps):
            place = p.peer(b)
            query_head = gq_in[chip, jnp.minimum(place, grps - 2)]
            cols[chip, :, b * HD : (b + 1) * HD] = jnp.where(place == grps - 1, last_head, query_head)
        part[chip] = jnp.dot(
            cols[chip], wq_ref[...], preferred_element_type=wide
        ).astype(low)

    def to_right(chip):
        return remote(part.at[chip], left_in.at[chip], r_send.at[0, chip], r_recv.at[0, chip], p.grp, p.seq + 2)

    def to_left(chip):
        return remote(part.at[chip], right_in.at[chip], r_send.at[1, chip], r_recv.at[1, chip], p.grp, p.seq - 2)

    def rail_step(order):
        far = last - order

        @pl.when(far > p.chip)
        def _():
            @pl.when(p.chip > 0)
            def _():
                to_right(far).wait_recv()
                part[far] = (part[far].astype(wide) + left_in[far].astype(wide)).astype(low)

            to_right(far).start()

        @pl.when(order < p.chip)
        def _():
            @pl.when(p.chip < last)
            def _():
                to_left(order).wait_recv()
                part[order] = (part[order].astype(wide) + right_in[order].astype(wide)).astype(low)

            to_left(order).start()

    rail_step(0)
    wgrad[...] = lax.dot_general(
        cols[...].reshape(chips * shard, grps * HD), n1x[...].reshape(chips * shard, width + HD),
        CONTRACT_FIRST, preferred_element_type=wide,
    ).reshape(grps, 2, half, width + HD)
    wm = remote(wgrad.at[:, 1 - p.core], wm_in, wm_send, wm_recv, p.grp, p.mate)
    wm.start()
    rail_step(1)
    wm.wait_recv()
    w_send_buf[...] = (wgrad[:, p.core] + wm_in[...]).astype(low)

    def w_copy(b):
        return remote(w_send_buf.at[b], w_in.at[b], w_send.at[b], w_recv.at[b], p.peer(b), p.seq)

    for b in range(1, grps):
        w_copy(b).start()
    rail_step(2)
    loads[2].wait()
    for b in range(1, grps):
        state_copy(b).wait_recv()
    o_terms[...] = lax.dot_general(
        at_all[...].reshape(grps * shard, slots * unit), stbuf[...].reshape(grps * shard, width),
        CONTRACT_FIRST, preferred_element_type=wide,
    ).reshape(chips, 2, unit, width)
    ob = remote(o_terms.at[:, 1 - p.core], ob_in, ob_send, ob_recv, p.grp, p.mate)
    ob.start()
    ob.wait_recv()
    o_send_buf[...] = (o_terms[:, p.core] + ob_in[...]).astype(low)

    def o_copy(chip):
        return remote(
            o_send_buf.at[chip], o_in.at[p.chip], o_send.at[chip], o_recv.at[p.chip], p.grp, 2 * chip + p.core
        )

    def o_arrival(chip):
        return remote(o_send_buf.at[chip], o_in.at[chip], o_send.at[chip], o_recv.at[chip], p.grp, p.mate)

    for chip in range(chips):
        pl.when(chip != p.chip)(lambda chip=chip: o_copy(chip).start())
    rail_step(3)

    tokens = tokens_ref[...].astype(wide)
    tok_grad_ref[...] = part[p.chip].astype(wide)

    @pl.when(p.chip > 0)
    def _():
        to_right(p.chip).wait_recv()
        tok_grad_ref[...] += left_in[p.chip].astype(wide)

    @pl.when(p.chip < last)
    def _():
        to_left(p.chip).wait_recv()
        tok_grad_ref[...] += right_in[p.chip].astype(wide)

    n1g = tok_grad_ref[...]
    scale_one = lax.rsqrt(jnp.mean(tokens * tokens, axis=-1, keepdims=True) + EPS)
    normed = tokens * scale_one
    gain_own[0] = jnp.sum(n1g * normed, axis=0, keepdims=True)
    lifted = n1g * gain_one_ref[...].astype(wide)
    tok_grad_ref[...] = state_grad[...] + scale_one * (
        lifted - normed * jnp.mean(lifted * normed, axis=-1, keepdims=True)
    )

    def g_copy(i):
        return remote(gain_own, gain_in.at[i], g_send.at[i], g_recv.at[i], p.grp, seq_peer(i))

    for i in range(1, slots):
        g_copy(i).start()
    total = gain_own[...]
    for i in range(1, slots):
        g_copy(i).wait_recv()
        total = total + gain_in[i]
    gain_mid[...] = total

    def h_copy(b):
        return remote(gain_mid, gain_mid_in.at[b], h_send.at[b], h_recv.at[b], p.peer(b), p.seq)

    for b in range(1, grps):
        h_copy(b).start()

    wq_grad = wgrad[0, p.core] + wm_in[0]
    for b in range(1, grps):
        w_copy(b).wait_recv()
        wq_grad = wq_grad + w_in[b].astype(wide)
    wq_grad_ref[...] = wq_grad
    wo_grad = o_terms[p.chip, p.core] + ob_in[p.chip]
    for chip in range(chips):
        pl.when(chip != p.chip)(lambda chip=chip: o_arrival(chip).wait_recv())
        wo_grad = wo_grad + jnp.where(chip == p.chip, 0.0, o_in[chip].astype(wide))
    wo_grad_ref[...] = wo_grad
    total = gain_mid[...]
    for b in range(1, grps):
        h_copy(b).wait_recv()
        total = total + gain_mid_in[b]
    gain_ref[...] = total

    for hop, kind in late_hops:
        if FIRST_HOPS[hop][0] < 3:
            m_first(hop, kind).wait_recv()
        m_first(hop, kind).wait_send()
    for kind in (2, 0, 1):
        for i in (0, 1):
            m_second(i, kind).wait_recv()
            m_second(i, kind).wait_send()
    for copy in early_copies:
        copy.wait()
    ob.wait_send()
    wm.wait_send()
    for i in range(1, slots):
        g_copy(i).wait_send()
    for b in range(1, grps):
        state_copy(b).wait_send()
        w_copy(b).wait_send()
        h_copy(b).wait_send()
    for chip in range(chips):
        km_copy(chip).wait_send()

        @pl.when(chip != p.chip)
        def _(chip=chip):
            q_copy(chip).wait_send()
            kr_copy(chip).wait_send()
            o_copy(chip).wait_send()

        pl.when(chip > p.chip)(lambda chip=chip: to_right(chip).wait_send())
        pl.when(chip < p.chip)(lambda chip=chip: to_left(chip).wait_send())


def back_call(n2g, state, cotangent, tokens, gain_one, gain_two, attn, q_heads, kv_heads, mask, cosine, sine,
              qkv_all, out_full, n1_all, terms, owned, passing, early):
    chips = cosine.shape[0]
    grps = 4
    slots = 2 * chips
    shard, width = tokens.shape
    att, block = out_full.shape[0], terms.shape[1] // grps
    unit, half = att // (grps * slots), HD // 2
    vm, dma = pltpu.VMEM, pltpu.SemaphoreType.DMA
    anyspace = pl.BlockSpec(memory_space=pl.ANY)
    vspec = pl.BlockSpec(memory_space=pltpu.VMEM)
    low, wide = jnp.bfloat16, jnp.float32
    struct = jax.ShapeDtypeStruct
    return pl.pallas_call(
        functools.partial(back_kernel, chips, 1.0 / math.sqrt(HD)),
        out_shape=(
            struct((shard, width), wide),
            struct((half, width + HD), wide),
            struct((unit, width), wide),
            struct((2, 1, width), wide),
            struct((3, block, width), low),
            struct((3, block, width), low),
        ),
        in_specs=[vspec] * 13 + [anyspace] * 6,
        out_specs=(vspec,) * 4 + (anyspace,) * 2,
        scratch_shapes=[
            vm((att, width), low),
            vm((grps, shard, width), low),
            vm((chips, shard, width + HD), low),
            vm((grps, shard, slots * unit), low),
            vm((chips, 3, shard, HD), low),
            vm((chips, 3, shard, HD), low),
            vm((chips, 2, chips, shard, HD), low),
            vm((chips, chips, shard, HD), low),
            vm((chips, chips, shard, HD), low),
            vm((chips, shard, HD), wide),
            vm((chips, chips, shard, HD), low),
            vm((chips, shard, grps * HD), low),
            vm((chips, shard, width), low),
            vm((chips, shard, width), low),
            vm((chips, shard, width), low),
            vm((grps, 2, half, width + HD), wide),
            vm((grps, half, width + HD), wide),
            vm((grps, half, width + HD), low),
            vm((grps, half, width + HD), low),
            vm((chips, 2, unit, width), wide),
            vm((chips, unit, width), wide),
            vm((chips, unit, width), low),
            vm((chips, unit, width), low),
            vm((2, 3, block // 2, width), low),
            vm((2, 3, block // 2, width), low),
            vm((2, 1, width), wide),
            vm((slots, 2, 1, width), wide),
            vm((2, 1, width), wide),
            vm((grps, 2, 1, width), wide),
            vm((shard, width), wide),
            dma((3,)),
            dma((grps,)), dma((grps,)),
            dma((chips,)), dma((chips,)),
            dma((chips,)), dma((chips,)),
            dma((chips,)), dma((chips,)),
            dma((2, chips)), dma((2, chips)),
            dma, dma,
            dma((grps,)), dma((grps,)),
            dma, dma,
            dma((chips,)), dma((chips,)),
            dma((6, 3)), dma((6, 3)),
            dma((5, 3)),
            dma((slots,)), dma((slots,)),
            dma((grps,)), dma((grps,)),
        ],
        compiler_params=pltpu.CompilerParams(
            collective_id=3, has_side_effects=True, vmem_limit_bytes=62 * 2**20
        ),
        name="back",
    )(n2g, state, cotangent, tokens, gain_one, gain_two, attn, q_heads, kv_heads, mask, cosine, sine,
      qkv_all, out_full, n1_all, terms, owned, passing, early)


def columns_to_owners(rows, row_unit):
    grp_count, seq_count = lax.axis_size("grp"), lax.axis_size("seq")
    tok_rows = rows.shape[0]
    split = rows.reshape(tok_rows, grp_count, seq_count, row_unit).transpose(2, 0, 1, 3)
    split = split.reshape(seq_count * tok_rows, grp_count * row_unit)
    return lax.all_to_all(split, "seq", split_axis=0, concat_axis=0, tiled=True)


def owners_to_columns(rows, row_unit):
    grp_count, seq_count = lax.axis_size("grp"), lax.axis_size("seq")
    tok_rows = rows.shape[0] // seq_count
    moved = lax.all_to_all(rows, "seq", split_axis=0, concat_axis=0, tiled=True)
    moved = moved.reshape(seq_count, tok_rows, grp_count, row_unit).transpose(1, 2, 0, 3)
    return moved.reshape(tok_rows, grp_count * seq_count * row_unit)


def plain_mlp(normed_two, cotangent_all, mlp_weight):
    contract_last, contract_first = CONTRACT_LAST, CONTRACT_FIRST
    mlp_rows = lax.all_gather(mlp_weight, "grp", axis=0, tiled=True)
    normed_two_all = lax.all_gather(normed_two, "seq", axis=0, tiled=True)
    gate_rows, upper_rows, down_rows = mlp_rows[:, 0, :], mlp_rows[:, 1, :], mlp_rows[:, 2, :]
    gate_vals = lax.dot_general(
        normed_two_all, gate_rows, contract_last, preferred_element_type=jnp.float32
    )
    upper_vals = lax.dot_general(
        normed_two_all, upper_rows, contract_last, preferred_element_type=jnp.float32
    )
    unit_wide, pull_back = jax.vjp(swish_product, gate_vals, upper_vals)
    unit_low = unit_wide.astype(jnp.bfloat16)
    unit_grad = lax.dot_general(
        cotangent_all, down_rows, contract_last, preferred_element_type=jnp.float32
    )
    gate_grad, upper_grad = pull_back(unit_grad)
    gate_grad = gate_grad.astype(jnp.bfloat16)
    upper_grad = upper_grad.astype(jnp.bfloat16)
    input_grad = jnp.dot(gate_grad, gate_rows, preferred_element_type=jnp.float32) + jnp.dot(
        upper_grad, upper_rows, preferred_element_type=jnp.float32
    )
    grad_part = lax.psum_scatter(
        input_grad.astype(jnp.bfloat16), "seq", scatter_dimension=0, tiled=True
    ).astype(jnp.float32)
    out_part = lax.psum_scatter(
        jnp.dot(unit_low, down_rows, preferred_element_type=jnp.float32).astype(jnp.bfloat16),
        "seq",
        scatter_dimension=0,
        tiled=True,
    ).astype(jnp.float32)
    mlp_terms = jnp.stack(
        [
            lax.dot_general(
                gate_grad, normed_two_all, contract_first, preferred_element_type=jnp.float32
            ),
            lax.dot_general(
                upper_grad, normed_two_all, contract_first, preferred_element_type=jnp.float32
            ),
            lax.dot_general(
                unit_low, cotangent_all, contract_first, preferred_element_type=jnp.float32
            ),
        ],
        axis=1,
    )
    mlp_grad = lax.psum_scatter(mlp_terms, "grp", scatter_dimension=0, tiled=True)
    return grad_part, out_part, mlp_grad


def padded_rows(mlp_weight):
    rows = mlp_weight.transpose(1, 0, 2)
    return jnp.pad(rows, ((0, 0), (0, -rows.shape[1] % 32), (0, 0)))


def per_device(
    tokens,
    cotangent,
    shard_segment,
    gain_attn,
    qkv_weight,
    qkv_bias,
    out_weight,
    gain_mlp,
    mlp_weight,
):
    tok_rows = tokens.shape[0]
    seq_count = lax.axis_size("seq")
    grp_count = lax.axis_size("grp")
    group_tok = tok_rows * seq_count
    heads_per = H // KVH
    kv_width = KVH * HD
    att_width = H * HD
    query_rows = heads_per * tok_rows
    score_scale = 1.0 / math.sqrt(HD)
    contract_last = CONTRACT_LAST
    contract_first = CONTRACT_FIRST
    seq_place = lax.axis_index("seq")
    grp_place = lax.axis_index("grp")
    use_kernels = (seq_count, grp_count, H, KVH, HD) == (8, 4, 12, 2, 128)
    if use_kernels:
        freqs = THETA ** (-(jnp.arange(HD // 2, dtype=jnp.float32) * 2.0) / HD)
        freqs = jnp.concatenate([freqs, freqs])[None, :]
        gain_rows = (gain_attn[None, :], gain_mlp[None, :])
        own_rows = padded_rows(mlp_weight)
        (
            attn_wide, state, cosine, sine, mask, q_heads, kv_heads, n1_all, n2_all, cot_all, out_all,
            qkv_all, columns, *peer_rows
        ) = front_call(
            tokens, *gain_rows, shard_segment, freqs, qkv_bias[None, :], cotangent, qkv_weight, out_weight,
            own_rows,
        )
        by_slot = lambda rows: rows.reshape((seq_count,) + rows.shape[2:])
        grad_part, out_part, mlp_terms, owned, passing, early = mlp_call(
            by_slot(n2_all), by_slot(cot_all), columns, [own_rows, *peer_rows]
        )
        output = (state + out_part).astype(jnp.bfloat16)
        token_grad, qkv_terms, out_grad, gain_sums, direct, second = back_call(
            grad_part, state, cotangent, tokens, *gain_rows, attn_wide, q_heads, kv_heads, mask,
            cosine, sine, qkv_all.reshape(-1, qkv_all.shape[-1]),
            out_all.reshape(att_width, -1), n1_all, mlp_terms, owned, passing, early,
        )
        units = mlp_weight.shape[0]
        mlp_sums = sum(
            rows[:, :units].astype(jnp.float32) for rows in (mlp_terms, direct, second)
        )
        width = tokens.shape[1]
        own = width // (grp_count * seq_count)
        gain_parts = lax.dynamic_slice_in_dim(
            gain_sums[:, 0], (grp_place * seq_count + seq_place) * own, own, 1
        )
        return (
            output,
            token_grad,
            gain_parts[0],
            qkv_terms[:, :width],
            qkv_terms[:, width],
            out_grad,
            gain_parts[1],
            mlp_sums.transpose(1, 0, 2),
        )
    segments = lax.dynamic_index_in_dim(shard_segment, grp_place, 0, keepdims=False)
    starts = shard_starts(segments, tok_rows, group_tok // 2)
    shard_order = jnp.arange(seq_count, dtype=jnp.int32)
    own_seg = jnp.sum(jnp.where(shard_order == seq_place, segments, 0))
    own_start = jnp.sum(jnp.where(shard_order == seq_place, starts, 0))
    positions = own_start + jnp.arange(tok_rows, dtype=jnp.int32)
    cosine_table, sine_table = rotary_tables(positions, HD)
    query_pos = jnp.tile(positions, heads_per)
    tokens_wide = tokens.astype(jnp.float32)
    gain_one = gain_attn.astype(jnp.float32)
    gain_two = gain_mlp.astype(jnp.float32)
    normed_one = rms_scale(tokens_wide, gain_one).astype(jnp.bfloat16)
    normed_one_all = lax.all_gather(normed_one, "seq", axis=0, tiled=True)
    qkv_rows = lax.all_gather(qkv_weight, "grp", axis=0, tiled=True)
    bias_rows = lax.all_gather(qkv_bias, "grp", axis=0, tiled=True)
    cotangent_all = lax.all_gather(cotangent, "seq", axis=0, tiled=True)
    out_full = lax.all_gather(out_weight, AXES, axis=0, tiled=True)
    projected = lax.dot_general(
        normed_one_all, qkv_rows, contract_last, preferred_element_type=jnp.float32
    )
    projected = (projected + bias_rows.astype(jnp.float32)[None, :]).astype(jnp.bfloat16)
    projected = owners_to_columns(projected, qkv_weight.shape[0]).astype(jnp.float32)
    query_rot = rotate(
        projected[:, :att_width].reshape(tok_rows, H, HD), cosine_table, sine_table
    ).astype(jnp.bfloat16)
    key_rot = rotate(
        projected[:, att_width : att_width + kv_width].reshape(tok_rows, KVH, HD),
        cosine_table,
        sine_table,
    ).astype(jnp.bfloat16)
    value_low = projected[:, att_width + kv_width :].astype(jnp.bfloat16)
    keys_all, values_all = (
        lax.all_gather(key_rot.reshape(tok_rows, kv_width), "seq", axis=0, tiled=True),
        lax.all_gather(value_low, "seq", axis=0, tiled=True),
    )
    queries = (
        query_rot.reshape(tok_rows, KVH, heads_per, HD)
        .transpose(1, 2, 0, 3)
        .reshape(KVH, query_rows, HD)
    )
    key_block = min(512, group_tok)
    block_count = group_tok // key_block
    block_order = jnp.arange(block_count, dtype=jnp.int32)

    def block_mask(block_index):
        key_index = block_index * key_block + jnp.arange(key_block, dtype=jnp.int32)
        key_shard = key_index // tok_rows
        onehot = key_shard[:, None] == shard_order[None, :]
        key_seg = jnp.sum(jnp.where(onehot, segments[None, :], 0), axis=1)
        key_pos = jnp.sum(jnp.where(onehot, starts[None, :], 0), axis=1) + key_index % tok_rows
        visible = (key_seg == 0) | (key_seg == own_seg)
        return visible[None, :] & (key_pos[None, :] <= query_pos[:, None])

    def block_keys(block_index):
        key_part = lax.dynamic_slice_in_dim(
            keys_all, block_index * key_block, key_block, 0
        ).reshape(key_block, KVH, HD)
        value_part = lax.dynamic_slice_in_dim(
            values_all, block_index * key_block, key_block, 0
        ).reshape(key_block, KVH, HD)
        return (key_part, value_part)

    def block_scores(key_part):
        return (
            jnp.einsum("krd,jkd->krj", queries, key_part, preferred_element_type=jnp.float32)
            * score_scale
        )

    def stat_step(stats_now, block_index):
        allowed = block_mask(block_index)

        def stat_visit(current):
            top_old, total_old = current
            key_part, value_part = block_keys(block_index)
            scores = jnp.where(allowed[None], block_scores(key_part), -1e30)
            top_new = jnp.maximum(top_old, jnp.max(scores, axis=-1))
            weights = jnp.where(allowed[None], jnp.exp(scores - top_new[..., None]), 0.0)
            return (top_new, total_old * jnp.exp(top_old - top_new) + jnp.sum(weights, axis=-1))

        return (lax.cond(jnp.any(allowed), stat_visit, lambda current: current, stats_now), None)

    start_stats = (
        jnp.full((KVH, query_rows), -1e30, jnp.float32),
        jnp.zeros((KVH, query_rows), jnp.float32),
    )
    (top_all, total_all), unused = lax.scan(stat_step, start_stats, block_order)
    log_total = top_all + jnp.log(total_all)

    def mix_step(mixed_sum, block_index):
        allowed = block_mask(block_index)

        def mix_visit(current):
            key_part, value_part = block_keys(block_index)
            prob_low = jnp.where(
                allowed[None], jnp.exp(block_scores(key_part) - log_total[..., None]), 0.0
            ).astype(jnp.bfloat16)
            return current + jnp.einsum(
                "krj,jkd->krd", prob_low, value_part, preferred_element_type=jnp.float32
            )

        return (lax.cond(jnp.any(allowed), mix_visit, lambda current: current, mixed_sum), None)

    mixed_sum, unused = lax.scan(
        mix_step, jnp.zeros((KVH, query_rows, HD), jnp.float32), block_order
    )
    attn_wide = (
        mixed_sum.reshape(KVH, heads_per, tok_rows, HD)
        .transpose(2, 0, 1, 3)
        .reshape(tok_rows, att_width)
    )
    attn_low = attn_wide.astype(jnp.bfloat16)
    attn_proj = jnp.dot(attn_low, out_full, preferred_element_type=jnp.float32)
    state = tokens_wide + attn_proj
    normed_two = rms_scale(state, gain_two).astype(jnp.bfloat16)
    grad_part, out_part, mlp_grad = plain_mlp(normed_two, cotangent_all, mlp_weight)
    output = (state + out_part).astype(jnp.bfloat16)
    unused_state, norm_two_back = jax.vjp(rms_scale, state, gain_two)
    state_norm_grad, gain_two_grad = norm_two_back(grad_part)
    state_grad = state_norm_grad + cotangent.astype(jnp.float32)
    state_low = state_grad.astype(jnp.bfloat16)
    attn_grad = lax.dot_general(
        state_low, out_full, contract_last, preferred_element_type=jnp.float32
    )
    attn_grad_low = attn_grad.astype(jnp.bfloat16)
    attn_owned = columns_to_owners(attn_low, out_weight.shape[0])
    state_low_all = lax.all_gather(state_low, "seq", axis=0, tiled=True)
    out_grad = lax.psum_scatter(
        lax.dot_general(
            attn_owned, state_low_all, contract_first, preferred_element_type=jnp.float32
        ),
        "grp",
        scatter_dimension=0,
        tiled=True,
    )
    grad_heads = (
        attn_grad_low.reshape(tok_rows, KVH, heads_per, HD)
        .transpose(1, 2, 0, 3)
        .reshape(KVH, query_rows, HD)
    )
    delta_rows = jnp.sum(
        (attn_grad_low.astype(jnp.float32) * attn_wide).reshape(tok_rows, H, HD), axis=-1
    )
    delta_rows = (
        delta_rows.reshape(tok_rows, KVH, heads_per).transpose(1, 2, 0).reshape(KVH, query_rows)
    )

    def back_step(query_grad, block_index):
        allowed = block_mask(block_index)

        def back_visit(current):
            key_part, value_part = block_keys(block_index)
            prob_vals = jnp.where(
                allowed[None], jnp.exp(block_scores(key_part) - log_total[..., None]), 0.0
            )
            prob_grad = jnp.einsum(
                "krd,jkd->krj", grad_heads, value_part, preferred_element_type=jnp.float32
            )
            score_grad = (prob_vals * (prob_grad - delta_rows[..., None])).astype(jnp.bfloat16)
            new_grad = (
                current
                + jnp.einsum(
                    "krj,jkd->krd", score_grad, key_part, preferred_element_type=jnp.float32
                )
                * score_scale
            )
            key_grad = (
                jnp.einsum("krj,krd->jkd", score_grad, queries, preferred_element_type=jnp.float32)
                * score_scale
            )
            value_grad = jnp.einsum(
                "krj,krd->jkd",
                prob_vals.astype(jnp.bfloat16),
                grad_heads,
                preferred_element_type=jnp.float32,
            )
            return (
                new_grad,
                (key_grad.reshape(key_block, kv_width), value_grad.reshape(key_block, kv_width)),
            )

        def skip_block(current):
            blank_rows = jnp.zeros((key_block, kv_width), jnp.float32)
            return (current, (blank_rows, blank_rows))

        return lax.cond(jnp.any(allowed), back_visit, skip_block, query_grad)

    query_grad, (key_grads, value_grads) = lax.scan(
        back_step, jnp.zeros((KVH, query_rows, HD), jnp.float32), block_order
    )
    key_own, value_own = (
        lax.psum_scatter(
            key_grads.reshape(group_tok, kv_width).astype(jnp.bfloat16),
            "seq",
            scatter_dimension=0,
            tiled=True,
        ).astype(jnp.float32),
        lax.psum_scatter(
            value_grads.reshape(group_tok, kv_width).astype(jnp.bfloat16),
            "seq",
            scatter_dimension=0,
            tiled=True,
        ).astype(jnp.float32),
    )
    query_back = unrotate(
        query_grad.reshape(KVH, heads_per, tok_rows, HD)
        .transpose(2, 0, 1, 3)
        .reshape(tok_rows, H, HD),
        cosine_table,
        sine_table,
    )
    key_back = unrotate(key_own.reshape(tok_rows, KVH, HD), cosine_table, sine_table)
    qkv_grad_low = jnp.concatenate(
        [query_back.reshape(tok_rows, att_width), key_back.reshape(tok_rows, kv_width), value_own],
        axis=1,
    ).astype(jnp.bfloat16)
    qkv_grad_owned = columns_to_owners(qkv_grad_low, qkv_weight.shape[0])
    bias_terms = jnp.sum(qkv_grad_owned.astype(jnp.float32), axis=0)
    normed_one_grad = lax.psum_scatter(
        jnp.dot(qkv_grad_owned, qkv_rows, preferred_element_type=jnp.float32).astype(jnp.bfloat16),
        "seq",
        scatter_dimension=0,
        tiled=True,
    ).astype(jnp.float32)
    qkv_grad = lax.psum_scatter(
        lax.dot_general(
            qkv_grad_owned, normed_one_all, contract_first, preferred_element_type=jnp.float32
        ),
        "grp",
        scatter_dimension=0,
        tiled=True,
    )
    unused_tokens, norm_one_back = jax.vjp(rms_scale, tokens_wide, gain_one)
    token_norm_grad, gain_one_grad = norm_one_back(normed_one_grad)
    token_grad = token_norm_grad + state_grad
    bias_part = lax.psum_scatter(bias_terms, "grp", scatter_dimension=0, tiled=True)
    gain_one_part, gain_two_part = (
        lax.psum_scatter(gain_one_grad, AXES, scatter_dimension=0, tiled=True),
        lax.psum_scatter(gain_two_grad, AXES, scatter_dimension=0, tiled=True),
    )
    return (
        output,
        token_grad,
        gain_one_part,
        qkv_grad,
        bias_part,
        out_grad,
        gain_two_part,
        mlp_grad,
    )


def solution(mesh):
    return jax.shard_map(
        per_device,
        mesh=mesh,
        in_specs=(
            P(("grp", "seq"), None),
            P(("grp", "seq"), None),
            P(),
            P(),
            P(("grp", "seq"), None),
            P(("grp", "seq")),
            P(("grp", "seq"), None),
            P(),
            P(("grp", "seq"), None, None),
        ),
        out_specs=(
            P(("grp", "seq"), None),
            P(("grp", "seq"), None),
            P(("grp", "seq")),
            P(("grp", "seq"), None),
            P(("grp", "seq")),
            P(("grp", "seq"), None),
            P(("grp", "seq")),
            P(("grp", "seq"), None, None),
        ),
        check_vma=False,
    )
```

```python
import functools
import math

import jax
import jax.numpy as jnp
from jax import lax
from jax.experimental import pallas as pl
from jax.experimental.pallas import tpu as pltpu
from jax.sharding import PartitionSpec as P

H = 12
KVH = 2
HD = 128
FF = 8960


EPS = 1e-06
THETA = 10000.0


def rms_scale(values, gain_vec):
    return values * lax.rsqrt(jnp.mean(values * values, axis=-1, keepdims=True) + EPS) * gain_vec


def rotary_tables(positions, head_dim):
    half_dim = head_dim // 2
    freqs = THETA ** (-(jnp.arange(half_dim, dtype=jnp.float32) * 2.0) / head_dim)
    angles = positions.astype(jnp.float32)[:, None] * freqs[None, :]
    cosine_table = jnp.concatenate([jnp.cos(angles), jnp.cos(angles)], axis=-1)
    sine_table = jnp.concatenate([jnp.sin(angles), jnp.sin(angles)], axis=-1)
    return (cosine_table, sine_table)


def rotate(values, cosine_table, sine_table):
    half_dim = values.shape[-1] // 2
    turned = jnp.concatenate([-values[..., half_dim:], values[..., :half_dim]], axis=-1)
    return values * cosine_table[:, None, :] + turned * sine_table[:, None, :]


def unrotate(grad_rows, cosine_table, sine_table):
    half_dim = grad_rows.shape[-1] // 2
    scaled = grad_rows * sine_table[:, None, :]
    turned = jnp.concatenate([scaled[..., half_dim:], -scaled[..., :half_dim]], axis=-1)
    return grad_rows * cosine_table[:, None, :] + turned


def shard_starts(segments, tok_dev, prompt_len):
    shard_total = segments.shape[0]
    shard_order = jnp.arange(shard_total, dtype=jnp.int32)
    same_seg = segments[:, None] == segments[None, :]
    first_shard = jnp.min(jnp.where(same_seg, shard_order[None, :], shard_total), axis=1)
    cont_start = prompt_len + (shard_order - first_shard) * tok_dev
    return jnp.where(segments == 0, shard_order * tok_dev, cont_start)


def swish_product(gate_vals, upper_vals):
    return jax.nn.silu(gate_vals) * upper_vals


AXES = ("grp", "seq")
CONTRACT_LAST = (((1,), (1,)), ((), ()))
CONTRACT_FIRST = (((0,), (0,)), ((), ()))


MESH = pl.DeviceIdType.MESH


def remote(src, dst, send_sem, recv_sem, grp, seq):
    return pltpu.make_async_remote_copy(
        src_ref=src, dst_ref=dst, send_sem=send_sem, recv_sem=recv_sem,
        device_id=(grp, seq), device_id_type=MESH,
    )


def nearest_chip(place, order, chips):
    both = 2 * jnp.minimum(place, chips - 1 - place)
    offset = (order + 1) // 2
    near = jnp.where(order % 2 == 1, place - offset, place + offset)
    rest = jnp.where(place < chips - 1 - place, order, chips - 1 - order)
    return jnp.where(order <= both, near, rest)


class Place:
    def __init__(self, chips):
        self.chips = chips
        self.grp, self.seq = lax.axis_index("grp"), lax.axis_index("seq")
        self.chip, self.core = self.seq // 2, self.seq % 2
        self.mate = self.seq + 1 - 2 * self.core

    def peer(self, offset):
        low, high = self.grp % 2, self.grp // 2
        low = 1 - low if offset % 2 else low
        high = 1 - high if offset // 2 else high
        return 2 * high + low

    def barrier(self, grps):
        barrier = pltpu.get_barrier_semaphore()
        for chip in range(self.chips):
            @pl.when(chip != self.chip)
            def _(chip=chip):
                pl.semaphore_signal(
                    barrier, inc=1, device_id=(self.grp, 2 * chip + self.core), device_id_type=MESH
                )
        pl.semaphore_signal(barrier, inc=1, device_id=(self.grp, self.mate), device_id_type=MESH)
        for offset in range(1, grps):
            pl.semaphore_signal(
                barrier, inc=1, device_id=(self.peer(offset), self.seq), device_id_type=MESH
            )
        pl.semaphore_wait(barrier, self.chips - 1 + 1 + grps - 1)


class RailGather:
    def __init__(self, place, view, send_sem, recv_sem):
        self.place, self.view, self.send_sem, self.recv_sem = place, view, send_sem, recv_sem

    def copy(self, way, chip, core):
        p = self.place
        to = (p.seq + 2, p.seq - 2, p.mate)[way]
        return remote(
            self.view(chip, core), self.view(chip, core), self.send_sem.at[way, chip],
            self.recv_sem.at[chip, core], p.grp, to,
        )

    def start(self):
        p = self.place
        pl.when(p.chip < p.chips - 1)(lambda: self.copy(0, p.chip, p.core).start())
        pl.when(p.chip > 0)(lambda: self.copy(1, p.chip, p.core).start())
        self.copy(2, p.chip, p.core).start()

    def forward(self, step):
        p = self.place

        @pl.when(p.chip - step >= 0)
        def _():
            chip = p.chip - step
            self.copy(2, chip, p.core).wait_recv()
            pl.when(p.chip < p.chips - 1)(lambda: self.copy(0, chip, p.core).start())
            self.copy(2, chip, p.core).start()

        @pl.when(p.chip + step < p.chips)
        def _():
            chip = p.chip + step
            self.copy(2, chip, p.core).wait_recv()
            pl.when(p.chip > 0)(lambda: self.copy(1, chip, p.core).start())
            self.copy(2, chip, p.core).start()

    def wait_mate(self, chip):
        self.copy(2, chip, 1 - self.place.core).wait_recv()

    def drain(self):
        p = self.place
        for chip in range(p.chips):
            self.copy(2, chip, p.core).wait_send()
            pl.when((chip <= p.chip) & (p.chip < p.chips - 1))(
                lambda chip=chip: self.copy(0, chip, p.core).wait_send()
            )
            pl.when((chip >= p.chip) & (p.chip > 0))(
                lambda chip=chip: self.copy(1, chip, p.core).wait_send()
            )


class LineScatter:
    def __init__(self, place, part, mate_in, left_in, right_in, send_sem, recv_sem):
        self.place, self.part = place, part
        self.mate_in, self.left_in, self.right_in = mate_in, left_in, right_in
        self.send_sem, self.recv_sem = send_sem, recv_sem

    def copy(self, way, src, landing, r, chip, to):
        return remote(
            src, landing.at[r, chip], self.send_sem.at[way, r, chip], self.recv_sem.at[way, r, chip],
            self.place.grp, to,
        )

    def to_mate(self, r, chip):
        p = self.place
        return self.copy(0, self.part.at[r, 2 * chip + 1 - p.core], self.mate_in, r, chip, p.mate)

    def to_right(self, r, chip):
        p = self.place
        return self.copy(1, self.part.at[r, 2 * chip + p.core], self.left_in, r, chip, p.seq + 2)

    def to_left(self, r, chip):
        p = self.place
        return self.copy(2, self.part.at[r, 2 * chip + p.core], self.right_in, r, chip, p.seq - 2)

    def step(self, r, chip):
        p = self.place
        last = p.chips - 1
        slot = 2 * chip + p.core

        @pl.when(chip != p.chip)
        def _():
            self.to_mate(r, chip).wait_recv()
            total = self.part[r, slot].astype(jnp.float32) + self.mate_in[r, chip].astype(jnp.float32)
            self.part[r, slot] = total.astype(jnp.bfloat16)

        @pl.when(chip > p.chip)
        def _():
            @pl.when(p.chip > 0)
            def _():
                self.to_right(r, chip).wait_recv()
                self.part[r, slot] = (
                    self.part[r, slot].astype(jnp.float32) + self.left_in[r, chip].astype(jnp.float32)
                ).astype(jnp.bfloat16)

            self.to_right(r, chip).start()

        @pl.when(chip < p.chip)
        def _():
            @pl.when(p.chip < last)
            def _():
                self.to_left(r, chip).wait_recv()
                self.part[r, slot] = (
                    self.part[r, slot].astype(jnp.float32) + self.right_in[r, chip].astype(jnp.float32)
                ).astype(jnp.bfloat16)

            self.to_left(r, chip).start()

    def finish(self, r, out_ref):
        p = self.place
        self.to_mate(r, p.chip).wait_recv()
        out_ref[...] = self.part[r, p.seq].astype(jnp.float32) + self.mate_in[r, p.chip].astype(jnp.float32)

        @pl.when(p.chip > 0)
        def _():
            self.to_right(r, p.chip).wait_recv()
            out_ref[...] += self.left_in[r, p.chip].astype(jnp.float32)

        @pl.when(p.chip < p.chips - 1)
        def _():
            self.to_left(r, p.chip).wait_recv()
            out_ref[...] += self.right_in[r, p.chip].astype(jnp.float32)

    def drain(self, r):
        p = self.place
        for other in range(p.chips):
            self.to_mate(r, other).wait_send()
            pl.when(other > p.chip)(lambda other=other: self.to_right(r, other).wait_send())
            pl.when(other < p.chip)(lambda other=other: self.to_left(r, other).wait_send())


def front_kernel(chips, scale,
                 tokens_ref, gain_one_ref, gain_two_ref, segment_ref, freq_ref, bias_ref,
                 cot_ref, wq_ref, wo_ref, wm_ref,
                 attn_ref, state_ref, cos_ref, sin_ref, mask_ref, q_out_ref, kv_out_ref, n1_all_ref, n2_all_ref,
                 cot_all_ref, wo_all_ref, wq_all_ref, columns_ref, wm1_ref, wm2_ref, wm3_ref,
                 nbuf, n2buf, wq, wo, bias_own, bias, stage, qbuf, kvbuf, columns,
                 lsem, n_send, n_recv, n2_send, n2_recv, c_send, c_recv, o_send, o_recv, ox_send, ox_recv,
                 om_send, om_recv, wq_send, wq_recv, b_send, b_recv, m_send, m_recv, q_send, q_recv, k_send, k_recv):
    p = Place(chips)
    grps = 4
    half = wq_ref.shape[0]
    rows = pl.ds(p.core * half, half)
    mates_rows = pl.ds((1 - p.core) * half, half)
    wm_refs = (wm_ref, wm1_ref, wm2_ref, wm3_ref)
    part = wm_ref.shape[1] // 2

    own = [
        pltpu.make_async_copy(wq_ref, wq.at[0, rows], lsem.at[0]),
        pltpu.make_async_copy(wo_ref, wo.at[p.grp, p.chip, p.core], lsem.at[2]),
        pltpu.make_async_copy(cot_ref, cot_all_ref.at[p.chip, p.core], lsem.at[3]),
    ]
    for copy in own:
        copy.start()
    tokens = tokens_ref[...].astype(jnp.float32)
    nbuf[p.chip, p.core] = rms_scale(tokens, gain_one_ref[...].astype(jnp.float32)).astype(jnp.bfloat16)
    shard = tokens.shape[0]
    lane = lax.broadcasted_iota(jnp.int32, (1, 2 * half), 1)
    bias_wide = bias_ref[...].astype(jnp.float32)
    bias_pair = jnp.concatenate([bias_wide, bias_wide], axis=1)
    bias_own[...] = jnp.broadcast_to(jnp.where(lane // half == p.core, bias_pair, 0.0), bias_own.shape)
    bias[0, p.core] = bias_own[...]
    p.barrier(grps)

    n1_line = RailGather(p, lambda chip, core: nbuf.at[chip, core], n_send, n_recv)
    cot_line = RailGather(p, lambda chip, core: cot_all_ref.at[chip, core], c_send, c_recv)
    n2_line = RailGather(p, lambda chip, core: n2buf.at[chip, core], n2_send, n2_recv)
    out_line = RailGather(p, lambda chip, core: wo.at[p.grp, chip, core], o_send, o_recv)

    def wq_direct(b):
        return remote(wq_ref, wq.at[b, rows], wq_send.at[0, b], wq_recv.at[b, 0], p.peer(b), p.seq)

    def wq_mate(b):
        return remote(wq.at[b, rows], wq.at[b, rows], wq_send.at[1, b], wq_recv.at[b, 1], p.grp, p.mate)

    def bias_direct(b):
        return remote(bias_own, bias.at[b, p.core], b_send.at[0, b], b_recv.at[b, 0], p.peer(b), p.seq)

    def bias_mate(b):
        return remote(bias.at[b, p.core], bias.at[b, p.core], b_send.at[1, b], b_recv.at[b, 1], p.grp, p.mate)

    def m_part(ref, i, j):
        return ref.at[j, pl.ds(i * part, part)]

    def m_direct(b, i, j):
        return remote(
            m_part(wm_ref, i, j), m_part(wm_refs[b], i, j), m_send.at[b, i, j], m_recv.at[b, i, j],
            p.peer(b), p.seq,
        )

    def m_forward(b, j):
        return remote(
            m_part(wm_refs[b], b - 1, j), m_part(wm3_ref, b - 1, j), m_send.at[3, b - 1, j],
            m_recv.at[3, b - 1, j], p.peer(3 - b), p.seq,
        )

    def out_cross(b, chip):
        view = wo.at[p.grp, chip, p.core]
        return remote(view, view, ox_send.at[b, chip], ox_recv.at[b, chip], p.peer(b), p.seq)

    def out_arrival(b, chip):
        view = wo.at[p.peer(b), chip, p.core]
        return remote(view, view, ox_send.at[b, chip], ox_recv.at[b, chip], p.grp, p.mate)

    def out_mate(b, core):
        view = wo.at[p.peer(b), :, core]
        return remote(view, view, om_send.at[b], om_recv.at[b], p.grp, p.mate)

    def q_copy(chip):
        return remote(
            stage.at[chip, pl.ds(0, 3)], qbuf.at[p.chip], q_send.at[chip], q_recv.at[p.chip],
            p.grp, 2 * chip + p.core,
        )

    def q_arrival(chip):
        return remote(stage.at[chip, pl.ds(0, 3)], qbuf.at[chip], q_send.at[chip], q_recv.at[chip], p.grp, p.mate)

    def k_copy(chip, to_chip):
        return remote(
            stage.at[chip, 3], kvbuf.at[p.chip, p.core, chip], k_send.at[0, chip, to_chip],
            k_recv.at[p.chip, p.core, chip], p.grp, 2 * to_chip + p.core,
        )

    def k_mate(head, chip, src=None):
        view = kvbuf.at[head, p.core, chip]
        return remote(
            view if src is None else src, view, k_send.at[1, head, chip],
            k_recv.at[head, p.core, chip], p.grp, p.mate,
        )

    def k_arrival(head, core, chip):
        view = kvbuf.at[head, core, chip]
        return remote(view, view, k_send.at[1, head, chip], k_recv.at[head, core, chip], p.grp, p.mate)

    def make_tables():
        segs = [segment_ref[p.grp, t] for t in range(2 * chips)]
        starts = []
        for t in range(2 * chips):
            first = jnp.int32(t)
            for other in reversed(range(t)):
                first = jnp.where(segs[other] == segs[t], jnp.int32(other), first)
            starts.append(
                jnp.where(segs[t] == 0, jnp.int32(t * shard), chips * shard + (t - first) * shard)
            )

        def own_of(values):
            own = values[0]
            for t in range(1, 2 * chips):
                own = jnp.where(p.seq == t, values[t], own)
            return own

        own_seg, own_start = own_of(segs), own_of(starts)
        row = lax.broadcasted_iota(jnp.int32, (shard, 2 * half), 0)
        column = lax.broadcasted_iota(jnp.int32, (shard, 2 * half), 1)
        freq = freq_ref[...]
        sign = jnp.where(column < half, -1.0, 1.0)
        for chip in range(chips):
            start = jnp.where(p.core == 0, starts[2 * chip], starts[2 * chip + 1])
            angle = (start + row).astype(jnp.float32) * freq
            cos_ref[chip] = jnp.cos(angle)
            sin_ref[chip] = jnp.sin(angle) * sign
        for core in range(2):
            for chip in range(chips):
                t = 2 * chip + core
                seen = jnp.where((segs[t] == 0) | (segs[t] == own_seg), jnp.int32(1), jnp.int32(0))
                allowed = (starts[t] + column <= own_start + row) & (row * 0 + seen > 0)
                block = core * chips + chip
                mask_ref[:, block * shard : (block + 1) * shard] = jnp.where(allowed, 0.0, -1e30)

    own[0].wait()
    for b in range(1, grps):
        wq_direct(b).start()
        bias_direct(b).start()
    wq_mate(0).start()
    bias_mate(0).start()
    n1_line.start()
    own[1].wait()
    out_line.start()
    for b in range(1, grps):
        wq_direct(b).wait_recv()
        wq_mate(b).start()
        bias_direct(b).wait_recv()
        bias_mate(b).start()
    for b in range(1, grps):
        out_cross(b, p.chip).start()
    for j in range(3):
        m_direct(1, 0, j).start()
        m_direct(2, 1, j).start()
    make_tables()
    for b in range(grps):
        wq_mate(b).wait_recv()
        bias_mate(b).wait_recv()

    @pl.loop(0, chips)
    def _(order):
        @pl.when(order > 0)
        def _():
            n1_line.forward(order)
            out_line.forward(order)
            for b in range(1, grps):
                pl.when(p.chip - order >= 0)(lambda b=b: out_cross(b, p.chip - order).start())
                pl.when(p.chip + order < chips)(lambda b=b: out_cross(b, p.chip + order).start())

        at = nearest_chip(p.chip, order, chips)
        x = nbuf[at, p.core]
        weights = wq[...].reshape(grps * 2 * half, x.shape[1])
        rows_all = lax.dot_general(x, weights, CONTRACT_LAST, preferred_element_type=jnp.float32)
        cosine, sine = cos_ref[at], sin_ref[at]
        for b in range(grps):
            u = rows_all[:, 2 * half * b : 2 * half * (b + 1)] + (bias[b, 0, 0:1] + bias[b, 1, 0:1])
            turned = u * cosine + pltpu.roll(u, half, 1) * sine
            place = p.peer(b)
            keep = jnp.where((place == grps - 1) & (p.chip >= chips // 2), 1.0, 0.0)
            value = (u * keep + turned * (1.0 - keep)).astype(jnp.bfloat16)
            stage[at, place] = value

            @pl.when(place == grps - 1)
            def _(value=value):
                kvbuf[p.chip, p.core, at] = value

            @pl.when((place < grps - 1) & (at == p.chip))
            def _(value=value, place=place):
                qbuf[p.chip, place] = value

        pl.when(at != p.chip)(lambda: q_copy(at).start())
        for to_chip in range(chips):
            pl.when(to_chip != p.chip)(lambda to_chip=to_chip: k_copy(at, to_chip).start())
        k_mate(p.chip, at, stage.at[at, 3]).start()


    @pl.loop(0, chips)
    def _(order):
        for head in range(chips):
            @pl.when(head != p.chip)
            def _(head=head):
                chip = nearest_chip(head, order, chips)
                k_arrival(head, p.core, chip).wait_recv()
                k_mate(head, chip).start()

    for chip in range(chips):
        pl.when(chip != p.chip)(lambda chip=chip: q_arrival(chip).wait_recv())
        for head in range(chips):
            k_arrival(head, 1 - p.core, chip).wait_recv()
    own[2].wait()
    cot_line.start()
    for j in (0, 1):
        for b in (1, 2):
            m_direct(b, b - 1, j).wait_recv()
            m_forward(b, j).start()
    for j in range(3):
        m_direct(1, 1, j).start()
        m_direct(2, 0, j).start()

    mask = mask_ref[...]
    heads_per = H // KVH
    for kv in range(KVH):
        heads = [kv * heads_per + i for i in range(heads_per)]
        queries = jnp.concatenate([qbuf[h % chips, h // chips] for h in heads], axis=0)
        keys = kvbuf[kv].reshape(mask.shape[1], 2 * half)
        values = kvbuf[KVH + kv].reshape(mask.shape[1], 2 * half)
        scores = lax.dot_general(queries, keys, CONTRACT_LAST, preferred_element_type=jnp.float32) * scale
        scores = scores.reshape(heads_per, shard, mask.shape[1]) + mask[None]
        weights = jnp.exp(scores - jnp.max(scores, axis=-1, keepdims=True))
        inverse = 1.0 / jnp.sum(weights, axis=-1, keepdims=True)
        probs = (weights * inverse).astype(jnp.bfloat16).reshape(heads_per * shard, mask.shape[1])
        mixed = jnp.dot(probs, values, preferred_element_type=jnp.float32)
        for i, h in enumerate(heads):
            attn_ref[:, h * 2 * half : (h + 1) * 2 * half] = mixed[i * shard : (i + 1) * shard]
        cot_line.forward(kv + 1)

    for b in range(1, grps):
        for chip in range(chips):
            out_arrival(b, chip).wait_recv()
        out_mate(b, p.core).start()
    for b in (1, 2):
        m_direct(b, b - 1, 2).wait_recv()
        m_forward(b, 2).start()
    attn_low = attn_ref[...].astype(jnp.bfloat16)
    unit = wo.shape[3]
    for owner in range(grps):
        columns[owner] = attn_low[:, owner * columns.shape[2] : (owner + 1) * columns.shape[2]]
    for b in range(1, grps):
        out_mate(b, 1 - p.core).wait_recv()
    for chip in range(chips):
        out_line.wait_mate(chip)
    state = tokens_ref[...].astype(jnp.float32) + jnp.dot(
        attn_low, wo[...].reshape(grps * chips * 2 * unit, tokens_ref.shape[1]),
        preferred_element_type=jnp.float32,
    )
    state_ref[...] = state
    n2buf[p.chip, p.core] = rms_scale(state, gain_two_ref[...].astype(jnp.float32)).astype(jnp.bfloat16)
    n2_line.start()
    cot_line.forward(3)
    outs = [
        pltpu.make_async_copy(nbuf, n1_all_ref, lsem.at[4]),
        pltpu.make_async_copy(wq, wq_all_ref, lsem.at[5]),
        pltpu.make_async_copy(qbuf, q_out_ref, lsem.at[6]),
        pltpu.make_async_copy(kvbuf, kv_out_ref, lsem.at[7]),
        pltpu.make_async_copy(wo, wo_all_ref, lsem.at[8]),
        pltpu.make_async_copy(columns, columns_ref, lsem.at[9]),
    ]
    for chip in range(chips):
        n1_line.wait_mate(chip)
    for copy in outs:
        copy.start()
    for step in range(1, chips):
        n2_line.forward(step)
    for chip in range(chips):
        cot_line.wait_mate(chip)
        n2_line.wait_mate(chip)
    last = pltpu.make_async_copy(n2buf, n2_all_ref, lsem.at[10])
    last.start()
    for b in (1, 2):
        for j in range(3):
            m_direct(b, 2 - b, j).wait_recv()
            m_forward(3 - b, j).wait_recv()
    for copy in outs:
        copy.wait()
    last.wait()
    n1_line.drain()
    n2_line.drain()
    out_line.drain()
    cot_line.drain()
    for b in range(grps):
        wq_mate(b).wait_send()
        bias_mate(b).wait_send()
    for b in range(1, grps):
        wq_direct(b).wait_send()
        bias_direct(b).wait_send()
        out_mate(b, p.core).wait_send()
        for chip in range(chips):
            out_cross(b, chip).wait_send()
    for b in (1, 2):
        for i in (0, 1):
            for j in range(3):
                m_direct(b, i, j).wait_send()
        for j in range(3):
            m_forward(b, j).wait_send()
    for chip in range(chips):
        pl.when(chip != p.chip)(lambda chip=chip: q_copy(chip).wait_send())
        for other in range(chips):
            pl.when(other != p.chip)(lambda chip=chip, other=other: k_copy(chip, other).wait_send())
            k_mate(other, chip).wait_send()


def front_call(tokens, gain_one, gain_two, segments, freqs, bias, cot, qkv_weight, out_weight, mlp_rows):
    chips = segments.shape[1] // 2
    grps = 4
    shard, width = tokens.shape
    half = qkv_weight.shape[0]
    vm, dma = pltpu.VMEM, pltpu.SemaphoreType.DMA
    anyspace = pl.BlockSpec(memory_space=pl.ANY)
    vspec = pl.BlockSpec(memory_space=pltpu.VMEM)
    low, wide = jnp.bfloat16, jnp.float32
    struct = jax.ShapeDtypeStruct
    wo_shape = (grps, chips, 2) + out_weight.shape
    columns_shape = (grps, shard, H * HD // grps)
    return pl.pallas_call(
        functools.partial(front_kernel, chips, 1.0 / math.sqrt(HD)),
        out_shape=(
            struct((shard, H * HD), wide),
            struct((shard, width), wide),
            struct((chips, shard, HD), wide),
            struct((chips, shard, HD), wide),
            struct((shard, 2 * chips * shard), wide),
            struct((chips, 3, shard, HD), low),
            struct((chips, 2, chips, shard, HD), low),
            struct((chips, 2, shard, width), low),
            struct((chips, 2, shard, width), low),
            struct((chips, 2, shard, width), low),
            struct(wo_shape, low),
            struct((grps, 2 * half, width), low),
            struct(columns_shape, low),
        ) + (struct(mlp_rows.shape, low),) * 3,
        in_specs=[vspec] * 3
        + [pl.BlockSpec(memory_space=pltpu.SMEM)]
        + [vspec] * 2
        + [anyspace] * 4,
        out_specs=(vspec,) * 5 + (anyspace,) * 11,
        scratch_shapes=[
            vm((chips, 2, shard, width), low),
            vm((chips, 2, shard, width), low),
            vm((grps, 2 * half, width), low),
            vm(wo_shape, low),
            vm((8, HD), wide),
            vm((grps, 2, 8, HD), wide),
            vm((chips, grps, shard, HD), low),
            vm((chips, 3, shard, HD), low),
            vm((chips, 2, chips, shard, HD), low),
            vm(columns_shape, low),
            dma((11,)),
            dma((3, chips)), dma((chips, 2)),
            dma((3, chips)), dma((chips, 2)),
            dma((3, chips)), dma((chips, 2)),
            dma((3, chips)), dma((chips, 2)),
            dma((grps, chips)), dma((grps, chips)), dma((grps,)), dma((grps,)),
            dma((2, grps)), dma((grps, 2)),
            dma((2, grps)), dma((grps, 2)),
            dma((grps, 2, 3)), dma((grps, 2, 3)),
            dma((chips,)), dma((chips,)),
            dma((2, chips, chips)), dma((chips, 2, chips)),
        ],
        compiler_params=pltpu.CompilerParams(
            collective_id=2, has_side_effects=True, vmem_limit_bytes=60 * 2**20
        ),
        name="front",
    )(tokens, gain_one, gain_two, segments, freqs, bias, cot, qkv_weight, out_weight, mlp_rows)


FIRST_HOPS = ((1, 0, 1), (3, 0, 1), (2, 1, 2), (3, 1, 2))
EARLY_HOPS = tuple((hop, kind) for kind in (2, 0) for hop in (1, 3, 0, 2))


def mlp_kernel(chips, grps, row_tiles, n2_ref, cot_ref, columns_ref, *refs):
    w_refs, refs = refs[:grps], refs[grps:]
    (
        n2g_ref, outp_ref, grads_ref, owned_ref, passing_ref, arrived_ref, tok, w, acts, part, mate_in, left_in, right_in, stage,
        lsem, ssend, srecv, wsem, osem, a_send, a_recv, e_send, e_recv,
    ) = refs
    p = Place(chips)
    shard, width = n2_ref.shape[1:]
    units = w.shape[1]
    block = units // grps
    tile = units // row_tiles
    loads = [
        pltpu.make_async_copy(n2_ref, tok.at[0], lsem.at[0]),
        pltpu.make_async_copy(cot_ref, tok.at[1], lsem.at[1]),
        pltpu.make_async_copy(columns_ref.at[p.grp], owned_ref.at[0], lsem.at[2]),
    ]
    for copy in loads:
        copy.start()

    def w_copy(j, b):
        return pltpu.make_async_copy(w_refs[b].at[j], w.at[j, pl.ds(b * block, block)], wsem.at[j, b])

    for j in range(3):
        for b in range(grps):
            w_copy(j, b).start()

    barrier = pltpu.get_barrier_semaphore()
    inner = jnp.where((p.chip > 0) & (p.chip < chips - 1), 1, 0)

    def greet(grp, seq):
        pl.semaphore_signal(barrier, inc=1, device_id=(grp, seq), device_id_type=MESH)

    greet(p.grp, p.mate)
    pl.when(p.chip > 0)(lambda: greet(p.grp, p.seq - 2))
    pl.when(p.chip < chips - 1)(lambda: greet(p.grp, p.seq + 2))
    for b in range(1, grps):
        greet(p.peer(b), p.seq)
    pl.semaphore_wait(barrier, 2 + inner + grps - 1)
    scatter = LineScatter(p, part, mate_in, left_in, right_in, ssend, srecv)

    def a_copy(b):
        return remote(
            columns_ref.at[p.peer(b)], owned_ref.at[b], a_send.at[b], a_recv.at[b], p.peer(b), p.seq
        )

    for b in range(1, grps):
        a_copy(b).start()
    for copy in loads:
        copy.wait()
    for j in range(3):
        for b in range(grps):
            w_copy(j, b).wait()

    def kind_of(t):
        return (t // row_tiles + 2) % 3

    def early(slot, kind):
        b, i, to = FIRST_HOPS[slot]
        half = block // 2
        rows = grads_ref.at[kind, pl.ds(b * block + i * half, half)]
        land = arrived_ref.at[kind // 2, pl.ds(i * half, half)] if b < 3 else passing_ref.at[i, kind]
        at = EARLY_HOPS.index((slot, kind))
        return remote(rows, land, e_send.at[at], e_recv.at[at], p.peer(to), p.seq)

    def out_copy(t):
        return pltpu.make_async_copy(
            stage.at[t % 2],
            grads_ref.at[kind_of(t), pl.ds((t % row_tiles) * tile, tile)],
            osem.at[t % 2],
        )

    def tile_grad(t):
        kind = kind_of(t)
        lhs = acts[kind, :, pl.ds(pl.multiple_of((t % row_tiles) * tile, 128), tile)]
        rhs = tok[kind // 2].reshape(2 * chips * shard, width)
        stage[t % 2] = lax.dot_general(
            lhs, rhs, CONTRACT_FIRST, preferred_element_type=jnp.float32
        ).astype(jnp.bfloat16)
        out_copy(t).start()

    def start_early(kind):
        for hop in EARLY_HOPS:
            if hop[1] == kind:
                early(*hop).start()

    def far_chip(order):
        return nearest_chip(p.chip, chips - 1 - order, chips)

    @pl.loop(0, chips + 1)
    def _(order):
        @pl.when(order < chips)
        def _():
            at = far_chip(order)
            x = tok[0, pl.ds(2 * at, 2)].reshape(2 * shard, width)
            gate = lax.dot_general(x, w[0], CONTRACT_LAST, preferred_element_type=jnp.float32)
            up = lax.dot_general(x, w[1], CONTRACT_LAST, preferred_element_type=jnp.float32)
            sig = 1.0 / (1.0 + jnp.exp(-gate))
            silu = gate * sig
            rows = pl.ds(at * (2 * shard), 2 * shard)
            acts[0, rows] = (up * sig * (1.0 + gate * (1.0 - sig))).astype(jnp.bfloat16)
            acts[1, rows] = silu.astype(jnp.bfloat16)
            hidden = (silu * up).astype(jnp.bfloat16)
            acts[2, rows] = hidden
            part[1, pl.ds(2 * at, 2)] = (
                jnp.dot(hidden, w[2], preferred_element_type=jnp.float32)
                .astype(jnp.bfloat16).reshape(2, shard, width)
            )
            scatter.to_mate(1, at).start()

        pl.when(order > 0)(lambda: scatter.step(1, far_chip(order - 1)))

    @pl.loop(0, row_tiles)
    def _(t):
        pl.when(t >= 2)(lambda: out_copy(t - 2).wait())
        tile_grad(t)

    @pl.loop(0, chips + 1)
    def _(order):
        @pl.when(order < chips)
        def _():
            at = far_chip(order)
            y = tok[1, pl.ds(2 * at, 2)].reshape(2 * shard, width)
            unit_grad = lax.dot_general(y, w[2], CONTRACT_LAST, preferred_element_type=jnp.float32)
            rows = pl.ds(at * (2 * shard), 2 * shard)
            gate_grad = (unit_grad * acts[0, rows].astype(jnp.float32)).astype(jnp.bfloat16)
            up_grad = (unit_grad * acts[1, rows].astype(jnp.float32)).astype(jnp.bfloat16)
            acts[0, rows] = gate_grad
            acts[1, rows] = up_grad
            back = jnp.dot(gate_grad, w[0], preferred_element_type=jnp.float32) + jnp.dot(
                up_grad, w[1], preferred_element_type=jnp.float32
            )
            part[0, pl.ds(2 * at, 2)] = back.astype(jnp.bfloat16).reshape(2, shard, width)
            scatter.to_mate(0, at).start()

        @pl.when(order == 1)
        def _():
            out_copy(row_tiles - 2).wait()
            out_copy(row_tiles - 1).wait()
            start_early(2)

        pl.when(order > 0)(lambda: scatter.step(0, far_chip(order - 1)))

    @pl.loop(row_tiles, 3 * row_tiles)
    def _(t):
        pl.when(t >= row_tiles + 2)(lambda: out_copy(t - 2).wait())
        pl.when(t == 2 * row_tiles + 1)(lambda: start_early(0))
        tile_grad(t)

    scatter.finish(0, n2g_ref)
    scatter.finish(1, outp_ref)
    out_copy(3 * row_tiles - 2).wait()
    out_copy(3 * row_tiles - 1).wait()
    for hop in EARLY_HOPS:
        early(*hop).wait_recv()
        early(*hop).wait_send()
    scatter.drain(0)
    scatter.drain(1)
    for b in range(1, grps):
        a_copy(b).wait_recv()
        a_copy(b).wait_send()


def mlp_call(n2_all, cot_all, columns, w_blocks, row_tiles=3):
    grps, (_, block, width) = len(w_blocks), w_blocks[0].shape
    slots, shard, _ = cot_all.shape
    chips = slots // 2
    units = grps * block
    vm, anyspace = pltpu.VMEM, pl.BlockSpec(memory_space=pl.ANY)
    vspec = pl.BlockSpec(memory_space=pltpu.VMEM)
    dma = pltpu.SemaphoreType.DMA
    return pl.pallas_call(
        functools.partial(mlp_kernel, chips, grps, row_tiles),
        out_shape=(
            jax.ShapeDtypeStruct((shard, width), jnp.float32),
            jax.ShapeDtypeStruct((shard, width), jnp.float32),
            jax.ShapeDtypeStruct((3, units, width), jnp.bfloat16),
            jax.ShapeDtypeStruct(columns.shape, jnp.bfloat16),
            jax.ShapeDtypeStruct((2, 3, block // 2, width), jnp.bfloat16),
            jax.ShapeDtypeStruct((2, block, width), jnp.bfloat16),
        ),
        in_specs=[anyspace] * (3 + grps),
        out_specs=(vspec, vspec) + (anyspace,) * 4,
        scratch_shapes=[
            vm((2, slots, shard, width), jnp.bfloat16),
            vm((3, units, width), jnp.bfloat16),
            vm((3, slots * shard, units), jnp.bfloat16),
            vm((2, slots, shard, width), jnp.bfloat16),
            vm((2, chips, shard, width), jnp.bfloat16),
            vm((2, chips, shard, width), jnp.bfloat16),
            vm((2, chips, shard, width), jnp.bfloat16),
            vm((2, units // row_tiles, width), jnp.bfloat16),
            dma((3,)), dma((3, 2, chips)), dma((3, 2, chips)),
            dma((3, grps)), dma((2,)), dma((grps,)), dma((grps,)),
            dma((len(EARLY_HOPS),)), dma((len(EARLY_HOPS),)),
        ],
        compiler_params=pltpu.CompilerParams(
            collective_id=1, has_side_effects=True, vmem_limit_bytes=62 * 2**20
        ),
        name="mlp",
    )(n2_all, cot_all, columns, *w_blocks)


def unturn(rows, cosine, sine, half):
    return rows * cosine + pltpu.roll(rows * sine, half, 1)


def back_kernel(chips, scale,
                n2g_ref, state_ref, cot_ref, tokens_ref, gain_one_ref, gain_two_ref, attn_ref, q_ref, kv_ref,
                mask_ref, cos_ref, sin_ref, wq_ref, wo_ref, n1_ref, terms_ref, owned_ref, passing_ref, early_ref,
                tok_grad_ref, wq_grad_ref, wo_grad_ref, gain_ref, direct_ref, second_ref,
                wo, stbuf, n1x, at_all, dq_stage, gq_in, kv_part, km_in, k_sum, k_own, kr_in,
                cols, part, left_in, right_in, wgrad, wm_in, w_send_buf, w_in, o_terms, ob_in, o_send_buf, o_in,
                m_own, m_in, gain_own, gain_in, gain_mid, gain_mid_in, state_grad,
                lsem, s_send, s_recv, q_send, q_recv, km_send, km_recv, kr_send, kr_recv,
                r_send, r_recv, wm_send, wm_recv, w_send, w_recv, ob_send, ob_recv, o_send, o_recv, m_send, m_recv,
                ml_sem, g_send, g_recv, h_send, h_recv):
    p = Place(chips)
    grps = 4
    shard, width = n2g_ref.shape
    slots = 2 * chips
    heads_per = H // KVH
    half = HD // 2
    low, wide = jnp.bfloat16, jnp.float32
    block = terms_ref.shape[1] // grps
    mhalf = block // 2
    last = chips - 1

    loads = [
        pltpu.make_async_copy(wo_ref, wo, lsem.at[0]),
        pltpu.make_async_copy(n1_ref.at[:, p.core], n1x.at[:, :, pl.ds(0, width)], lsem.at[1]),
        pltpu.make_async_copy(owned_ref, at_all, lsem.at[2]),
    ]
    for copy in loads:
        copy.start()

    def seq_peer(i):
        return (p.seq + i) % slots

    barrier = pltpu.get_barrier_semaphore()
    for i in range(1, slots):
        pl.semaphore_signal(barrier, inc=1, device_id=(p.grp, seq_peer(i)), device_id_type=MESH)
    for b in range(1, grps):
        pl.semaphore_signal(barrier, inc=1, device_id=(p.peer(b), p.seq), device_id_type=MESH)
    pl.semaphore_wait(barrier, slots - 1 + grps - 1)

    def m_rows(b, i, kind):
        return terms_ref.at[kind, pl.ds(b * block + i * mhalf, mhalf)]

    def m_first(hop, kind):
        b, i, to = FIRST_HOPS[hop]
        land = direct_ref.at[kind, pl.ds(i * mhalf, mhalf)] if b < 3 else m_in.at[i, kind]
        return remote(
            m_rows(b, i, kind), land, m_send.at[hop, kind], m_recv.at[hop, kind], p.peer(to), p.seq
        )

    def m_second(i, kind):
        return remote(
            m_own.at[i, kind], second_ref.at[kind, pl.ds(i * mhalf, mhalf)], m_send.at[4 + i, kind],
            m_recv.at[4 + i, kind], p.peer(2 - i), p.seq,
        )

    late_hops = [(hop, kind) for kind in (1, 0, 2) for hop in (1, 3, 0, 2) if (hop, kind) not in EARLY_HOPS]
    for hop in late_hops:
        m_first(*hop).start()
    m_loads = [
        pltpu.make_async_copy(m_rows(2 - i, i, kind), m_own.at[i, kind], ml_sem.at[i, kind])
        for i in (0, 1)
        for kind in range(3)
    ]
    for hop, kind in EARLY_HOPS:
        if FIRST_HOPS[hop][0] == 3:
            i = FIRST_HOPS[hop][1]
            m_loads.append(pltpu.make_async_copy(passing_ref.at[i, kind], m_in.at[i, kind], ml_sem.at[2 + i, kind]))
    early_copies = [
        pltpu.make_async_copy(early_ref.at[kind // 2], direct_ref.at[kind], ml_sem.at[4, kind])
        for kind in (0, 2)
        if (0, kind) in EARLY_HOPS
    ]
    for copy in early_copies:
        copy.start()
    for copy in m_loads:
        copy.start()

    def m_turn(kind):
        for i in (0, 1):
            if (1 + 2 * i, kind) in late_hops:
                m_first(1 + 2 * i, kind).wait_recv()

            @pl.loop(0, mhalf // 16)
            def _(t, i=i):
                rows = pl.ds(pl.multiple_of(t * 16, 16), 16)
                m_own[i, kind, rows] = (
                    m_own[i, kind, rows].astype(wide) + m_in[i, kind, rows].astype(wide)
                ).astype(low)

            m_second(i, kind).start()

    state = state_ref[...]
    gain_two = gain_two_ref[...].astype(wide)
    n2g = n2g_ref[...]
    scale_two = lax.rsqrt(jnp.mean(state * state, axis=-1, keepdims=True) + EPS)
    normed = state * scale_two
    gain_own[1] = jnp.sum(n2g * normed, axis=0, keepdims=True)
    lifted = n2g * gain_two
    state_grad[...] = cot_ref[...].astype(wide) + scale_two * (
        lifted - normed * jnp.mean(lifted * normed, axis=-1, keepdims=True)
    )
    state_low = state_grad[...].astype(low)
    stbuf[0] = state_low

    def state_copy(b):
        return remote(stbuf.at[0], stbuf.at[b], s_send.at[b], s_recv.at[b], p.peer(b), p.seq)

    attn = attn_ref[...]
    unit = wo.shape[0] // (grps * slots)
    loads[0].wait()
    attn_grad = lax.dot_general(state_low, wo[...], CONTRACT_LAST, preferred_element_type=wide).astype(low)
    mask = mask_ref[...]
    keys_total = mask.shape[1]
    own_cos, own_sin = cos_ref[p.chip], sin_ref[p.chip]

    def km_copy(head):
        return remote(
            kv_part.at[head, 1 - p.core], km_in.at[head], km_send.at[head], km_recv.at[head], p.grp, p.mate
        )

    def kr_copy(head):
        return remote(
            k_sum.at[head], kr_in.at[p.chip], kr_send.at[head], kr_recv.at[p.chip], p.grp, 2 * head + p.core
        )

    def kr_arrival(chip):
        return remote(k_sum.at[chip], kr_in.at[chip], kr_send.at[chip], kr_recv.at[chip], p.grp, p.mate)

    q_parts = (pl.ds(0, 1), pl.ds(1, 2))

    def q_copy(chip, i):
        return remote(
            dq_stage.at[chip, q_parts[i]], gq_in.at[p.chip, q_parts[i]], q_send.at[chip, i],
            q_recv.at[p.chip, i], p.grp, 2 * chip + p.core,
        )

    def q_arrival(chip, i):
        return remote(
            dq_stage.at[chip, q_parts[i]], gq_in.at[chip, q_parts[i]], q_send.at[chip, i],
            q_recv.at[chip, i], p.grp, p.mate,
        )

    def key_sum(head):
        km_copy(head).wait_recv()
        total = kv_part[head, p.core].astype(wide) + km_in[head].astype(wide)

        @pl.when(p.chip == head)
        def _():
            k_own[...] = total

        @pl.when(p.chip != head)
        def _():
            k_sum[head] = total.astype(low)
            kr_copy(head).start()

    for kv in range(KVH):
        heads = [kv * heads_per + i for i in range(heads_per)]
        queries = jnp.concatenate([q_ref[h % chips, h // chips] for h in heads], axis=0)
        grads = jnp.concatenate([attn_grad[:, h * HD : (h + 1) * HD] for h in heads], axis=0)
        mixed = jnp.concatenate([attn[:, h * HD : (h + 1) * HD] for h in heads], axis=0)
        delta = jnp.sum(grads.astype(wide) * mixed, axis=-1, keepdims=True)
        keys = kv_ref[kv].reshape(keys_total, HD)
        values = kv_ref[KVH + kv].reshape(keys_total, HD)
        scores = lax.dot_general(queries, keys, CONTRACT_LAST, preferred_element_type=wide) * scale
        scores = (scores.reshape(heads_per, shard, keys_total) + mask[None]).reshape(heads_per * shard, keys_total)
        weights = jnp.exp(scores - jnp.max(scores, axis=-1, keepdims=True))
        probs = weights * (1.0 / jnp.sum(weights, axis=-1, keepdims=True))
        prob_grad = lax.dot_general(grads, values, CONTRACT_LAST, preferred_element_type=wide)
        score_grad = (probs * (prob_grad - delta)).astype(low)
        key_grad = lax.dot_general(score_grad, queries, CONTRACT_FIRST, preferred_element_type=wide) * scale
        value_grad = lax.dot_general(probs.astype(low), grads, CONTRACT_FIRST, preferred_element_type=wide)
        kv_part[kv] = key_grad.astype(low).reshape(2, chips, shard, HD)
        kv_part[KVH + kv] = value_grad.astype(low).reshape(2, chips, shard, HD)
        km_copy(kv).start()
        km_copy(KVH + kv).start()
        query_grad = jnp.dot(score_grad, keys, preferred_element_type=wide) * scale
        for i, h in enumerate(heads):
            turned = unturn(query_grad[i * shard : (i + 1) * shard], own_cos, own_sin, half).astype(low)
            dq_stage[h % chips, h // chips] = turned

            @pl.when(p.chip == h % chips)
            def _(turned=turned, h=h):
                gq_in[h % chips, h // chips] = turned

        for chip in range(chips):
            pl.when(chip != p.chip)(lambda chip=chip: q_copy(chip, kv).start())
        if kv == 0:
            for copy in m_loads:
                copy.wait()
            m_turn(2)
            m_turn(0)
            for b in range(1, grps):
                state_copy(b).start()
            key_sum(0)
            key_sum(KVH)
    key_sum(1)
    key_sum(KVH + 1)
    m_turn(1)
    loads[1].wait()
    lane = lax.broadcasted_iota(jnp.int32, (chips, shard, HD), 2)
    n1x[:, :, width:] = jnp.where(lane == 0, 1.0, 0.0).astype(low)

    for chip in range(chips):
        for i in (0, 1):
            pl.when(chip != p.chip)(lambda chip=chip, i=i: q_arrival(chip, i).wait_recv())
        pl.when(chip != p.chip)(lambda chip=chip: kr_arrival(chip).wait_recv())
    is_value = jnp.where(p.chip >= chips // 2, 1.0, 0.0)

    gain_one = gain_one_ref[...].astype(wide)
    gain_own[0] = jnp.zeros_like(gain_own[0])

    def to_right(chip):
        return remote(part.at[chip], left_in.at[chip], r_send.at[0, chip], r_recv.at[0, chip], p.grp, p.seq + 2)

    def to_left(chip):
        return remote(part.at[chip], right_in.at[chip], r_send.at[1, chip], r_recv.at[1, chip], p.grp, p.seq - 2)

    @pl.loop(0, chips)
    def _(order):
        chip = nearest_chip(p.chip, last - order, chips)
        key_total = k_own[chip]
        for other in range(chips):
            key_total = key_total + jnp.where(other == p.chip, 0.0, kr_in[other, chip].astype(wide))
        turned = unturn(key_total, cos_ref[chip], sin_ref[chip], half)
        last_head = (key_total * is_value + turned * (1.0 - is_value)).astype(low)
        for b in range(grps):
            place = p.peer(b)
            query_head = gq_in[chip, jnp.minimum(place, grps - 2)]
            cols[chip, :, b * HD : (b + 1) * HD] = jnp.where(place == grps - 1, last_head, query_head)
        terms = jnp.dot(cols[chip], wq_ref[...], preferred_element_type=wide)
        part[chip] = terms.astype(low)
        gain_own[0] += jnp.sum(terms * n1x[chip, :, 0:width].astype(wide), axis=0, keepdims=True)
        pl.when((p.chip == 0) & (chip > 0))(lambda: to_right(chip).start())
        pl.when((p.chip == last) & (chip < last))(lambda: to_left(chip).start())

    gain_own[0] = gain_own[0] / gain_one

    def g_copy(i):
        return remote(gain_own, gain_in.at[i], g_send.at[i], g_recv.at[i], p.grp, seq_peer(i))

    def h_copy(b):
        return remote(gain_mid, gain_mid_in.at[b], h_send.at[b], h_recv.at[b], p.peer(b), p.seq)

    for i in range(1, slots):
        g_copy(i).start()

    def rail_step(order):
        far = last - order

        @pl.when((far > p.chip) & (p.chip > 0))
        def _():
            to_right(far).wait_recv()
            part[far] = (part[far].astype(wide) + left_in[far].astype(wide)).astype(low)
            to_right(far).start()

        @pl.when((order < p.chip) & (p.chip < last))
        def _():
            to_left(order).wait_recv()
            part[order] = (part[order].astype(wide) + right_in[order].astype(wide)).astype(low)
            to_left(order).start()

    rail_step(0)
    wgrad[...] = lax.dot_general(
        cols[...].reshape(chips * shard, grps * HD), n1x[...].reshape(chips * shard, width + HD),
        CONTRACT_FIRST, preferred_element_type=wide,
    ).reshape(grps, 2, half, width + HD)
    wm = remote(wgrad.at[:, 1 - p.core], wm_in, wm_send, wm_recv, p.grp, p.mate)
    wm.start()
    rail_step(1)
    wm.wait_recv()
    w_send_buf[...] = (wgrad[:, p.core] + wm_in[...]).astype(low)

    def w_copy(b):
        return remote(w_send_buf.at[b], w_in.at[b], w_send.at[b], w_recv.at[b], p.peer(b), p.seq)

    for b in range(1, grps):
        w_copy(b).start()
    rail_step(2)
    loads[2].wait()
    for b in range(1, grps):
        state_copy(b).wait_recv()
    o_terms[...] = lax.dot_general(
        at_all[...].reshape(grps * shard, slots * unit), stbuf[...].reshape(grps * shard, width),
        CONTRACT_FIRST, preferred_element_type=wide,
    ).reshape(chips, 2, unit, width)
    ob = remote(o_terms.at[:, 1 - p.core], ob_in, ob_send, ob_recv, p.grp, p.mate)
    ob.start()
    ob.wait_recv()
    o_send_buf[...] = (o_terms[:, p.core] + ob_in[...]).astype(low)

    def o_copy(chip):
        return remote(
            o_send_buf.at[chip], o_in.at[p.chip], o_send.at[chip], o_recv.at[p.chip], p.grp, 2 * chip + p.core
        )

    def o_arrival(chip):
        return remote(o_send_buf.at[chip], o_in.at[chip], o_send.at[chip], o_recv.at[chip], p.grp, p.mate)

    for chip in range(chips):
        pl.when(chip != p.chip)(lambda chip=chip: o_copy(chip).start())
    rail_step(3)
    total = gain_own[...]
    for i in range(1, slots):
        g_copy(i).wait_recv()
        total = total + gain_in[i]
    gain_mid[...] = total
    for b in range(1, grps):
        h_copy(b).start()

    tokens = tokens_ref[...].astype(wide)
    tok_grad_ref[...] = part[p.chip].astype(wide)

    @pl.when(p.chip > 0)
    def _():
        to_right(p.chip).wait_recv()
        tok_grad_ref[...] += left_in[p.chip].astype(wide)

    @pl.when(p.chip < last)
    def _():
        to_left(p.chip).wait_recv()
        tok_grad_ref[...] += right_in[p.chip].astype(wide)

    n1g = tok_grad_ref[...]
    scale_one = lax.rsqrt(jnp.mean(tokens * tokens, axis=-1, keepdims=True) + EPS)
    normed = tokens * scale_one
    lifted = n1g * gain_one
    tok_grad_ref[...] = state_grad[...] + scale_one * (
        lifted - normed * jnp.mean(lifted * normed, axis=-1, keepdims=True)
    )

    wq_grad = wgrad[0, p.core] + wm_in[0]
    for b in range(1, grps):
        w_copy(b).wait_recv()
        wq_grad = wq_grad + w_in[b].astype(wide)
    wq_grad_ref[...] = wq_grad
    wo_grad = o_terms[p.chip, p.core] + ob_in[p.chip]
    for chip in range(chips):
        pl.when(chip != p.chip)(lambda chip=chip: o_arrival(chip).wait_recv())
        wo_grad = wo_grad + jnp.where(chip == p.chip, 0.0, o_in[chip].astype(wide))
    wo_grad_ref[...] = wo_grad
    total = gain_mid[...]
    for b in range(1, grps):
        h_copy(b).wait_recv()
        total = total + gain_mid_in[b]
    gain_ref[...] = total

    for hop, kind in late_hops:
        if FIRST_HOPS[hop][0] < 3:
            m_first(hop, kind).wait_recv()
        m_first(hop, kind).wait_send()
    for kind in (2, 0, 1):
        for i in (0, 1):
            m_second(i, kind).wait_recv()
            m_second(i, kind).wait_send()
    for copy in early_copies:
        copy.wait()
    ob.wait_send()
    wm.wait_send()
    for i in range(1, slots):
        g_copy(i).wait_send()
    for b in range(1, grps):
        state_copy(b).wait_send()
        w_copy(b).wait_send()
        h_copy(b).wait_send()
    for chip in range(chips):
        km_copy(chip).wait_send()

        @pl.when(chip != p.chip)
        def _(chip=chip):
            q_copy(chip, 0).wait_send()
            q_copy(chip, 1).wait_send()
            kr_copy(chip).wait_send()
            o_copy(chip).wait_send()

        pl.when(chip > p.chip)(lambda chip=chip: to_right(chip).wait_send())
        pl.when(chip < p.chip)(lambda chip=chip: to_left(chip).wait_send())


def back_call(n2g, state, cotangent, tokens, gain_one, gain_two, attn, q_heads, kv_heads, mask, cosine, sine,
              qkv_all, out_full, n1_all, terms, owned, passing, early):
    chips = cosine.shape[0]
    grps = 4
    slots = 2 * chips
    shard, width = tokens.shape
    att, block = out_full.shape[0], terms.shape[1] // grps
    unit, half = att // (grps * slots), HD // 2
    vm, dma = pltpu.VMEM, pltpu.SemaphoreType.DMA
    anyspace = pl.BlockSpec(memory_space=pl.ANY)
    vspec = pl.BlockSpec(memory_space=pltpu.VMEM)
    low, wide = jnp.bfloat16, jnp.float32
    struct = jax.ShapeDtypeStruct
    return pl.pallas_call(
        functools.partial(back_kernel, chips, 1.0 / math.sqrt(HD)),
        out_shape=(
            struct((shard, width), wide),
            struct((half, width + HD), wide),
            struct((unit, width), wide),
            struct((2, 1, width), wide),
            struct((3, block, width), low),
            struct((3, block, width), low),
        ),
        in_specs=[vspec] * 13 + [anyspace] * 6,
        out_specs=(vspec,) * 4 + (anyspace,) * 2,
        scratch_shapes=[
            vm((att, width), low),
            vm((grps, shard, width), low),
            vm((chips, shard, width + HD), low),
            vm((grps, shard, slots * unit), low),
            vm((chips, 3, shard, HD), low),
            vm((chips, 3, shard, HD), low),
            vm((chips, 2, chips, shard, HD), low),
            vm((chips, chips, shard, HD), low),
            vm((chips, chips, shard, HD), low),
            vm((chips, shard, HD), wide),
            vm((chips, chips, shard, HD), low),
            vm((chips, shard, grps * HD), low),
            vm((chips, shard, width), low),
            vm((chips, shard, width), low),
            vm((chips, shard, width), low),
            vm((grps, 2, half, width + HD), wide),
            vm((grps, half, width + HD), wide),
            vm((grps, half, width + HD), low),
            vm((grps, half, width + HD), low),
            vm((chips, 2, unit, width), wide),
            vm((chips, unit, width), wide),
            vm((chips, unit, width), low),
            vm((chips, unit, width), low),
            vm((2, 3, block // 2, width), low),
            vm((2, 3, block // 2, width), low),
            vm((2, 1, width), wide),
            vm((slots, 2, 1, width), wide),
            vm((2, 1, width), wide),
            vm((grps, 2, 1, width), wide),
            vm((shard, width), wide),
            dma((3,)),
            dma((grps,)), dma((grps,)),
            dma((chips, 2)), dma((chips, 2)),
            dma((chips,)), dma((chips,)),
            dma((chips,)), dma((chips,)),
            dma((2, chips)), dma((2, chips)),
            dma, dma,
            dma((grps,)), dma((grps,)),
            dma, dma,
            dma((chips,)), dma((chips,)),
            dma((6, 3)), dma((6, 3)),
            dma((5, 3)),
            dma((slots,)), dma((slots,)),
            dma((grps,)), dma((grps,)),
        ],
        compiler_params=pltpu.CompilerParams(
            collective_id=3, has_side_effects=True, vmem_limit_bytes=62 * 2**20
        ),
        name="back",
    )(n2g, state, cotangent, tokens, gain_one, gain_two, attn, q_heads, kv_heads, mask, cosine, sine,
      qkv_all, out_full, n1_all, terms, owned, passing, early)


def columns_to_owners(rows, row_unit):
    grp_count, seq_count = lax.axis_size("grp"), lax.axis_size("seq")
    tok_rows = rows.shape[0]
    split = rows.reshape(tok_rows, grp_count, seq_count, row_unit).transpose(2, 0, 1, 3)
    split = split.reshape(seq_count * tok_rows, grp_count * row_unit)
    return lax.all_to_all(split, "seq", split_axis=0, concat_axis=0, tiled=True)


def owners_to_columns(rows, row_unit):
    grp_count, seq_count = lax.axis_size("grp"), lax.axis_size("seq")
    tok_rows = rows.shape[0] // seq_count
    moved = lax.all_to_all(rows, "seq", split_axis=0, concat_axis=0, tiled=True)
    moved = moved.reshape(seq_count, tok_rows, grp_count, row_unit).transpose(1, 2, 0, 3)
    return moved.reshape(tok_rows, grp_count * seq_count * row_unit)


def plain_mlp(normed_two, cotangent_all, mlp_weight):
    contract_last, contract_first = CONTRACT_LAST, CONTRACT_FIRST
    mlp_rows = lax.all_gather(mlp_weight, "grp", axis=0, tiled=True)
    normed_two_all = lax.all_gather(normed_two, "seq", axis=0, tiled=True)
    gate_rows, upper_rows, down_rows = mlp_rows[:, 0, :], mlp_rows[:, 1, :], mlp_rows[:, 2, :]
    gate_vals = lax.dot_general(
        normed_two_all, gate_rows, contract_last, preferred_element_type=jnp.float32
    )
    upper_vals = lax.dot_general(
        normed_two_all, upper_rows, contract_last, preferred_element_type=jnp.float32
    )
    unit_wide, pull_back = jax.vjp(swish_product, gate_vals, upper_vals)
    unit_low = unit_wide.astype(jnp.bfloat16)
    unit_grad = lax.dot_general(
        cotangent_all, down_rows, contract_last, preferred_element_type=jnp.float32
    )
    gate_grad, upper_grad = pull_back(unit_grad)
    gate_grad = gate_grad.astype(jnp.bfloat16)
    upper_grad = upper_grad.astype(jnp.bfloat16)
    input_grad = jnp.dot(gate_grad, gate_rows, preferred_element_type=jnp.float32) + jnp.dot(
        upper_grad, upper_rows, preferred_element_type=jnp.float32
    )
    grad_part = lax.psum_scatter(
        input_grad.astype(jnp.bfloat16), "seq", scatter_dimension=0, tiled=True
    ).astype(jnp.float32)
    out_part = lax.psum_scatter(
        jnp.dot(unit_low, down_rows, preferred_element_type=jnp.float32).astype(jnp.bfloat16),
        "seq",
        scatter_dimension=0,
        tiled=True,
    ).astype(jnp.float32)
    mlp_terms = jnp.stack(
        [
            lax.dot_general(
                gate_grad, normed_two_all, contract_first, preferred_element_type=jnp.float32
            ),
            lax.dot_general(
                upper_grad, normed_two_all, contract_first, preferred_element_type=jnp.float32
            ),
            lax.dot_general(
                unit_low, cotangent_all, contract_first, preferred_element_type=jnp.float32
            ),
        ],
        axis=1,
    )
    mlp_grad = lax.psum_scatter(mlp_terms, "grp", scatter_dimension=0, tiled=True)
    return grad_part, out_part, mlp_grad


def padded_rows(mlp_weight):
    rows = mlp_weight.transpose(1, 0, 2)
    return jnp.pad(rows, ((0, 0), (0, -rows.shape[1] % 32), (0, 0)))


def per_device(
    tokens,
    cotangent,
    shard_segment,
    gain_attn,
    qkv_weight,
    qkv_bias,
    out_weight,
    gain_mlp,
    mlp_weight,
):
    tok_rows = tokens.shape[0]
    seq_count = lax.axis_size("seq")
    grp_count = lax.axis_size("grp")
    group_tok = tok_rows * seq_count
    heads_per = H // KVH
    kv_width = KVH * HD
    att_width = H * HD
    query_rows = heads_per * tok_rows
    score_scale = 1.0 / math.sqrt(HD)
    contract_last = CONTRACT_LAST
    contract_first = CONTRACT_FIRST
    seq_place = lax.axis_index("seq")
    grp_place = lax.axis_index("grp")
    use_kernels = (seq_count, grp_count, H, KVH, HD) == (8, 4, 12, 2, 128)
    if use_kernels:
        freqs = THETA ** (-(jnp.arange(HD // 2, dtype=jnp.float32) * 2.0) / HD)
        freqs = jnp.concatenate([freqs, freqs])[None, :]
        gain_rows = (gain_attn[None, :], gain_mlp[None, :])
        own_rows = padded_rows(mlp_weight)
        (
            attn_wide, state, cosine, sine, mask, q_heads, kv_heads, n1_all, n2_all, cot_all, out_all,
            qkv_all, columns, *peer_rows
        ) = front_call(
            tokens, *gain_rows, shard_segment, freqs, qkv_bias[None, :], cotangent, qkv_weight, out_weight,
            own_rows,
        )
        by_slot = lambda rows: rows.reshape((seq_count,) + rows.shape[2:])
        grad_part, out_part, mlp_terms, owned, passing, early = mlp_call(
            by_slot(n2_all), by_slot(cot_all), columns, [own_rows, *peer_rows]
        )
        output = (state + out_part).astype(jnp.bfloat16)
        token_grad, qkv_terms, out_grad, gain_sums, direct, second = back_call(
            grad_part, state, cotangent, tokens, *gain_rows, attn_wide, q_heads, kv_heads, mask,
            cosine, sine, qkv_all.reshape(-1, qkv_all.shape[-1]),
            out_all.reshape(att_width, -1), n1_all, mlp_terms, owned, passing, early,
        )
        units = mlp_weight.shape[0]
        mlp_sums = sum(
            rows[:, :units].astype(jnp.float32) for rows in (mlp_terms, direct, second)
        )
        width = tokens.shape[1]
        own = width // (grp_count * seq_count)
        gain_parts = lax.dynamic_slice_in_dim(
            gain_sums[:, 0], (grp_place * seq_count + seq_place) * own, own, 1
        )
        return (
            output,
            token_grad,
            gain_parts[0],
            qkv_terms[:, :width],
            qkv_terms[:, width],
            out_grad,
            gain_parts[1],
            mlp_sums.transpose(1, 0, 2),
        )
    segments = lax.dynamic_index_in_dim(shard_segment, grp_place, 0, keepdims=False)
    starts = shard_starts(segments, tok_rows, group_tok // 2)
    shard_order = jnp.arange(seq_count, dtype=jnp.int32)
    own_seg = jnp.sum(jnp.where(shard_order == seq_place, segments, 0))
    own_start = jnp.sum(jnp.where(shard_order == seq_place, starts, 0))
    positions = own_start + jnp.arange(tok_rows, dtype=jnp.int32)
    cosine_table, sine_table = rotary_tables(positions, HD)
    query_pos = jnp.tile(positions, heads_per)
    tokens_wide = tokens.astype(jnp.float32)
    gain_one = gain_attn.astype(jnp.float32)
    gain_two = gain_mlp.astype(jnp.float32)
    normed_one = rms_scale(tokens_wide, gain_one).astype(jnp.bfloat16)
    normed_one_all = lax.all_gather(normed_one, "seq", axis=0, tiled=True)
    qkv_rows = lax.all_gather(qkv_weight, "grp", axis=0, tiled=True)
    bias_rows = lax.all_gather(qkv_bias, "grp", axis=0, tiled=True)
    cotangent_all = lax.all_gather(cotangent, "seq", axis=0, tiled=True)
    out_full = lax.all_gather(out_weight, AXES, axis=0, tiled=True)
    projected = lax.dot_general(
        normed_one_all, qkv_rows, contract_last, preferred_element_type=jnp.float32
    )
    projected = (projected + bias_rows.astype(jnp.float32)[None, :]).astype(jnp.bfloat16)
    projected = owners_to_columns(projected, qkv_weight.shape[0]).astype(jnp.float32)
    query_rot = rotate(
        projected[:, :att_width].reshape(tok_rows, H, HD), cosine_table, sine_table
    ).astype(jnp.bfloat16)
    key_rot = rotate(
        projected[:, att_width : att_width + kv_width].reshape(tok_rows, KVH, HD),
        cosine_table,
        sine_table,
    ).astype(jnp.bfloat16)
    value_low = projected[:, att_width + kv_width :].astype(jnp.bfloat16)
    keys_all, values_all = (
        lax.all_gather(key_rot.reshape(tok_rows, kv_width), "seq", axis=0, tiled=True),
        lax.all_gather(value_low, "seq", axis=0, tiled=True),
    )
    queries = (
        query_rot.reshape(tok_rows, KVH, heads_per, HD)
        .transpose(1, 2, 0, 3)
        .reshape(KVH, query_rows, HD)
    )
    key_block = min(512, group_tok)
    block_count = group_tok // key_block
    block_order = jnp.arange(block_count, dtype=jnp.int32)

    def block_mask(block_index):
        key_index = block_index * key_block + jnp.arange(key_block, dtype=jnp.int32)
        key_shard = key_index // tok_rows
        onehot = key_shard[:, None] == shard_order[None, :]
        key_seg = jnp.sum(jnp.where(onehot, segments[None, :], 0), axis=1)
        key_pos = jnp.sum(jnp.where(onehot, starts[None, :], 0), axis=1) + key_index % tok_rows
        visible = (key_seg == 0) | (key_seg == own_seg)
        return visible[None, :] & (key_pos[None, :] <= query_pos[:, None])

    def block_keys(block_index):
        key_part = lax.dynamic_slice_in_dim(
            keys_all, block_index * key_block, key_block, 0
        ).reshape(key_block, KVH, HD)
        value_part = lax.dynamic_slice_in_dim(
            values_all, block_index * key_block, key_block, 0
        ).reshape(key_block, KVH, HD)
        return (key_part, value_part)

    def block_scores(key_part):
        return (
            jnp.einsum("krd,jkd->krj", queries, key_part, preferred_element_type=jnp.float32)
            * score_scale
        )

    def stat_step(stats_now, block_index):
        allowed = block_mask(block_index)

        def stat_visit(current):
            top_old, total_old = current
            key_part, value_part = block_keys(block_index)
            scores = jnp.where(allowed[None], block_scores(key_part), -1e30)
            top_new = jnp.maximum(top_old, jnp.max(scores, axis=-1))
            weights = jnp.where(allowed[None], jnp.exp(scores - top_new[..., None]), 0.0)
            return (top_new, total_old * jnp.exp(top_old - top_new) + jnp.sum(weights, axis=-1))

        return (lax.cond(jnp.any(allowed), stat_visit, lambda current: current, stats_now), None)

    start_stats = (
        jnp.full((KVH, query_rows), -1e30, jnp.float32),
        jnp.zeros((KVH, query_rows), jnp.float32),
    )
    (top_all, total_all), unused = lax.scan(stat_step, start_stats, block_order)
    log_total = top_all + jnp.log(total_all)

    def mix_step(mixed_sum, block_index):
        allowed = block_mask(block_index)

        def mix_visit(current):
            key_part, value_part = block_keys(block_index)
            prob_low = jnp.where(
                allowed[None], jnp.exp(block_scores(key_part) - log_total[..., None]), 0.0
            ).astype(jnp.bfloat16)
            return current + jnp.einsum(
                "krj,jkd->krd", prob_low, value_part, preferred_element_type=jnp.float32
            )

        return (lax.cond(jnp.any(allowed), mix_visit, lambda current: current, mixed_sum), None)

    mixed_sum, unused = lax.scan(
        mix_step, jnp.zeros((KVH, query_rows, HD), jnp.float32), block_order
    )
    attn_wide = (
        mixed_sum.reshape(KVH, heads_per, tok_rows, HD)
        .transpose(2, 0, 1, 3)
        .reshape(tok_rows, att_width)
    )
    attn_low = attn_wide.astype(jnp.bfloat16)
    attn_proj = jnp.dot(attn_low, out_full, preferred_element_type=jnp.float32)
    state = tokens_wide + attn_proj
    normed_two = rms_scale(state, gain_two).astype(jnp.bfloat16)
    grad_part, out_part, mlp_grad = plain_mlp(normed_two, cotangent_all, mlp_weight)
    output = (state + out_part).astype(jnp.bfloat16)
    unused_state, norm_two_back = jax.vjp(rms_scale, state, gain_two)
    state_norm_grad, gain_two_grad = norm_two_back(grad_part)
    state_grad = state_norm_grad + cotangent.astype(jnp.float32)
    state_low = state_grad.astype(jnp.bfloat16)
    attn_grad = lax.dot_general(
        state_low, out_full, contract_last, preferred_element_type=jnp.float32
    )
    attn_grad_low = attn_grad.astype(jnp.bfloat16)
    attn_owned = columns_to_owners(attn_low, out_weight.shape[0])
    state_low_all = lax.all_gather(state_low, "seq", axis=0, tiled=True)
    out_grad = lax.psum_scatter(
        lax.dot_general(
            attn_owned, state_low_all, contract_first, preferred_element_type=jnp.float32
        ),
        "grp",
        scatter_dimension=0,
        tiled=True,
    )
    grad_heads = (
        attn_grad_low.reshape(tok_rows, KVH, heads_per, HD)
        .transpose(1, 2, 0, 3)
        .reshape(KVH, query_rows, HD)
    )
    delta_rows = jnp.sum(
        (attn_grad_low.astype(jnp.float32) * attn_wide).reshape(tok_rows, H, HD), axis=-1
    )
    delta_rows = (
        delta_rows.reshape(tok_rows, KVH, heads_per).transpose(1, 2, 0).reshape(KVH, query_rows)
    )

    def back_step(query_grad, block_index):
        allowed = block_mask(block_index)

        def back_visit(current):
            key_part, value_part = block_keys(block_index)
            prob_vals = jnp.where(
                allowed[None], jnp.exp(block_scores(key_part) - log_total[..., None]), 0.0
            )
            prob_grad = jnp.einsum(
                "krd,jkd->krj", grad_heads, value_part, preferred_element_type=jnp.float32
            )
            score_grad = (prob_vals * (prob_grad - delta_rows[..., None])).astype(jnp.bfloat16)
            new_grad = (
                current
                + jnp.einsum(
                    "krj,jkd->krd", score_grad, key_part, preferred_element_type=jnp.float32
                )
                * score_scale
            )
            key_grad = (
                jnp.einsum("krj,krd->jkd", score_grad, queries, preferred_element_type=jnp.float32)
                * score_scale
            )
            value_grad = jnp.einsum(
                "krj,krd->jkd",
                prob_vals.astype(jnp.bfloat16),
                grad_heads,
                preferred_element_type=jnp.float32,
            )
            return (
                new_grad,
                (key_grad.reshape(key_block, kv_width), value_grad.reshape(key_block, kv_width)),
            )

        def skip_block(current):
            blank_rows = jnp.zeros((key_block, kv_width), jnp.float32)
            return (current, (blank_rows, blank_rows))

        return lax.cond(jnp.any(allowed), back_visit, skip_block, query_grad)

    query_grad, (key_grads, value_grads) = lax.scan(
        back_step, jnp.zeros((KVH, query_rows, HD), jnp.float32), block_order
    )
    key_own, value_own = (
        lax.psum_scatter(
            key_grads.reshape(group_tok, kv_width).astype(jnp.bfloat16),
            "seq",
            scatter_dimension=0,
            tiled=True,
        ).astype(jnp.float32),
        lax.psum_scatter(
            value_grads.reshape(group_tok, kv_width).astype(jnp.bfloat16),
            "seq",
            scatter_dimension=0,
            tiled=True,
        ).astype(jnp.float32),
    )
    query_back = unrotate(
        query_grad.reshape(KVH, heads_per, tok_rows, HD)
        .transpose(2, 0, 1, 3)
        .reshape(tok_rows, H, HD),
        cosine_table,
        sine_table,
    )
    key_back = unrotate(key_own.reshape(tok_rows, KVH, HD), cosine_table, sine_table)
    qkv_grad_low = jnp.concatenate(
        [query_back.reshape(tok_rows, att_width), key_back.reshape(tok_rows, kv_width), value_own],
        axis=1,
    ).astype(jnp.bfloat16)
    qkv_grad_owned = columns_to_owners(qkv_grad_low, qkv_weight.shape[0])
    bias_terms = jnp.sum(qkv_grad_owned.astype(jnp.float32), axis=0)
    normed_one_grad = lax.psum_scatter(
        jnp.dot(qkv_grad_owned, qkv_rows, preferred_element_type=jnp.float32).astype(jnp.bfloat16),
        "seq",
        scatter_dimension=0,
        tiled=True,
    ).astype(jnp.float32)
    qkv_grad = lax.psum_scatter(
        lax.dot_general(
            qkv_grad_owned, normed_one_all, contract_first, preferred_element_type=jnp.float32
        ),
        "grp",
        scatter_dimension=0,
        tiled=True,
    )
    unused_tokens, norm_one_back = jax.vjp(rms_scale, tokens_wide, gain_one)
    token_norm_grad, gain_one_grad = norm_one_back(normed_one_grad)
    token_grad = token_norm_grad + state_grad
    bias_part = lax.psum_scatter(bias_terms, "grp", scatter_dimension=0, tiled=True)
    gain_one_part, gain_two_part = (
        lax.psum_scatter(gain_one_grad, AXES, scatter_dimension=0, tiled=True),
        lax.psum_scatter(gain_two_grad, AXES, scatter_dimension=0, tiled=True),
    )
    return (
        output,
        token_grad,
        gain_one_part,
        qkv_grad,
        bias_part,
        out_grad,
        gain_two_part,
        mlp_grad,
    )


def solution(mesh):
    return jax.shard_map(
        per_device,
        mesh=mesh,
        in_specs=(
            P(("grp", "seq"), None),
            P(("grp", "seq"), None),
            P(),
            P(),
            P(("grp", "seq"), None),
            P(("grp", "seq")),
            P(("grp", "seq"), None),
            P(),
            P(("grp", "seq"), None, None),
        ),
        out_specs=(
            P(("grp", "seq"), None),
            P(("grp", "seq"), None),
            P(("grp", "seq")),
            P(("grp", "seq"), None),
            P(("grp", "seq")),
            P(("grp", "seq"), None),
            P(("grp", "seq")),
            P(("grp", "seq"), None, None),
        ),
        check_vma=False,
    )
```

```python
import functools
import math

import jax
import jax.numpy as jnp
from jax import lax
from jax.experimental import pallas as pl
from jax.experimental.pallas import tpu as pltpu
from jax.sharding import PartitionSpec as P

H = 12
KVH = 2
HD = 128
FF = 8960


EPS = 1e-06
THETA = 10000.0


def rms_scale(values, gain_vec):
    return values * lax.rsqrt(jnp.mean(values * values, axis=-1, keepdims=True) + EPS) * gain_vec


def rotary_tables(positions, head_dim):
    half_dim = head_dim // 2
    freqs = THETA ** (-(jnp.arange(half_dim, dtype=jnp.float32) * 2.0) / head_dim)
    angles = positions.astype(jnp.float32)[:, None] * freqs[None, :]
    cosine_table = jnp.concatenate([jnp.cos(angles), jnp.cos(angles)], axis=-1)
    sine_table = jnp.concatenate([jnp.sin(angles), jnp.sin(angles)], axis=-1)
    return (cosine_table, sine_table)


def rotate(values, cosine_table, sine_table):
    half_dim = values.shape[-1] // 2
    turned = jnp.concatenate([-values[..., half_dim:], values[..., :half_dim]], axis=-1)
    return values * cosine_table[:, None, :] + turned * sine_table[:, None, :]


def unrotate(grad_rows, cosine_table, sine_table):
    half_dim = grad_rows.shape[-1] // 2
    scaled = grad_rows * sine_table[:, None, :]
    turned = jnp.concatenate([scaled[..., half_dim:], -scaled[..., :half_dim]], axis=-1)
    return grad_rows * cosine_table[:, None, :] + turned


def shard_starts(segments, tok_dev, prompt_len):
    shard_total = segments.shape[0]
    shard_order = jnp.arange(shard_total, dtype=jnp.int32)
    same_seg = segments[:, None] == segments[None, :]
    first_shard = jnp.min(jnp.where(same_seg, shard_order[None, :], shard_total), axis=1)
    cont_start = prompt_len + (shard_order - first_shard) * tok_dev
    return jnp.where(segments == 0, shard_order * tok_dev, cont_start)


def swish_product(gate_vals, upper_vals):
    return jax.nn.silu(gate_vals) * upper_vals


AXES = ("grp", "seq")
CONTRACT_LAST = (((1,), (1,)), ((), ()))
CONTRACT_FIRST = (((0,), (0,)), ((), ()))


MESH = pl.DeviceIdType.MESH


def remote(src, dst, send_sem, recv_sem, grp, seq):
    return pltpu.make_async_remote_copy(
        src_ref=src, dst_ref=dst, send_sem=send_sem, recv_sem=recv_sem,
        device_id=(grp, seq), device_id_type=MESH,
    )


def nearest_chip(place, order, chips):
    both = 2 * jnp.minimum(place, chips - 1 - place)
    offset = (order + 1) // 2
    near = jnp.where(order % 2 == 1, place - offset, place + offset)
    rest = jnp.where(place < chips - 1 - place, order, chips - 1 - order)
    return jnp.where(order <= both, near, rest)


class Place:
    def __init__(self, chips):
        self.chips = chips
        self.grp, self.seq = lax.axis_index("grp"), lax.axis_index("seq")
        self.chip, self.core = self.seq // 2, self.seq % 2
        self.mate = self.seq + 1 - 2 * self.core

    def peer(self, offset):
        low, high = self.grp % 2, self.grp // 2
        low = 1 - low if offset % 2 else low
        high = 1 - high if offset // 2 else high
        return 2 * high + low

    def barrier(self, grps):
        barrier = pltpu.get_barrier_semaphore()
        for chip in range(self.chips):
            @pl.when(chip != self.chip)
            def _(chip=chip):
                pl.semaphore_signal(
                    barrier, inc=1, device_id=(self.grp, 2 * chip + self.core), device_id_type=MESH
                )
        pl.semaphore_signal(barrier, inc=1, device_id=(self.grp, self.mate), device_id_type=MESH)
        for offset in range(1, grps):
            pl.semaphore_signal(
                barrier, inc=1, device_id=(self.peer(offset), self.seq), device_id_type=MESH
            )
        pl.semaphore_wait(barrier, self.chips - 1 + 1 + grps - 1)


class RailGather:
    def __init__(self, place, view, send_sem, recv_sem):
        self.place, self.view, self.send_sem, self.recv_sem = place, view, send_sem, recv_sem

    def copy(self, way, chip, core):
        p = self.place
        to = (p.seq + 2, p.seq - 2, p.mate)[way]
        return remote(
            self.view(chip, core), self.view(chip, core), self.send_sem.at[way, chip],
            self.recv_sem.at[chip, core], p.grp, to,
        )

    def start(self):
        p = self.place
        pl.when(p.chip < p.chips - 1)(lambda: self.copy(0, p.chip, p.core).start())
        pl.when(p.chip > 0)(lambda: self.copy(1, p.chip, p.core).start())
        self.copy(2, p.chip, p.core).start()

    def forward(self, step):
        p = self.place

        @pl.when(p.chip - step >= 0)
        def _():
            chip = p.chip - step
            self.copy(2, chip, p.core).wait_recv()
            pl.when(p.chip < p.chips - 1)(lambda: self.copy(0, chip, p.core).start())
            self.copy(2, chip, p.core).start()

        @pl.when(p.chip + step < p.chips)
        def _():
            chip = p.chip + step
            self.copy(2, chip, p.core).wait_recv()
            pl.when(p.chip > 0)(lambda: self.copy(1, chip, p.core).start())
            self.copy(2, chip, p.core).start()

    def wait_mate(self, chip):
        self.copy(2, chip, 1 - self.place.core).wait_recv()

    def drain(self):
        p = self.place
        for chip in range(p.chips):
            self.copy(2, chip, p.core).wait_send()
            pl.when((chip <= p.chip) & (p.chip < p.chips - 1))(
                lambda chip=chip: self.copy(0, chip, p.core).wait_send()
            )
            pl.when((chip >= p.chip) & (p.chip > 0))(
                lambda chip=chip: self.copy(1, chip, p.core).wait_send()
            )


class LineScatter:
    def __init__(self, place, part, mate_in, left_in, right_in, send_sem, recv_sem):
        self.place, self.part = place, part
        self.mate_in, self.left_in, self.right_in = mate_in, left_in, right_in
        self.send_sem, self.recv_sem = send_sem, recv_sem

    def copy(self, way, src, landing, r, chip, to):
        return remote(
            src, landing.at[r, chip], self.send_sem.at[way, r, chip], self.recv_sem.at[way, r, chip],
            self.place.grp, to,
        )

    def to_mate(self, r, chip):
        p = self.place
        return self.copy(0, self.part.at[r, 2 * chip + 1 - p.core], self.mate_in, r, chip, p.mate)

    def to_right(self, r, chip):
        p = self.place
        return self.copy(1, self.part.at[r, 2 * chip + p.core], self.left_in, r, chip, p.seq + 2)

    def to_left(self, r, chip):
        p = self.place
        return self.copy(2, self.part.at[r, 2 * chip + p.core], self.right_in, r, chip, p.seq - 2)

    def step(self, r, chip):
        p = self.place
        last = p.chips - 1
        slot = 2 * chip + p.core

        @pl.when(chip != p.chip)
        def _():
            self.to_mate(r, chip).wait_recv()
            total = self.part[r, slot].astype(jnp.float32) + self.mate_in[r, chip].astype(jnp.float32)
            self.part[r, slot] = total.astype(jnp.bfloat16)

        @pl.when(chip > p.chip)
        def _():
            @pl.when(p.chip > 0)
            def _():
                self.to_right(r, chip).wait_recv()
                self.part[r, slot] = (
                    self.part[r, slot].astype(jnp.float32) + self.left_in[r, chip].astype(jnp.float32)
                ).astype(jnp.bfloat16)

            self.to_right(r, chip).start()

        @pl.when(chip < p.chip)
        def _():
            @pl.when(p.chip < last)
            def _():
                self.to_left(r, chip).wait_recv()
                self.part[r, slot] = (
                    self.part[r, slot].astype(jnp.float32) + self.right_in[r, chip].astype(jnp.float32)
                ).astype(jnp.bfloat16)

            self.to_left(r, chip).start()

    def finish(self, r, out_ref):
        p = self.place
        self.to_mate(r, p.chip).wait_recv()
        out_ref[...] = self.part[r, p.seq].astype(jnp.float32) + self.mate_in[r, p.chip].astype(jnp.float32)

        @pl.when(p.chip > 0)
        def _():
            self.to_right(r, p.chip).wait_recv()
            out_ref[...] += self.left_in[r, p.chip].astype(jnp.float32)

        @pl.when(p.chip < p.chips - 1)
        def _():
            self.to_left(r, p.chip).wait_recv()
            out_ref[...] += self.right_in[r, p.chip].astype(jnp.float32)

    def drain(self, r):
        p = self.place
        for other in range(p.chips):
            self.to_mate(r, other).wait_send()
            pl.when(other > p.chip)(lambda other=other: self.to_right(r, other).wait_send())
            pl.when(other < p.chip)(lambda other=other: self.to_left(r, other).wait_send())


def front_kernel(chips, scale,
                 tokens_ref, gain_one_ref, gain_two_ref, segment_ref, freq_ref, bias_ref,
                 cot_ref, wq_ref, wo_ref, wm_ref,
                 attn_ref, state_ref, cos_ref, sin_ref, mask_ref, q_out_ref, kv_out_ref, n1_all_ref, n2_all_ref,
                 cot_all_ref, wo_all_ref, wq_all_ref, columns_ref, wm1_ref, wm2_ref, wm3_ref,
                 nbuf, n2buf, wq, wo, bias_own, bias, stage, qbuf, kvbuf, columns,
                 lsem, n_send, n_recv, n2_send, n2_recv, c_send, c_recv, o_send, o_recv, ox_send, ox_recv,
                 om_send, om_recv, wq_send, wq_recv, b_send, b_recv, m_send, m_recv, q_send, q_recv, k_send, k_recv):
    p = Place(chips)
    grps = 4
    half = wq_ref.shape[0]
    rows = pl.ds(p.core * half, half)
    mates_rows = pl.ds((1 - p.core) * half, half)
    wm_refs = (wm_ref, wm1_ref, wm2_ref, wm3_ref)
    part = wm_ref.shape[1] // 2

    own = [
        pltpu.make_async_copy(wq_ref, wq.at[0, rows], lsem.at[0]),
        pltpu.make_async_copy(wo_ref, wo.at[p.grp, p.chip, p.core], lsem.at[2]),
        pltpu.make_async_copy(cot_ref, cot_all_ref.at[p.chip, p.core], lsem.at[3]),
    ]
    for copy in own:
        copy.start()
    tokens = tokens_ref[...].astype(jnp.float32)
    nbuf[p.chip, p.core] = rms_scale(tokens, gain_one_ref[...].astype(jnp.float32)).astype(jnp.bfloat16)
    shard = tokens.shape[0]
    lane = lax.broadcasted_iota(jnp.int32, (1, 2 * half), 1)
    bias_wide = bias_ref[...].astype(jnp.float32)
    bias_pair = jnp.concatenate([bias_wide, bias_wide], axis=1)
    bias_own[...] = jnp.broadcast_to(jnp.where(lane // half == p.core, bias_pair, 0.0), bias_own.shape)
    bias[0, p.core] = bias_own[...]
    p.barrier(grps)

    n1_line = RailGather(p, lambda chip, core: nbuf.at[chip, core], n_send, n_recv)
    cot_line = RailGather(p, lambda chip, core: cot_all_ref.at[chip, core], c_send, c_recv)
    n2_line = RailGather(p, lambda chip, core: n2buf.at[chip, core], n2_send, n2_recv)
    out_line = RailGather(p, lambda chip, core: wo.at[p.grp, chip, core], o_send, o_recv)

    def wq_direct(b):
        return remote(wq_ref, wq.at[b, rows], wq_send.at[0, b], wq_recv.at[b, 0], p.peer(b), p.seq)

    def wq_mate(b):
        return remote(wq.at[b, rows], wq.at[b, rows], wq_send.at[1, b], wq_recv.at[b, 1], p.grp, p.mate)

    def bias_direct(b):
        return remote(bias_own, bias.at[b, p.core], b_send.at[0, b], b_recv.at[b, 0], p.peer(b), p.seq)

    def bias_mate(b):
        return remote(bias.at[b, p.core], bias.at[b, p.core], b_send.at[1, b], b_recv.at[b, 1], p.grp, p.mate)

    def m_part(ref, i, j):
        return ref.at[j, pl.ds(i * part, part)]

    def m_direct(b, i, j):
        return remote(
            m_part(wm_ref, i, j), m_part(wm_refs[b], i, j), m_send.at[b, i, j], m_recv.at[b, i, j],
            p.peer(b), p.seq,
        )

    def m_forward(b, j):
        return remote(
            m_part(wm_refs[b], b - 1, j), m_part(wm3_ref, b - 1, j), m_send.at[3, b - 1, j],
            m_recv.at[3, b - 1, j], p.peer(3 - b), p.seq,
        )

    def out_cross(b, chip):
        view = wo.at[p.grp, chip, p.core]
        return remote(view, view, ox_send.at[b, chip], ox_recv.at[b, chip], p.peer(b), p.seq)

    def out_arrival(b, chip):
        view = wo.at[p.peer(b), chip, p.core]
        return remote(view, view, ox_send.at[b, chip], ox_recv.at[b, chip], p.grp, p.mate)

    def out_mate(b, core):
        view = wo.at[p.peer(b), :, core]
        return remote(view, view, om_send.at[b], om_recv.at[b], p.grp, p.mate)

    def q_copy(chip):
        return remote(
            stage.at[chip, pl.ds(0, 3)], qbuf.at[p.chip], q_send.at[chip], q_recv.at[p.chip],
            p.grp, 2 * chip + p.core,
        )

    def q_arrival(chip):
        return remote(stage.at[chip, pl.ds(0, 3)], qbuf.at[chip], q_send.at[chip], q_recv.at[chip], p.grp, p.mate)

    def k_copy(chip, to_chip):
        return remote(
            stage.at[chip, 3], kvbuf.at[p.chip, p.core, chip], k_send.at[0, chip, to_chip],
            k_recv.at[p.chip, p.core, chip], p.grp, 2 * to_chip + p.core,
        )

    def k_mate(head, chip, src=None):
        view = kvbuf.at[head, p.core, chip]
        return remote(
            view if src is None else src, view, k_send.at[1, head, chip],
            k_recv.at[head, p.core, chip], p.grp, p.mate,
        )

    def k_arrival(head, core, chip):
        view = kvbuf.at[head, core, chip]
        return remote(view, view, k_send.at[1, head, chip], k_recv.at[head, core, chip], p.grp, p.mate)

    def make_tables():
        segs = [segment_ref[p.grp, t] for t in range(2 * chips)]
        starts = []
        for t in range(2 * chips):
            first = jnp.int32(t)
            for other in reversed(range(t)):
                first = jnp.where(segs[other] == segs[t], jnp.int32(other), first)
            starts.append(
                jnp.where(segs[t] == 0, jnp.int32(t * shard), chips * shard + (t - first) * shard)
            )

        def own_of(values):
            own = values[0]
            for t in range(1, 2 * chips):
                own = jnp.where(p.seq == t, values[t], own)
            return own

        own_seg, own_start = own_of(segs), own_of(starts)
        row = lax.broadcasted_iota(jnp.int32, (shard, 2 * half), 0)
        column = lax.broadcasted_iota(jnp.int32, (shard, 2 * half), 1)
        freq = freq_ref[...]
        sign = jnp.where(column < half, -1.0, 1.0)
        for chip in range(chips):
            start = jnp.where(p.core == 0, starts[2 * chip], starts[2 * chip + 1])
            angle = (start + row).astype(jnp.float32) * freq
            cos_ref[chip] = jnp.cos(angle)
            sin_ref[chip] = jnp.sin(angle) * sign
        for core in range(2):
            for chip in range(chips):
                t = 2 * chip + core
                seen = jnp.where((segs[t] == 0) | (segs[t] == own_seg), jnp.int32(1), jnp.int32(0))
                allowed = (starts[t] + column <= own_start + row) & (row * 0 + seen > 0)
                block = core * chips + chip
                mask_ref[:, block * shard : (block + 1) * shard] = jnp.where(allowed, 0.0, -1e30)

    own[0].wait()
    for b in range(1, grps):
        wq_direct(b).start()
        bias_direct(b).start()
    wq_mate(0).start()
    bias_mate(0).start()
    n1_line.start()
    own[1].wait()
    out_line.start()
    for b in range(1, grps):
        wq_direct(b).wait_recv()
        wq_mate(b).start()
        bias_direct(b).wait_recv()
        bias_mate(b).start()
    for b in range(1, grps):
        out_cross(b, p.chip).start()
    for j in range(3):
        m_direct(1, 0, j).start()
        m_direct(2, 1, j).start()
    make_tables()
    for b in range(grps):
        wq_mate(b).wait_recv()
        bias_mate(b).wait_recv()

    @pl.loop(0, chips)
    def _(order):
        @pl.when(order > 0)
        def _():
            n1_line.forward(order)
            out_line.forward(order)
            for b in range(1, grps):
                pl.when(p.chip - order >= 0)(lambda b=b: out_cross(b, p.chip - order).start())
                pl.when(p.chip + order < chips)(lambda b=b: out_cross(b, p.chip + order).start())

        at = nearest_chip(p.chip, order, chips)
        x = nbuf[at, p.core]
        weights = wq[...].reshape(grps * 2 * half, x.shape[1])
        rows_all = lax.dot_general(x, weights, CONTRACT_LAST, preferred_element_type=jnp.float32)
        cosine, sine = cos_ref[at], sin_ref[at]
        for b in range(grps):
            u = rows_all[:, 2 * half * b : 2 * half * (b + 1)] + (bias[b, 0, 0:1] + bias[b, 1, 0:1])
            turned = u * cosine + pltpu.roll(u, half, 1) * sine
            place = p.peer(b)
            keep = jnp.where((place == grps - 1) & (p.chip >= chips // 2), 1.0, 0.0)
            value = (u * keep + turned * (1.0 - keep)).astype(jnp.bfloat16)
            stage[at, place] = value

            @pl.when(place == grps - 1)
            def _(value=value):
                kvbuf[p.chip, p.core, at] = value

            @pl.when((place < grps - 1) & (at == p.chip))
            def _(value=value, place=place):
                qbuf[p.chip, place] = value

        pl.when(at != p.chip)(lambda: q_copy(at).start())
        for to_chip in range(chips):
            pl.when(to_chip != p.chip)(lambda to_chip=to_chip: k_copy(at, to_chip).start())
        k_mate(p.chip, at, stage.at[at, 3]).start()


    @pl.loop(0, chips)
    def _(order):
        for head in range(chips):
            @pl.when(head != p.chip)
            def _(head=head):
                chip = nearest_chip(head, order, chips)
                k_arrival(head, p.core, chip).wait_recv()
                k_mate(head, chip).start()

    for chip in range(chips):
        pl.when(chip != p.chip)(lambda chip=chip: q_arrival(chip).wait_recv())
        for head in range(chips):
            k_arrival(head, 1 - p.core, chip).wait_recv()
    own[2].wait()
    cot_line.start()
    for j in (0, 1):
        for b in (1, 2):
            m_direct(b, b - 1, j).wait_recv()
            m_forward(b, j).start()
    for j in range(3):
        m_direct(1, 1, j).start()
        m_direct(2, 0, j).start()

    mask = mask_ref[...]
    heads_per = H // KVH
    for kv in range(KVH):
        heads = [kv * heads_per + i for i in range(heads_per)]
        queries = jnp.concatenate([qbuf[h % chips, h // chips] for h in heads], axis=0)
        keys = kvbuf[kv].reshape(mask.shape[1], 2 * half)
        values = kvbuf[KVH + kv].reshape(mask.shape[1], 2 * half)
        scores = lax.dot_general(queries, keys, CONTRACT_LAST, preferred_element_type=jnp.float32) * scale
        scores = scores.reshape(heads_per, shard, mask.shape[1]) + mask[None]
        weights = jnp.exp(scores - jnp.max(scores, axis=-1, keepdims=True))
        inverse = 1.0 / jnp.sum(weights, axis=-1, keepdims=True)
        probs = (weights * inverse).astype(jnp.bfloat16).reshape(heads_per * shard, mask.shape[1])
        mixed = jnp.dot(probs, values, preferred_element_type=jnp.float32)
        for i, h in enumerate(heads):
            attn_ref[:, h * 2 * half : (h + 1) * 2 * half] = mixed[i * shard : (i + 1) * shard]
        cot_line.forward(kv + 1)

    for b in range(1, grps):
        for chip in range(chips):
            out_arrival(b, chip).wait_recv()
        out_mate(b, p.core).start()
    for b in (1, 2):
        m_direct(b, b - 1, 2).wait_recv()
        m_forward(b, 2).start()
    attn_low = attn_ref[...].astype(jnp.bfloat16)
    unit = wo.shape[3]
    for owner in range(grps):
        columns[owner] = attn_low[:, owner * columns.shape[2] : (owner + 1) * columns.shape[2]]
    for b in range(1, grps):
        out_mate(b, 1 - p.core).wait_recv()
    for chip in range(chips):
        out_line.wait_mate(chip)
    state = tokens_ref[...].astype(jnp.float32) + jnp.dot(
        attn_low, wo[...].reshape(grps * chips * 2 * unit, tokens_ref.shape[1]),
        preferred_element_type=jnp.float32,
    )
    state_ref[...] = state
    n2buf[p.chip, p.core] = rms_scale(state, gain_two_ref[...].astype(jnp.float32)).astype(jnp.bfloat16)
    n2_line.start()
    cot_line.forward(3)
    outs = [
        pltpu.make_async_copy(nbuf, n1_all_ref, lsem.at[4]),
        pltpu.make_async_copy(wq, wq_all_ref, lsem.at[5]),
        pltpu.make_async_copy(qbuf, q_out_ref, lsem.at[6]),
        pltpu.make_async_copy(kvbuf, kv_out_ref, lsem.at[7]),
        pltpu.make_async_copy(wo, wo_all_ref, lsem.at[8]),
        pltpu.make_async_copy(columns, columns_ref, lsem.at[9]),
    ]
    for chip in range(chips):
        n1_line.wait_mate(chip)
    for copy in outs:
        copy.start()
    for step in range(1, chips):
        n2_line.forward(step)
    for chip in range(chips):
        cot_line.wait_mate(chip)
        n2_line.wait_mate(chip)
    last = pltpu.make_async_copy(n2buf, n2_all_ref, lsem.at[10])
    last.start()
    for b in (1, 2):
        for j in range(3):
            m_direct(b, 2 - b, j).wait_recv()
            m_forward(3 - b, j).wait_recv()
    for copy in outs:
        copy.wait()
    last.wait()
    n1_line.drain()
    n2_line.drain()
    out_line.drain()
    cot_line.drain()
    for b in range(grps):
        wq_mate(b).wait_send()
        bias_mate(b).wait_send()
    for b in range(1, grps):
        wq_direct(b).wait_send()
        bias_direct(b).wait_send()
        out_mate(b, p.core).wait_send()
        for chip in range(chips):
            out_cross(b, chip).wait_send()
    for b in (1, 2):
        for i in (0, 1):
            for j in range(3):
                m_direct(b, i, j).wait_send()
        for j in range(3):
            m_forward(b, j).wait_send()
    for chip in range(chips):
        pl.when(chip != p.chip)(lambda chip=chip: q_copy(chip).wait_send())
        for other in range(chips):
            pl.when(other != p.chip)(lambda chip=chip, other=other: k_copy(chip, other).wait_send())
            k_mate(other, chip).wait_send()


def front_call(tokens, gain_one, gain_two, segments, freqs, bias, cot, qkv_weight, out_weight, mlp_rows):
    chips = segments.shape[1] // 2
    grps = 4
    shard, width = tokens.shape
    half = qkv_weight.shape[0]
    vm, dma = pltpu.VMEM, pltpu.SemaphoreType.DMA
    anyspace = pl.BlockSpec(memory_space=pl.ANY)
    vspec = pl.BlockSpec(memory_space=pltpu.VMEM)
    low, wide = jnp.bfloat16, jnp.float32
    struct = jax.ShapeDtypeStruct
    wo_shape = (grps, chips, 2) + out_weight.shape
    columns_shape = (grps, shard, H * HD // grps)
    return pl.pallas_call(
        functools.partial(front_kernel, chips, 1.0 / math.sqrt(HD)),
        out_shape=(
            struct((shard, H * HD), wide),
            struct((shard, width), wide),
            struct((chips, shard, HD), wide),
            struct((chips, shard, HD), wide),
            struct((shard, 2 * chips * shard), wide),
            struct((chips, 3, shard, HD), low),
            struct((chips, 2, chips, shard, HD), low),
            struct((chips, 2, shard, width), low),
            struct((chips, 2, shard, width), low),
            struct((chips, 2, shard, width), low),
            struct(wo_shape, low),
            struct((grps, 2 * half, width), low),
            struct(columns_shape, low),
        ) + (struct(mlp_rows.shape, low),) * 3,
        in_specs=[vspec] * 3
        + [pl.BlockSpec(memory_space=pltpu.SMEM)]
        + [vspec] * 2
        + [anyspace] * 4,
        out_specs=(vspec,) * 5 + (anyspace,) * 11,
        scratch_shapes=[
            vm((chips, 2, shard, width), low),
            vm((chips, 2, shard, width), low),
            vm((grps, 2 * half, width), low),
            vm(wo_shape, low),
            vm((8, HD), wide),
            vm((grps, 2, 8, HD), wide),
            vm((chips, grps, shard, HD), low),
            vm((chips, 3, shard, HD), low),
            vm((chips, 2, chips, shard, HD), low),
            vm(columns_shape, low),
            dma((11,)),
            dma((3, chips)), dma((chips, 2)),
            dma((3, chips)), dma((chips, 2)),
            dma((3, chips)), dma((chips, 2)),
            dma((3, chips)), dma((chips, 2)),
            dma((grps, chips)), dma((grps, chips)), dma((grps,)), dma((grps,)),
            dma((2, grps)), dma((grps, 2)),
            dma((2, grps)), dma((grps, 2)),
            dma((grps, 2, 3)), dma((grps, 2, 3)),
            dma((chips,)), dma((chips,)),
            dma((2, chips, chips)), dma((chips, 2, chips)),
        ],
        compiler_params=pltpu.CompilerParams(
            collective_id=2, has_side_effects=True, vmem_limit_bytes=60 * 2**20
        ),
        name="front",
    )(tokens, gain_one, gain_two, segments, freqs, bias, cot, qkv_weight, out_weight, mlp_rows)


FIRST_HOPS = ((1, 0, 1), (3, 0, 1), (2, 1, 2), (3, 1, 2))
EARLY_HOPS = tuple((hop, kind) for kind in (2, 0) for hop in (1, 3, 0, 2))


def mlp_kernel(chips, grps, row_tiles, n2_ref, cot_ref, columns_ref, *refs):
    w_refs, refs = refs[:grps], refs[grps:]
    (
        n2g_ref, outp_ref, grads_ref, owned_ref, passing_ref, arrived_ref, tok, w, acts, part, mate_in, left_in, right_in, stage,
        lsem, ssend, srecv, wsem, osem, a_send, a_recv, e_send, e_recv,
    ) = refs
    p = Place(chips)
    shard, width = n2_ref.shape[1:]
    units = w.shape[1]
    block = units // grps
    tile = units // row_tiles
    loads = [
        pltpu.make_async_copy(n2_ref, tok.at[0], lsem.at[0]),
        pltpu.make_async_copy(cot_ref, tok.at[1], lsem.at[1]),
        pltpu.make_async_copy(columns_ref.at[p.grp], owned_ref.at[0], lsem.at[2]),
    ]
    for copy in loads:
        copy.start()

    def w_copy(j, b):
        return pltpu.make_async_copy(w_refs[b].at[j], w.at[j, pl.ds(b * block, block)], wsem.at[j, b])

    for j in range(3):
        for b in range(grps):
            w_copy(j, b).start()

    barrier = pltpu.get_barrier_semaphore()
    inner = jnp.where((p.chip > 0) & (p.chip < chips - 1), 1, 0)

    def greet(grp, seq):
        pl.semaphore_signal(barrier, inc=1, device_id=(grp, seq), device_id_type=MESH)

    greet(p.grp, p.mate)
    pl.when(p.chip > 0)(lambda: greet(p.grp, p.seq - 2))
    pl.when(p.chip < chips - 1)(lambda: greet(p.grp, p.seq + 2))
    for b in range(1, grps):
        greet(p.peer(b), p.seq)
    pl.semaphore_wait(barrier, 2 + inner + grps - 1)
    scatter = LineScatter(p, part, mate_in, left_in, right_in, ssend, srecv)

    def a_copy(b):
        return remote(
            columns_ref.at[p.peer(b)], owned_ref.at[b], a_send.at[b], a_recv.at[b], p.peer(b), p.seq
        )

    for b in range(1, grps):
        a_copy(b).start()
    for copy in loads:
        copy.wait()
    for j in range(3):
        for b in range(grps):
            w_copy(j, b).wait()

    def kind_of(t):
        return (t // row_tiles + 2) % 3

    def early(slot, kind):
        b, i, to = FIRST_HOPS[slot]
        half = block // 2
        rows = grads_ref.at[kind, pl.ds(b * block + i * half, half)]
        land = arrived_ref.at[kind // 2, pl.ds(i * half, half)] if b < 3 else passing_ref.at[i, kind]
        at = EARLY_HOPS.index((slot, kind))
        return remote(rows, land, e_send.at[at], e_recv.at[at], p.peer(to), p.seq)

    def out_copy(t):
        return pltpu.make_async_copy(
            stage.at[t % 2],
            grads_ref.at[kind_of(t), pl.ds((t % row_tiles) * tile, tile)],
            osem.at[t % 2],
        )

    def tile_grad(t):
        kind = kind_of(t)
        lhs = acts[kind, :, pl.ds(pl.multiple_of((t % row_tiles) * tile, 128), tile)]
        rhs = tok[kind // 2].reshape(2 * chips * shard, width)
        stage[t % 2] = lax.dot_general(
            lhs, rhs, CONTRACT_FIRST, preferred_element_type=jnp.float32
        ).astype(jnp.bfloat16)
        out_copy(t).start()

    def start_early(kind):
        for hop in EARLY_HOPS:
            if hop[1] == kind:
                early(*hop).start()

    def far_chip(order):
        return nearest_chip(p.chip, chips - 1 - order, chips)

    @pl.loop(0, chips + 1)
    def _(order):
        @pl.when(order < chips)
        def _():
            at = far_chip(order)
            x = tok[0, pl.ds(2 * at, 2)].reshape(2 * shard, width)
            gate = lax.dot_general(x, w[0], CONTRACT_LAST, preferred_element_type=jnp.float32)
            up = lax.dot_general(x, w[1], CONTRACT_LAST, preferred_element_type=jnp.float32)
            sig = 1.0 / (1.0 + jnp.exp(-gate))
            silu = gate * sig
            rows = pl.ds(at * (2 * shard), 2 * shard)
            acts[0, rows] = (up * sig * (1.0 + gate * (1.0 - sig))).astype(jnp.bfloat16)
            acts[1, rows] = silu.astype(jnp.bfloat16)
            hidden = (silu * up).astype(jnp.bfloat16)
            acts[2, rows] = hidden
            part[1, pl.ds(2 * at, 2)] = (
                jnp.dot(hidden, w[2], preferred_element_type=jnp.float32)
                .astype(jnp.bfloat16).reshape(2, shard, width)
            )
            scatter.to_mate(1, at).start()

        pl.when(order > 0)(lambda: scatter.step(1, far_chip(order - 1)))

    @pl.loop(0, row_tiles)
    def _(t):
        pl.when(t >= 2)(lambda: out_copy(t - 2).wait())
        tile_grad(t)

    @pl.loop(0, chips)
    def _(order):
        at = far_chip(order)
        y = tok[1, pl.ds(2 * at, 2)].reshape(2 * shard, width)
        unit_grad = lax.dot_general(y, w[2], CONTRACT_LAST, preferred_element_type=jnp.float32)
        rows = pl.ds(at * (2 * shard), 2 * shard)
        acts[0, rows] = (unit_grad * acts[0, rows].astype(jnp.float32)).astype(jnp.bfloat16)
        acts[1, rows] = (unit_grad * acts[1, rows].astype(jnp.float32)).astype(jnp.bfloat16)

        @pl.when(order == 0)
        def _():
            out_copy(row_tiles - 2).wait()
            out_copy(row_tiles - 1).wait()
            start_early(2)

    @pl.loop(0, chips + 1)
    def _(order):
        @pl.when(order < chips)
        def _():
            at = far_chip(order)
            rows = pl.ds(at * (2 * shard), 2 * shard)
            back = jnp.dot(acts[0, rows], w[0], preferred_element_type=jnp.float32) + jnp.dot(
                acts[1, rows], w[1], preferred_element_type=jnp.float32
            )
            part[0, pl.ds(2 * at, 2)] = back.astype(jnp.bfloat16).reshape(2, shard, width)
            scatter.to_mate(0, at).start()

        @pl.when(order < row_tiles)
        def _():
            t = row_tiles + order
            pl.when(order >= 2)(lambda: out_copy(t - 2).wait())
            tile_grad(t)

        @pl.when(order == row_tiles)
        def _():
            out_copy(2 * row_tiles - 2).wait()
            out_copy(2 * row_tiles - 1).wait()
            start_early(0)

        pl.when(order > 0)(lambda: scatter.step(0, far_chip(order - 1)))

    @pl.loop(2 * row_tiles, 3 * row_tiles)
    def _(t):
        pl.when(t >= 2 * row_tiles + 2)(lambda: out_copy(t - 2).wait())
        tile_grad(t)

    scatter.finish(0, n2g_ref)
    scatter.finish(1, outp_ref)
    out_copy(3 * row_tiles - 2).wait()
    out_copy(3 * row_tiles - 1).wait()
    for hop in EARLY_HOPS:
        early(*hop).wait_recv()
        early(*hop).wait_send()
    scatter.drain(0)
    scatter.drain(1)
    for b in range(1, grps):
        a_copy(b).wait_recv()
        a_copy(b).wait_send()


def mlp_call(n2_all, cot_all, columns, w_blocks, row_tiles=3):
    grps, (_, block, width) = len(w_blocks), w_blocks[0].shape
    slots, shard, _ = cot_all.shape
    chips = slots // 2
    units = grps * block
    vm, anyspace = pltpu.VMEM, pl.BlockSpec(memory_space=pl.ANY)
    vspec = pl.BlockSpec(memory_space=pltpu.VMEM)
    dma = pltpu.SemaphoreType.DMA
    return pl.pallas_call(
        functools.partial(mlp_kernel, chips, grps, row_tiles),
        out_shape=(
            jax.ShapeDtypeStruct((shard, width), jnp.float32),
            jax.ShapeDtypeStruct((shard, width), jnp.float32),
            jax.ShapeDtypeStruct((3, units, width), jnp.bfloat16),
            jax.ShapeDtypeStruct(columns.shape, jnp.bfloat16),
            jax.ShapeDtypeStruct((2, 3, block // 2, width), jnp.bfloat16),
            jax.ShapeDtypeStruct((2, block, width), jnp.bfloat16),
        ),
        in_specs=[anyspace] * (3 + grps),
        out_specs=(vspec, vspec) + (anyspace,) * 4,
        scratch_shapes=[
            vm((2, slots, shard, width), jnp.bfloat16),
            vm((3, units, width), jnp.bfloat16),
            vm((3, slots * shard, units), jnp.bfloat16),
            vm((2, slots, shard, width), jnp.bfloat16),
            vm((2, chips, shard, width), jnp.bfloat16),
            vm((2, chips, shard, width), jnp.bfloat16),
            vm((2, chips, shard, width), jnp.bfloat16),
            vm((2, units // row_tiles, width), jnp.bfloat16),
            dma((3,)), dma((3, 2, chips)), dma((3, 2, chips)),
            dma((3, grps)), dma((2,)), dma((grps,)), dma((grps,)),
            dma((len(EARLY_HOPS),)), dma((len(EARLY_HOPS),)),
        ],
        compiler_params=pltpu.CompilerParams(
            collective_id=1, has_side_effects=True, vmem_limit_bytes=62 * 2**20
        ),
        name="mlp",
    )(n2_all, cot_all, columns, *w_blocks)


def unturn(rows, cosine, sine, half):
    return rows * cosine + pltpu.roll(rows * sine, half, 1)


def back_kernel(chips, scale,
                n2g_ref, state_ref, cot_ref, tokens_ref, gain_one_ref, gain_two_ref, attn_ref, q_ref, kv_ref,
                mask_ref, cos_ref, sin_ref, wq_ref, wo_ref, n1_ref, terms_ref, owned_ref, passing_ref, early_ref,
                tok_grad_ref, wq_grad_ref, wo_grad_ref, gain_ref, direct_ref, second_ref,
                wo, stbuf, n1x, at_all, dq_stage, gq_in, kv_part, km_in, k_sum, k_own, kr_in,
                cols, part, left_in, right_in, wgrad, wm_in, w_send_buf, w_in, o_terms, ob_in, o_send_buf, o_in,
                m_own, m_in, early_rows, gain_own, gain_in, gain_mid, gain_mid_in, state_grad,
                lsem, s_send, s_recv, q_send, q_recv, km_send, km_recv, kr_send, kr_recv,
                r_send, r_recv, wm_send, wm_recv, w_send, w_recv, ob_send, ob_recv, o_send, o_recv, m_send, m_recv,
                ml_sem, g_send, g_recv, h_send, h_recv):
    p = Place(chips)
    grps = 4
    shard, width = n2g_ref.shape
    slots = 2 * chips
    heads_per = H // KVH
    half = HD // 2
    low, wide = jnp.bfloat16, jnp.float32
    block = terms_ref.shape[1] // grps
    mhalf = block // 2
    last = chips - 1

    loads = [
        pltpu.make_async_copy(wo_ref, wo, lsem.at[0]),
        pltpu.make_async_copy(n1_ref.at[:, p.core], n1x.at[:, :, pl.ds(0, width)], lsem.at[1]),
        pltpu.make_async_copy(owned_ref, at_all, lsem.at[2]),
    ]
    for copy in loads:
        copy.start()

    def seq_peer(i):
        return (p.seq + i) % slots

    barrier = pltpu.get_barrier_semaphore()
    for i in range(1, slots):
        pl.semaphore_signal(barrier, inc=1, device_id=(p.grp, seq_peer(i)), device_id_type=MESH)
    for b in range(1, grps):
        pl.semaphore_signal(barrier, inc=1, device_id=(p.peer(b), p.seq), device_id_type=MESH)
    pl.semaphore_wait(barrier, slots - 1 + grps - 1)

    def m_rows(b, i, kind):
        return terms_ref.at[kind, pl.ds(b * block + i * mhalf, mhalf)]

    def m_first(hop, kind):
        b, i, to = FIRST_HOPS[hop]
        land = direct_ref.at[kind, pl.ds(i * mhalf, mhalf)] if b < 3 else m_in.at[i, kind]
        return remote(
            m_rows(b, i, kind), land, m_send.at[hop, kind], m_recv.at[hop, kind], p.peer(to), p.seq
        )

    def m_second(i, kind):
        return remote(
            m_own.at[i, kind], second_ref.at[kind, pl.ds(i * mhalf, mhalf)], m_send.at[4 + i, kind],
            m_recv.at[4 + i, kind], p.peer(2 - i), p.seq,
        )

    late_hops = [(hop, kind) for kind in (1, 0, 2) for hop in (1, 3, 0, 2) if (hop, kind) not in EARLY_HOPS]
    for hop in late_hops:
        m_first(*hop).start()
    m_loads = [
        pltpu.make_async_copy(m_rows(2 - i, i, kind), m_own.at[i, kind], ml_sem.at[i, kind])
        for i in (0, 1)
        for kind in range(3)
    ]
    for hop, kind in EARLY_HOPS:
        if FIRST_HOPS[hop][0] == 3:
            i = FIRST_HOPS[hop][1]
            m_loads.append(pltpu.make_async_copy(passing_ref.at[i, kind], m_in.at[i, kind], ml_sem.at[2 + i, kind]))
    early_kinds = [kind for kind in (0, 2) if (0, kind) in EARLY_HOPS]
    early_loads = [
        pltpu.make_async_copy(early_ref.at[kind // 2], early_rows.at[kind // 2], ml_sem.at[4, kind])
        for kind in early_kinds
    ]
    early_copies = [
        pltpu.make_async_copy(early_rows.at[kind // 2], direct_ref.at[kind], ml_sem.at[4, kind])
        for kind in early_kinds
    ]
    m_loads += early_loads
    for copy in m_loads:
        copy.start()

    def m_turn(kind):
        for i in (0, 1):
            if (1 + 2 * i, kind) in late_hops:
                m_first(1 + 2 * i, kind).wait_recv()

            @pl.loop(0, mhalf // 16)
            def _(t, i=i):
                rows = pl.ds(pl.multiple_of(t * 16, 16), 16)
                m_own[i, kind, rows] = (
                    m_own[i, kind, rows].astype(wide) + m_in[i, kind, rows].astype(wide)
                ).astype(low)

            m_second(i, kind).start()

    state = state_ref[...]
    gain_two = gain_two_ref[...].astype(wide)
    n2g = n2g_ref[...]
    scale_two = lax.rsqrt(jnp.mean(state * state, axis=-1, keepdims=True) + EPS)
    normed = state * scale_two
    gain_own[1] = jnp.sum(n2g * normed, axis=0, keepdims=True)
    lifted = n2g * gain_two
    state_grad[...] = cot_ref[...].astype(wide) + scale_two * (
        lifted - normed * jnp.mean(lifted * normed, axis=-1, keepdims=True)
    )
    state_low = state_grad[...].astype(low)
    stbuf[0] = state_low

    def state_copy(b):
        return remote(stbuf.at[0], stbuf.at[b], s_send.at[b], s_recv.at[b], p.peer(b), p.seq)

    attn = attn_ref[...]
    unit = wo.shape[0] // (grps * slots)
    loads[0].wait()
    attn_grad = lax.dot_general(state_low, wo[...], CONTRACT_LAST, preferred_element_type=wide).astype(low)
    mask = mask_ref[...]
    keys_total = mask.shape[1]
    own_cos, own_sin = cos_ref[p.chip], sin_ref[p.chip]

    def km_copy(head):
        return remote(
            kv_part.at[head, 1 - p.core], km_in.at[head], km_send.at[head], km_recv.at[head], p.grp, p.mate
        )

    def kr_copy(head):
        return remote(
            k_sum.at[head], kr_in.at[p.chip], kr_send.at[head], kr_recv.at[p.chip], p.grp, 2 * head + p.core
        )

    def kr_arrival(chip):
        return remote(k_sum.at[chip], kr_in.at[chip], kr_send.at[chip], kr_recv.at[chip], p.grp, p.mate)

    q_parts = (pl.ds(0, 1), pl.ds(1, 2))

    def q_copy(chip, i):
        return remote(
            dq_stage.at[chip, q_parts[i]], gq_in.at[p.chip, q_parts[i]], q_send.at[chip, i],
            q_recv.at[p.chip, i], p.grp, 2 * chip + p.core,
        )

    def q_arrival(chip, i):
        return remote(
            dq_stage.at[chip, q_parts[i]], gq_in.at[chip, q_parts[i]], q_send.at[chip, i],
            q_recv.at[chip, i], p.grp, p.mate,
        )

    def key_sum(head):
        km_copy(head).wait_recv()
        total = kv_part[head, p.core].astype(wide) + km_in[head].astype(wide)

        @pl.when(p.chip == head)
        def _():
            k_own[...] = total

        @pl.when(p.chip != head)
        def _():
            k_sum[head] = total.astype(low)
            kr_copy(head).start()

    for kv in range(KVH):
        heads = [kv * heads_per + i for i in range(heads_per)]
        queries = jnp.concatenate([q_ref[h % chips, h // chips] for h in heads], axis=0)
        grads = jnp.concatenate([attn_grad[:, h * HD : (h + 1) * HD] for h in heads], axis=0)
        mixed = jnp.concatenate([attn[:, h * HD : (h + 1) * HD] for h in heads], axis=0)
        delta = jnp.sum(grads.astype(wide) * mixed, axis=-1, keepdims=True)
        keys = kv_ref[kv].reshape(keys_total, HD)
        values = kv_ref[KVH + kv].reshape(keys_total, HD)
        scores = lax.dot_general(queries, keys, CONTRACT_LAST, preferred_element_type=wide) * scale
        scores = (scores.reshape(heads_per, shard, keys_total) + mask[None]).reshape(heads_per * shard, keys_total)
        weights = jnp.exp(scores - jnp.max(scores, axis=-1, keepdims=True))
        probs = weights * (1.0 / jnp.sum(weights, axis=-1, keepdims=True))
        prob_grad = lax.dot_general(grads, values, CONTRACT_LAST, preferred_element_type=wide)
        score_grad = (probs * (prob_grad - delta)).astype(low)
        key_grad = lax.dot_general(score_grad, queries, CONTRACT_FIRST, preferred_element_type=wide) * scale
        value_grad = lax.dot_general(probs.astype(low), grads, CONTRACT_FIRST, preferred_element_type=wide)
        kv_part[kv] = key_grad.astype(low).reshape(2, chips, shard, HD)
        kv_part[KVH + kv] = value_grad.astype(low).reshape(2, chips, shard, HD)
        km_copy(kv).start()
        km_copy(KVH + kv).start()
        query_grad = jnp.dot(score_grad, keys, preferred_element_type=wide) * scale
        for i, h in enumerate(heads):
            turned = unturn(query_grad[i * shard : (i + 1) * shard], own_cos, own_sin, half).astype(low)
            dq_stage[h % chips, h // chips] = turned

            @pl.when(p.chip == h % chips)
            def _(turned=turned, h=h):
                gq_in[h % chips, h // chips] = turned

        for chip in range(chips):
            pl.when(chip != p.chip)(lambda chip=chip: q_copy(chip, kv).start())
        if kv == 0:
            for copy in m_loads:
                copy.wait()
            for copy in early_copies:
                copy.start()
            m_turn(2)
            m_turn(0)
            for b in range(1, grps):
                state_copy(b).start()
            key_sum(0)
            key_sum(KVH)
    key_sum(1)
    key_sum(KVH + 1)
    m_turn(1)
    loads[1].wait()
    lane = lax.broadcasted_iota(jnp.int32, (chips, shard, HD), 2)
    n1x[:, :, width:] = jnp.where(lane == 0, 1.0, 0.0).astype(low)

    for chip in range(chips):
        for i in (0, 1):
            pl.when(chip != p.chip)(lambda chip=chip, i=i: q_arrival(chip, i).wait_recv())
        pl.when(chip != p.chip)(lambda chip=chip: kr_arrival(chip).wait_recv())
    is_value = jnp.where(p.chip >= chips // 2, 1.0, 0.0)

    gain_one = gain_one_ref[...].astype(wide)
    gain_own[0] = jnp.zeros_like(gain_own[0])

    def to_right(chip):
        return remote(part.at[chip], left_in.at[chip], r_send.at[0, chip], r_recv.at[0, chip], p.grp, p.seq + 2)

    def to_left(chip):
        return remote(part.at[chip], right_in.at[chip], r_send.at[1, chip], r_recv.at[1, chip], p.grp, p.seq - 2)

    @pl.loop(0, chips)
    def _(order):
        chip = nearest_chip(p.chip, last - order, chips)
        key_total = k_own[chip]
        for other in range(chips):
            key_total = key_total + jnp.where(other == p.chip, 0.0, kr_in[other, chip].astype(wide))
        turned = unturn(key_total, cos_ref[chip], sin_ref[chip], half)
        last_head = (key_total * is_value + turned * (1.0 - is_value)).astype(low)
        for b in range(grps):
            place = p.peer(b)
            query_head = gq_in[chip, jnp.minimum(place, grps - 2)]
            cols[chip, :, b * HD : (b + 1) * HD] = jnp.where(place == grps - 1, last_head, query_head)
        terms = jnp.dot(cols[chip], wq_ref[...], preferred_element_type=wide)
        part[chip] = terms.astype(low)
        gain_own[0] += jnp.sum(terms * n1x[chip, :, 0:width].astype(wide), axis=0, keepdims=True)
        pl.when((p.chip == 0) & (chip > 0))(lambda: to_right(chip).start())
        pl.when((p.chip == last) & (chip < last))(lambda: to_left(chip).start())

    gain_own[0] = gain_own[0] / gain_one

    def g_copy(i):
        return remote(gain_own, gain_in.at[i], g_send.at[i], g_recv.at[i], p.grp, seq_peer(i))

    def h_copy(b):
        return remote(gain_mid, gain_mid_in.at[b], h_send.at[b], h_recv.at[b], p.peer(b), p.seq)

    for i in range(1, slots):
        g_copy(i).start()

    def rail_step(order):
        far = last - order

        @pl.when((far > p.chip) & (p.chip > 0))
        def _():
            to_right(far).wait_recv()
            part[far] = (part[far].astype(wide) + left_in[far].astype(wide)).astype(low)
            to_right(far).start()

        @pl.when((order < p.chip) & (p.chip < last))
        def _():
            to_left(order).wait_recv()
            part[order] = (part[order].astype(wide) + right_in[order].astype(wide)).astype(low)
            to_left(order).start()

    rail_step(0)
    wgrad[...] = lax.dot_general(
        cols[...].reshape(chips * shard, grps * HD), n1x[...].reshape(chips * shard, width + HD),
        CONTRACT_FIRST, preferred_element_type=wide,
    ).reshape(grps, 2, half, width + HD)
    wm = remote(wgrad.at[:, 1 - p.core], wm_in, wm_send, wm_recv, p.grp, p.mate)
    wm.start()
    rail_step(1)
    wm.wait_recv()
    w_send_buf[...] = (wgrad[:, p.core] + wm_in[...]).astype(low)

    def w_copy(b):
        return remote(w_send_buf.at[b], w_in.at[b], w_send.at[b], w_recv.at[b], p.peer(b), p.seq)

    for b in range(1, grps):
        w_copy(b).start()
    rail_step(2)
    loads[2].wait()
    for b in range(1, grps):
        state_copy(b).wait_recv()
    o_terms[...] = lax.dot_general(
        at_all[...].reshape(grps * shard, slots * unit), stbuf[...].reshape(grps * shard, width),
        CONTRACT_FIRST, preferred_element_type=wide,
    ).reshape(chips, 2, unit, width)
    ob = remote(o_terms.at[:, 1 - p.core], ob_in, ob_send, ob_recv, p.grp, p.mate)
    ob.start()
    ob.wait_recv()
    o_send_buf[...] = (o_terms[:, p.core] + ob_in[...]).astype(low)

    def o_copy(chip):
        return remote(
            o_send_buf.at[chip], o_in.at[p.chip], o_send.at[chip], o_recv.at[p.chip], p.grp, 2 * chip + p.core
        )

    def o_arrival(chip):
        return remote(o_send_buf.at[chip], o_in.at[chip], o_send.at[chip], o_recv.at[chip], p.grp, p.mate)

    for chip in range(chips):
        pl.when(chip != p.chip)(lambda chip=chip: o_copy(chip).start())
    rail_step(3)
    total = gain_own[...]
    for i in range(1, slots):
        g_copy(i).wait_recv()
        total = total + gain_in[i]
    gain_mid[...] = total
    for b in range(1, grps):
        h_copy(b).start()

    tokens = tokens_ref[...].astype(wide)
    tok_grad_ref[...] = part[p.chip].astype(wide)

    @pl.when(p.chip > 0)
    def _():
        to_right(p.chip).wait_recv()
        tok_grad_ref[...] += left_in[p.chip].astype(wide)

    @pl.when(p.chip < last)
    def _():
        to_left(p.chip).wait_recv()
        tok_grad_ref[...] += right_in[p.chip].astype(wide)

    n1g = tok_grad_ref[...]
    scale_one = lax.rsqrt(jnp.mean(tokens * tokens, axis=-1, keepdims=True) + EPS)
    normed = tokens * scale_one
    lifted = n1g * gain_one
    tok_grad_ref[...] = state_grad[...] + scale_one * (
        lifted - normed * jnp.mean(lifted * normed, axis=-1, keepdims=True)
    )

    wq_grad = wgrad[0, p.core] + wm_in[0]
    for b in range(1, grps):
        w_copy(b).wait_recv()
        wq_grad = wq_grad + w_in[b].astype(wide)
    wq_grad_ref[...] = wq_grad
    wo_grad = o_terms[p.chip, p.core] + ob_in[p.chip]
    for chip in range(chips):
        pl.when(chip != p.chip)(lambda chip=chip: o_arrival(chip).wait_recv())
        wo_grad = wo_grad + jnp.where(chip == p.chip, 0.0, o_in[chip].astype(wide))
    wo_grad_ref[...] = wo_grad
    total = gain_mid[...]
    for b in range(1, grps):
        h_copy(b).wait_recv()
        total = total + gain_mid_in[b]
    gain_ref[...] = total

    for hop, kind in late_hops:
        if FIRST_HOPS[hop][0] < 3:
            m_first(hop, kind).wait_recv()
        m_first(hop, kind).wait_send()
    for kind in (2, 0, 1):
        for i in (0, 1):
            m_second(i, kind).wait_recv()
            m_second(i, kind).wait_send()
    for copy in early_copies:
        copy.wait()
    ob.wait_send()
    wm.wait_send()
    for i in range(1, slots):
        g_copy(i).wait_send()
    for b in range(1, grps):
        state_copy(b).wait_send()
        w_copy(b).wait_send()
        h_copy(b).wait_send()
    for chip in range(chips):
        km_copy(chip).wait_send()

        @pl.when(chip != p.chip)
        def _(chip=chip):
            q_copy(chip, 0).wait_send()
            q_copy(chip, 1).wait_send()
            kr_copy(chip).wait_send()
            o_copy(chip).wait_send()

        pl.when(chip > p.chip)(lambda chip=chip: to_right(chip).wait_send())
        pl.when(chip < p.chip)(lambda chip=chip: to_left(chip).wait_send())


def back_call(n2g, state, cotangent, tokens, gain_one, gain_two, attn, q_heads, kv_heads, mask, cosine, sine,
              qkv_all, out_full, n1_all, terms, owned, passing, early):
    chips = cosine.shape[0]
    grps = 4
    slots = 2 * chips
    shard, width = tokens.shape
    att, block = out_full.shape[0], terms.shape[1] // grps
    unit, half = att // (grps * slots), HD // 2
    vm, dma = pltpu.VMEM, pltpu.SemaphoreType.DMA
    anyspace = pl.BlockSpec(memory_space=pl.ANY)
    vspec = pl.BlockSpec(memory_space=pltpu.VMEM)
    low, wide = jnp.bfloat16, jnp.float32
    struct = jax.ShapeDtypeStruct
    return pl.pallas_call(
        functools.partial(back_kernel, chips, 1.0 / math.sqrt(HD)),
        out_shape=(
            struct((shard, width), wide),
            struct((half, width + HD), wide),
            struct((unit, width), wide),
            struct((2, 1, width), wide),
            struct((3, block, width), low),
            struct((3, block, width), low),
        ),
        in_specs=[vspec] * 13 + [anyspace] * 6,
        out_specs=(vspec,) * 4 + (anyspace,) * 2,
        scratch_shapes=[
            vm((att, width), low),
            vm((grps, shard, width), low),
            vm((chips, shard, width + HD), low),
            vm((grps, shard, slots * unit), low),
            vm((chips, 3, shard, HD), low),
            vm((chips, 3, shard, HD), low),
            vm((chips, 2, chips, shard, HD), low),
            vm((chips, chips, shard, HD), low),
            vm((chips, chips, shard, HD), low),
            vm((chips, shard, HD), wide),
            vm((chips, chips, shard, HD), low),
            vm((chips, shard, grps * HD), low),
            vm((chips, shard, width), low),
            vm((chips, shard, width), low),
            vm((chips, shard, width), low),
            vm((grps, 2, half, width + HD), wide),
            vm((grps, half, width + HD), wide),
            vm((grps, half, width + HD), low),
            vm((grps, half, width + HD), low),
            vm((chips, 2, unit, width), wide),
            vm((chips, unit, width), wide),
            vm((chips, unit, width), low),
            vm((chips, unit, width), low),
            vm((2, 3, block // 2, width), low),
            vm((2, 3, block // 2, width), low),
            vm((2, block, width), low),
            vm((2, 1, width), wide),
            vm((slots, 2, 1, width), wide),
            vm((2, 1, width), wide),
            vm((grps, 2, 1, width), wide),
            vm((shard, width), wide),
            dma((3,)),
            dma((grps,)), dma((grps,)),
            dma((chips, 2)), dma((chips, 2)),
            dma((chips,)), dma((chips,)),
            dma((chips,)), dma((chips,)),
            dma((2, chips)), dma((2, chips)),
            dma, dma,
            dma((grps,)), dma((grps,)),
            dma, dma,
            dma((chips,)), dma((chips,)),
            dma((6, 3)), dma((6, 3)),
            dma((5, 3)),
            dma((slots,)), dma((slots,)),
            dma((grps,)), dma((grps,)),
        ],
        compiler_params=pltpu.CompilerParams(
            collective_id=3, has_side_effects=True, vmem_limit_bytes=62 * 2**20
        ),
        name="back",
    )(n2g, state, cotangent, tokens, gain_one, gain_two, attn, q_heads, kv_heads, mask, cosine, sine,
      qkv_all, out_full, n1_all, terms, owned, passing, early)


def columns_to_owners(rows, row_unit):
    grp_count, seq_count = lax.axis_size("grp"), lax.axis_size("seq")
    tok_rows = rows.shape[0]
    split = rows.reshape(tok_rows, grp_count, seq_count, row_unit).transpose(2, 0, 1, 3)
    split = split.reshape(seq_count * tok_rows, grp_count * row_unit)
    return lax.all_to_all(split, "seq", split_axis=0, concat_axis=0, tiled=True)


def owners_to_columns(rows, row_unit):
    grp_count, seq_count = lax.axis_size("grp"), lax.axis_size("seq")
    tok_rows = rows.shape[0] // seq_count
    moved = lax.all_to_all(rows, "seq", split_axis=0, concat_axis=0, tiled=True)
    moved = moved.reshape(seq_count, tok_rows, grp_count, row_unit).transpose(1, 2, 0, 3)
    return moved.reshape(tok_rows, grp_count * seq_count * row_unit)


def plain_mlp(normed_two, cotangent_all, mlp_weight):
    contract_last, contract_first = CONTRACT_LAST, CONTRACT_FIRST
    mlp_rows = lax.all_gather(mlp_weight, "grp", axis=0, tiled=True)
    normed_two_all = lax.all_gather(normed_two, "seq", axis=0, tiled=True)
    gate_rows, upper_rows, down_rows = mlp_rows[:, 0, :], mlp_rows[:, 1, :], mlp_rows[:, 2, :]
    gate_vals = lax.dot_general(
        normed_two_all, gate_rows, contract_last, preferred_element_type=jnp.float32
    )
    upper_vals = lax.dot_general(
        normed_two_all, upper_rows, contract_last, preferred_element_type=jnp.float32
    )
    unit_wide, pull_back = jax.vjp(swish_product, gate_vals, upper_vals)
    unit_low = unit_wide.astype(jnp.bfloat16)
    unit_grad = lax.dot_general(
        cotangent_all, down_rows, contract_last, preferred_element_type=jnp.float32
    )
    gate_grad, upper_grad = pull_back(unit_grad)
    gate_grad = gate_grad.astype(jnp.bfloat16)
    upper_grad = upper_grad.astype(jnp.bfloat16)
    input_grad = jnp.dot(gate_grad, gate_rows, preferred_element_type=jnp.float32) + jnp.dot(
        upper_grad, upper_rows, preferred_element_type=jnp.float32
    )
    grad_part = lax.psum_scatter(
        input_grad.astype(jnp.bfloat16), "seq", scatter_dimension=0, tiled=True
    ).astype(jnp.float32)
    out_part = lax.psum_scatter(
        jnp.dot(unit_low, down_rows, preferred_element_type=jnp.float32).astype(jnp.bfloat16),
        "seq",
        scatter_dimension=0,
        tiled=True,
    ).astype(jnp.float32)
    mlp_terms = jnp.stack(
        [
            lax.dot_general(
                gate_grad, normed_two_all, contract_first, preferred_element_type=jnp.float32
            ),
            lax.dot_general(
                upper_grad, normed_two_all, contract_first, preferred_element_type=jnp.float32
            ),
            lax.dot_general(
                unit_low, cotangent_all, contract_first, preferred_element_type=jnp.float32
            ),
        ],
        axis=1,
    )
    mlp_grad = lax.psum_scatter(mlp_terms, "grp", scatter_dimension=0, tiled=True)
    return grad_part, out_part, mlp_grad


def padded_rows(mlp_weight):
    rows = mlp_weight.transpose(1, 0, 2)
    return jnp.pad(rows, ((0, 0), (0, -rows.shape[1] % 32), (0, 0)))


def per_device(
    tokens,
    cotangent,
    shard_segment,
    gain_attn,
    qkv_weight,
    qkv_bias,
    out_weight,
    gain_mlp,
    mlp_weight,
):
    tok_rows = tokens.shape[0]
    seq_count = lax.axis_size("seq")
    grp_count = lax.axis_size("grp")
    group_tok = tok_rows * seq_count
    heads_per = H // KVH
    kv_width = KVH * HD
    att_width = H * HD
    query_rows = heads_per * tok_rows
    score_scale = 1.0 / math.sqrt(HD)
    contract_last = CONTRACT_LAST
    contract_first = CONTRACT_FIRST
    seq_place = lax.axis_index("seq")
    grp_place = lax.axis_index("grp")
    use_kernels = (seq_count, grp_count, H, KVH, HD) == (8, 4, 12, 2, 128)
    if use_kernels:
        freqs = THETA ** (-(jnp.arange(HD // 2, dtype=jnp.float32) * 2.0) / HD)
        freqs = jnp.concatenate([freqs, freqs])[None, :]
        gain_rows = (gain_attn[None, :], gain_mlp[None, :])
        own_rows = padded_rows(mlp_weight)
        (
            attn_wide, state, cosine, sine, mask, q_heads, kv_heads, n1_all, n2_all, cot_all, out_all,
            qkv_all, columns, *peer_rows
        ) = front_call(
            tokens, *gain_rows, shard_segment, freqs, qkv_bias[None, :], cotangent, qkv_weight, out_weight,
            own_rows,
        )
        by_slot = lambda rows: rows.reshape((seq_count,) + rows.shape[2:])
        grad_part, out_part, mlp_terms, owned, passing, early = mlp_call(
            by_slot(n2_all), by_slot(cot_all), columns, [own_rows, *peer_rows]
        )
        output = (state + out_part).astype(jnp.bfloat16)
        token_grad, qkv_terms, out_grad, gain_sums, direct, second = back_call(
            grad_part, state, cotangent, tokens, *gain_rows, attn_wide, q_heads, kv_heads, mask,
            cosine, sine, qkv_all.reshape(-1, qkv_all.shape[-1]),
            out_all.reshape(att_width, -1), n1_all, mlp_terms, owned, passing, early,
        )
        units = mlp_weight.shape[0]
        mlp_sums = sum(
            rows[:, :units].astype(jnp.float32) for rows in (mlp_terms, direct, second)
        )
        width = tokens.shape[1]
        own = width // (grp_count * seq_count)
        gain_parts = lax.dynamic_slice_in_dim(
            gain_sums[:, 0], (grp_place * seq_count + seq_place) * own, own, 1
        )
        return (
            output,
            token_grad,
            gain_parts[0],
            qkv_terms[:, :width],
            qkv_terms[:, width],
            out_grad,
            gain_parts[1],
            mlp_sums.transpose(1, 0, 2),
        )
    segments = lax.dynamic_index_in_dim(shard_segment, grp_place, 0, keepdims=False)
    starts = shard_starts(segments, tok_rows, group_tok // 2)
    shard_order = jnp.arange(seq_count, dtype=jnp.int32)
    own_seg = jnp.sum(jnp.where(shard_order == seq_place, segments, 0))
    own_start = jnp.sum(jnp.where(shard_order == seq_place, starts, 0))
    positions = own_start + jnp.arange(tok_rows, dtype=jnp.int32)
    cosine_table, sine_table = rotary_tables(positions, HD)
    query_pos = jnp.tile(positions, heads_per)
    tokens_wide = tokens.astype(jnp.float32)
    gain_one = gain_attn.astype(jnp.float32)
    gain_two = gain_mlp.astype(jnp.float32)
    normed_one = rms_scale(tokens_wide, gain_one).astype(jnp.bfloat16)
    normed_one_all = lax.all_gather(normed_one, "seq", axis=0, tiled=True)
    qkv_rows = lax.all_gather(qkv_weight, "grp", axis=0, tiled=True)
    bias_rows = lax.all_gather(qkv_bias, "grp", axis=0, tiled=True)
    cotangent_all = lax.all_gather(cotangent, "seq", axis=0, tiled=True)
    out_full = lax.all_gather(out_weight, AXES, axis=0, tiled=True)
    projected = lax.dot_general(
        normed_one_all, qkv_rows, contract_last, preferred_element_type=jnp.float32
    )
    projected = (projected + bias_rows.astype(jnp.float32)[None, :]).astype(jnp.bfloat16)
    projected = owners_to_columns(projected, qkv_weight.shape[0]).astype(jnp.float32)
    query_rot = rotate(
        projected[:, :att_width].reshape(tok_rows, H, HD), cosine_table, sine_table
    ).astype(jnp.bfloat16)
    key_rot = rotate(
        projected[:, att_width : att_width + kv_width].reshape(tok_rows, KVH, HD),
        cosine_table,
        sine_table,
    ).astype(jnp.bfloat16)
    value_low = projected[:, att_width + kv_width :].astype(jnp.bfloat16)
    keys_all, values_all = (
        lax.all_gather(key_rot.reshape(tok_rows, kv_width), "seq", axis=0, tiled=True),
        lax.all_gather(value_low, "seq", axis=0, tiled=True),
    )
    queries = (
        query_rot.reshape(tok_rows, KVH, heads_per, HD)
        .transpose(1, 2, 0, 3)
        .reshape(KVH, query_rows, HD)
    )
    key_block = min(512, group_tok)
    block_count = group_tok // key_block
    block_order = jnp.arange(block_count, dtype=jnp.int32)

    def block_mask(block_index):
        key_index = block_index * key_block + jnp.arange(key_block, dtype=jnp.int32)
        key_shard = key_index // tok_rows
        onehot = key_shard[:, None] == shard_order[None, :]
        key_seg = jnp.sum(jnp.where(onehot, segments[None, :], 0), axis=1)
        key_pos = jnp.sum(jnp.where(onehot, starts[None, :], 0), axis=1) + key_index % tok_rows
        visible = (key_seg == 0) | (key_seg == own_seg)
        return visible[None, :] & (key_pos[None, :] <= query_pos[:, None])

    def block_keys(block_index):
        key_part = lax.dynamic_slice_in_dim(
            keys_all, block_index * key_block, key_block, 0
        ).reshape(key_block, KVH, HD)
        value_part = lax.dynamic_slice_in_dim(
            values_all, block_index * key_block, key_block, 0
        ).reshape(key_block, KVH, HD)
        return (key_part, value_part)

    def block_scores(key_part):
        return (
            jnp.einsum("krd,jkd->krj", queries, key_part, preferred_element_type=jnp.float32)
            * score_scale
        )

    def stat_step(stats_now, block_index):
        allowed = block_mask(block_index)

        def stat_visit(current):
            top_old, total_old = current
            key_part, value_part = block_keys(block_index)
            scores = jnp.where(allowed[None], block_scores(key_part), -1e30)
            top_new = jnp.maximum(top_old, jnp.max(scores, axis=-1))
            weights = jnp.where(allowed[None], jnp.exp(scores - top_new[..., None]), 0.0)
            return (top_new, total_old * jnp.exp(top_old - top_new) + jnp.sum(weights, axis=-1))

        return (lax.cond(jnp.any(allowed), stat_visit, lambda current: current, stats_now), None)

    start_stats = (
        jnp.full((KVH, query_rows), -1e30, jnp.float32),
        jnp.zeros((KVH, query_rows), jnp.float32),
    )
    (top_all, total_all), unused = lax.scan(stat_step, start_stats, block_order)
    log_total = top_all + jnp.log(total_all)

    def mix_step(mixed_sum, block_index):
        allowed = block_mask(block_index)

        def mix_visit(current):
            key_part, value_part = block_keys(block_index)
            prob_low = jnp.where(
                allowed[None], jnp.exp(block_scores(key_part) - log_total[..., None]), 0.0
            ).astype(jnp.bfloat16)
            return current + jnp.einsum(
                "krj,jkd->krd", prob_low, value_part, preferred_element_type=jnp.float32
            )

        return (lax.cond(jnp.any(allowed), mix_visit, lambda current: current, mixed_sum), None)

    mixed_sum, unused = lax.scan(
        mix_step, jnp.zeros((KVH, query_rows, HD), jnp.float32), block_order
    )
    attn_wide = (
        mixed_sum.reshape(KVH, heads_per, tok_rows, HD)
        .transpose(2, 0, 1, 3)
        .reshape(tok_rows, att_width)
    )
    attn_low = attn_wide.astype(jnp.bfloat16)
    attn_proj = jnp.dot(attn_low, out_full, preferred_element_type=jnp.float32)
    state = tokens_wide + attn_proj
    normed_two = rms_scale(state, gain_two).astype(jnp.bfloat16)
    grad_part, out_part, mlp_grad = plain_mlp(normed_two, cotangent_all, mlp_weight)
    output = (state + out_part).astype(jnp.bfloat16)
    unused_state, norm_two_back = jax.vjp(rms_scale, state, gain_two)
    state_norm_grad, gain_two_grad = norm_two_back(grad_part)
    state_grad = state_norm_grad + cotangent.astype(jnp.float32)
    state_low = state_grad.astype(jnp.bfloat16)
    attn_grad = lax.dot_general(
        state_low, out_full, contract_last, preferred_element_type=jnp.float32
    )
    attn_grad_low = attn_grad.astype(jnp.bfloat16)
    attn_owned = columns_to_owners(attn_low, out_weight.shape[0])
    state_low_all = lax.all_gather(state_low, "seq", axis=0, tiled=True)
    out_grad = lax.psum_scatter(
        lax.dot_general(
            attn_owned, state_low_all, contract_first, preferred_element_type=jnp.float32
        ),
        "grp",
        scatter_dimension=0,
        tiled=True,
    )
    grad_heads = (
        attn_grad_low.reshape(tok_rows, KVH, heads_per, HD)
        .transpose(1, 2, 0, 3)
        .reshape(KVH, query_rows, HD)
    )
    delta_rows = jnp.sum(
        (attn_grad_low.astype(jnp.float32) * attn_wide).reshape(tok_rows, H, HD), axis=-1
    )
    delta_rows = (
        delta_rows.reshape(tok_rows, KVH, heads_per).transpose(1, 2, 0).reshape(KVH, query_rows)
    )

    def back_step(query_grad, block_index):
        allowed = block_mask(block_index)

        def back_visit(current):
            key_part, value_part = block_keys(block_index)
            prob_vals = jnp.where(
                allowed[None], jnp.exp(block_scores(key_part) - log_total[..., None]), 0.0
            )
            prob_grad = jnp.einsum(
                "krd,jkd->krj", grad_heads, value_part, preferred_element_type=jnp.float32
            )
            score_grad = (prob_vals * (prob_grad - delta_rows[..., None])).astype(jnp.bfloat16)
            new_grad = (
                current
                + jnp.einsum(
                    "krj,jkd->krd", score_grad, key_part, preferred_element_type=jnp.float32
                )
                * score_scale
            )
            key_grad = (
                jnp.einsum("krj,krd->jkd", score_grad, queries, preferred_element_type=jnp.float32)
                * score_scale
            )
            value_grad = jnp.einsum(
                "krj,krd->jkd",
                prob_vals.astype(jnp.bfloat16),
                grad_heads,
                preferred_element_type=jnp.float32,
            )
            return (
                new_grad,
                (key_grad.reshape(key_block, kv_width), value_grad.reshape(key_block, kv_width)),
            )

        def skip_block(current):
            blank_rows = jnp.zeros((key_block, kv_width), jnp.float32)
            return (current, (blank_rows, blank_rows))

        return lax.cond(jnp.any(allowed), back_visit, skip_block, query_grad)

    query_grad, (key_grads, value_grads) = lax.scan(
        back_step, jnp.zeros((KVH, query_rows, HD), jnp.float32), block_order
    )
    key_own, value_own = (
        lax.psum_scatter(
            key_grads.reshape(group_tok, kv_width).astype(jnp.bfloat16),
            "seq",
            scatter_dimension=0,
            tiled=True,
        ).astype(jnp.float32),
        lax.psum_scatter(
            value_grads.reshape(group_tok, kv_width).astype(jnp.bfloat16),
            "seq",
            scatter_dimension=0,
            tiled=True,
        ).astype(jnp.float32),
    )
    query_back = unrotate(
        query_grad.reshape(KVH, heads_per, tok_rows, HD)
        .transpose(2, 0, 1, 3)
        .reshape(tok_rows, H, HD),
        cosine_table,
        sine_table,
    )
    key_back = unrotate(key_own.reshape(tok_rows, KVH, HD), cosine_table, sine_table)
    qkv_grad_low = jnp.concatenate(
        [query_back.reshape(tok_rows, att_width), key_back.reshape(tok_rows, kv_width), value_own],
        axis=1,
    ).astype(jnp.bfloat16)
    qkv_grad_owned = columns_to_owners(qkv_grad_low, qkv_weight.shape[0])
    bias_terms = jnp.sum(qkv_grad_owned.astype(jnp.float32), axis=0)
    normed_one_grad = lax.psum_scatter(
        jnp.dot(qkv_grad_owned, qkv_rows, preferred_element_type=jnp.float32).astype(jnp.bfloat16),
        "seq",
        scatter_dimension=0,
        tiled=True,
    ).astype(jnp.float32)
    qkv_grad = lax.psum_scatter(
        lax.dot_general(
            qkv_grad_owned, normed_one_all, contract_first, preferred_element_type=jnp.float32
        ),
        "grp",
        scatter_dimension=0,
        tiled=True,
    )
    unused_tokens, norm_one_back = jax.vjp(rms_scale, tokens_wide, gain_one)
    token_norm_grad, gain_one_grad = norm_one_back(normed_one_grad)
    token_grad = token_norm_grad + state_grad
    bias_part = lax.psum_scatter(bias_terms, "grp", scatter_dimension=0, tiled=True)
    gain_one_part, gain_two_part = (
        lax.psum_scatter(gain_one_grad, AXES, scatter_dimension=0, tiled=True),
        lax.psum_scatter(gain_two_grad, AXES, scatter_dimension=0, tiled=True),
    )
    return (
        output,
        token_grad,
        gain_one_part,
        qkv_grad,
        bias_part,
        out_grad,
        gain_two_part,
        mlp_grad,
    )


def solution(mesh):
    return jax.shard_map(
        per_device,
        mesh=mesh,
        in_specs=(
            P(("grp", "seq"), None),
            P(("grp", "seq"), None),
            P(),
            P(),
            P(("grp", "seq"), None),
            P(("grp", "seq")),
            P(("grp", "seq"), None),
            P(),
            P(("grp", "seq"), None, None),
        ),
        out_specs=(
            P(("grp", "seq"), None),
            P(("grp", "seq"), None),
            P(("grp", "seq")),
            P(("grp", "seq"), None),
            P(("grp", "seq")),
            P(("grp", "seq"), None),
            P(("grp", "seq")),
            P(("grp", "seq"), None, None),
        ),
        check_vma=False,
    )
```

```python
import functools
import math

import jax
import jax.numpy as jnp
from jax import lax
from jax.experimental import pallas as pl
from jax.experimental.pallas import tpu as pltpu
from jax.sharding import PartitionSpec as P

H = 12
KVH = 2
HD = 128
FF = 8960


EPS = 1e-06
THETA = 10000.0


def rms_scale(values, gain_vec):
    return values * lax.rsqrt(jnp.mean(values * values, axis=-1, keepdims=True) + EPS) * gain_vec


def rotary_tables(positions, head_dim):
    half_dim = head_dim // 2
    freqs = THETA ** (-(jnp.arange(half_dim, dtype=jnp.float32) * 2.0) / head_dim)
    angles = positions.astype(jnp.float32)[:, None] * freqs[None, :]
    cosine_table = jnp.concatenate([jnp.cos(angles), jnp.cos(angles)], axis=-1)
    sine_table = jnp.concatenate([jnp.sin(angles), jnp.sin(angles)], axis=-1)
    return (cosine_table, sine_table)


def rotate(values, cosine_table, sine_table):
    half_dim = values.shape[-1] // 2
    turned = jnp.concatenate([-values[..., half_dim:], values[..., :half_dim]], axis=-1)
    return values * cosine_table[:, None, :] + turned * sine_table[:, None, :]


def unrotate(grad_rows, cosine_table, sine_table):
    half_dim = grad_rows.shape[-1] // 2
    scaled = grad_rows * sine_table[:, None, :]
    turned = jnp.concatenate([scaled[..., half_dim:], -scaled[..., :half_dim]], axis=-1)
    return grad_rows * cosine_table[:, None, :] + turned


def shard_starts(segments, tok_dev, prompt_len):
    shard_total = segments.shape[0]
    shard_order = jnp.arange(shard_total, dtype=jnp.int32)
    same_seg = segments[:, None] == segments[None, :]
    first_shard = jnp.min(jnp.where(same_seg, shard_order[None, :], shard_total), axis=1)
    cont_start = prompt_len + (shard_order - first_shard) * tok_dev
    return jnp.where(segments == 0, shard_order * tok_dev, cont_start)


def swish_product(gate_vals, upper_vals):
    return jax.nn.silu(gate_vals) * upper_vals


AXES = ("grp", "seq")
CONTRACT_LAST = (((1,), (1,)), ((), ()))
CONTRACT_FIRST = (((0,), (0,)), ((), ()))


MESH = pl.DeviceIdType.MESH


def remote(src, dst, send_sem, recv_sem, grp, seq):
    return pltpu.make_async_remote_copy(
        src_ref=src, dst_ref=dst, send_sem=send_sem, recv_sem=recv_sem,
        device_id=(grp, seq), device_id_type=MESH,
    )


def nearest_chip(place, order, chips):
    both = 2 * jnp.minimum(place, chips - 1 - place)
    offset = (order + 1) // 2
    near = jnp.where(order % 2 == 1, place - offset, place + offset)
    rest = jnp.where(place < chips - 1 - place, order, chips - 1 - order)
    return jnp.where(order <= both, near, rest)


class Place:
    def __init__(self, chips):
        self.chips = chips
        self.grp, self.seq = lax.axis_index("grp"), lax.axis_index("seq")
        self.chip, self.core = self.seq // 2, self.seq % 2
        self.mate = self.seq + 1 - 2 * self.core

    def peer(self, offset):
        low, high = self.grp % 2, self.grp // 2
        low = 1 - low if offset % 2 else low
        high = 1 - high if offset // 2 else high
        return 2 * high + low

    def barrier(self, grps):
        barrier = pltpu.get_barrier_semaphore()
        for chip in range(self.chips):
            @pl.when(chip != self.chip)
            def _(chip=chip):
                pl.semaphore_signal(
                    barrier, inc=1, device_id=(self.grp, 2 * chip + self.core), device_id_type=MESH
                )
        pl.semaphore_signal(barrier, inc=1, device_id=(self.grp, self.mate), device_id_type=MESH)
        for offset in range(1, grps):
            pl.semaphore_signal(
                barrier, inc=1, device_id=(self.peer(offset), self.seq), device_id_type=MESH
            )
        pl.semaphore_wait(barrier, self.chips - 1 + 1 + grps - 1)


class RailGather:
    def __init__(self, place, view, send_sem, recv_sem):
        self.place, self.view, self.send_sem, self.recv_sem = place, view, send_sem, recv_sem

    def copy(self, way, chip, core):
        p = self.place
        to = (p.seq + 2, p.seq - 2, p.mate)[way]
        return remote(
            self.view(chip, core), self.view(chip, core), self.send_sem.at[way, chip],
            self.recv_sem.at[chip, core], p.grp, to,
        )

    def start(self):
        p = self.place
        pl.when(p.chip < p.chips - 1)(lambda: self.copy(0, p.chip, p.core).start())
        pl.when(p.chip > 0)(lambda: self.copy(1, p.chip, p.core).start())
        self.copy(2, p.chip, p.core).start()

    def forward(self, step):
        p = self.place

        @pl.when(p.chip - step >= 0)
        def _():
            chip = p.chip - step
            self.copy(2, chip, p.core).wait_recv()
            pl.when(p.chip < p.chips - 1)(lambda: self.copy(0, chip, p.core).start())
            self.copy(2, chip, p.core).start()

        @pl.when(p.chip + step < p.chips)
        def _():
            chip = p.chip + step
            self.copy(2, chip, p.core).wait_recv()
            pl.when(p.chip > 0)(lambda: self.copy(1, chip, p.core).start())
            self.copy(2, chip, p.core).start()

    def wait_mate(self, chip):
        self.copy(2, chip, 1 - self.place.core).wait_recv()

    def drain(self):
        p = self.place
        for chip in range(p.chips):
            self.copy(2, chip, p.core).wait_send()
            pl.when((chip <= p.chip) & (p.chip < p.chips - 1))(
                lambda chip=chip: self.copy(0, chip, p.core).wait_send()
            )
            pl.when((chip >= p.chip) & (p.chip > 0))(
                lambda chip=chip: self.copy(1, chip, p.core).wait_send()
            )


class LineScatter:
    def __init__(self, place, part, mate_in, left_in, right_in, send_sem, recv_sem):
        self.place, self.part = place, part
        self.mate_in, self.left_in, self.right_in = mate_in, left_in, right_in
        self.send_sem, self.recv_sem = send_sem, recv_sem

    def copy(self, way, src, landing, r, chip, to):
        return remote(
            src, landing.at[r, chip], self.send_sem.at[way, r, chip], self.recv_sem.at[way, r, chip],
            self.place.grp, to,
        )

    def to_mate(self, r, chip):
        p = self.place
        return self.copy(0, self.part.at[r, 2 * chip + 1 - p.core], self.mate_in, r, chip, p.mate)

    def to_right(self, r, chip):
        p = self.place
        return self.copy(1, self.part.at[r, 2 * chip + p.core], self.left_in, r, chip, p.seq + 2)

    def to_left(self, r, chip):
        p = self.place
        return self.copy(2, self.part.at[r, 2 * chip + p.core], self.right_in, r, chip, p.seq - 2)

    def step(self, r, chip):
        p = self.place
        last = p.chips - 1
        slot = 2 * chip + p.core

        @pl.when(chip != p.chip)
        def _():
            self.to_mate(r, chip).wait_recv()
            total = self.part[r, slot].astype(jnp.float32) + self.mate_in[r, chip].astype(jnp.float32)
            self.part[r, slot] = total.astype(jnp.bfloat16)

        @pl.when(chip > p.chip)
        def _():
            @pl.when(p.chip > 0)
            def _():
                self.to_right(r, chip).wait_recv()
                self.part[r, slot] = (
                    self.part[r, slot].astype(jnp.float32) + self.left_in[r, chip].astype(jnp.float32)
                ).astype(jnp.bfloat16)

            self.to_right(r, chip).start()

        @pl.when(chip < p.chip)
        def _():
            @pl.when(p.chip < last)
            def _():
                self.to_left(r, chip).wait_recv()
                self.part[r, slot] = (
                    self.part[r, slot].astype(jnp.float32) + self.right_in[r, chip].astype(jnp.float32)
                ).astype(jnp.bfloat16)

            self.to_left(r, chip).start()

    def finish(self, r, out_ref):
        p = self.place
        self.to_mate(r, p.chip).wait_recv()
        out_ref[...] = self.part[r, p.seq].astype(jnp.float32) + self.mate_in[r, p.chip].astype(jnp.float32)

        @pl.when(p.chip > 0)
        def _():
            self.to_right(r, p.chip).wait_recv()
            out_ref[...] += self.left_in[r, p.chip].astype(jnp.float32)

        @pl.when(p.chip < p.chips - 1)
        def _():
            self.to_left(r, p.chip).wait_recv()
            out_ref[...] += self.right_in[r, p.chip].astype(jnp.float32)

    def drain(self, r):
        p = self.place
        for other in range(p.chips):
            self.to_mate(r, other).wait_send()
            pl.when(other > p.chip)(lambda other=other: self.to_right(r, other).wait_send())
            pl.when(other < p.chip)(lambda other=other: self.to_left(r, other).wait_send())


def front_kernel(chips, scale,
                 tokens_ref, gain_one_ref, gain_two_ref, segment_ref, freq_ref, bias_ref,
                 cot_ref, wq_ref, wo_ref, wm_ref,
                 attn_ref, state_ref, cos_ref, sin_ref, mask_ref, q_out_ref, kv_out_ref, n1_all_ref, n2_all_ref,
                 cot_all_ref, wo_all_ref, wq_all_ref, columns_ref, wm1_ref, wm2_ref, wm3_ref,
                 nbuf, n2buf, wq, wo, bias_own, bias, stage, qbuf, kvbuf, columns,
                 lsem, n_send, n_recv, n2_send, n2_recv, c_send, c_recv, o_send, o_recv, ox_send, ox_recv,
                 om_send, om_recv, wq_send, wq_recv, b_send, b_recv, m_send, m_recv, q_send, q_recv, k_send, k_recv):
    p = Place(chips)
    grps = 4
    half = wq_ref.shape[0]
    rows = pl.ds(p.core * half, half)
    mates_rows = pl.ds((1 - p.core) * half, half)
    wm_refs = (wm_ref, wm1_ref, wm2_ref, wm3_ref)
    part = wm_ref.shape[1] // 2

    own = [
        pltpu.make_async_copy(wq_ref, wq.at[0, rows], lsem.at[0]),
        pltpu.make_async_copy(wo_ref, wo.at[p.grp, p.chip, p.core], lsem.at[2]),
        pltpu.make_async_copy(cot_ref, cot_all_ref.at[p.chip, p.core], lsem.at[3]),
    ]
    for copy in own:
        copy.start()
    tokens = tokens_ref[...].astype(jnp.float32)
    nbuf[p.chip, p.core] = rms_scale(tokens, gain_one_ref[...].astype(jnp.float32)).astype(jnp.bfloat16)
    shard = tokens.shape[0]
    lane = lax.broadcasted_iota(jnp.int32, (1, 2 * half), 1)
    bias_wide = bias_ref[...].astype(jnp.float32)
    bias_pair = jnp.concatenate([bias_wide, bias_wide], axis=1)
    bias_own[...] = jnp.broadcast_to(jnp.where(lane // half == p.core, bias_pair, 0.0), bias_own.shape)
    bias[0, p.core] = bias_own[...]
    p.barrier(grps)

    n1_line = RailGather(p, lambda chip, core: nbuf.at[chip, core], n_send, n_recv)
    cot_line = RailGather(p, lambda chip, core: cot_all_ref.at[chip, core], c_send, c_recv)
    n2_line = RailGather(p, lambda chip, core: n2buf.at[chip, core], n2_send, n2_recv)
    out_line = RailGather(p, lambda chip, core: wo.at[p.grp, chip, core], o_send, o_recv)

    def wq_direct(b):
        return remote(wq_ref, wq.at[b, rows], wq_send.at[0, b], wq_recv.at[b, 0], p.peer(b), p.seq)

    def wq_mate(b):
        return remote(wq.at[b, rows], wq.at[b, rows], wq_send.at[1, b], wq_recv.at[b, 1], p.grp, p.mate)

    def bias_direct(b):
        return remote(bias_own, bias.at[b, p.core], b_send.at[0, b], b_recv.at[b, 0], p.peer(b), p.seq)

    def bias_mate(b):
        return remote(bias.at[b, p.core], bias.at[b, p.core], b_send.at[1, b], b_recv.at[b, 1], p.grp, p.mate)

    def m_part(ref, i, j):
        return ref.at[j, pl.ds(i * part, part)]

    def m_direct(b, i, j):
        return remote(
            m_part(wm_ref, i, j), m_part(wm_refs[b], i, j), m_send.at[b, i, j], m_recv.at[b, i, j],
            p.peer(b), p.seq,
        )

    def m_forward(b, j):
        return remote(
            m_part(wm_refs[b], b - 1, j), m_part(wm3_ref, b - 1, j), m_send.at[3, b - 1, j],
            m_recv.at[3, b - 1, j], p.peer(3 - b), p.seq,
        )

    def out_cross(b, chip):
        view = wo.at[p.grp, chip, p.core]
        return remote(view, view, ox_send.at[b, chip], ox_recv.at[b, chip], p.peer(b), p.seq)

    def out_arrival(b, chip):
        view = wo.at[p.peer(b), chip, p.core]
        return remote(view, view, ox_send.at[b, chip], ox_recv.at[b, chip], p.grp, p.mate)

    def out_mate(b, core):
        view = wo.at[p.peer(b), :, core]
        return remote(view, view, om_send.at[b], om_recv.at[b], p.grp, p.mate)

    def q_copy(chip):
        return remote(
            stage.at[chip, pl.ds(0, 3)], qbuf.at[p.chip], q_send.at[chip], q_recv.at[p.chip],
            p.grp, 2 * chip + p.core,
        )

    def q_arrival(chip):
        return remote(stage.at[chip, pl.ds(0, 3)], qbuf.at[chip], q_send.at[chip], q_recv.at[chip], p.grp, p.mate)

    def k_copy(chip, to_chip):
        return remote(
            stage.at[chip, 3], kvbuf.at[p.chip, p.core, chip], k_send.at[0, chip, to_chip],
            k_recv.at[p.chip, p.core, chip], p.grp, 2 * to_chip + p.core,
        )

    def k_mate(head, chip, src=None):
        view = kvbuf.at[head, p.core, chip]
        return remote(
            view if src is None else src, view, k_send.at[1, head, chip],
            k_recv.at[head, p.core, chip], p.grp, p.mate,
        )

    def k_arrival(head, core, chip):
        view = kvbuf.at[head, core, chip]
        return remote(view, view, k_send.at[1, head, chip], k_recv.at[head, core, chip], p.grp, p.mate)

    def make_tables():
        segs = [segment_ref[p.grp, t] for t in range(2 * chips)]
        starts = []
        for t in range(2 * chips):
            first = jnp.int32(t)
            for other in reversed(range(t)):
                first = jnp.where(segs[other] == segs[t], jnp.int32(other), first)
            starts.append(
                jnp.where(segs[t] == 0, jnp.int32(t * shard), chips * shard + (t - first) * shard)
            )

        def own_of(values):
            own = values[0]
            for t in range(1, 2 * chips):
                own = jnp.where(p.seq == t, values[t], own)
            return own

        own_seg, own_start = own_of(segs), own_of(starts)
        row = lax.broadcasted_iota(jnp.int32, (shard, 2 * half), 0)
        column = lax.broadcasted_iota(jnp.int32, (shard, 2 * half), 1)
        freq = freq_ref[...]
        sign = jnp.where(column < half, -1.0, 1.0)
        for chip in range(chips):
            start = jnp.where(p.core == 0, starts[2 * chip], starts[2 * chip + 1])
            angle = (start + row).astype(jnp.float32) * freq
            cos_ref[chip] = jnp.cos(angle)
            sin_ref[chip] = jnp.sin(angle) * sign
        for core in range(2):
            for chip in range(chips):
                t = 2 * chip + core
                seen = jnp.where((segs[t] == 0) | (segs[t] == own_seg), jnp.int32(1), jnp.int32(0))
                allowed = (starts[t] + column <= own_start + row) & (row * 0 + seen > 0)
                block = core * chips + chip
                mask_ref[:, block * shard : (block + 1) * shard] = jnp.where(allowed, 0.0, -1e30)

    own[0].wait()
    for b in range(1, grps):
        wq_direct(b).start()
        bias_direct(b).start()
    wq_mate(0).start()
    bias_mate(0).start()
    n1_line.start()
    own[1].wait()
    out_line.start()
    for b in range(1, grps):
        wq_direct(b).wait_recv()
        wq_mate(b).start()
        bias_direct(b).wait_recv()
        bias_mate(b).start()
    for b in range(1, grps):
        out_cross(b, p.chip).start()
    for j in range(3):
        m_direct(1, 0, j).start()
        m_direct(2, 1, j).start()
    make_tables()
    for b in range(grps):
        wq_mate(b).wait_recv()
        bias_mate(b).wait_recv()

    @pl.loop(0, chips)
    def _(order):
        @pl.when(order > 0)
        def _():
            n1_line.forward(order)
            out_line.forward(order)
            for b in range(1, grps):
                pl.when(p.chip - order >= 0)(lambda b=b: out_cross(b, p.chip - order).start())
                pl.when(p.chip + order < chips)(lambda b=b: out_cross(b, p.chip + order).start())

        at = nearest_chip(p.chip, order, chips)
        x = nbuf[at, p.core]
        weights = wq[...].reshape(grps * 2 * half, x.shape[1])
        rows_all = lax.dot_general(x, weights, CONTRACT_LAST, preferred_element_type=jnp.float32)
        cosine, sine = cos_ref[at], sin_ref[at]
        for b in range(grps):
            u = rows_all[:, 2 * half * b : 2 * half * (b + 1)] + (bias[b, 0, 0:1] + bias[b, 1, 0:1])
            turned = u * cosine + pltpu.roll(u, half, 1) * sine
            place = p.peer(b)
            keep = jnp.where((place == grps - 1) & (p.chip >= chips // 2), 1.0, 0.0)
            value = (u * keep + turned * (1.0 - keep)).astype(jnp.bfloat16)
            stage[at, place] = value

            @pl.when(place == grps - 1)
            def _(value=value):
                kvbuf[p.chip, p.core, at] = value

            @pl.when((place < grps - 1) & (at == p.chip))
            def _(value=value, place=place):
                qbuf[p.chip, place] = value

        pl.when(at != p.chip)(lambda: q_copy(at).start())
        for to_chip in range(chips):
            pl.when(to_chip != p.chip)(lambda to_chip=to_chip: k_copy(at, to_chip).start())
        k_mate(p.chip, at, stage.at[at, 3]).start()


    @pl.loop(0, chips)
    def _(order):
        for head in range(chips):
            @pl.when(head != p.chip)
            def _(head=head):
                chip = nearest_chip(head, order, chips)
                k_arrival(head, p.core, chip).wait_recv()
                k_mate(head, chip).start()

    for chip in range(chips):
        pl.when(chip != p.chip)(lambda chip=chip: q_arrival(chip).wait_recv())
        for head in range(chips):
            k_arrival(head, 1 - p.core, chip).wait_recv()
    own[2].wait()
    cot_line.start()
    for j in (0, 1):
        for b in (1, 2):
            m_direct(b, b - 1, j).wait_recv()
            m_forward(b, j).start()
    for j in range(3):
        m_direct(1, 1, j).start()
        m_direct(2, 0, j).start()

    mask = mask_ref[...]
    heads_per = H // KVH
    for kv in range(KVH):
        heads = [kv * heads_per + i for i in range(heads_per)]
        queries = jnp.concatenate([qbuf[h % chips, h // chips] for h in heads], axis=0)
        keys = kvbuf[kv].reshape(mask.shape[1], 2 * half)
        values = kvbuf[KVH + kv].reshape(mask.shape[1], 2 * half)
        scores = lax.dot_general(queries, keys, CONTRACT_LAST, preferred_element_type=jnp.float32) * scale
        scores = scores.reshape(heads_per, shard, mask.shape[1]) + mask[None]
        weights = jnp.exp(scores - jnp.max(scores, axis=-1, keepdims=True))
        inverse = 1.0 / jnp.sum(weights, axis=-1, keepdims=True)
        probs = (weights * inverse).astype(jnp.bfloat16).reshape(heads_per * shard, mask.shape[1])
        mixed = jnp.dot(probs, values, preferred_element_type=jnp.float32)
        for i, h in enumerate(heads):
            attn_ref[:, h * 2 * half : (h + 1) * 2 * half] = mixed[i * shard : (i + 1) * shard]
        cot_line.forward(kv + 1)

    for b in range(1, grps):
        for chip in range(chips):
            out_arrival(b, chip).wait_recv()
        out_mate(b, p.core).start()
    for b in (1, 2):
        m_direct(b, b - 1, 2).wait_recv()
        m_forward(b, 2).start()
    attn_low = attn_ref[...].astype(jnp.bfloat16)
    unit = wo.shape[3]
    for owner in range(grps):
        columns[owner] = attn_low[:, owner * columns.shape[2] : (owner + 1) * columns.shape[2]]
    for b in range(1, grps):
        out_mate(b, 1 - p.core).wait_recv()
    for chip in range(chips):
        out_line.wait_mate(chip)
    state = tokens_ref[...].astype(jnp.float32) + jnp.dot(
        attn_low, wo[...].reshape(grps * chips * 2 * unit, tokens_ref.shape[1]),
        preferred_element_type=jnp.float32,
    )
    state_ref[...] = state
    n2buf[p.chip, p.core] = rms_scale(state, gain_two_ref[...].astype(jnp.float32)).astype(jnp.bfloat16)
    n2_line.start()
    cot_line.forward(3)
    outs = [
        pltpu.make_async_copy(nbuf, n1_all_ref, lsem.at[4]),
        pltpu.make_async_copy(wq, wq_all_ref, lsem.at[5]),
        pltpu.make_async_copy(qbuf, q_out_ref, lsem.at[6]),
        pltpu.make_async_copy(kvbuf, kv_out_ref, lsem.at[7]),
        pltpu.make_async_copy(wo, wo_all_ref, lsem.at[8]),
        pltpu.make_async_copy(columns, columns_ref, lsem.at[9]),
    ]
    for chip in range(chips):
        n1_line.wait_mate(chip)
    for copy in outs:
        copy.start()
    for step in range(1, chips):
        n2_line.forward(step)
    for chip in range(chips):
        cot_line.wait_mate(chip)
        n2_line.wait_mate(chip)
    last = pltpu.make_async_copy(n2buf, n2_all_ref, lsem.at[10])
    last.start()
    for b in (1, 2):
        for j in range(3):
            m_direct(b, 2 - b, j).wait_recv()
            m_forward(3 - b, j).wait_recv()
    for copy in outs:
        copy.wait()
    last.wait()
    n1_line.drain()
    n2_line.drain()
    out_line.drain()
    cot_line.drain()
    for b in range(grps):
        wq_mate(b).wait_send()
        bias_mate(b).wait_send()
    for b in range(1, grps):
        wq_direct(b).wait_send()
        bias_direct(b).wait_send()
        out_mate(b, p.core).wait_send()
        for chip in range(chips):
            out_cross(b, chip).wait_send()
    for b in (1, 2):
        for i in (0, 1):
            for j in range(3):
                m_direct(b, i, j).wait_send()
        for j in range(3):
            m_forward(b, j).wait_send()
    for chip in range(chips):
        pl.when(chip != p.chip)(lambda chip=chip: q_copy(chip).wait_send())
        for other in range(chips):
            pl.when(other != p.chip)(lambda chip=chip, other=other: k_copy(chip, other).wait_send())
            k_mate(other, chip).wait_send()


def front_call(tokens, gain_one, gain_two, segments, freqs, bias, cot, qkv_weight, out_weight, mlp_rows):
    chips = segments.shape[1] // 2
    grps = 4
    shard, width = tokens.shape
    half = qkv_weight.shape[0]
    vm, dma = pltpu.VMEM, pltpu.SemaphoreType.DMA
    anyspace = pl.BlockSpec(memory_space=pl.ANY)
    vspec = pl.BlockSpec(memory_space=pltpu.VMEM)
    low, wide = jnp.bfloat16, jnp.float32
    struct = jax.ShapeDtypeStruct
    wo_shape = (grps, chips, 2) + out_weight.shape
    columns_shape = (grps, shard, H * HD // grps)
    return pl.pallas_call(
        functools.partial(front_kernel, chips, 1.0 / math.sqrt(HD)),
        out_shape=(
            struct((shard, H * HD), wide),
            struct((shard, width), wide),
            struct((chips, shard, HD), wide),
            struct((chips, shard, HD), wide),
            struct((shard, 2 * chips * shard), wide),
            struct((chips, 3, shard, HD), low),
            struct((chips, 2, chips, shard, HD), low),
            struct((chips, 2, shard, width), low),
            struct((chips, 2, shard, width), low),
            struct((chips, 2, shard, width), low),
            struct(wo_shape, low),
            struct((grps, 2 * half, width), low),
            struct(columns_shape, low),
        ) + (struct(mlp_rows.shape, low),) * 3,
        in_specs=[vspec] * 3
        + [pl.BlockSpec(memory_space=pltpu.SMEM)]
        + [vspec] * 2
        + [anyspace] * 4,
        out_specs=(vspec,) * 5 + (anyspace,) * 11,
        scratch_shapes=[
            vm((chips, 2, shard, width), low),
            vm((chips, 2, shard, width), low),
            vm((grps, 2 * half, width), low),
            vm(wo_shape, low),
            vm((8, HD), wide),
            vm((grps, 2, 8, HD), wide),
            vm((chips, grps, shard, HD), low),
            vm((chips, 3, shard, HD), low),
            vm((chips, 2, chips, shard, HD), low),
            vm(columns_shape, low),
            dma((11,)),
            dma((3, chips)), dma((chips, 2)),
            dma((3, chips)), dma((chips, 2)),
            dma((3, chips)), dma((chips, 2)),
            dma((3, chips)), dma((chips, 2)),
            dma((grps, chips)), dma((grps, chips)), dma((grps,)), dma((grps,)),
            dma((2, grps)), dma((grps, 2)),
            dma((2, grps)), dma((grps, 2)),
            dma((grps, 2, 3)), dma((grps, 2, 3)),
            dma((chips,)), dma((chips,)),
            dma((2, chips, chips)), dma((chips, 2, chips)),
        ],
        compiler_params=pltpu.CompilerParams(
            collective_id=2, has_side_effects=True, vmem_limit_bytes=60 * 2**20
        ),
        name="front",
    )(tokens, gain_one, gain_two, segments, freqs, bias, cot, qkv_weight, out_weight, mlp_rows)


FIRST_HOPS = ((1, 0, 1), (3, 0, 1), (2, 1, 2), (3, 1, 2))
EARLY_HOPS = tuple((hop, kind) for kind in (2, 0) for hop in (1, 3, 0, 2))


def mlp_kernel(chips, grps, row_tiles, n2_ref, cot_ref, columns_ref, *refs):
    w_refs, refs = refs[:grps], refs[grps:]
    (
        n2g_ref, outp_ref, grads_ref, owned_ref, passing_ref, arrived_ref, tok, w, acts, part, mate_in, left_in, right_in, stage,
        lsem, ssend, srecv, wsem, osem, a_send, a_recv, e_send, e_recv,
    ) = refs
    p = Place(chips)
    shard, width = n2_ref.shape[1:]
    units = w.shape[1]
    block = units // grps
    tile = units // row_tiles
    loads = [
        pltpu.make_async_copy(n2_ref, tok.at[0], lsem.at[0]),
        pltpu.make_async_copy(cot_ref, tok.at[1], lsem.at[1]),
        pltpu.make_async_copy(columns_ref.at[p.grp], owned_ref.at[0], lsem.at[2]),
    ]
    loads[0].start()

    def w_copy(j, b):
        return pltpu.make_async_copy(w_refs[b].at[j], w.at[j, pl.ds(b * block, block)], wsem.at[j, b])

    for j in range(3):
        for b in range(grps):
            w_copy(j, b).start()
    for copy in loads[1:]:
        copy.start()

    barrier = pltpu.get_barrier_semaphore()
    inner = jnp.where((p.chip > 0) & (p.chip < chips - 1), 1, 0)

    def greet(grp, seq):
        pl.semaphore_signal(barrier, inc=1, device_id=(grp, seq), device_id_type=MESH)

    greet(p.grp, p.mate)
    pl.when(p.chip > 0)(lambda: greet(p.grp, p.seq - 2))
    pl.when(p.chip < chips - 1)(lambda: greet(p.grp, p.seq + 2))
    for b in range(1, grps):
        greet(p.peer(b), p.seq)
    pl.semaphore_wait(barrier, 2 + inner + grps - 1)
    scatter = LineScatter(p, part, mate_in, left_in, right_in, ssend, srecv)

    def a_copy(b):
        return remote(
            columns_ref.at[p.peer(b)], owned_ref.at[b], a_send.at[b], a_recv.at[b], p.peer(b), p.seq
        )

    for b in range(1, grps):
        a_copy(b).start()
    loads[0].wait()
    for j in range(2):
        for b in range(grps):
            w_copy(j, b).wait()

    def kind_of(t):
        return (t // row_tiles + 2) % 3

    def early(slot, kind):
        b, i, to = FIRST_HOPS[slot]
        half = block // 2
        rows = grads_ref.at[kind, pl.ds(b * block + i * half, half)]
        land = arrived_ref.at[kind // 2, pl.ds(i * half, half)] if b < 3 else passing_ref.at[i, kind]
        at = EARLY_HOPS.index((slot, kind))
        return remote(rows, land, e_send.at[at], e_recv.at[at], p.peer(to), p.seq)

    def out_copy(t):
        return pltpu.make_async_copy(
            stage.at[t % 2],
            grads_ref.at[kind_of(t), pl.ds((t % row_tiles) * tile, tile)],
            osem.at[t % 2],
        )

    def tile_grad(t):
        kind = kind_of(t)
        lhs = acts[kind, :, pl.ds(pl.multiple_of((t % row_tiles) * tile, 128), tile)]
        rhs = tok[kind // 2].reshape(2 * chips * shard, width)
        stage[t % 2] = lax.dot_general(
            lhs, rhs, CONTRACT_FIRST, preferred_element_type=jnp.float32
        ).astype(jnp.bfloat16)
        out_copy(t).start()

    def start_early(kind):
        for hop in EARLY_HOPS:
            if hop[1] == kind:
                early(*hop).start()

    def far_chip(order):
        return nearest_chip(p.chip, chips - 1 - order, chips)

    outer = (p.chip == 0) | (p.chip == chips - 1)

    @pl.loop(0, chips + 1)
    def _(order):
        @pl.when(order < chips)
        def _():
            at = far_chip(order)
            x = tok[0, pl.ds(2 * at, 2)].reshape(2 * shard, width)
            gate = lax.dot_general(x, w[0], CONTRACT_LAST, preferred_element_type=jnp.float32)
            up = lax.dot_general(x, w[1], CONTRACT_LAST, preferred_element_type=jnp.float32)
            sig = 1.0 / (1.0 + jnp.exp(-gate))
            silu = gate * sig
            rows = pl.ds(at * (2 * shard), 2 * shard)
            acts[0, rows] = (up * sig * (1.0 + gate * (1.0 - sig))).astype(jnp.bfloat16)
            acts[1, rows] = silu.astype(jnp.bfloat16)
            hidden = (silu * up).astype(jnp.bfloat16)
            acts[2, rows] = hidden

            @pl.when(order == 0)
            def _():
                for b in range(grps):
                    w_copy(2, b).wait()

            part[1, pl.ds(2 * at, 2)] = (
                jnp.dot(hidden, w[2], preferred_element_type=jnp.float32)
                .astype(jnp.bfloat16).reshape(2, shard, width)
            )
            scatter.to_mate(1, at).start()

        pl.when(outer & (order > 0))(lambda: scatter.step(1, far_chip(order - 1)))

    for copy in loads[1:]:
        copy.wait()

    @pl.loop(0, row_tiles)
    def _(t):
        pl.when(t >= 2)(lambda: out_copy(t - 2).wait())
        tile_grad(t)
        pl.when(jnp.logical_not(outer))(lambda: scatter.step(1, far_chip(t)))

    @pl.loop(0, chips)
    def _(order):
        at = far_chip(order)
        y = tok[1, pl.ds(2 * at, 2)].reshape(2 * shard, width)
        unit_grad = lax.dot_general(y, w[2], CONTRACT_LAST, preferred_element_type=jnp.float32)
        rows = pl.ds(at * (2 * shard), 2 * shard)
        acts[0, rows] = (unit_grad * acts[0, rows].astype(jnp.float32)).astype(jnp.bfloat16)
        acts[1, rows] = (unit_grad * acts[1, rows].astype(jnp.float32)).astype(jnp.bfloat16)

        @pl.when(order == 0)
        def _():
            out_copy(row_tiles - 2).wait()
            out_copy(row_tiles - 1).wait()
            start_early(2)

    @pl.loop(0, chips + 1)
    def _(order):
        @pl.when(order < chips)
        def _():
            at = far_chip(order)
            rows = pl.ds(at * (2 * shard), 2 * shard)
            back = jnp.dot(acts[0, rows], w[0], preferred_element_type=jnp.float32) + jnp.dot(
                acts[1, rows], w[1], preferred_element_type=jnp.float32
            )
            part[0, pl.ds(2 * at, 2)] = back.astype(jnp.bfloat16).reshape(2, shard, width)
            scatter.to_mate(0, at).start()

        @pl.when(order < row_tiles)
        def _():
            t = row_tiles + order
            pl.when(order >= 2)(lambda: out_copy(t - 2).wait())
            tile_grad(t)

        @pl.when(order == row_tiles)
        def _():
            out_copy(2 * row_tiles - 2).wait()
            out_copy(2 * row_tiles - 1).wait()
            start_early(0)

        pl.when(outer & (order > 0))(lambda: scatter.step(0, far_chip(order - 1)))
        pl.when(jnp.logical_not(outer) & (order >= 3))(lambda: scatter.step(0, far_chip(order - 3)))

    @pl.loop(2 * row_tiles, 3 * row_tiles)
    def _(t):
        pl.when(t >= 2 * row_tiles + 2)(lambda: out_copy(t - 2).wait())
        late = t - 2 * row_tiles + chips + 1 - 3
        pl.when(jnp.logical_not(outer) & (late < chips))(lambda: scatter.step(0, far_chip(late)))
        tile_grad(t)

    scatter.finish(0, n2g_ref)
    scatter.finish(1, outp_ref)
    out_copy(3 * row_tiles - 2).wait()
    out_copy(3 * row_tiles - 1).wait()
    for hop in EARLY_HOPS:
        early(*hop).wait_recv()
        early(*hop).wait_send()
    scatter.drain(0)
    scatter.drain(1)
    for b in range(1, grps):
        a_copy(b).wait_recv()
        a_copy(b).wait_send()


def mlp_call(n2_all, cot_all, columns, w_blocks, row_tiles=3):
    grps, (_, block, width) = len(w_blocks), w_blocks[0].shape
    slots, shard, _ = cot_all.shape
    chips = slots // 2
    units = grps * block
    vm, anyspace = pltpu.VMEM, pl.BlockSpec(memory_space=pl.ANY)
    vspec = pl.BlockSpec(memory_space=pltpu.VMEM)
    dma = pltpu.SemaphoreType.DMA
    return pl.pallas_call(
        functools.partial(mlp_kernel, chips, grps, row_tiles),
        out_shape=(
            jax.ShapeDtypeStruct((shard, width), jnp.float32),
            jax.ShapeDtypeStruct((shard, width), jnp.float32),
            jax.ShapeDtypeStruct((3, units, width), jnp.bfloat16),
            jax.ShapeDtypeStruct(columns.shape, jnp.bfloat16),
            jax.ShapeDtypeStruct((2, 3, block // 2, width), jnp.bfloat16),
            jax.ShapeDtypeStruct((2, block, width), jnp.bfloat16),
        ),
        in_specs=[anyspace] * (3 + grps),
        out_specs=(vspec, vspec) + (anyspace,) * 4,
        scratch_shapes=[
            vm((2, slots, shard, width), jnp.bfloat16),
            vm((3, units, width), jnp.bfloat16),
            vm((3, slots * shard, units), jnp.bfloat16),
            vm((2, slots, shard, width), jnp.bfloat16),
            vm((2, chips, shard, width), jnp.bfloat16),
            vm((2, chips, shard, width), jnp.bfloat16),
            vm((2, chips, shard, width), jnp.bfloat16),
            vm((2, units // row_tiles, width), jnp.bfloat16),
            dma((3,)), dma((3, 2, chips)), dma((3, 2, chips)),
            dma((3, grps)), dma((2,)), dma((grps,)), dma((grps,)),
            dma((len(EARLY_HOPS),)), dma((len(EARLY_HOPS),)),
        ],
        compiler_params=pltpu.CompilerParams(
            collective_id=1, has_side_effects=True, vmem_limit_bytes=62 * 2**20
        ),
        name="mlp",
    )(n2_all, cot_all, columns, *w_blocks)


def unturn(rows, cosine, sine, half):
    return rows * cosine + pltpu.roll(rows * sine, half, 1)


def back_kernel(chips, scale,
                n2g_ref, state_ref, cot_ref, tokens_ref, gain_one_ref, gain_two_ref, attn_ref, q_ref, kv_ref,
                mask_ref, cos_ref, sin_ref, wq_ref, wo_ref, n1_ref, terms_ref, owned_ref, passing_ref, early_ref,
                tok_grad_ref, wq_grad_ref, wo_grad_ref, gain_ref, direct_ref, second_ref,
                wo, stbuf, n1x, at_all, dq_stage, gq_in, kv_part, km_in, k_sum, k_own, kr_in,
                cols, part, left_in, right_in, wgrad, wm_in, w_send_buf, w_in, o_terms, ob_in, o_send_buf, o_in,
                m_own, m_in, early_rows, gain_own, gain_in, gain_mid, gain_mid_in, state_grad,
                lsem, s_send, s_recv, q_send, q_recv, km_send, km_recv, kr_send, kr_recv,
                r_send, r_recv, wm_send, wm_recv, w_send, w_recv, ob_send, ob_recv, o_send, o_recv, m_send, m_recv,
                ml_sem, g_send, g_recv, h_send, h_recv):
    p = Place(chips)
    grps = 4
    shard, width = n2g_ref.shape
    slots = 2 * chips
    heads_per = H // KVH
    half = HD // 2
    low, wide = jnp.bfloat16, jnp.float32
    block = terms_ref.shape[1] // grps
    mhalf = block // 2
    last = chips - 1

    loads = [
        pltpu.make_async_copy(wo_ref, wo, lsem.at[0]),
        pltpu.make_async_copy(n1_ref.at[:, p.core], n1x.at[:, :, pl.ds(0, width)], lsem.at[1]),
        pltpu.make_async_copy(owned_ref, at_all, lsem.at[2]),
    ]
    for copy in loads:
        copy.start()

    def seq_peer(i):
        return (p.seq + i) % slots

    barrier = pltpu.get_barrier_semaphore()
    for i in range(1, slots):
        pl.semaphore_signal(barrier, inc=1, device_id=(p.grp, seq_peer(i)), device_id_type=MESH)
    for b in range(1, grps):
        pl.semaphore_signal(barrier, inc=1, device_id=(p.peer(b), p.seq), device_id_type=MESH)
    pl.semaphore_wait(barrier, slots - 1 + grps - 1)

    def m_rows(b, i, kind):
        return terms_ref.at[kind, pl.ds(b * block + i * mhalf, mhalf)]

    def m_first(hop, kind):
        b, i, to = FIRST_HOPS[hop]
        land = direct_ref.at[kind, pl.ds(i * mhalf, mhalf)] if b < 3 else m_in.at[i, kind]
        return remote(
            m_rows(b, i, kind), land, m_send.at[hop, kind], m_recv.at[hop, kind], p.peer(to), p.seq
        )

    def m_second(i, kind):
        return remote(
            m_own.at[i, kind], second_ref.at[kind, pl.ds(i * mhalf, mhalf)], m_send.at[4 + i, kind],
            m_recv.at[4 + i, kind], p.peer(2 - i), p.seq,
        )

    late_hops = [(hop, kind) for kind in (1, 0, 2) for hop in (1, 3, 0, 2) if (hop, kind) not in EARLY_HOPS]
    for hop in late_hops:
        m_first(*hop).start()
    m_loads = [
        pltpu.make_async_copy(m_rows(2 - i, i, kind), m_own.at[i, kind], ml_sem.at[i, kind])
        for i in (0, 1)
        for kind in range(3)
    ]
    for hop, kind in EARLY_HOPS:
        if FIRST_HOPS[hop][0] == 3:
            i = FIRST_HOPS[hop][1]
            m_loads.append(pltpu.make_async_copy(passing_ref.at[i, kind], m_in.at[i, kind], ml_sem.at[2 + i, kind]))
    early_kinds = [kind for kind in (0, 2) if (0, kind) in EARLY_HOPS]
    early_loads = [
        pltpu.make_async_copy(early_ref.at[kind // 2], early_rows.at[kind // 2], ml_sem.at[4, kind])
        for kind in early_kinds
    ]
    early_copies = [
        pltpu.make_async_copy(early_rows.at[kind // 2], direct_ref.at[kind], ml_sem.at[4, kind])
        for kind in early_kinds
    ]
    m_loads += early_loads
    for copy in m_loads:
        copy.start()

    def m_turn(kind):
        for i in (0, 1):
            if (1 + 2 * i, kind) in late_hops:
                m_first(1 + 2 * i, kind).wait_recv()

            @pl.loop(0, mhalf // 16)
            def _(t, i=i):
                rows = pl.ds(pl.multiple_of(t * 16, 16), 16)
                m_own[i, kind, rows] = (
                    m_own[i, kind, rows].astype(wide) + m_in[i, kind, rows].astype(wide)
                ).astype(low)

            m_second(i, kind).start()

    state = state_ref[...]
    gain_two = gain_two_ref[...].astype(wide)
    n2g = n2g_ref[...]
    scale_two = lax.rsqrt(jnp.mean(state * state, axis=-1, keepdims=True) + EPS)
    normed = state * scale_two
    gain_own[1] = jnp.sum(n2g * normed, axis=0, keepdims=True)
    lifted = n2g * gain_two
    state_grad[...] = cot_ref[...].astype(wide) + scale_two * (
        lifted - normed * jnp.mean(lifted * normed, axis=-1, keepdims=True)
    )
    state_low = state_grad[...].astype(low)
    stbuf[0] = state_low

    def state_copy(b):
        return remote(stbuf.at[0], stbuf.at[b], s_send.at[b], s_recv.at[b], p.peer(b), p.seq)

    attn = attn_ref[...]
    unit = wo.shape[0] // (grps * slots)
    loads[0].wait()
    attn_grad = lax.dot_general(state_low, wo[...], CONTRACT_LAST, preferred_element_type=wide).astype(low)
    mask = mask_ref[...]
    keys_total = mask.shape[1]
    own_cos, own_sin = cos_ref[p.chip], sin_ref[p.chip]

    def km_copy(head):
        return remote(
            kv_part.at[head, 1 - p.core], km_in.at[head], km_send.at[head], km_recv.at[head], p.grp, p.mate
        )

    def kr_copy(head):
        return remote(
            k_sum.at[head], kr_in.at[p.chip], kr_send.at[head], kr_recv.at[p.chip], p.grp, 2 * head + p.core
        )

    def kr_arrival(chip):
        return remote(k_sum.at[chip], kr_in.at[chip], kr_send.at[chip], kr_recv.at[chip], p.grp, p.mate)

    q_parts = (pl.ds(0, 1), pl.ds(1, 2))

    def q_copy(chip, i):
        return remote(
            dq_stage.at[chip, q_parts[i]], gq_in.at[p.chip, q_parts[i]], q_send.at[chip, i],
            q_recv.at[p.chip, i], p.grp, 2 * chip + p.core,
        )

    def q_arrival(chip, i):
        return remote(
            dq_stage.at[chip, q_parts[i]], gq_in.at[chip, q_parts[i]], q_send.at[chip, i],
            q_recv.at[chip, i], p.grp, p.mate,
        )

    def key_sum(head):
        km_copy(head).wait_recv()
        total = kv_part[head, p.core].astype(wide) + km_in[head].astype(wide)

        @pl.when(p.chip == head)
        def _():
            k_own[...] = total

        @pl.when(p.chip != head)
        def _():
            k_sum[head] = total.astype(low)
            kr_copy(head).start()

    for kv in range(KVH):
        heads = [kv * heads_per + i for i in range(heads_per)]
        queries = jnp.concatenate([q_ref[h % chips, h // chips] for h in heads], axis=0)
        grads = jnp.concatenate([attn_grad[:, h * HD : (h + 1) * HD] for h in heads], axis=0)
        mixed = jnp.concatenate([attn[:, h * HD : (h + 1) * HD] for h in heads], axis=0)
        delta = jnp.sum(grads.astype(wide) * mixed, axis=-1, keepdims=True)
        keys = kv_ref[kv].reshape(keys_total, HD)
        values = kv_ref[KVH + kv].reshape(keys_total, HD)
        scores = lax.dot_general(queries, keys, CONTRACT_LAST, preferred_element_type=wide) * scale
        scores = (scores.reshape(heads_per, shard, keys_total) + mask[None]).reshape(heads_per * shard, keys_total)
        weights = jnp.exp(scores - jnp.max(scores, axis=-1, keepdims=True))
        probs = weights * (1.0 / jnp.sum(weights, axis=-1, keepdims=True))
        prob_grad = lax.dot_general(grads, values, CONTRACT_LAST, preferred_element_type=wide)
        score_grad = (probs * (prob_grad - delta)).astype(low)
        key_grad = lax.dot_general(score_grad, queries, CONTRACT_FIRST, preferred_element_type=wide) * scale
        value_grad = lax.dot_general(probs.astype(low), grads, CONTRACT_FIRST, preferred_element_type=wide)
        kv_part[kv] = key_grad.astype(low).reshape(2, chips, shard, HD)
        kv_part[KVH + kv] = value_grad.astype(low).reshape(2, chips, shard, HD)
        km_copy(kv).start()
        km_copy(KVH + kv).start()
        query_grad = jnp.dot(score_grad, keys, preferred_element_type=wide) * scale
        for i, h in enumerate(heads):
            turned = unturn(query_grad[i * shard : (i + 1) * shard], own_cos, own_sin, half).astype(low)
            dq_stage[h % chips, h // chips] = turned

            @pl.when(p.chip == h % chips)
            def _(turned=turned, h=h):
                gq_in[h % chips, h // chips] = turned

        for chip in range(chips):
            pl.when(chip != p.chip)(lambda chip=chip: q_copy(chip, kv).start())
        if kv == 0:
            for copy in m_loads:
                copy.wait()
            for copy in early_copies:
                copy.start()
            m_turn(2)
            m_turn(0)
            for b in range(1, grps):
                state_copy(b).start()
            key_sum(0)
            key_sum(KVH)
    key_sum(1)
    key_sum(KVH + 1)
    m_turn(1)
    loads[1].wait()
    lane = lax.broadcasted_iota(jnp.int32, (chips, shard, HD), 2)
    n1x[:, :, width:] = jnp.where(lane == 0, 1.0, 0.0).astype(low)

    for chip in range(chips):
        for i in (0, 1):
            pl.when(chip != p.chip)(lambda chip=chip, i=i: q_arrival(chip, i).wait_recv())
        pl.when(chip != p.chip)(lambda chip=chip: kr_arrival(chip).wait_recv())
    is_value = jnp.where(p.chip >= chips // 2, 1.0, 0.0)

    gain_one = gain_one_ref[...].astype(wide)
    gain_own[0] = jnp.zeros_like(gain_own[0])

    def to_right(chip):
        return remote(part.at[chip], left_in.at[chip], r_send.at[0, chip], r_recv.at[0, chip], p.grp, p.seq + 2)

    def to_left(chip):
        return remote(part.at[chip], right_in.at[chip], r_send.at[1, chip], r_recv.at[1, chip], p.grp, p.seq - 2)

    @pl.loop(0, chips)
    def _(order):
        chip = nearest_chip(p.chip, last - order, chips)
        key_total = k_own[chip]
        for other in range(chips):
            key_total = key_total + jnp.where(other == p.chip, 0.0, kr_in[other, chip].astype(wide))
        turned = unturn(key_total, cos_ref[chip], sin_ref[chip], half)
        last_head = (key_total * is_value + turned * (1.0 - is_value)).astype(low)
        for b in range(grps):
            place = p.peer(b)
            query_head = gq_in[chip, jnp.minimum(place, grps - 2)]
            cols[chip, :, b * HD : (b + 1) * HD] = jnp.where(place == grps - 1, last_head, query_head)
        terms = jnp.dot(cols[chip], wq_ref[...], preferred_element_type=wide)
        part[chip] = terms.astype(low)
        gain_own[0] += jnp.sum(terms * n1x[chip, :, 0:width].astype(wide), axis=0, keepdims=True)
        pl.when((p.chip == 0) & (chip > 0))(lambda: to_right(chip).start())
        pl.when((p.chip == last) & (chip < last))(lambda: to_left(chip).start())

    gain_own[0] = gain_own[0] / gain_one

    def g_copy(i):
        return remote(gain_own, gain_in.at[i], g_send.at[i], g_recv.at[i], p.grp, seq_peer(i))

    def h_copy(b):
        return remote(gain_mid, gain_mid_in.at[b], h_send.at[b], h_recv.at[b], p.peer(b), p.seq)

    for i in range(1, slots):
        g_copy(i).start()

    def rail_step(order):
        far = last - order

        @pl.when((far > p.chip) & (p.chip > 0))
        def _():
            to_right(far).wait_recv()
            part[far] = (part[far].astype(wide) + left_in[far].astype(wide)).astype(low)
            to_right(far).start()

        @pl.when((order < p.chip) & (p.chip < last))
        def _():
            to_left(order).wait_recv()
            part[order] = (part[order].astype(wide) + right_in[order].astype(wide)).astype(low)
            to_left(order).start()

    rail_step(0)
    wgrad[...] = lax.dot_general(
        cols[...].reshape(chips * shard, grps * HD), n1x[...].reshape(chips * shard, width + HD),
        CONTRACT_FIRST, preferred_element_type=wide,
    ).reshape(grps, 2, half, width + HD)
    wm = remote(wgrad.at[:, 1 - p.core], wm_in, wm_send, wm_recv, p.grp, p.mate)
    wm.start()
    rail_step(1)
    wm.wait_recv()
    w_send_buf[...] = (wgrad[:, p.core] + wm_in[...]).astype(low)

    def w_copy(b):
        return remote(w_send_buf.at[b], w_in.at[b], w_send.at[b], w_recv.at[b], p.peer(b), p.seq)

    for b in range(1, grps):
        w_copy(b).start()
    rail_step(2)
    loads[2].wait()
    for b in range(1, grps):
        state_copy(b).wait_recv()
    o_terms[...] = lax.dot_general(
        at_all[...].reshape(grps * shard, slots * unit), stbuf[...].reshape(grps * shard, width),
        CONTRACT_FIRST, preferred_element_type=wide,
    ).reshape(chips, 2, unit, width)
    ob = remote(o_terms.at[:, 1 - p.core], ob_in, ob_send, ob_recv, p.grp, p.mate)
    ob.start()
    ob.wait_recv()
    o_send_buf[...] = (o_terms[:, p.core] + ob_in[...]).astype(low)

    def o_copy(chip):
        return remote(
            o_send_buf.at[chip], o_in.at[p.chip], o_send.at[chip], o_recv.at[p.chip], p.grp, 2 * chip + p.core
        )

    def o_arrival(chip):
        return remote(o_send_buf.at[chip], o_in.at[chip], o_send.at[chip], o_recv.at[chip], p.grp, p.mate)

    for chip in range(chips):
        pl.when(chip != p.chip)(lambda chip=chip: o_copy(chip).start())
    rail_step(3)
    total = gain_own[...]
    for i in range(1, slots):
        g_copy(i).wait_recv()
        total = total + gain_in[i]
    gain_mid[...] = total
    for b in range(1, grps):
        h_copy(b).start()

    tokens = tokens_ref[...].astype(wide)
    tok_grad_ref[...] = part[p.chip].astype(wide)

    @pl.when(p.chip > 0)
    def _():
        to_right(p.chip).wait_recv()
        tok_grad_ref[...] += left_in[p.chip].astype(wide)

    @pl.when(p.chip < last)
    def _():
        to_left(p.chip).wait_recv()
        tok_grad_ref[...] += right_in[p.chip].astype(wide)

    n1g = tok_grad_ref[...]
    scale_one = lax.rsqrt(jnp.mean(tokens * tokens, axis=-1, keepdims=True) + EPS)
    normed = tokens * scale_one
    lifted = n1g * gain_one
    tok_grad_ref[...] = state_grad[...] + scale_one * (
        lifted - normed * jnp.mean(lifted * normed, axis=-1, keepdims=True)
    )

    wq_grad = wgrad[0, p.core] + wm_in[0]
    for b in range(1, grps):
        w_copy(b).wait_recv()
        wq_grad = wq_grad + w_in[b].astype(wide)
    wq_grad_ref[...] = wq_grad
    wo_grad = o_terms[p.chip, p.core] + ob_in[p.chip]
    for chip in range(chips):
        pl.when(chip != p.chip)(lambda chip=chip: o_arrival(chip).wait_recv())
        wo_grad = wo_grad + jnp.where(chip == p.chip, 0.0, o_in[chip].astype(wide))
    wo_grad_ref[...] = wo_grad
    total = gain_mid[...]
    for b in range(1, grps):
        h_copy(b).wait_recv()
        total = total + gain_mid_in[b]
    gain_ref[...] = total

    for hop, kind in late_hops:
        if FIRST_HOPS[hop][0] < 3:
            m_first(hop, kind).wait_recv()
        m_first(hop, kind).wait_send()
    for kind in (2, 0, 1):
        for i in (0, 1):
            m_second(i, kind).wait_recv()
            m_second(i, kind).wait_send()
    for copy in early_copies:
        copy.wait()
    ob.wait_send()
    wm.wait_send()
    for i in range(1, slots):
        g_copy(i).wait_send()
    for b in range(1, grps):
        state_copy(b).wait_send()
        w_copy(b).wait_send()
        h_copy(b).wait_send()
    for chip in range(chips):
        km_copy(chip).wait_send()

        @pl.when(chip != p.chip)
        def _(chip=chip):
            q_copy(chip, 0).wait_send()
            q_copy(chip, 1).wait_send()
            kr_copy(chip).wait_send()
            o_copy(chip).wait_send()

        pl.when(chip > p.chip)(lambda chip=chip: to_right(chip).wait_send())
        pl.when(chip < p.chip)(lambda chip=chip: to_left(chip).wait_send())


def back_call(n2g, state, cotangent, tokens, gain_one, gain_two, attn, q_heads, kv_heads, mask, cosine, sine,
              qkv_all, out_full, n1_all, terms, owned, passing, early):
    chips = cosine.shape[0]
    grps = 4
    slots = 2 * chips
    shard, width = tokens.shape
    att, block = out_full.shape[0], terms.shape[1] // grps
    unit, half = att // (grps * slots), HD // 2
    vm, dma = pltpu.VMEM, pltpu.SemaphoreType.DMA
    anyspace = pl.BlockSpec(memory_space=pl.ANY)
    vspec = pl.BlockSpec(memory_space=pltpu.VMEM)
    low, wide = jnp.bfloat16, jnp.float32
    struct = jax.ShapeDtypeStruct
    return pl.pallas_call(
        functools.partial(back_kernel, chips, 1.0 / math.sqrt(HD)),
        out_shape=(
            struct((shard, width), wide),
            struct((half, width + HD), wide),
            struct((unit, width), wide),
            struct((2, 1, width), wide),
            struct((3, block, width), low),
            struct((3, block, width), low),
        ),
        in_specs=[vspec] * 13 + [anyspace] * 6,
        out_specs=(vspec,) * 4 + (anyspace,) * 2,
        scratch_shapes=[
            vm((att, width), low),
            vm((grps, shard, width), low),
            vm((chips, shard, width + HD), low),
            vm((grps, shard, slots * unit), low),
            vm((chips, 3, shard, HD), low),
            vm((chips, 3, shard, HD), low),
            vm((chips, 2, chips, shard, HD), low),
            vm((chips, chips, shard, HD), low),
            vm((chips, chips, shard, HD), low),
            vm((chips, shard, HD), wide),
            vm((chips, chips, shard, HD), low),
            vm((chips, shard, grps * HD), low),
            vm((chips, shard, width), low),
            vm((chips, shard, width), low),
            vm((chips, shard, width), low),
            vm((grps, 2, half, width + HD), wide),
            vm((grps, half, width + HD), wide),
            vm((grps, half, width + HD), low),
            vm((grps, half, width + HD), low),
            vm((chips, 2, unit, width), wide),
            vm((chips, unit, width), wide),
            vm((chips, unit, width), low),
            vm((chips, unit, width), low),
            vm((2, 3, block // 2, width), low),
            vm((2, 3, block // 2, width), low),
            vm((2, block, width), low),
            vm((2, 1, width), wide),
            vm((slots, 2, 1, width), wide),
            vm((2, 1, width), wide),
            vm((grps, 2, 1, width), wide),
            vm((shard, width), wide),
            dma((3,)),
            dma((grps,)), dma((grps,)),
            dma((chips, 2)), dma((chips, 2)),
            dma((chips,)), dma((chips,)),
            dma((chips,)), dma((chips,)),
            dma((2, chips)), dma((2, chips)),
            dma, dma,
            dma((grps,)), dma((grps,)),
            dma, dma,
            dma((chips,)), dma((chips,)),
            dma((6, 3)), dma((6, 3)),
            dma((5, 3)),
            dma((slots,)), dma((slots,)),
            dma((grps,)), dma((grps,)),
        ],
        compiler_params=pltpu.CompilerParams(
            collective_id=3, has_side_effects=True, vmem_limit_bytes=62 * 2**20
        ),
        name="back",
    )(n2g, state, cotangent, tokens, gain_one, gain_two, attn, q_heads, kv_heads, mask, cosine, sine,
      qkv_all, out_full, n1_all, terms, owned, passing, early)


def columns_to_owners(rows, row_unit):
    grp_count, seq_count = lax.axis_size("grp"), lax.axis_size("seq")
    tok_rows = rows.shape[0]
    split = rows.reshape(tok_rows, grp_count, seq_count, row_unit).transpose(2, 0, 1, 3)
    split = split.reshape(seq_count * tok_rows, grp_count * row_unit)
    return lax.all_to_all(split, "seq", split_axis=0, concat_axis=0, tiled=True)


def owners_to_columns(rows, row_unit):
    grp_count, seq_count = lax.axis_size("grp"), lax.axis_size("seq")
    tok_rows = rows.shape[0] // seq_count
    moved = lax.all_to_all(rows, "seq", split_axis=0, concat_axis=0, tiled=True)
    moved = moved.reshape(seq_count, tok_rows, grp_count, row_unit).transpose(1, 2, 0, 3)
    return moved.reshape(tok_rows, grp_count * seq_count * row_unit)


def plain_mlp(normed_two, cotangent_all, mlp_weight):
    contract_last, contract_first = CONTRACT_LAST, CONTRACT_FIRST
    mlp_rows = lax.all_gather(mlp_weight, "grp", axis=0, tiled=True)
    normed_two_all = lax.all_gather(normed_two, "seq", axis=0, tiled=True)
    gate_rows, upper_rows, down_rows = mlp_rows[:, 0, :], mlp_rows[:, 1, :], mlp_rows[:, 2, :]
    gate_vals = lax.dot_general(
        normed_two_all, gate_rows, contract_last, preferred_element_type=jnp.float32
    )
    upper_vals = lax.dot_general(
        normed_two_all, upper_rows, contract_last, preferred_element_type=jnp.float32
    )
    unit_wide, pull_back = jax.vjp(swish_product, gate_vals, upper_vals)
    unit_low = unit_wide.astype(jnp.bfloat16)
    unit_grad = lax.dot_general(
        cotangent_all, down_rows, contract_last, preferred_element_type=jnp.float32
    )
    gate_grad, upper_grad = pull_back(unit_grad)
    gate_grad = gate_grad.astype(jnp.bfloat16)
    upper_grad = upper_grad.astype(jnp.bfloat16)
    input_grad = jnp.dot(gate_grad, gate_rows, preferred_element_type=jnp.float32) + jnp.dot(
        upper_grad, upper_rows, preferred_element_type=jnp.float32
    )
    grad_part = lax.psum_scatter(
        input_grad.astype(jnp.bfloat16), "seq", scatter_dimension=0, tiled=True
    ).astype(jnp.float32)
    out_part = lax.psum_scatter(
        jnp.dot(unit_low, down_rows, preferred_element_type=jnp.float32).astype(jnp.bfloat16),
        "seq",
        scatter_dimension=0,
        tiled=True,
    ).astype(jnp.float32)
    mlp_terms = jnp.stack(
        [
            lax.dot_general(
                gate_grad, normed_two_all, contract_first, preferred_element_type=jnp.float32
            ),
            lax.dot_general(
                upper_grad, normed_two_all, contract_first, preferred_element_type=jnp.float32
            ),
            lax.dot_general(
                unit_low, cotangent_all, contract_first, preferred_element_type=jnp.float32
            ),
        ],
        axis=1,
    )
    mlp_grad = lax.psum_scatter(mlp_terms, "grp", scatter_dimension=0, tiled=True)
    return grad_part, out_part, mlp_grad


def padded_rows(mlp_weight):
    rows = mlp_weight.transpose(1, 0, 2)
    return jnp.pad(rows, ((0, 0), (0, -rows.shape[1] % 32), (0, 0)))


def per_device(
    tokens,
    cotangent,
    shard_segment,
    gain_attn,
    qkv_weight,
    qkv_bias,
    out_weight,
    gain_mlp,
    mlp_weight,
):
    tok_rows = tokens.shape[0]
    seq_count = lax.axis_size("seq")
    grp_count = lax.axis_size("grp")
    group_tok = tok_rows * seq_count
    heads_per = H // KVH
    kv_width = KVH * HD
    att_width = H * HD
    query_rows = heads_per * tok_rows
    score_scale = 1.0 / math.sqrt(HD)
    contract_last = CONTRACT_LAST
    contract_first = CONTRACT_FIRST
    seq_place = lax.axis_index("seq")
    grp_place = lax.axis_index("grp")
    use_kernels = (seq_count, grp_count, H, KVH, HD) == (8, 4, 12, 2, 128)
    if use_kernels:
        freqs = THETA ** (-(jnp.arange(HD // 2, dtype=jnp.float32) * 2.0) / HD)
        freqs = jnp.concatenate([freqs, freqs])[None, :]
        gain_rows = (gain_attn[None, :], gain_mlp[None, :])
        own_rows = padded_rows(mlp_weight)
        (
            attn_wide, state, cosine, sine, mask, q_heads, kv_heads, n1_all, n2_all, cot_all, out_all,
            qkv_all, columns, *peer_rows
        ) = front_call(
            tokens, *gain_rows, shard_segment, freqs, qkv_bias[None, :], cotangent, qkv_weight, out_weight,
            own_rows,
        )
        by_slot = lambda rows: rows.reshape((seq_count,) + rows.shape[2:])
        grad_part, out_part, mlp_terms, owned, passing, early = mlp_call(
            by_slot(n2_all), by_slot(cot_all), columns, [own_rows, *peer_rows]
        )
        output = (state + out_part).astype(jnp.bfloat16)
        token_grad, qkv_terms, out_grad, gain_sums, direct, second = back_call(
            grad_part, state, cotangent, tokens, *gain_rows, attn_wide, q_heads, kv_heads, mask,
            cosine, sine, qkv_all.reshape(-1, qkv_all.shape[-1]),
            out_all.reshape(att_width, -1), n1_all, mlp_terms, owned, passing, early,
        )
        units = mlp_weight.shape[0]
        mlp_sums = sum(
            rows[:, :units].astype(jnp.float32) for rows in (mlp_terms, direct, second)
        )
        width = tokens.shape[1]
        own = width // (grp_count * seq_count)
        gain_parts = lax.dynamic_slice_in_dim(
            gain_sums[:, 0], (grp_place * seq_count + seq_place) * own, own, 1
        )
        return (
            output,
            token_grad,
            gain_parts[0],
            qkv_terms[:, :width],
            qkv_terms[:, width],
            out_grad,
            gain_parts[1],
            mlp_sums.transpose(1, 0, 2),
        )
    segments = lax.dynamic_index_in_dim(shard_segment, grp_place, 0, keepdims=False)
    starts = shard_starts(segments, tok_rows, group_tok // 2)
    shard_order = jnp.arange(seq_count, dtype=jnp.int32)
    own_seg = jnp.sum(jnp.where(shard_order == seq_place, segments, 0))
    own_start = jnp.sum(jnp.where(shard_order == seq_place, starts, 0))
    positions = own_start + jnp.arange(tok_rows, dtype=jnp.int32)
    cosine_table, sine_table = rotary_tables(positions, HD)
    query_pos = jnp.tile(positions, heads_per)
    tokens_wide = tokens.astype(jnp.float32)
    gain_one = gain_attn.astype(jnp.float32)
    gain_two = gain_mlp.astype(jnp.float32)
    normed_one = rms_scale(tokens_wide, gain_one).astype(jnp.bfloat16)
    normed_one_all = lax.all_gather(normed_one, "seq", axis=0, tiled=True)
    qkv_rows = lax.all_gather(qkv_weight, "grp", axis=0, tiled=True)
    bias_rows = lax.all_gather(qkv_bias, "grp", axis=0, tiled=True)
    cotangent_all = lax.all_gather(cotangent, "seq", axis=0, tiled=True)
    out_full = lax.all_gather(out_weight, AXES, axis=0, tiled=True)
    projected = lax.dot_general(
        normed_one_all, qkv_rows, contract_last, preferred_element_type=jnp.float32
    )
    projected = (projected + bias_rows.astype(jnp.float32)[None, :]).astype(jnp.bfloat16)
    projected = owners_to_columns(projected, qkv_weight.shape[0]).astype(jnp.float32)
    query_rot = rotate(
        projected[:, :att_width].reshape(tok_rows, H, HD), cosine_table, sine_table
    ).astype(jnp.bfloat16)
    key_rot = rotate(
        projected[:, att_width : att_width + kv_width].reshape(tok_rows, KVH, HD),
        cosine_table,
        sine_table,
    ).astype(jnp.bfloat16)
    value_low = projected[:, att_width + kv_width :].astype(jnp.bfloat16)
    keys_all, values_all = (
        lax.all_gather(key_rot.reshape(tok_rows, kv_width), "seq", axis=0, tiled=True),
        lax.all_gather(value_low, "seq", axis=0, tiled=True),
    )
    queries = (
        query_rot.reshape(tok_rows, KVH, heads_per, HD)
        .transpose(1, 2, 0, 3)
        .reshape(KVH, query_rows, HD)
    )
    key_block = min(512, group_tok)
    block_count = group_tok // key_block
    block_order = jnp.arange(block_count, dtype=jnp.int32)

    def block_mask(block_index):
        key_index = block_index * key_block + jnp.arange(key_block, dtype=jnp.int32)
        key_shard = key_index // tok_rows
        onehot = key_shard[:, None] == shard_order[None, :]
        key_seg = jnp.sum(jnp.where(onehot, segments[None, :], 0), axis=1)
        key_pos = jnp.sum(jnp.where(onehot, starts[None, :], 0), axis=1) + key_index % tok_rows
        visible = (key_seg == 0) | (key_seg == own_seg)
        return visible[None, :] & (key_pos[None, :] <= query_pos[:, None])

    def block_keys(block_index):
        key_part = lax.dynamic_slice_in_dim(
            keys_all, block_index * key_block, key_block, 0
        ).reshape(key_block, KVH, HD)
        value_part = lax.dynamic_slice_in_dim(
            values_all, block_index * key_block, key_block, 0
        ).reshape(key_block, KVH, HD)
        return (key_part, value_part)

    def block_scores(key_part):
        return (
            jnp.einsum("krd,jkd->krj", queries, key_part, preferred_element_type=jnp.float32)
            * score_scale
        )

    def stat_step(stats_now, block_index):
        allowed = block_mask(block_index)

        def stat_visit(current):
            top_old, total_old = current
            key_part, value_part = block_keys(block_index)
            scores = jnp.where(allowed[None], block_scores(key_part), -1e30)
            top_new = jnp.maximum(top_old, jnp.max(scores, axis=-1))
            weights = jnp.where(allowed[None], jnp.exp(scores - top_new[..., None]), 0.0)
            return (top_new, total_old * jnp.exp(top_old - top_new) + jnp.sum(weights, axis=-1))

        return (lax.cond(jnp.any(allowed), stat_visit, lambda current: current, stats_now), None)

    start_stats = (
        jnp.full((KVH, query_rows), -1e30, jnp.float32),
        jnp.zeros((KVH, query_rows), jnp.float32),
    )
    (top_all, total_all), unused = lax.scan(stat_step, start_stats, block_order)
    log_total = top_all + jnp.log(total_all)

    def mix_step(mixed_sum, block_index):
        allowed = block_mask(block_index)

        def mix_visit(current):
            key_part, value_part = block_keys(block_index)
            prob_low = jnp.where(
                allowed[None], jnp.exp(block_scores(key_part) - log_total[..., None]), 0.0
            ).astype(jnp.bfloat16)
            return current + jnp.einsum(
                "krj,jkd->krd", prob_low, value_part, preferred_element_type=jnp.float32
            )

        return (lax.cond(jnp.any(allowed), mix_visit, lambda current: current, mixed_sum), None)

    mixed_sum, unused = lax.scan(
        mix_step, jnp.zeros((KVH, query_rows, HD), jnp.float32), block_order
    )
    attn_wide = (
        mixed_sum.reshape(KVH, heads_per, tok_rows, HD)
        .transpose(2, 0, 1, 3)
        .reshape(tok_rows, att_width)
    )
    attn_low = attn_wide.astype(jnp.bfloat16)
    attn_proj = jnp.dot(attn_low, out_full, preferred_element_type=jnp.float32)
    state = tokens_wide + attn_proj
    normed_two = rms_scale(state, gain_two).astype(jnp.bfloat16)
    grad_part, out_part, mlp_grad = plain_mlp(normed_two, cotangent_all, mlp_weight)
    output = (state + out_part).astype(jnp.bfloat16)
    unused_state, norm_two_back = jax.vjp(rms_scale, state, gain_two)
    state_norm_grad, gain_two_grad = norm_two_back(grad_part)
    state_grad = state_norm_grad + cotangent.astype(jnp.float32)
    state_low = state_grad.astype(jnp.bfloat16)
    attn_grad = lax.dot_general(
        state_low, out_full, contract_last, preferred_element_type=jnp.float32
    )
    attn_grad_low = attn_grad.astype(jnp.bfloat16)
    attn_owned = columns_to_owners(attn_low, out_weight.shape[0])
    state_low_all = lax.all_gather(state_low, "seq", axis=0, tiled=True)
    out_grad = lax.psum_scatter(
        lax.dot_general(
            attn_owned, state_low_all, contract_first, preferred_element_type=jnp.float32
        ),
        "grp",
        scatter_dimension=0,
        tiled=True,
    )
    grad_heads = (
        attn_grad_low.reshape(tok_rows, KVH, heads_per, HD)
        .transpose(1, 2, 0, 3)
        .reshape(KVH, query_rows, HD)
    )
    delta_rows = jnp.sum(
        (attn_grad_low.astype(jnp.float32) * attn_wide).reshape(tok_rows, H, HD), axis=-1
    )
    delta_rows = (
        delta_rows.reshape(tok_rows, KVH, heads_per).transpose(1, 2, 0).reshape(KVH, query_rows)
    )

    def back_step(query_grad, block_index):
        allowed = block_mask(block_index)

        def back_visit(current):
            key_part, value_part = block_keys(block_index)
            prob_vals = jnp.where(
                allowed[None], jnp.exp(block_scores(key_part) - log_total[..., None]), 0.0
            )
            prob_grad = jnp.einsum(
                "krd,jkd->krj", grad_heads, value_part, preferred_element_type=jnp.float32
            )
            score_grad = (prob_vals * (prob_grad - delta_rows[..., None])).astype(jnp.bfloat16)
            new_grad = (
                current
                + jnp.einsum(
                    "krj,jkd->krd", score_grad, key_part, preferred_element_type=jnp.float32
                )
                * score_scale
            )
            key_grad = (
                jnp.einsum("krj,krd->jkd", score_grad, queries, preferred_element_type=jnp.float32)
                * score_scale
            )
            value_grad = jnp.einsum(
                "krj,krd->jkd",
                prob_vals.astype(jnp.bfloat16),
                grad_heads,
                preferred_element_type=jnp.float32,
            )
            return (
                new_grad,
                (key_grad.reshape(key_block, kv_width), value_grad.reshape(key_block, kv_width)),
            )

        def skip_block(current):
            blank_rows = jnp.zeros((key_block, kv_width), jnp.float32)
            return (current, (blank_rows, blank_rows))

        return lax.cond(jnp.any(allowed), back_visit, skip_block, query_grad)

    query_grad, (key_grads, value_grads) = lax.scan(
        back_step, jnp.zeros((KVH, query_rows, HD), jnp.float32), block_order
    )
    key_own, value_own = (
        lax.psum_scatter(
            key_grads.reshape(group_tok, kv_width).astype(jnp.bfloat16),
            "seq",
            scatter_dimension=0,
            tiled=True,
        ).astype(jnp.float32),
        lax.psum_scatter(
            value_grads.reshape(group_tok, kv_width).astype(jnp.bfloat16),
            "seq",
            scatter_dimension=0,
            tiled=True,
        ).astype(jnp.float32),
    )
    query_back = unrotate(
        query_grad.reshape(KVH, heads_per, tok_rows, HD)
        .transpose(2, 0, 1, 3)
        .reshape(tok_rows, H, HD),
        cosine_table,
        sine_table,
    )
    key_back = unrotate(key_own.reshape(tok_rows, KVH, HD), cosine_table, sine_table)
    qkv_grad_low = jnp.concatenate(
        [query_back.reshape(tok_rows, att_width), key_back.reshape(tok_rows, kv_width), value_own],
        axis=1,
    ).astype(jnp.bfloat16)
    qkv_grad_owned = columns_to_owners(qkv_grad_low, qkv_weight.shape[0])
    bias_terms = jnp.sum(qkv_grad_owned.astype(jnp.float32), axis=0)
    normed_one_grad = lax.psum_scatter(
        jnp.dot(qkv_grad_owned, qkv_rows, preferred_element_type=jnp.float32).astype(jnp.bfloat16),
        "seq",
        scatter_dimension=0,
        tiled=True,
    ).astype(jnp.float32)
    qkv_grad = lax.psum_scatter(
        lax.dot_general(
            qkv_grad_owned, normed_one_all, contract_first, preferred_element_type=jnp.float32
        ),
        "grp",
        scatter_dimension=0,
        tiled=True,
    )
    unused_tokens, norm_one_back = jax.vjp(rms_scale, tokens_wide, gain_one)
    token_norm_grad, gain_one_grad = norm_one_back(normed_one_grad)
    token_grad = token_norm_grad + state_grad
    bias_part = lax.psum_scatter(bias_terms, "grp", scatter_dimension=0, tiled=True)
    gain_one_part, gain_two_part = (
        lax.psum_scatter(gain_one_grad, AXES, scatter_dimension=0, tiled=True),
        lax.psum_scatter(gain_two_grad, AXES, scatter_dimension=0, tiled=True),
    )
    return (
        output,
        token_grad,
        gain_one_part,
        qkv_grad,
        bias_part,
        out_grad,
        gain_two_part,
        mlp_grad,
    )


def solution(mesh):
    return jax.shard_map(
        per_device,
        mesh=mesh,
        in_specs=(
            P(("grp", "seq"), None),
            P(("grp", "seq"), None),
            P(),
            P(),
            P(("grp", "seq"), None),
            P(("grp", "seq")),
            P(("grp", "seq"), None),
            P(),
            P(("grp", "seq"), None, None),
        ),
        out_specs=(
            P(("grp", "seq"), None),
            P(("grp", "seq"), None),
            P(("grp", "seq")),
            P(("grp", "seq"), None),
            P(("grp", "seq")),
            P(("grp", "seq"), None),
            P(("grp", "seq")),
            P(("grp", "seq"), None, None),
        ),
        check_vma=False,
    )
```

```python
import functools
import math

import jax
import jax.numpy as jnp
import numpy as np
from jax import lax
from jax.experimental import pallas as pl
from jax.experimental.pallas import tpu as pltpu
from jax.sharding import PartitionSpec as P

H = 12
KVH = 2
HD = 128
FF = 8960


EPS = 1e-06
THETA = 10000.0


def rms_scale(values, gain_vec):
    return values * lax.rsqrt(jnp.mean(values * values, axis=-1, keepdims=True) + EPS) * gain_vec


def rotary_tables(positions, head_dim):
    half_dim = head_dim // 2
    freqs = THETA ** (-(jnp.arange(half_dim, dtype=jnp.float32) * 2.0) / head_dim)
    angles = positions.astype(jnp.float32)[:, None] * freqs[None, :]
    cosine_table = jnp.concatenate([jnp.cos(angles), jnp.cos(angles)], axis=-1)
    sine_table = jnp.concatenate([jnp.sin(angles), jnp.sin(angles)], axis=-1)
    return (cosine_table, sine_table)


def rotate(values, cosine_table, sine_table):
    half_dim = values.shape[-1] // 2
    turned = jnp.concatenate([-values[..., half_dim:], values[..., :half_dim]], axis=-1)
    return values * cosine_table[:, None, :] + turned * sine_table[:, None, :]


def unrotate(grad_rows, cosine_table, sine_table):
    half_dim = grad_rows.shape[-1] // 2
    scaled = grad_rows * sine_table[:, None, :]
    turned = jnp.concatenate([scaled[..., half_dim:], -scaled[..., :half_dim]], axis=-1)
    return grad_rows * cosine_table[:, None, :] + turned


def shard_starts(segments, tok_dev, prompt_len):
    shard_total = segments.shape[0]
    shard_order = jnp.arange(shard_total, dtype=jnp.int32)
    same_seg = segments[:, None] == segments[None, :]
    first_shard = jnp.min(jnp.where(same_seg, shard_order[None, :], shard_total), axis=1)
    cont_start = prompt_len + (shard_order - first_shard) * tok_dev
    return jnp.where(segments == 0, shard_order * tok_dev, cont_start)


def swish_product(gate_vals, upper_vals):
    return jax.nn.silu(gate_vals) * upper_vals


AXES = ("grp", "seq")
CONTRACT_LAST = (((1,), (1,)), ((), ()))
CONTRACT_FIRST = (((0,), (0,)), ((), ()))


MESH = pl.DeviceIdType.MESH


def remote(src, dst, send_sem, recv_sem, grp, seq):
    return pltpu.make_async_remote_copy(
        src_ref=src, dst_ref=dst, send_sem=send_sem, recv_sem=recv_sem,
        device_id=(grp, seq), device_id_type=MESH,
    )


def nearest_chip(place, order, chips):
    both = 2 * jnp.minimum(place, chips - 1 - place)
    offset = (order + 1) // 2
    side = jnp.where((order % 2 == 1) == (place < chips - 1 - place), -1, 1)
    near = place + side * offset
    rest = jnp.where(place < chips - 1 - place, order, chips - 1 - order)
    return jnp.where(order <= both, near, rest)


class Place:
    def __init__(self, chips):
        self.chips = chips
        self.grp, self.seq = lax.axis_index("grp"), lax.axis_index("seq")
        self.chip, self.core = self.seq // 2, self.seq % 2
        self.mate = self.seq + 1 - 2 * self.core

    def peer(self, offset):
        low, high = self.grp % 2, self.grp // 2
        low = 1 - low if offset % 2 else low
        high = 1 - high if offset // 2 else high
        return 2 * high + low

    def barrier(self, grps):
        barrier = pltpu.get_barrier_semaphore()
        for chip in range(self.chips):
            @pl.when(chip != self.chip)
            def _(chip=chip):
                pl.semaphore_signal(
                    barrier, inc=1, device_id=(self.grp, 2 * chip + self.core), device_id_type=MESH
                )
        pl.semaphore_signal(barrier, inc=1, device_id=(self.grp, self.mate), device_id_type=MESH)
        for offset in range(1, grps):
            pl.semaphore_signal(
                barrier, inc=1, device_id=(self.peer(offset), self.seq), device_id_type=MESH
            )
        pl.semaphore_wait(barrier, self.chips - 1 + 1 + grps - 1)


class RailGather:
    def __init__(self, place, view, send_sem, recv_sem):
        self.place, self.view, self.send_sem, self.recv_sem = place, view, send_sem, recv_sem

    def copy(self, way, chip, core):
        p = self.place
        to = (p.seq + 2, p.seq - 2, p.mate)[way]
        return remote(
            self.view(chip, core), self.view(chip, core), self.send_sem.at[way, chip],
            self.recv_sem.at[chip, core], p.grp, to,
        )

    def start(self):
        p = self.place
        pl.when(p.chip < p.chips - 1)(lambda: self.copy(0, p.chip, p.core).start())
        pl.when(p.chip > 0)(lambda: self.copy(1, p.chip, p.core).start())
        self.copy(2, p.chip, p.core).start()

    def forward(self, step):
        p = self.place

        @pl.when(p.chip - step >= 0)
        def _():
            chip = p.chip - step
            self.copy(2, chip, p.core).wait_recv()
            pl.when(p.chip < p.chips - 1)(lambda: self.copy(0, chip, p.core).start())
            self.copy(2, chip, p.core).start()

        @pl.when(p.chip + step < p.chips)
        def _():
            chip = p.chip + step
            self.copy(2, chip, p.core).wait_recv()
            pl.when(p.chip > 0)(lambda: self.copy(1, chip, p.core).start())
            self.copy(2, chip, p.core).start()

    def wait_mate(self, chip):
        self.copy(2, chip, 1 - self.place.core).wait_recv()

    def drain(self):
        p = self.place
        for chip in range(p.chips):
            self.copy(2, chip, p.core).wait_send()
            pl.when((chip <= p.chip) & (p.chip < p.chips - 1))(
                lambda chip=chip: self.copy(0, chip, p.core).wait_send()
            )
            pl.when((chip >= p.chip) & (p.chip > 0))(
                lambda chip=chip: self.copy(1, chip, p.core).wait_send()
            )


class LineScatter:
    def __init__(self, place, part, mate_in, left_in, right_in, send_sem, recv_sem):
        self.place, self.part = place, part
        self.mate_in, self.left_in, self.right_in = mate_in, left_in, right_in
        self.send_sem, self.recv_sem = send_sem, recv_sem

    def copy(self, way, src, landing, r, chip, to):
        return remote(
            src, landing.at[r, chip], self.send_sem.at[way, r, chip], self.recv_sem.at[way, r, chip],
            self.place.grp, to,
        )

    def to_mate(self, r, chip):
        p = self.place
        return self.copy(0, self.part.at[r, 2 * chip + 1 - p.core], self.mate_in, r, chip, p.mate)

    def to_right(self, r, chip):
        p = self.place
        return self.copy(1, self.part.at[r, 2 * chip + p.core], self.left_in, r, chip, p.seq + 2)

    def to_left(self, r, chip):
        p = self.place
        return self.copy(2, self.part.at[r, 2 * chip + p.core], self.right_in, r, chip, p.seq - 2)

    def step(self, r, chip):
        p = self.place
        last = p.chips - 1
        slot = 2 * chip + p.core

        @pl.when(chip != p.chip)
        def _():
            self.to_mate(r, chip).wait_recv()
            total = self.part[r, slot].astype(jnp.float32) + self.mate_in[r, chip].astype(jnp.float32)
            self.part[r, slot] = total.astype(jnp.bfloat16)

        @pl.when(chip > p.chip)
        def _():
            @pl.when(p.chip > 0)
            def _():
                self.to_right(r, chip).wait_recv()
                self.part[r, slot] = (
                    self.part[r, slot].astype(jnp.float32) + self.left_in[r, chip].astype(jnp.float32)
                ).astype(jnp.bfloat16)

            self.to_right(r, chip).start()

        @pl.when(chip < p.chip)
        def _():
            @pl.when(p.chip < last)
            def _():
                self.to_left(r, chip).wait_recv()
                self.part[r, slot] = (
                    self.part[r, slot].astype(jnp.float32) + self.right_in[r, chip].astype(jnp.float32)
                ).astype(jnp.bfloat16)

            self.to_left(r, chip).start()

    def finish(self, r, out_ref):
        p = self.place
        self.to_mate(r, p.chip).wait_recv()
        out_ref[...] = self.part[r, p.seq].astype(jnp.float32) + self.mate_in[r, p.chip].astype(jnp.float32)

        @pl.when(p.chip > 0)
        def _():
            self.to_right(r, p.chip).wait_recv()
            out_ref[...] += self.left_in[r, p.chip].astype(jnp.float32)

        @pl.when(p.chip < p.chips - 1)
        def _():
            self.to_left(r, p.chip).wait_recv()
            out_ref[...] += self.right_in[r, p.chip].astype(jnp.float32)

    def drain(self, r):
        p = self.place
        for other in range(p.chips):
            self.to_mate(r, other).wait_send()
            pl.when(other > p.chip)(lambda other=other: self.to_right(r, other).wait_send())
            pl.when(other < p.chip)(lambda other=other: self.to_left(r, other).wait_send())


def front_kernel(chips, scale,
                 tokens_ref, gain_one_ref, gain_two_ref, segment_ref, freq_ref, bias_ref,
                 cot_ref, wq_ref, wo_ref, wm_ref,
                 attn_ref, state_ref, cos_ref, sin_ref, mask_ref, q_out_ref, kv_out_ref, n1_all_ref, n2_all_ref,
                 cot_all_ref, wo_all_ref, wq_all_ref, columns_ref, wm1_ref, wm2_ref, wm3_ref,
                 nbuf, n2buf, wq, wo, bias_own, bias, stage, qbuf, kvbuf, columns,
                 lsem, n_send, n_recv, n2_send, n2_recv, c_send, c_recv, o_send, o_recv, ox_send, ox_recv,
                 om_send, om_recv, wq_send, wq_recv, b_send, b_recv, m_send, m_recv, q_send, q_recv, k_send, k_recv):
    p = Place(chips)
    grps = 4
    half = wq_ref.shape[0]
    rows = pl.ds(p.core * half, half)
    mates_rows = pl.ds((1 - p.core) * half, half)
    wm_refs = (wm_ref, wm1_ref, wm2_ref, wm3_ref)
    part = wm_ref.shape[1] // 2

    own = [
        pltpu.make_async_copy(wq_ref, wq.at[0, rows], lsem.at[0]),
        pltpu.make_async_copy(wo_ref, wo.at[p.grp, p.chip, p.core], lsem.at[2]),
        pltpu.make_async_copy(cot_ref, cot_all_ref.at[p.chip, p.core], lsem.at[3]),
    ]
    for copy in own:
        copy.start()
    tokens = tokens_ref[...].astype(jnp.float32)
    nbuf[p.chip, p.core] = rms_scale(tokens, gain_one_ref[...].astype(jnp.float32)).astype(jnp.bfloat16)
    shard = tokens.shape[0]
    lane = lax.broadcasted_iota(jnp.int32, (1, 2 * half), 1)
    bias_wide = bias_ref[...].astype(jnp.float32)
    bias_pair = jnp.concatenate([bias_wide, bias_wide], axis=1)
    bias_own[...] = jnp.broadcast_to(jnp.where(lane // half == p.core, bias_pair, 0.0), bias_own.shape)
    bias[0, p.core] = bias_own[...]
    p.barrier(grps)

    n1_line = RailGather(p, lambda chip, core: nbuf.at[chip, core], n_send, n_recv)
    cot_line = RailGather(p, lambda chip, core: cot_all_ref.at[chip, core], c_send, c_recv)
    n2_line = RailGather(p, lambda chip, core: n2buf.at[chip, core], n2_send, n2_recv)
    out_line = RailGather(p, lambda chip, core: wo.at[p.grp, chip, core], o_send, o_recv)

    def wq_direct(b):
        return remote(wq_ref, wq.at[b, rows], wq_send.at[0, b], wq_recv.at[b, 0], p.peer(b), p.seq)

    def wq_mate(b):
        return remote(wq.at[b, rows], wq.at[b, rows], wq_send.at[1, b], wq_recv.at[b, 1], p.grp, p.mate)

    def bias_direct(b):
        return remote(bias_own, bias.at[b, p.core], b_send.at[0, b], b_recv.at[b, 0], p.peer(b), p.seq)

    def bias_mate(b):
        return remote(bias.at[b, p.core], bias.at[b, p.core], b_send.at[1, b], b_recv.at[b, 1], p.grp, p.mate)

    def m_part(ref, i, j):
        return ref.at[j, pl.ds(i * part, part)]

    def m_direct(b, i, j):
        return remote(
            m_part(wm_ref, i, j), m_part(wm_refs[b], i, j), m_send.at[b, i, j], m_recv.at[b, i, j],
            p.peer(b), p.seq,
        )

    def m_forward(b, j):
        return remote(
            m_part(wm_refs[b], b - 1, j), m_part(wm3_ref, b - 1, j), m_send.at[3, b - 1, j],
            m_recv.at[3, b - 1, j], p.peer(3 - b), p.seq,
        )

    def out_cross(b, chip):
        view = wo.at[p.grp, chip, p.core]
        return remote(view, view, ox_send.at[b, chip], ox_recv.at[b, chip], p.peer(b), p.seq)

    def out_arrival(b, chip):
        view = wo.at[p.peer(b), chip, p.core]
        return remote(view, view, ox_send.at[b, chip], ox_recv.at[b, chip], p.grp, p.mate)

    def out_mate(b, core):
        view = wo.at[p.peer(b), :, core]
        return remote(view, view, om_send.at[b], om_recv.at[b], p.grp, p.mate)

    def q_copy(chip):
        return remote(
            stage.at[chip, pl.ds(0, 3)], qbuf.at[p.chip], q_send.at[chip], q_recv.at[p.chip],
            p.grp, 2 * chip + p.core,
        )

    def q_arrival(chip):
        return remote(stage.at[chip, pl.ds(0, 3)], qbuf.at[chip], q_send.at[chip], q_recv.at[chip], p.grp, p.mate)

    def k_copy(chip, to_chip):
        return remote(
            stage.at[chip, 3], kvbuf.at[p.chip, p.core, chip], k_send.at[0, chip, to_chip],
            k_recv.at[p.chip, p.core, chip], p.grp, 2 * to_chip + p.core,
        )

    def k_mate(head, chip, src=None):
        view = kvbuf.at[head, p.core, chip]
        return remote(
            view if src is None else src, view, k_send.at[1, head, chip],
            k_recv.at[head, p.core, chip], p.grp, p.mate,
        )

    def k_arrival(head, core, chip):
        view = kvbuf.at[head, core, chip]
        return remote(view, view, k_send.at[1, head, chip], k_recv.at[head, core, chip], p.grp, p.mate)

    def make_tables():
        segs = [segment_ref[p.grp, t] for t in range(2 * chips)]
        starts = []
        for t in range(2 * chips):
            first = jnp.int32(t)
            for other in reversed(range(t)):
                first = jnp.where(segs[other] == segs[t], jnp.int32(other), first)
            starts.append(
                jnp.where(segs[t] == 0, jnp.int32(t * shard), chips * shard + (t - first) * shard)
            )

        def own_of(values):
            own = values[0]
            for t in range(1, 2 * chips):
                own = jnp.where(p.seq == t, values[t], own)
            return own

        own_seg, own_start = own_of(segs), own_of(starts)
        row = lax.broadcasted_iota(jnp.int32, (shard, 2 * half), 0)
        column = lax.broadcasted_iota(jnp.int32, (shard, 2 * half), 1)
        freq = freq_ref[...]
        sign = jnp.where(column < half, -1.0, 1.0)
        for chip in range(chips):
            start = jnp.where(p.core == 0, starts[2 * chip], starts[2 * chip + 1])
            angle = (start + row).astype(jnp.float32) * freq
            cos_ref[chip] = jnp.cos(angle)
            sin_ref[chip] = jnp.sin(angle) * sign
        for core in range(2):
            for chip in range(chips):
                t = 2 * chip + core
                seen = jnp.where((segs[t] == 0) | (segs[t] == own_seg), jnp.int32(1), jnp.int32(0))
                allowed = (starts[t] + column <= own_start + row) & (row * 0 + seen > 0)
                block = core * chips + chip
                mask_ref[:, block * shard : (block + 1) * shard] = jnp.where(allowed, 0.0, -1e30)

    own[0].wait()
    for b in range(1, grps):
        wq_direct(b).start()
        bias_direct(b).start()
    wq_mate(0).start()
    bias_mate(0).start()
    n1_line.start()
    own[1].wait()
    out_line.start()
    for b in range(1, grps):
        wq_direct(b).wait_recv()
        wq_mate(b).start()
        bias_direct(b).wait_recv()
        bias_mate(b).start()
    for b in range(1, grps):
        out_cross(b, p.chip).start()
    for j in range(3):
        m_direct(1, 0, j).start()
        m_direct(2, 1, j).start()
    make_tables()
    for b in range(grps):
        wq_mate(b).wait_recv()
        bias_mate(b).wait_recv()

    @pl.loop(0, chips)
    def _(order):
        @pl.when(order > 0)
        def _():
            n1_line.forward(order)
            out_line.forward(order)
            for b in range(1, grps):
                pl.when(p.chip - order >= 0)(lambda b=b: out_cross(b, p.chip - order).start())
                pl.when(p.chip + order < chips)(lambda b=b: out_cross(b, p.chip + order).start())

        at = nearest_chip(p.chip, order, chips)
        x = nbuf[at, p.core]
        weights = wq[...].reshape(grps * 2 * half, x.shape[1])
        rows_all = lax.dot_general(x, weights, CONTRACT_LAST, preferred_element_type=jnp.float32)
        cosine, sine = cos_ref[at], sin_ref[at]
        for b in range(grps):
            u = rows_all[:, 2 * half * b : 2 * half * (b + 1)] + (bias[b, 0, 0:1] + bias[b, 1, 0:1])
            turned = u * cosine + pltpu.roll(u, half, 1) * sine
            place = p.peer(b)
            keep = jnp.where((place == grps - 1) & (p.chip >= chips // 2), 1.0, 0.0)
            value = (u * keep + turned * (1.0 - keep)).astype(jnp.bfloat16)
            stage[at, place] = value

            @pl.when(place == grps - 1)
            def _(value=value):
                kvbuf[p.chip, p.core, at] = value

            @pl.when((place < grps - 1) & (at == p.chip))
            def _(value=value, place=place):
                qbuf[p.chip, place] = value

        pl.when(at != p.chip)(lambda: q_copy(at).start())
        for to_chip in range(chips):
            pl.when(to_chip != p.chip)(lambda to_chip=to_chip: k_copy(at, to_chip).start())
        k_mate(p.chip, at, stage.at[at, 3]).start()


    @pl.loop(0, chips)
    def _(order):
        for head in range(chips):
            @pl.when(head != p.chip)
            def _(head=head):
                chip = nearest_chip(head, order, chips)
                k_arrival(head, p.core, chip).wait_recv()
                k_mate(head, chip).start()

    for chip in range(chips):
        pl.when(chip != p.chip)(lambda chip=chip: q_arrival(chip).wait_recv())
        for head in range(chips):
            k_arrival(head, 1 - p.core, chip).wait_recv()
    own[2].wait()
    cot_line.start()
    for j in (0, 1):
        for b in (1, 2):
            m_direct(b, b - 1, j).wait_recv()
            m_forward(b, j).start()
    for j in range(3):
        m_direct(1, 1, j).start()
        m_direct(2, 0, j).start()

    mask = mask_ref[...]
    heads_per = H // KVH
    for kv in range(KVH):
        heads = [kv * heads_per + i for i in range(heads_per)]
        queries = jnp.concatenate([qbuf[h % chips, h // chips] for h in heads], axis=0)
        keys = kvbuf[kv].reshape(mask.shape[1], 2 * half)
        values = kvbuf[KVH + kv].reshape(mask.shape[1], 2 * half)
        scores = lax.dot_general(queries, keys, CONTRACT_LAST, preferred_element_type=jnp.float32) * scale
        scores = scores.reshape(heads_per, shard, mask.shape[1]) + mask[None]
        weights = jnp.exp(scores - jnp.max(scores, axis=-1, keepdims=True))
        inverse = 1.0 / jnp.sum(weights, axis=-1, keepdims=True)
        probs = (weights * inverse).astype(jnp.bfloat16).reshape(heads_per * shard, mask.shape[1])
        mixed = jnp.dot(probs, values, preferred_element_type=jnp.float32)
        for i, h in enumerate(heads):
            attn_ref[:, h * 2 * half : (h + 1) * 2 * half] = mixed[i * shard : (i + 1) * shard]
        cot_line.forward(kv + 1)

    for b in range(1, grps):
        for chip in range(chips):
            out_arrival(b, chip).wait_recv()
        out_mate(b, p.core).start()
    for b in (1, 2):
        m_direct(b, b - 1, 2).wait_recv()
        m_forward(b, 2).start()
    attn_low = attn_ref[...].astype(jnp.bfloat16)
    unit = wo.shape[3]
    for owner in range(grps):
        columns[owner] = attn_low[:, owner * columns.shape[2] : (owner + 1) * columns.shape[2]]
    for b in range(1, grps):
        out_mate(b, 1 - p.core).wait_recv()
    for chip in range(chips):
        out_line.wait_mate(chip)
    state = tokens_ref[...].astype(jnp.float32) + jnp.dot(
        attn_low, wo[...].reshape(grps * chips * 2 * unit, tokens_ref.shape[1]),
        preferred_element_type=jnp.float32,
    )
    state_ref[...] = state
    n2buf[p.chip, p.core] = rms_scale(state, gain_two_ref[...].astype(jnp.float32)).astype(jnp.bfloat16)
    n2_line.start()
    cot_line.forward(3)
    outs = [
        pltpu.make_async_copy(nbuf, n1_all_ref, lsem.at[4]),
        pltpu.make_async_copy(wq, wq_all_ref, lsem.at[5]),
        pltpu.make_async_copy(qbuf, q_out_ref, lsem.at[6]),
        pltpu.make_async_copy(kvbuf, kv_out_ref, lsem.at[7]),
        pltpu.make_async_copy(wo, wo_all_ref, lsem.at[8]),
        pltpu.make_async_copy(columns, columns_ref, lsem.at[9]),
    ]
    for chip in range(chips):
        n1_line.wait_mate(chip)
    for copy in outs:
        copy.start()
    for step in range(1, chips):
        n2_line.forward(step)
    for chip in range(chips):
        cot_line.wait_mate(chip)
        n2_line.wait_mate(chip)
    last = pltpu.make_async_copy(n2buf, n2_all_ref, lsem.at[10])
    last.start()
    for b in (1, 2):
        for j in range(3):
            m_direct(b, 2 - b, j).wait_recv()
            m_forward(3 - b, j).wait_recv()
    for copy in outs:
        copy.wait()
    last.wait()
    n1_line.drain()
    n2_line.drain()
    out_line.drain()
    cot_line.drain()
    for b in range(grps):
        wq_mate(b).wait_send()
        bias_mate(b).wait_send()
    for b in range(1, grps):
        wq_direct(b).wait_send()
        bias_direct(b).wait_send()
        out_mate(b, p.core).wait_send()
        for chip in range(chips):
            out_cross(b, chip).wait_send()
    for b in (1, 2):
        for i in (0, 1):
            for j in range(3):
                m_direct(b, i, j).wait_send()
        for j in range(3):
            m_forward(b, j).wait_send()
    for chip in range(chips):
        pl.when(chip != p.chip)(lambda chip=chip: q_copy(chip).wait_send())
        for other in range(chips):
            pl.when(other != p.chip)(lambda chip=chip, other=other: k_copy(chip, other).wait_send())
            k_mate(other, chip).wait_send()


def front_call(tokens, gain_one, gain_two, segments, freqs, bias, cot, qkv_weight, out_weight, mlp_rows):
    chips = segments.shape[1] // 2
    grps = 4
    shard, width = tokens.shape
    half = qkv_weight.shape[0]
    vm, dma = pltpu.VMEM, pltpu.SemaphoreType.DMA
    anyspace = pl.BlockSpec(memory_space=pl.ANY)
    vspec = pl.BlockSpec(memory_space=pltpu.VMEM)
    low, wide = jnp.bfloat16, jnp.float32
    struct = jax.ShapeDtypeStruct
    wo_shape = (grps, chips, 2) + out_weight.shape
    columns_shape = (grps, shard, H * HD // grps)
    return pl.pallas_call(
        functools.partial(front_kernel, chips, 1.0 / math.sqrt(HD)),
        out_shape=(
            struct((shard, H * HD), wide),
            struct((shard, width), wide),
            struct((chips, shard, HD), wide),
            struct((chips, shard, HD), wide),
            struct((shard, 2 * chips * shard), wide),
            struct((chips, 3, shard, HD), low),
            struct((chips, 2, chips, shard, HD), low),
            struct((chips, 2, shard, width), low),
            struct((chips, 2, shard, width), low),
            struct((chips, 2, shard, width), low),
            struct(wo_shape, low),
            struct((grps, 2 * half, width), low),
            struct(columns_shape, low),
        ) + (struct(mlp_rows.shape, low),) * 3,
        in_specs=[vspec] * 3
        + [pl.BlockSpec(memory_space=pltpu.SMEM)]
        + [vspec] * 2
        + [anyspace] * 4,
        out_specs=(vspec,) * 5 + (anyspace,) * 11,
        scratch_shapes=[
            vm((chips, 2, shard, width), low),
            vm((chips, 2, shard, width), low),
            vm((grps, 2 * half, width), low),
            vm(wo_shape, low),
            vm((8, HD), wide),
            vm((grps, 2, 8, HD), wide),
            vm((chips, grps, shard, HD), low),
            vm((chips, 3, shard, HD), low),
            vm((chips, 2, chips, shard, HD), low),
            vm(columns_shape, low),
            dma((11,)),
            dma((3, chips)), dma((chips, 2)),
            dma((3, chips)), dma((chips, 2)),
            dma((3, chips)), dma((chips, 2)),
            dma((3, chips)), dma((chips, 2)),
            dma((grps, chips)), dma((grps, chips)), dma((grps,)), dma((grps,)),
            dma((2, grps)), dma((grps, 2)),
            dma((2, grps)), dma((grps, 2)),
            dma((grps, 2, 3)), dma((grps, 2, 3)),
            dma((chips,)), dma((chips,)),
            dma((2, chips, chips)), dma((chips, 2, chips)),
        ],
        compiler_params=pltpu.CompilerParams(
            collective_id=2, has_side_effects=True, vmem_limit_bytes=60 * 2**20
        ),
        name="front",
    )(tokens, gain_one, gain_two, segments, freqs, bias, cot, qkv_weight, out_weight, mlp_rows)


FIRST_HOPS = ((1, 0, 1), (3, 0, 1), (2, 1, 2), (3, 1, 2))
EARLY_HOPS = tuple((hop, kind) for kind in (2, 0) for hop in (1, 3, 0, 2))


def mlp_kernel(chips, grps, row_tiles, n2_ref, cot_ref, columns_ref, *refs):
    w_refs, refs = refs[:grps], refs[grps:]
    (
        n2g_ref, outp_ref, grads_ref, owned_ref, passing_ref, arrived_ref, tok, w, acts, part, mate_in, left_in, right_in, stage,
        lsem, ssend, srecv, wsem, osem, a_send, a_recv, e_send, e_recv,
    ) = refs
    p = Place(chips)
    shard, width = n2_ref.shape[1:]
    units = w.shape[1]
    block = units // grps
    tile = units // row_tiles
    loads = [
        pltpu.make_async_copy(n2_ref, tok.at[0], lsem.at[0]),
        pltpu.make_async_copy(cot_ref, tok.at[1], lsem.at[1]),
        pltpu.make_async_copy(columns_ref.at[p.grp], owned_ref.at[0], lsem.at[2]),
    ]
    loads[0].start()

    def w_copy(j, b):
        return pltpu.make_async_copy(w_refs[b].at[j], w.at[j, pl.ds(b * block, block)], wsem.at[j, b])

    for j in range(3):
        for b in range(grps):
            w_copy(j, b).start()
    for copy in loads[1:]:
        copy.start()

    barrier = pltpu.get_barrier_semaphore()
    inner = jnp.where((p.chip > 0) & (p.chip < chips - 1), 1, 0)

    def greet(grp, seq):
        pl.semaphore_signal(barrier, inc=1, device_id=(grp, seq), device_id_type=MESH)

    greet(p.grp, p.mate)
    pl.when(p.chip > 0)(lambda: greet(p.grp, p.seq - 2))
    pl.when(p.chip < chips - 1)(lambda: greet(p.grp, p.seq + 2))
    for b in range(1, grps):
        greet(p.peer(b), p.seq)
    pl.semaphore_wait(barrier, 2 + inner + grps - 1)
    scatter = LineScatter(p, part, mate_in, left_in, right_in, ssend, srecv)

    def a_copy(b):
        return remote(
            columns_ref.at[p.peer(b)], owned_ref.at[b], a_send.at[b], a_recv.at[b], p.peer(b), p.seq
        )

    for b in range(1, grps):
        a_copy(b).start()
    loads[0].wait()
    for j in range(2):
        for b in range(grps):
            w_copy(j, b).wait()

    def kind_of(t):
        return (t // row_tiles + 2) % 3

    def early(slot, kind):
        b, i, to = FIRST_HOPS[slot]
        half = block // 2
        rows = grads_ref.at[kind, pl.ds(b * block + i * half, half)]
        land = arrived_ref.at[kind // 2, pl.ds(i * half, half)] if b < 3 else passing_ref.at[i, kind]
        at = EARLY_HOPS.index((slot, kind))
        return remote(rows, land, e_send.at[at], e_recv.at[at], p.peer(to), p.seq)

    def out_copy(t):
        return pltpu.make_async_copy(
            stage.at[t % 2],
            grads_ref.at[kind_of(t), pl.ds((t % row_tiles) * tile, tile)],
            osem.at[t % 2],
        )

    def tile_grad(t):
        kind = kind_of(t)
        lhs = acts[kind, :, pl.ds(pl.multiple_of((t % row_tiles) * tile, 128), tile)]
        rhs = tok[kind // 2].reshape(2 * chips * shard, width)
        stage[t % 2] = lax.dot_general(
            lhs, rhs, CONTRACT_FIRST, preferred_element_type=jnp.float32
        ).astype(jnp.bfloat16)
        out_copy(t).start()

    def start_early(kind):
        for hop in EARLY_HOPS:
            if hop[1] == kind:
                early(*hop).start()

    def far_chip(order):
        return nearest_chip(p.chip, chips - 1 - order, chips)

    outer = (p.chip == 0) | (p.chip == chips - 1)

    @pl.loop(0, chips + 1)
    def _(order):
        @pl.when(order < chips)
        def _():
            at = far_chip(order)
            x = tok[0, pl.ds(2 * at, 2)].reshape(2 * shard, width)
            gate = lax.dot_general(x, w[0], CONTRACT_LAST, preferred_element_type=jnp.float32)
            up = lax.dot_general(x, w[1], CONTRACT_LAST, preferred_element_type=jnp.float32)
            sig = 1.0 / (1.0 + jnp.exp(-gate))
            silu = gate * sig
            rows = pl.ds(at * (2 * shard), 2 * shard)
            acts[0, rows] = (up * sig * (1.0 + gate * (1.0 - sig))).astype(jnp.bfloat16)
            acts[1, rows] = silu.astype(jnp.bfloat16)
            hidden = (silu * up).astype(jnp.bfloat16)
            acts[2, rows] = hidden

            @pl.when(order == 0)
            def _():
                for b in range(grps):
                    w_copy(2, b).wait()

            part[1, pl.ds(2 * at, 2)] = (
                jnp.dot(hidden, w[2], preferred_element_type=jnp.float32)
                .astype(jnp.bfloat16).reshape(2, shard, width)
            )
            scatter.to_mate(1, at).start()

        pl.when(outer & (order > 0))(lambda: scatter.step(1, far_chip(order - 1)))

    for copy in loads[1:]:
        copy.wait()

    @pl.loop(0, row_tiles)
    def _(t):
        pl.when(t >= 2)(lambda: out_copy(t - 2).wait())
        tile_grad(t)
        pl.when(jnp.logical_not(outer))(lambda: scatter.step(1, far_chip(t)))

    @pl.loop(0, chips)
    def _(order):
        at = far_chip(order)
        y = tok[1, pl.ds(2 * at, 2)].reshape(2 * shard, width)
        unit_grad = lax.dot_general(y, w[2], CONTRACT_LAST, preferred_element_type=jnp.float32)
        rows = pl.ds(at * (2 * shard), 2 * shard)
        acts[0, rows] = (unit_grad * acts[0, rows].astype(jnp.float32)).astype(jnp.bfloat16)
        acts[1, rows] = (unit_grad * acts[1, rows].astype(jnp.float32)).astype(jnp.bfloat16)

        @pl.when(order == 0)
        def _():
            out_copy(row_tiles - 2).wait()
            out_copy(row_tiles - 1).wait()
            start_early(2)

    @pl.loop(0, chips + 1)
    def _(order):
        @pl.when(order < chips)
        def _():
            at = far_chip(order)
            rows = pl.ds(at * (2 * shard), 2 * shard)
            back = jnp.dot(acts[0, rows], w[0], preferred_element_type=jnp.float32) + jnp.dot(
                acts[1, rows], w[1], preferred_element_type=jnp.float32
            )
            part[0, pl.ds(2 * at, 2)] = back.astype(jnp.bfloat16).reshape(2, shard, width)
            scatter.to_mate(0, at).start()

        @pl.when(order < row_tiles)
        def _():
            t = row_tiles + order
            pl.when(order >= 2)(lambda: out_copy(t - 2).wait())
            tile_grad(t)

        @pl.when(order == row_tiles)
        def _():
            out_copy(2 * row_tiles - 2).wait()
            out_copy(2 * row_tiles - 1).wait()
            start_early(0)

        pl.when(outer & (order > 0))(lambda: scatter.step(0, far_chip(order - 1)))
        pl.when(jnp.logical_not(outer) & (order >= 3))(lambda: scatter.step(0, far_chip(order - 3)))

    @pl.loop(2 * row_tiles, 3 * row_tiles)
    def _(t):
        pl.when(t >= 2 * row_tiles + 2)(lambda: out_copy(t - 2).wait())
        late = t - 2 * row_tiles + chips + 1 - 3
        pl.when(jnp.logical_not(outer) & (late < chips))(lambda: scatter.step(0, far_chip(late)))
        tile_grad(t)

    scatter.finish(0, n2g_ref)
    scatter.finish(1, outp_ref)
    out_copy(3 * row_tiles - 2).wait()
    out_copy(3 * row_tiles - 1).wait()
    for hop in EARLY_HOPS:
        early(*hop).wait_recv()
        early(*hop).wait_send()
    scatter.drain(0)
    scatter.drain(1)
    for b in range(1, grps):
        a_copy(b).wait_recv()
        a_copy(b).wait_send()


def mlp_call(n2_all, cot_all, columns, w_blocks, row_tiles=3):
    grps, (_, block, width) = len(w_blocks), w_blocks[0].shape
    slots, shard, _ = cot_all.shape
    chips = slots // 2
    units = grps * block
    vm, anyspace = pltpu.VMEM, pl.BlockSpec(memory_space=pl.ANY)
    vspec = pl.BlockSpec(memory_space=pltpu.VMEM)
    dma = pltpu.SemaphoreType.DMA
    return pl.pallas_call(
        functools.partial(mlp_kernel, chips, grps, row_tiles),
        out_shape=(
            jax.ShapeDtypeStruct((shard, width), jnp.float32),
            jax.ShapeDtypeStruct((shard, width), jnp.float32),
            jax.ShapeDtypeStruct((3, units, width), jnp.bfloat16),
            jax.ShapeDtypeStruct(columns.shape, jnp.bfloat16),
            jax.ShapeDtypeStruct((2, 3, block // 2, width), jnp.bfloat16),
            jax.ShapeDtypeStruct((2, block, width), jnp.bfloat16),
        ),
        in_specs=[anyspace] * (3 + grps),
        out_specs=(vspec, vspec) + (anyspace,) * 4,
        scratch_shapes=[
            vm((2, slots, shard, width), jnp.bfloat16),
            vm((3, units, width), jnp.bfloat16),
            vm((3, slots * shard, units), jnp.bfloat16),
            vm((2, slots, shard, width), jnp.bfloat16),
            vm((2, chips, shard, width), jnp.bfloat16),
            vm((2, chips, shard, width), jnp.bfloat16),
            vm((2, chips, shard, width), jnp.bfloat16),
            vm((2, units // row_tiles, width), jnp.bfloat16),
            dma((3,)), dma((3, 2, chips)), dma((3, 2, chips)),
            dma((3, grps)), dma((2,)), dma((grps,)), dma((grps,)),
            dma((len(EARLY_HOPS),)), dma((len(EARLY_HOPS),)),
        ],
        compiler_params=pltpu.CompilerParams(
            collective_id=1, has_side_effects=True, vmem_limit_bytes=62 * 2**20
        ),
        name="mlp",
    )(n2_all, cot_all, columns, *w_blocks)


def unturn(rows, cosine, sine, half):
    return rows * cosine + pltpu.roll(rows * sine, half, 1)


def back_kernel(chips, scale,
                n2g_ref, state_ref, cot_ref, tokens_ref, gain_one_ref, gain_two_ref, attn_ref, q_ref, kv_ref,
                mask_ref, cos_ref, sin_ref, wq_ref, wo_ref, n1_ref, terms_ref, owned_ref, passing_ref, early_ref,
                tok_grad_ref, wq_grad_ref, wo_grad_ref, gain_ref, direct_ref, second_ref,
                wo, stbuf, n1x, at_all, dq_stage, gq_in, kv_part, km_in, k_sum, k_own, kr_in,
                cols, part, left_in, right_in, wgrad, wm_in, w_send_buf, w_in, o_terms, ob_in, o_send_buf, o_in,
                m_own, m_in, early_rows, gain_own, gain_in, gain_mid, gain_mid_in, state_grad,
                lsem, s_send, s_recv, q_send, q_recv, km_send, km_recv, kr_send, kr_recv,
                r_send, r_recv, wm_send, wm_recv, w_send, w_recv, ob_send, ob_recv, o_send, o_recv, m_send, m_recv,
                ml_sem, g_send, g_recv, h_send, h_recv):
    p = Place(chips)
    grps = 4
    shard, width = n2g_ref.shape
    slots = 2 * chips
    heads_per = H // KVH
    half = HD // 2
    low, wide = jnp.bfloat16, jnp.float32
    block = terms_ref.shape[1] // grps
    mhalf = block // 2
    last = chips - 1

    loads = [
        pltpu.make_async_copy(wo_ref, wo, lsem.at[0]),
        pltpu.make_async_copy(n1_ref.at[:, p.core], n1x.at[:, :, pl.ds(0, width)], lsem.at[1]),
        pltpu.make_async_copy(owned_ref, at_all, lsem.at[2]),
    ]
    for copy in loads:
        copy.start()

    def seq_peer(i):
        return (p.seq + i) % slots

    barrier = pltpu.get_barrier_semaphore()
    for i in range(1, slots):
        pl.semaphore_signal(barrier, inc=1, device_id=(p.grp, seq_peer(i)), device_id_type=MESH)
    for b in range(1, grps):
        pl.semaphore_signal(barrier, inc=1, device_id=(p.peer(b), p.seq), device_id_type=MESH)
    pl.semaphore_wait(barrier, slots - 1 + grps - 1)

    def m_rows(b, i, kind):
        return terms_ref.at[kind, pl.ds(b * block + i * mhalf, mhalf)]

    def m_first(hop, kind):
        b, i, to = FIRST_HOPS[hop]
        land = direct_ref.at[kind, pl.ds(i * mhalf, mhalf)] if b < 3 else m_in.at[i, kind]
        return remote(
            m_rows(b, i, kind), land, m_send.at[hop, kind], m_recv.at[hop, kind], p.peer(to), p.seq
        )

    def m_second(i, kind):
        return remote(
            m_own.at[i, kind], second_ref.at[kind, pl.ds(i * mhalf, mhalf)], m_send.at[4 + i, kind],
            m_recv.at[4 + i, kind], p.peer(2 - i), p.seq,
        )

    late_hops = [(hop, kind) for kind in (1, 0, 2) for hop in (1, 3, 0, 2) if (hop, kind) not in EARLY_HOPS]
    for hop in late_hops:
        m_first(*hop).start()
    m_loads = [
        pltpu.make_async_copy(m_rows(2 - i, i, kind), m_own.at[i, kind], ml_sem.at[i, kind])
        for i in (0, 1)
        for kind in range(3)
    ]
    for hop, kind in EARLY_HOPS:
        if FIRST_HOPS[hop][0] == 3:
            i = FIRST_HOPS[hop][1]
            m_loads.append(pltpu.make_async_copy(passing_ref.at[i, kind], m_in.at[i, kind], ml_sem.at[2 + i, kind]))
    early_kinds = [kind for kind in (0, 2) if (0, kind) in EARLY_HOPS]
    early_loads = [
        pltpu.make_async_copy(early_ref.at[kind // 2], early_rows.at[kind // 2], ml_sem.at[4, kind])
        for kind in early_kinds
    ]
    early_copies = [
        pltpu.make_async_copy(early_rows.at[kind // 2], direct_ref.at[kind], ml_sem.at[4, kind])
        for kind in early_kinds
    ]
    m_loads += early_loads
    for copy in m_loads:
        copy.start()

    def m_turn(kind):
        for i in (0, 1):
            if (1 + 2 * i, kind) in late_hops:
                m_first(1 + 2 * i, kind).wait_recv()

            @pl.loop(0, mhalf // 16)
            def _(t, i=i):
                rows = pl.ds(pl.multiple_of(t * 16, 16), 16)
                m_own[i, kind, rows] = (
                    m_own[i, kind, rows].astype(wide) + m_in[i, kind, rows].astype(wide)
                ).astype(low)

            m_second(i, kind).start()

    state = state_ref[...]
    gain_two = gain_two_ref[...].astype(wide)
    n2g = n2g_ref[...]
    scale_two = lax.rsqrt(jnp.mean(state * state, axis=-1, keepdims=True) + EPS)
    normed = state * scale_two
    gain_own[1] = jnp.sum(n2g * normed, axis=0, keepdims=True)
    lifted = n2g * gain_two
    state_grad[...] = cot_ref[...].astype(wide) + scale_two * (
        lifted - normed * jnp.mean(lifted * normed, axis=-1, keepdims=True)
    )
    state_low = state_grad[...].astype(low)
    stbuf[0] = state_low

    def state_copy(b):
        return remote(stbuf.at[0], stbuf.at[b], s_send.at[b], s_recv.at[b], p.peer(b), p.seq)

    attn = attn_ref[...]
    unit = wo.shape[0] // (grps * slots)
    loads[0].wait()
    attn_grad = lax.dot_general(state_low, wo[...], CONTRACT_LAST, preferred_element_type=wide).astype(low)
    mask = mask_ref[...]
    keys_total = mask.shape[1]
    own_cos, own_sin = cos_ref[p.chip], sin_ref[p.chip]

    def km_copy(head):
        return remote(
            kv_part.at[head, 1 - p.core], km_in.at[head], km_send.at[head], km_recv.at[head], p.grp, p.mate
        )

    def kr_copy(head):
        return remote(
            k_sum.at[head], kr_in.at[p.chip], kr_send.at[head], kr_recv.at[p.chip], p.grp, 2 * head + p.core
        )

    def kr_arrival(chip):
        return remote(k_sum.at[chip], kr_in.at[chip], kr_send.at[chip], kr_recv.at[chip], p.grp, p.mate)

    q_parts = (pl.ds(0, 1), pl.ds(1, 2))

    def q_copy(chip, i):
        return remote(
            dq_stage.at[chip, q_parts[i]], gq_in.at[p.chip, q_parts[i]], q_send.at[chip, i],
            q_recv.at[p.chip, i], p.grp, 2 * chip + p.core,
        )

    def q_arrival(chip, i):
        return remote(
            dq_stage.at[chip, q_parts[i]], gq_in.at[chip, q_parts[i]], q_send.at[chip, i],
            q_recv.at[chip, i], p.grp, p.mate,
        )

    def key_sum(head):
        km_copy(head).wait_recv()
        total = kv_part[head, p.core].astype(wide) + km_in[head].astype(wide)

        @pl.when(p.chip == head)
        def _():
            k_own[...] = total

        @pl.when(p.chip != head)
        def _():
            k_sum[head] = total.astype(low)
            kr_copy(head).start()

    for kv in range(KVH):
        heads = [kv * heads_per + i for i in range(heads_per)]
        queries = jnp.concatenate([q_ref[h % chips, h // chips] for h in heads], axis=0)
        grads = jnp.concatenate([attn_grad[:, h * HD : (h + 1) * HD] for h in heads], axis=0)
        mixed = jnp.concatenate([attn[:, h * HD : (h + 1) * HD] for h in heads], axis=0)
        delta = jnp.sum(grads.astype(wide) * mixed, axis=-1, keepdims=True)
        keys = kv_ref[kv].reshape(keys_total, HD)
        values = kv_ref[KVH + kv].reshape(keys_total, HD)
        scores = lax.dot_general(queries, keys, CONTRACT_LAST, preferred_element_type=wide) * scale
        scores = (scores.reshape(heads_per, shard, keys_total) + mask[None]).reshape(heads_per * shard, keys_total)
        weights = jnp.exp(scores - jnp.max(scores, axis=-1, keepdims=True))
        probs = weights * (1.0 / jnp.sum(weights, axis=-1, keepdims=True))
        prob_grad = lax.dot_general(grads, values, CONTRACT_LAST, preferred_element_type=wide)
        score_grad = (probs * (prob_grad - delta)).astype(low)
        key_grad = lax.dot_general(score_grad, queries, CONTRACT_FIRST, preferred_element_type=wide) * scale
        value_grad = lax.dot_general(probs.astype(low), grads, CONTRACT_FIRST, preferred_element_type=wide)
        kv_part[kv] = key_grad.astype(low).reshape(2, chips, shard, HD)
        kv_part[KVH + kv] = value_grad.astype(low).reshape(2, chips, shard, HD)
        km_copy(kv).start()
        km_copy(KVH + kv).start()
        query_grad = jnp.dot(score_grad, keys, preferred_element_type=wide) * scale
        for i, h in enumerate(heads):
            turned = unturn(query_grad[i * shard : (i + 1) * shard], own_cos, own_sin, half).astype(low)
            dq_stage[h % chips, h // chips] = turned

            @pl.when(p.chip == h % chips)
            def _(turned=turned, h=h):
                gq_in[h % chips, h // chips] = turned

        for chip in range(chips):
            pl.when(chip != p.chip)(lambda chip=chip: q_copy(chip, kv).start())
        if kv == 0:
            for copy in m_loads:
                copy.wait()
            for copy in early_copies:
                copy.start()
            m_turn(2)
            m_turn(0)
            for b in range(1, grps):
                state_copy(b).start()
            key_sum(0)
            key_sum(KVH)
    key_sum(1)
    key_sum(KVH + 1)
    m_turn(1)
    loads[1].wait()
    lane = lax.broadcasted_iota(jnp.int32, (chips, shard, HD), 2)
    n1x[:, :, width:] = jnp.where(lane == 0, 1.0, 0.0).astype(low)

    for chip in range(chips):
        for i in (0, 1):
            pl.when(chip != p.chip)(lambda chip=chip, i=i: q_arrival(chip, i).wait_recv())
        pl.when(chip != p.chip)(lambda chip=chip: kr_arrival(chip).wait_recv())
    is_value = jnp.where(p.chip >= chips // 2, 1.0, 0.0)

    gain_one = gain_one_ref[...].astype(wide)
    gain_own[0] = jnp.zeros_like(gain_own[0])

    def to_right(chip):
        return remote(part.at[chip], left_in.at[chip], r_send.at[0, chip], r_recv.at[0, chip], p.grp, p.seq + 2)

    def to_left(chip):
        return remote(part.at[chip], right_in.at[chip], r_send.at[1, chip], r_recv.at[1, chip], p.grp, p.seq - 2)

    @pl.loop(0, chips)
    def _(order):
        chip = nearest_chip(p.chip, last - order, chips)
        key_total = k_own[chip]
        for other in range(chips):
            key_total = key_total + jnp.where(other == p.chip, 0.0, kr_in[other, chip].astype(wide))
        turned = unturn(key_total, cos_ref[chip], sin_ref[chip], half)
        last_head = (key_total * is_value + turned * (1.0 - is_value)).astype(low)
        for b in range(grps):
            place = p.peer(b)
            query_head = gq_in[chip, jnp.minimum(place, grps - 2)]
            cols[chip, :, b * HD : (b + 1) * HD] = jnp.where(place == grps - 1, last_head, query_head)
        terms = jnp.dot(cols[chip], wq_ref[...], preferred_element_type=wide)
        part[chip] = terms.astype(low)
        gain_own[0] += jnp.sum(terms * n1x[chip, :, 0:width].astype(wide), axis=0, keepdims=True)
        pl.when((p.chip == 0) & (chip > 0))(lambda: to_right(chip).start())
        pl.when((p.chip == last) & (chip < last))(lambda: to_left(chip).start())

    gain_own[0] = gain_own[0] / gain_one

    def g_copy(i):
        return remote(gain_own, gain_in.at[i], g_send.at[i], g_recv.at[i], p.grp, seq_peer(i))

    def h_copy(b):
        return remote(gain_mid, gain_mid_in.at[b], h_send.at[b], h_recv.at[b], p.peer(b), p.seq)

    for i in range(1, slots):
        g_copy(i).start()

    def right_step(chip):
        @pl.when((chip > p.chip) & (p.chip > 0))
        def _():
            to_right(chip).wait_recv()
            part[chip] = (part[chip].astype(wide) + left_in[chip].astype(wide)).astype(low)
            to_right(chip).start()

    def left_step(chip):
        @pl.when((chip < p.chip) & (p.chip < last))
        def _():
            to_left(chip).wait_recv()
            part[chip] = (part[chip].astype(wide) + right_in[chip].astype(wide)).astype(low)
            to_left(chip).start()

    near_left = p.chip < chips // 2

    def rail_step(order):
        if order < chips:
            pl.when(near_left)(lambda: right_step(last - order))
            pl.when(jnp.logical_not(near_left))(lambda: left_step(order))
        else:
            pl.when(near_left)(lambda: left_step(order - chips))
            pl.when(jnp.logical_not(near_left))(lambda: right_step(2 * chips - 1 - order))

    rail_step(0)
    wgrad[...] = lax.dot_general(
        cols[...].reshape(chips * shard, grps * HD), n1x[...].reshape(chips * shard, width + HD),
        CONTRACT_FIRST, preferred_element_type=wide,
    ).reshape(grps, 2, half, width + HD)
    wm = remote(wgrad.at[:, 1 - p.core], wm_in, wm_send, wm_recv, p.grp, p.mate)
    wm.start()
    rail_step(1)
    wm.wait_recv()
    w_send_buf[...] = (wgrad[:, p.core] + wm_in[...]).astype(low)

    def w_copy(b):
        return remote(w_send_buf.at[b], w_in.at[b], w_send.at[b], w_recv.at[b], p.peer(b), p.seq)

    for b in range(1, grps):
        w_copy(b).start()
    for order in range(2, 2 * chips):
        rail_step(order)
    loads[2].wait()
    for b in range(1, grps):
        state_copy(b).wait_recv()
    o_terms[...] = lax.dot_general(
        at_all[...].reshape(grps * shard, slots * unit), stbuf[...].reshape(grps * shard, width),
        CONTRACT_FIRST, preferred_element_type=wide,
    ).reshape(chips, 2, unit, width)
    ob = remote(o_terms.at[:, 1 - p.core], ob_in, ob_send, ob_recv, p.grp, p.mate)
    ob.start()
    ob.wait_recv()
    o_send_buf[...] = (o_terms[:, p.core] + ob_in[...]).astype(low)

    def o_copy(chip):
        return remote(
            o_send_buf.at[chip], o_in.at[p.chip], o_send.at[chip], o_recv.at[p.chip], p.grp, 2 * chip + p.core
        )

    def o_arrival(chip):
        return remote(o_send_buf.at[chip], o_in.at[chip], o_send.at[chip], o_recv.at[chip], p.grp, p.mate)

    for chip in range(chips):
        pl.when(chip != p.chip)(lambda chip=chip: o_copy(chip).start())
    total = gain_own[...]
    for i in range(1, slots):
        g_copy(i).wait_recv()
        total = total + gain_in[i]
    gain_mid[...] = total
    for b in range(1, grps):
        h_copy(b).start()

    tokens = tokens_ref[...].astype(wide)
    tok_grad_ref[...] = part[p.chip].astype(wide)

    @pl.when(p.chip > 0)
    def _():
        to_right(p.chip).wait_recv()
        tok_grad_ref[...] += left_in[p.chip].astype(wide)

    @pl.when(p.chip < last)
    def _():
        to_left(p.chip).wait_recv()
        tok_grad_ref[...] += right_in[p.chip].astype(wide)

    n1g = tok_grad_ref[...]
    scale_one = lax.rsqrt(jnp.mean(tokens * tokens, axis=-1, keepdims=True) + EPS)
    normed = tokens * scale_one
    lifted = n1g * gain_one
    tok_grad_ref[...] = state_grad[...] + scale_one * (
        lifted - normed * jnp.mean(lifted * normed, axis=-1, keepdims=True)
    )

    wq_grad = wgrad[0, p.core] + wm_in[0]
    for b in range(1, grps):
        w_copy(b).wait_recv()
        wq_grad = wq_grad + w_in[b].astype(wide)
    wq_grad_ref[...] = wq_grad
    wo_grad = o_terms[p.chip, p.core] + ob_in[p.chip]
    for chip in range(chips):
        pl.when(chip != p.chip)(lambda chip=chip: o_arrival(chip).wait_recv())
        wo_grad = wo_grad + jnp.where(chip == p.chip, 0.0, o_in[chip].astype(wide))
    wo_grad_ref[...] = wo_grad
    total = gain_mid[...]
    for b in range(1, grps):
        h_copy(b).wait_recv()
        total = total + gain_mid_in[b]
    gain_ref[...] = total

    for hop, kind in late_hops:
        if FIRST_HOPS[hop][0] < 3:
            m_first(hop, kind).wait_recv()
        m_first(hop, kind).wait_send()
    for kind in (2, 0, 1):
        for i in (0, 1):
            m_second(i, kind).wait_recv()
            m_second(i, kind).wait_send()
    for copy in early_copies:
        copy.wait()
    ob.wait_send()
    wm.wait_send()
    for i in range(1, slots):
        g_copy(i).wait_send()
    for b in range(1, grps):
        state_copy(b).wait_send()
        w_copy(b).wait_send()
        h_copy(b).wait_send()
    for chip in range(chips):
        km_copy(chip).wait_send()

        @pl.when(chip != p.chip)
        def _(chip=chip):
            q_copy(chip, 0).wait_send()
            q_copy(chip, 1).wait_send()
            kr_copy(chip).wait_send()
            o_copy(chip).wait_send()

        pl.when(chip > p.chip)(lambda chip=chip: to_right(chip).wait_send())
        pl.when(chip < p.chip)(lambda chip=chip: to_left(chip).wait_send())


def back_call(n2g, state, cotangent, tokens, gain_one, gain_two, attn, q_heads, kv_heads, mask, cosine, sine,
              qkv_all, out_full, n1_all, terms, owned, passing, early):
    chips = cosine.shape[0]
    grps = 4
    slots = 2 * chips
    shard, width = tokens.shape
    att, block = out_full.shape[0], terms.shape[1] // grps
    unit, half = att // (grps * slots), HD // 2
    vm, dma = pltpu.VMEM, pltpu.SemaphoreType.DMA
    anyspace = pl.BlockSpec(memory_space=pl.ANY)
    vspec = pl.BlockSpec(memory_space=pltpu.VMEM)
    low, wide = jnp.bfloat16, jnp.float32
    struct = jax.ShapeDtypeStruct
    return pl.pallas_call(
        functools.partial(back_kernel, chips, 1.0 / math.sqrt(HD)),
        out_shape=(
            struct((shard, width), wide),
            struct((half, width + HD), wide),
            struct((unit, width), wide),
            struct((2, 1, width), wide),
            struct((3, block, width), low),
            struct((3, block, width), low),
        ),
        in_specs=[vspec] * 13 + [anyspace] * 6,
        out_specs=(vspec,) * 4 + (anyspace,) * 2,
        scratch_shapes=[
            vm((att, width), low),
            vm((grps, shard, width), low),
            vm((chips, shard, width + HD), low),
            vm((grps, shard, slots * unit), low),
            vm((chips, 3, shard, HD), low),
            vm((chips, 3, shard, HD), low),
            vm((chips, 2, chips, shard, HD), low),
            vm((chips, chips, shard, HD), low),
            vm((chips, chips, shard, HD), low),
            vm((chips, shard, HD), wide),
            vm((chips, chips, shard, HD), low),
            vm((chips, shard, grps * HD), low),
            vm((chips, shard, width), low),
            vm((chips, shard, width), low),
            vm((chips, shard, width), low),
            vm((grps, 2, half, width + HD), wide),
            vm((grps, half, width + HD), wide),
            vm((grps, half, width + HD), low),
            vm((grps, half, width + HD), low),
            vm((chips, 2, unit, width), wide),
            vm((chips, unit, width), wide),
            vm((chips, unit, width), low),
            vm((chips, unit, width), low),
            vm((2, 3, block // 2, width), low),
            vm((2, 3, block // 2, width), low),
            vm((2, block, width), low),
            vm((2, 1, width), wide),
            vm((slots, 2, 1, width), wide),
            vm((2, 1, width), wide),
            vm((grps, 2, 1, width), wide),
            vm((shard, width), wide),
            dma((3,)),
            dma((grps,)), dma((grps,)),
            dma((chips, 2)), dma((chips, 2)),
            dma((chips,)), dma((chips,)),
            dma((chips,)), dma((chips,)),
            dma((2, chips)), dma((2, chips)),
            dma, dma,
            dma((grps,)), dma((grps,)),
            dma, dma,
            dma((chips,)), dma((chips,)),
            dma((6, 3)), dma((6, 3)),
            dma((5, 3)),
            dma((slots,)), dma((slots,)),
            dma((grps,)), dma((grps,)),
        ],
        compiler_params=pltpu.CompilerParams(
            collective_id=3, has_side_effects=True, vmem_limit_bytes=62 * 2**20
        ),
        name="back",
    )(n2g, state, cotangent, tokens, gain_one, gain_two, attn, q_heads, kv_heads, mask, cosine, sine,
      qkv_all, out_full, n1_all, terms, owned, passing, early)


def columns_to_owners(rows, row_unit):
    grp_count, seq_count = lax.axis_size("grp"), lax.axis_size("seq")
    tok_rows = rows.shape[0]
    split = rows.reshape(tok_rows, grp_count, seq_count, row_unit).transpose(2, 0, 1, 3)
    split = split.reshape(seq_count * tok_rows, grp_count * row_unit)
    return lax.all_to_all(split, "seq", split_axis=0, concat_axis=0, tiled=True)


def owners_to_columns(rows, row_unit):
    grp_count, seq_count = lax.axis_size("grp"), lax.axis_size("seq")
    tok_rows = rows.shape[0] // seq_count
    moved = lax.all_to_all(rows, "seq", split_axis=0, concat_axis=0, tiled=True)
    moved = moved.reshape(seq_count, tok_rows, grp_count, row_unit).transpose(1, 2, 0, 3)
    return moved.reshape(tok_rows, grp_count * seq_count * row_unit)


def plain_mlp(normed_two, cotangent_all, mlp_weight):
    contract_last, contract_first = CONTRACT_LAST, CONTRACT_FIRST
    mlp_rows = lax.all_gather(mlp_weight, "grp", axis=0, tiled=True)
    normed_two_all = lax.all_gather(normed_two, "seq", axis=0, tiled=True)
    gate_rows, upper_rows, down_rows = mlp_rows[:, 0, :], mlp_rows[:, 1, :], mlp_rows[:, 2, :]
    gate_vals = lax.dot_general(
        normed_two_all, gate_rows, contract_last, preferred_element_type=jnp.float32
    )
    upper_vals = lax.dot_general(
        normed_two_all, upper_rows, contract_last, preferred_element_type=jnp.float32
    )
    unit_wide, pull_back = jax.vjp(swish_product, gate_vals, upper_vals)
    unit_low = unit_wide.astype(jnp.bfloat16)
    unit_grad = lax.dot_general(
        cotangent_all, down_rows, contract_last, preferred_element_type=jnp.float32
    )
    gate_grad, upper_grad = pull_back(unit_grad)
    gate_grad = gate_grad.astype(jnp.bfloat16)
    upper_grad = upper_grad.astype(jnp.bfloat16)
    input_grad = jnp.dot(gate_grad, gate_rows, preferred_element_type=jnp.float32) + jnp.dot(
        upper_grad, upper_rows, preferred_element_type=jnp.float32
    )
    grad_part = lax.psum_scatter(
        input_grad.astype(jnp.bfloat16), "seq", scatter_dimension=0, tiled=True
    ).astype(jnp.float32)
    out_part = lax.psum_scatter(
        jnp.dot(unit_low, down_rows, preferred_element_type=jnp.float32).astype(jnp.bfloat16),
        "seq",
        scatter_dimension=0,
        tiled=True,
    ).astype(jnp.float32)
    mlp_terms = jnp.stack(
        [
            lax.dot_general(
                gate_grad, normed_two_all, contract_first, preferred_element_type=jnp.float32
            ),
            lax.dot_general(
                upper_grad, normed_two_all, contract_first, preferred_element_type=jnp.float32
            ),
            lax.dot_general(
                unit_low, cotangent_all, contract_first, preferred_element_type=jnp.float32
            ),
        ],
        axis=1,
    )
    mlp_grad = lax.psum_scatter(mlp_terms, "grp", scatter_dimension=0, tiled=True)
    return grad_part, out_part, mlp_grad


def padded_rows(mlp_weight):
    rows = mlp_weight.transpose(1, 0, 2)
    return jnp.pad(rows, ((0, 0), (0, -rows.shape[1] % 32), (0, 0)))


def per_device(
    tokens,
    cotangent,
    shard_segment,
    gain_attn,
    qkv_weight,
    qkv_bias,
    out_weight,
    gain_mlp,
    mlp_weight,
):
    tok_rows = tokens.shape[0]
    seq_count = lax.axis_size("seq")
    grp_count = lax.axis_size("grp")
    group_tok = tok_rows * seq_count
    heads_per = H // KVH
    kv_width = KVH * HD
    att_width = H * HD
    query_rows = heads_per * tok_rows
    score_scale = 1.0 / math.sqrt(HD)
    contract_last = CONTRACT_LAST
    contract_first = CONTRACT_FIRST
    seq_place = lax.axis_index("seq")
    grp_place = lax.axis_index("grp")
    use_kernels = (seq_count, grp_count, H, KVH, HD) == (8, 4, 12, 2, 128)
    if use_kernels:
        half_freqs = np.float32(THETA) ** (-(np.arange(HD // 2, dtype=np.float32) * np.float32(2.0)) / np.float32(HD))
        freqs = np.concatenate([half_freqs, half_freqs])[None, :].astype(np.float32)
        gain_rows = (gain_attn[None, :], gain_mlp[None, :])
        own_rows = padded_rows(mlp_weight)
        (
            attn_wide, state, cosine, sine, mask, q_heads, kv_heads, n1_all, n2_all, cot_all, out_all,
            qkv_all, columns, *peer_rows
        ) = front_call(
            tokens, *gain_rows, shard_segment, freqs, qkv_bias[None, :], cotangent, qkv_weight, out_weight,
            own_rows,
        )
        by_slot = lambda rows: rows.reshape((seq_count,) + rows.shape[2:])
        grad_part, out_part, mlp_terms, owned, passing, early = mlp_call(
            by_slot(n2_all), by_slot(cot_all), columns, [own_rows, *peer_rows]
        )
        output = (state + out_part).astype(jnp.bfloat16)
        token_grad, qkv_terms, out_grad, gain_sums, direct, second = back_call(
            grad_part, state, cotangent, tokens, *gain_rows, attn_wide, q_heads, kv_heads, mask,
            cosine, sine, qkv_all.reshape(-1, qkv_all.shape[-1]),
            out_all.reshape(att_width, -1), n1_all, mlp_terms, owned, passing, early,
        )
        units = mlp_weight.shape[0]
        mlp_sums = sum(
            rows[:, :units].astype(jnp.float32) for rows in (mlp_terms, direct, second)
        )
        width = tokens.shape[1]
        own = width // (grp_count * seq_count)
        gain_parts = lax.dynamic_slice_in_dim(
            gain_sums[:, 0], (grp_place * seq_count + seq_place) * own, own, 1
        )
        return (
            output,
            token_grad,
            gain_parts[0],
            qkv_terms[:, :width],
            qkv_terms[:, width],
            out_grad,
            gain_parts[1],
            mlp_sums.transpose(1, 0, 2),
        )
    segments = lax.dynamic_index_in_dim(shard_segment, grp_place, 0, keepdims=False)
    starts = shard_starts(segments, tok_rows, group_tok // 2)
    shard_order = jnp.arange(seq_count, dtype=jnp.int32)
    own_seg = jnp.sum(jnp.where(shard_order == seq_place, segments, 0))
    own_start = jnp.sum(jnp.where(shard_order == seq_place, starts, 0))
    positions = own_start + jnp.arange(tok_rows, dtype=jnp.int32)
    cosine_table, sine_table = rotary_tables(positions, HD)
    query_pos = jnp.tile(positions, heads_per)
    tokens_wide = tokens.astype(jnp.float32)
    gain_one = gain_attn.astype(jnp.float32)
    gain_two = gain_mlp.astype(jnp.float32)
    normed_one = rms_scale(tokens_wide, gain_one).astype(jnp.bfloat16)
    normed_one_all = lax.all_gather(normed_one, "seq", axis=0, tiled=True)
    qkv_rows = lax.all_gather(qkv_weight, "grp", axis=0, tiled=True)
    bias_rows = lax.all_gather(qkv_bias, "grp", axis=0, tiled=True)
    cotangent_all = lax.all_gather(cotangent, "seq", axis=0, tiled=True)
    out_full = lax.all_gather(out_weight, AXES, axis=0, tiled=True)
    projected = lax.dot_general(
        normed_one_all, qkv_rows, contract_last, preferred_element_type=jnp.float32
    )
    projected = (projected + bias_rows.astype(jnp.float32)[None, :]).astype(jnp.bfloat16)
    projected = owners_to_columns(projected, qkv_weight.shape[0]).astype(jnp.float32)
    query_rot = rotate(
        projected[:, :att_width].reshape(tok_rows, H, HD), cosine_table, sine_table
    ).astype(jnp.bfloat16)
    key_rot = rotate(
        projected[:, att_width : att_width + kv_width].reshape(tok_rows, KVH, HD),
        cosine_table,
        sine_table,
    ).astype(jnp.bfloat16)
    value_low = projected[:, att_width + kv_width :].astype(jnp.bfloat16)
    keys_all, values_all = (
        lax.all_gather(key_rot.reshape(tok_rows, kv_width), "seq", axis=0, tiled=True),
        lax.all_gather(value_low, "seq", axis=0, tiled=True),
    )
    queries = (
        query_rot.reshape(tok_rows, KVH, heads_per, HD)
        .transpose(1, 2, 0, 3)
        .reshape(KVH, query_rows, HD)
    )
    key_block = min(512, group_tok)
    block_count = group_tok // key_block
    block_order = jnp.arange(block_count, dtype=jnp.int32)

    def block_mask(block_index):
        key_index = block_index * key_block + jnp.arange(key_block, dtype=jnp.int32)
        key_shard = key_index // tok_rows
        onehot = key_shard[:, None] == shard_order[None, :]
        key_seg = jnp.sum(jnp.where(onehot, segments[None, :], 0), axis=1)
        key_pos = jnp.sum(jnp.where(onehot, starts[None, :], 0), axis=1) + key_index % tok_rows
        visible = (key_seg == 0) | (key_seg == own_seg)
        return visible[None, :] & (key_pos[None, :] <= query_pos[:, None])

    def block_keys(block_index):
        key_part = lax.dynamic_slice_in_dim(
            keys_all, block_index * key_block, key_block, 0
        ).reshape(key_block, KVH, HD)
        value_part = lax.dynamic_slice_in_dim(
            values_all, block_index * key_block, key_block, 0
        ).reshape(key_block, KVH, HD)
        return (key_part, value_part)

    def block_scores(key_part):
        return (
            jnp.einsum("krd,jkd->krj", queries, key_part, preferred_element_type=jnp.float32)
            * score_scale
        )

    def stat_step(stats_now, block_index):
        allowed = block_mask(block_index)

        def stat_visit(current):
            top_old, total_old = current
            key_part, value_part = block_keys(block_index)
            scores = jnp.where(allowed[None], block_scores(key_part), -1e30)
            top_new = jnp.maximum(top_old, jnp.max(scores, axis=-1))
            weights = jnp.where(allowed[None], jnp.exp(scores - top_new[..., None]), 0.0)
            return (top_new, total_old * jnp.exp(top_old - top_new) + jnp.sum(weights, axis=-1))

        return (lax.cond(jnp.any(allowed), stat_visit, lambda current: current, stats_now), None)

    start_stats = (
        jnp.full((KVH, query_rows), -1e30, jnp.float32),
        jnp.zeros((KVH, query_rows), jnp.float32),
    )
    (top_all, total_all), unused = lax.scan(stat_step, start_stats, block_order)
    log_total = top_all + jnp.log(total_all)

    def mix_step(mixed_sum, block_index):
        allowed = block_mask(block_index)

        def mix_visit(current):
            key_part, value_part = block_keys(block_index)
            prob_low = jnp.where(
                allowed[None], jnp.exp(block_scores(key_part) - log_total[..., None]), 0.0
            ).astype(jnp.bfloat16)
            return current + jnp.einsum(
                "krj,jkd->krd", prob_low, value_part, preferred_element_type=jnp.float32
            )

        return (lax.cond(jnp.any(allowed), mix_visit, lambda current: current, mixed_sum), None)

    mixed_sum, unused = lax.scan(
        mix_step, jnp.zeros((KVH, query_rows, HD), jnp.float32), block_order
    )
    attn_wide = (
        mixed_sum.reshape(KVH, heads_per, tok_rows, HD)
        .transpose(2, 0, 1, 3)
        .reshape(tok_rows, att_width)
    )
    attn_low = attn_wide.astype(jnp.bfloat16)
    attn_proj = jnp.dot(attn_low, out_full, preferred_element_type=jnp.float32)
    state = tokens_wide + attn_proj
    normed_two = rms_scale(state, gain_two).astype(jnp.bfloat16)
    grad_part, out_part, mlp_grad = plain_mlp(normed_two, cotangent_all, mlp_weight)
    output = (state + out_part).astype(jnp.bfloat16)
    unused_state, norm_two_back = jax.vjp(rms_scale, state, gain_two)
    state_norm_grad, gain_two_grad = norm_two_back(grad_part)
    state_grad = state_norm_grad + cotangent.astype(jnp.float32)
    state_low = state_grad.astype(jnp.bfloat16)
    attn_grad = lax.dot_general(
        state_low, out_full, contract_last, preferred_element_type=jnp.float32
    )
    attn_grad_low = attn_grad.astype(jnp.bfloat16)
    attn_owned = columns_to_owners(attn_low, out_weight.shape[0])
    state_low_all = lax.all_gather(state_low, "seq", axis=0, tiled=True)
    out_grad = lax.psum_scatter(
        lax.dot_general(
            attn_owned, state_low_all, contract_first, preferred_element_type=jnp.float32
        ),
        "grp",
        scatter_dimension=0,
        tiled=True,
    )
    grad_heads = (
        attn_grad_low.reshape(tok_rows, KVH, heads_per, HD)
        .transpose(1, 2, 0, 3)
        .reshape(KVH, query_rows, HD)
    )
    delta_rows = jnp.sum(
        (attn_grad_low.astype(jnp.float32) * attn_wide).reshape(tok_rows, H, HD), axis=-1
    )
    delta_rows = (
        delta_rows.reshape(tok_rows, KVH, heads_per).transpose(1, 2, 0).reshape(KVH, query_rows)
    )

    def back_step(query_grad, block_index):
        allowed = block_mask(block_index)

        def back_visit(current):
            key_part, value_part = block_keys(block_index)
            prob_vals = jnp.where(
                allowed[None], jnp.exp(block_scores(key_part) - log_total[..., None]), 0.0
            )
            prob_grad = jnp.einsum(
                "krd,jkd->krj", grad_heads, value_part, preferred_element_type=jnp.float32
            )
            score_grad = (prob_vals * (prob_grad - delta_rows[..., None])).astype(jnp.bfloat16)
            new_grad = (
                current
                + jnp.einsum(
                    "krj,jkd->krd", score_grad, key_part, preferred_element_type=jnp.float32
                )
                * score_scale
            )
            key_grad = (
                jnp.einsum("krj,krd->jkd", score_grad, queries, preferred_element_type=jnp.float32)
                * score_scale
            )
            value_grad = jnp.einsum(
                "krj,krd->jkd",
                prob_vals.astype(jnp.bfloat16),
                grad_heads,
                preferred_element_type=jnp.float32,
            )
            return (
                new_grad,
                (key_grad.reshape(key_block, kv_width), value_grad.reshape(key_block, kv_width)),
            )

        def skip_block(current):
            blank_rows = jnp.zeros((key_block, kv_width), jnp.float32)
            return (current, (blank_rows, blank_rows))

        return lax.cond(jnp.any(allowed), back_visit, skip_block, query_grad)

    query_grad, (key_grads, value_grads) = lax.scan(
        back_step, jnp.zeros((KVH, query_rows, HD), jnp.float32), block_order
    )
    key_own, value_own = (
        lax.psum_scatter(
            key_grads.reshape(group_tok, kv_width).astype(jnp.bfloat16),
            "seq",
            scatter_dimension=0,
            tiled=True,
        ).astype(jnp.float32),
        lax.psum_scatter(
            value_grads.reshape(group_tok, kv_width).astype(jnp.bfloat16),
            "seq",
            scatter_dimension=0,
            tiled=True,
        ).astype(jnp.float32),
    )
    query_back = unrotate(
        query_grad.reshape(KVH, heads_per, tok_rows, HD)
        .transpose(2, 0, 1, 3)
        .reshape(tok_rows, H, HD),
        cosine_table,
        sine_table,
    )
    key_back = unrotate(key_own.reshape(tok_rows, KVH, HD), cosine_table, sine_table)
    qkv_grad_low = jnp.concatenate(
        [query_back.reshape(tok_rows, att_width), key_back.reshape(tok_rows, kv_width), value_own],
        axis=1,
    ).astype(jnp.bfloat16)
    qkv_grad_owned = columns_to_owners(qkv_grad_low, qkv_weight.shape[0])
    bias_terms = jnp.sum(qkv_grad_owned.astype(jnp.float32), axis=0)
    normed_one_grad = lax.psum_scatter(
        jnp.dot(qkv_grad_owned, qkv_rows, preferred_element_type=jnp.float32).astype(jnp.bfloat16),
        "seq",
        scatter_dimension=0,
        tiled=True,
    ).astype(jnp.float32)
    qkv_grad = lax.psum_scatter(
        lax.dot_general(
            qkv_grad_owned, normed_one_all, contract_first, preferred_element_type=jnp.float32
        ),
        "grp",
        scatter_dimension=0,
        tiled=True,
    )
    unused_tokens, norm_one_back = jax.vjp(rms_scale, tokens_wide, gain_one)
    token_norm_grad, gain_one_grad = norm_one_back(normed_one_grad)
    token_grad = token_norm_grad + state_grad
    bias_part = lax.psum_scatter(bias_terms, "grp", scatter_dimension=0, tiled=True)
    gain_one_part, gain_two_part = (
        lax.psum_scatter(gain_one_grad, AXES, scatter_dimension=0, tiled=True),
        lax.psum_scatter(gain_two_grad, AXES, scatter_dimension=0, tiled=True),
    )
    return (
        output,
        token_grad,
        gain_one_part,
        qkv_grad,
        bias_part,
        out_grad,
        gain_two_part,
        mlp_grad,
    )


def solution(mesh):
    return jax.shard_map(
        per_device,
        mesh=mesh,
        in_specs=(
            P(("grp", "seq"), None),
            P(("grp", "seq"), None),
            P(),
            P(),
            P(("grp", "seq"), None),
            P(("grp", "seq")),
            P(("grp", "seq"), None),
            P(),
            P(("grp", "seq"), None, None),
        ),
        out_specs=(
            P(("grp", "seq"), None),
            P(("grp", "seq"), None),
            P(("grp", "seq")),
            P(("grp", "seq"), None),
            P(("grp", "seq")),
            P(("grp", "seq"), None),
            P(("grp", "seq")),
            P(("grp", "seq"), None, None),
        ),
        check_vma=False,
    )
```

```python
import functools
import math

import jax
import jax.numpy as jnp
import numpy as np
from jax import lax
from jax.experimental import pallas as pl
from jax.experimental.pallas import tpu as pltpu
from jax.sharding import PartitionSpec as P

H = 12
KVH = 2
HD = 128
FF = 8960


EPS = 1e-06
THETA = 10000.0


def rms_scale(values, gain_vec):
    return values * lax.rsqrt(jnp.mean(values * values, axis=-1, keepdims=True) + EPS) * gain_vec


def rotary_tables(positions, head_dim):
    half_dim = head_dim // 2
    freqs = THETA ** (-(jnp.arange(half_dim, dtype=jnp.float32) * 2.0) / head_dim)
    angles = positions.astype(jnp.float32)[:, None] * freqs[None, :]
    cosine_table = jnp.concatenate([jnp.cos(angles), jnp.cos(angles)], axis=-1)
    sine_table = jnp.concatenate([jnp.sin(angles), jnp.sin(angles)], axis=-1)
    return (cosine_table, sine_table)


def rotate(values, cosine_table, sine_table):
    half_dim = values.shape[-1] // 2
    turned = jnp.concatenate([-values[..., half_dim:], values[..., :half_dim]], axis=-1)
    return values * cosine_table[:, None, :] + turned * sine_table[:, None, :]


def unrotate(grad_rows, cosine_table, sine_table):
    half_dim = grad_rows.shape[-1] // 2
    scaled = grad_rows * sine_table[:, None, :]
    turned = jnp.concatenate([scaled[..., half_dim:], -scaled[..., :half_dim]], axis=-1)
    return grad_rows * cosine_table[:, None, :] + turned


def shard_starts(segments, tok_dev, prompt_len):
    shard_total = segments.shape[0]
    shard_order = jnp.arange(shard_total, dtype=jnp.int32)
    same_seg = segments[:, None] == segments[None, :]
    first_shard = jnp.min(jnp.where(same_seg, shard_order[None, :], shard_total), axis=1)
    cont_start = prompt_len + (shard_order - first_shard) * tok_dev
    return jnp.where(segments == 0, shard_order * tok_dev, cont_start)


def swish_product(gate_vals, upper_vals):
    return jax.nn.silu(gate_vals) * upper_vals


AXES = ("grp", "seq")
CONTRACT_LAST = (((1,), (1,)), ((), ()))
CONTRACT_FIRST = (((0,), (0,)), ((), ()))


MESH = pl.DeviceIdType.MESH


def remote(src, dst, send_sem, recv_sem, grp, seq):
    return pltpu.make_async_remote_copy(
        src_ref=src, dst_ref=dst, send_sem=send_sem, recv_sem=recv_sem,
        device_id=(grp, seq), device_id_type=MESH,
    )


def nearest_chip(place, order, chips):
    both = 2 * jnp.minimum(place, chips - 1 - place)
    offset = (order + 1) // 2
    side = jnp.where((order % 2 == 1) == (place < chips - 1 - place), -1, 1)
    near = place + side * offset
    rest = jnp.where(place < chips - 1 - place, order, chips - 1 - order)
    return jnp.where(order <= both, near, rest)


class Place:
    def __init__(self, chips):
        self.chips = chips
        self.grp, self.seq = lax.axis_index("grp"), lax.axis_index("seq")
        self.chip, self.core = self.seq // 2, self.seq % 2
        self.mate = self.seq + 1 - 2 * self.core

    def peer(self, offset):
        low, high = self.grp % 2, self.grp // 2
        low = 1 - low if offset % 2 else low
        high = 1 - high if offset // 2 else high
        return 2 * high + low

    def barrier(self, grps):
        barrier = pltpu.get_barrier_semaphore()
        for chip in range(self.chips):
            @pl.when(chip != self.chip)
            def _(chip=chip):
                pl.semaphore_signal(
                    barrier, inc=1, device_id=(self.grp, 2 * chip + self.core), device_id_type=MESH
                )
        pl.semaphore_signal(barrier, inc=1, device_id=(self.grp, self.mate), device_id_type=MESH)
        for offset in range(1, grps):
            pl.semaphore_signal(
                barrier, inc=1, device_id=(self.peer(offset), self.seq), device_id_type=MESH
            )
        pl.semaphore_wait(barrier, self.chips - 1 + 1 + grps - 1)


class RailGather:
    def __init__(self, place, view, send_sem, recv_sem):
        self.place, self.view, self.send_sem, self.recv_sem = place, view, send_sem, recv_sem

    def copy(self, way, chip, core):
        p = self.place
        to = (p.seq + 2, p.seq - 2, p.mate)[way]
        return remote(
            self.view(chip, core), self.view(chip, core), self.send_sem.at[way, chip],
            self.recv_sem.at[chip, core], p.grp, to,
        )

    def start(self):
        p = self.place
        pl.when(p.chip < p.chips - 1)(lambda: self.copy(0, p.chip, p.core).start())
        pl.when(p.chip > 0)(lambda: self.copy(1, p.chip, p.core).start())
        self.copy(2, p.chip, p.core).start()

    def forward(self, step):
        p = self.place

        @pl.when(p.chip - step >= 0)
        def _():
            chip = p.chip - step
            self.copy(2, chip, p.core).wait_recv()
            pl.when(p.chip < p.chips - 1)(lambda: self.copy(0, chip, p.core).start())
            self.copy(2, chip, p.core).start()

        @pl.when(p.chip + step < p.chips)
        def _():
            chip = p.chip + step
            self.copy(2, chip, p.core).wait_recv()
            pl.when(p.chip > 0)(lambda: self.copy(1, chip, p.core).start())
            self.copy(2, chip, p.core).start()

    def wait_mate(self, chip):
        self.copy(2, chip, 1 - self.place.core).wait_recv()

    def drain(self):
        p = self.place
        for chip in range(p.chips):
            self.copy(2, chip, p.core).wait_send()
            pl.when((chip <= p.chip) & (p.chip < p.chips - 1))(
                lambda chip=chip: self.copy(0, chip, p.core).wait_send()
            )
            pl.when((chip >= p.chip) & (p.chip > 0))(
                lambda chip=chip: self.copy(1, chip, p.core).wait_send()
            )


class LineScatter:
    def __init__(self, place, part, mate_in, left_in, right_in, send_sem, recv_sem):
        self.place, self.part = place, part
        self.mate_in, self.left_in, self.right_in = mate_in, left_in, right_in
        self.send_sem, self.recv_sem = send_sem, recv_sem

    def copy(self, way, src, landing, r, chip, to):
        return remote(
            src, landing.at[r, chip], self.send_sem.at[way, r, chip], self.recv_sem.at[way, r, chip],
            self.place.grp, to,
        )

    def to_mate(self, r, chip):
        p = self.place
        return self.copy(0, self.part.at[r, 2 * chip + 1 - p.core], self.mate_in, r, chip, p.mate)

    def to_right(self, r, chip):
        p = self.place
        return self.copy(1, self.part.at[r, 2 * chip + p.core], self.left_in, r, chip, p.seq + 2)

    def to_left(self, r, chip):
        p = self.place
        return self.copy(2, self.part.at[r, 2 * chip + p.core], self.right_in, r, chip, p.seq - 2)

    def step(self, r, chip):
        p = self.place
        last = p.chips - 1
        slot = 2 * chip + p.core

        @pl.when(chip != p.chip)
        def _():
            self.to_mate(r, chip).wait_recv()
            total = self.part[r, slot].astype(jnp.float32) + self.mate_in[r, chip].astype(jnp.float32)
            self.part[r, slot] = total.astype(jnp.bfloat16)

        @pl.when(chip > p.chip)
        def _():
            @pl.when(p.chip > 0)
            def _():
                self.to_right(r, chip).wait_recv()
                self.part[r, slot] = (
                    self.part[r, slot].astype(jnp.float32) + self.left_in[r, chip].astype(jnp.float32)
                ).astype(jnp.bfloat16)

            self.to_right(r, chip).start()

        @pl.when(chip < p.chip)
        def _():
            @pl.when(p.chip < last)
            def _():
                self.to_left(r, chip).wait_recv()
                self.part[r, slot] = (
                    self.part[r, slot].astype(jnp.float32) + self.right_in[r, chip].astype(jnp.float32)
                ).astype(jnp.bfloat16)

            self.to_left(r, chip).start()

    def finish(self, r, out_ref):
        p = self.place
        self.to_mate(r, p.chip).wait_recv()
        out_ref[...] = self.part[r, p.seq].astype(jnp.float32) + self.mate_in[r, p.chip].astype(jnp.float32)

        @pl.when(p.chip > 0)
        def _():
            self.to_right(r, p.chip).wait_recv()
            out_ref[...] += self.left_in[r, p.chip].astype(jnp.float32)

        @pl.when(p.chip < p.chips - 1)
        def _():
            self.to_left(r, p.chip).wait_recv()
            out_ref[...] += self.right_in[r, p.chip].astype(jnp.float32)

    def drain(self, r):
        p = self.place
        for other in range(p.chips):
            self.to_mate(r, other).wait_send()
            pl.when(other > p.chip)(lambda other=other: self.to_right(r, other).wait_send())
            pl.when(other < p.chip)(lambda other=other: self.to_left(r, other).wait_send())


def front_kernel(chips, scale,
                 tokens_ref, gain_one_ref, gain_two_ref, segment_ref, freq_ref, bias_ref,
                 cot_ref, wq_ref, wo_ref, wm_ref,
                 attn_ref, state_ref, cos_ref, sin_ref, mask_ref, q_out_ref, kv_out_ref, n1_all_ref, n2_all_ref,
                 cot_all_ref, wo_all_ref, wq_all_ref, columns_ref, wm1_ref, wm2_ref, wm3_ref,
                 nbuf, n2buf, wq, wo, bias_own, bias, stage, qbuf, kvbuf, columns,
                 lsem, n_send, n_recv, n2_send, n2_recv, c_send, c_recv, o_send, o_recv, ox_send, ox_recv,
                 om_send, om_recv, wq_send, wq_recv, b_send, b_recv, m_send, m_recv, q_send, q_recv, k_send, k_recv):
    p = Place(chips)
    grps = 4
    half = wq_ref.shape[0]
    rows = pl.ds(p.core * half, half)
    mates_rows = pl.ds((1 - p.core) * half, half)
    wm_refs = (wm_ref, wm1_ref, wm2_ref, wm3_ref)
    part = wm_ref.shape[1] // 2

    own = [
        pltpu.make_async_copy(wq_ref, wq.at[0, rows], lsem.at[0]),
        pltpu.make_async_copy(wo_ref, wo.at[p.grp, p.chip, p.core], lsem.at[2]),
        pltpu.make_async_copy(cot_ref, cot_all_ref.at[p.chip, p.core], lsem.at[3]),
    ]
    for copy in own:
        copy.start()
    tokens = tokens_ref[...].astype(jnp.float32)
    nbuf[p.chip, p.core] = rms_scale(tokens, gain_one_ref[...].astype(jnp.float32)).astype(jnp.bfloat16)
    shard = tokens.shape[0]
    lane = lax.broadcasted_iota(jnp.int32, (1, 2 * half), 1)
    bias_wide = bias_ref[...].astype(jnp.float32)
    bias_pair = jnp.concatenate([bias_wide, bias_wide], axis=1)
    bias_own[...] = jnp.broadcast_to(jnp.where(lane // half == p.core, bias_pair, 0.0), bias_own.shape)
    bias[0, p.core] = bias_own[...]
    p.barrier(grps)

    n1_line = RailGather(p, lambda chip, core: nbuf.at[chip, core], n_send, n_recv)
    cot_line = RailGather(p, lambda chip, core: cot_all_ref.at[chip, core], c_send, c_recv)
    n2_line = RailGather(p, lambda chip, core: n2buf.at[chip, core], n2_send, n2_recv)
    out_line = RailGather(p, lambda chip, core: wo.at[p.grp, chip, core], o_send, o_recv)

    def wq_direct(b):
        return remote(wq_ref, wq.at[b, rows], wq_send.at[0, b], wq_recv.at[b, 0], p.peer(b), p.seq)

    def wq_mate(b):
        return remote(wq.at[b, rows], wq.at[b, rows], wq_send.at[1, b], wq_recv.at[b, 1], p.grp, p.mate)

    def bias_direct(b):
        return remote(bias_own, bias.at[b, p.core], b_send.at[0, b], b_recv.at[b, 0], p.peer(b), p.seq)

    def bias_mate(b):
        return remote(bias.at[b, p.core], bias.at[b, p.core], b_send.at[1, b], b_recv.at[b, 1], p.grp, p.mate)

    def m_part(ref, i, j):
        return ref.at[j, pl.ds(i * part, part)]

    def m_direct(b, i, j):
        return remote(
            m_part(wm_ref, i, j), m_part(wm_refs[b], i, j), m_send.at[b, i, j], m_recv.at[b, i, j],
            p.peer(b), p.seq,
        )

    def m_forward(b, j):
        return remote(
            m_part(wm_refs[b], b - 1, j), m_part(wm3_ref, b - 1, j), m_send.at[3, b - 1, j],
            m_recv.at[3, b - 1, j], p.peer(3 - b), p.seq,
        )

    def out_cross(b, chip):
        view = wo.at[p.grp, chip, p.core]
        return remote(view, view, ox_send.at[b, chip], ox_recv.at[b, chip], p.peer(b), p.seq)

    def out_arrival(b, chip):
        view = wo.at[p.peer(b), chip, p.core]
        return remote(view, view, ox_send.at[b, chip], ox_recv.at[b, chip], p.grp, p.mate)

    def out_mate(b, core):
        view = wo.at[p.peer(b), :, core]
        return remote(view, view, om_send.at[b], om_recv.at[b], p.grp, p.mate)

    def q_copy(chip):
        return remote(
            stage.at[chip, pl.ds(0, 3)], qbuf.at[p.chip], q_send.at[chip], q_recv.at[p.chip],
            p.grp, 2 * chip + p.core,
        )

    def q_arrival(chip):
        return remote(stage.at[chip, pl.ds(0, 3)], qbuf.at[chip], q_send.at[chip], q_recv.at[chip], p.grp, p.mate)

    def k_copy(chip, to_chip):
        return remote(
            stage.at[chip, 3], kvbuf.at[p.chip, p.core, chip], k_send.at[0, chip, to_chip],
            k_recv.at[p.chip, p.core, chip], p.grp, 2 * to_chip + p.core,
        )

    def k_mate(head, chip, src=None):
        view = kvbuf.at[head, p.core, chip]
        return remote(
            view if src is None else src, view, k_send.at[1, head, chip],
            k_recv.at[head, p.core, chip], p.grp, p.mate,
        )

    def k_arrival(head, core, chip):
        view = kvbuf.at[head, core, chip]
        return remote(view, view, k_send.at[1, head, chip], k_recv.at[head, core, chip], p.grp, p.mate)

    def make_tables():
        segs = [segment_ref[p.grp, t] for t in range(2 * chips)]
        starts = []
        for t in range(2 * chips):
            first = jnp.int32(t)
            for other in reversed(range(t)):
                first = jnp.where(segs[other] == segs[t], jnp.int32(other), first)
            starts.append(
                jnp.where(segs[t] == 0, jnp.int32(t * shard), chips * shard + (t - first) * shard)
            )

        def own_of(values):
            own = values[0]
            for t in range(1, 2 * chips):
                own = jnp.where(p.seq == t, values[t], own)
            return own

        own_seg, own_start = own_of(segs), own_of(starts)
        row = lax.broadcasted_iota(jnp.int32, (shard, 2 * half), 0)
        column = lax.broadcasted_iota(jnp.int32, (shard, 2 * half), 1)
        freq = freq_ref[...]
        sign = jnp.where(column < half, -1.0, 1.0)
        for chip in range(chips):
            start = jnp.where(p.core == 0, starts[2 * chip], starts[2 * chip + 1])
            angle = (start + row).astype(jnp.float32) * freq
            cos_ref[chip] = jnp.cos(angle)
            sin_ref[chip] = jnp.sin(angle) * sign
        for core in range(2):
            for chip in range(chips):
                t = 2 * chip + core
                seen = jnp.where((segs[t] == 0) | (segs[t] == own_seg), jnp.int32(1), jnp.int32(0))
                allowed = (starts[t] + column <= own_start + row) & (row * 0 + seen > 0)
                block = core * chips + chip
                mask_ref[:, block * shard : (block + 1) * shard] = jnp.where(allowed, 0.0, -1e30)

    own[0].wait()
    for b in range(1, grps):
        wq_direct(b).start()
        bias_direct(b).start()
    wq_mate(0).start()
    bias_mate(0).start()
    n1_line.start()
    own[1].wait()
    out_line.start()
    for b in range(1, grps):
        wq_direct(b).wait_recv()
        wq_mate(b).start()
        bias_direct(b).wait_recv()
        bias_mate(b).start()
    for b in range(1, grps):
        out_cross(b, p.chip).start()
    for j in range(3):
        m_direct(1, 0, j).start()
        m_direct(2, 1, j).start()
    make_tables()
    for b in range(grps):
        wq_mate(b).wait_recv()
        bias_mate(b).wait_recv()

    @pl.loop(0, chips)
    def _(order):
        @pl.when(order > 0)
        def _():
            n1_line.forward(order)
            out_line.forward(order)
            for b in range(1, grps):
                pl.when(p.chip - order >= 0)(lambda b=b: out_cross(b, p.chip - order).start())
                pl.when(p.chip + order < chips)(lambda b=b: out_cross(b, p.chip + order).start())

        at = nearest_chip(p.chip, order, chips)
        x = nbuf[at, p.core]
        weights = wq[...].reshape(grps * 2 * half, x.shape[1])
        rows_all = lax.dot_general(x, weights, CONTRACT_LAST, preferred_element_type=jnp.float32)
        cosine, sine = cos_ref[at], sin_ref[at]
        for b in range(grps):
            u = rows_all[:, 2 * half * b : 2 * half * (b + 1)] + (bias[b, 0, 0:1] + bias[b, 1, 0:1])
            turned = u * cosine + pltpu.roll(u, half, 1) * sine
            place = p.peer(b)
            keep = jnp.where((place == grps - 1) & (p.chip >= chips // 2), 1.0, 0.0)
            value = (u * keep + turned * (1.0 - keep)).astype(jnp.bfloat16)
            stage[at, place] = value

            @pl.when(place == grps - 1)
            def _(value=value):
                kvbuf[p.chip, p.core, at] = value

            @pl.when((place < grps - 1) & (at == p.chip))
            def _(value=value, place=place):
                qbuf[p.chip, place] = value

        pl.when(at != p.chip)(lambda: q_copy(at).start())
        for to_chip in range(chips):
            pl.when(to_chip != p.chip)(lambda to_chip=to_chip: k_copy(at, to_chip).start())
        k_mate(p.chip, at, stage.at[at, 3]).start()


    @pl.loop(0, chips)
    def _(order):
        for head in range(chips):
            @pl.when(head != p.chip)
            def _(head=head):
                chip = nearest_chip(head, order, chips)
                k_arrival(head, p.core, chip).wait_recv()
                k_mate(head, chip).start()

    for chip in range(chips):
        pl.when(chip != p.chip)(lambda chip=chip: q_arrival(chip).wait_recv())
        for head in range(chips):
            k_arrival(head, 1 - p.core, chip).wait_recv()
    own[2].wait()
    cot_line.start()
    for j in (0, 1):
        for b in (1, 2):
            m_direct(b, b - 1, j).wait_recv()
            m_forward(b, j).start()
    for j in range(3):
        m_direct(1, 1, j).start()
        m_direct(2, 0, j).start()

    mask = mask_ref[...]
    heads_per = H // KVH
    for kv in range(KVH):
        heads = [kv * heads_per + i for i in range(heads_per)]
        queries = jnp.concatenate([qbuf[h % chips, h // chips] for h in heads], axis=0)
        keys = kvbuf[kv].reshape(mask.shape[1], 2 * half)
        values = kvbuf[KVH + kv].reshape(mask.shape[1], 2 * half)
        scores = lax.dot_general(queries, keys, CONTRACT_LAST, preferred_element_type=jnp.float32) * scale
        scores = scores.reshape(heads_per, shard, mask.shape[1]) + mask[None]
        weights = jnp.exp(scores - jnp.max(scores, axis=-1, keepdims=True))
        inverse = 1.0 / jnp.sum(weights, axis=-1, keepdims=True)
        probs = (weights * inverse).astype(jnp.bfloat16).reshape(heads_per * shard, mask.shape[1])
        mixed = jnp.dot(probs, values, preferred_element_type=jnp.float32)
        for i, h in enumerate(heads):
            attn_ref[:, h * 2 * half : (h + 1) * 2 * half] = mixed[i * shard : (i + 1) * shard]
        cot_line.forward(kv + 1)

    for b in range(1, grps):
        for chip in range(chips):
            out_arrival(b, chip).wait_recv()
        out_mate(b, p.core).start()
    for b in (1, 2):
        m_direct(b, b - 1, 2).wait_recv()
        m_forward(b, 2).start()
    attn_low = attn_ref[...].astype(jnp.bfloat16)
    unit = wo.shape[3]
    for owner in range(grps):
        columns[owner] = attn_low[:, owner * columns.shape[2] : (owner + 1) * columns.shape[2]]
    for b in range(1, grps):
        out_mate(b, 1 - p.core).wait_recv()
    for chip in range(chips):
        out_line.wait_mate(chip)
    state = tokens_ref[...].astype(jnp.float32) + jnp.dot(
        attn_low, wo[...].reshape(grps * chips * 2 * unit, tokens_ref.shape[1]),
        preferred_element_type=jnp.float32,
    )
    state_ref[...] = state
    n2buf[p.chip, p.core] = rms_scale(state, gain_two_ref[...].astype(jnp.float32)).astype(jnp.bfloat16)
    n2_line.start()
    cot_line.forward(3)
    outs = [
        pltpu.make_async_copy(nbuf, n1_all_ref, lsem.at[4]),
        pltpu.make_async_copy(wq, wq_all_ref, lsem.at[5]),
        pltpu.make_async_copy(qbuf, q_out_ref, lsem.at[6]),
        pltpu.make_async_copy(kvbuf, kv_out_ref, lsem.at[7]),
        pltpu.make_async_copy(wo, wo_all_ref, lsem.at[8]),
        pltpu.make_async_copy(columns, columns_ref, lsem.at[9]),
    ]
    for chip in range(chips):
        n1_line.wait_mate(chip)
    for copy in outs:
        copy.start()
    for step in range(1, chips):
        n2_line.forward(step)
    for chip in range(chips):
        cot_line.wait_mate(chip)
        n2_line.wait_mate(chip)
    last = pltpu.make_async_copy(n2buf, n2_all_ref, lsem.at[10])
    last.start()
    for b in (1, 2):
        for j in range(3):
            m_direct(b, 2 - b, j).wait_recv()
            m_forward(3 - b, j).wait_recv()
    for copy in outs:
        copy.wait()
    last.wait()
    n1_line.drain()
    n2_line.drain()
    out_line.drain()
    cot_line.drain()
    for b in range(grps):
        wq_mate(b).wait_send()
        bias_mate(b).wait_send()
    for b in range(1, grps):
        wq_direct(b).wait_send()
        bias_direct(b).wait_send()
        out_mate(b, p.core).wait_send()
        for chip in range(chips):
            out_cross(b, chip).wait_send()
    for b in (1, 2):
        for i in (0, 1):
            for j in range(3):
                m_direct(b, i, j).wait_send()
        for j in range(3):
            m_forward(b, j).wait_send()
    for chip in range(chips):
        pl.when(chip != p.chip)(lambda chip=chip: q_copy(chip).wait_send())
        for other in range(chips):
            pl.when(other != p.chip)(lambda chip=chip, other=other: k_copy(chip, other).wait_send())
            k_mate(other, chip).wait_send()


def front_call(tokens, gain_one, gain_two, segments, freqs, bias, cot, qkv_weight, out_weight, mlp_rows):
    chips = segments.shape[1] // 2
    grps = 4
    shard, width = tokens.shape
    half = qkv_weight.shape[0]
    vm, dma = pltpu.VMEM, pltpu.SemaphoreType.DMA
    anyspace = pl.BlockSpec(memory_space=pl.ANY)
    vspec = pl.BlockSpec(memory_space=pltpu.VMEM)
    low, wide = jnp.bfloat16, jnp.float32
    struct = jax.ShapeDtypeStruct
    wo_shape = (grps, chips, 2) + out_weight.shape
    columns_shape = (grps, shard, H * HD // grps)
    return pl.pallas_call(
        functools.partial(front_kernel, chips, 1.0 / math.sqrt(HD)),
        out_shape=(
            struct((shard, H * HD), wide),
            struct((shard, width), wide),
            struct((chips, shard, HD), wide),
            struct((chips, shard, HD), wide),
            struct((shard, 2 * chips * shard), wide),
            struct((chips, 3, shard, HD), low),
            struct((chips, 2, chips, shard, HD), low),
            struct((chips, 2, shard, width), low),
            struct((chips, 2, shard, width), low),
            struct((chips, 2, shard, width), low),
            struct(wo_shape, low),
            struct((grps, 2 * half, width), low),
            struct(columns_shape, low),
        ) + (struct(mlp_rows.shape, low),) * 3,
        in_specs=[vspec] * 3
        + [pl.BlockSpec(memory_space=pltpu.SMEM)]
        + [vspec] * 2
        + [anyspace] * 4,
        out_specs=(vspec,) * 5 + (anyspace,) * 11,
        scratch_shapes=[
            vm((chips, 2, shard, width), low),
            vm((chips, 2, shard, width), low),
            vm((grps, 2 * half, width), low),
            vm(wo_shape, low),
            vm((8, HD), wide),
            vm((grps, 2, 8, HD), wide),
            vm((chips, grps, shard, HD), low),
            vm((chips, 3, shard, HD), low),
            vm((chips, 2, chips, shard, HD), low),
            vm(columns_shape, low),
            dma((11,)),
            dma((3, chips)), dma((chips, 2)),
            dma((3, chips)), dma((chips, 2)),
            dma((3, chips)), dma((chips, 2)),
            dma((3, chips)), dma((chips, 2)),
            dma((grps, chips)), dma((grps, chips)), dma((grps,)), dma((grps,)),
            dma((2, grps)), dma((grps, 2)),
            dma((2, grps)), dma((grps, 2)),
            dma((grps, 2, 3)), dma((grps, 2, 3)),
            dma((chips,)), dma((chips,)),
            dma((2, chips, chips)), dma((chips, 2, chips)),
        ],
        compiler_params=pltpu.CompilerParams(
            collective_id=2, has_side_effects=True, vmem_limit_bytes=60 * 2**20
        ),
        name="front",
    )(tokens, gain_one, gain_two, segments, freqs, bias, cot, qkv_weight, out_weight, mlp_rows)


FIRST_HOPS = ((1, 0, 1), (3, 0, 1), (2, 1, 2), (3, 1, 2))
EARLY_HOPS = tuple((hop, kind) for kind in (2, 0) for hop in (1, 3, 0, 2))


def mlp_kernel(chips, grps, row_tiles, n2_ref, cot_ref, columns_ref, *refs):
    w_refs, refs = refs[:grps], refs[grps:]
    (
        n2g_ref, outp_ref, grads_ref, owned_ref, passing_ref, arrived_ref, tok, w, acts, part, mate_in, left_in, right_in, stage,
        lsem, ssend, srecv, wsem, osem, a_send, a_recv, e_send, e_recv,
    ) = refs
    p = Place(chips)
    shard, width = n2_ref.shape[1:]
    units = w.shape[1]
    block = units // grps
    tile = units // row_tiles
    loads = [
        pltpu.make_async_copy(n2_ref, tok.at[0], lsem.at[0]),
        pltpu.make_async_copy(cot_ref, tok.at[1], lsem.at[1]),
        pltpu.make_async_copy(columns_ref.at[p.grp], owned_ref.at[0], lsem.at[2]),
    ]
    loads[0].start()

    def w_copy(j, b):
        return pltpu.make_async_copy(w_refs[b].at[j], w.at[j, pl.ds(b * block, block)], wsem.at[j, b])

    for j in range(3):
        for b in range(grps):
            w_copy(j, b).start()
    for copy in loads[1:]:
        copy.start()

    barrier = pltpu.get_barrier_semaphore()
    inner = jnp.where((p.chip > 0) & (p.chip < chips - 1), 1, 0)

    def greet(grp, seq):
        pl.semaphore_signal(barrier, inc=1, device_id=(grp, seq), device_id_type=MESH)

    greet(p.grp, p.mate)
    pl.when(p.chip > 0)(lambda: greet(p.grp, p.seq - 2))
    pl.when(p.chip < chips - 1)(lambda: greet(p.grp, p.seq + 2))
    for b in range(1, grps):
        greet(p.peer(b), p.seq)
    pl.semaphore_wait(barrier, 2 + inner + grps - 1)
    scatter = LineScatter(p, part, mate_in, left_in, right_in, ssend, srecv)

    def a_copy(b):
        return remote(
            columns_ref.at[p.peer(b)], owned_ref.at[b], a_send.at[b], a_recv.at[b], p.peer(b), p.seq
        )

    for b in range(1, grps):
        a_copy(b).start()
    loads[0].wait()
    for j in range(2):
        for b in range(grps):
            w_copy(j, b).wait()

    def kind_of(t):
        return (t // row_tiles + 2) % 3

    def early(slot, kind):
        b, i, to = FIRST_HOPS[slot]
        half = block // 2
        rows = grads_ref.at[kind, pl.ds(b * block + i * half, half)]
        land = arrived_ref.at[kind // 2, pl.ds(i * half, half)] if b < 3 else passing_ref.at[i, kind]
        at = EARLY_HOPS.index((slot, kind))
        return remote(rows, land, e_send.at[at], e_recv.at[at], p.peer(to), p.seq)

    def out_copy(t):
        return pltpu.make_async_copy(
            stage.at[t % 2],
            grads_ref.at[kind_of(t), pl.ds((t % row_tiles) * tile, tile)],
            osem.at[t % 2],
        )

    def tile_grad(t):
        kind = kind_of(t)
        lhs = acts[kind, :, pl.ds(pl.multiple_of((t % row_tiles) * tile, 128), tile)]
        rhs = tok[kind // 2].reshape(2 * chips * shard, width)
        stage[t % 2] = lax.dot_general(
            lhs, rhs, CONTRACT_FIRST, preferred_element_type=jnp.float32
        ).astype(jnp.bfloat16)
        out_copy(t).start()

    def start_early(kind):
        for hop in EARLY_HOPS:
            if hop[1] == kind:
                early(*hop).start()

    def far_chip(order):
        return nearest_chip(p.chip, chips - 1 - order, chips)

    outer = (p.chip == 0) | (p.chip == chips - 1)

    @pl.loop(0, chips + 1)
    def _(order):
        @pl.when(order < chips)
        def _():
            at = far_chip(order)
            x = tok[0, pl.ds(2 * at, 2)].reshape(2 * shard, width)
            gate = lax.dot_general(x, w[0], CONTRACT_LAST, preferred_element_type=jnp.float32)
            up = lax.dot_general(x, w[1], CONTRACT_LAST, preferred_element_type=jnp.float32)
            sig = 1.0 / (1.0 + jnp.exp(-gate))
            silu = gate * sig
            rows = pl.ds(at * (2 * shard), 2 * shard)
            acts[0, rows] = (up * sig * (1.0 + gate * (1.0 - sig))).astype(jnp.bfloat16)
            acts[1, rows] = silu.astype(jnp.bfloat16)
            hidden = (silu * up).astype(jnp.bfloat16)
            acts[2, rows] = hidden

            @pl.when(order == 0)
            def _():
                for b in range(grps):
                    w_copy(2, b).wait()

            part[1, pl.ds(2 * at, 2)] = (
                jnp.dot(hidden, w[2], preferred_element_type=jnp.float32)
                .astype(jnp.bfloat16).reshape(2, shard, width)
            )
            scatter.to_mate(1, at).start()

        pl.when(outer & (order > 0))(lambda: scatter.step(1, far_chip(order - 1)))

    for copy in loads[1:]:
        copy.wait()

    @pl.loop(0, row_tiles)
    def _(t):
        pl.when(t >= 2)(lambda: out_copy(t - 2).wait())
        tile_grad(t)
        pl.when(jnp.logical_not(outer))(lambda: scatter.step(1, far_chip(t)))

    @pl.loop(0, chips)
    def _(order):
        at = far_chip(order)
        y = tok[1, pl.ds(2 * at, 2)].reshape(2 * shard, width)
        unit_grad = lax.dot_general(y, w[2], CONTRACT_LAST, preferred_element_type=jnp.float32)
        rows = pl.ds(at * (2 * shard), 2 * shard)
        acts[0, rows] = (unit_grad * acts[0, rows].astype(jnp.float32)).astype(jnp.bfloat16)
        acts[1, rows] = (unit_grad * acts[1, rows].astype(jnp.float32)).astype(jnp.bfloat16)

        @pl.when(order == 0)
        def _():
            out_copy(row_tiles - 2).wait()
            out_copy(row_tiles - 1).wait()
            start_early(2)

    @pl.loop(0, chips + 1)
    def _(order):
        @pl.when(order < chips)
        def _():
            at = far_chip(order)
            rows = pl.ds(at * (2 * shard), 2 * shard)
            back = jnp.dot(acts[0, rows], w[0], preferred_element_type=jnp.float32) + jnp.dot(
                acts[1, rows], w[1], preferred_element_type=jnp.float32
            )
            part[0, pl.ds(2 * at, 2)] = back.astype(jnp.bfloat16).reshape(2, shard, width)
            scatter.to_mate(0, at).start()

        @pl.when(order < row_tiles)
        def _():
            t = row_tiles + order
            pl.when(order >= 2)(lambda: out_copy(t - 2).wait())
            tile_grad(t)

        @pl.when(order == row_tiles)
        def _():
            out_copy(2 * row_tiles - 2).wait()
            out_copy(2 * row_tiles - 1).wait()
            start_early(0)

        pl.when(outer & (order > 0))(lambda: scatter.step(0, far_chip(order - 1)))
        pl.when(jnp.logical_not(outer) & (order >= 3))(lambda: scatter.step(0, far_chip(order - 3)))

    @pl.loop(2 * row_tiles, 3 * row_tiles)
    def _(t):
        pl.when(t >= 2 * row_tiles + 2)(lambda: out_copy(t - 2).wait())
        late = t - 2 * row_tiles + chips + 1 - 3
        pl.when(jnp.logical_not(outer) & (late < chips))(lambda: scatter.step(0, far_chip(late)))
        tile_grad(t)

    scatter.finish(0, n2g_ref)
    scatter.finish(1, outp_ref)
    out_copy(3 * row_tiles - 2).wait()
    out_copy(3 * row_tiles - 1).wait()
    for hop in EARLY_HOPS:
        early(*hop).wait_recv()
        early(*hop).wait_send()
    scatter.drain(0)
    scatter.drain(1)
    for b in range(1, grps):
        a_copy(b).wait_recv()
        a_copy(b).wait_send()


def mlp_call(n2_all, cot_all, columns, w_blocks, row_tiles=3):
    grps, (_, block, width) = len(w_blocks), w_blocks[0].shape
    slots, shard, _ = cot_all.shape
    chips = slots // 2
    units = grps * block
    vm, anyspace = pltpu.VMEM, pl.BlockSpec(memory_space=pl.ANY)
    vspec = pl.BlockSpec(memory_space=pltpu.VMEM)
    dma = pltpu.SemaphoreType.DMA
    return pl.pallas_call(
        functools.partial(mlp_kernel, chips, grps, row_tiles),
        out_shape=(
            jax.ShapeDtypeStruct((shard, width), jnp.float32),
            jax.ShapeDtypeStruct((shard, width), jnp.float32),
            jax.ShapeDtypeStruct((3, units, width), jnp.bfloat16),
            jax.ShapeDtypeStruct(columns.shape, jnp.bfloat16),
            jax.ShapeDtypeStruct((2, 3, block // 2, width), jnp.bfloat16),
            jax.ShapeDtypeStruct((2, block, width), jnp.bfloat16),
        ),
        in_specs=[anyspace] * (3 + grps),
        out_specs=(vspec, vspec) + (anyspace,) * 4,
        scratch_shapes=[
            vm((2, slots, shard, width), jnp.bfloat16),
            vm((3, units, width), jnp.bfloat16),
            vm((3, slots * shard, units), jnp.bfloat16),
            vm((2, slots, shard, width), jnp.bfloat16),
            vm((2, chips, shard, width), jnp.bfloat16),
            vm((2, chips, shard, width), jnp.bfloat16),
            vm((2, chips, shard, width), jnp.bfloat16),
            vm((2, units // row_tiles, width), jnp.bfloat16),
            dma((3,)), dma((3, 2, chips)), dma((3, 2, chips)),
            dma((3, grps)), dma((2,)), dma((grps,)), dma((grps,)),
            dma((len(EARLY_HOPS),)), dma((len(EARLY_HOPS),)),
        ],
        compiler_params=pltpu.CompilerParams(
            collective_id=1, has_side_effects=True, vmem_limit_bytes=62 * 2**20
        ),
        name="mlp",
    )(n2_all, cot_all, columns, *w_blocks)


def unturn(rows, cosine, sine, half):
    return rows * cosine + pltpu.roll(rows * sine, half, 1)


def back_kernel(chips, scale,
                n2g_ref, state_ref, cot_ref, tokens_ref, gain_one_ref, gain_two_ref, attn_ref, q_ref, kv_ref,
                mask_ref, cos_ref, sin_ref, wq_ref, wo_ref, n1_ref, terms_ref, owned_ref, passing_ref, early_ref,
                tok_grad_ref, wq_grad_ref, wo_grad_ref, gain_ref, direct_ref, second_ref,
                wo, stbuf, n1x, at_all, dq_stage, gq_in, kv_part, km_in, k_sum, k_own, kr_in,
                cols, part, left_in, right_in, wgrad, wm_in, w_send_buf, w_in, o_terms, ob_in, o_send_buf, o_in,
                m_own, m_in, early_rows, gain_own, gain_in, gain_mid, gain_mid_in, state_grad,
                lsem, s_send, s_recv, q_send, q_recv, km_send, km_recv, kr_send, kr_recv,
                r_send, r_recv, wm_send, wm_recv, w_send, w_recv, ob_send, ob_recv, o_send, o_recv, m_send, m_recv,
                ml_sem, g_send, g_recv, h_send, h_recv):
    p = Place(chips)
    grps = 4
    shard, width = n2g_ref.shape
    slots = 2 * chips
    heads_per = H // KVH
    half = HD // 2
    low, wide = jnp.bfloat16, jnp.float32
    block = terms_ref.shape[1] // grps
    mhalf = block // 2
    last = chips - 1

    loads = [
        pltpu.make_async_copy(wo_ref, wo, lsem.at[0]),
        pltpu.make_async_copy(n1_ref.at[:, p.core], n1x.at[:, :, pl.ds(0, width)], lsem.at[1]),
        pltpu.make_async_copy(owned_ref, at_all, lsem.at[2]),
    ]
    for copy in loads:
        copy.start()

    def seq_peer(i):
        return (p.seq + i) % slots

    barrier = pltpu.get_barrier_semaphore()
    for i in range(1, slots):
        pl.semaphore_signal(barrier, inc=1, device_id=(p.grp, seq_peer(i)), device_id_type=MESH)
    for b in range(1, grps):
        pl.semaphore_signal(barrier, inc=1, device_id=(p.peer(b), p.seq), device_id_type=MESH)
    pl.semaphore_wait(barrier, slots - 1 + grps - 1)

    def m_rows(b, i, kind):
        return terms_ref.at[kind, pl.ds(b * block + i * mhalf, mhalf)]

    def m_first(hop, kind):
        b, i, to = FIRST_HOPS[hop]
        land = direct_ref.at[kind, pl.ds(i * mhalf, mhalf)] if b < 3 else m_in.at[i, kind]
        return remote(
            m_rows(b, i, kind), land, m_send.at[hop, kind], m_recv.at[hop, kind], p.peer(to), p.seq
        )

    def m_second(i, kind):
        return remote(
            m_own.at[i, kind], second_ref.at[kind, pl.ds(i * mhalf, mhalf)], m_send.at[4 + i, kind],
            m_recv.at[4 + i, kind], p.peer(2 - i), p.seq,
        )

    late_hops = [(hop, kind) for kind in (1, 0, 2) for hop in (1, 3, 0, 2) if (hop, kind) not in EARLY_HOPS]
    for hop in late_hops:
        m_first(*hop).start()
    m_loads = [
        pltpu.make_async_copy(m_rows(2 - i, i, kind), m_own.at[i, kind], ml_sem.at[i, kind])
        for i in (0, 1)
        for kind in range(3)
    ]
    for hop, kind in EARLY_HOPS:
        if FIRST_HOPS[hop][0] == 3:
            i = FIRST_HOPS[hop][1]
            m_loads.append(pltpu.make_async_copy(passing_ref.at[i, kind], m_in.at[i, kind], ml_sem.at[2 + i, kind]))
    early_kinds = [kind for kind in (0, 2) if (0, kind) in EARLY_HOPS]
    early_loads = [
        pltpu.make_async_copy(early_ref.at[kind // 2], early_rows.at[kind // 2], ml_sem.at[4, kind])
        for kind in early_kinds
    ]
    early_copies = [
        pltpu.make_async_copy(early_rows.at[kind // 2], direct_ref.at[kind], ml_sem.at[4, kind])
        for kind in early_kinds
    ]
    m_loads += early_loads
    for copy in m_loads:
        copy.start()

    def m_turn(kind):
        for i in (0, 1):
            if (1 + 2 * i, kind) in late_hops:
                m_first(1 + 2 * i, kind).wait_recv()

            @pl.loop(0, mhalf // 16)
            def _(t, i=i):
                rows = pl.ds(pl.multiple_of(t * 16, 16), 16)
                m_own[i, kind, rows] = (
                    m_own[i, kind, rows].astype(wide) + m_in[i, kind, rows].astype(wide)
                ).astype(low)

            m_second(i, kind).start()

    state = state_ref[...]
    gain_two = gain_two_ref[...].astype(wide)
    n2g = n2g_ref[...]
    scale_two = lax.rsqrt(jnp.mean(state * state, axis=-1, keepdims=True) + EPS)
    normed = state * scale_two
    gain_own[1] = jnp.sum(n2g * normed, axis=0, keepdims=True)
    lifted = n2g * gain_two
    state_grad[...] = cot_ref[...].astype(wide) + scale_two * (
        lifted - normed * jnp.mean(lifted * normed, axis=-1, keepdims=True)
    )
    state_low = state_grad[...].astype(low)
    stbuf[0] = state_low

    def state_copy(b):
        return remote(stbuf.at[0], stbuf.at[b], s_send.at[b], s_recv.at[b], p.peer(b), p.seq)

    for b in range(1, grps):
        state_copy(b).start()
    attn = attn_ref[...]
    unit = wo.shape[0] // (grps * slots)
    loads[0].wait()
    attn_grad = lax.dot_general(state_low, wo[...], CONTRACT_LAST, preferred_element_type=wide).astype(low)
    mask = mask_ref[...]
    keys_total = mask.shape[1]
    own_cos, own_sin = cos_ref[p.chip], sin_ref[p.chip]

    def km_copy(head):
        return remote(
            kv_part.at[head, 1 - p.core], km_in.at[head], km_send.at[head], km_recv.at[head], p.grp, p.mate
        )

    def kr_copy(head):
        return remote(
            k_sum.at[head], kr_in.at[p.chip], kr_send.at[head], kr_recv.at[p.chip], p.grp, 2 * head + p.core
        )

    def kr_arrival(chip):
        return remote(k_sum.at[chip], kr_in.at[chip], kr_send.at[chip], kr_recv.at[chip], p.grp, p.mate)

    q_parts = (pl.ds(0, 1), pl.ds(1, 2))

    def q_copy(chip, i):
        return remote(
            dq_stage.at[chip, q_parts[i]], gq_in.at[p.chip, q_parts[i]], q_send.at[chip, i],
            q_recv.at[p.chip, i], p.grp, 2 * chip + p.core,
        )

    def q_arrival(chip, i):
        return remote(
            dq_stage.at[chip, q_parts[i]], gq_in.at[chip, q_parts[i]], q_send.at[chip, i],
            q_recv.at[chip, i], p.grp, p.mate,
        )

    def key_sum(head):
        km_copy(head).wait_recv()
        total = kv_part[head, p.core].astype(wide) + km_in[head].astype(wide)

        @pl.when(p.chip == head)
        def _():
            k_own[...] = total

        @pl.when(p.chip != head)
        def _():
            k_sum[head] = total.astype(low)
            kr_copy(head).start()

    for kv in range(KVH):
        heads = [kv * heads_per + i for i in range(heads_per)]
        queries = jnp.concatenate([q_ref[h % chips, h // chips] for h in heads], axis=0)
        grads = jnp.concatenate([attn_grad[:, h * HD : (h + 1) * HD] for h in heads], axis=0)
        mixed = jnp.concatenate([attn[:, h * HD : (h + 1) * HD] for h in heads], axis=0)
        delta = jnp.sum(grads.astype(wide) * mixed, axis=-1, keepdims=True)
        keys = kv_ref[kv].reshape(keys_total, HD)
        values = kv_ref[KVH + kv].reshape(keys_total, HD)
        scores = lax.dot_general(queries, keys, CONTRACT_LAST, preferred_element_type=wide) * scale
        scores = (scores.reshape(heads_per, shard, keys_total) + mask[None]).reshape(heads_per * shard, keys_total)
        weights = jnp.exp(scores - jnp.max(scores, axis=-1, keepdims=True))
        probs = weights * (1.0 / jnp.sum(weights, axis=-1, keepdims=True))
        prob_grad = lax.dot_general(grads, values, CONTRACT_LAST, preferred_element_type=wide)
        score_grad = (probs * (prob_grad - delta)).astype(low)
        key_grad = lax.dot_general(score_grad, queries, CONTRACT_FIRST, preferred_element_type=wide) * scale
        value_grad = lax.dot_general(probs.astype(low), grads, CONTRACT_FIRST, preferred_element_type=wide)
        kv_part[kv] = key_grad.astype(low).reshape(2, chips, shard, HD)
        kv_part[KVH + kv] = value_grad.astype(low).reshape(2, chips, shard, HD)
        km_copy(kv).start()
        km_copy(KVH + kv).start()
        query_grad = jnp.dot(score_grad, keys, preferred_element_type=wide) * scale
        for i, h in enumerate(heads):
            turned = unturn(query_grad[i * shard : (i + 1) * shard], own_cos, own_sin, half).astype(low)
            dq_stage[h % chips, h // chips] = turned

            @pl.when(p.chip == h % chips)
            def _(turned=turned, h=h):
                gq_in[h % chips, h // chips] = turned

        for chip in range(chips):
            pl.when(chip != p.chip)(lambda chip=chip: q_copy(chip, kv).start())
        if kv == 0:
            for copy in m_loads:
                copy.wait()
            for copy in early_copies:
                copy.start()
            m_turn(2)
            m_turn(0)
            key_sum(0)
            key_sum(KVH)
    key_sum(1)
    key_sum(KVH + 1)
    m_turn(1)
    loads[1].wait()
    lane = lax.broadcasted_iota(jnp.int32, (chips, shard, HD), 2)
    n1x[:, :, width:] = jnp.where(lane == 0, 1.0, 0.0).astype(low)

    for chip in range(chips):
        for i in (0, 1):
            pl.when(chip != p.chip)(lambda chip=chip, i=i: q_arrival(chip, i).wait_recv())
        pl.when(chip != p.chip)(lambda chip=chip: kr_arrival(chip).wait_recv())
    is_value = jnp.where(p.chip >= chips // 2, 1.0, 0.0)

    gain_one = gain_one_ref[...].astype(wide)
    gain_own[0] = jnp.zeros_like(gain_own[0])

    def to_right(chip):
        return remote(part.at[chip], left_in.at[chip], r_send.at[0, chip], r_recv.at[0, chip], p.grp, p.seq + 2)

    def to_left(chip):
        return remote(part.at[chip], right_in.at[chip], r_send.at[1, chip], r_recv.at[1, chip], p.grp, p.seq - 2)

    @pl.loop(0, chips)
    def _(order):
        chip = nearest_chip(p.chip, last - order, chips)
        key_total = k_own[chip]
        for other in range(chips):
            key_total = key_total + jnp.where(other == p.chip, 0.0, kr_in[other, chip].astype(wide))
        turned = unturn(key_total, cos_ref[chip], sin_ref[chip], half)
        last_head = (key_total * is_value + turned * (1.0 - is_value)).astype(low)
        for b in range(grps):
            place = p.peer(b)
            query_head = gq_in[chip, jnp.minimum(place, grps - 2)]
            cols[chip, :, b * HD : (b + 1) * HD] = jnp.where(place == grps - 1, last_head, query_head)
        terms = jnp.dot(cols[chip], wq_ref[...], preferred_element_type=wide)
        part[chip] = terms.astype(low)
        gain_own[0] += jnp.sum(terms * n1x[chip, :, 0:width].astype(wide), axis=0, keepdims=True)
        pl.when((p.chip == 0) & (chip > 0))(lambda: to_right(chip).start())
        pl.when((p.chip == last) & (chip < last))(lambda: to_left(chip).start())

    gain_own[0] = gain_own[0] / gain_one

    def g_copy(i):
        return remote(gain_own, gain_in.at[i], g_send.at[i], g_recv.at[i], p.grp, seq_peer(i))

    def h_copy(b):
        return remote(gain_mid, gain_mid_in.at[b], h_send.at[b], h_recv.at[b], p.peer(b), p.seq)

    for i in range(1, slots):
        g_copy(i).start()

    def right_step(chip):
        @pl.when((chip > p.chip) & (p.chip > 0))
        def _():
            to_right(chip).wait_recv()
            part[chip] = (part[chip].astype(wide) + left_in[chip].astype(wide)).astype(low)
            to_right(chip).start()

    def left_step(chip):
        @pl.when((chip < p.chip) & (p.chip < last))
        def _():
            to_left(chip).wait_recv()
            part[chip] = (part[chip].astype(wide) + right_in[chip].astype(wide)).astype(low)
            to_left(chip).start()

    near_left = p.chip < chips // 2

    def rail_step(order):
        if order < chips:
            pl.when(near_left)(lambda: right_step(last - order))
            pl.when(jnp.logical_not(near_left))(lambda: left_step(order))
        else:
            pl.when(near_left)(lambda: left_step(order - chips))
            pl.when(jnp.logical_not(near_left))(lambda: right_step(2 * chips - 1 - order))

    rail_step(0)
    wgrad[...] = lax.dot_general(
        cols[...].reshape(chips * shard, grps * HD), n1x[...].reshape(chips * shard, width + HD),
        CONTRACT_FIRST, preferred_element_type=wide,
    ).reshape(grps, 2, half, width + HD)
    wm = remote(wgrad.at[:, 1 - p.core], wm_in, wm_send, wm_recv, p.grp, p.mate)
    wm.start()
    rail_step(1)
    wm.wait_recv()
    w_send_buf[...] = (wgrad[:, p.core] + wm_in[...]).astype(low)

    def w_copy(b):
        return remote(w_send_buf.at[b], w_in.at[b], w_send.at[b], w_recv.at[b], p.peer(b), p.seq)

    for b in range(1, grps):
        w_copy(b).start()
    for order in range(2, 2 * chips):
        rail_step(order)
    loads[2].wait()
    for b in range(1, grps):
        state_copy(b).wait_recv()
    o_terms[...] = lax.dot_general(
        at_all[...].reshape(grps * shard, slots * unit), stbuf[...].reshape(grps * shard, width),
        CONTRACT_FIRST, preferred_element_type=wide,
    ).reshape(chips, 2, unit, width)
    ob = remote(o_terms.at[:, 1 - p.core], ob_in, ob_send, ob_recv, p.grp, p.mate)
    ob.start()
    ob.wait_recv()
    o_send_buf[...] = (o_terms[:, p.core] + ob_in[...]).astype(low)

    def o_copy(chip):
        return remote(
            o_send_buf.at[chip], o_in.at[p.chip], o_send.at[chip], o_recv.at[p.chip], p.grp, 2 * chip + p.core
        )

    def o_arrival(chip):
        return remote(o_send_buf.at[chip], o_in.at[chip], o_send.at[chip], o_recv.at[chip], p.grp, p.mate)

    for chip in range(chips):
        pl.when(chip != p.chip)(lambda chip=chip: o_copy(chip).start())
    total = gain_own[...]
    for i in range(1, slots):
        g_copy(i).wait_recv()
        total = total + gain_in[i]
    gain_mid[...] = total
    for b in range(1, grps):
        h_copy(b).start()

    tokens = tokens_ref[...].astype(wide)
    tok_grad_ref[...] = part[p.chip].astype(wide)

    @pl.when(p.chip > 0)
    def _():
        to_right(p.chip).wait_recv()
        tok_grad_ref[...] += left_in[p.chip].astype(wide)

    @pl.when(p.chip < last)
    def _():
        to_left(p.chip).wait_recv()
        tok_grad_ref[...] += right_in[p.chip].astype(wide)

    n1g = tok_grad_ref[...]
    scale_one = lax.rsqrt(jnp.mean(tokens * tokens, axis=-1, keepdims=True) + EPS)
    normed = tokens * scale_one
    lifted = n1g * gain_one
    tok_grad_ref[...] = state_grad[...] + scale_one * (
        lifted - normed * jnp.mean(lifted * normed, axis=-1, keepdims=True)
    )

    wq_grad = wgrad[0, p.core] + wm_in[0]
    for b in range(1, grps):
        w_copy(b).wait_recv()
        wq_grad = wq_grad + w_in[b].astype(wide)
    wq_grad_ref[...] = wq_grad
    wo_grad = o_terms[p.chip, p.core] + ob_in[p.chip]
    for chip in range(chips):
        pl.when(chip != p.chip)(lambda chip=chip: o_arrival(chip).wait_recv())
        wo_grad = wo_grad + jnp.where(chip == p.chip, 0.0, o_in[chip].astype(wide))
    wo_grad_ref[...] = wo_grad
    total = gain_mid[...]
    for b in range(1, grps):
        h_copy(b).wait_recv()
        total = total + gain_mid_in[b]
    gain_ref[...] = total

    for hop, kind in late_hops:
        if FIRST_HOPS[hop][0] < 3:
            m_first(hop, kind).wait_recv()
        m_first(hop, kind).wait_send()
    for kind in (2, 0, 1):
        for i in (0, 1):
            m_second(i, kind).wait_recv()
            m_second(i, kind).wait_send()
    for copy in early_copies:
        copy.wait()
    ob.wait_send()
    wm.wait_send()
    for i in range(1, slots):
        g_copy(i).wait_send()
    for b in range(1, grps):
        state_copy(b).wait_send()
        w_copy(b).wait_send()
        h_copy(b).wait_send()
    for chip in range(chips):
        km_copy(chip).wait_send()

        @pl.when(chip != p.chip)
        def _(chip=chip):
            q_copy(chip, 0).wait_send()
            q_copy(chip, 1).wait_send()
            kr_copy(chip).wait_send()
            o_copy(chip).wait_send()

        pl.when(chip > p.chip)(lambda chip=chip: to_right(chip).wait_send())
        pl.when(chip < p.chip)(lambda chip=chip: to_left(chip).wait_send())


def back_call(n2g, state, cotangent, tokens, gain_one, gain_two, attn, q_heads, kv_heads, mask, cosine, sine,
              qkv_all, out_full, n1_all, terms, owned, passing, early):
    chips = cosine.shape[0]
    grps = 4
    slots = 2 * chips
    shard, width = tokens.shape
    att, block = out_full.shape[0], terms.shape[1] // grps
    unit, half = att // (grps * slots), HD // 2
    vm, dma = pltpu.VMEM, pltpu.SemaphoreType.DMA
    anyspace = pl.BlockSpec(memory_space=pl.ANY)
    vspec = pl.BlockSpec(memory_space=pltpu.VMEM)
    low, wide = jnp.bfloat16, jnp.float32
    struct = jax.ShapeDtypeStruct
    return pl.pallas_call(
        functools.partial(back_kernel, chips, 1.0 / math.sqrt(HD)),
        out_shape=(
            struct((shard, width), wide),
            struct((half, width + HD), wide),
            struct((unit, width), wide),
            struct((2, 1, width), wide),
            struct((3, block, width), low),
            struct((3, block, width), low),
        ),
        in_specs=[vspec] * 13 + [anyspace] * 6,
        out_specs=(vspec,) * 4 + (anyspace,) * 2,
        scratch_shapes=[
            vm((att, width), low),
            vm((grps, shard, width), low),
            vm((chips, shard, width + HD), low),
            vm((grps, shard, slots * unit), low),
            vm((chips, 3, shard, HD), low),
            vm((chips, 3, shard, HD), low),
            vm((chips, 2, chips, shard, HD), low),
            vm((chips, chips, shard, HD), low),
            vm((chips, chips, shard, HD), low),
            vm((chips, shard, HD), wide),
            vm((chips, chips, shard, HD), low),
            vm((chips, shard, grps * HD), low),
            vm((chips, shard, width), low),
            vm((chips, shard, width), low),
            vm((chips, shard, width), low),
            vm((grps, 2, half, width + HD), wide),
            vm((grps, half, width + HD), wide),
            vm((grps, half, width + HD), low),
            vm((grps, half, width + HD), low),
            vm((chips, 2, unit, width), wide),
            vm((chips, unit, width), wide),
            vm((chips, unit, width), low),
            vm((chips, unit, width), low),
            vm((2, 3, block // 2, width), low),
            vm((2, 3, block // 2, width), low),
            vm((2, block, width), low),
            vm((2, 1, width), wide),
            vm((slots, 2, 1, width), wide),
            vm((2, 1, width), wide),
            vm((grps, 2, 1, width), wide),
            vm((shard, width), wide),
            dma((3,)),
            dma((grps,)), dma((grps,)),
            dma((chips, 2)), dma((chips, 2)),
            dma((chips,)), dma((chips,)),
            dma((chips,)), dma((chips,)),
            dma((2, chips)), dma((2, chips)),
            dma, dma,
            dma((grps,)), dma((grps,)),
            dma, dma,
            dma((chips,)), dma((chips,)),
            dma((6, 3)), dma((6, 3)),
            dma((5, 3)),
            dma((slots,)), dma((slots,)),
            dma((grps,)), dma((grps,)),
        ],
        compiler_params=pltpu.CompilerParams(
            collective_id=3, has_side_effects=True, vmem_limit_bytes=62 * 2**20
        ),
        name="back",
    )(n2g, state, cotangent, tokens, gain_one, gain_two, attn, q_heads, kv_heads, mask, cosine, sine,
      qkv_all, out_full, n1_all, terms, owned, passing, early)


def columns_to_owners(rows, row_unit):
    grp_count, seq_count = lax.axis_size("grp"), lax.axis_size("seq")
    tok_rows = rows.shape[0]
    split = rows.reshape(tok_rows, grp_count, seq_count, row_unit).transpose(2, 0, 1, 3)
    split = split.reshape(seq_count * tok_rows, grp_count * row_unit)
    return lax.all_to_all(split, "seq", split_axis=0, concat_axis=0, tiled=True)


def owners_to_columns(rows, row_unit):
    grp_count, seq_count = lax.axis_size("grp"), lax.axis_size("seq")
    tok_rows = rows.shape[0] // seq_count
    moved = lax.all_to_all(rows, "seq", split_axis=0, concat_axis=0, tiled=True)
    moved = moved.reshape(seq_count, tok_rows, grp_count, row_unit).transpose(1, 2, 0, 3)
    return moved.reshape(tok_rows, grp_count * seq_count * row_unit)


def plain_mlp(normed_two, cotangent_all, mlp_weight):
    contract_last, contract_first = CONTRACT_LAST, CONTRACT_FIRST
    mlp_rows = lax.all_gather(mlp_weight, "grp", axis=0, tiled=True)
    normed_two_all = lax.all_gather(normed_two, "seq", axis=0, tiled=True)
    gate_rows, upper_rows, down_rows = mlp_rows[:, 0, :], mlp_rows[:, 1, :], mlp_rows[:, 2, :]
    gate_vals = lax.dot_general(
        normed_two_all, gate_rows, contract_last, preferred_element_type=jnp.float32
    )
    upper_vals = lax.dot_general(
        normed_two_all, upper_rows, contract_last, preferred_element_type=jnp.float32
    )
    unit_wide, pull_back = jax.vjp(swish_product, gate_vals, upper_vals)
    unit_low = unit_wide.astype(jnp.bfloat16)
    unit_grad = lax.dot_general(
        cotangent_all, down_rows, contract_last, preferred_element_type=jnp.float32
    )
    gate_grad, upper_grad = pull_back(unit_grad)
    gate_grad = gate_grad.astype(jnp.bfloat16)
    upper_grad = upper_grad.astype(jnp.bfloat16)
    input_grad = jnp.dot(gate_grad, gate_rows, preferred_element_type=jnp.float32) + jnp.dot(
        upper_grad, upper_rows, preferred_element_type=jnp.float32
    )
    grad_part = lax.psum_scatter(
        input_grad.astype(jnp.bfloat16), "seq", scatter_dimension=0, tiled=True
    ).astype(jnp.float32)
    out_part = lax.psum_scatter(
        jnp.dot(unit_low, down_rows, preferred_element_type=jnp.float32).astype(jnp.bfloat16),
        "seq",
        scatter_dimension=0,
        tiled=True,
    ).astype(jnp.float32)
    mlp_terms = jnp.stack(
        [
            lax.dot_general(
                gate_grad, normed_two_all, contract_first, preferred_element_type=jnp.float32
            ),
            lax.dot_general(
                upper_grad, normed_two_all, contract_first, preferred_element_type=jnp.float32
            ),
            lax.dot_general(
                unit_low, cotangent_all, contract_first, preferred_element_type=jnp.float32
            ),
        ],
        axis=1,
    )
    mlp_grad = lax.psum_scatter(mlp_terms, "grp", scatter_dimension=0, tiled=True)
    return grad_part, out_part, mlp_grad


def padded_rows(mlp_weight):
    rows = mlp_weight.transpose(1, 0, 2)
    return jnp.pad(rows, ((0, 0), (0, -rows.shape[1] % 32), (0, 0)))


def per_device(
    tokens,
    cotangent,
    shard_segment,
    gain_attn,
    qkv_weight,
    qkv_bias,
    out_weight,
    gain_mlp,
    mlp_weight,
):
    tok_rows = tokens.shape[0]
    seq_count = lax.axis_size("seq")
    grp_count = lax.axis_size("grp")
    group_tok = tok_rows * seq_count
    heads_per = H // KVH
    kv_width = KVH * HD
    att_width = H * HD
    query_rows = heads_per * tok_rows
    score_scale = 1.0 / math.sqrt(HD)
    contract_last = CONTRACT_LAST
    contract_first = CONTRACT_FIRST
    seq_place = lax.axis_index("seq")
    grp_place = lax.axis_index("grp")
    use_kernels = (seq_count, grp_count, H, KVH, HD) == (8, 4, 12, 2, 128)
    if use_kernels:
        half_freqs = np.float32(THETA) ** (-(np.arange(HD // 2, dtype=np.float32) * np.float32(2.0)) / np.float32(HD))
        freqs = np.concatenate([half_freqs, half_freqs])[None, :].astype(np.float32)
        gain_rows = (gain_attn[None, :], gain_mlp[None, :])
        own_rows = padded_rows(mlp_weight)
        (
            attn_wide, state, cosine, sine, mask, q_heads, kv_heads, n1_all, n2_all, cot_all, out_all,
            qkv_all, columns, *peer_rows
        ) = front_call(
            tokens, *gain_rows, shard_segment, freqs, qkv_bias[None, :], cotangent, qkv_weight, out_weight,
            own_rows,
        )
        by_slot = lambda rows: rows.reshape((seq_count,) + rows.shape[2:])
        grad_part, out_part, mlp_terms, owned, passing, early = mlp_call(
            by_slot(n2_all), by_slot(cot_all), columns, [own_rows, *peer_rows]
        )
        output = (state + out_part).astype(jnp.bfloat16)
        token_grad, qkv_terms, out_grad, gain_sums, direct, second = back_call(
            grad_part, state, cotangent, tokens, *gain_rows, attn_wide, q_heads, kv_heads, mask,
            cosine, sine, qkv_all.reshape(-1, qkv_all.shape[-1]),
            out_all.reshape(att_width, -1), n1_all, mlp_terms, owned, passing, early,
        )
        units = mlp_weight.shape[0]
        mlp_sums = sum(
            rows[:, :units].astype(jnp.float32) for rows in (mlp_terms, direct, second)
        )
        width = tokens.shape[1]
        own = width // (grp_count * seq_count)
        gain_parts = lax.dynamic_slice_in_dim(
            gain_sums[:, 0], (grp_place * seq_count + seq_place) * own, own, 1
        )
        return (
            output,
            token_grad,
            gain_parts[0],
            qkv_terms[:, :width],
            qkv_terms[:, width],
            out_grad,
            gain_parts[1],
            mlp_sums.transpose(1, 0, 2),
        )
    segments = lax.dynamic_index_in_dim(shard_segment, grp_place, 0, keepdims=False)
    starts = shard_starts(segments, tok_rows, group_tok // 2)
    shard_order = jnp.arange(seq_count, dtype=jnp.int32)
    own_seg = jnp.sum(jnp.where(shard_order == seq_place, segments, 0))
    own_start = jnp.sum(jnp.where(shard_order == seq_place, starts, 0))
    positions = own_start + jnp.arange(tok_rows, dtype=jnp.int32)
    cosine_table, sine_table = rotary_tables(positions, HD)
    query_pos = jnp.tile(positions, heads_per)
    tokens_wide = tokens.astype(jnp.float32)
    gain_one = gain_attn.astype(jnp.float32)
    gain_two = gain_mlp.astype(jnp.float32)
    normed_one = rms_scale(tokens_wide, gain_one).astype(jnp.bfloat16)
    normed_one_all = lax.all_gather(normed_one, "seq", axis=0, tiled=True)
    qkv_rows = lax.all_gather(qkv_weight, "grp", axis=0, tiled=True)
    bias_rows = lax.all_gather(qkv_bias, "grp", axis=0, tiled=True)
    cotangent_all = lax.all_gather(cotangent, "seq", axis=0, tiled=True)
    out_full = lax.all_gather(out_weight, AXES, axis=0, tiled=True)
    projected = lax.dot_general(
        normed_one_all, qkv_rows, contract_last, preferred_element_type=jnp.float32
    )
    projected = (projected + bias_rows.astype(jnp.float32)[None, :]).astype(jnp.bfloat16)
    projected = owners_to_columns(projected, qkv_weight.shape[0]).astype(jnp.float32)
    query_rot = rotate(
        projected[:, :att_width].reshape(tok_rows, H, HD), cosine_table, sine_table
    ).astype(jnp.bfloat16)
    key_rot = rotate(
        projected[:, att_width : att_width + kv_width].reshape(tok_rows, KVH, HD),
        cosine_table,
        sine_table,
    ).astype(jnp.bfloat16)
    value_low = projected[:, att_width + kv_width :].astype(jnp.bfloat16)
    keys_all, values_all = (
        lax.all_gather(key_rot.reshape(tok_rows, kv_width), "seq", axis=0, tiled=True),
        lax.all_gather(value_low, "seq", axis=0, tiled=True),
    )
    queries = (
        query_rot.reshape(tok_rows, KVH, heads_per, HD)
        .transpose(1, 2, 0, 3)
        .reshape(KVH, query_rows, HD)
    )
    key_block = min(512, group_tok)
    block_count = group_tok // key_block
    block_order = jnp.arange(block_count, dtype=jnp.int32)

    def block_mask(block_index):
        key_index = block_index * key_block + jnp.arange(key_block, dtype=jnp.int32)
        key_shard = key_index // tok_rows
        onehot = key_shard[:, None] == shard_order[None, :]
        key_seg = jnp.sum(jnp.where(onehot, segments[None, :], 0), axis=1)
        key_pos = jnp.sum(jnp.where(onehot, starts[None, :], 0), axis=1) + key_index % tok_rows
        visible = (key_seg == 0) | (key_seg == own_seg)
        return visible[None, :] & (key_pos[None, :] <= query_pos[:, None])

    def block_keys(block_index):
        key_part = lax.dynamic_slice_in_dim(
            keys_all, block_index * key_block, key_block, 0
        ).reshape(key_block, KVH, HD)
        value_part = lax.dynamic_slice_in_dim(
            values_all, block_index * key_block, key_block, 0
        ).reshape(key_block, KVH, HD)
        return (key_part, value_part)

    def block_scores(key_part):
        return (
            jnp.einsum("krd,jkd->krj", queries, key_part, preferred_element_type=jnp.float32)
            * score_scale
        )

    def stat_step(stats_now, block_index):
        allowed = block_mask(block_index)

        def stat_visit(current):
            top_old, total_old = current
            key_part, value_part = block_keys(block_index)
            scores = jnp.where(allowed[None], block_scores(key_part), -1e30)
            top_new = jnp.maximum(top_old, jnp.max(scores, axis=-1))
            weights = jnp.where(allowed[None], jnp.exp(scores - top_new[..., None]), 0.0)
            return (top_new, total_old * jnp.exp(top_old - top_new) + jnp.sum(weights, axis=-1))

        return (lax.cond(jnp.any(allowed), stat_visit, lambda current: current, stats_now), None)

    start_stats = (
        jnp.full((KVH, query_rows), -1e30, jnp.float32),
        jnp.zeros((KVH, query_rows), jnp.float32),
    )
    (top_all, total_all), unused = lax.scan(stat_step, start_stats, block_order)
    log_total = top_all + jnp.log(total_all)

    def mix_step(mixed_sum, block_index):
        allowed = block_mask(block_index)

        def mix_visit(current):
            key_part, value_part = block_keys(block_index)
            prob_low = jnp.where(
                allowed[None], jnp.exp(block_scores(key_part) - log_total[..., None]), 0.0
            ).astype(jnp.bfloat16)
            return current + jnp.einsum(
                "krj,jkd->krd", prob_low, value_part, preferred_element_type=jnp.float32
            )

        return (lax.cond(jnp.any(allowed), mix_visit, lambda current: current, mixed_sum), None)

    mixed_sum, unused = lax.scan(
        mix_step, jnp.zeros((KVH, query_rows, HD), jnp.float32), block_order
    )
    attn_wide = (
        mixed_sum.reshape(KVH, heads_per, tok_rows, HD)
        .transpose(2, 0, 1, 3)
        .reshape(tok_rows, att_width)
    )
    attn_low = attn_wide.astype(jnp.bfloat16)
    attn_proj = jnp.dot(attn_low, out_full, preferred_element_type=jnp.float32)
    state = tokens_wide + attn_proj
    normed_two = rms_scale(state, gain_two).astype(jnp.bfloat16)
    grad_part, out_part, mlp_grad = plain_mlp(normed_two, cotangent_all, mlp_weight)
    output = (state + out_part).astype(jnp.bfloat16)
    unused_state, norm_two_back = jax.vjp(rms_scale, state, gain_two)
    state_norm_grad, gain_two_grad = norm_two_back(grad_part)
    state_grad = state_norm_grad + cotangent.astype(jnp.float32)
    state_low = state_grad.astype(jnp.bfloat16)
    attn_grad = lax.dot_general(
        state_low, out_full, contract_last, preferred_element_type=jnp.float32
    )
    attn_grad_low = attn_grad.astype(jnp.bfloat16)
    attn_owned = columns_to_owners(attn_low, out_weight.shape[0])
    state_low_all = lax.all_gather(state_low, "seq", axis=0, tiled=True)
    out_grad = lax.psum_scatter(
        lax.dot_general(
            attn_owned, state_low_all, contract_first, preferred_element_type=jnp.float32
        ),
        "grp",
        scatter_dimension=0,
        tiled=True,
    )
    grad_heads = (
        attn_grad_low.reshape(tok_rows, KVH, heads_per, HD)
        .transpose(1, 2, 0, 3)
        .reshape(KVH, query_rows, HD)
    )
    delta_rows = jnp.sum(
        (attn_grad_low.astype(jnp.float32) * attn_wide).reshape(tok_rows, H, HD), axis=-1
    )
    delta_rows = (
        delta_rows.reshape(tok_rows, KVH, heads_per).transpose(1, 2, 0).reshape(KVH, query_rows)
    )

    def back_step(query_grad, block_index):
        allowed = block_mask(block_index)

        def back_visit(current):
            key_part, value_part = block_keys(block_index)
            prob_vals = jnp.where(
                allowed[None], jnp.exp(block_scores(key_part) - log_total[..., None]), 0.0
            )
            prob_grad = jnp.einsum(
                "krd,jkd->krj", grad_heads, value_part, preferred_element_type=jnp.float32
            )
            score_grad = (prob_vals * (prob_grad - delta_rows[..., None])).astype(jnp.bfloat16)
            new_grad = (
                current
                + jnp.einsum(
                    "krj,jkd->krd", score_grad, key_part, preferred_element_type=jnp.float32
                )
                * score_scale
            )
            key_grad = (
                jnp.einsum("krj,krd->jkd", score_grad, queries, preferred_element_type=jnp.float32)
                * score_scale
            )
            value_grad = jnp.einsum(
                "krj,krd->jkd",
                prob_vals.astype(jnp.bfloat16),
                grad_heads,
                preferred_element_type=jnp.float32,
            )
            return (
                new_grad,
                (key_grad.reshape(key_block, kv_width), value_grad.reshape(key_block, kv_width)),
            )

        def skip_block(current):
            blank_rows = jnp.zeros((key_block, kv_width), jnp.float32)
            return (current, (blank_rows, blank_rows))

        return lax.cond(jnp.any(allowed), back_visit, skip_block, query_grad)

    query_grad, (key_grads, value_grads) = lax.scan(
        back_step, jnp.zeros((KVH, query_rows, HD), jnp.float32), block_order
    )
    key_own, value_own = (
        lax.psum_scatter(
            key_grads.reshape(group_tok, kv_width).astype(jnp.bfloat16),
            "seq",
            scatter_dimension=0,
            tiled=True,
        ).astype(jnp.float32),
        lax.psum_scatter(
            value_grads.reshape(group_tok, kv_width).astype(jnp.bfloat16),
            "seq",
            scatter_dimension=0,
            tiled=True,
        ).astype(jnp.float32),
    )
    query_back = unrotate(
        query_grad.reshape(KVH, heads_per, tok_rows, HD)
        .transpose(2, 0, 1, 3)
        .reshape(tok_rows, H, HD),
        cosine_table,
        sine_table,
    )
    key_back = unrotate(key_own.reshape(tok_rows, KVH, HD), cosine_table, sine_table)
    qkv_grad_low = jnp.concatenate(
        [query_back.reshape(tok_rows, att_width), key_back.reshape(tok_rows, kv_width), value_own],
        axis=1,
    ).astype(jnp.bfloat16)
    qkv_grad_owned = columns_to_owners(qkv_grad_low, qkv_weight.shape[0])
    bias_terms = jnp.sum(qkv_grad_owned.astype(jnp.float32), axis=0)
    normed_one_grad = lax.psum_scatter(
        jnp.dot(qkv_grad_owned, qkv_rows, preferred_element_type=jnp.float32).astype(jnp.bfloat16),
        "seq",
        scatter_dimension=0,
        tiled=True,
    ).astype(jnp.float32)
    qkv_grad = lax.psum_scatter(
        lax.dot_general(
            qkv_grad_owned, normed_one_all, contract_first, preferred_element_type=jnp.float32
        ),
        "grp",
        scatter_dimension=0,
        tiled=True,
    )
    unused_tokens, norm_one_back = jax.vjp(rms_scale, tokens_wide, gain_one)
    token_norm_grad, gain_one_grad = norm_one_back(normed_one_grad)
    token_grad = token_norm_grad + state_grad
    bias_part = lax.psum_scatter(bias_terms, "grp", scatter_dimension=0, tiled=True)
    gain_one_part, gain_two_part = (
        lax.psum_scatter(gain_one_grad, AXES, scatter_dimension=0, tiled=True),
        lax.psum_scatter(gain_two_grad, AXES, scatter_dimension=0, tiled=True),
    )
    return (
        output,
        token_grad,
        gain_one_part,
        qkv_grad,
        bias_part,
        out_grad,
        gain_two_part,
        mlp_grad,
    )


def solution(mesh):
    return jax.shard_map(
        per_device,
        mesh=mesh,
        in_specs=(
            P(("grp", "seq"), None),
            P(("grp", "seq"), None),
            P(),
            P(),
            P(("grp", "seq"), None),
            P(("grp", "seq")),
            P(("grp", "seq"), None),
            P(),
            P(("grp", "seq"), None, None),
        ),
        out_specs=(
            P(("grp", "seq"), None),
            P(("grp", "seq"), None),
            P(("grp", "seq")),
            P(("grp", "seq"), None),
            P(("grp", "seq")),
            P(("grp", "seq"), None),
            P(("grp", "seq")),
            P(("grp", "seq"), None, None),
        ),
        check_vma=False,
    )
```
